32 devices in a mesh: dp: 2 (over core), space: 16 (over z, y, x).
Axes of the slice: x: 2, y: 2, z: 4, core: 2. Of those that a mesh axis runs over, the one named last changes fastest.
Arguments:
- master: float32 [1156352], P(('dp', 'space')), may hold values from -0.375 to 0.375
- moment1: float32 [1156352], P(('dp', 'space')), may hold values from -7.6293945e-05 to 7.6293945e-05
- moment2: float32 [1156352], P(('dp', 'space')), may hold values from 2.1619713e-12 to 8.647885e-12
- inputs: bfloat16 [2, 78, 8192], P('dp', None, 'space'), may hold values from -6 to 6
- targets: bfloat16 [2, 78, 8192], P('dp', None, 'space'), may hold values from -6 to 6
- valid: int32 [2, 78, 8192], P('dp', None, 'space'), may hold values from 0 to 1
- owner: int32 [2, 8192, 1], P('dp', 'space'), may hold values from 0 to 15; in each aligned block of 512 rows (0 to 511, 512 to 1023, ..., all dimensions but the last counted through in order) at most 64 rows name the same one
- slot: int32 [2, 8192], P('dp', 'space'), may hold values from 0 to 2047
- neighbours: int32 [32768, 6], P('space'), may hold values from 0 to 32767, as said below
- partner: int32 [8192], P('space'), may hold values from 0 to 8191, as said below
Outputs:
- loss_total: float32 [1], replicated
- valid_count: float32 [1], replicated
- grad_norm: float32 [1], replicated
- new_master: float32 [1156352], P(('dp', 'space'))
- new_moment1: float32 [1156352], P(('dp', 'space'))
- new_moment2: float32 [1156352], P(('dp', 'space'))
- new_copy: bfloat16 [1156352], P(('dp', 'space'))
- final_mesh: float32 [2, 32768, 256], P('dp', 'space')
- node_grads: float32 [2, 32768, 256], P('dp', 'space')
- pred_grads: float32 [2, 78, 8192], P('dp', None, 'space')
The draws below stay inside these ranges and needn't reach their ends.
Inputs may be any that keep to these rules, and one draw needn't show every extreme that they name: `neighbours`: each entry is a node number within 2048 of its row's own number, counted cyclically over 32768; a distance of exactly 2048 occurs in both directions. partner[g] - g lies in 358 to 360; where that passes the last point, partner[g] = g.
All inputs are finite; a program needn't handle non-finite values.
Results may differ from the reference program's by a relative error of at most 0.014.
Values may be sent and summed in bfloat16 or wider, within the bound.
No kernel may reach another device: no remote copies, remote signals or barrier semaphores. Data moves between devices by JAX's collectives and lax.ppermute only.
A program may use at most 192 MiB of HBM per device.

```python
import math
import jax
import jax.numpy as jnp
import numpy as np
from jax import lax

D = 256
CH = 78
ROUNDS = 3
K = 6
ROWW = 360
STEP = 10
G_DEV = 512
M_DEV = 2048
H = 2048
SAMPLES = 2
GRID = 8192
MESH = 32768
CAP = 64
NPAR = 1156352
N_DP = 2
N_SPACE = 16


def draw_neighbours(key, part):
    node = jnp.arange(MESH, dtype=jnp.int32)[:, None]
    magnitude = jax.random.randint(key, (MESH, K), 1, H + 1)
    signs = jax.random.randint(jax.random.fold_in(key, 1), (MESH, K), 0, 2) * 2 - 1
    offset = magnitude * signs
    offset = offset.at[0, 0].set(H).at[1, 1].set(-H)
    return ((node + offset) % MESH).astype(jnp.int32)


def draw_partner(key, part):
    point = jnp.arange(GRID, dtype=jnp.int32)
    offset = ROWW - jax.random.randint(key, (GRID,), 0, 3)
    target = point + offset
    return jnp.where(target < GRID, target, point).astype(jnp.int32)


def draw_valid(key, part):
    last_band = max(GRID // G_DEV - 1, 1)
    band_index = (jnp.arange(GRID, dtype=jnp.int32) // G_DEV)[None, None, :]
    sample_index = jnp.arange(SAMPLES, dtype=jnp.int32)[:, None, None]
    threshold = 100 * (2 + sample_index) * (last_band + 2 * band_index) // last_band
    score = jax.random.randint(jax.random.fold_in(key, 7), (SAMPLES, CH, GRID), 0, 1000)
    return (score < threshold).astype(jnp.int32)


def plant(array, key, smallest, largest):
    place = [jax.random.randint(jax.random.fold_in(key, axis), (), 0, length) for axis, length in enumerate(array.shape)]
    main_axis = array.shape.index(max(array.shape))
    beside = place[:main_axis] + [(place[main_axis] + 1) % array.shape[main_axis]] + place[main_axis + 1:]
    return array.at[tuple(place)].set(smallest).at[tuple(beside)].set(largest)


def steps_of(own_key, extent, cuts, least, high):
    def one(position, blocks):
        heights = jax.random.uniform(jax.random.fold_in(jax.random.fold_in(own_key, 6), position), (blocks,), jnp.float32, least / len(cuts), high / len(cuts))
        return jnp.repeat(jnp.exp(heights), extent[position] // blocks).reshape((-1,) + (1,) * (len(extent) - position - 1))

    loudness = one(*cuts[0])
    for cut in cuts[1:]:
        loudness = loudness * one(*cut)
    return loudness


def shared_out(key, own, number, rows, amount, top, reach, skew):
    sequence = jax.random.permutation(key, amount)
    packed, common = load_shares(amount, rows * top, reach, skew, True), load_shares(amount, rows * top, reach, skew, False)
    places = jnp.arange(amount)

    def named(lengths, turn):
        used = int((lengths > 0).sum())
        fixed = max(1, used // 4)
        passed = fixed + (places - fixed + turn * (used - fixed)) % max(1, amount - fixed)
        return jnp.zeros((amount,), jnp.int32).at[sequence[jnp.where(places < fixed, places, passed)]].set(jnp.asarray(lengths, jnp.int32))

    lengths = jnp.where(number % 4 == 0, named(packed, number // 4), named(common, number - number // 4 - 1))
    mixed = jax.random.permutation(jax.random.fold_in(own, 3), amount)
    source_of, taker = mixed[0:amount // 2 * 2:2], mixed[1:amount // 2 * 2:2]
    slack = jnp.minimum(lengths[source_of] - 1, reach - lengths[taker]) // 2
    slack = jnp.where((source_of == sequence[0]) | (taker == sequence[0]) | (lengths[taker] == 0), 0, jnp.maximum(slack, 0))
    passed = jax.random.randint(jax.random.fold_in(own, 4), (amount // 2,), 0, 1 << 20) % (slack + 1)
    lengths = lengths.at[source_of].add(-passed).at[taker].add(passed)
    labels = jnp.searchsorted(jnp.cumsum(lengths), jnp.arange(rows * top), side="right").astype(jnp.int32)
    listing = labels.reshape(top, rows).T
    listing = listing[jax.random.permutation(jax.random.fold_in(own, 1), rows)]
    turn = jax.random.randint(jax.random.fold_in(own, 2), (rows, 1), 0, top)
    return jnp.take_along_axis(listing, (jnp.arange(top)[None, :] + turn) % top, axis=1)


def load_shares(amount, total, reach, slope, full):
    portions = [(1 << 20) // math.isqrt(grade ** slope) + 1 for grade in range(1, amount + 1)]
    largest = reach if full else min(reach, max(-(-total // amount), total * portions[0] // sum(portions)))
    least = 1 if total - largest >= amount - 1 else 0
    holding, spare = [largest] + [least] * (amount - 1), total - largest - least * (amount - 1)
    while spare > 0:
        free = [i for i in range(1, amount) if holding[i] < largest] or [i for i in range(1, amount) if holding[i] < reach]
        whole, budget = sum([portions[i] for i in free]), spare
        for i in free:
            addition = min(reach - holding[i], max(1, budget * portions[i] // whole), spare)
            holding[i] = holding[i] + addition
            spare = spare - addition
    return np.array(holding)


def scatter_about(key, dims, spread, bound, shards=(), kind=jnp.bfloat16):
    drawn = spread * jax.random.normal(key, dims, jnp.float32)
    if shards:
        drawn = drawn * steps_of(key, dims, shards, -0.22, 0.18)
    return jnp.clip(drawn, -bound, bound).astype(kind)


def setup_inputs(seed: int = 0) -> dict:
    key_list = jax.random.split(jax.random.key(seed), 11)
    master = scatter_about(key_list[0], (NPAR,), (D ** -0.5), 0.375, ((0, 32),), jnp.float32)
    moment1 = scatter_about(key_list[1], (NPAR,), (0.111 * 0.05 / NPAR ** 0.5), 7.62939453125e-05, ((0, 32),), jnp.float32)
    moment2 = jnp.clip(jnp.exp(math.log(8.647885359203134e-12) - 1.3862944 * jax.random.uniform(key_list[2], (NPAR,), jnp.float32) ** steps_of(key_list[2], (NPAR,), ((0, 32),), -0.2, 0.2)), 2.1619713398007834e-12, 8.647885359203134e-12)
    inputs = scatter_about(key_list[3], (SAMPLES, CH, GRID), 1.0, 6.0, ((0, 2), (2, 16)))
    targets = scatter_about(key_list[4], (SAMPLES, CH, GRID), 1.0, 6.0, ((0, 2), (2, 16)))
    valid = draw_valid(jax.random.fold_in(key_list[10], 71), 0)
    owner_keys = jax.random.split(jax.random.fold_in(key_list[6], 1), SAMPLES * GRID // G_DEV)
    owner_turns = jax.random.permutation(jax.random.fold_in(key_list[6], 3), SAMPLES * GRID // G_DEV)
    owner = jax.vmap(lambda own, number: shared_out(jax.random.fold_in(key_list[6], 2), own, number, G_DEV, N_SPACE, 1, CAP, 2))(owner_keys, owner_turns).reshape((SAMPLES, GRID, 1))
    slot = plant(jax.random.randint(key_list[7], (SAMPLES, GRID), 0, M_DEV), jax.random.fold_in(key_list[7], 1), 0, M_DEV - 1).astype(jnp.int32)
    neighbours = draw_neighbours(jax.random.fold_in(key_list[10], 71), 0)
    partner = draw_partner(jax.random.fold_in(key_list[10], 71), 0)
    return dict(master=master, moment1=moment1, moment2=moment2, inputs=inputs, targets=targets, valid=valid, owner=owner, slot=slot, neighbours=neighbours, partner=partner)


@jax.custom_vjp
def low(v):
    return lax.optimization_barrier(v.astype(jnp.bfloat16)).astype(jnp.float32)

@jax.custom_vjp
def low_back(v):
    return v

def low_keep(v):
    return (low(v), None)

def low_pass(kept, grad):
    return (grad,)

def back_keep(v):
    return (v, None)

def back_low(kept, grad):
    return (low(grad),)
low.defvjp(low_keep, low_pass)
low_back.defvjp(back_keep, back_low)

def layout():
    return [(CH, D), (D, D), (D, D), (D, CH), (ROUNDS, 5, D, D), (3, D), (ROUNDS, 2, D)]

def unpack(flat):
    pieces = []
    start = 0
    for shape in layout():
        count = math.prod(shape)
        pieces.append(flat[start:start + count].reshape(shape))
        start = start + count
    return pieces

def matmul(left, right):
    return jnp.dot(left, right, precision=lax.Precision.HIGHEST)

def round_step(mesh, mats, bias, neighbours):
    lowered = low(mesh)
    sent = low_back(low(matmul(lowered, mats[0])))
    dest = low_back(matmul(lowered, mats[1]) + bias[0])
    agg = jnp.zeros_like(mesh)
    for edge in range(K):
        agg = agg + jax.nn.silu(sent[neighbours[:, edge]] + dest)
    agg = agg / K
    upd = jax.nn.silu(low_back(matmul(low(agg), mats[2]) + matmul(lowered, mats[3]) + bias[1]))
    return mesh + low_back(matmul(low(upd), mats[4]))

def forward(params, xs, ys, vs, nodes, neighbours, partner, count):
    flat, mesh_shift, pred_shift = params
    w_in, w_node, w_dec, w_out, w_round, b_head, b_round = unpack(low(flat))
    stepper = jax.checkpoint(round_step)
    total = jnp.float32(0.0)
    finals = []
    for sample in range(N_DP):
        inputs = xs[sample]
        encoded = low_back(low(jax.nn.silu(matmul(inputs.T, w_in) + b_head[0])))
        gathered = jax.ops.segment_sum(encoded, nodes[sample], num_segments=MESH)
        mesh = jax.nn.silu(low_back(matmul(low(gathered), w_node) + b_head[1])) + mesh_shift[sample]
        for layer in range(ROUNDS):
            mesh = stepper(mesh, w_round[layer], b_round[layer], neighbours)
        finals.append(mesh)
        fetched = low_back(low(mesh)[nodes[sample]])
        decoded = jax.nn.silu(low_back(matmul(fetched, w_dec) + b_head[2]))
        branch = low_back(matmul(low(decoded), w_out))
        err = inputs + branch.T + pred_shift[sample] - ys[sample]
        valid = vs[sample]
        err_far = err[:, partner]
        valid_far = valid[:, partner]
        total = total + jnp.sum(valid * err * err) + 0.5 * jnp.sum(valid * valid_far * (err - err_far) ** 2)
    return (total / count, (total, jnp.stack(finals)))

def reference(master, moment1, moment2, inputs, targets, valid, owner, slot, neighbours, partner):
    xs = inputs.astype(jnp.float32)
    ys = targets.astype(jnp.float32)
    vs = valid.astype(jnp.float32)
    nodes = (owner[:, :, 0] * M_DEV + slot).astype(jnp.int32)
    count = jnp.sum(vs)
    mesh_zero = jnp.zeros((SAMPLES, MESH, D), jnp.float32)
    pred_zero = jnp.zeros((SAMPLES, CH, GRID), jnp.float32)
    loss, pull, extra = jax.vjp(lambda params: forward(params, xs, ys, vs, nodes, neighbours, partner, count), (master, mesh_zero, pred_zero), has_aux=True)
    total, finals = extra
    gradient, node_grads, pred_grads = pull(jnp.ones_like(loss))[0]
    norm = jnp.sqrt(jnp.sum(gradient * gradient))
    clipped = gradient * jnp.minimum(1.0, 0.05 / norm)
    first = 0.9 * moment1 + 0.1 * clipped
    second = 0.999 * moment2 + 0.001 * clipped * clipped
    first_hat = first / (1.0 - 0.9 ** STEP)
    second_hat = second / (1.0 - 0.999 ** STEP)
    updated = master - 0.1 * (first_hat / (jnp.sqrt(second_hat) + 1e-08) + 0.1 * master)
    return (total.reshape(1), count.reshape(1), norm.reshape(1), updated, first, second, updated.astype(jnp.bfloat16), finals, node_grads, pred_grads)
```

```python
import math

import jax
import jax.numpy as jnp
from jax import lax
from jax.experimental import pallas as pl
from jax.experimental.pallas import tpu as pltpu
from jax.sharding import PartitionSpec as P

D = 256
HALF = 128
CH = 78
ROUNDS = 3
K = 6
ROWW = 360
NEAR = 358
STEP = 10
H = 2048
TABLES = 4
UNROLL = 32
ALL = ("dp", "space")
LIMIT = pltpu.CompilerParams(vmem_limit_bytes=56 * 2**20)


def inner(left, right, left_dim, right_dim):
    return lax.dot_general(
        left, right, (((left_dim,), (right_dim,)), ((), ())), preferred_element_type=jnp.float32
    )


def sigmoid(value):
    return 0.5 * jnp.tanh(0.5 * value) + 0.5


def silu(value):
    return value * sigmoid(value)


def slope(value):
    sigma = sigmoid(value)
    return sigma * (1.0 + value * (1.0 - sigma))


def shifted(shard, axis, by):
    peers = lax.axis_size(axis)
    pairs = [(i, i + by) for i in range(peers) if 0 <= i + by < peers]
    return lax.ppermute(shard, axis, pairs)


def halo(last, initial):
    peers = lax.axis_size("space")
    up = [(i, (i + 1) % peers) for i in range(peers)]
    down = [(j, i) for i, j in up]
    return lax.ppermute(last, "space", up), lax.ppermute(initial, "space", down)


def pieces_of(total, peers):
    share = total // peers
    starts = [share * d // D for d in range(peers)]
    counts = [-(-share * (d + 1) // D) - starts[d] for d in range(peers)]
    shared = [share * d % D != 0 for d in range(peers)]
    height = -(-max(counts) // 16) * 16
    return starts, counts, shared, height


def parts_of():
    return [CH, D, D, CH, ROUNDS * 5 * D, 3 + 2 * ROUNDS]


def spread_rows(gathered, total):
    peers, height, _ = gathered.shape
    starts, counts, shared, _ = pieces_of(total, peers)
    rows = -(-total // D)
    sizes = parts_of()

    def body(source, *refs):
        outs, buffer = refs[:-1], refs[-1]
        for d in range(peers):
            piece = source[d].astype(jnp.float32)
            at, count = starts[d], counts[d]
            if shared[d]:
                buffer[at : at + 1, :] = buffer[at : at + 1, :] + piece[:1]
                buffer[at + 1 : at + count, :] = piece[1:count]
            else:
                buffer[at : at + count, :] = piece[:count]
        start = 0
        for out, size in zip(outs, sizes):
            out[...] = buffer[start : start + size, :].astype(out.dtype)
            start = start + size

    kinds = [jnp.bfloat16] * 5 + [jnp.float32]
    return pl.pallas_call(
        body,
        out_shape=[jax.ShapeDtypeStruct((size, D), kind) for size, kind in zip(sizes, kinds)],
        scratch_shapes=[pltpu.VMEM((-(-rows // 8) * 8 + 8, D), jnp.float32)],
        compiler_params=LIMIT,
        name="spread_rows",
    )(gathered)


def collect_rows(parts, total, peers):
    starts, counts, shared, height = pieces_of(total, peers)
    rows = -(-total // D)
    used = sum(part.shape[0] for part in parts)

    def body(*refs):
        sources, out, buffer = refs[:-2], refs[-2], refs[-1]
        start = 0
        for source in sources:
            size = source.shape[0]
            buffer[start : start + size, :] = source[...]
            start = start + size
        if buffer.shape[0] > start:
            buffer[start:, :] = jnp.zeros((buffer.shape[0] - start, D), jnp.float32)
        for d in range(peers):
            out[d] = buffer[starts[d] : starts[d] + height, :]

    return pl.pallas_call(
        body,
        out_shape=jax.ShapeDtypeStruct((peers, height, D), jnp.float32),
        scratch_shapes=[pltpu.VMEM((-(-max(rows, used) // 8) * 8 + height + 8, D), jnp.float32)],
        compiler_params=LIMIT,
        name="collect_rows",
    )(*parts)


def gather_rows(index, before, own, after):
    edges = index.shape[0]
    chunk = 1024
    spans = [before.shape[0], own.shape[0], after.shape[0]]

    def body(index_ref, before_ref, own_ref, after_ref, out_ref, table, sems):
        step = pl.program_id(0)

        @pl.when(step == 0)
        def _():
            copies = []
            start = 0
            for n, (source, span) in enumerate(zip((before_ref, own_ref, after_ref), spans)):
                copies.append(
                    pltpu.make_async_copy(source, table.at[pl.ds(start, span)], sems.at[n])
                )
                start = start + span
            for copy in copies:
                copy.start()
            for copy in copies:
                copy.wait()

        def some(i, carry):
            at = i * UNROLL
            base = step * chunk + at
            rows = [table[index_ref[base + u]] for u in range(UNROLL)]
            for u in range(UNROLL):
                out_ref[at + u] = rows[u]
            return carry

        lax.fori_loop(0, chunk // UNROLL, some, 0)

    return pl.pallas_call(
        body,
        grid_spec=pltpu.PrefetchScalarGridSpec(
            num_scalar_prefetch=1,
            grid=(edges // chunk,),
            in_specs=[pl.BlockSpec(memory_space=pl.ANY)] * 3,
            out_specs=pl.BlockSpec((chunk, 2, HALF), lambda i, *_: (i, 0, 0)),
            scratch_shapes=[
                pltpu.VMEM((sum(spans), 2, HALF), own.dtype),
                pltpu.SemaphoreType.DMA((3,)),
            ],
        ),
        out_shape=jax.ShapeDtypeStruct((edges, 2, HALF), own.dtype),
        compiler_params=LIMIT,
        name="gather_rows",
    )(index, before, own, after)


def weave(ref, value):
    rows = value.shape[0]
    ref[pl.ds(0, rows, stride=2), :] = value[:, :HALF]
    ref[pl.ds(1, rows, stride=2), :] = value[:, HALF:]


def unweave(ref):
    rows = ref.shape[0] // 2
    return ref[pl.ds(0, rows, stride=2), :], ref[pl.ds(1, rows, stride=2), :]


def whole(shape):
    return pl.BlockSpec(shape, lambda *_: (0,) * len(shape))


def round_forward(mesh, edges, mats, bias, following):
    blocks = mesh.shape[0]
    tile = 256
    more = following is not None

    def body(*refs):
        if more:
            (mesh_ref, edge_ref, mats_ref, bias_ref, next_ref, new_ref, uin_ref, agg_ref, sent_ref, wide) = refs
        else:
            (mesh_ref, edge_ref, mats_ref, bias_ref, new_ref, uin_ref, agg_ref, wide) = refs
        mesh_in = mesh_ref[...]
        lowered = mesh_in.astype(jnp.bfloat16)
        weave(wide, inner(lowered, mats_ref[1], 1, 0) + bias_ref[0:1, :])
        dest = wide[...]
        total = jnp.zeros(dest.shape, jnp.float32)
        for edge in range(K):
            total = total + silu(edge_ref[edge].astype(jnp.float32) + dest)
        wide[...] = total * (1.0 / K)
        first, second = unweave(wide)
        first, second = first.astype(jnp.bfloat16), second.astype(jnp.bfloat16)
        agg_ref[:, :HALF] = first
        agg_ref[:, HALF:] = second
        update_in = (
            inner(first, mats_ref[2, :HALF, :], 1, 0)
            + inner(second, mats_ref[2, HALF:, :], 1, 0)
            + inner(lowered, mats_ref[3], 1, 0)
            + bias_ref[1:2, :]
        )
        uin_ref[...] = update_in
        update = silu(update_in).astype(jnp.bfloat16)
        new = mesh_in + inner(update, mats_ref[4], 1, 0)
        new_ref[...] = new
        if more:
            weave(wide, inner(new.astype(jnp.bfloat16), next_ref[...], 1, 0))
            sent_ref[...] = wide[...].astype(jnp.bfloat16)

    rows = pl.BlockSpec((tile, D), lambda i: (i, 0))
    woven = pl.BlockSpec((2 * tile, HALF), lambda i: (i, 0))
    ins = [rows, pl.BlockSpec((K, 2 * tile, HALF), lambda i: (0, i, 0)), whole(mats.shape), whole(bias.shape)]
    outs = [rows, rows, rows]
    shapes = [
        jax.ShapeDtypeStruct((blocks, D), jnp.float32),
        jax.ShapeDtypeStruct((blocks, D), jnp.float32),
        jax.ShapeDtypeStruct((blocks, D), jnp.bfloat16),
    ]
    args = [mesh, edges, mats, bias]
    if more:
        ins.append(whole(following.shape))
        outs.append(woven)
        shapes.append(jax.ShapeDtypeStruct((2 * blocks, HALF), jnp.bfloat16))
        args.append(following)
    return pl.pallas_call(
        body,
        grid=(blocks // tile,),
        in_specs=ins,
        out_specs=outs,
        out_shape=shapes,
        scratch_shapes=[pltpu.VMEM((2 * tile, HALF), jnp.float32)],
        compiler_params=LIMIT,
        name="round_forward",
    )(*args)


def edges_backward(index, grad_mesh, mesh, uin, edges, mats, bias):
    blocks = mesh.shape[0]
    tile = 256
    steps = blocks // tile
    reach = 2 * (blocks + 2 * H)

    def body(
        index_ref, grad_ref, mesh_ref, uin_ref, edge_ref, mats_ref, bias_ref,
        guin_ref, low_ref, before_ref, own_ref, after_ref, wide, wider, flows, *tables,
    ):
        step = pl.program_id(0)

        @pl.when(step == 0)
        def _():
            for table in tables:
                table[...] = jnp.zeros(table.shape, jnp.float32)

        grad_out = grad_ref[...].astype(jnp.bfloat16)
        grad_update = inner(grad_out, mats_ref[4], 1, 1)
        grad_uin = (grad_update * slope(uin_ref[...])).astype(jnp.bfloat16)
        guin_ref[...] = grad_uin
        weave(wide, inner(grad_uin, mats_ref[2], 1, 1) * (1.0 / K))
        lowered = mesh_ref[...].astype(jnp.bfloat16)
        weave(wider, inner(lowered, mats_ref[1], 1, 0) + bias_ref[0:1, :])
        grad_agg = wide[...]
        dest = wider[...]
        grad_dest = jnp.zeros(dest.shape, jnp.float32)
        for edge in range(K):
            flow = grad_agg * slope(edge_ref[edge].astype(jnp.float32) + dest)
            grad_dest = grad_dest + flow
            flows[edge * 2 * tile : (edge + 1) * 2 * tile, :] = flow
        wide[...] = grad_dest
        first, second = unweave(wide)
        low_ref[:, :HALF] = first.astype(jnp.bfloat16)
        low_ref[:, HALF:] = second.astype(jnp.bfloat16)
        for edge in range(K):

            def some(i, carry):
                at = i * UNROLL
                base = edge * blocks + step * tile + at
                for first in range(0, UNROLL, TABLES):
                    spots, rows, sums = [], [], []
                    for u in range(first, first + TABLES):
                        spots.append(pl.multiple_of(index_ref[base + u] * 2, 2))
                        spot = pl.multiple_of(2 * (edge * tile + at + u), 2)
                        rows.append(flows[pl.ds(spot, 2), :])
                    for u in range(TABLES):
                        sums.append(tables[u][pl.ds(spots[u], 2), :] + rows[u])
                    for u in range(TABLES):
                        tables[u][pl.ds(spots[u], 2), :] = sums[u]
                return carry

            lax.fori_loop(0, tile // UNROLL, some, 0)

        @pl.when(step == steps - 1)
        def _():
            def summed(start, size):
                value = tables[0][start : start + size, :]
                for table in tables[1:]:
                    value = value + table[start : start + size, :]
                return value

            before_ref[...] = summed(0, 2 * H).astype(jnp.bfloat16)
            own_ref[...] = summed(2 * H, 2 * blocks)
            after_ref[...] = summed(2 * H + 2 * blocks, 2 * H).astype(jnp.bfloat16)

    rows = pl.BlockSpec((tile, D), lambda i, *_: (i, 0))
    return pl.pallas_call(
        body,
        grid_spec=pltpu.PrefetchScalarGridSpec(
            num_scalar_prefetch=1,
            grid=(steps,),
            in_specs=[
                rows, rows, rows,
                pl.BlockSpec((K, 2 * tile, HALF), lambda i, *_: (0, i, 0)),
                whole(mats.shape), whole(bias.shape),
            ],
            out_specs=[
                rows, rows,
                whole((2 * H, HALF)), whole((2 * blocks, HALF)), whole((2 * H, HALF)),
            ],
            scratch_shapes=[
                pltpu.VMEM((2 * tile, HALF), jnp.float32),
                pltpu.VMEM((2 * tile, HALF), jnp.float32),
                pltpu.VMEM((2 * tile * K, HALF), jnp.float32),
            ]
            + [pltpu.VMEM((reach, HALF), jnp.float32)] * TABLES,
        ),
        out_shape=[
            jax.ShapeDtypeStruct((blocks, D), jnp.bfloat16),
            jax.ShapeDtypeStruct((blocks, D), jnp.bfloat16),
            jax.ShapeDtypeStruct((2 * H, HALF), jnp.bfloat16),
            jax.ShapeDtypeStruct((2 * blocks, HALF), jnp.float32),
            jax.ShapeDtypeStruct((2 * H, HALF), jnp.bfloat16),
        ],
        compiler_params=LIMIT,
        name="edges_backward",
    )(index, grad_mesh, mesh, uin, edges, mats, bias)


def round_backward(grad_mesh, own, first, last, grad_uin, dest_low, mats):
    blocks = grad_mesh.shape[0]
    tile = 256

    def body(grad_ref, own_ref, first_ref, last_ref, guin_ref, dest_ref, mats_ref, new_ref, sent_ref, wide):
        wide[...] = (
            own_ref[...] + first_ref[...].astype(jnp.float32) + last_ref[...].astype(jnp.float32)
        )
        one, two = unweave(wide)
        one, two = one.astype(jnp.bfloat16), two.astype(jnp.bfloat16)
        sent_ref[:, :HALF] = one
        sent_ref[:, HALF:] = two
        new_ref[...] = (
            grad_ref[...]
            + inner(guin_ref[...], mats_ref[3], 1, 1)
            + inner(dest_ref[...], mats_ref[1], 1, 1)
            + inner(one, mats_ref[0, :, :HALF], 1, 1)
            + inner(two, mats_ref[0, :, HALF:], 1, 1)
        )

    rows = pl.BlockSpec((tile, D), lambda i: (i, 0))
    woven = pl.BlockSpec((2 * tile, HALF), lambda i: (i, 0))
    return pl.pallas_call(
        body,
        grid=(blocks // tile,),
        in_specs=[rows, woven, woven, woven, rows, rows, whole(mats.shape)],
        out_specs=[rows, rows],
        out_shape=[
            jax.ShapeDtypeStruct((blocks, D), jnp.float32),
            jax.ShapeDtypeStruct((blocks, D), jnp.bfloat16),
        ],
        scratch_shapes=[pltpu.VMEM((2 * tile, HALF), jnp.float32)],
        compiler_params=LIMIT,
        name="round_backward",
    )(grad_mesh, own, first, last, grad_uin, dest_low, mats)


def shards(master, moment1, moment2, inputs, targets, valid, owner, slot, neighbours, partner):
    bands = lax.axis_size("space")
    band = lax.axis_index("space")
    peers = lax.axis_size(ALL)
    place = lax.axis_index(ALL)
    shard = master.shape[0]
    total_size = shard * peers
    height = pieces_of(total_size, peers)[3]
    offset = lax.rem(lax.rem(shard, D) * place, D)
    piece = lax.dynamic_update_slice_in_dim(
        jnp.zeros((height * D,), jnp.bfloat16), master.astype(jnp.bfloat16), offset, 0
    )
    everything = lax.all_gather(piece.reshape(height, D), ALL, axis=0, tiled=True)
    w_in, w_node, w_dec, w_out, w_round, biases = spread_rows(
        everything.reshape(peers, height, D), total_size
    )
    w_out = w_out.reshape(D, CH)
    w_round = w_round.reshape(ROUNDS, 5, D, D)
    b_head = biases[:3]
    b_round = biases[3:].reshape(ROUNDS, 2, D)
    state_in = inputs[0]
    wanted = targets[0].astype(jnp.float32)
    counted = valid[0].astype(jnp.float32)
    points = state_in.shape[1]
    blocks = neighbours.shape[0]
    count = lax.psum(jnp.sum(counted), ALL)
    capacity = max(2, 2 * points // bands)
    target_band = owner[0, :, 0]
    hits = (target_band[:, None] == jnp.arange(bands, dtype=jnp.int32)[None, :]).astype(jnp.int32)
    ranks = jnp.sum(jnp.cumsum(hits, 0) * hits, 1) - 1
    places_out = target_band * capacity + ranks
    enc_in = inner(state_in, w_in, 0, 0) + b_head[0]
    encoded = jax.nn.silu(enc_in).astype(jnp.bfloat16)
    outbox = jnp.zeros((bands * capacity, D), jnp.bfloat16).at[places_out].set(encoded)
    labels = jnp.full((bands * capacity,), -1, jnp.int32).at[places_out].set(slot[0])
    arrived, arrived_ids = (
        lax.all_to_all(
            outbox.reshape(bands, capacity, D), "space", split_axis=0, concat_axis=0, tiled=True
        ),
        lax.all_to_all(
            labels.reshape(bands, capacity), "space", split_axis=0, concat_axis=0, tiled=True
        ),
    )
    chooser = (
        arrived_ids.reshape(-1)[:, None] == jnp.arange(blocks, dtype=jnp.int32)[None, :]
    ).astype(jnp.bfloat16)
    gathered = inner(chooser, arrived.reshape(-1, D), 0, 0).astype(jnp.bfloat16)
    node_in = inner(gathered, w_node, 1, 0) + b_head[1]
    mesh = jax.nn.silu(node_in)
    index = ((neighbours - band * blocks + H) % (blocks * bands)).T.reshape(-1)
    kept = []
    sent = inner(mesh.astype(jnp.bfloat16), w_round[0, 0], 1, 0).astype(jnp.bfloat16)
    sent = sent.reshape(2 * blocks, HALF)
    for layer in range(ROUNDS):
        before, after = halo(sent[2 * (blocks - H) :], sent[: 2 * H])
        edges = gather_rows(
            index,
            before.reshape(H, 2, HALF),
            sent.reshape(blocks, 2, HALF),
            after.reshape(H, 2, HALF),
        ).reshape(K, 2 * blocks, HALF)
        following = w_round[layer + 1, 0] if layer + 1 < ROUNDS else None
        new, uin, agg, *rest = round_forward(mesh, edges, w_round[layer], b_round[layer], following)
        kept.append((mesh, edges, uin, agg))
        mesh = new
        sent = rest[0] if rest else None
    reply = inner(chooser, mesh.astype(jnp.bfloat16), 1, 0).astype(jnp.bfloat16)
    returned = lax.all_to_all(
        reply.reshape(bands, capacity, D), "space", split_axis=0, concat_axis=0, tiled=True
    )
    fetched = returned.reshape(-1, D)[places_out]
    dec_in = inner(fetched, w_dec, 1, 0) + b_head[2]
    decoded = jax.nn.silu(dec_in).astype(jnp.bfloat16)
    err = state_in.astype(jnp.float32) + inner(w_out, decoded, 0, 1) - wanted
    head_err, head_valid = (
        shifted(err[:, :ROWW].astype(jnp.bfloat16), "space", -1).astype(jnp.float32),
        shifted(counted[:, :ROWW].astype(jnp.bfloat16), "space", -1).astype(jnp.float32),
    )
    wide_err = jnp.concatenate([err, head_err], 1)
    wide_valid = jnp.concatenate([counted, head_valid], 1)
    ahead = partner - band * points - jnp.arange(points, dtype=jnp.int32)
    picks = [(ahead == by)[None, :] for by in range(NEAR, ROWW + 1)]
    err_far = err
    valid_far = counted
    for by, pick in zip(range(NEAR, ROWW + 1), picks):
        err_far = jnp.where(pick, wide_err[:, by : by + points], err_far)
        valid_far = jnp.where(pick, wide_valid[:, by : by + points], valid_far)
    gap = err - err_far
    local_total = jnp.sum(counted * err * err) + 0.5 * jnp.sum(counted * valid_far * gap * gap)
    total = lax.psum(local_total, ALL)
    paired = counted * valid_far * gap / count
    grad_err = 2.0 * counted * err / count + paired
    grad_wide = jnp.zeros(wide_err.shape, jnp.float32)
    for by, pick in zip(range(NEAR, ROWW + 1), picks):
        grad_wide = grad_wide - jnp.pad(
            jnp.where(pick, paired, 0.0), ((0, 0), (by, ROWW - by))
        )
    carried = shifted(grad_wide[:, points:].astype(jnp.bfloat16), "space", 1).astype(jnp.float32)
    stays = jnp.where((ahead == 0)[None, :], paired, 0.0)
    grad_pred = (
        grad_err - stays + grad_wide[:, :points] + jnp.pad(carried, ((0, 0), (0, points - ROWW)))
    )
    grad_branch = grad_pred.astype(jnp.bfloat16)
    grad_wout = inner(decoded, grad_branch, 0, 1)
    grad_dec = (inner(grad_branch, w_out, 0, 1) * slope(dec_in)).astype(jnp.bfloat16)
    grad_bdec = jnp.sum(grad_dec.astype(jnp.float32), 0)
    grad_wdec = inner(fetched, grad_dec, 0, 0)
    grad_fetched = inner(grad_dec, w_dec, 1, 1).astype(jnp.bfloat16)
    backbox = jnp.zeros((bands * capacity, D), jnp.bfloat16).at[places_out].set(grad_fetched)
    landed = lax.all_to_all(
        backbox.reshape(bands, capacity, D), "space", split_axis=0, concat_axis=0, tiled=True
    )
    grad_mesh = inner(chooser, landed.reshape(-1, D), 0, 0)
    mats_grads = [None] * (5 * ROUNDS)
    bias_grads = [None] * (2 * ROUNDS)
    for layer in reversed(range(ROUNDS)):
        old, edges, uin, agg = kept[layer]
        mats = w_round[layer]
        grad_uin, dest_low, to_before, own, to_after = edges_backward(
            index, grad_mesh, old, uin, edges, mats, b_round[layer]
        )
        from_before, from_after = halo(to_after, to_before)
        lowered = old.astype(jnp.bfloat16)
        grad_out = grad_mesh.astype(jnp.bfloat16)
        update = silu(uin).astype(jnp.bfloat16)
        grads = [
            None,
            inner(lowered, dest_low, 0, 0),
            inner(agg, grad_uin, 0, 0),
            inner(lowered, grad_uin, 0, 0),
            inner(update, grad_out, 0, 0),
        ]
        bias_grads[2 * layer] = jnp.sum(dest_low.astype(jnp.float32), 0, keepdims=True)
        bias_grads[2 * layer + 1] = jnp.sum(grad_uin.astype(jnp.float32), 0, keepdims=True)
        grad_mesh, sent_low = round_backward(
            grad_mesh, own, from_before, from_after, grad_uin, dest_low, mats
        )
        grads[0] = inner(lowered, sent_low, 0, 0)
        mats_grads[5 * layer : 5 * layer + 5] = grads
    grad_node = (grad_mesh * slope(node_in)).astype(jnp.bfloat16)
    grad_bnode = jnp.sum(grad_node.astype(jnp.float32), 0)
    grad_wnode = inner(gathered, grad_node, 0, 0)
    grad_gathered = inner(grad_node, w_node, 1, 1).astype(jnp.bfloat16)
    sendback = inner(chooser, grad_gathered, 1, 0).astype(jnp.bfloat16)
    homeward = lax.all_to_all(
        sendback.reshape(bands, capacity, D), "space", split_axis=0, concat_axis=0, tiled=True
    )
    grad_encoded = homeward.reshape(-1, D)[places_out].astype(jnp.float32)
    grad_enc = (grad_encoded * slope(enc_in)).astype(jnp.bfloat16)
    grad_bin = jnp.sum(grad_enc.astype(jnp.float32), 0)
    grad_win = inner(state_in, grad_enc, 1, 0)
    parts = [grad_win, grad_wnode, grad_wdec, grad_wout.reshape(CH, D)]
    parts = parts + mats_grads
    parts.append(jnp.concatenate([jnp.stack([grad_bin, grad_bnode, grad_bdec])] + bias_grads, 0))
    packed = collect_rows(parts, total_size, peers)
    summed = lax.psum_scatter(
        packed.reshape(peers * height, D), ALL, scatter_dimension=0, tiled=True
    )
    mine = lax.dynamic_slice_in_dim(summed.reshape(-1), offset, shard)
    norm = jnp.sqrt(lax.psum(jnp.sum(mine * mine), ALL))
    clipped = mine * jnp.minimum(1.0, 0.05 / norm)
    first = 0.9 * moment1 + 0.1 * clipped
    second = 0.999 * moment2 + 0.001 * clipped * clipped
    first_hat = first / (1.0 - 0.9**STEP)
    second_hat = second / (1.0 - 0.999**STEP)
    updated = master - 0.1 * (first_hat / (jnp.sqrt(second_hat) + 1e-08) + 0.1 * master)
    return (
        total.reshape(1),
        count.reshape(1),
        norm.reshape(1),
        updated,
        first,
        second,
        updated.astype(jnp.bfloat16),
        mesh.reshape(1, blocks, D),
        grad_mesh.reshape(1, blocks, D),
        grad_pred.reshape(1, grad_pred.shape[0], points),
    )


def solution(mesh):
    return jax.shard_map(
        shards,
        mesh=mesh,
        in_specs=(
            P(("dp", "space")),
            P(("dp", "space")),
            P(("dp", "space")),
            P("dp", None, "space"),
            P("dp", None, "space"),
            P("dp", None, "space"),
            P("dp", "space", None),
            P("dp", "space"),
            P("space", None),
            P("space"),
        ),
        out_specs=(
            P(),
            P(),
            P(),
            P(("dp", "space")),
            P(("dp", "space")),
            P(("dp", "space")),
            P(("dp", "space")),
            P("dp", "space", None),
            P("dp", "space", None),
            P("dp", None, "space"),
        ),
        check_vma=False,
    )
```

```python
import math

import jax
import jax.numpy as jnp
from jax import lax
from jax.experimental import pallas as pl
from jax.experimental.pallas import tpu as pltpu
from jax.sharding import PartitionSpec as P

D = 256
HALF = 128
CH = 78
ROUNDS = 3
K = 6
ROWW = 360
NEAR = 358
STEP = 10
H = 2048
TABLES = 4
UNROLL = 32
ALL = ("dp", "space")
LIMIT = pltpu.CompilerParams(vmem_limit_bytes=56 * 2**20)


def inner(left, right, left_dim, right_dim):
    return lax.dot_general(
        left, right, (((left_dim,), (right_dim,)), ((), ())), preferred_element_type=jnp.float32
    )


def sigmoid(value):
    return 0.5 * jnp.tanh(0.5 * value) + 0.5


def silu(value):
    return value * sigmoid(value)


def slope(value):
    sigma = sigmoid(value)
    return sigma * (1.0 + value * (1.0 - sigma))


def shifted(shard, axis, by):
    peers = lax.axis_size(axis)
    pairs = [(i, i + by) for i in range(peers) if 0 <= i + by < peers]
    return lax.ppermute(shard, axis, pairs)


def halo(last, initial):
    peers = lax.axis_size("space")
    up = [(i, (i + 1) % peers) for i in range(peers)]
    down = [(j, i) for i, j in up]
    return lax.ppermute(last, "space", up), lax.ppermute(initial, "space", down)


def pieces_of(total, peers):
    share = total // peers
    starts = [share * d // D for d in range(peers)]
    counts = [-(-share * (d + 1) // D) - starts[d] for d in range(peers)]
    shared = [share * d % D != 0 for d in range(peers)]
    height = -(-max(counts) // 16) * 16
    return starts, counts, shared, height


def parts_of():
    return [CH, D, D, CH, ROUNDS * 5 * D, 3 + 2 * ROUNDS]


def swapped(value, axis, bit):
    return lax.ppermute(value, axis, [(i, i ^ bit) for i in range(lax.axis_size(axis))])


def bits_of(axis):
    return [1 << n for n in range(lax.axis_size(axis).bit_length() - 1)]


def summed_everywhere(value):
    for axis in ALL:
        for bit in bits_of(axis):
            value = value + swapped(value, axis, bit)
    return value


def orders():
    bits = bits_of("space")
    return bits, bits[1:2] + bits[:1] + bits[2:]


def gathered_blocks(piece):
    half = piece.shape[0] // 2
    held = []
    for part, order in zip((piece[:half], piece[half:]), orders()):
        names, part = [], part[None]
        for bit in reversed(order):
            part = jnp.concatenate([part, swapped(part, "space", bit)], 0)
            names.insert(0, bit)
        held.append(part)
    return held, [swapped(part, "dp", 1) for part in held]


def spread_rows(gathered, total, peers, place):
    (first, second), (first_far, second_far) = gathered
    starts, counts, shared, height = pieces_of(total, peers)
    half, group = height // 2, first.shape[0]
    rows = -(-total // D)
    sizes = parts_of()
    ranks = []
    for order in orders():
        ranks.append({bit: group >> (n + 1) for n, bit in enumerate(order)})

    def at(rank, relative):
        spot = 0
        for bit, weight in rank.items():
            spot = spot + jnp.where((relative & bit) != 0, weight, 0)
        return spot

    def body(place_ref, *refs):
        sources, outs, buffer = refs[:4], refs[4:-1], refs[-1]
        me = place_ref[0]
        mine = me // group
        for d in range(peers):
            relative = (me ^ d) & (group - 1)
            spots = [at(rank, relative) for rank in ranks]

            def lay(one, two, d=d, spots=spots):
                piece = jnp.concatenate([one[spots[0]], two[spots[1]]], 0).astype(jnp.float32)
                start, count = starts[d], counts[d]
                if shared[d]:
                    buffer[start : start + 1, :] = buffer[start : start + 1, :] + piece[:1]
                    buffer[start + 1 : start + count, :] = piece[1:count]
                else:
                    buffer[start : start + count, :] = piece[:count]

            @pl.when(mine == d // group)
            def _():
                lay(sources[0], sources[1])

            @pl.when(mine != d // group)
            def _():
                lay(sources[2], sources[3])

        start = 0
        for out, size in zip(outs, sizes):
            out[:size, :] = buffer[start : start + size, :].astype(out.dtype)
            if out.shape[0] > size:
                out[size:, :] = jnp.zeros((out.shape[0] - size, D), out.dtype)
            start = start + size

    kinds = [jnp.bfloat16] * 5 + [jnp.float32]
    talls = [HALF] + sizes[1:]
    return pl.pallas_call(
        body,
        grid_spec=pltpu.PrefetchScalarGridSpec(
            num_scalar_prefetch=1,
            grid=(1,),
            in_specs=[whole(first.shape)] * 4,
            out_specs=[whole((tall, D)) for tall in talls],
            scratch_shapes=[pltpu.VMEM((-(-rows // 8) * 8 + 8, D), jnp.float32)],
        ),
        out_shape=[jax.ShapeDtypeStruct((tall, D), kind) for tall, kind in zip(talls, kinds)],
        compiler_params=LIMIT,
        name="spread_rows",
    )(place.reshape(1), first, second, first_far, second_far)


def collect_rows(parts, total, peers, place):
    starts, counts, shared, height = pieces_of(total, peers)
    rows = -(-total // D)
    sizes = [min(part.shape[0], size) for part, size in zip(parts, tall_parts())]
    group = lax.axis_size("space")

    def body(place_ref, *refs):
        sources, keep, send, buffer = refs[:-3], refs[-3], refs[-2], refs[-1]
        start = 0
        for source, size in zip(sources, sizes):
            buffer[start : start + size, :] = source[:size, :]
            start = start + size
        if buffer.shape[0] > start:
            buffer[start:, :] = jnp.zeros((buffer.shape[0] - start, D), jnp.float32)
        me = place_ref[0]
        mine = me // group
        for d in range(peers):
            relative = (me ^ d) & (group - 1)

            @pl.when(mine == d // group)
            def _():
                keep[relative] = buffer[starts[d] : starts[d] + height, :]

            @pl.when(mine != d // group)
            def _():
                send[relative] = buffer[starts[d] : starts[d] + height, :].astype(jnp.bfloat16)

    shape = (group, height, D)
    return pl.pallas_call(
        body,
        grid_spec=pltpu.PrefetchScalarGridSpec(
            num_scalar_prefetch=1,
            grid=(1,),
            in_specs=[whole(part.shape) for part in parts],
            out_specs=[whole(shape), whole(shape)],
            scratch_shapes=[pltpu.VMEM((-(-rows // 8) * 8 + height + 8, D), jnp.float32)],
        ),
        out_shape=[
            jax.ShapeDtypeStruct(shape, jnp.float32),
            jax.ShapeDtypeStruct(shape, jnp.bfloat16),
        ],
        compiler_params=LIMIT,
        name="collect_rows",
    )(place.reshape(1), *parts)


def reduced_piece(keep, send):
    kept = keep + swapped(send, "dp", 1).astype(jnp.float32)
    half = kept.shape[1] // 2
    done = []
    for part, order in zip((kept[:, :half], kept[:, half:]), orders()):
        names = bits_of("space")[::-1]
        part = part.reshape((2,) * len(names) + (half, D))
        for bit in order:
            spot = names.index(bit)
            names.pop(spot)
            stay = lax.index_in_dim(part, 0, spot, keepdims=False)
            leave = lax.index_in_dim(part, 1, spot, keepdims=False)
            part = stay + swapped(leave.astype(jnp.bfloat16), "space", bit).astype(jnp.float32)
        done.append(part)
    return jnp.concatenate(done, 0)


def tall_parts():
    return [CH, D, D, CH] + [D] * (5 * ROUNDS) + [3 + 2 * ROUNDS]


def gather_rows(index, before, own, after):
    edges = index.shape[0]
    chunk = 1024
    spans = [before.shape[0], own.shape[0], after.shape[0]]

    def body(index_ref, before_ref, own_ref, after_ref, out_ref, table, sems):
        step = pl.program_id(0)

        @pl.when(step == 0)
        def _():
            copies = []
            start = 0
            for n, (source, span) in enumerate(zip((before_ref, own_ref, after_ref), spans)):
                copies.append(
                    pltpu.make_async_copy(source, table.at[pl.ds(start, span)], sems.at[n])
                )
                start = start + span
            for copy in copies:
                copy.start()
            for copy in copies:
                copy.wait()

        def some(i, carry):
            at = i * UNROLL
            base = step * chunk + at
            rows = [table[index_ref[base + u]] for u in range(UNROLL)]
            for u in range(UNROLL):
                out_ref[at + u] = rows[u]
            return carry

        lax.fori_loop(0, chunk // UNROLL, some, 0)

    return pl.pallas_call(
        body,
        grid_spec=pltpu.PrefetchScalarGridSpec(
            num_scalar_prefetch=1,
            grid=(edges // chunk,),
            in_specs=[pl.BlockSpec(memory_space=pl.ANY)] * 3,
            out_specs=pl.BlockSpec((chunk, 2, HALF), lambda i, *_: (i, 0, 0)),
            scratch_shapes=[
                pltpu.VMEM((sum(spans), 2, HALF), own.dtype),
                pltpu.SemaphoreType.DMA((3,)),
            ],
        ),
        out_shape=jax.ShapeDtypeStruct((edges, 2, HALF), own.dtype),
        compiler_params=LIMIT,
        name="gather_rows",
    )(index, before, own, after)


def weave(ref, value):
    rows = value.shape[0]
    ref[pl.ds(0, rows, stride=2), :] = value[:, :HALF]
    ref[pl.ds(1, rows, stride=2), :] = value[:, HALF:]


def unweave(ref):
    rows = ref.shape[0] // 2
    return ref[pl.ds(0, rows, stride=2), :], ref[pl.ds(1, rows, stride=2), :]


def whole(shape):
    return pl.BlockSpec(shape, lambda *_: (0,) * len(shape))


def round_forward(mesh, edges, mats, bias, following):
    blocks = mesh.shape[0]
    tile = 256
    more = following is not None

    def body(*refs):
        if more:
            (mesh_ref, edge_ref, mats_ref, bias_ref, next_ref, new_ref, uin_ref, agg_ref, sent_ref, wide) = refs
        else:
            (mesh_ref, edge_ref, mats_ref, bias_ref, new_ref, uin_ref, agg_ref, wide) = refs
        mesh_in = mesh_ref[...]
        lowered = mesh_in.astype(jnp.bfloat16)
        weave(wide, inner(lowered, mats_ref[1], 1, 0) + bias_ref[0:1, :])
        dest = wide[...]
        total = jnp.zeros(dest.shape, jnp.float32)
        for edge in range(K):
            total = total + silu(edge_ref[edge].astype(jnp.float32) + dest)
        wide[...] = total * (1.0 / K)
        first, second = unweave(wide)
        first, second = first.astype(jnp.bfloat16), second.astype(jnp.bfloat16)
        agg_ref[:, :HALF] = first
        agg_ref[:, HALF:] = second
        update_in = (
            inner(first, mats_ref[2, :HALF, :], 1, 0)
            + inner(second, mats_ref[2, HALF:, :], 1, 0)
            + inner(lowered, mats_ref[3], 1, 0)
            + bias_ref[1:2, :]
        )
        uin_ref[...] = update_in
        update = silu(update_in).astype(jnp.bfloat16)
        new = mesh_in + inner(update, mats_ref[4], 1, 0)
        new_ref[...] = new
        if more:
            weave(wide, inner(new.astype(jnp.bfloat16), next_ref[...], 1, 0))
            sent_ref[...] = wide[...].astype(jnp.bfloat16)

    rows = pl.BlockSpec((tile, D), lambda i: (i, 0))
    woven = pl.BlockSpec((2 * tile, HALF), lambda i: (i, 0))
    ins = [rows, pl.BlockSpec((K, 2 * tile, HALF), lambda i: (0, i, 0)), whole(mats.shape), whole(bias.shape)]
    outs = [rows, rows, rows]
    shapes = [
        jax.ShapeDtypeStruct((blocks, D), jnp.float32),
        jax.ShapeDtypeStruct((blocks, D), jnp.float32),
        jax.ShapeDtypeStruct((blocks, D), jnp.bfloat16),
    ]
    args = [mesh, edges, mats, bias]
    if more:
        ins.append(whole(following.shape))
        outs.append(woven)
        shapes.append(jax.ShapeDtypeStruct((2 * blocks, HALF), jnp.bfloat16))
        args.append(following)
    return pl.pallas_call(
        body,
        grid=(blocks // tile,),
        in_specs=ins,
        out_specs=outs,
        out_shape=shapes,
        scratch_shapes=[pltpu.VMEM((2 * tile, HALF), jnp.float32)],
        compiler_params=LIMIT,
        name="round_forward",
    )(*args)


def edges_backward(index, grad_mesh, mesh, uin, edges, mats, bias):
    blocks = mesh.shape[0]
    tile = 256
    steps = blocks // tile
    reach = 2 * (blocks + 2 * H)

    def body(
        index_ref, grad_ref, mesh_ref, uin_ref, edge_ref, mats_ref, bias_ref,
        guin_ref, low_ref, before_ref, own_ref, after_ref, wide, wider, flows, *tables,
    ):
        step = pl.program_id(0)

        @pl.when(step == 0)
        def _():
            for table in tables:
                table[...] = jnp.zeros(table.shape, jnp.float32)

        grad_out = grad_ref[...].astype(jnp.bfloat16)
        grad_update = inner(grad_out, mats_ref[4], 1, 1)
        grad_uin = (grad_update * slope(uin_ref[...])).astype(jnp.bfloat16)
        guin_ref[...] = grad_uin
        weave(wide, inner(grad_uin, mats_ref[2], 1, 1) * (1.0 / K))
        lowered = mesh_ref[...].astype(jnp.bfloat16)
        weave(wider, inner(lowered, mats_ref[1], 1, 0) + bias_ref[0:1, :])
        grad_agg = wide[...]
        dest = wider[...]
        grad_dest = jnp.zeros(dest.shape, jnp.float32)
        for edge in range(K):
            flow = grad_agg * slope(edge_ref[edge].astype(jnp.float32) + dest)
            grad_dest = grad_dest + flow
            flows[edge * 2 * tile : (edge + 1) * 2 * tile, :] = flow
        wide[...] = grad_dest
        first, second = unweave(wide)
        low_ref[:, :HALF] = first.astype(jnp.bfloat16)
        low_ref[:, HALF:] = second.astype(jnp.bfloat16)
        for edge in range(K):

            def some(i, carry):
                at = i * UNROLL
                base = edge * blocks + step * tile + at
                for first in range(0, UNROLL, TABLES):
                    spots, rows, sums = [], [], []
                    for u in range(first, first + TABLES):
                        spots.append(pl.multiple_of(index_ref[base + u] * 2, 2))
                        spot = pl.multiple_of(2 * (edge * tile + at + u), 2)
                        rows.append(flows[pl.ds(spot, 2), :])
                    for u in range(TABLES):
                        sums.append(tables[u][pl.ds(spots[u], 2), :] + rows[u])
                    for u in range(TABLES):
                        tables[u][pl.ds(spots[u], 2), :] = sums[u]
                return carry

            lax.fori_loop(0, tile // UNROLL, some, 0)

        @pl.when(step == steps - 1)
        def _():
            def summed(start, size):
                value = tables[0][start : start + size, :]
                for table in tables[1:]:
                    value = value + table[start : start + size, :]
                return value

            before_ref[...] = summed(0, 2 * H).astype(jnp.bfloat16)
            own_ref[...] = summed(2 * H, 2 * blocks)
            after_ref[...] = summed(2 * H + 2 * blocks, 2 * H).astype(jnp.bfloat16)

    rows = pl.BlockSpec((tile, D), lambda i, *_: (i, 0))
    return pl.pallas_call(
        body,
        grid_spec=pltpu.PrefetchScalarGridSpec(
            num_scalar_prefetch=1,
            grid=(steps,),
            in_specs=[
                rows, rows, rows,
                pl.BlockSpec((K, 2 * tile, HALF), lambda i, *_: (0, i, 0)),
                whole(mats.shape), whole(bias.shape),
            ],
            out_specs=[
                rows, rows,
                whole((2 * H, HALF)), whole((2 * blocks, HALF)), whole((2 * H, HALF)),
            ],
            scratch_shapes=[
                pltpu.VMEM((2 * tile, HALF), jnp.float32),
                pltpu.VMEM((2 * tile, HALF), jnp.float32),
                pltpu.VMEM((2 * tile * K, HALF), jnp.float32),
            ]
            + [pltpu.VMEM((reach, HALF), jnp.float32)] * TABLES,
        ),
        out_shape=[
            jax.ShapeDtypeStruct((blocks, D), jnp.bfloat16),
            jax.ShapeDtypeStruct((blocks, D), jnp.bfloat16),
            jax.ShapeDtypeStruct((2 * H, HALF), jnp.bfloat16),
            jax.ShapeDtypeStruct((2 * blocks, HALF), jnp.float32),
            jax.ShapeDtypeStruct((2 * H, HALF), jnp.bfloat16),
        ],
        compiler_params=LIMIT,
        name="edges_backward",
    )(index, grad_mesh, mesh, uin, edges, mats, bias)


def round_backward(grad_mesh, own, first, last, grad_uin, dest_low, mats):
    blocks = grad_mesh.shape[0]
    tile = 256

    def body(grad_ref, own_ref, first_ref, last_ref, guin_ref, dest_ref, mats_ref, new_ref, sent_ref, wide):
        wide[...] = (
            own_ref[...] + first_ref[...].astype(jnp.float32) + last_ref[...].astype(jnp.float32)
        )
        one, two = unweave(wide)
        one, two = one.astype(jnp.bfloat16), two.astype(jnp.bfloat16)
        sent_ref[:, :HALF] = one
        sent_ref[:, HALF:] = two
        new_ref[...] = (
            grad_ref[...]
            + inner(guin_ref[...], mats_ref[3], 1, 1)
            + inner(dest_ref[...], mats_ref[1], 1, 1)
            + inner(one, mats_ref[0, :, :HALF], 1, 1)
            + inner(two, mats_ref[0, :, HALF:], 1, 1)
        )

    rows = pl.BlockSpec((tile, D), lambda i: (i, 0))
    woven = pl.BlockSpec((2 * tile, HALF), lambda i: (i, 0))
    return pl.pallas_call(
        body,
        grid=(blocks // tile,),
        in_specs=[rows, woven, woven, woven, rows, rows, whole(mats.shape)],
        out_specs=[rows, rows],
        out_shape=[
            jax.ShapeDtypeStruct((blocks, D), jnp.float32),
            jax.ShapeDtypeStruct((blocks, D), jnp.bfloat16),
        ],
        scratch_shapes=[pltpu.VMEM((2 * tile, HALF), jnp.float32)],
        compiler_params=LIMIT,
        name="round_backward",
    )(grad_mesh, own, first, last, grad_uin, dest_low, mats)


def shards(master, moment1, moment2, inputs, targets, valid, owner, slot, neighbours, partner):
    bands = lax.axis_size("space")
    band = lax.axis_index("space")
    peers = lax.axis_size(ALL)
    place = lax.axis_index(ALL)
    shard = master.shape[0]
    total_size = shard * peers
    height = pieces_of(total_size, peers)[3]
    offset = lax.rem(lax.rem(shard, D) * place, D)
    piece = lax.dynamic_update_slice_in_dim(
        jnp.zeros((height * D,), jnp.bfloat16), master.astype(jnp.bfloat16), offset, 0
    )
    state_in = inputs[0]
    counted = valid[0].astype(jnp.float32)
    points = state_in.shape[1]
    blocks = neighbours.shape[0]
    assert blocks == H
    capacity = max(2, 2 * points // bands)
    target_band = owner[0, :, 0]
    hits = (target_band[:, None] == jnp.arange(bands, dtype=jnp.int32)[None, :]).astype(jnp.int32)
    ranks = jnp.sum(jnp.cumsum(hits, 0) * hits, 1) - 1
    places_out = target_band * capacity + ranks
    poster = (
        jnp.arange(bands * capacity, dtype=jnp.int32)[:, None] == places_out[None, :]
    ).astype(jnp.bfloat16)
    spots = slot[0][None, :]
    columns = jnp.concatenate(
        [
            state_in,
            (spots // 64).astype(jnp.bfloat16),
            (spots % 64).astype(jnp.bfloat16),
            jnp.ones((1, points), jnp.bfloat16),
            jnp.zeros((HALF - CH - 3, points), jnp.bfloat16),
        ],
        0,
    )

    def exchanged(rows):
        return lax.all_to_all(
            rows.reshape(bands, capacity, HALF), "space", split_axis=0, concat_axis=0, tiled=True
        ).reshape(bands * capacity, HALF)

    arrived = exchanged(inner(poster, columns, 1, 1).astype(jnp.bfloat16))
    w_in, w_node, w_dec, w_out, w_round, biases = spread_rows(
        gathered_blocks(piece.reshape(height, D)), total_size, peers, place
    )
    w_out = jnp.pad(w_out.reshape(D, CH), ((0, 0), (0, HALF - CH)))
    w_round = w_round.reshape(ROUNDS, 5, D, D)
    b_head = biases[:3]
    b_round = biases[3:].reshape(ROUNDS, 2, D)
    count = summed_everywhere(jnp.full((8, HALF), jnp.sum(counted)))[0, 0]
    ids = arrived[:, CH : CH + 3].astype(jnp.int32)
    ids = jnp.where(ids[:, 2:3] > 0, ids[:, 0:1] * 64 + ids[:, 1:2], -1)
    chooser = (ids == jnp.arange(blocks, dtype=jnp.int32)[None, :]).astype(jnp.bfloat16)
    enc_in = inner(arrived, w_in, 1, 0) + b_head[0]
    encoded = silu(enc_in).astype(jnp.bfloat16)
    gathered = inner(chooser, encoded, 0, 0).astype(jnp.bfloat16)
    node_in = inner(gathered, w_node, 1, 0) + b_head[1]
    mesh = silu(node_in)
    index = ((neighbours - band * blocks + H) % (blocks * bands)).T.reshape(-1)
    kept = []
    sent = inner(mesh.astype(jnp.bfloat16), w_round[0, 0], 1, 0).astype(jnp.bfloat16)
    sent = sent.reshape(2 * blocks, HALF)
    for layer in range(ROUNDS):
        before, after = halo(sent[2 * (blocks - H) :], sent[: 2 * H])
        edges = gather_rows(
            index,
            before.reshape(H, 2, HALF),
            sent.reshape(blocks, 2, HALF),
            after.reshape(H, 2, HALF),
        ).reshape(K, 2 * blocks, HALF)
        following = w_round[layer + 1, 0] if layer + 1 < ROUNDS else None
        new, uin, agg, *rest = round_forward(mesh, edges, w_round[layer], b_round[layer], following)
        kept.append((mesh, edges, uin, agg))
        mesh = new
        sent = rest[0] if rest else None
    fetched = inner(chooser, mesh.astype(jnp.bfloat16), 1, 0).astype(jnp.bfloat16)
    dec_in = inner(fetched, w_dec, 1, 0) + b_head[2]
    decoded = silu(dec_in).astype(jnp.bfloat16)
    returned = exchanged(inner(decoded, w_out, 1, 0).astype(jnp.bfloat16))
    branch = inner(returned, poster, 0, 0)[:CH]
    err = state_in.astype(jnp.float32) + branch - targets[0].astype(jnp.float32)
    head_err, head_valid = (
        shifted(err[:, :ROWW].astype(jnp.bfloat16), "space", -1).astype(jnp.float32),
        shifted(counted[:, :ROWW].astype(jnp.bfloat16), "space", -1).astype(jnp.float32),
    )
    wide_err = jnp.concatenate([err, head_err], 1)
    wide_valid = jnp.concatenate([counted, head_valid], 1)
    ahead = partner - band * points - jnp.arange(points, dtype=jnp.int32)
    picks = [(ahead == by)[None, :] for by in range(NEAR, ROWW + 1)]
    err_far = err
    valid_far = counted
    for by, pick in zip(range(NEAR, ROWW + 1), picks):
        err_far = jnp.where(pick, wide_err[:, by : by + points], err_far)
        valid_far = jnp.where(pick, wide_valid[:, by : by + points], valid_far)
    gap = err - err_far
    local_total = jnp.sum(counted * err * err) + 0.5 * jnp.sum(counted * valid_far * gap * gap)
    paired = counted * valid_far * gap / count
    grad_err = 2.0 * counted * err / count + paired
    grad_wide = jnp.zeros(wide_err.shape, jnp.float32)
    for by, pick in zip(range(NEAR, ROWW + 1), picks):
        grad_wide = grad_wide - jnp.pad(
            jnp.where(pick, paired, 0.0), ((0, 0), (by, ROWW - by))
        )
    carried = shifted(grad_wide[:, points:].astype(jnp.bfloat16), "space", 1).astype(jnp.float32)
    stays = jnp.where((ahead == 0)[None, :], paired, 0.0)
    grad_pred = (
        grad_err - stays + grad_wide[:, :points] + jnp.pad(carried, ((0, 0), (0, points - ROWW)))
    )
    grad_rows = jnp.pad(grad_pred.astype(jnp.bfloat16), ((0, HALF - CH), (0, 0)))
    landed = exchanged(inner(poster, grad_rows, 1, 1).astype(jnp.bfloat16))
    grad_wout = inner(decoded, landed, 0, 0)[:, :CH]
    grad_dec = (inner(landed, w_out, 1, 1) * slope(dec_in)).astype(jnp.bfloat16)
    grad_bdec = jnp.sum(grad_dec.astype(jnp.float32), 0)
    grad_wdec = inner(fetched, grad_dec, 0, 0)
    grad_fetched = inner(grad_dec, w_dec, 1, 1).astype(jnp.bfloat16)
    grad_mesh = inner(chooser, grad_fetched, 0, 0)
    mats_grads = [None] * (5 * ROUNDS)
    bias_grads = [None] * (2 * ROUNDS)
    for layer in reversed(range(ROUNDS)):
        old, edges, uin, agg = kept[layer]
        mats = w_round[layer]
        grad_uin, dest_low, to_before, own, to_after = edges_backward(
            index, grad_mesh, old, uin, edges, mats, b_round[layer]
        )
        from_before, from_after = halo(to_after, to_before)
        lowered = old.astype(jnp.bfloat16)
        grad_out = grad_mesh.astype(jnp.bfloat16)
        update = silu(uin).astype(jnp.bfloat16)
        grads = [
            None,
            inner(lowered, dest_low, 0, 0),
            inner(agg, grad_uin, 0, 0),
            inner(lowered, grad_uin, 0, 0),
            inner(update, grad_out, 0, 0),
        ]
        bias_grads[2 * layer] = jnp.sum(dest_low.astype(jnp.float32), 0, keepdims=True)
        bias_grads[2 * layer + 1] = jnp.sum(grad_uin.astype(jnp.float32), 0, keepdims=True)
        grad_mesh, sent_low = round_backward(
            grad_mesh, own, from_before, from_after, grad_uin, dest_low, mats
        )
        grads[0] = inner(lowered, sent_low, 0, 0)
        mats_grads[5 * layer : 5 * layer + 5] = grads
    grad_node = (grad_mesh * slope(node_in)).astype(jnp.bfloat16)
    grad_bnode = jnp.sum(grad_node.astype(jnp.float32), 0)
    grad_wnode = inner(gathered, grad_node, 0, 0)
    grad_gathered = inner(grad_node, w_node, 1, 1).astype(jnp.bfloat16)
    grad_encoded = inner(chooser, grad_gathered, 1, 0)
    grad_enc = (grad_encoded * slope(enc_in)).astype(jnp.bfloat16)
    grad_bin = jnp.sum(grad_enc.astype(jnp.float32), 0)
    grad_win = inner(arrived, grad_enc, 0, 0)
    parts = [grad_win, grad_wnode, grad_wdec, grad_wout.reshape(CH, D)]
    parts = parts + mats_grads
    parts.append(jnp.concatenate([jnp.stack([grad_bin, grad_bnode, grad_bdec])] + bias_grads, 0))
    mine = reduced_piece(*collect_rows(parts, total_size, peers, place))
    mine = lax.dynamic_slice_in_dim(mine.reshape(-1), offset, shard)
    lane = lax.broadcasted_iota(jnp.int32, (8, HALF), 1)
    sums = summed_everywhere(jnp.where(lane == 0, local_total, jnp.sum(mine * mine)))
    total, norm = sums[0, 0], jnp.sqrt(sums[0, 1])
    clipped = mine * jnp.minimum(1.0, 0.05 / norm)
    first = 0.9 * moment1 + 0.1 * clipped
    second = 0.999 * moment2 + 0.001 * clipped * clipped
    first_hat = first / (1.0 - 0.9**STEP)
    second_hat = second / (1.0 - 0.999**STEP)
    updated = master - 0.1 * (first_hat / (jnp.sqrt(second_hat) + 1e-08) + 0.1 * master)
    return (
        total.reshape(1),
        count.reshape(1),
        norm.reshape(1),
        updated,
        first,
        second,
        updated.astype(jnp.bfloat16),
        mesh.reshape(1, blocks, D),
        grad_mesh.reshape(1, blocks, D),
        grad_pred.reshape(1, grad_pred.shape[0], points),
    )


def solution(mesh):
    return jax.shard_map(
        shards,
        mesh=mesh,
        in_specs=(
            P(("dp", "space")),
            P(("dp", "space")),
            P(("dp", "space")),
            P("dp", None, "space"),
            P("dp", None, "space"),
            P("dp", None, "space"),
            P("dp", "space", None),
            P("dp", "space"),
            P("space", None),
            P("space"),
        ),
        out_specs=(
            P(),
            P(),
            P(),
            P(("dp", "space")),
            P(("dp", "space")),
            P(("dp", "space")),
            P(("dp", "space")),
            P("dp", "space", None),
            P("dp", "space", None),
            P("dp", None, "space"),
        ),
        check_vma=False,
    )
```

```python
import functools

import jax
import jax.numpy as jnp
from jax import lax
from jax.experimental import pallas as pl
from jax.experimental.pallas import tpu as pltpu
from jax.sharding import PartitionSpec as P

D = 256
HALF = 128
CH = 78
ROUNDS = 3
K = 6
ROWW = 360
NEAR = 358
STEP = 10
H = 2048
TABLES = 4
UNROLL = 32
ALL = ("dp", "space")
LIMIT = pltpu.CompilerParams(vmem_limit_bytes=56 * 2**20)


def inner(left, right, left_dim, right_dim):
    return lax.dot_general(
        left, right, (((left_dim,), (right_dim,)), ((), ())), preferred_element_type=jnp.float32
    )


def sigmoid(value):
    return 0.5 * jnp.tanh(0.5 * value) + 0.5


def silu(value):
    return value * sigmoid(value)


def slope(value):
    sigma = sigmoid(value)
    return sigma * (1.0 + value * (1.0 - sigma))


def shifted(shard, axis, by):
    peers = lax.axis_size(axis)
    pairs = [(i, i + by) for i in range(peers) if 0 <= i + by < peers]
    return lax.ppermute(shard, axis, pairs)


def walk_of(mesh):
    count = mesh.shape["space"]
    chips = [getattr(device, "coords", None) for device in mesh.devices[0].reshape(-1)]
    if any(chip is None for chip in chips) or len(set(map(tuple, chips))) != count:
        return list(range(count))
    at = {tuple(chip): n for n, chip in enumerate(chips)}
    xs, ys, zs = (sorted({chip[n] for chip in at}) for n in range(3))
    if len(xs) * len(ys) * len(zs) != count:
        return list(range(count))
    if (len(xs), len(ys), len(zs)) == (2, 2, 4):
        corners = [(0, 0), (1, 0), (0, 1), (1, 1)]
        planes = [(0, 1, 3, 2), (2, 0, 1, 3), (3, 1, 0, 2), (2, 3, 1, 0)]
        steps = [(*corners[n], z) for z, plane in enumerate(planes) for n in plane]
        return [at[(xs[x], ys[y], zs[z])] for x, y, z in steps]
    walk, plane = [], []
    for n, y in enumerate(ys):
        plane = plane + [(x, y) for x in (xs if n % 2 == 0 else xs[::-1])]
    for n, z in enumerate(zs):
        walk = walk + [at[(x, y, z)] for x, y in (plane if n % 2 == 0 else plane[::-1])]
    return walk


def halo(walk, last, initial):
    up = list(zip(walk, walk[1:] + walk[:1]))
    down = [(j, i) for i, j in up]
    return lax.ppermute(last, "space", up), lax.ppermute(initial, "space", down)


def pieces_of(total, peers):
    share = total // peers
    starts = [share * d // D for d in range(peers)]
    counts = [-(-share * (d + 1) // D) - starts[d] for d in range(peers)]
    shared = [share * d % D != 0 for d in range(peers)]
    height = -(-max(counts) // 16) * 16
    return starts, counts, shared, height


def parts_of():
    return [CH, D, D, CH, ROUNDS * 5 * D, 3 + 2 * ROUNDS]


def swapped(value, axis, bit):
    return lax.ppermute(value, axis, [(i, i ^ bit) for i in range(lax.axis_size(axis))])


def bits_of(axis):
    return [1 << n for n in range(lax.axis_size(axis).bit_length() - 1)]


def summed_everywhere(value):
    for axis in ALL:
        for bit in bits_of(axis):
            value = value + swapped(value, axis, bit)
    return value


def orders():
    bits = bits_of("space")
    return bits, bits[1:2] + bits[:1] + bits[2:]


def gathered_blocks(piece):
    half = piece.shape[0] // 2
    held = []
    for part, order in zip((piece[:half], piece[half:]), orders()):
        names, part = [], part[None]
        for bit in reversed(order):
            part = jnp.concatenate([part, swapped(part, "space", bit)], 0)
            names.insert(0, bit)
        held.append(part)
    return held, [swapped(part, "dp", 1) for part in held]


def spread_rows(gathered, total, peers, place):
    (first, second), (first_far, second_far) = gathered
    starts, counts, shared, height = pieces_of(total, peers)
    half, group = height // 2, first.shape[0]
    rows = -(-total // D)
    sizes = parts_of()
    ranks = []
    for order in orders():
        ranks.append({bit: group >> (n + 1) for n, bit in enumerate(order)})

    def at(rank, relative):
        spot = 0
        for bit, weight in rank.items():
            spot = spot + jnp.where((relative & bit) != 0, weight, 0)
        return spot

    def body(place_ref, *refs):
        sources, outs, buffer = refs[:4], refs[4:-1], refs[-1]
        me = place_ref[0]
        mine = me // group
        for d in range(peers):
            relative = (me ^ d) & (group - 1)
            spots = [at(rank, relative) for rank in ranks]

            def lay(one, two, d=d, spots=spots):
                piece = jnp.concatenate([one[spots[0]], two[spots[1]]], 0).astype(jnp.float32)
                start, count = starts[d], counts[d]
                if shared[d]:
                    buffer[start : start + 1, :] = buffer[start : start + 1, :] + piece[:1]
                    buffer[start + 1 : start + count, :] = piece[1:count]
                else:
                    buffer[start : start + count, :] = piece[:count]

            @pl.when(mine == d // group)
            def _():
                lay(sources[0], sources[1])

            @pl.when(mine != d // group)
            def _():
                lay(sources[2], sources[3])

        start = 0
        for out, size in zip(outs, sizes):
            out[:size, :] = buffer[start : start + size, :].astype(out.dtype)
            if out.shape[0] > size:
                out[size:, :] = jnp.zeros((out.shape[0] - size, D), out.dtype)
            start = start + size

    kinds = [jnp.bfloat16] * 5 + [jnp.float32]
    talls = [HALF] + sizes[1:]
    return pl.pallas_call(
        body,
        grid_spec=pltpu.PrefetchScalarGridSpec(
            num_scalar_prefetch=1,
            grid=(1,),
            in_specs=[whole(first.shape)] * 4,
            out_specs=[whole((tall, D)) for tall in talls],
            scratch_shapes=[pltpu.VMEM((-(-rows // 8) * 8 + 8, D), jnp.float32)],
        ),
        out_shape=[jax.ShapeDtypeStruct((tall, D), kind) for tall, kind in zip(talls, kinds)],
        compiler_params=LIMIT,
        name="spread_rows",
    )(place.reshape(1), first, second, first_far, second_far)


def collect_rows(parts, total, peers, place):
    starts, counts, shared, height = pieces_of(total, peers)
    rows = -(-total // D)
    sizes = [min(part.shape[0], size) for part, size in zip(parts, tall_parts())]
    group = lax.axis_size("space")

    def body(place_ref, *refs):
        sources, keep, send, buffer = refs[:-3], refs[-3], refs[-2], refs[-1]
        start = 0
        for source, size in zip(sources, sizes):
            buffer[start : start + size, :] = source[:size, :]
            start = start + size
        if buffer.shape[0] > start:
            buffer[start:, :] = jnp.zeros((buffer.shape[0] - start, D), jnp.float32)
        me = place_ref[0]
        mine = me // group
        for d in range(peers):
            relative = (me ^ d) & (group - 1)

            @pl.when(mine == d // group)
            def _():
                keep[relative] = buffer[starts[d] : starts[d] + height, :]

            @pl.when(mine != d // group)
            def _():
                send[relative] = buffer[starts[d] : starts[d] + height, :].astype(jnp.bfloat16)

    shape = (group, height, D)
    return pl.pallas_call(
        body,
        grid_spec=pltpu.PrefetchScalarGridSpec(
            num_scalar_prefetch=1,
            grid=(1,),
            in_specs=[whole(part.shape) for part in parts],
            out_specs=[whole(shape), whole(shape)],
            scratch_shapes=[pltpu.VMEM((-(-rows // 8) * 8 + height + 8, D), jnp.float32)],
        ),
        out_shape=[
            jax.ShapeDtypeStruct(shape, jnp.float32),
            jax.ShapeDtypeStruct(shape, jnp.bfloat16),
        ],
        compiler_params=LIMIT,
        name="collect_rows",
    )(place.reshape(1), *parts)


def reduced_piece(keep, send):
    kept = keep + swapped(send, "dp", 1).astype(jnp.float32)
    half = kept.shape[1] // 2
    done = []
    for part, order in zip((kept[:, :half], kept[:, half:]), orders()):
        names = bits_of("space")[::-1]
        part = part.reshape((2,) * len(names) + (half, D))
        for bit in order:
            spot = names.index(bit)
            names.pop(spot)
            stay = lax.index_in_dim(part, 0, spot, keepdims=False)
            leave = lax.index_in_dim(part, 1, spot, keepdims=False)
            part = stay + swapped(leave.astype(jnp.bfloat16), "space", bit).astype(jnp.float32)
        done.append(part)
    return jnp.concatenate(done, 0)


def tall_parts():
    return [CH, D, D, CH] + [D] * (5 * ROUNDS) + [3 + 2 * ROUNDS]


def gather_rows(index, before, own, after):
    edges = index.shape[0]
    chunk = 1024
    spans = [before.shape[0], own.shape[0], after.shape[0]]

    def body(index_ref, before_ref, own_ref, after_ref, out_ref, table, sems):
        step = pl.program_id(0)

        @pl.when(step == 0)
        def _():
            copies = []
            start = 0
            for n, (source, span) in enumerate(zip((before_ref, own_ref, after_ref), spans)):
                copies.append(
                    pltpu.make_async_copy(source, table.at[pl.ds(start, span)], sems.at[n])
                )
                start = start + span
            for copy in copies:
                copy.start()
            for copy in copies:
                copy.wait()

        def some(i, carry):
            at = i * UNROLL
            base = step * chunk + at
            rows = [table[index_ref[base + u]] for u in range(UNROLL)]
            for u in range(UNROLL):
                out_ref[at + u] = rows[u]
            return carry

        lax.fori_loop(0, chunk // UNROLL, some, 0)

    return pl.pallas_call(
        body,
        grid_spec=pltpu.PrefetchScalarGridSpec(
            num_scalar_prefetch=1,
            grid=(edges // chunk,),
            in_specs=[pl.BlockSpec(memory_space=pl.ANY)] * 3,
            out_specs=pl.BlockSpec((chunk, 2, HALF), lambda i, *_: (i, 0, 0)),
            scratch_shapes=[
                pltpu.VMEM((sum(spans), 2, HALF), own.dtype),
                pltpu.SemaphoreType.DMA((3,)),
            ],
        ),
        out_shape=jax.ShapeDtypeStruct((edges, 2, HALF), own.dtype),
        compiler_params=LIMIT,
        name="gather_rows",
    )(index, before, own, after)


def weave(ref, value):
    rows = value.shape[0]
    ref[pl.ds(0, rows, stride=2), :] = value[:, :HALF]
    ref[pl.ds(1, rows, stride=2), :] = value[:, HALF:]


def unweave(ref):
    rows = ref.shape[0] // 2
    return ref[pl.ds(0, rows, stride=2), :], ref[pl.ds(1, rows, stride=2), :]


def whole(shape):
    return pl.BlockSpec(shape, lambda *_: (0,) * len(shape))


def round_forward(mesh, edges, mats, bias, following):
    blocks = mesh.shape[0]
    tile = 256
    more = following is not None

    def body(*refs):
        if more:
            (mesh_ref, edge_ref, mats_ref, bias_ref, next_ref, new_ref, uin_ref, agg_ref, sent_ref, wide) = refs
        else:
            (mesh_ref, edge_ref, mats_ref, bias_ref, new_ref, uin_ref, agg_ref, wide) = refs
        mesh_in = mesh_ref[...]
        lowered = mesh_in.astype(jnp.bfloat16)
        weave(wide, inner(lowered, mats_ref[1], 1, 0) + bias_ref[0:1, :])
        dest = wide[...]
        total = jnp.zeros(dest.shape, jnp.float32)
        for edge in range(K):
            total = total + silu(edge_ref[edge].astype(jnp.float32) + dest)
        wide[...] = total * (1.0 / K)
        first, second = unweave(wide)
        first, second = first.astype(jnp.bfloat16), second.astype(jnp.bfloat16)
        agg_ref[:, :HALF] = first
        agg_ref[:, HALF:] = second
        update_in = (
            inner(first, mats_ref[2, :HALF, :], 1, 0)
            + inner(second, mats_ref[2, HALF:, :], 1, 0)
            + inner(lowered, mats_ref[3], 1, 0)
            + bias_ref[1:2, :]
        )
        uin_ref[...] = update_in
        update = silu(update_in).astype(jnp.bfloat16)
        new = mesh_in + inner(update, mats_ref[4], 1, 0)
        new_ref[...] = new
        if more:
            weave(wide, inner(new.astype(jnp.bfloat16), next_ref[...], 1, 0))
            sent_ref[...] = wide[...].astype(jnp.bfloat16)

    rows = pl.BlockSpec((tile, D), lambda i: (i, 0))
    woven = pl.BlockSpec((2 * tile, HALF), lambda i: (i, 0))
    ins = [rows, pl.BlockSpec((K, 2 * tile, HALF), lambda i: (0, i, 0)), whole(mats.shape), whole(bias.shape)]
    outs = [rows, rows, rows]
    shapes = [
        jax.ShapeDtypeStruct((blocks, D), jnp.float32),
        jax.ShapeDtypeStruct((blocks, D), jnp.float32),
        jax.ShapeDtypeStruct((blocks, D), jnp.bfloat16),
    ]
    args = [mesh, edges, mats, bias]
    if more:
        ins.append(whole(following.shape))
        outs.append(woven)
        shapes.append(jax.ShapeDtypeStruct((2 * blocks, HALF), jnp.bfloat16))
        args.append(following)
    return pl.pallas_call(
        body,
        grid=(blocks // tile,),
        in_specs=ins,
        out_specs=outs,
        out_shape=shapes,
        scratch_shapes=[pltpu.VMEM((2 * tile, HALF), jnp.float32)],
        compiler_params=LIMIT,
        name="round_forward",
    )(*args)


def edges_backward(index, grad_mesh, mesh, uin, edges, mats, bias):
    blocks = mesh.shape[0]
    tile = 256
    steps = blocks // tile
    reach = 2 * (blocks + 2 * H)

    def body(
        index_ref, grad_ref, mesh_ref, uin_ref, edge_ref, mats_ref, bias_ref,
        guin_ref, low_ref, before_ref, own_ref, after_ref, wide, wider, flows, *tables,
    ):
        step = pl.program_id(0)

        @pl.when(step == 0)
        def _():
            for table in tables:
                table[...] = jnp.zeros(table.shape, jnp.float32)

        grad_out = grad_ref[...].astype(jnp.bfloat16)
        grad_update = inner(grad_out, mats_ref[4], 1, 1)
        grad_uin = (grad_update * slope(uin_ref[...])).astype(jnp.bfloat16)
        guin_ref[...] = grad_uin
        weave(wide, inner(grad_uin, mats_ref[2], 1, 1) * (1.0 / K))
        lowered = mesh_ref[...].astype(jnp.bfloat16)
        weave(wider, inner(lowered, mats_ref[1], 1, 0) + bias_ref[0:1, :])
        grad_agg = wide[...]
        dest = wider[...]
        grad_dest = jnp.zeros(dest.shape, jnp.float32)
        for edge in range(K):
            flow = grad_agg * slope(edge_ref[edge].astype(jnp.float32) + dest)
            grad_dest = grad_dest + flow
            flows[edge * 2 * tile : (edge + 1) * 2 * tile, :] = flow
        wide[...] = grad_dest
        first, second = unweave(wide)
        low_ref[:, :HALF] = first.astype(jnp.bfloat16)
        low_ref[:, HALF:] = second.astype(jnp.bfloat16)
        for edge in range(K):

            def some(i, carry):
                at = i * UNROLL
                base = edge * blocks + step * tile + at
                for first in range(0, UNROLL, TABLES):
                    spots, rows, sums = [], [], []
                    for u in range(first, first + TABLES):
                        spots.append(pl.multiple_of(index_ref[base + u] * 2, 2))
                        spot = pl.multiple_of(2 * (edge * tile + at + u), 2)
                        rows.append(flows[pl.ds(spot, 2), :])
                    for u in range(TABLES):
                        sums.append(tables[u][pl.ds(spots[u], 2), :] + rows[u])
                    for u in range(TABLES):
                        tables[u][pl.ds(spots[u], 2), :] = sums[u]
                return carry

            lax.fori_loop(0, tile // UNROLL, some, 0)

        @pl.when(step == steps - 1)
        def _():
            def summed(start, size):
                value = tables[0][start : start + size, :]
                for table in tables[1:]:
                    value = value + table[start : start + size, :]
                return value

            before_ref[...] = summed(0, 2 * H).astype(jnp.bfloat16)
            own_ref[...] = summed(2 * H, 2 * blocks)
            after_ref[...] = summed(2 * H + 2 * blocks, 2 * H).astype(jnp.bfloat16)

    rows = pl.BlockSpec((tile, D), lambda i, *_: (i, 0))
    return pl.pallas_call(
        body,
        grid_spec=pltpu.PrefetchScalarGridSpec(
            num_scalar_prefetch=1,
            grid=(steps,),
            in_specs=[
                rows, rows, rows,
                pl.BlockSpec((K, 2 * tile, HALF), lambda i, *_: (0, i, 0)),
                whole(mats.shape), whole(bias.shape),
            ],
            out_specs=[
                rows, rows,
                whole((2 * H, HALF)), whole((2 * blocks, HALF)), whole((2 * H, HALF)),
            ],
            scratch_shapes=[
                pltpu.VMEM((2 * tile, HALF), jnp.float32),
                pltpu.VMEM((2 * tile, HALF), jnp.float32),
                pltpu.VMEM((2 * tile * K, HALF), jnp.float32),
            ]
            + [pltpu.VMEM((reach, HALF), jnp.float32)] * TABLES,
        ),
        out_shape=[
            jax.ShapeDtypeStruct((blocks, D), jnp.bfloat16),
            jax.ShapeDtypeStruct((blocks, D), jnp.bfloat16),
            jax.ShapeDtypeStruct((2 * H, HALF), jnp.bfloat16),
            jax.ShapeDtypeStruct((2 * blocks, HALF), jnp.float32),
            jax.ShapeDtypeStruct((2 * H, HALF), jnp.bfloat16),
        ],
        compiler_params=LIMIT,
        name="edges_backward",
    )(index, grad_mesh, mesh, uin, edges, mats, bias)


def round_backward(grad_mesh, own, first, last, grad_uin, dest_low, mats):
    blocks = grad_mesh.shape[0]
    tile = 256

    def body(grad_ref, own_ref, first_ref, last_ref, guin_ref, dest_ref, mats_ref, new_ref, sent_ref, wide):
        wide[...] = (
            own_ref[...] + first_ref[...].astype(jnp.float32) + last_ref[...].astype(jnp.float32)
        )
        one, two = unweave(wide)
        one, two = one.astype(jnp.bfloat16), two.astype(jnp.bfloat16)
        sent_ref[:, :HALF] = one
        sent_ref[:, HALF:] = two
        new_ref[...] = (
            grad_ref[...]
            + inner(guin_ref[...], mats_ref[3], 1, 1)
            + inner(dest_ref[...], mats_ref[1], 1, 1)
            + inner(one, mats_ref[0, :, :HALF], 1, 1)
            + inner(two, mats_ref[0, :, HALF:], 1, 1)
        )

    rows = pl.BlockSpec((tile, D), lambda i: (i, 0))
    woven = pl.BlockSpec((2 * tile, HALF), lambda i: (i, 0))
    return pl.pallas_call(
        body,
        grid=(blocks // tile,),
        in_specs=[rows, woven, woven, woven, rows, rows, whole(mats.shape)],
        out_specs=[rows, rows],
        out_shape=[
            jax.ShapeDtypeStruct((blocks, D), jnp.float32),
            jax.ShapeDtypeStruct((blocks, D), jnp.bfloat16),
        ],
        scratch_shapes=[pltpu.VMEM((2 * tile, HALF), jnp.float32)],
        compiler_params=LIMIT,
        name="round_backward",
    )(grad_mesh, own, first, last, grad_uin, dest_low, mats)


def shards(walk, master, moment1, moment2, inputs, targets, valid, owner, slot, neighbours, partner):
    bands = lax.axis_size("space")
    band = lax.axis_index("space")
    peers = lax.axis_size(ALL)
    place = lax.axis_index(ALL)
    shard = master.shape[0]
    total_size = shard * peers
    height = pieces_of(total_size, peers)[3]
    offset = lax.rem(lax.rem(shard, D) * place, D)
    piece = lax.dynamic_update_slice_in_dim(
        jnp.zeros((height * D,), jnp.bfloat16), master.astype(jnp.bfloat16), offset, 0
    )
    state_in = inputs[0]
    counted = valid[0].astype(jnp.float32)
    points = state_in.shape[1]
    blocks = neighbours.shape[0]
    assert blocks == H
    capacity = max(2, 2 * points // bands)
    target_band = owner[0, :, 0]
    hits = (target_band[:, None] == jnp.arange(bands, dtype=jnp.int32)[None, :]).astype(jnp.int32)
    ranks = jnp.sum(jnp.cumsum(hits, 0) * hits, 1) - 1
    places_out = jnp.sum(hits * jnp.asarray(walk, jnp.int32)[None, :], 1) * capacity + ranks
    poster = (
        jnp.arange(bands * capacity, dtype=jnp.int32)[:, None] == places_out[None, :]
    ).astype(jnp.bfloat16)
    spots = slot[0][None, :]
    columns = jnp.concatenate(
        [
            state_in,
            (spots // 64).astype(jnp.bfloat16),
            (spots % 64).astype(jnp.bfloat16),
            jnp.ones((1, points), jnp.bfloat16),
            jnp.zeros((HALF - CH - 3, points), jnp.bfloat16),
        ],
        0,
    )

    def exchanged(rows):
        return lax.all_to_all(
            rows.reshape(bands, capacity, HALF), "space", split_axis=0, concat_axis=0, tiled=True
        ).reshape(bands * capacity, HALF)

    arrived = exchanged(inner(poster, columns, 1, 1).astype(jnp.bfloat16))
    w_in, w_node, w_dec, w_out, w_round, biases = spread_rows(
        gathered_blocks(piece.reshape(height, D)), total_size, peers, place
    )
    w_out = jnp.pad(w_out.reshape(D, CH), ((0, 0), (0, HALF - CH)))
    w_round = w_round.reshape(ROUNDS, 5, D, D)
    b_head = biases[:3]
    b_round = biases[3:].reshape(ROUNDS, 2, D)
    count = summed_everywhere(jnp.full((8, HALF), jnp.sum(counted)))[0, 0]
    ids = arrived[:, CH : CH + 3].astype(jnp.int32)
    ids = jnp.where(ids[:, 2:3] > 0, ids[:, 0:1] * 64 + ids[:, 1:2], -1)
    chooser = (ids == jnp.arange(blocks, dtype=jnp.int32)[None, :]).astype(jnp.bfloat16)
    enc_in = inner(arrived, w_in, 1, 0) + b_head[0]
    encoded = silu(enc_in).astype(jnp.bfloat16)
    gathered = inner(chooser, encoded, 0, 0).astype(jnp.bfloat16)
    gathered, count = lax.optimization_barrier((gathered, count))
    node_in = inner(gathered, w_node, 1, 0) + b_head[1]
    mesh = silu(node_in)
    index = ((neighbours - band * blocks + H) % (blocks * bands)).T.reshape(-1)
    index = lax.ppermute(index, "space", list(enumerate(walk)))
    home = [(place, n) for n, place in enumerate(walk)]
    kept = []
    sent = inner(mesh.astype(jnp.bfloat16), w_round[0, 0], 1, 0).astype(jnp.bfloat16)
    sent = sent.reshape(2 * blocks, HALF)
    for layer in range(ROUNDS):
        before, after = halo(walk, sent[2 * (blocks - H) :], sent[: 2 * H])
        edges = gather_rows(
            index,
            before.reshape(H, 2, HALF),
            sent.reshape(blocks, 2, HALF),
            after.reshape(H, 2, HALF),
        ).reshape(K, 2 * blocks, HALF)
        following = w_round[layer + 1, 0] if layer + 1 < ROUNDS else None
        new, uin, agg, *rest = round_forward(mesh, edges, w_round[layer], b_round[layer], following)
        kept.append((mesh, edges, uin, agg))
        mesh = new
        sent = rest[0] if rest else None
    fetched = inner(chooser, mesh.astype(jnp.bfloat16), 1, 0).astype(jnp.bfloat16)
    dec_in = inner(fetched, w_dec, 1, 0) + b_head[2]
    decoded = silu(dec_in).astype(jnp.bfloat16)
    returned = exchanged(inner(decoded, w_out, 1, 0).astype(jnp.bfloat16))
    branch = inner(returned, poster, 0, 0)[:CH]
    err = state_in.astype(jnp.float32) + branch - targets[0].astype(jnp.float32)
    head_err, head_valid = (
        shifted(err[:, :ROWW].astype(jnp.bfloat16), "space", -1).astype(jnp.float32),
        shifted(counted[:, :ROWW].astype(jnp.bfloat16), "space", -1).astype(jnp.float32),
    )
    wide_err = jnp.concatenate([err, head_err], 1)
    wide_valid = jnp.concatenate([counted, head_valid], 1)
    ahead = partner - band * points - jnp.arange(points, dtype=jnp.int32)
    picks = [(ahead == by)[None, :] for by in range(NEAR, ROWW + 1)]
    err_far = err
    valid_far = counted
    for by, pick in zip(range(NEAR, ROWW + 1), picks):
        err_far = jnp.where(pick, wide_err[:, by : by + points], err_far)
        valid_far = jnp.where(pick, wide_valid[:, by : by + points], valid_far)
    gap = err - err_far
    local_total = jnp.sum(counted * err * err) + 0.5 * jnp.sum(counted * valid_far * gap * gap)
    paired = counted * valid_far * gap / count
    grad_err = 2.0 * counted * err / count + paired
    grad_wide = jnp.zeros(wide_err.shape, jnp.float32)
    for by, pick in zip(range(NEAR, ROWW + 1), picks):
        grad_wide = grad_wide - jnp.pad(
            jnp.where(pick, paired, 0.0), ((0, 0), (by, ROWW - by))
        )
    carried = shifted(grad_wide[:, points:].astype(jnp.bfloat16), "space", 1).astype(jnp.float32)
    stays = jnp.where((ahead == 0)[None, :], paired, 0.0)
    grad_pred = (
        grad_err - stays + grad_wide[:, :points] + jnp.pad(carried, ((0, 0), (0, points - ROWW)))
    )
    grad_rows = jnp.pad(grad_pred.astype(jnp.bfloat16), ((0, HALF - CH), (0, 0)))
    landed = exchanged(inner(poster, grad_rows, 1, 1).astype(jnp.bfloat16))
    grad_wout = inner(decoded, landed, 0, 0)[:, :CH]
    grad_dec = (inner(landed, w_out, 1, 1) * slope(dec_in)).astype(jnp.bfloat16)
    grad_bdec = jnp.sum(grad_dec.astype(jnp.float32), 0)
    grad_wdec = inner(fetched, grad_dec, 0, 0)
    grad_fetched = inner(grad_dec, w_dec, 1, 1).astype(jnp.bfloat16)
    grad_mesh = inner(chooser, grad_fetched, 0, 0)
    grad_mesh, leaving = lax.optimization_barrier((grad_mesh, mesh.astype(jnp.bfloat16)))
    final_mesh = lax.ppermute(leaving, "space", home).astype(jnp.float32)
    mats_grads = [None] * (5 * ROUNDS)
    bias_grads = [None] * (2 * ROUNDS)
    for layer in reversed(range(ROUNDS)):
        old, edges, uin, agg = kept[layer]
        mats = w_round[layer]
        grad_uin, dest_low, to_before, own, to_after = edges_backward(
            index, grad_mesh, old, uin, edges, mats, b_round[layer]
        )
        from_before, from_after = halo(walk, to_after, to_before)
        lowered = old.astype(jnp.bfloat16)
        grad_out = grad_mesh.astype(jnp.bfloat16)
        update = silu(uin).astype(jnp.bfloat16)
        grads = [
            None,
            inner(lowered, dest_low, 0, 0),
            inner(agg, grad_uin, 0, 0),
            inner(lowered, grad_uin, 0, 0),
            inner(update, grad_out, 0, 0),
        ]
        bias_grads[2 * layer] = jnp.sum(dest_low.astype(jnp.float32), 0, keepdims=True)
        bias_grads[2 * layer + 1] = jnp.sum(grad_uin.astype(jnp.float32), 0, keepdims=True)
        grad_mesh, sent_low = round_backward(
            grad_mesh, own, from_before, from_after, grad_uin, dest_low, mats
        )
        grads[0] = inner(lowered, sent_low, 0, 0)
        mats_grads[5 * layer : 5 * layer + 5] = grads
    node_grads = lax.ppermute(grad_mesh.astype(jnp.bfloat16), "space", home).astype(jnp.float32)
    grad_node = (grad_mesh * slope(node_in)).astype(jnp.bfloat16)
    grad_bnode = jnp.sum(grad_node.astype(jnp.float32), 0)
    grad_wnode = inner(gathered, grad_node, 0, 0)
    grad_gathered = inner(grad_node, w_node, 1, 1).astype(jnp.bfloat16)
    grad_encoded = inner(chooser, grad_gathered, 1, 0)
    grad_enc = (grad_encoded * slope(enc_in)).astype(jnp.bfloat16)
    grad_bin = jnp.sum(grad_enc.astype(jnp.float32), 0)
    grad_win = inner(arrived, grad_enc, 0, 0)
    parts = [grad_win, grad_wnode, grad_wdec, grad_wout.reshape(CH, D)]
    parts = parts + mats_grads
    parts.append(jnp.concatenate([jnp.stack([grad_bin, grad_bnode, grad_bdec])] + bias_grads, 0))
    mine = reduced_piece(*collect_rows(parts, total_size, peers, place))
    mine = lax.dynamic_slice_in_dim(mine.reshape(-1), offset, shard)
    lane = lax.broadcasted_iota(jnp.int32, (8, HALF), 1)
    sums = summed_everywhere(jnp.where(lane == 0, local_total, jnp.sum(mine * mine)))
    total, norm = sums[0, 0], jnp.sqrt(sums[0, 1])
    clipped = mine * jnp.minimum(1.0, 0.05 / norm)
    first = 0.9 * moment1 + 0.1 * clipped
    second = 0.999 * moment2 + 0.001 * clipped * clipped
    first_hat = first / (1.0 - 0.9**STEP)
    second_hat = second / (1.0 - 0.999**STEP)
    updated = master - 0.1 * (first_hat / (jnp.sqrt(second_hat) + 1e-08) + 0.1 * master)
    return (
        total.reshape(1),
        count.reshape(1),
        norm.reshape(1),
        updated,
        first,
        second,
        updated.astype(jnp.bfloat16),
        final_mesh.reshape(1, blocks, D),
        node_grads.reshape(1, blocks, D),
        grad_pred.reshape(1, grad_pred.shape[0], points),
    )


def solution(mesh):
    return jax.shard_map(
        functools.partial(shards, walk_of(mesh)),
        mesh=mesh,
        in_specs=(
            P(("dp", "space")),
            P(("dp", "space")),
            P(("dp", "space")),
            P("dp", None, "space"),
            P("dp", None, "space"),
            P("dp", None, "space"),
            P("dp", "space", None),
            P("dp", "space"),
            P("space", None),
            P("space"),
        ),
        out_specs=(
            P(),
            P(),
            P(),
            P(("dp", "space")),
            P(("dp", "space")),
            P(("dp", "space")),
            P(("dp", "space")),
            P("dp", "space", None),
            P("dp", "space", None),
            P("dp", None, "space"),
        ),
        check_vma=False,
    )
```

```python
import functools

import jax
import jax.numpy as jnp
from jax import lax
from jax.experimental import pallas as pl
from jax.experimental.pallas import tpu as pltpu
from jax.sharding import PartitionSpec as P

D = 256
HALF = 128
CH = 78
ROUNDS = 3
K = 6
ROWW = 360
NEAR = 358
STEP = 10
H = 2048
TABLES = 4
UNROLL = 32
ALL = ("dp", "space")
LIMIT = pltpu.CompilerParams(vmem_limit_bytes=56 * 2**20)


def cost(micros):
    return pl.CostEstimate(flops=0, bytes_accessed=micros * 3_000_000, transcendentals=0)


def inner(left, right, left_dim, right_dim):
    return lax.dot_general(
        left, right, (((left_dim,), (right_dim,)), ((), ())), preferred_element_type=jnp.float32
    )


def sigmoid(value):
    return 0.5 * jnp.tanh(0.5 * value) + 0.5


def silu(value):
    return value * sigmoid(value)


def slope(value):
    sigma = sigmoid(value)
    return sigma * (1.0 + value * (1.0 - sigma))


def shifted(shard, axis, by):
    peers = lax.axis_size(axis)
    pairs = [(i, i + by) for i in range(peers) if 0 <= i + by < peers]
    return lax.ppermute(shard, axis, pairs)


def walk_of(mesh):
    count = mesh.shape["space"]
    chips = [getattr(device, "coords", None) for device in mesh.devices[0].reshape(-1)]
    if any(chip is None for chip in chips) or len(set(map(tuple, chips))) != count:
        return list(range(count))
    at = {tuple(chip): n for n, chip in enumerate(chips)}
    xs, ys, zs = (sorted({chip[n] for chip in at}) for n in range(3))
    if len(xs) * len(ys) * len(zs) != count:
        return list(range(count))
    if (len(xs), len(ys), len(zs)) == (2, 2, 4):
        corners = [(0, 0), (1, 0), (0, 1), (1, 1)]
        planes = [(0, 1, 3, 2), (2, 0, 1, 3), (3, 1, 0, 2), (2, 3, 1, 0)]
        steps = [(*corners[n], z) for z, plane in enumerate(planes) for n in plane]
        return [at[(xs[x], ys[y], zs[z])] for x, y, z in steps]
    walk, plane = [], []
    for n, y in enumerate(ys):
        plane = plane + [(x, y) for x in (xs if n % 2 == 0 else xs[::-1])]
    for n, z in enumerate(zs):
        walk = walk + [at[(x, y, z)] for x, y in (plane if n % 2 == 0 else plane[::-1])]
    return walk


def halo(walk, last, initial):
    up = list(zip(walk, walk[1:] + walk[:1]))
    down = [(j, i) for i, j in up]
    return lax.ppermute(last, "space", up), lax.ppermute(initial, "space", down)


def pieces_of(total, peers):
    share = total // peers
    starts = [share * d // D for d in range(peers)]
    counts = [-(-share * (d + 1) // D) - starts[d] for d in range(peers)]
    shared = [share * d % D != 0 for d in range(peers)]
    height = -(-(max(counts) + 1) // 16) * 16
    return starts, counts, shared, height


def parts_of():
    return [CH, D, D, CH, ROUNDS * 5 * D, 3 + 2 * ROUNDS]


def swapped(value, axis, bit):
    return lax.ppermute(value, axis, [(i, i ^ bit) for i in range(lax.axis_size(axis))])


def bits_of(axis):
    return [1 << n for n in range(lax.axis_size(axis).bit_length() - 1)]


def summed_everywhere(value):
    for axis in ALL:
        for bit in bits_of(axis):
            value = value + swapped(value, axis, bit)
    return value


def orders():
    bits = bits_of("space")
    return bits, bits[1:2] + bits[:1] + bits[2:]


def gathered_blocks(piece):
    half = piece.shape[0] // 2
    held = []
    for part, order in zip((piece[:half], piece[half:]), orders()):
        names, part = [], part[None]
        for bit in reversed(order):
            part = jnp.concatenate([part, swapped(part, "space", bit)], 0)
            names.insert(0, bit)
        held.append(part)
    return held, [swapped(part, "dp", 1) for part in held]


def spread_rows(gathered, total, peers, place):
    (first, second), (first_far, second_far) = gathered
    starts, counts, shared, height = pieces_of(total, peers)
    half, group = height // 2, first.shape[0]
    rows = -(-total // D)
    sizes = parts_of()
    ranks = []
    for order in orders():
        ranks.append({bit: group >> (n + 1) for n, bit in enumerate(order)})

    def at(rank, relative):
        spot = 0
        for bit, weight in rank.items():
            spot = spot + jnp.where((relative & bit) != 0, weight, 0)
        return spot

    def body(place_ref, *refs):
        sources, outs, buffer = refs[:4], refs[4:-1], refs[-1]
        me = place_ref[0]
        mine = me // group
        for d in range(peers):
            relative = (me ^ d) & (group - 1)
            spots = [at(rank, relative) for rank in ranks]

            def lay(one, two, d=d, spots=spots):
                piece = jnp.concatenate([one[spots[0]], two[spots[1]]], 0).astype(jnp.float32)
                start, count = starts[d], counts[d]
                if shared[d]:
                    buffer[start : start + 1, :] = buffer[start : start + 1, :] + piece[:1]
                    buffer[start + 1 : start + count, :] = piece[1:count]
                else:
                    buffer[start : start + count, :] = piece[:count]

            @pl.when(mine == d // group)
            def _():
                lay(sources[0], sources[1])

            @pl.when(mine != d // group)
            def _():
                lay(sources[2], sources[3])

        count = jnp.zeros((1, D), jnp.float32)
        for source in (sources[1], sources[3]):
            for spot in range(group):
                count = count + source[spot, half - 1 : half, :].astype(jnp.float32)
        outs[-1][...] = count
        start = 0
        for out, size in zip(outs[:-1], sizes):
            out[:size, :] = buffer[start : start + size, :].astype(out.dtype)
            if out.shape[0] > size:
                out[size:, :] = jnp.zeros((out.shape[0] - size, D), out.dtype)
            start = start + size

    kinds = [jnp.bfloat16] * 5 + [jnp.float32]
    talls = [HALF] + sizes[1:]
    return pl.pallas_call(
        body,
        grid_spec=pltpu.PrefetchScalarGridSpec(
            num_scalar_prefetch=1,
            grid=(1,),
            in_specs=[whole(first.shape)] * 4,
            out_specs=[whole((tall, D)) for tall in talls + [1]],
            scratch_shapes=[pltpu.VMEM((-(-rows // 8) * 8 + 8, D), jnp.float32)],
        ),
        out_shape=[
            jax.ShapeDtypeStruct((tall, D), kind)
            for tall, kind in zip(talls + [1], kinds + [jnp.float32])
        ],
        compiler_params=LIMIT,
        cost_estimate=cost(4),
        name="spread_rows",
    )(place.reshape(1), first, second, first_far, second_far)


def collect_rows(parts, total, peers, place):
    starts, counts, shared, height = pieces_of(total, peers)
    rows = -(-total // D)
    sizes = [min(part.shape[0], size) for part, size in zip(parts, tall_parts())]
    group = lax.axis_size("space")

    def body(place_ref, *refs):
        sources, keep, send, buffer = refs[:-3], refs[-3], refs[-2], refs[-1]
        start = 0
        for source, size in zip(sources, sizes):
            buffer[start : start + size, :] = source[:size, :]
            start = start + size
        if buffer.shape[0] > start:
            buffer[start:, :] = jnp.zeros((buffer.shape[0] - start, D), jnp.float32)
        me = place_ref[0]
        mine = me // group
        for d in range(peers):
            relative = (me ^ d) & (group - 1)

            @pl.when(mine == d // group)
            def _():
                keep[relative] = buffer[starts[d] : starts[d] + height, :]

            @pl.when(mine != d // group)
            def _():
                send[relative] = buffer[starts[d] : starts[d] + height, :].astype(jnp.bfloat16)

    shape = (group, height, D)
    return pl.pallas_call(
        body,
        grid_spec=pltpu.PrefetchScalarGridSpec(
            num_scalar_prefetch=1,
            grid=(1,),
            in_specs=[whole(part.shape) for part in parts],
            out_specs=[whole(shape), whole(shape)],
            scratch_shapes=[pltpu.VMEM((-(-rows // 8) * 8 + height + 8, D), jnp.float32)],
        ),
        out_shape=[
            jax.ShapeDtypeStruct(shape, jnp.float32),
            jax.ShapeDtypeStruct(shape, jnp.bfloat16),
        ],
        compiler_params=LIMIT,
        cost_estimate=cost(5),
        name="collect_rows",
    )(place.reshape(1), *parts)


def reduced_piece(keep, send, leaving):
    kept = keep + swapped(send, "dp", 1).astype(jnp.float32)
    half = kept.shape[1] // 2
    names = [bits_of("space")[::-1], bits_of("space")[::-1]]
    parts = [kept[:, :half], kept[:, half:]]
    parts = [part.reshape((2,) * len(names[0]) + (half, D)) for part in parts]
    for turn, bits in enumerate(zip(*orders())):
        for n, bit in enumerate(bits):
            spot = names[n].index(bit)
            names[n].pop(spot)
            stay = lax.index_in_dim(parts[n], 0, spot, keepdims=False)
            leave = lax.index_in_dim(parts[n], 1, spot, keepdims=False)
            parts[n] = stay + swapped(leave.astype(jnp.bfloat16), "space", bit).astype(jnp.float32)
        if turn == 1:
            parts[0], parts[1], leaving = lax.optimization_barrier((*parts, leaving))
    return jnp.concatenate(parts, 0), leaving


def tall_parts():
    return [CH, D, D, CH] + [D] * (5 * ROUNDS) + [3 + 2 * ROUNDS]


def gather_rows(index, before, own, after):
    edges = index.shape[0]
    chunk = 1024
    spans = [before.shape[0], own.shape[0], after.shape[0]]

    def body(index_ref, before_ref, own_ref, after_ref, out_ref, table, sems):
        step = pl.program_id(0)

        @pl.when(step == 0)
        def _():
            copies = []
            start = 0
            for n, (source, span) in enumerate(zip((before_ref, own_ref, after_ref), spans)):
                copies.append(
                    pltpu.make_async_copy(source, table.at[pl.ds(start, span)], sems.at[n])
                )
                start = start + span
            for copy in copies:
                copy.start()
            for copy in copies:
                copy.wait()

        def some(i, carry):
            at = i * UNROLL
            base = step * chunk + at
            rows = [table[index_ref[base + u]] for u in range(UNROLL)]
            for u in range(UNROLL):
                out_ref[at + u] = rows[u]
            return carry

        lax.fori_loop(0, chunk // UNROLL, some, 0)

    return pl.pallas_call(
        body,
        grid_spec=pltpu.PrefetchScalarGridSpec(
            num_scalar_prefetch=1,
            grid=(edges // chunk,),
            in_specs=[pl.BlockSpec(memory_space=pl.ANY)] * 3,
            out_specs=pl.BlockSpec((chunk, 2, HALF), lambda i, *_: (i, 0, 0)),
            scratch_shapes=[
                pltpu.VMEM((sum(spans), 2, HALF), own.dtype),
                pltpu.SemaphoreType.DMA((3,)),
            ],
        ),
        out_shape=jax.ShapeDtypeStruct((edges, 2, HALF), own.dtype),
        compiler_params=LIMIT,
        cost_estimate=cost(16),
        name="gather_rows",
    )(index, before, own, after)


def weave(ref, value):
    rows = value.shape[0]
    ref[pl.ds(0, rows, stride=2), :] = value[:, :HALF]
    ref[pl.ds(1, rows, stride=2), :] = value[:, HALF:]


def unweave(ref):
    rows = ref.shape[0] // 2
    return ref[pl.ds(0, rows, stride=2), :], ref[pl.ds(1, rows, stride=2), :]


def whole(shape):
    return pl.BlockSpec(shape, lambda *_: (0,) * len(shape))


def round_forward(mesh, edges, mats, bias, following):
    blocks = mesh.shape[0]
    tile = 256
    more = following is not None

    def body(*refs):
        if more:
            (mesh_ref, edge_ref, mats_ref, bias_ref, next_ref, new_ref, uin_ref, agg_ref, sent_ref, wide) = refs
        else:
            (mesh_ref, edge_ref, mats_ref, bias_ref, new_ref, uin_ref, agg_ref, wide) = refs
        mesh_in = mesh_ref[...]
        lowered = mesh_in.astype(jnp.bfloat16)
        weave(wide, inner(lowered, mats_ref[1], 1, 0) + bias_ref[0:1, :])
        dest = wide[...]
        total = jnp.zeros(dest.shape, jnp.float32)
        for edge in range(K):
            total = total + silu(edge_ref[edge].astype(jnp.float32) + dest)
        wide[...] = total * (1.0 / K)
        first, second = unweave(wide)
        first, second = first.astype(jnp.bfloat16), second.astype(jnp.bfloat16)
        agg_ref[:, :HALF] = first
        agg_ref[:, HALF:] = second
        update_in = (
            inner(first, mats_ref[2, :HALF, :], 1, 0)
            + inner(second, mats_ref[2, HALF:, :], 1, 0)
            + inner(lowered, mats_ref[3], 1, 0)
            + bias_ref[1:2, :]
        )
        uin_ref[...] = update_in
        update = silu(update_in).astype(jnp.bfloat16)
        new = mesh_in + inner(update, mats_ref[4], 1, 0)
        new_ref[...] = new
        if more:
            weave(wide, inner(new.astype(jnp.bfloat16), next_ref[...], 1, 0))
            sent_ref[...] = wide[...].astype(jnp.bfloat16)

    rows = pl.BlockSpec((tile, D), lambda i: (i, 0))
    woven = pl.BlockSpec((2 * tile, HALF), lambda i: (i, 0))
    ins = [rows, pl.BlockSpec((K, 2 * tile, HALF), lambda i: (0, i, 0)), whole(mats.shape), whole(bias.shape)]
    outs = [rows, rows, rows]
    shapes = [
        jax.ShapeDtypeStruct((blocks, D), jnp.float32),
        jax.ShapeDtypeStruct((blocks, D), jnp.float32),
        jax.ShapeDtypeStruct((blocks, D), jnp.bfloat16),
    ]
    args = [mesh, edges, mats, bias]
    if more:
        ins.append(whole(following.shape))
        outs.append(woven)
        shapes.append(jax.ShapeDtypeStruct((2 * blocks, HALF), jnp.bfloat16))
        args.append(following)
    return pl.pallas_call(
        body,
        grid=(blocks // tile,),
        in_specs=ins,
        out_specs=outs,
        out_shape=shapes,
        scratch_shapes=[pltpu.VMEM((2 * tile, HALF), jnp.float32)],
        compiler_params=LIMIT,
        cost_estimate=cost(11),
        name="round_forward",
    )(*args)


def edges_backward(index, grad_mesh, mesh, uin, edges, mats, bias):
    blocks = mesh.shape[0]
    tile = 256
    steps = blocks // tile
    reach = 2 * (blocks + 2 * H)

    def body(
        index_ref, grad_ref, mesh_ref, uin_ref, edge_ref, mats_ref, bias_ref,
        guin_ref, low_ref, before_ref, own_ref, after_ref, wide, wider, flows, *tables,
    ):
        step = pl.program_id(0)

        @pl.when(step == 0)
        def _():
            for table in tables:
                table[...] = jnp.zeros(table.shape, jnp.float32)

        grad_out = grad_ref[...].astype(jnp.bfloat16)
        grad_update = inner(grad_out, mats_ref[4], 1, 1)
        grad_uin = (grad_update * slope(uin_ref[...])).astype(jnp.bfloat16)
        guin_ref[...] = grad_uin
        weave(wide, inner(grad_uin, mats_ref[2], 1, 1) * (1.0 / K))
        lowered = mesh_ref[...].astype(jnp.bfloat16)
        weave(wider, inner(lowered, mats_ref[1], 1, 0) + bias_ref[0:1, :])
        grad_agg = wide[...]
        dest = wider[...]
        grad_dest = jnp.zeros(dest.shape, jnp.float32)
        for edge in range(K):
            flow = grad_agg * slope(edge_ref[edge].astype(jnp.float32) + dest)
            grad_dest = grad_dest + flow
            flows[edge * 2 * tile : (edge + 1) * 2 * tile, :] = flow
        wide[...] = grad_dest
        first, second = unweave(wide)
        low_ref[:, :HALF] = first.astype(jnp.bfloat16)
        low_ref[:, HALF:] = second.astype(jnp.bfloat16)
        for edge in range(K):

            def some(i, carry):
                at = i * UNROLL
                base = edge * blocks + step * tile + at
                for first in range(0, UNROLL, TABLES):
                    spots, rows, sums = [], [], []
                    for u in range(first, first + TABLES):
                        spots.append(pl.multiple_of(index_ref[base + u] * 2, 2))
                        spot = pl.multiple_of(2 * (edge * tile + at + u), 2)
                        rows.append(flows[pl.ds(spot, 2), :])
                    for u in range(TABLES):
                        sums.append(tables[u][pl.ds(spots[u], 2), :] + rows[u])
                    for u in range(TABLES):
                        tables[u][pl.ds(spots[u], 2), :] = sums[u]
                return carry

            lax.fori_loop(0, tile // UNROLL, some, 0)

        @pl.when(step == steps - 1)
        def _():
            def summed(start, size):
                value = tables[0][start : start + size, :]
                for table in tables[1:]:
                    value = value + table[start : start + size, :]
                return value

            before_ref[...] = summed(0, 2 * H).astype(jnp.bfloat16)
            own_ref[...] = summed(2 * H, 2 * blocks)
            after_ref[...] = summed(2 * H + 2 * blocks, 2 * H).astype(jnp.bfloat16)

    rows = pl.BlockSpec((tile, D), lambda i, *_: (i, 0))
    return pl.pallas_call(
        body,
        grid_spec=pltpu.PrefetchScalarGridSpec(
            num_scalar_prefetch=1,
            grid=(steps,),
            in_specs=[
                rows, rows, rows,
                pl.BlockSpec((K, 2 * tile, HALF), lambda i, *_: (0, i, 0)),
                whole(mats.shape), whole(bias.shape),
            ],
            out_specs=[
                rows, rows,
                whole((2 * H, HALF)), whole((2 * blocks, HALF)), whole((2 * H, HALF)),
            ],
            scratch_shapes=[
                pltpu.VMEM((2 * tile, HALF), jnp.float32),
                pltpu.VMEM((2 * tile, HALF), jnp.float32),
                pltpu.VMEM((2 * tile * K, HALF), jnp.float32),
            ]
            + [pltpu.VMEM((reach, HALF), jnp.float32)] * TABLES,
        ),
        out_shape=[
            jax.ShapeDtypeStruct((blocks, D), jnp.bfloat16),
            jax.ShapeDtypeStruct((blocks, D), jnp.bfloat16),
            jax.ShapeDtypeStruct((2 * H, HALF), jnp.bfloat16),
            jax.ShapeDtypeStruct((2 * blocks, HALF), jnp.float32),
            jax.ShapeDtypeStruct((2 * H, HALF), jnp.bfloat16),
        ],
        compiler_params=LIMIT,
        cost_estimate=cost(33),
        name="edges_backward",
    )(index, grad_mesh, mesh, uin, edges, mats, bias)


def round_backward(grad_mesh, own, first, last, grad_uin, dest_low, mats):
    blocks = grad_mesh.shape[0]
    tile = 256

    def body(grad_ref, own_ref, first_ref, last_ref, guin_ref, dest_ref, mats_ref, new_ref, sent_ref, wide):
        wide[...] = (
            own_ref[...] + first_ref[...].astype(jnp.float32) + last_ref[...].astype(jnp.float32)
        )
        one, two = unweave(wide)
        one, two = one.astype(jnp.bfloat16), two.astype(jnp.bfloat16)
        sent_ref[:, :HALF] = one
        sent_ref[:, HALF:] = two
        new_ref[...] = (
            grad_ref[...]
            + inner(guin_ref[...], mats_ref[3], 1, 1)
            + inner(dest_ref[...], mats_ref[1], 1, 1)
            + inner(one, mats_ref[0, :, :HALF], 1, 1)
            + inner(two, mats_ref[0, :, HALF:], 1, 1)
        )

    rows = pl.BlockSpec((tile, D), lambda i: (i, 0))
    woven = pl.BlockSpec((2 * tile, HALF), lambda i: (i, 0))
    return pl.pallas_call(
        body,
        grid=(blocks // tile,),
        in_specs=[rows, woven, woven, woven, rows, rows, whole(mats.shape)],
        out_specs=[rows, rows],
        out_shape=[
            jax.ShapeDtypeStruct((blocks, D), jnp.float32),
            jax.ShapeDtypeStruct((blocks, D), jnp.bfloat16),
        ],
        scratch_shapes=[pltpu.VMEM((2 * tile, HALF), jnp.float32)],
        compiler_params=LIMIT,
        cost_estimate=cost(8),
        name="round_backward",
    )(grad_mesh, own, first, last, grad_uin, dest_low, mats)


def shards(walk, master, moment1, moment2, inputs, targets, valid, owner, slot, neighbours, partner):
    bands = lax.axis_size("space")
    band = lax.axis_index("space")
    peers = lax.axis_size(ALL)
    place = lax.axis_index(ALL)
    shard = master.shape[0]
    total_size = shard * peers
    height = pieces_of(total_size, peers)[3]
    offset = lax.rem(lax.rem(shard, D) * place, D)
    piece = lax.dynamic_update_slice_in_dim(
        jnp.zeros((height * D,), jnp.bfloat16), master.astype(jnp.bfloat16), offset, 0
    )
    state_in = inputs[0]
    counted = valid[0].astype(jnp.float32)
    local_count = jnp.sum(valid[0])
    digits = (local_count >> jnp.array([16, 8, 0], jnp.int32)) & 255
    piece = lax.dynamic_update_slice(
        piece.reshape(height, D), digits.astype(jnp.bfloat16)[None, :], (height - 1, 0)
    )
    points = state_in.shape[1]
    blocks = neighbours.shape[0]
    assert blocks == H
    capacity = max(2, 2 * points // bands)
    target_band = owner[0, :, 0]
    hits = (target_band[:, None] == jnp.arange(bands, dtype=jnp.int32)[None, :]).astype(jnp.int32)
    ranks = jnp.sum(jnp.cumsum(hits, 0) * hits, 1) - 1
    places_out = jnp.sum(hits * jnp.asarray(walk, jnp.int32)[None, :], 1) * capacity + ranks
    poster = (
        jnp.arange(bands * capacity, dtype=jnp.int32)[:, None] == places_out[None, :]
    ).astype(jnp.bfloat16)
    spots = slot[0][None, :]
    columns = jnp.concatenate(
        [
            state_in,
            (spots // 64).astype(jnp.bfloat16),
            (spots % 64).astype(jnp.bfloat16),
            jnp.ones((1, points), jnp.bfloat16),
            jnp.zeros((HALF - CH - 3, points), jnp.bfloat16),
        ],
        0,
    )

    def exchanged(rows):
        return lax.all_to_all(
            rows.reshape(bands, capacity, HALF), "space", split_axis=0, concat_axis=0, tiled=True
        ).reshape(bands * capacity, HALF)

    arrived = exchanged(inner(poster, columns, 1, 1).astype(jnp.bfloat16))
    w_in, w_node, w_dec, w_out, w_round, biases, digits = spread_rows(
        gathered_blocks(piece), total_size, peers, place
    )
    count = digits[0, 0] * 65536.0 + digits[0, 1] * 256.0 + digits[0, 2]
    w_out = jnp.pad(w_out.reshape(D, CH), ((0, 0), (0, HALF - CH)))
    w_round = w_round.reshape(ROUNDS, 5, D, D)
    b_head = biases[:3]
    b_round = biases[3:].reshape(ROUNDS, 2, D)
    ids = arrived[:, CH : CH + 3].astype(jnp.int32)
    ids = jnp.where(ids[:, 2:3] > 0, ids[:, 0:1] * 64 + ids[:, 1:2], -1)
    chooser = (ids == jnp.arange(blocks, dtype=jnp.int32)[None, :]).astype(jnp.bfloat16)
    enc_in = inner(arrived, w_in, 1, 0) + b_head[0]
    encoded = silu(enc_in).astype(jnp.bfloat16)
    gathered = inner(chooser, encoded, 0, 0).astype(jnp.bfloat16)
    node_in = inner(gathered, w_node, 1, 0) + b_head[1]
    mesh = silu(node_in)
    index = ((neighbours - band * blocks + H) % (blocks * bands)).T.reshape(-1)
    index = lax.ppermute(index, "space", list(enumerate(walk)))
    home = [(place, n) for n, place in enumerate(walk)]
    kept = []
    sent = inner(mesh.astype(jnp.bfloat16), w_round[0, 0], 1, 0).astype(jnp.bfloat16)
    sent = sent.reshape(2 * blocks, HALF)
    for layer in range(ROUNDS):
        before, after = halo(walk, sent[2 * (blocks - H) :], sent[: 2 * H])
        edges = gather_rows(
            index,
            before.reshape(H, 2, HALF),
            sent.reshape(blocks, 2, HALF),
            after.reshape(H, 2, HALF),
        ).reshape(K, 2 * blocks, HALF)
        following = w_round[layer + 1, 0] if layer + 1 < ROUNDS else None
        new, uin, agg, *rest = round_forward(mesh, edges, w_round[layer], b_round[layer], following)
        kept.append((mesh, edges, uin, agg))
        mesh = new
        sent = rest[0] if rest else None
    fetched = inner(chooser, mesh.astype(jnp.bfloat16), 1, 0).astype(jnp.bfloat16)
    dec_in = inner(fetched, w_dec, 1, 0) + b_head[2]
    decoded = silu(dec_in).astype(jnp.bfloat16)
    returned = exchanged(inner(decoded, w_out, 1, 0).astype(jnp.bfloat16))
    branch = inner(returned, poster, 0, 0)[:CH]
    err = state_in.astype(jnp.float32) + branch - targets[0].astype(jnp.float32)
    head_err, head_valid = (
        shifted(err[:, :ROWW].astype(jnp.bfloat16), "space", -1).astype(jnp.float32),
        shifted(counted[:, :ROWW].astype(jnp.bfloat16), "space", -1).astype(jnp.float32),
    )
    wide_err = jnp.concatenate([err, head_err], 1)
    wide_valid = jnp.concatenate([counted, head_valid], 1)
    ahead = partner - band * points - jnp.arange(points, dtype=jnp.int32)
    picks = [(ahead == by)[None, :] for by in range(NEAR, ROWW + 1)]
    err_far = err
    valid_far = counted
    for by, pick in zip(range(NEAR, ROWW + 1), picks):
        err_far = jnp.where(pick, wide_err[:, by : by + points], err_far)
        valid_far = jnp.where(pick, wide_valid[:, by : by + points], valid_far)
    gap = err - err_far
    local_total = jnp.sum(counted * err * err) + 0.5 * jnp.sum(counted * valid_far * gap * gap)
    paired = counted * valid_far * gap / count
    grad_err = 2.0 * counted * err / count + paired
    grad_wide = jnp.zeros(wide_err.shape, jnp.float32)
    for by, pick in zip(range(NEAR, ROWW + 1), picks):
        grad_wide = grad_wide - jnp.pad(
            jnp.where(pick, paired, 0.0), ((0, 0), (by, ROWW - by))
        )
    carried = shifted(grad_wide[:, points:].astype(jnp.bfloat16), "space", 1).astype(jnp.float32)
    stays = jnp.where((ahead == 0)[None, :], paired, 0.0)
    grad_pred = (
        grad_err - stays + grad_wide[:, :points] + jnp.pad(carried, ((0, 0), (0, points - ROWW)))
    )
    grad_rows = jnp.pad(grad_pred.astype(jnp.bfloat16), ((0, HALF - CH), (0, 0)))
    landed = exchanged(inner(poster, grad_rows, 1, 1).astype(jnp.bfloat16))
    grad_wout = inner(decoded, landed, 0, 0)[:, :CH]
    grad_dec = (inner(landed, w_out, 1, 1) * slope(dec_in)).astype(jnp.bfloat16)
    grad_bdec = jnp.sum(grad_dec.astype(jnp.float32), 0)
    grad_wdec = inner(fetched, grad_dec, 0, 0)
    grad_fetched = inner(grad_dec, w_dec, 1, 1).astype(jnp.bfloat16)
    grad_mesh = inner(chooser, grad_fetched, 0, 0)
    grad_mesh, leaving = lax.optimization_barrier((grad_mesh, mesh.astype(jnp.bfloat16)))
    final_mesh = lax.ppermute(leaving, "space", home)
    mats_grads = [None] * (5 * ROUNDS)
    bias_grads = [None] * (2 * ROUNDS)
    for layer in reversed(range(ROUNDS)):
        old, edges, uin, agg = kept[layer]
        mats = w_round[layer]
        grad_uin, dest_low, to_before, own, to_after = edges_backward(
            index, grad_mesh, old, uin, edges, mats, b_round[layer]
        )
        if layer == ROUNDS - 1:
            to_before, to_after, final_mesh = lax.optimization_barrier(
                (to_before, to_after, final_mesh)
            )
        from_before, from_after = halo(walk, to_after, to_before)
        lowered = old.astype(jnp.bfloat16)
        grad_out = grad_mesh.astype(jnp.bfloat16)
        update = silu(uin).astype(jnp.bfloat16)
        grads = [
            None,
            inner(lowered, dest_low, 0, 0),
            inner(agg, grad_uin, 0, 0),
            inner(lowered, grad_uin, 0, 0),
            inner(update, grad_out, 0, 0),
        ]
        bias_grads[2 * layer] = jnp.sum(dest_low.astype(jnp.float32), 0, keepdims=True)
        bias_grads[2 * layer + 1] = jnp.sum(grad_uin.astype(jnp.float32), 0, keepdims=True)
        grad_mesh, sent_low = round_backward(
            grad_mesh, own, from_before, from_after, grad_uin, dest_low, mats
        )
        grads[0] = inner(lowered, sent_low, 0, 0)
        mats_grads[5 * layer : 5 * layer + 5] = grads
    leaving = grad_mesh.astype(jnp.bfloat16)
    grad_node = (grad_mesh * slope(node_in)).astype(jnp.bfloat16)
    grad_bnode = jnp.sum(grad_node.astype(jnp.float32), 0)
    grad_wnode = inner(gathered, grad_node, 0, 0)
    grad_gathered = inner(grad_node, w_node, 1, 1).astype(jnp.bfloat16)
    grad_encoded = inner(chooser, grad_gathered, 1, 0)
    grad_enc = (grad_encoded * slope(enc_in)).astype(jnp.bfloat16)
    grad_bin = jnp.sum(grad_enc.astype(jnp.float32), 0)
    grad_win = inner(arrived, grad_enc, 0, 0)
    parts = [grad_win, grad_wnode, grad_wdec, grad_wout.reshape(CH, D)]
    parts = parts + mats_grads
    parts.append(jnp.concatenate([jnp.stack([grad_bin, grad_bnode, grad_bdec])] + bias_grads, 0))
    keep, send = collect_rows(parts, total_size, peers, place)
    mine, leaving = reduced_piece(keep, send, leaving)
    node_grads = lax.ppermute(leaving, "space", home)
    mine = lax.dynamic_slice_in_dim(mine.reshape(-1), offset, shard)
    lane = lax.broadcasted_iota(jnp.int32, (8, HALF), 1)
    sums = summed_everywhere(jnp.where(lane == 0, local_total, jnp.sum(mine * mine)))
    total, norm = sums[0, 0], jnp.sqrt(sums[0, 1])
    clipped = mine * jnp.minimum(1.0, 0.05 / norm)
    first = 0.9 * moment1 + 0.1 * clipped
    second = 0.999 * moment2 + 0.001 * clipped * clipped
    first_hat = first / (1.0 - 0.9**STEP)
    second_hat = second / (1.0 - 0.999**STEP)
    updated = master - 0.1 * (first_hat / (jnp.sqrt(second_hat) + 1e-08) + 0.1 * master)
    return (
        total.reshape(1),
        count.reshape(1),
        norm.reshape(1),
        updated,
        first,
        second,
        updated.astype(jnp.bfloat16),
        final_mesh.astype(jnp.float32).reshape(1, blocks, D),
        node_grads.astype(jnp.float32).reshape(1, blocks, D),
        grad_pred.reshape(1, grad_pred.shape[0], points),
    )


def solution(mesh):
    return jax.shard_map(
        functools.partial(shards, walk_of(mesh)),
        mesh=mesh,
        in_specs=(
            P(("dp", "space")),
            P(("dp", "space")),
            P(("dp", "space")),
            P("dp", None, "space"),
            P("dp", None, "space"),
            P("dp", None, "space"),
            P("dp", "space", None),
            P("dp", "space"),
            P("space", None),
            P("space"),
        ),
        out_specs=(
            P(),
            P(),
            P(),
            P(("dp", "space")),
            P(("dp", "space")),
            P(("dp", "space")),
            P(("dp", "space")),
            P("dp", "space", None),
            P("dp", "space", None),
            P("dp", None, "space"),
        ),
        check_vma=False,
    )
```

```python
import functools

import jax
import jax.numpy as jnp
from jax import lax
from jax.experimental import pallas as pl
from jax.experimental.pallas import tpu as pltpu
from jax.sharding import PartitionSpec as P

D = 256
HALF = 128
CH = 78
ROUNDS = 3
K = 6
ROWW = 360
NEAR = 358
STEP = 10
H = 2048
ALL = ("dp", "space")
LIMIT = pltpu.CompilerParams(vmem_limit_bytes=56 * 2**20)


def cost(micros):
    return pl.CostEstimate(flops=0, bytes_accessed=micros * 3_000_000, transcendentals=0)


def inner(left, right, left_dim, right_dim):
    return lax.dot_general(
        left, right, (((left_dim,), (right_dim,)), ((), ())), preferred_element_type=jnp.float32
    )


def sigmoid(value):
    return 0.5 * jnp.tanh(0.5 * value) + 0.5


def silu(value):
    return value * sigmoid(value)


def slope(value):
    sigma = sigmoid(value)
    return sigma * (1.0 + value * (1.0 - sigma))


def shifted(shard, axis, by):
    peers = lax.axis_size(axis)
    pairs = [(i, i + by) for i in range(peers) if 0 <= i + by < peers]
    return lax.ppermute(shard, axis, pairs)


def walk_of(mesh):
    count = mesh.shape["space"]
    chips = [getattr(device, "coords", None) for device in mesh.devices[0].reshape(-1)]
    if any(chip is None for chip in chips) or len(set(map(tuple, chips))) != count:
        return list(range(count))
    at = {tuple(chip): n for n, chip in enumerate(chips)}
    xs, ys, zs = (sorted({chip[n] for chip in at}) for n in range(3))
    if len(xs) * len(ys) * len(zs) != count:
        return list(range(count))
    if (len(xs), len(ys), len(zs)) == (2, 2, 4):
        corners = [(0, 0), (1, 0), (0, 1), (1, 1)]
        planes = [(0, 1, 3, 2), (2, 0, 1, 3), (3, 1, 0, 2), (2, 3, 1, 0)]
        steps = [(*corners[n], z) for z, plane in enumerate(planes) for n in plane]
        return [at[(xs[x], ys[y], zs[z])] for x, y, z in steps]
    walk, plane = [], []
    for n, y in enumerate(ys):
        plane = plane + [(x, y) for x in (xs if n % 2 == 0 else xs[::-1])]
    for n, z in enumerate(zs):
        walk = walk + [at[(x, y, z)] for x, y in (plane if n % 2 == 0 else plane[::-1])]
    return walk


def halo(walk, last, initial):
    up = list(zip(walk, walk[1:] + walk[:1]))
    down = [(j, i) for i, j in up]
    return lax.ppermute(last, "space", up), lax.ppermute(initial, "space", down)


def pieces_of(total, peers):
    share = total // peers
    starts = [share * d // D for d in range(peers)]
    counts = [-(-share * (d + 1) // D) - starts[d] for d in range(peers)]
    shared = [share * d % D != 0 for d in range(peers)]
    height = -(-(max(counts) + 1) // 16) * 16
    return starts, counts, shared, height


def parts_of():
    return [CH, D, D, CH, ROUNDS * 5 * D, 3 + 2 * ROUNDS]


def swapped(value, axis, bit):
    return lax.ppermute(value, axis, [(i, i ^ bit) for i in range(lax.axis_size(axis))])


def bits_of(axis):
    return [1 << n for n in range(lax.axis_size(axis).bit_length() - 1)]


def summed_everywhere(value):
    for axis in ALL:
        for bit in bits_of(axis):
            value = value + swapped(value, axis, bit)
    return value


def orders():
    bits = bits_of("space")
    return bits, bits[1:2] + bits[:1] + bits[2:]


def gathered_blocks(piece):
    half = piece.shape[0] // 2
    held = []
    for part, order in zip((piece[:half], piece[half:]), orders()):
        names, part = [], part[None]
        for bit in reversed(order):
            part = jnp.concatenate([part, swapped(part, "space", bit)], 0)
            names.insert(0, bit)
        held.append(part)
    return held, [swapped(part, "dp", 1) for part in held]


def spread_rows(gathered, total, peers, place):
    (first, second), (first_far, second_far) = gathered
    starts, counts, shared, height = pieces_of(total, peers)
    half, group = height // 2, first.shape[0]
    rows = -(-total // D)
    sizes = parts_of()
    ranks = []
    for order in orders():
        ranks.append({bit: group >> (n + 1) for n, bit in enumerate(order)})

    def at(rank, relative):
        spot = 0
        for bit, weight in rank.items():
            spot = spot + jnp.where((relative & bit) != 0, weight, 0)
        return spot

    def body(place_ref, *refs):
        sources, outs, buffer = refs[:4], refs[4:-1], refs[-1]
        me = place_ref[0]
        mine = me // group
        for d in range(peers):
            relative = (me ^ d) & (group - 1)
            spots = [at(rank, relative) for rank in ranks]

            def lay(one, two, d=d, spots=spots):
                piece = jnp.concatenate([one[spots[0]], two[spots[1]]], 0).astype(jnp.float32)
                start, count = starts[d], counts[d]
                if shared[d]:
                    buffer[start : start + 1, :] = buffer[start : start + 1, :] + piece[:1]
                    buffer[start + 1 : start + count, :] = piece[1:count]
                else:
                    buffer[start : start + count, :] = piece[:count]

            @pl.when(mine == d // group)
            def _():
                lay(sources[0], sources[1])

            @pl.when(mine != d // group)
            def _():
                lay(sources[2], sources[3])

        count = jnp.zeros((1, D), jnp.float32)
        for source in (sources[1], sources[3]):
            for spot in range(group):
                count = count + source[spot, half - 1 : half, :].astype(jnp.float32)
        outs[-1][...] = count
        start = 0
        for out, size in zip(outs[:-1], sizes):
            out[:size, :] = buffer[start : start + size, :].astype(out.dtype)
            if out.shape[0] > size:
                out[size:, :] = jnp.zeros((out.shape[0] - size, D), out.dtype)
            start = start + size

    kinds = [jnp.bfloat16] * 5 + [jnp.float32]
    talls = [HALF] + sizes[1:]
    return pl.pallas_call(
        body,
        grid_spec=pltpu.PrefetchScalarGridSpec(
            num_scalar_prefetch=1,
            grid=(1,),
            in_specs=[whole(first.shape)] * 4,
            out_specs=[whole((tall, D)) for tall in talls + [1]],
            scratch_shapes=[pltpu.VMEM((-(-rows // 8) * 8 + 8, D), jnp.float32)],
        ),
        out_shape=[
            jax.ShapeDtypeStruct((tall, D), kind)
            for tall, kind in zip(talls + [1], kinds + [jnp.float32])
        ],
        compiler_params=LIMIT,
        cost_estimate=cost(4),
        name="spread_rows",
    )(place.reshape(1), first, second, first_far, second_far)


def collect_rows(parts, total, peers, place):
    starts, counts, shared, height = pieces_of(total, peers)
    rows = -(-total // D)
    sizes = [min(part.shape[0], size) for part, size in zip(parts, tall_parts())]
    group = lax.axis_size("space")

    def body(place_ref, *refs):
        sources, keep, send, buffer = refs[:-3], refs[-3], refs[-2], refs[-1]
        start = 0
        for source, size in zip(sources, sizes):
            buffer[start : start + size, :] = source[:size, :]
            start = start + size
        if buffer.shape[0] > start:
            buffer[start:, :] = jnp.zeros((buffer.shape[0] - start, D), jnp.float32)
        me = place_ref[0]
        mine = me // group
        for d in range(peers):
            relative = (me ^ d) & (group - 1)

            @pl.when(mine == d // group)
            def _():
                keep[relative] = buffer[starts[d] : starts[d] + height, :]

            @pl.when(mine != d // group)
            def _():
                send[relative] = buffer[starts[d] : starts[d] + height, :].astype(jnp.bfloat16)

    shape = (group, height, D)
    return pl.pallas_call(
        body,
        grid_spec=pltpu.PrefetchScalarGridSpec(
            num_scalar_prefetch=1,
            grid=(1,),
            in_specs=[whole(part.shape) for part in parts],
            out_specs=[whole(shape), whole(shape)],
            scratch_shapes=[pltpu.VMEM((-(-rows // 8) * 8 + height + 8, D), jnp.float32)],
        ),
        out_shape=[
            jax.ShapeDtypeStruct(shape, jnp.float32),
            jax.ShapeDtypeStruct(shape, jnp.bfloat16),
        ],
        compiler_params=LIMIT,
        cost_estimate=cost(5),
        name="collect_rows",
    )(place.reshape(1), *parts)


def reduced_piece(keep, send, leaving):
    kept = keep + swapped(send, "dp", 1).astype(jnp.float32)
    half = kept.shape[1] // 2
    names = [bits_of("space")[::-1], bits_of("space")[::-1]]
    parts = [kept[:, :half], kept[:, half:]]
    parts = [part.reshape((2,) * len(names[0]) + (half, D)) for part in parts]
    for turn, bits in enumerate(zip(*orders())):
        for n, bit in enumerate(bits):
            spot = names[n].index(bit)
            names[n].pop(spot)
            stay = lax.index_in_dim(parts[n], 0, spot, keepdims=False)
            leave = lax.index_in_dim(parts[n], 1, spot, keepdims=False)
            parts[n] = stay + swapped(leave.astype(jnp.bfloat16), "space", bit).astype(jnp.float32)
        if turn == 1:
            parts[0], parts[1], leaving = lax.optimization_barrier((*parts, leaving))
    return jnp.concatenate(parts, 0), leaving


def tall_parts():
    return [CH, D, D, CH] + [D] * (5 * ROUNDS) + [3 + 2 * ROUNDS]


def weave(ref, value):
    rows = value.shape[0]
    ref[pl.ds(0, rows, stride=2), :] = value[:, :HALF]
    ref[pl.ds(1, rows, stride=2), :] = value[:, HALF:]


def unweave(ref):
    rows = ref.shape[0] // 2
    return ref[pl.ds(0, rows, stride=2), :], ref[pl.ds(1, rows, stride=2), :]


def whole(shape):
    return pl.BlockSpec(shape, lambda *_: (0,) * len(shape))


def round_forward(index, mesh, before, own, after, mats, bias, following):
    blocks = mesh.shape[0]
    tile, chunk = 512, 16
    turns, high = tile // chunk, 2 * chunk
    more = following is not None
    spans = [before.shape[0], own.shape[0], after.shape[0]]
    reach = sum(spans)

    def body(*refs):
        index_ref, mesh_ref, before_ref, own_ref, after_ref, mats_ref, bias_ref = refs[:7]
        next_ref, sent_ref = (refs[7], refs[13]) if more else (None, None)
        new_ref, back_ref, update_ref, agg_ref, slope_ref = refs[8:13] if more else refs[7:12]
        raw, table, rows, wide, wider, sems = refs[-6:]
        step = pl.program_id(0)

        @pl.when(step == 0)
        def _():
            copies = []
            start = 0
            for n, (source, span) in enumerate(zip((before_ref, own_ref, after_ref), spans)):
                copies.append(
                    pltpu.make_async_copy(source, raw.at[pl.ds(start, span)], sems.at[n])
                )
                start = start + span
            for copy in copies:
                copy.start()
            for copy in copies:
                copy.wait()

            @pl.loop(0, reach // 256)
            def _(i):
                at = pl.multiple_of(i * 256, 256)
                table[pl.ds(at, 256), :] = raw[pl.ds(at, 256), :].astype(jnp.float32)

        mesh_in = mesh_ref[...]
        lowered = mesh_in.astype(jnp.bfloat16)
        weave(wide, inner(lowered, mats_ref[1], 1, 0) + bias_ref[0:1, :])

        def fetch(turn):
            for edge in range(K):
                base = edge * blocks + step * tile + turn * chunk
                values = [
                    table[pl.ds(pl.multiple_of(index_ref[base + u], 2), 2), :] for u in range(chunk)
                ]
                for u in range(chunk):
                    spot = pl.multiple_of(edge * 2 * tile + turn * high + 2 * u, 2)
                    rows[pl.ds(spot, 2), :] = values[u]

        def load(turn):
            at = pl.multiple_of(turn * high, high)
            taken = [
                rows[pl.ds(pl.multiple_of(edge * 2 * tile + turn * high, high), high), :]
                for edge in range(K)
            ]
            return at, wide[pl.ds(at, high), :], taken

        def dense(at, dest, taken):
            total = None
            for edge in range(K):
                value = taken[edge] + dest
                sigma = sigmoid(value)
                out = value * sigma
                slope_ref[edge, pl.ds(at, high), :] = (sigma + out * (1.0 - sigma)).astype(
                    jnp.bfloat16
                )
                total = out if total is None else total + out
            wider[pl.ds(at, high), :] = total * (1.0 / K)

        def some(turn, carry):
            loaded = load(turn - 1)
            fetch(turn)
            dense(*loaded)
            return carry

        fetch(0)
        lax.fori_loop(1, turns, some, 0)
        dense(*load(turns - 1))
        first, second = unweave(wider)
        first, second = first.astype(jnp.bfloat16), second.astype(jnp.bfloat16)
        agg_ref[:, :HALF] = first
        agg_ref[:, HALF:] = second
        update_in = (
            inner(first, mats_ref[2, :HALF, :], 1, 0)
            + inner(second, mats_ref[2, HALF:, :], 1, 0)
            + inner(lowered, mats_ref[3], 1, 0)
            + bias_ref[1:2, :]
        )
        sigma = sigmoid(update_in)
        out = update_in * sigma
        back_ref[...] = sigma + out * (1.0 - sigma)
        update = out.astype(jnp.bfloat16)
        update_ref[...] = update
        new = mesh_in + inner(update, mats_ref[4], 1, 0)
        new_ref[...] = new
        if more:
            weave(wide, inner(new.astype(jnp.bfloat16), next_ref[...], 1, 0))
            sent_ref[...] = wide[...].astype(jnp.bfloat16)

    whole_rows = pl.BlockSpec((tile, D), lambda i, *_: (i, 0))
    woven = pl.BlockSpec((2 * tile, HALF), lambda i, *_: (i, 0))
    ins = [whole_rows] + [pl.BlockSpec(memory_space=pl.ANY)] * 3 + [whole(mats.shape), whole(bias.shape)]
    outs = [whole_rows] * 4 + [pl.BlockSpec((K, 2 * tile, HALF), lambda i, *_: (0, i, 0))]
    shapes = [
        jax.ShapeDtypeStruct((blocks, D), jnp.float32),
        jax.ShapeDtypeStruct((blocks, D), jnp.float32),
        jax.ShapeDtypeStruct((blocks, D), jnp.bfloat16),
        jax.ShapeDtypeStruct((blocks, D), jnp.bfloat16),
        jax.ShapeDtypeStruct((K, 2 * blocks, HALF), jnp.bfloat16),
    ]
    args = [index, mesh, before, own, after, mats, bias]
    if more:
        ins.append(whole(following.shape))
        outs.append(woven)
        shapes.append(jax.ShapeDtypeStruct((2 * blocks, HALF), jnp.bfloat16))
        args.append(following)
    return pl.pallas_call(
        body,
        grid_spec=pltpu.PrefetchScalarGridSpec(
            num_scalar_prefetch=1,
            grid=(blocks // tile,),
            in_specs=ins,
            out_specs=outs,
            scratch_shapes=[
                pltpu.VMEM((reach, HALF), jnp.bfloat16),
                pltpu.VMEM((reach, HALF), jnp.float32),
                pltpu.VMEM((K * 2 * tile, HALF), jnp.float32),
                pltpu.VMEM((2 * tile, HALF), jnp.float32),
                pltpu.VMEM((2 * tile, HALF), jnp.float32),
                pltpu.SemaphoreType.DMA((3,)),
            ],
        ),
        out_shape=shapes,
        compiler_params=LIMIT,
        cost_estimate=cost(25),
        name="round_forward",
    )(*args)


def edges_backward(index, grad_mesh, back, slopes, turned):
    blocks = grad_mesh.shape[0]
    tile, chunk = 512, 16
    steps, turns, high = blocks // tile, tile // chunk, 2 * chunk
    reach = 2 * (blocks + 2 * H)

    def body(
        index_ref, grad_ref, back_ref, slope_ref, turned_ref,
        guin_ref, low_ref, before_ref, own_ref, after_ref, wide, wider, flows, *tables,
    ):
        step = pl.program_id(0)

        @pl.when(step == 0)
        def _():
            @pl.loop(0, reach // 256)
            def _(i):
                for table in tables:
                    table[pl.ds(pl.multiple_of(i * 256, 256), 256), :] = jnp.zeros(
                        (256, HALF), jnp.float32
                    )

        grad_out = grad_ref[...].astype(jnp.bfloat16)
        grad_uin = (inner(grad_out, turned_ref[4], 1, 0) * back_ref[...]).astype(jnp.bfloat16)
        guin_ref[...] = grad_uin
        weave(wide, inner(grad_uin, turned_ref[2], 1, 0) * (1.0 / K))

        def dense(turn):
            at = pl.multiple_of(turn * high, high)
            grad_agg = wide[pl.ds(at, high), :]
            total, parts = None, []
            for edge in range(K):
                flow = grad_agg * slope_ref[edge, pl.ds(at, high), :].astype(jnp.float32)
                parts.append(flow)
                total = flow if total is None else total + flow
            return at, total, parts

        def keep(turn, at, total, parts):
            for edge in range(K):
                spot = pl.multiple_of(edge * 2 * tile + turn * high, high)
                flows[pl.ds(spot, high), :] = parts[edge]
            wider[pl.ds(at, high), :] = total

        def scatter(turn):
            for u in range(chunk):
                spots, sums = [], []
                for edge in range(K):
                    base = edge * blocks + step * tile + turn * chunk
                    spots.append(pl.multiple_of(index_ref[base + u], 2))
                for edge in range(K):
                    spot = pl.multiple_of(edge * 2 * tile + turn * high + 2 * u, 2)
                    sums.append(tables[edge][pl.ds(spots[edge], 2), :] + flows[pl.ds(spot, 2), :])
                for edge in range(K):
                    tables[edge][pl.ds(spots[edge], 2), :] = sums[edge]

        def some(turn, carry):
            found = dense(turn)
            scatter(turn - 1)
            keep(turn, *found)
            return carry

        keep(0, *dense(0))
        lax.fori_loop(1, turns, some, 0)
        scatter(turns - 1)
        first, second = unweave(wider)
        low_ref[:, :HALF] = first.astype(jnp.bfloat16)
        low_ref[:, HALF:] = second.astype(jnp.bfloat16)

        @pl.when(step == steps - 1)
        def _():
            def summed(at):
                value = tables[0][pl.ds(at, 256), :]
                for table in tables[1:]:
                    value = value + table[pl.ds(at, 256), :]
                return value

            @pl.loop(0, 2 * H // 256)
            def _(i):
                at = pl.multiple_of(i * 256, 256)
                far = pl.multiple_of(2 * H + 2 * blocks + at, 256)
                before_ref[pl.ds(at, 256), :] = summed(at).astype(jnp.bfloat16)
                after_ref[pl.ds(at, 256), :] = summed(far).astype(jnp.bfloat16)

            @pl.loop(0, 2 * blocks // 256)
            def _(i):
                at = pl.multiple_of(i * 256, 256)
                own_ref[pl.ds(at, 256), :] = summed(pl.multiple_of(2 * H + at, 256))

    rows = pl.BlockSpec((tile, D), lambda i, *_: (i, 0))
    return pl.pallas_call(
        body,
        grid_spec=pltpu.PrefetchScalarGridSpec(
            num_scalar_prefetch=1,
            grid=(steps,),
            in_specs=[
                rows, rows,
                pl.BlockSpec((K, 2 * tile, HALF), lambda i, *_: (0, i, 0)),
                whole(turned.shape),
            ],
            out_specs=[
                rows, rows,
                whole((2 * H, HALF)), whole((2 * blocks, HALF)), whole((2 * H, HALF)),
            ],
            scratch_shapes=[
                pltpu.VMEM((2 * tile, HALF), jnp.float32),
                pltpu.VMEM((2 * tile, HALF), jnp.float32),
                pltpu.VMEM((2 * tile * K, HALF), jnp.float32),
            ]
            + [pltpu.VMEM((reach, HALF), jnp.float32)] * K,
        ),
        out_shape=[
            jax.ShapeDtypeStruct((blocks, D), jnp.bfloat16),
            jax.ShapeDtypeStruct((blocks, D), jnp.bfloat16),
            jax.ShapeDtypeStruct((2 * H, HALF), jnp.bfloat16),
            jax.ShapeDtypeStruct((2 * blocks, HALF), jnp.float32),
            jax.ShapeDtypeStruct((2 * H, HALF), jnp.bfloat16),
        ],
        compiler_params=LIMIT,
        cost_estimate=cost(25),
        name="edges_backward",
    )(index, grad_mesh, back, slopes, turned)


def round_backward(grad_mesh, own, first, last, grad_uin, dest_low, turned):
    blocks = grad_mesh.shape[0]
    tile = 1024

    def body(
        grad_ref, own_ref, first_ref, last_ref, guin_ref, dest_ref, turned_ref, new_ref, sent_ref, wide
    ):
        wide[...] = (
            own_ref[...] + first_ref[...].astype(jnp.float32) + last_ref[...].astype(jnp.float32)
        )
        one, two = unweave(wide)
        one, two = one.astype(jnp.bfloat16), two.astype(jnp.bfloat16)
        sent_ref[:, :HALF] = one
        sent_ref[:, HALF:] = two
        new_ref[...] = (
            grad_ref[...]
            + inner(guin_ref[...], turned_ref[3], 1, 0)
            + inner(dest_ref[...], turned_ref[1], 1, 0)
            + inner(one, turned_ref[0, :HALF, :], 1, 0)
            + inner(two, turned_ref[0, HALF:, :], 1, 0)
        )

    rows = pl.BlockSpec((tile, D), lambda i: (i, 0))
    woven = pl.BlockSpec((2 * tile, HALF), lambda i: (i, 0))
    return pl.pallas_call(
        body,
        grid=(blocks // tile,),
        in_specs=[rows, woven, woven, woven, rows, rows, whole(turned.shape)],
        out_specs=[rows, rows],
        out_shape=[
            jax.ShapeDtypeStruct((blocks, D), jnp.float32),
            jax.ShapeDtypeStruct((blocks, D), jnp.bfloat16),
        ],
        scratch_shapes=[pltpu.VMEM((2 * tile, HALF), jnp.float32)],
        compiler_params=LIMIT,
        cost_estimate=cost(7),
        name="round_backward",
    )(grad_mesh, own, first, last, grad_uin, dest_low, turned)


def shards(walk, master, moment1, moment2, inputs, targets, valid, owner, slot, neighbours, partner):
    bands = lax.axis_size("space")
    band = lax.axis_index("space")
    peers = lax.axis_size(ALL)
    place = lax.axis_index(ALL)
    shard = master.shape[0]
    total_size = shard * peers
    height = pieces_of(total_size, peers)[3]
    offset = lax.rem(lax.rem(shard, D) * place, D)
    piece = lax.dynamic_update_slice_in_dim(
        jnp.zeros((height * D,), jnp.bfloat16), master.astype(jnp.bfloat16), offset, 0
    )
    state_in = inputs[0]
    counted = valid[0].astype(jnp.float32)
    local_count = jnp.sum(valid[0])
    digits = (local_count >> jnp.array([16, 8, 0], jnp.int32)) & 255
    piece = lax.dynamic_update_slice(
        piece.reshape(height, D), digits.astype(jnp.bfloat16)[None, :], (height - 1, 0)
    )
    points = state_in.shape[1]
    blocks = neighbours.shape[0]
    assert blocks == H
    capacity = max(2, 2 * points // bands)
    target_band = owner[0, :, 0]
    hits = (target_band[:, None] == jnp.arange(bands, dtype=jnp.int32)[None, :]).astype(jnp.int32)
    ranks = jnp.sum(jnp.cumsum(hits, 0) * hits, 1) - 1
    places_out = jnp.sum(hits * jnp.asarray(walk, jnp.int32)[None, :], 1) * capacity + ranks
    poster = (
        jnp.arange(bands * capacity, dtype=jnp.int32)[:, None] == places_out[None, :]
    ).astype(jnp.bfloat16)
    spots = slot[0][None, :]
    columns = jnp.concatenate(
        [
            state_in,
            (spots // 64).astype(jnp.bfloat16),
            (spots % 64).astype(jnp.bfloat16),
            jnp.ones((1, points), jnp.bfloat16),
            jnp.zeros((HALF - CH - 3, points), jnp.bfloat16),
        ],
        0,
    )

    def exchanged(rows):
        return lax.all_to_all(
            rows.reshape(bands, capacity, HALF), "space", split_axis=0, concat_axis=0, tiled=True
        ).reshape(bands * capacity, HALF)

    arrived = exchanged(inner(poster, columns, 1, 1).astype(jnp.bfloat16))
    w_in, w_node, w_dec, w_out, w_round, biases, digits = spread_rows(
        gathered_blocks(piece), total_size, peers, place
    )
    count = digits[0, 0] * 65536.0 + digits[0, 1] * 256.0 + digits[0, 2]
    w_out = jnp.pad(w_out.reshape(D, CH), ((0, 0), (0, HALF - CH)))
    w_round = w_round.reshape(ROUNDS, 5, D, D)
    b_head = biases[:3]
    b_round = biases[3:].reshape(ROUNDS, 2, D)
    ids = arrived[:, CH : CH + 3].astype(jnp.int32)
    ids = jnp.where(ids[:, 2:3] > 0, ids[:, 0:1] * 64 + ids[:, 1:2], -1)
    chooser = (ids == jnp.arange(blocks, dtype=jnp.int32)[None, :]).astype(jnp.bfloat16)
    enc_in = inner(arrived, w_in, 1, 0) + b_head[0]
    encoded = silu(enc_in).astype(jnp.bfloat16)
    gathered = inner(chooser, encoded, 0, 0).astype(jnp.bfloat16)
    node_in = inner(gathered, w_node, 1, 0) + b_head[1]
    mesh = silu(node_in)
    index = 2 * ((neighbours - band * blocks + H) % (blocks * bands)).T.reshape(-1)
    index = lax.ppermute(index, "space", list(enumerate(walk)))
    home = [(place, n) for n, place in enumerate(walk)]
    kept = []
    sent = inner(mesh.astype(jnp.bfloat16), w_round[0, 0], 1, 0).astype(jnp.bfloat16)
    sent = sent.reshape(2 * blocks, HALF)
    for layer in range(ROUNDS):
        before, after = halo(walk, sent[2 * (blocks - H) :], sent[: 2 * H])
        if layer == 0:
            before, turned = lax.optimization_barrier((before, jnp.swapaxes(w_round, 2, 3)))
        following = w_round[layer + 1, 0] if layer + 1 < ROUNDS else None
        new, back, update, agg, slopes, *rest = round_forward(
            index, mesh, before, sent, after, w_round[layer], b_round[layer], following
        )
        kept.append((mesh, back, update, agg, slopes))
        mesh = new
        sent = rest[0] if rest else None
    fetched = inner(chooser, mesh.astype(jnp.bfloat16), 1, 0).astype(jnp.bfloat16)
    dec_in = inner(fetched, w_dec, 1, 0) + b_head[2]
    decoded = silu(dec_in).astype(jnp.bfloat16)
    returned = exchanged(inner(decoded, w_out, 1, 0).astype(jnp.bfloat16))
    branch = inner(returned, poster, 0, 0)[:CH]
    err = state_in.astype(jnp.float32) + branch - targets[0].astype(jnp.float32)
    head_err, head_valid = (
        shifted(err[:, :ROWW].astype(jnp.bfloat16), "space", -1).astype(jnp.float32),
        shifted(counted[:, :ROWW].astype(jnp.bfloat16), "space", -1).astype(jnp.float32),
    )
    wide_err = jnp.concatenate([err, head_err], 1)
    wide_valid = jnp.concatenate([counted, head_valid], 1)
    ahead = partner - band * points - jnp.arange(points, dtype=jnp.int32)
    picks = [(ahead == by)[None, :] for by in range(NEAR, ROWW + 1)]
    err_far = err
    valid_far = counted
    for by, pick in zip(range(NEAR, ROWW + 1), picks):
        err_far = jnp.where(pick, wide_err[:, by : by + points], err_far)
        valid_far = jnp.where(pick, wide_valid[:, by : by + points], valid_far)
    gap = err - err_far
    local_total = jnp.sum(counted * err * err) + 0.5 * jnp.sum(counted * valid_far * gap * gap)
    paired = counted * valid_far * gap / count
    grad_err = 2.0 * counted * err / count + paired
    grad_wide = jnp.zeros(wide_err.shape, jnp.float32)
    for by, pick in zip(range(NEAR, ROWW + 1), picks):
        grad_wide = grad_wide - jnp.pad(
            jnp.where(pick, paired, 0.0), ((0, 0), (by, ROWW - by))
        )
    carried = shifted(grad_wide[:, points:].astype(jnp.bfloat16), "space", 1).astype(jnp.float32)
    stays = jnp.where((ahead == 0)[None, :], paired, 0.0)
    grad_pred = (
        grad_err - stays + grad_wide[:, :points] + jnp.pad(carried, ((0, 0), (0, points - ROWW)))
    )
    grad_rows = jnp.pad(grad_pred.astype(jnp.bfloat16), ((0, HALF - CH), (0, 0)))
    landed = exchanged(inner(poster, grad_rows, 1, 1).astype(jnp.bfloat16))
    grad_wout = inner(decoded, landed, 0, 0)[:, :CH]
    grad_dec = (inner(landed, w_out, 1, 1) * slope(dec_in)).astype(jnp.bfloat16)
    grad_bdec = jnp.sum(grad_dec.astype(jnp.float32), 0)
    grad_wdec = inner(fetched, grad_dec, 0, 0)
    grad_fetched = inner(grad_dec, w_dec, 1, 1).astype(jnp.bfloat16)
    grad_mesh = inner(chooser, grad_fetched, 0, 0)
    grad_mesh, leaving = lax.optimization_barrier((grad_mesh, mesh.astype(jnp.bfloat16)))
    final_mesh = lax.ppermute(leaving, "space", home)
    mats_grads = [None] * (5 * ROUNDS)
    bias_grads = [None] * (2 * ROUNDS)
    for layer in reversed(range(ROUNDS)):
        old, back, update, agg, slopes = kept[layer]
        grad_uin, dest_low, to_before, own, to_after = edges_backward(
            index, grad_mesh, back, slopes, turned[layer]
        )
        if layer == ROUNDS - 1:
            to_before, to_after, final_mesh = lax.optimization_barrier(
                (to_before, to_after, final_mesh)
            )
        from_before, from_after = halo(walk, to_after, to_before)
        lowered = old.astype(jnp.bfloat16)
        grad_out = grad_mesh.astype(jnp.bfloat16)
        grads = [
            None,
            inner(lowered, dest_low, 0, 0),
            inner(agg, grad_uin, 0, 0),
            inner(lowered, grad_uin, 0, 0),
            inner(update, grad_out, 0, 0),
        ]
        bias_grads[2 * layer] = jnp.sum(dest_low.astype(jnp.float32), 0, keepdims=True)
        bias_grads[2 * layer + 1] = jnp.sum(grad_uin.astype(jnp.float32), 0, keepdims=True)
        grad_mesh, sent_low = round_backward(
            grad_mesh, own, from_before, from_after, grad_uin, dest_low, turned[layer]
        )
        grads[0] = inner(lowered, sent_low, 0, 0)
        mats_grads[5 * layer : 5 * layer + 5] = grads
    leaving = grad_mesh.astype(jnp.bfloat16)
    early = lax.ppermute(leaving[: blocks // 2], "space", home)
    leaving = leaving[blocks // 2 :]
    grad_node = (grad_mesh * slope(node_in)).astype(jnp.bfloat16)
    grad_bnode = jnp.sum(grad_node.astype(jnp.float32), 0)
    grad_wnode = inner(gathered, grad_node, 0, 0)
    grad_gathered = inner(grad_node, w_node, 1, 1).astype(jnp.bfloat16)
    grad_encoded = inner(chooser, grad_gathered, 1, 0)
    grad_enc = (grad_encoded * slope(enc_in)).astype(jnp.bfloat16)
    grad_bin = jnp.sum(grad_enc.astype(jnp.float32), 0)
    grad_win = inner(arrived, grad_enc, 0, 0)
    grad_win, early = lax.optimization_barrier((grad_win, early))
    parts = [grad_win, grad_wnode, grad_wdec, grad_wout.reshape(CH, D)]
    parts = parts + mats_grads
    parts.append(jnp.concatenate([jnp.stack([grad_bin, grad_bnode, grad_bdec])] + bias_grads, 0))
    keep, send = collect_rows(parts, total_size, peers, place)
    mine, leaving = reduced_piece(keep, send, leaving)
    late = lax.ppermute(leaving, "space", home)
    mine = lax.dynamic_slice_in_dim(mine.reshape(-1), offset, shard)
    lane = lax.broadcasted_iota(jnp.int32, (8, HALF), 1)
    sums = summed_everywhere(jnp.where(lane == 0, local_total, jnp.sum(mine * mine)))
    total, norm = sums[0, 0], jnp.sqrt(sums[0, 1])
    node_grads = jnp.concatenate([early, late], 0)
    clipped = mine * jnp.minimum(1.0, 0.05 / norm)
    first = 0.9 * moment1 + 0.1 * clipped
    second = 0.999 * moment2 + 0.001 * clipped * clipped
    first_hat = first / (1.0 - 0.9**STEP)
    second_hat = second / (1.0 - 0.999**STEP)
    updated = master - 0.1 * (first_hat / (jnp.sqrt(second_hat) + 1e-08) + 0.1 * master)
    return (
        total.reshape(1),
        count.reshape(1),
        norm.reshape(1),
        updated,
        first,
        second,
        updated.astype(jnp.bfloat16),
        final_mesh.astype(jnp.float32).reshape(1, blocks, D),
        node_grads.astype(jnp.float32).reshape(1, blocks, D),
        grad_pred.reshape(1, grad_pred.shape[0], points),
    )


def solution(mesh):
    return jax.shard_map(
        functools.partial(shards, walk_of(mesh)),
        mesh=mesh,
        in_specs=(
            P(("dp", "space")),
            P(("dp", "space")),
            P(("dp", "space")),
            P("dp", None, "space"),
            P("dp", None, "space"),
            P("dp", None, "space"),
            P("dp", "space", None),
            P("dp", "space"),
            P("space", None),
            P("space"),
        ),
        out_specs=(
            P(),
            P(),
            P(),
            P(("dp", "space")),
            P(("dp", "space")),
            P(("dp", "space")),
            P(("dp", "space")),
            P("dp", "space", None),
            P("dp", "space", None),
            P("dp", None, "space"),
        ),
        check_vma=False,
    )
```

```python
import functools

import jax
import jax.numpy as jnp
from jax import lax
from jax.experimental import pallas as pl
from jax.experimental.pallas import tpu as pltpu
from jax.sharding import PartitionSpec as P

D = 256
HALF = 128
CH = 78
ROUNDS = 3
K = 6
ROWW = 360
NEAR = 358
STEP = 10
H = 2048
ALL = ("dp", "space")
LIMIT = pltpu.CompilerParams(vmem_limit_bytes=56 * 2**20)


def cost(micros):
    return pl.CostEstimate(flops=0, bytes_accessed=micros * 3_000_000, transcendentals=0)


def inner(left, right, left_dim, right_dim):
    return lax.dot_general(
        left, right, (((left_dim,), (right_dim,)), ((), ())), preferred_element_type=jnp.float32
    )


def sigmoid(value):
    return 0.5 * jnp.tanh(0.5 * value) + 0.5


def silu(value):
    return value * sigmoid(value)


def slope(value):
    sigma = sigmoid(value)
    return sigma * (1.0 + value * (1.0 - sigma))


def shifted(shard, axis, by):
    peers = lax.axis_size(axis)
    pairs = [(i, i + by) for i in range(peers) if 0 <= i + by < peers]
    return lax.ppermute(shard, axis, pairs)


def walk_of(mesh):
    count = mesh.shape["space"]
    chips = [getattr(device, "coords", None) for device in mesh.devices[0].reshape(-1)]
    if any(chip is None for chip in chips) or len(set(map(tuple, chips))) != count:
        return list(range(count))
    at = {tuple(chip): n for n, chip in enumerate(chips)}
    xs, ys, zs = (sorted({chip[n] for chip in at}) for n in range(3))
    if len(xs) * len(ys) * len(zs) != count:
        return list(range(count))
    if (len(xs), len(ys), len(zs)) == (2, 2, 4):
        corners = [(0, 0), (1, 0), (0, 1), (1, 1)]
        planes = [(0, 1, 3, 2), (2, 0, 1, 3), (3, 1, 0, 2), (2, 3, 1, 0)]
        steps = [(*corners[n], z) for z, plane in enumerate(planes) for n in plane]
        return [at[(xs[x], ys[y], zs[z])] for x, y, z in steps]
    walk, plane = [], []
    for n, y in enumerate(ys):
        plane = plane + [(x, y) for x in (xs if n % 2 == 0 else xs[::-1])]
    for n, z in enumerate(zs):
        walk = walk + [at[(x, y, z)] for x, y in (plane if n % 2 == 0 else plane[::-1])]
    return walk


def halo(walk, last, initial):
    up = list(zip(walk, walk[1:] + walk[:1]))
    down = [(j, i) for i, j in up]
    return lax.ppermute(last, "space", up), lax.ppermute(initial, "space", down)


def pieces_of(total, peers):
    share = total // peers
    starts = [share * d // D for d in range(peers)]
    counts = [-(-share * (d + 1) // D) - starts[d] for d in range(peers)]
    shared = [share * d % D != 0 for d in range(peers)]
    height = -(-(max(counts) + 1) // 16) * 16
    return starts, counts, shared, height


def parts_of():
    return [CH, D, D, CH, ROUNDS * 5 * D, 3 + 2 * ROUNDS]


def swapped(value, axis, bit):
    return lax.ppermute(value, axis, [(i, i ^ bit) for i in range(lax.axis_size(axis))])


def bits_of(axis):
    return [1 << n for n in range(lax.axis_size(axis).bit_length() - 1)]


def summed_everywhere(value):
    for axis in ALL:
        for bit in bits_of(axis):
            value = value + swapped(value, axis, bit)
    return value


def orders():
    bits = bits_of("space")
    return bits, bits[1:2] + bits[:1] + bits[2:]


def gathered_blocks(piece):
    half = piece.shape[0] // 2
    held = []
    for part, order in zip((piece[:half], piece[half:]), orders()):
        names, part = [], part[None]
        for bit in reversed(order):
            part = jnp.concatenate([part, swapped(part, "space", bit)], 0)
            names.insert(0, bit)
        held.append(part)
    return held, [swapped(part, "dp", 1) for part in held]


def spread_rows(gathered, total, peers, place):
    (first, second), (first_far, second_far) = gathered
    starts, counts, shared, height = pieces_of(total, peers)
    half, group = height // 2, first.shape[0]
    rows = -(-total // D)
    sizes = parts_of()
    ranks = []
    for order in orders():
        ranks.append({bit: group >> (n + 1) for n, bit in enumerate(order)})

    def at(rank, relative):
        spot = 0
        for bit, weight in rank.items():
            spot = spot + jnp.where((relative & bit) != 0, weight, 0)
        return spot

    def body(place_ref, *refs):
        sources, outs, buffer = refs[:4], refs[4:-1], refs[-1]
        me = place_ref[0]
        mine = me // group
        for d in range(peers):
            relative = (me ^ d) & (group - 1)
            spots = [at(rank, relative) for rank in ranks]

            def lay(one, two, d=d, spots=spots):
                piece = jnp.concatenate([one[spots[0]], two[spots[1]]], 0).astype(jnp.float32)
                start, count = starts[d], counts[d]
                if shared[d]:
                    buffer[start : start + 1, :] = buffer[start : start + 1, :] + piece[:1]
                    buffer[start + 1 : start + count, :] = piece[1:count]
                else:
                    buffer[start : start + count, :] = piece[:count]

            @pl.when(mine == d // group)
            def _():
                lay(sources[0], sources[1])

            @pl.when(mine != d // group)
            def _():
                lay(sources[2], sources[3])

        count = jnp.zeros((1, D), jnp.float32)
        for source in (sources[1], sources[3]):
            for spot in range(group):
                count = count + source[spot, half - 1 : half, :].astype(jnp.float32)
        outs[-1][...] = count
        start = 0
        for out, size in zip(outs[:-1], sizes):
            out[:size, :] = buffer[start : start + size, :].astype(out.dtype)
            if out.shape[0] > size:
                out[size:, :] = jnp.zeros((out.shape[0] - size, D), out.dtype)
            start = start + size

    kinds = [jnp.bfloat16] * 5 + [jnp.float32]
    talls = [HALF] + sizes[1:]
    return pl.pallas_call(
        body,
        grid_spec=pltpu.PrefetchScalarGridSpec(
            num_scalar_prefetch=1,
            grid=(1,),
            in_specs=[whole(first.shape)] * 4,
            out_specs=[whole((tall, D)) for tall in talls + [1]],
            scratch_shapes=[pltpu.VMEM((-(-rows // 8) * 8 + 8, D), jnp.float32)],
        ),
        out_shape=[
            jax.ShapeDtypeStruct((tall, D), kind)
            for tall, kind in zip(talls + [1], kinds + [jnp.float32])
        ],
        compiler_params=LIMIT,
        cost_estimate=cost(4),
        name="spread_rows",
    )(place.reshape(1), first, second, first_far, second_far)


def collect_rows(parts, total, peers, place):
    starts, counts, shared, height = pieces_of(total, peers)
    rows = -(-total // D)
    sizes = [min(part.shape[0], size) for part, size in zip(parts, tall_parts())]
    group = lax.axis_size("space")

    def body(place_ref, *refs):
        sources, keep, send, buffer = refs[:-3], refs[-3], refs[-2], refs[-1]
        start = 0
        for source, size in zip(sources, sizes):
            buffer[start : start + size, :] = source[:size, :]
            start = start + size
        if buffer.shape[0] > start:
            buffer[start:, :] = jnp.zeros((buffer.shape[0] - start, D), jnp.float32)
        me = place_ref[0]
        mine = me // group
        for d in range(peers):
            relative = (me ^ d) & (group - 1)

            @pl.when(mine == d // group)
            def _():
                keep[relative] = buffer[starts[d] : starts[d] + height, :]

            @pl.when(mine != d // group)
            def _():
                send[relative] = buffer[starts[d] : starts[d] + height, :].astype(jnp.bfloat16)

    shape = (group, height, D)
    return pl.pallas_call(
        body,
        grid_spec=pltpu.PrefetchScalarGridSpec(
            num_scalar_prefetch=1,
            grid=(1,),
            in_specs=[whole(part.shape) for part in parts],
            out_specs=[whole(shape), whole(shape)],
            scratch_shapes=[pltpu.VMEM((-(-rows // 8) * 8 + height + 8, D), jnp.float32)],
        ),
        out_shape=[
            jax.ShapeDtypeStruct(shape, jnp.float32),
            jax.ShapeDtypeStruct(shape, jnp.bfloat16),
        ],
        compiler_params=LIMIT,
        cost_estimate=cost(5),
        name="collect_rows",
    )(place.reshape(1), *parts)


def reduced_piece(keep, send, leaving):
    kept = keep + swapped(send, "dp", 1).astype(jnp.float32)
    half = kept.shape[1] // 2
    names = [bits_of("space")[::-1], bits_of("space")[::-1]]
    parts = [kept[:, :half], kept[:, half:]]
    parts = [part.reshape((2,) * len(names[0]) + (half, D)) for part in parts]
    for turn, bits in enumerate(zip(*orders())):
        for n, bit in enumerate(bits):
            spot = names[n].index(bit)
            names[n].pop(spot)
            stay = lax.index_in_dim(parts[n], 0, spot, keepdims=False)
            leave = lax.index_in_dim(parts[n], 1, spot, keepdims=False)
            parts[n] = stay + swapped(leave.astype(jnp.bfloat16), "space", bit).astype(jnp.float32)
        if turn == 1:
            parts[0], parts[1], leaving = lax.optimization_barrier((*parts, leaving))
    return jnp.concatenate(parts, 0), leaving


def tall_parts():
    return [CH, D, D, CH] + [D] * (5 * ROUNDS) + [2] + [1] * (1 + 2 * ROUNDS)


def weave(ref, value):
    rows = value.shape[0]
    ref[pl.ds(0, rows, stride=2), :] = value[:, :HALF]
    ref[pl.ds(1, rows, stride=2), :] = value[:, HALF:]


def unweave(ref):
    rows = ref.shape[0] // 2
    return ref[pl.ds(0, rows, stride=2), :], ref[pl.ds(1, rows, stride=2), :]


def whole(shape):
    return pl.BlockSpec(shape, lambda *_: (0,) * len(shape))


def round_forward(index, mesh, before, own, after, mats, bias, following):
    blocks = mesh.shape[0]
    tile, chunk = 512, 16
    turns, high = tile // chunk, 2 * chunk
    more = following is not None
    spans = [before.shape[0], own.shape[0], after.shape[0]]
    reach = sum(spans)

    def body(*refs):
        index_ref, mesh_ref, before_ref, own_ref, after_ref, mats_ref, bias_ref = refs[:7]
        next_ref, sent_ref = (refs[7], refs[13]) if more else (None, None)
        new_ref, back_ref, update_ref, agg_ref, slope_ref = refs[8:13] if more else refs[7:12]
        raw, table, rows, wide, wider, sems = refs[-6:]
        step = pl.program_id(0)

        @pl.when(step == 0)
        def _():
            copies = []
            start = 0
            for n, (source, span) in enumerate(zip((before_ref, own_ref, after_ref), spans)):
                copies.append(
                    pltpu.make_async_copy(source, raw.at[pl.ds(start, span)], sems.at[n])
                )
                start = start + span
            for copy in copies:
                copy.start()
            for copy in copies:
                copy.wait()

            @pl.loop(0, reach // 256)
            def _(i):
                at = pl.multiple_of(i * 256, 256)
                table[pl.ds(at, 256), :] = raw[pl.ds(at, 256), :].astype(jnp.float32)

        mesh_in = mesh_ref[...]
        lowered = mesh_in.astype(jnp.bfloat16)
        weave(wide, inner(lowered, mats_ref[1], 1, 0) + bias_ref[0:1, :])

        def fetch(turn):
            for edge in range(K):
                base = edge * blocks + step * tile + turn * chunk
                values = [
                    table[pl.ds(pl.multiple_of(index_ref[base + u], 2), 2), :] for u in range(chunk)
                ]
                for u in range(chunk):
                    spot = pl.multiple_of(edge * 2 * tile + turn * high + 2 * u, 2)
                    rows[pl.ds(spot, 2), :] = values[u]

        def load(turn):
            at = pl.multiple_of(turn * high, high)
            taken = [
                rows[pl.ds(pl.multiple_of(edge * 2 * tile + turn * high, high), high), :]
                for edge in range(K)
            ]
            return at, wide[pl.ds(at, high), :], taken

        def dense(at, dest, taken):
            total = None
            for edge in range(K):
                value = taken[edge] + dest
                sigma = sigmoid(value)
                out = value * sigma
                slope_ref[edge, pl.ds(at, high), :] = (sigma + out * (1.0 - sigma)).astype(
                    jnp.bfloat16
                )
                total = out if total is None else total + out
            wider[pl.ds(at, high), :] = total * (1.0 / K)

        def some(turn, carry):
            loaded = load(turn - 1)
            fetch(turn)
            dense(*loaded)
            return carry

        fetch(0)
        lax.fori_loop(1, turns, some, 0)
        dense(*load(turns - 1))
        first, second = unweave(wider)
        first, second = first.astype(jnp.bfloat16), second.astype(jnp.bfloat16)
        agg_ref[:, :HALF] = first
        agg_ref[:, HALF:] = second
        update_in = (
            inner(first, mats_ref[2, :HALF, :], 1, 0)
            + inner(second, mats_ref[2, HALF:, :], 1, 0)
            + inner(lowered, mats_ref[3], 1, 0)
            + bias_ref[1:2, :]
        )
        sigma = sigmoid(update_in)
        out = update_in * sigma
        back_ref[...] = sigma + out * (1.0 - sigma)
        update = out.astype(jnp.bfloat16)
        update_ref[...] = update
        new = mesh_in + inner(update, mats_ref[4], 1, 0)
        new_ref[...] = new
        if more:
            weave(wide, inner(new.astype(jnp.bfloat16), next_ref[...], 1, 0))
            sent_ref[...] = wide[...].astype(jnp.bfloat16)

    whole_rows = pl.BlockSpec((tile, D), lambda i, *_: (i, 0))
    woven = pl.BlockSpec((2 * tile, HALF), lambda i, *_: (i, 0))
    ins = [whole_rows] + [pl.BlockSpec(memory_space=pl.ANY)] * 3 + [whole(mats.shape), whole(bias.shape)]
    outs = [whole_rows] * 4 + [pl.BlockSpec((K, 2 * tile, HALF), lambda i, *_: (0, i, 0))]
    shapes = [
        jax.ShapeDtypeStruct((blocks, D), jnp.float32),
        jax.ShapeDtypeStruct((blocks, D), jnp.float32),
        jax.ShapeDtypeStruct((blocks, D), jnp.bfloat16),
        jax.ShapeDtypeStruct((blocks, D), jnp.bfloat16),
        jax.ShapeDtypeStruct((K, 2 * blocks, HALF), jnp.bfloat16),
    ]
    args = [index, mesh, before, own, after, mats, bias]
    if more:
        ins.append(whole(following.shape))
        outs.append(woven)
        shapes.append(jax.ShapeDtypeStruct((2 * blocks, HALF), jnp.bfloat16))
        args.append(following)
    return pl.pallas_call(
        body,
        grid_spec=pltpu.PrefetchScalarGridSpec(
            num_scalar_prefetch=1,
            grid=(blocks // tile,),
            in_specs=ins,
            out_specs=outs,
            scratch_shapes=[
                pltpu.VMEM((reach, HALF), jnp.bfloat16),
                pltpu.VMEM((reach, HALF), jnp.float32),
                pltpu.VMEM((K * 2 * tile, HALF), jnp.float32),
                pltpu.VMEM((2 * tile, HALF), jnp.float32),
                pltpu.VMEM((2 * tile, HALF), jnp.float32),
                pltpu.SemaphoreType.DMA((3,)),
            ],
        ),
        out_shape=shapes,
        compiler_params=LIMIT,
        cost_estimate=cost(25),
        name="round_forward",
    )(*args)


def edges_backward(index, grad_mesh, back, slopes, turned):
    blocks = grad_mesh.shape[0]
    tile, chunk = 512, 16
    steps, turns, high = blocks // tile, tile // chunk, 2 * chunk
    reach = 2 * (blocks + 2 * H)

    def body(
        index_ref, grad_ref, back_ref, slope_ref, turned_ref,
        guin_ref, low_ref, before_ref, own_ref, after_ref, wide, wider, flows, *tables,
    ):
        step = pl.program_id(0)

        @pl.when(step == 0)
        def _():
            @pl.loop(0, reach // 256)
            def _(i):
                for table in tables:
                    table[pl.ds(pl.multiple_of(i * 256, 256), 256), :] = jnp.zeros(
                        (256, HALF), jnp.float32
                    )

        grad_out = grad_ref[...].astype(jnp.bfloat16)
        grad_uin = (inner(grad_out, turned_ref[4], 1, 0) * back_ref[...]).astype(jnp.bfloat16)
        guin_ref[...] = grad_uin
        weave(wide, inner(grad_uin, turned_ref[2], 1, 0) * (1.0 / K))

        def dense(turn):
            at = pl.multiple_of(turn * high, high)
            grad_agg = wide[pl.ds(at, high), :]
            total, parts = None, []
            for edge in range(K):
                flow = grad_agg * slope_ref[edge, pl.ds(at, high), :].astype(jnp.float32)
                parts.append(flow)
                total = flow if total is None else total + flow
            return at, total, parts

        def keep(turn, at, total, parts):
            for edge in range(K):
                spot = pl.multiple_of(edge * 2 * tile + turn * high, high)
                flows[pl.ds(spot, high), :] = parts[edge]
            wider[pl.ds(at, high), :] = total

        def scatter(turn):
            for u in range(chunk):
                spots, sums = [], []
                for edge in range(K):
                    base = edge * blocks + step * tile + turn * chunk
                    spots.append(pl.multiple_of(index_ref[base + u], 2))
                for edge in range(K):
                    spot = pl.multiple_of(edge * 2 * tile + turn * high + 2 * u, 2)
                    sums.append(tables[edge][pl.ds(spots[edge], 2), :] + flows[pl.ds(spot, 2), :])
                for edge in range(K):
                    tables[edge][pl.ds(spots[edge], 2), :] = sums[edge]

        def some(turn, carry):
            found = dense(turn)
            scatter(turn - 1)
            keep(turn, *found)
            return carry

        keep(0, *dense(0))
        lax.fori_loop(1, turns, some, 0)
        scatter(turns - 1)
        first, second = unweave(wider)
        low_ref[:, :HALF] = first.astype(jnp.bfloat16)
        low_ref[:, HALF:] = second.astype(jnp.bfloat16)

        @pl.when(step == steps - 1)
        def _():
            def summed(at):
                value = tables[0][pl.ds(at, 256), :]
                for table in tables[1:]:
                    value = value + table[pl.ds(at, 256), :]
                return value

            @pl.loop(0, 2 * H // 256)
            def _(i):
                at = pl.multiple_of(i * 256, 256)
                far = pl.multiple_of(2 * H + 2 * blocks + at, 256)
                before_ref[pl.ds(at, 256), :] = summed(at).astype(jnp.bfloat16)
                after_ref[pl.ds(at, 256), :] = summed(far).astype(jnp.bfloat16)

            @pl.loop(0, 2 * blocks // 256)
            def _(i):
                at = pl.multiple_of(i * 256, 256)
                own_ref[pl.ds(at, 256), :] = summed(pl.multiple_of(2 * H + at, 256))

    rows = pl.BlockSpec((tile, D), lambda i, *_: (i, 0))
    return pl.pallas_call(
        body,
        grid_spec=pltpu.PrefetchScalarGridSpec(
            num_scalar_prefetch=1,
            grid=(steps,),
            in_specs=[
                rows, rows,
                pl.BlockSpec((K, 2 * tile, HALF), lambda i, *_: (0, i, 0)),
                whole(turned.shape),
            ],
            out_specs=[
                rows, rows,
                whole((2 * H, HALF)), whole((2 * blocks, HALF)), whole((2 * H, HALF)),
            ],
            scratch_shapes=[
                pltpu.VMEM((2 * tile, HALF), jnp.float32),
                pltpu.VMEM((2 * tile, HALF), jnp.float32),
                pltpu.VMEM((2 * tile * K, HALF), jnp.float32),
            ]
            + [pltpu.VMEM((reach, HALF), jnp.float32)] * K,
        ),
        out_shape=[
            jax.ShapeDtypeStruct((blocks, D), jnp.bfloat16),
            jax.ShapeDtypeStruct((blocks, D), jnp.bfloat16),
            jax.ShapeDtypeStruct((2 * H, HALF), jnp.bfloat16),
            jax.ShapeDtypeStruct((2 * blocks, HALF), jnp.float32),
            jax.ShapeDtypeStruct((2 * H, HALF), jnp.bfloat16),
        ],
        compiler_params=LIMIT,
        cost_estimate=cost(25),
        name="edges_backward",
    )(index, grad_mesh, back, slopes, turned)


def round_backward(grad_mesh, own, first, last, grad_uin, dest_low, turned):
    blocks = grad_mesh.shape[0]
    tile = 1024

    def body(
        grad_ref, own_ref, first_ref, last_ref, guin_ref, dest_ref, turned_ref, new_ref, sent_ref, wide
    ):
        wide[...] = (
            own_ref[...] + first_ref[...].astype(jnp.float32) + last_ref[...].astype(jnp.float32)
        )
        one, two = unweave(wide)
        one, two = one.astype(jnp.bfloat16), two.astype(jnp.bfloat16)
        sent_ref[:, :HALF] = one
        sent_ref[:, HALF:] = two
        new_ref[...] = (
            grad_ref[...]
            + inner(guin_ref[...], turned_ref[3], 1, 0)
            + inner(dest_ref[...], turned_ref[1], 1, 0)
            + inner(one, turned_ref[0, :HALF, :], 1, 0)
            + inner(two, turned_ref[0, HALF:, :], 1, 0)
        )

    rows = pl.BlockSpec((tile, D), lambda i: (i, 0))
    woven = pl.BlockSpec((2 * tile, HALF), lambda i: (i, 0))
    return pl.pallas_call(
        body,
        grid=(blocks // tile,),
        in_specs=[rows, woven, woven, woven, rows, rows, whole(turned.shape)],
        out_specs=[rows, rows],
        out_shape=[
            jax.ShapeDtypeStruct((blocks, D), jnp.float32),
            jax.ShapeDtypeStruct((blocks, D), jnp.bfloat16),
        ],
        scratch_shapes=[pltpu.VMEM((2 * tile, HALF), jnp.float32)],
        compiler_params=LIMIT,
        cost_estimate=cost(7),
        name="round_backward",
    )(grad_mesh, own, first, last, grad_uin, dest_low, turned)


def encode_rows(arrived, ids, w_in, w_node, biases, source):
    posts = arrived.shape[0]
    tile = 512

    def body(arrived_ref, ids_ref, in_ref, node_ref, bias_ref, source_ref, mesh_ref, gathered_ref, sent_ref, encoded, wide):
        step = pl.program_id(0)

        @pl.when(step == 0)
        def _():
            entering = inner(arrived_ref[...], in_ref[...], 1, 0) + bias_ref[0:1, :]
            encoded[...] = silu(entering).astype(jnp.bfloat16)

        nodes = lax.broadcasted_iota(jnp.int32, (tile, posts), 0) + step * tile
        chooser = jnp.where(nodes == ids_ref[...], 1.0, 0.0).astype(jnp.bfloat16)
        gathered = inner(chooser, encoded[...], 1, 0).astype(jnp.bfloat16)
        gathered_ref[...] = gathered
        mesh = silu(inner(gathered, node_ref[...], 1, 0) + bias_ref[1:2, :])
        mesh_ref[...] = mesh
        weave(wide, inner(mesh.astype(jnp.bfloat16), source_ref[...], 1, 0))
        sent_ref[...] = wide[...].astype(jnp.bfloat16)

    rows = pl.BlockSpec((tile, D), lambda i: (i, 0))
    args = (arrived, ids, w_in, w_node, biases, source)
    return pl.pallas_call(
        body,
        grid=(H // tile,),
        in_specs=[whole(arg.shape) for arg in args],
        out_specs=[rows, rows, pl.BlockSpec((2 * tile, HALF), lambda i: (i, 0))],
        out_shape=[
            jax.ShapeDtypeStruct((H, D), jnp.float32),
            jax.ShapeDtypeStruct((H, D), jnp.bfloat16),
            jax.ShapeDtypeStruct((2 * H, HALF), jnp.bfloat16),
        ],
        scratch_shapes=[pltpu.VMEM((posts, D), jnp.bfloat16), pltpu.VMEM((2 * tile, HALF), jnp.float32)],
        compiler_params=LIMIT,
        cost_estimate=cost(5),
        name="encode_rows",
    )(*args)


def encode_backward(grad_mesh, gathered, arrived, ids, w_in, w_node, biases):
    posts = arrived.shape[0]
    tile = 512
    steps = H // tile

    def body(grad_ref, gathered_ref, arrived_ref, ids_ref, in_ref, node_ref, bias_ref, gin_ref, gnode_ref, gbias_ref, total):
        step = pl.program_id(0)

        @pl.when(step == 0)
        def _():
            total[...] = jnp.zeros(total.shape, jnp.float32)
            gnode_ref[...] = jnp.zeros(gnode_ref.shape, jnp.float32)
            gbias_ref[...] = jnp.zeros(gbias_ref.shape, jnp.float32)

        node_in = inner(gathered_ref[...], node_ref[...], 1, 0) + bias_ref[1:2, :]
        grad_node = (grad_ref[...] * slope(node_in)).astype(jnp.bfloat16)
        gbias_ref[1:2, :] += jnp.sum(grad_node.astype(jnp.float32), 0, keepdims=True)
        gnode_ref[...] += inner(gathered_ref[...], grad_node, 0, 0)
        back = inner(grad_node, node_ref[...], 1, 1).astype(jnp.bfloat16)
        nodes = lax.broadcasted_iota(jnp.int32, (posts, tile), 1) + step * tile
        chooser = jnp.where(nodes == ids_ref[...], 1.0, 0.0).astype(jnp.bfloat16)
        total[...] += inner(chooser, back, 1, 0)

        @pl.when(step == steps - 1)
        def _():
            entering = inner(arrived_ref[...], in_ref[...], 1, 0) + bias_ref[0:1, :]
            grad_enc = (total[...] * slope(entering)).astype(jnp.bfloat16)
            gbias_ref[0:1, :] = jnp.sum(grad_enc.astype(jnp.float32), 0, keepdims=True)
            gin_ref[...] = inner(arrived_ref[...], grad_enc, 0, 0)

    rows = pl.BlockSpec((tile, D), lambda i: (i, 0))
    args = (grad_mesh, gathered, arrived, ids, w_in, w_node, biases)
    shapes = [(HALF, D), (D, D), (2, D)]
    return pl.pallas_call(
        body,
        grid=(steps,),
        in_specs=[rows, rows] + [whole(arg.shape) for arg in args[2:]],
        out_specs=[whole(shape) for shape in shapes],
        out_shape=[jax.ShapeDtypeStruct(shape, jnp.float32) for shape in shapes],
        scratch_shapes=[pltpu.VMEM((posts, D), jnp.float32)],
        compiler_params=LIMIT,
        cost_estimate=cost(7),
        name="encode_backward",
    )(*args)


def shards(walk, master, moment1, moment2, inputs, targets, valid, owner, slot, neighbours, partner):
    bands = lax.axis_size("space")
    band = lax.axis_index("space")
    peers = lax.axis_size(ALL)
    place = lax.axis_index(ALL)
    shard = master.shape[0]
    total_size = shard * peers
    height = pieces_of(total_size, peers)[3]
    offset = lax.rem(lax.rem(shard, D) * place, D)
    piece = lax.dynamic_update_slice_in_dim(
        jnp.zeros((height * D,), jnp.bfloat16), master.astype(jnp.bfloat16), offset, 0
    )
    state_in = inputs[0]
    counted = valid[0].astype(jnp.float32)
    local_count = jnp.sum(valid[0])
    digits = (local_count >> jnp.array([16, 8, 0], jnp.int32)) & 255
    piece = lax.dynamic_update_slice(
        piece.reshape(height, D), digits.astype(jnp.bfloat16)[None, :], (height - 1, 0)
    )
    points = state_in.shape[1]
    blocks = neighbours.shape[0]
    assert blocks == H
    capacity = max(2, 2 * points // bands)
    target_band = owner[0, :, 0]
    hits = (target_band[:, None] == jnp.arange(bands, dtype=jnp.int32)[None, :]).astype(jnp.int32)
    ranks = jnp.sum(jnp.cumsum(hits, 0) * hits, 1) - 1
    places_out = jnp.sum(hits * jnp.asarray(walk, jnp.int32)[None, :], 1) * capacity + ranks
    poster = (
        jnp.arange(bands * capacity, dtype=jnp.int32)[:, None] == places_out[None, :]
    ).astype(jnp.bfloat16)
    spots = slot[0][None, :]
    columns = jnp.concatenate(
        [
            state_in,
            (spots // 64).astype(jnp.bfloat16),
            (spots % 64).astype(jnp.bfloat16),
            jnp.ones((1, points), jnp.bfloat16),
            jnp.zeros((HALF - CH - 3, points), jnp.bfloat16),
        ],
        0,
    )

    def exchanged(rows):
        return lax.all_to_all(
            rows.reshape(bands, capacity, HALF), "space", split_axis=0, concat_axis=0, tiled=True
        ).reshape(bands * capacity, HALF)

    arrived = exchanged(inner(poster, columns, 1, 1).astype(jnp.bfloat16))
    w_in, w_node, w_dec, w_out, w_round, biases, digits = spread_rows(
        gathered_blocks(piece), total_size, peers, place
    )
    count = digits[0, 0] * 65536.0 + digits[0, 1] * 256.0 + digits[0, 2]
    w_out = jnp.pad(w_out.reshape(D, CH), ((0, 0), (0, HALF - CH)))
    w_round = w_round.reshape(ROUNDS, 5, D, D)
    b_head = biases[:3]
    b_round = biases[3:].reshape(ROUNDS, 2, D)
    ids = arrived[:, CH : CH + 3].astype(jnp.int32)
    ids = jnp.where(ids[:, 2:3] > 0, ids[:, 0:1] * 64 + ids[:, 1:2], -1)
    chooser = (ids == jnp.arange(blocks, dtype=jnp.int32)[None, :]).astype(jnp.bfloat16)
    mesh, gathered, sent = encode_rows(
        arrived, ids.reshape(1, -1), w_in, w_node, biases, w_round[0, 0]
    )
    index = 2 * ((neighbours - band * blocks + H) % (blocks * bands)).T.reshape(-1)
    moved = [(n, place) for n, place in enumerate(walk) if n != place]
    stays = jnp.asarray([n == place for n, place in enumerate(walk)])[band]
    index = jnp.where(stays, index, lax.ppermute(index, "space", moved))

    def at_home(rows):
        return lax.ppermute(rows, "space", [(j, i) for i, j in moved])

    def settled(own, came):
        return jnp.where(stays, own, came.astype(jnp.float32))

    low_valid = counted.astype(jnp.bfloat16)
    valid_around = jnp.concatenate(
        [
            shifted(low_valid[:, points - ROWW :], "space", 1),
            low_valid,
            shifted(low_valid[:, :ROWW], "space", -1),
        ],
        1,
    ).astype(jnp.float32)
    kept = []
    for layer in range(ROUNDS):
        before, after = halo(walk, sent[2 * (blocks - H) :], sent[: 2 * H])
        if layer == 0:
            before, turned = lax.optimization_barrier((before, jnp.swapaxes(w_round, 2, 3)))
        following = w_round[layer + 1, 0] if layer + 1 < ROUNDS else None
        new, back, update, agg, slopes, *rest = round_forward(
            index, mesh, before, sent, after, w_round[layer], b_round[layer], following
        )
        kept.append((mesh, back, update, agg, slopes))
        mesh = new
        sent = rest[0] if rest else None
    partner_by = partner - band * points - jnp.arange(points, dtype=jnp.int32)
    partner_by = jnp.concatenate(
        [shifted(partner_by[points - ROWW :], "space", 1), partner_by], 0
    )[None, :]
    wide_valid = valid_around
    weights = [
        (
            by,
            jnp.where(partner_by == by, 1.0, 0.0)
            * wide_valid[:, : points + ROWW]
            * wide_valid[:, by : by + points + ROWW],
        )
        for by in range(NEAR, ROWW + 1)
    ]
    fetched = inner(chooser, mesh.astype(jnp.bfloat16), 1, 0).astype(jnp.bfloat16)
    dec_in = inner(fetched, w_dec, 1, 0) + b_head[2]
    decoded = silu(dec_in).astype(jnp.bfloat16)
    returned = exchanged(inner(decoded, w_out, 1, 0).astype(jnp.bfloat16))
    branch = inner(returned, poster, 0, 0)[:CH]
    err = state_in.astype(jnp.float32) + branch - targets[0].astype(jnp.float32)
    def widened(values):
        low = values.astype(jnp.bfloat16)
        before = shifted(low[:, points - ROWW :], "space", 1).astype(jnp.float32)
        after = shifted(low[:, :ROWW], "space", -1).astype(jnp.float32)
        return jnp.concatenate([before, values, after], 1)

    wide_err = widened(err)
    paired = jnp.zeros((CH, points + ROWW), jnp.float32)
    pair_total = jnp.zeros((CH, points), jnp.float32)
    for by, both in weights:
        gap = both * (wide_err[:, : points + ROWW] - wide_err[:, by : by + points + ROWW])
        paired = paired + gap
        pair_total = pair_total + gap[:, ROWW:] * (
            wide_err[:, ROWW : ROWW + points] - wide_err[:, ROWW + by : ROWW + by + points]
        )
    local_total = jnp.sum(counted * err * err) + 0.5 * jnp.sum(pair_total)
    grad_pred = 2.0 * counted * err + paired[:, ROWW:]
    for by, both in weights:
        gap = both * (wide_err[:, : points + ROWW] - wide_err[:, by : by + points + ROWW])
        grad_pred = grad_pred - gap[:, ROWW - by : ROWW - by + points]
    grad_pred = grad_pred / count
    grad_rows = jnp.pad(grad_pred.astype(jnp.bfloat16), ((0, HALF - CH), (0, 0)))
    landed = exchanged(inner(poster, grad_rows, 1, 1).astype(jnp.bfloat16))
    grad_wout = inner(decoded, landed, 0, 0)[:, :CH]
    grad_dec = (inner(landed, w_out, 1, 1) * slope(dec_in)).astype(jnp.bfloat16)
    grad_bdec = jnp.sum(grad_dec.astype(jnp.float32), 0, keepdims=True)
    grad_wdec = inner(fetched, grad_dec, 0, 0)
    grad_fetched = inner(grad_dec, w_dec, 1, 1).astype(jnp.bfloat16)
    grad_mesh = inner(chooser, grad_fetched, 0, 0)
    grad_mesh, leaving = lax.optimization_barrier((grad_mesh, mesh.astype(jnp.bfloat16)))
    final_mesh = at_home(leaving)
    mats_grads = [None] * (5 * ROUNDS)
    bias_grads = [None] * (2 * ROUNDS)
    for layer in reversed(range(ROUNDS)):
        old, back, update, agg, slopes = kept[layer]
        grad_uin, dest_low, to_before, own, to_after = edges_backward(
            index, grad_mesh, back, slopes, turned[layer]
        )
        if layer == ROUNDS - 1:
            to_before, to_after, final_mesh = lax.optimization_barrier(
                (to_before, to_after, final_mesh)
            )
        from_before, from_after = halo(walk, to_after, to_before)
        lowered = old.astype(jnp.bfloat16)
        grad_out = grad_mesh.astype(jnp.bfloat16)
        grads = [
            None,
            inner(lowered, dest_low, 0, 0),
            inner(agg, grad_uin, 0, 0),
            inner(lowered, grad_uin, 0, 0),
            inner(update, grad_out, 0, 0),
        ]
        bias_grads[2 * layer] = jnp.sum(dest_low.astype(jnp.float32), 0, keepdims=True)
        bias_grads[2 * layer + 1] = jnp.sum(grad_uin.astype(jnp.float32), 0, keepdims=True)
        grad_mesh, sent_low = round_backward(
            grad_mesh, own, from_before, from_after, grad_uin, dest_low, turned[layer]
        )
        grads[0] = inner(lowered, sent_low, 0, 0)
        mats_grads[5 * layer : 5 * layer + 5] = grads
    third = blocks // 4 // 16 * 16
    leaving = grad_mesh.astype(jnp.bfloat16)
    early = at_home(leaving[:third])
    grad_win, grad_wnode, grad_bpair = encode_backward(
        grad_mesh, gathered, arrived, ids, w_in, w_node, biases
    )
    grad_win, grad_wnode, grad_bpair, early = lax.optimization_barrier(
        (grad_win, grad_wnode, grad_bpair, early)
    )
    middle = at_home(leaving[third : 2 * third])
    parts = [grad_win, grad_wnode, grad_wdec, grad_wout.reshape(CH, D)]
    parts = parts + mats_grads
    parts = parts + [grad_bpair, grad_bdec] + bias_grads
    keep, send = collect_rows(parts, total_size, peers, place)
    keep, send, middle = lax.optimization_barrier((keep, send, middle))
    mine, leaving = reduced_piece(keep, send, leaving[2 * third :])
    late = at_home(leaving)
    mine = lax.dynamic_slice_in_dim(mine.reshape(-1), offset, shard)
    lane = lax.broadcasted_iota(jnp.int32, (8, HALF), 1)
    sums = summed_everywhere(jnp.where(lane == 0, local_total, jnp.sum(mine * mine)))
    total, norm = sums[0, 0], jnp.sqrt(sums[0, 1])
    node_grads = settled(grad_mesh, jnp.concatenate([early, middle, late], 0))
    clipped = mine * jnp.minimum(1.0, 0.05 / norm)
    first = 0.9 * moment1 + 0.1 * clipped
    second = 0.999 * moment2 + 0.001 * clipped * clipped
    first_hat = first / (1.0 - 0.9**STEP)
    second_hat = second / (1.0 - 0.999**STEP)
    updated = master - 0.1 * (first_hat / (jnp.sqrt(second_hat) + 1e-08) + 0.1 * master)
    return (
        total.reshape(1),
        count.reshape(1),
        norm.reshape(1),
        updated,
        first,
        second,
        updated.astype(jnp.bfloat16),
        settled(mesh, final_mesh).reshape(1, blocks, D),
        node_grads.reshape(1, blocks, D),
        grad_pred.reshape(1, grad_pred.shape[0], points),
    )


def solution(mesh):
    return jax.shard_map(
        functools.partial(shards, walk_of(mesh)),
        mesh=mesh,
        in_specs=(
            P(("dp", "space")),
            P(("dp", "space")),
            P(("dp", "space")),
            P("dp", None, "space"),
            P("dp", None, "space"),
            P("dp", None, "space"),
            P("dp", "space", None),
            P("dp", "space"),
            P("space", None),
            P("space"),
        ),
        out_specs=(
            P(),
            P(),
            P(),
            P(("dp", "space")),
            P(("dp", "space")),
            P(("dp", "space")),
            P(("dp", "space")),
            P("dp", "space", None),
            P("dp", "space", None),
            P("dp", None, "space"),
        ),
        check_vma=False,
    )
```

```python
import functools

import jax
import jax.numpy as jnp
from jax import lax
from jax.experimental import pallas as pl
from jax.experimental.pallas import tpu as pltpu
from jax.sharding import PartitionSpec as P

D = 256
HALF = 128
CH = 78
ROUNDS = 3
K = 6
ROWW = 360
NEAR = 358
STEP = 10
H = 2048
ALL = ("dp", "space")
LIMIT = pltpu.CompilerParams(vmem_limit_bytes=56 * 2**20)


def cost(micros):
    return pl.CostEstimate(flops=0, bytes_accessed=micros * 3_000_000, transcendentals=0)


def inner(left, right, left_dim, right_dim):
    return lax.dot_general(
        left, right, (((left_dim,), (right_dim,)), ((), ())), preferred_element_type=jnp.float32
    )


def sigmoid(value):
    return 0.5 * jnp.tanh(0.5 * value) + 0.5


def silu(value):
    return value * sigmoid(value)


def slope(value):
    sigma = sigmoid(value)
    return sigma * (1.0 + value * (1.0 - sigma))


def shifted(shard, axis, by):
    peers = lax.axis_size(axis)
    pairs = [(i, i + by) for i in range(peers) if 0 <= i + by < peers]
    return lax.ppermute(shard, axis, pairs)


def walk_of(mesh):
    count = mesh.shape["space"]
    chips = [getattr(device, "coords", None) for device in mesh.devices[0].reshape(-1)]
    if any(chip is None for chip in chips) or len(set(map(tuple, chips))) != count:
        return list(range(count))
    at = {tuple(chip): n for n, chip in enumerate(chips)}
    xs, ys, zs = (sorted({chip[n] for chip in at}) for n in range(3))
    if len(xs) * len(ys) * len(zs) != count:
        return list(range(count))
    if (len(xs), len(ys), len(zs)) == (2, 2, 4):
        corners = [(0, 0), (1, 0), (0, 1), (1, 1)]
        planes = [(0, 1, 3, 2), (2, 0, 1, 3), (3, 1, 0, 2), (2, 3, 1, 0)]
        steps = [(*corners[n], z) for z, plane in enumerate(planes) for n in plane]
        return [at[(xs[x], ys[y], zs[z])] for x, y, z in steps]
    walk, plane = [], []
    for n, y in enumerate(ys):
        plane = plane + [(x, y) for x in (xs if n % 2 == 0 else xs[::-1])]
    for n, z in enumerate(zs):
        walk = walk + [at[(x, y, z)] for x, y in (plane if n % 2 == 0 else plane[::-1])]
    return walk


def halo(walk, last, initial):
    up = list(zip(walk, walk[1:] + walk[:1]))
    down = [(j, i) for i, j in up]
    return lax.ppermute(last, "space", up), lax.ppermute(initial, "space", down)


def pieces_of(total, peers):
    share = total // peers
    starts = [share * d // D for d in range(peers)]
    counts = [-(-share * (d + 1) // D) - starts[d] for d in range(peers)]
    shared = [share * d % D != 0 for d in range(peers)]
    height = -(-(max(counts) + 1) // 16) * 16
    return starts, counts, shared, height


def parts_of():
    return [CH, D, D, CH] + [5 * D] * ROUNDS + [3 + 2 * ROUNDS]


def swapped(value, axis, bit):
    return lax.ppermute(value, axis, [(i, i ^ bit) for i in range(lax.axis_size(axis))])


def bits_of(axis):
    return [1 << n for n in range(lax.axis_size(axis).bit_length() - 1)]


def summed_everywhere(value, arriving):
    turns = [(axis, bit) for axis in ALL for bit in bits_of(axis)]
    for turn, (axis, bit) in enumerate(turns):
        value = value + swapped(value, axis, bit)
        if turn == len(turns) - 3:
            value, arriving = lax.optimization_barrier((value, arriving))
    return value, arriving


def orders():
    bits = bits_of("space")
    return bits, bits[1:2] + bits[:1] + bits[2:]


def gathered_blocks(piece, posted):
    half = piece.shape[0] // 2
    held = [piece[None, :half], piece[None, half:]]
    last = len(orders()[0]) - 1
    for turn, bits in enumerate(reversed(list(zip(*orders())))):
        if turn == last:
            held[0], held[1], posted = lax.optimization_barrier((*held, posted))
        for n, bit in enumerate(bits):
            held[n] = jnp.concatenate([held[n], swapped(held[n], "space", bit)], 0)
    return (held, [swapped(part, "dp", 1) for part in held]), posted


def spread_rows(gathered, total, peers, place):
    (first, second), (first_far, second_far) = gathered
    starts, counts, shared, height = pieces_of(total, peers)
    half, group = height // 2, first.shape[0]
    rows = -(-total // D)
    sizes = parts_of()
    ranks = []
    for order in orders():
        ranks.append({bit: group >> (n + 1) for n, bit in enumerate(order)})

    def at(rank, relative):
        spot = 0
        for bit, weight in rank.items():
            spot = spot + jnp.where((relative & bit) != 0, weight, 0)
        return spot

    def body(place_ref, *refs):
        sources, outs, buffer = refs[:4], refs[4:-1], refs[-1]
        me = place_ref[0]
        mine = me // group
        for d in range(peers):
            relative = (me ^ d) & (group - 1)
            spots = [at(rank, relative) for rank in ranks]

            def lay(one, two, d=d, spots=spots):
                piece = jnp.concatenate([one[spots[0]], two[spots[1]]], 0).astype(jnp.float32)
                start, count = starts[d], counts[d]
                if shared[d]:
                    buffer[start : start + 1, :] = buffer[start : start + 1, :] + piece[:1]
                    buffer[start + 1 : start + count, :] = piece[1:count]
                else:
                    buffer[start : start + count, :] = piece[:count]

            @pl.when(mine == d // group)
            def _():
                lay(sources[0], sources[1])

            @pl.when(mine != d // group)
            def _():
                lay(sources[2], sources[3])

        count = jnp.zeros((1, D), jnp.float32)
        for source in (sources[1], sources[3]):
            for spot in range(group):
                count = count + source[spot, half - 1 : half, :].astype(jnp.float32)
        outs[-1][...] = count
        start = 0
        for out, size in zip(outs[:-1], sizes):
            out[:size, :] = buffer[start : start + size, :].astype(out.dtype)
            if out.shape[0] > size:
                out[size:, :] = jnp.zeros((out.shape[0] - size, D), out.dtype)
            start = start + size

    kinds = [jnp.bfloat16] * (4 + ROUNDS) + [jnp.float32]
    talls = [HALF] + sizes[1:]
    return pl.pallas_call(
        body,
        grid_spec=pltpu.PrefetchScalarGridSpec(
            num_scalar_prefetch=1,
            grid=(1,),
            in_specs=[whole(first.shape)] * 4,
            out_specs=[whole((tall, D)) for tall in talls + [1]],
            scratch_shapes=[pltpu.VMEM((-(-rows // 8) * 8 + 8, D), jnp.float32)],
        ),
        out_shape=[
            jax.ShapeDtypeStruct((tall, D), kind)
            for tall, kind in zip(talls + [1], kinds + [jnp.float32])
        ],
        compiler_params=LIMIT,
        cost_estimate=cost(4),
        name="spread_rows",
    )(place.reshape(1), first, second, first_far, second_far)


def collect_rows(parts, total, peers, place):
    starts, counts, shared, height = pieces_of(total, peers)
    rows = -(-total // D)
    sizes = [min(part.shape[0], size) for part, size in zip(parts, tall_parts())]
    group = lax.axis_size("space")

    def body(place_ref, *refs):
        sources, keep, send, buffer = refs[:-3], refs[-3], refs[-2], refs[-1]
        start = 0
        for source, size in zip(sources, sizes):
            buffer[start : start + size, :] = source[:size, :]
            start = start + size
        if buffer.shape[0] > start:
            buffer[start:, :] = jnp.zeros((buffer.shape[0] - start, D), jnp.float32)
        me = place_ref[0]
        mine = me // group
        for d in range(peers):
            relative = (me ^ d) & (group - 1)

            @pl.when(mine == d // group)
            def _():
                keep[relative] = buffer[starts[d] : starts[d] + height, :]

            @pl.when(mine != d // group)
            def _():
                send[relative] = buffer[starts[d] : starts[d] + height, :].astype(jnp.bfloat16)

    shape = (group, height, D)
    return pl.pallas_call(
        body,
        grid_spec=pltpu.PrefetchScalarGridSpec(
            num_scalar_prefetch=1,
            grid=(1,),
            in_specs=[whole(part.shape) for part in parts],
            out_specs=[whole(shape), whole(shape)],
            scratch_shapes=[pltpu.VMEM((-(-rows // 8) * 8 + height + 8, D), jnp.float32)],
        ),
        out_shape=[
            jax.ShapeDtypeStruct(shape, jnp.float32),
            jax.ShapeDtypeStruct(shape, jnp.bfloat16),
        ],
        compiler_params=LIMIT,
        cost_estimate=cost(5),
        name="collect_rows",
    )(place.reshape(1), *parts)


def reduced_piece(keep, send, leaving):
    kept = keep + swapped(send, "dp", 1).astype(jnp.float32)
    half = kept.shape[1] // 2
    names = [bits_of("space")[::-1], bits_of("space")[::-1]]
    parts = [kept[:, :half], kept[:, half:]]
    parts = [part.reshape((2,) * len(names[0]) + (half, D)) for part in parts]
    for turn, bits in enumerate(zip(*orders())):
        for n, bit in enumerate(bits):
            spot = names[n].index(bit)
            names[n].pop(spot)
            stay = lax.index_in_dim(parts[n], 0, spot, keepdims=False)
            leave = lax.index_in_dim(parts[n], 1, spot, keepdims=False)
            parts[n] = stay + swapped(leave.astype(jnp.bfloat16), "space", bit).astype(jnp.float32)
        if turn == 1:
            parts[0], parts[1], leaving = lax.optimization_barrier((*parts, leaving))
    return jnp.concatenate(parts, 0), leaving


def tall_parts():
    return [CH, D, D, CH] + [D] * (5 * ROUNDS) + [2] + [1] * (1 + 2 * ROUNDS)


def weave(ref, value):
    rows = value.shape[0]
    ref[pl.ds(0, rows, stride=2), :] = value[:, :HALF]
    ref[pl.ds(1, rows, stride=2), :] = value[:, HALF:]


def unweave(ref):
    rows = ref.shape[0] // 2
    return ref[pl.ds(0, rows, stride=2), :], ref[pl.ds(1, rows, stride=2), :]


def whole(shape):
    return pl.BlockSpec(shape, lambda *_: (0,) * len(shape))


def round_forward(index, mesh, before, own, after, mats, bias, following):
    blocks = mesh.shape[0]
    tile, chunk = 512, 16
    turns, high = tile // chunk, 2 * chunk
    more = following is not None
    spans = [before.shape[0], own.shape[0], after.shape[0]]
    reach = sum(spans)

    def body(*refs):
        index_ref, mesh_ref, before_ref, own_ref, after_ref, mats_ref, bias_ref = refs[:7]
        next_ref, sent_ref = (refs[7], refs[13]) if more else (None, None)
        new_ref, back_ref, update_ref, agg_ref, slope_ref = refs[8:13] if more else refs[7:12]
        raw, table, rows, wide, wider, sems = refs[-6:]
        step = pl.program_id(0)

        @pl.when(step == 0)
        def _():
            copies = []
            start = 0
            for n, (source, span) in enumerate(zip((before_ref, own_ref, after_ref), spans)):
                copies.append(
                    pltpu.make_async_copy(source, raw.at[pl.ds(start, span)], sems.at[n])
                )
                start = start + span
            for copy in copies:
                copy.start()
            for copy in copies:
                copy.wait()

            @pl.loop(0, reach // 256)
            def _(i):
                at = pl.multiple_of(i * 256, 256)
                table[pl.ds(at, 256), :] = raw[pl.ds(at, 256), :].astype(jnp.float32)

        mesh_in = mesh_ref[...]
        lowered = mesh_in.astype(jnp.bfloat16)
        weave(wide, inner(lowered, mats_ref[1], 1, 0) + bias_ref[0:1, :])

        def fetch(turn):
            for edge in range(K):
                base = edge * blocks + step * tile + turn * chunk
                values = [
                    table[pl.ds(pl.multiple_of(index_ref[base + u], 2), 2), :] for u in range(chunk)
                ]
                for u in range(chunk):
                    spot = pl.multiple_of(edge * 2 * tile + turn * high + 2 * u, 2)
                    rows[pl.ds(spot, 2), :] = values[u]

        def load(turn):
            at = pl.multiple_of(turn * high, high)
            taken = [
                rows[pl.ds(pl.multiple_of(edge * 2 * tile + turn * high, high), high), :]
                for edge in range(K)
            ]
            return at, wide[pl.ds(at, high), :], taken

        def dense(at, dest, taken):
            total = None
            for edge in range(K):
                value = taken[edge] + dest
                sigma = sigmoid(value)
                out = value * sigma
                slope_ref[edge, pl.ds(at, high), :] = (sigma + out * (1.0 - sigma)).astype(
                    jnp.bfloat16
                )
                total = out if total is None else total + out
            wider[pl.ds(at, high), :] = total * (1.0 / K)

        def some(turn, carry):
            loaded = load(turn - 1)
            fetch(turn)
            dense(*loaded)
            return carry

        fetch(0)
        lax.fori_loop(1, turns, some, 0)
        dense(*load(turns - 1))
        first, second = unweave(wider)
        first, second = first.astype(jnp.bfloat16), second.astype(jnp.bfloat16)
        agg_ref[:, :HALF] = first
        agg_ref[:, HALF:] = second
        update_in = (
            inner(first, mats_ref[2, :HALF, :], 1, 0)
            + inner(second, mats_ref[2, HALF:, :], 1, 0)
            + inner(lowered, mats_ref[3], 1, 0)
            + bias_ref[1:2, :]
        )
        sigma = sigmoid(update_in)
        out = update_in * sigma
        back_ref[...] = sigma + out * (1.0 - sigma)
        update = out.astype(jnp.bfloat16)
        update_ref[...] = update
        new = mesh_in + inner(update, mats_ref[4], 1, 0)
        new_ref[...] = new
        if more:
            weave(wide, inner(new.astype(jnp.bfloat16), next_ref[0], 1, 0))
            sent_ref[...] = wide[...].astype(jnp.bfloat16)

    whole_rows = pl.BlockSpec((tile, D), lambda i, *_: (i, 0))
    woven = pl.BlockSpec((2 * tile, HALF), lambda i, *_: (i, 0))
    ins = [whole_rows] + [pl.BlockSpec(memory_space=pl.ANY)] * 3 + [whole(mats.shape), whole(bias.shape)]
    outs = [whole_rows] * 4 + [pl.BlockSpec((K, 2 * tile, HALF), lambda i, *_: (0, i, 0))]
    shapes = [
        jax.ShapeDtypeStruct((blocks, D), jnp.float32),
        jax.ShapeDtypeStruct((blocks, D), jnp.float32),
        jax.ShapeDtypeStruct((blocks, D), jnp.bfloat16),
        jax.ShapeDtypeStruct((blocks, D), jnp.bfloat16),
        jax.ShapeDtypeStruct((K, 2 * blocks, HALF), jnp.bfloat16),
    ]
    args = [index, mesh, before, own, after, mats, bias]
    if more:
        ins.append(pl.BlockSpec((1, D, D), lambda *_: (0, 0, 0)))
        outs.append(woven)
        shapes.append(jax.ShapeDtypeStruct((2 * blocks, HALF), jnp.bfloat16))
        args.append(following)
    return pl.pallas_call(
        body,
        grid_spec=pltpu.PrefetchScalarGridSpec(
            num_scalar_prefetch=1,
            grid=(blocks // tile,),
            in_specs=ins,
            out_specs=outs,
            scratch_shapes=[
                pltpu.VMEM((reach, HALF), jnp.bfloat16),
                pltpu.VMEM((reach, HALF), jnp.float32),
                pltpu.VMEM((K * 2 * tile, HALF), jnp.float32),
                pltpu.VMEM((2 * tile, HALF), jnp.float32),
                pltpu.VMEM((2 * tile, HALF), jnp.float32),
                pltpu.SemaphoreType.DMA((3,)),
            ],
        ),
        out_shape=shapes,
        compiler_params=LIMIT,
        cost_estimate=cost(25),
        name="round_forward",
    )(*args)


def edges_backward(index, grad_mesh, back, slopes, turned):
    blocks = grad_mesh.shape[0]
    tile, chunk = 512, 16
    steps, turns, high = blocks // tile, tile // chunk, 2 * chunk
    reach = 2 * (blocks + 2 * H)

    def body(
        index_ref, grad_ref, back_ref, slope_ref, turned_ref,
        guin_ref, low_ref, before_ref, own_ref, after_ref, wide, wider, flows, *tables,
    ):
        step = pl.program_id(0)

        @pl.when(step == 0)
        def _():
            @pl.loop(0, reach // 256)
            def _(i):
                for table in tables:
                    table[pl.ds(pl.multiple_of(i * 256, 256), 256), :] = jnp.zeros(
                        (256, HALF), jnp.float32
                    )

        grad_out = grad_ref[...].astype(jnp.bfloat16)
        grad_uin = (inner(grad_out, turned_ref[4], 1, 0) * back_ref[...]).astype(jnp.bfloat16)
        guin_ref[...] = grad_uin
        weave(wide, inner(grad_uin, turned_ref[2], 1, 0) * (1.0 / K))

        def dense(turn):
            at = pl.multiple_of(turn * high, high)
            grad_agg = wide[pl.ds(at, high), :]
            total, parts = None, []
            for edge in range(K):
                flow = grad_agg * slope_ref[edge, pl.ds(at, high), :].astype(jnp.float32)
                parts.append(flow)
                total = flow if total is None else total + flow
            return at, total, parts

        def keep(turn, at, total, parts):
            for edge in range(K):
                spot = pl.multiple_of(edge * 2 * tile + turn * high, high)
                flows[pl.ds(spot, high), :] = parts[edge]
            wider[pl.ds(at, high), :] = total

        def scatter(turn):
            for u in range(chunk):
                spots, sums = [], []
                for edge in range(K):
                    base = edge * blocks + step * tile + turn * chunk
                    spots.append(pl.multiple_of(index_ref[base + u], 2))
                for edge in range(K):
                    spot = pl.multiple_of(edge * 2 * tile + turn * high + 2 * u, 2)
                    sums.append(tables[edge][pl.ds(spots[edge], 2), :] + flows[pl.ds(spot, 2), :])
                for edge in range(K):
                    tables[edge][pl.ds(spots[edge], 2), :] = sums[edge]

        def some(turn, carry):
            found = dense(turn)
            scatter(turn - 1)
            keep(turn, *found)
            return carry

        keep(0, *dense(0))
        lax.fori_loop(1, turns, some, 0)
        scatter(turns - 1)
        first, second = unweave(wider)
        low_ref[:, :HALF] = first.astype(jnp.bfloat16)
        low_ref[:, HALF:] = second.astype(jnp.bfloat16)

        @pl.when(step == steps - 1)
        def _():
            def summed(at):
                value = tables[0][pl.ds(at, 256), :]
                for table in tables[1:]:
                    value = value + table[pl.ds(at, 256), :]
                return value

            @pl.loop(0, 2 * H // 256)
            def _(i):
                at = pl.multiple_of(i * 256, 256)
                far = pl.multiple_of(2 * H + 2 * blocks + at, 256)
                before_ref[pl.ds(at, 256), :] = summed(at).astype(jnp.bfloat16)
                after_ref[pl.ds(at, 256), :] = summed(far).astype(jnp.bfloat16)

            @pl.loop(0, 2 * blocks // 256)
            def _(i):
                at = pl.multiple_of(i * 256, 256)
                own_ref[pl.ds(at, 256), :] = summed(pl.multiple_of(2 * H + at, 256))

    rows = pl.BlockSpec((tile, D), lambda i, *_: (i, 0))
    return pl.pallas_call(
        body,
        grid_spec=pltpu.PrefetchScalarGridSpec(
            num_scalar_prefetch=1,
            grid=(steps,),
            in_specs=[
                rows, rows,
                pl.BlockSpec((K, 2 * tile, HALF), lambda i, *_: (0, i, 0)),
                whole(turned.shape),
            ],
            out_specs=[
                rows, rows,
                whole((2 * H, HALF)), whole((2 * blocks, HALF)), whole((2 * H, HALF)),
            ],
            scratch_shapes=[
                pltpu.VMEM((2 * tile, HALF), jnp.float32),
                pltpu.VMEM((2 * tile, HALF), jnp.float32),
                pltpu.VMEM((2 * tile * K, HALF), jnp.float32),
            ]
            + [pltpu.VMEM((reach, HALF), jnp.float32)] * K,
        ),
        out_shape=[
            jax.ShapeDtypeStruct((blocks, D), jnp.bfloat16),
            jax.ShapeDtypeStruct((blocks, D), jnp.bfloat16),
            jax.ShapeDtypeStruct((2 * H, HALF), jnp.bfloat16),
            jax.ShapeDtypeStruct((2 * blocks, HALF), jnp.float32),
            jax.ShapeDtypeStruct((2 * H, HALF), jnp.bfloat16),
        ],
        compiler_params=LIMIT,
        cost_estimate=cost(25),
        name="edges_backward",
    )(index, grad_mesh, back, slopes, turned)


def round_backward(grad_mesh, own, first, last, grad_uin, dest_low, turned):
    blocks = grad_mesh.shape[0]
    tile = 1024

    def body(
        grad_ref, own_ref, first_ref, last_ref, guin_ref, dest_ref, turned_ref, new_ref, sent_ref, out_ref, wide
    ):
        wide[...] = (
            own_ref[...] + first_ref[...].astype(jnp.float32) + last_ref[...].astype(jnp.float32)
        )
        one, two = unweave(wide)
        one, two = one.astype(jnp.bfloat16), two.astype(jnp.bfloat16)
        sent_ref[:, :HALF] = one
        sent_ref[:, HALF:] = two
        new = (
            grad_ref[...]
            + inner(guin_ref[...], turned_ref[3], 1, 0)
            + inner(dest_ref[...], turned_ref[1], 1, 0)
            + inner(one, turned_ref[0, :HALF, :], 1, 0)
            + inner(two, turned_ref[0, HALF:, :], 1, 0)
        )
        new_ref[...] = new
        out_ref[...] = new.astype(jnp.bfloat16)

    rows = pl.BlockSpec((tile, D), lambda i: (i, 0))
    woven = pl.BlockSpec((2 * tile, HALF), lambda i: (i, 0))
    return pl.pallas_call(
        body,
        grid=(blocks // tile,),
        in_specs=[rows, woven, woven, woven, rows, rows, whole(turned.shape)],
        out_specs=[rows, rows, rows],
        out_shape=[
            jax.ShapeDtypeStruct((blocks, D), jnp.float32),
            jax.ShapeDtypeStruct((blocks, D), jnp.bfloat16),
            jax.ShapeDtypeStruct((blocks, D), jnp.bfloat16),
        ],
        scratch_shapes=[pltpu.VMEM((2 * tile, HALF), jnp.float32)],
        compiler_params=LIMIT,
        cost_estimate=cost(7),
        name="round_backward",
    )(grad_mesh, own, first, last, grad_uin, dest_low, turned)


def encode_rows(arrived, ids, w_in, w_node, biases, source):
    posts = arrived.shape[0]
    tile = 512

    def body(arrived_ref, ids_ref, in_ref, node_ref, bias_ref, source_ref, mesh_ref, gathered_ref, sent_ref, encoded, wide):
        step = pl.program_id(0)

        @pl.when(step == 0)
        def _():
            entering = inner(arrived_ref[...], in_ref[...], 1, 0) + bias_ref[0:1, :]
            encoded[...] = silu(entering).astype(jnp.bfloat16)

        nodes = lax.broadcasted_iota(jnp.int32, (tile, posts), 0) + step * tile
        chooser = jnp.where(nodes == ids_ref[...], 1.0, 0.0).astype(jnp.bfloat16)
        gathered = inner(chooser, encoded[...], 1, 0).astype(jnp.bfloat16)
        gathered_ref[...] = gathered
        mesh = silu(inner(gathered, node_ref[...], 1, 0) + bias_ref[1:2, :])
        mesh_ref[...] = mesh
        weave(wide, inner(mesh.astype(jnp.bfloat16), source_ref[0], 1, 0))
        sent_ref[...] = wide[...].astype(jnp.bfloat16)

    rows = pl.BlockSpec((tile, D), lambda i: (i, 0))
    args = (arrived, ids, w_in, w_node, biases, source)
    return pl.pallas_call(
        body,
        grid=(H // tile,),
        in_specs=[whole(arg.shape) for arg in args[:-1]]
        + [pl.BlockSpec((1, D, D), lambda *_: (0, 0, 0))],
        out_specs=[rows, rows, pl.BlockSpec((2 * tile, HALF), lambda i: (i, 0))],
        out_shape=[
            jax.ShapeDtypeStruct((H, D), jnp.float32),
            jax.ShapeDtypeStruct((H, D), jnp.bfloat16),
            jax.ShapeDtypeStruct((2 * H, HALF), jnp.bfloat16),
        ],
        scratch_shapes=[pltpu.VMEM((posts, D), jnp.bfloat16), pltpu.VMEM((2 * tile, HALF), jnp.float32)],
        compiler_params=LIMIT,
        cost_estimate=cost(5),
        name="encode_rows",
    )(*args)


def encode_backward(grad_mesh, gathered, arrived, ids, w_in, w_node, biases):
    posts = arrived.shape[0]
    tile = 512
    steps = H // tile

    def body(grad_ref, gathered_ref, arrived_ref, ids_ref, in_ref, node_ref, bias_ref, gin_ref, gnode_ref, gbias_ref, total):
        step = pl.program_id(0)

        @pl.when(step == 0)
        def _():
            total[...] = jnp.zeros(total.shape, jnp.float32)
            gnode_ref[...] = jnp.zeros(gnode_ref.shape, jnp.float32)
            gbias_ref[...] = jnp.zeros(gbias_ref.shape, jnp.float32)

        node_in = inner(gathered_ref[...], node_ref[...], 1, 0) + bias_ref[1:2, :]
        grad_node = (grad_ref[...] * slope(node_in)).astype(jnp.bfloat16)
        gbias_ref[1:2, :] += jnp.sum(grad_node.astype(jnp.float32), 0, keepdims=True)
        gnode_ref[...] += inner(gathered_ref[...], grad_node, 0, 0)
        back = inner(grad_node, node_ref[...], 1, 1).astype(jnp.bfloat16)
        nodes = lax.broadcasted_iota(jnp.int32, (posts, tile), 1) + step * tile
        chooser = jnp.where(nodes == ids_ref[...], 1.0, 0.0).astype(jnp.bfloat16)
        total[...] += inner(chooser, back, 1, 0)

        @pl.when(step == steps - 1)
        def _():
            entering = inner(arrived_ref[...], in_ref[...], 1, 0) + bias_ref[0:1, :]
            grad_enc = (total[...] * slope(entering)).astype(jnp.bfloat16)
            gbias_ref[0:1, :] = jnp.sum(grad_enc.astype(jnp.float32), 0, keepdims=True)
            gin_ref[...] = inner(arrived_ref[...], grad_enc, 0, 0)

    rows = pl.BlockSpec((tile, D), lambda i: (i, 0))
    args = (grad_mesh, gathered, arrived, ids, w_in, w_node, biases)
    shapes = [(HALF, D), (D, D), (2, D)]
    return pl.pallas_call(
        body,
        grid=(steps,),
        in_specs=[rows, rows] + [whole(arg.shape) for arg in args[2:]],
        out_specs=[whole(shape) for shape in shapes],
        out_shape=[jax.ShapeDtypeStruct(shape, jnp.float32) for shape in shapes],
        scratch_shapes=[pltpu.VMEM((posts, D), jnp.float32)],
        compiler_params=LIMIT,
        cost_estimate=cost(7),
        name="encode_backward",
    )(*args)


def shards(walk, master, moment1, moment2, inputs, targets, valid, owner, slot, neighbours, partner):
    bands = lax.axis_size("space")
    band = lax.axis_index("space")
    peers = lax.axis_size(ALL)
    place = lax.axis_index(ALL)
    shard = master.shape[0]
    total_size = shard * peers
    height = pieces_of(total_size, peers)[3]
    offset = lax.rem(lax.rem(shard, D) * place, D)
    piece = lax.dynamic_update_slice_in_dim(
        jnp.zeros((height * D,), jnp.bfloat16), master.astype(jnp.bfloat16), offset, 0
    )
    state_in = inputs[0]
    counted = valid[0].astype(jnp.float32)
    local_count = jnp.sum(valid[0])
    digits = (local_count >> jnp.array([16, 8, 0], jnp.int32)) & 255
    piece = lax.dynamic_update_slice(
        piece.reshape(height, D), digits.astype(jnp.bfloat16)[None, :], (height - 1, 0)
    )
    points = state_in.shape[1]
    blocks = neighbours.shape[0]
    assert blocks == H
    capacity = max(2, 2 * points // bands)
    target_band = owner[0, :, 0]
    hits = (target_band[:, None] == jnp.arange(bands, dtype=jnp.int32)[None, :]).astype(jnp.int32)
    ranks = jnp.sum(jnp.cumsum(hits, 0) * hits, 1) - 1
    places_out = jnp.sum(hits * jnp.asarray(walk, jnp.int32)[None, :], 1) * capacity + ranks
    poster = (
        jnp.arange(bands * capacity, dtype=jnp.int32)[:, None] == places_out[None, :]
    ).astype(jnp.bfloat16)
    spots = slot[0][None, :]
    columns = jnp.concatenate(
        [
            state_in,
            (spots // 64).astype(jnp.bfloat16),
            (spots % 64).astype(jnp.bfloat16),
            jnp.ones((1, points), jnp.bfloat16),
            jnp.zeros((HALF - CH - 3, points), jnp.bfloat16),
        ],
        0,
    )

    def exchanged(rows):
        return lax.all_to_all(
            rows.reshape(bands, capacity, HALF), "space", split_axis=0, concat_axis=0, tiled=True
        ).reshape(bands * capacity, HALF)

    held, posted = gathered_blocks(piece, inner(poster, columns, 1, 1).astype(jnp.bfloat16))
    arrived = exchanged(posted)
    w_in, w_node, w_dec, w_out, *w_round, biases, digits = spread_rows(
        held, total_size, peers, place
    )
    count = digits[0, 0] * 65536.0 + digits[0, 1] * 256.0 + digits[0, 2]
    w_out = jnp.pad(w_out.reshape(D, CH), ((0, 0), (0, HALF - CH)))
    w_round = [mats.reshape(5, D, D) for mats in w_round]
    b_head = biases[:3]
    b_round = biases[3:].reshape(ROUNDS, 2, D)
    ids = arrived[:, CH : CH + 3].astype(jnp.int32)
    ids = jnp.where(ids[:, 2:3] > 0, ids[:, 0:1] * 64 + ids[:, 1:2], -1)
    chooser = (ids == jnp.arange(blocks, dtype=jnp.int32)[None, :]).astype(jnp.bfloat16)
    mesh, gathered, sent = encode_rows(
        arrived, ids.reshape(1, -1), w_in, w_node, biases, w_round[0]
    )
    index = 2 * ((neighbours - band * blocks + H) % (blocks * bands)).T.reshape(-1)
    moved = [(n, place) for n, place in enumerate(walk) if n != place]
    stays = jnp.asarray([n == place for n, place in enumerate(walk)])[band]
    index = jnp.where(stays, index, lax.ppermute(index, "space", moved))

    def at_home(rows):
        return lax.ppermute(rows, "space", [(j, i) for i, j in moved])

    def settled(own, came):
        return jnp.where(stays, own, came.astype(jnp.float32))

    partner_by = partner - band * points - jnp.arange(points, dtype=jnp.int32)
    partner_by = jnp.concatenate(
        [shifted(partner_by[points - ROWW :], "space", 1), partner_by], 0
    )[None, :]
    low_valid = counted.astype(jnp.bfloat16)
    valid_around = jnp.concatenate(
        [
            shifted(low_valid[:, points - ROWW :], "space", 1),
            low_valid,
            shifted(low_valid[:, :ROWW], "space", -1),
        ],
        1,
    )
    kept = []
    for layer in range(ROUNDS):
        before, after = halo(walk, sent[2 * (blocks - H) :], sent[: 2 * H])
        if layer == 0:
            turned = [jnp.swapaxes(mats, 1, 2) for mats in w_round]
            before, turned, valid_around, partner_by = lax.optimization_barrier(
                (before, turned, valid_around, partner_by)
            )
        following = w_round[layer + 1] if layer + 1 < ROUNDS else None
        new, back, update, agg, slopes, *rest = round_forward(
            index, mesh, before, sent, after, w_round[layer], b_round[layer], following
        )
        kept.append((mesh, back, update, agg, slopes))
        mesh = new
        sent = rest[0] if rest else None
    wide_valid = valid_around.astype(jnp.float32)
    weights = [
        (
            by,
            jnp.where(partner_by == by, 1.0, 0.0)
            * wide_valid[:, : points + ROWW]
            * wide_valid[:, by : by + points + ROWW],
        )
        for by in range(NEAR, ROWW + 1)
    ]
    fetched = inner(chooser, mesh.astype(jnp.bfloat16), 1, 0).astype(jnp.bfloat16)
    dec_in = inner(fetched, w_dec, 1, 0) + b_head[2]
    decoded = silu(dec_in).astype(jnp.bfloat16)
    returned = exchanged(inner(decoded, w_out, 1, 0).astype(jnp.bfloat16))
    branch = inner(returned, poster, 0, 0)[:CH]
    err = state_in.astype(jnp.float32) + branch - targets[0].astype(jnp.float32)
    def widened(values):
        low = values.astype(jnp.bfloat16)
        before = shifted(low[:, points - ROWW :], "space", 1).astype(jnp.float32)
        after = shifted(low[:, :ROWW], "space", -1).astype(jnp.float32)
        return jnp.concatenate([before, values, after], 1)

    wide_err = widened(err)
    paired = jnp.zeros((CH, points + ROWW), jnp.float32)
    pair_total = jnp.zeros((CH, points), jnp.float32)
    for by, both in weights:
        gap = both * (wide_err[:, : points + ROWW] - wide_err[:, by : by + points + ROWW])
        paired = paired + gap
        pair_total = pair_total + gap[:, ROWW:] * (
            wide_err[:, ROWW : ROWW + points] - wide_err[:, ROWW + by : ROWW + by + points]
        )
    local_total = jnp.sum(counted * err * err) + 0.5 * jnp.sum(pair_total)
    grad_pred = 2.0 * counted * err + paired[:, ROWW:]
    for by, both in weights:
        gap = both * (wide_err[:, : points + ROWW] - wide_err[:, by : by + points + ROWW])
        grad_pred = grad_pred - gap[:, ROWW - by : ROWW - by + points]
    grad_pred = grad_pred / count
    grad_rows = jnp.pad(grad_pred.astype(jnp.bfloat16), ((0, HALF - CH), (0, 0)))
    landed = exchanged(inner(poster, grad_rows, 1, 1).astype(jnp.bfloat16))
    grad_wout = inner(decoded, landed, 0, 0)[:, :CH]
    grad_dec = (inner(landed, w_out, 1, 1) * slope(dec_in)).astype(jnp.bfloat16)
    grad_bdec = jnp.sum(grad_dec.astype(jnp.float32), 0, keepdims=True)
    grad_wdec = inner(fetched, grad_dec, 0, 0)
    grad_fetched = inner(grad_dec, w_dec, 1, 1).astype(jnp.bfloat16)
    grad_mesh = inner(chooser, grad_fetched, 0, 0)
    grad_mesh, final_mesh = lax.optimization_barrier((grad_mesh, mesh.astype(jnp.bfloat16)))
    final_mesh = at_home(final_mesh)
    leaving = grad_mesh.astype(jnp.bfloat16)
    mats_grads = [None] * (5 * ROUNDS)
    bias_grads = [None] * (2 * ROUNDS)
    for layer in reversed(range(ROUNDS)):
        old, back, update, agg, slopes = kept[layer]
        grad_uin, dest_low, to_before, own, to_after = edges_backward(
            index, grad_mesh, back, slopes, turned[layer]
        )
        if layer == ROUNDS - 1:
            to_before, to_after, final_mesh = lax.optimization_barrier(
                (to_before, to_after, final_mesh)
            )
        from_before, from_after = halo(walk, to_after, to_before)
        if layer == ROUNDS - 1:
            from_before, final_mesh = lax.optimization_barrier(
                (from_before, settled(mesh, final_mesh))
            )
        lowered = old.astype(jnp.bfloat16)
        grad_out = leaving
        grads = [
            None,
            inner(lowered, dest_low, 0, 0),
            inner(agg, grad_uin, 0, 0),
            inner(lowered, grad_uin, 0, 0),
            inner(update, grad_out, 0, 0),
        ]
        bias_grads[2 * layer] = jnp.sum(dest_low.astype(jnp.float32), 0, keepdims=True)
        bias_grads[2 * layer + 1] = jnp.sum(grad_uin.astype(jnp.float32), 0, keepdims=True)
        grad_mesh, sent_low, leaving = round_backward(
            grad_mesh, own, from_before, from_after, grad_uin, dest_low, turned[layer]
        )
        grads[0] = inner(lowered, sent_low, 0, 0)
        mats_grads[5 * layer : 5 * layer + 5] = grads
    third = blocks // 4 // 16 * 16
    early = at_home(leaving[:third])
    grad_win, grad_wnode, grad_bpair = encode_backward(
        grad_mesh, gathered, arrived, ids, w_in, w_node, biases
    )
    grad_win, grad_wnode, grad_bpair, early = lax.optimization_barrier(
        (grad_win, grad_wnode, grad_bpair, early)
    )
    middle = at_home(leaving[third : 2 * third])
    parts = [grad_win, grad_wnode, grad_wdec, grad_wout.reshape(CH, D)]
    parts = parts + mats_grads
    parts = parts + [grad_bpair, grad_bdec] + bias_grads
    keep, send = collect_rows(parts, total_size, peers, place)
    keep, send, middle = lax.optimization_barrier((keep, send, middle))
    mine, leaving = reduced_piece(keep, send, leaving[2 * third :])
    late = at_home(leaving)
    mine = lax.dynamic_slice_in_dim(mine.reshape(-1), offset, shard)
    lane = lax.broadcasted_iota(jnp.int32, (8, HALF), 1)
    sums, late = summed_everywhere(
        jnp.where(lane == 0, local_total, jnp.sum(mine * mine)), late
    )
    total, norm = sums[0, 0], jnp.sqrt(sums[0, 1])
    node_grads = settled(grad_mesh, jnp.concatenate([early, middle, late], 0))
    clipped = mine * jnp.minimum(1.0, 0.05 / norm)
    first = 0.9 * moment1 + 0.1 * clipped
    second = 0.999 * moment2 + 0.001 * clipped * clipped
    first_hat = first / (1.0 - 0.9**STEP)
    second_hat = second / (1.0 - 0.999**STEP)
    updated = master - 0.1 * (first_hat / (jnp.sqrt(second_hat) + 1e-08) + 0.1 * master)
    return (
        total.reshape(1),
        count.reshape(1),
        norm.reshape(1),
        updated,
        first,
        second,
        updated.astype(jnp.bfloat16),
        final_mesh.reshape(1, blocks, D),
        node_grads.reshape(1, blocks, D),
        grad_pred.reshape(1, grad_pred.shape[0], points),
    )


def solution(mesh):
    return jax.shard_map(
        functools.partial(shards, walk_of(mesh)),
        mesh=mesh,
        in_specs=(
            P(("dp", "space")),
            P(("dp", "space")),
            P(("dp", "space")),
            P("dp", None, "space"),
            P("dp", None, "space"),
            P("dp", None, "space"),
            P("dp", "space", None),
            P("dp", "space"),
            P("space", None),
            P("space"),
        ),
        out_specs=(
            P(),
            P(),
            P(),
            P(("dp", "space")),
            P(("dp", "space")),
            P(("dp", "space")),
            P(("dp", "space")),
            P("dp", "space", None),
            P("dp", "space", None),
            P("dp", None, "space"),
        ),
        check_vma=False,
    )
```

```python
import functools

import jax
import jax.numpy as jnp
from jax import lax
from jax.experimental import pallas as pl
from jax.experimental.pallas import tpu as pltpu
from jax.sharding import PartitionSpec as P

D = 256
HALF = 128
CH = 78
ROUNDS = 3
K = 6
ROWW = 360
NEAR = 358
STEP = 10
H = 2048
ALL = ("dp", "space")
LIMIT = pltpu.CompilerParams(vmem_limit_bytes=60 * 2**20)


def cost(micros):
    return pl.CostEstimate(flops=0, bytes_accessed=micros * 3_000_000, transcendentals=0)


def inner(left, right, left_dim, right_dim):
    return lax.dot_general(
        left, right, (((left_dim,), (right_dim,)), ((), ())), preferred_element_type=jnp.float32
    )


def sigmoid(value):
    return 0.5 * jnp.tanh(0.5 * value) + 0.5


def silu(value):
    return value * sigmoid(value)


def slope(value):
    sigma = sigmoid(value)
    return sigma * (1.0 + value * (1.0 - sigma))


def shifted(shard, axis, by):
    peers = lax.axis_size(axis)
    pairs = [(i, i + by) for i in range(peers) if 0 <= i + by < peers]
    return lax.ppermute(shard, axis, pairs)


def walk_of(mesh):
    count = mesh.shape["space"]
    chips = [getattr(device, "coords", None) for device in mesh.devices[0].reshape(-1)]
    if any(chip is None for chip in chips) or len(set(map(tuple, chips))) != count:
        return list(range(count))
    at = {tuple(chip): n for n, chip in enumerate(chips)}
    xs, ys, zs = (sorted({chip[n] for chip in at}) for n in range(3))
    if len(xs) * len(ys) * len(zs) != count:
        return list(range(count))
    if (len(xs), len(ys), len(zs)) == (2, 2, 4):
        corners = [(0, 0), (1, 0), (0, 1), (1, 1)]
        planes = [(0, 1, 3, 2), (2, 0, 1, 3), (3, 1, 0, 2), (2, 3, 1, 0)]
        steps = [(*corners[n], z) for z, plane in enumerate(planes) for n in plane]
        return [at[(xs[x], ys[y], zs[z])] for x, y, z in steps]
    walk, plane = [], []
    for n, y in enumerate(ys):
        plane = plane + [(x, y) for x in (xs if n % 2 == 0 else xs[::-1])]
    for n, z in enumerate(zs):
        walk = walk + [at[(x, y, z)] for x, y in (plane if n % 2 == 0 else plane[::-1])]
    return walk


def halo(walk, last, initial):
    up = list(zip(walk, walk[1:] + walk[:1]))
    down = [(j, i) for i, j in up]
    return lax.ppermute(last, "space", up), lax.ppermute(initial, "space", down)


def pieces_of(total, peers):
    share = total // peers
    starts = [share * d // D for d in range(peers)]
    counts = [-(-share * (d + 1) // D) - starts[d] for d in range(peers)]
    shared = [share * d % D != 0 for d in range(peers)]
    height = -(-(max(counts) + 1) // 16) * 16
    return starts, counts, shared, height


def parts_of():
    return [CH, D, D, CH] + [5 * D] * ROUNDS + [3 + 2 * ROUNDS]


def swapped(value, axis, bit):
    return lax.ppermute(value, axis, [(i, i ^ bit) for i in range(lax.axis_size(axis))])


def bits_of(axis):
    return [1 << n for n in range(lax.axis_size(axis).bit_length() - 1)]


def summed_everywhere(value, arriving):
    turns = [(axis, bit) for axis in ALL for bit in bits_of(axis)]
    for turn, (axis, bit) in enumerate(turns):
        value = value + swapped(value, axis, bit)
        if turn == len(turns) - 2:
            value, arriving = lax.optimization_barrier((value, arriving))
    return value, arriving


def orders():
    bits = bits_of("space")
    return bits, bits[1:2] + bits[:1] + bits[2:]


def gathered_blocks(piece, posted):
    half = piece.shape[0] // 2
    held = [piece[None, :half], piece[None, half:]]
    last = len(orders()[0]) - 1
    for turn, bits in enumerate(reversed(list(zip(*orders())))):
        if turn == last:
            held[0], held[1], posted = lax.optimization_barrier((*held, posted))
        for n, bit in enumerate(bits):
            held[n] = jnp.concatenate([held[n], swapped(held[n], "space", bit)], 0)
    return (held, [swapped(part, "dp", 1) for part in held]), posted


def spread_rows(gathered, total, peers, place):
    (first, second), (first_far, second_far) = gathered
    starts, counts, shared, height = pieces_of(total, peers)
    half, group = height // 2, first.shape[0]
    rows = -(-total // D)
    sizes = parts_of()
    ranks = []
    for order in orders():
        ranks.append({bit: group >> (n + 1) for n, bit in enumerate(order)})

    def at(rank, relative):
        spot = 0
        for bit, weight in rank.items():
            spot = spot + jnp.where((relative & bit) != 0, weight, 0)
        return spot

    def body(place_ref, *refs):
        sources, outs, buffer = refs[:4], refs[4:-1], refs[-1]
        me = place_ref[0]
        mine = me // group
        for d in range(peers):
            relative = (me ^ d) & (group - 1)
            spots = [at(rank, relative) for rank in ranks]

            def lay(one, two, d=d, spots=spots):
                piece = jnp.concatenate([one[spots[0]], two[spots[1]]], 0).astype(jnp.float32)
                start, count = starts[d], counts[d]
                if shared[d]:
                    buffer[start : start + 1, :] = buffer[start : start + 1, :] + piece[:1]
                    buffer[start + 1 : start + count, :] = piece[1:count]
                else:
                    buffer[start : start + count, :] = piece[:count]

            @pl.when(mine == d // group)
            def _():
                lay(sources[0], sources[1])

            @pl.when(mine != d // group)
            def _():
                lay(sources[2], sources[3])

        count = jnp.zeros((1, D), jnp.float32)
        for source in (sources[1], sources[3]):
            for spot in range(group):
                count = count + source[spot, half - 1 : half, :].astype(jnp.float32)
        outs[-1][...] = count
        start = 0
        for out, size in zip(outs[:-1], sizes):
            out[:size, :] = buffer[start : start + size, :].astype(out.dtype)
            if out.shape[0] > size:
                out[size:, :] = jnp.zeros((out.shape[0] - size, D), out.dtype)
            start = start + size

    kinds = [jnp.bfloat16] * (4 + ROUNDS) + [jnp.float32]
    talls = [HALF] + sizes[1:]
    return pl.pallas_call(
        body,
        grid_spec=pltpu.PrefetchScalarGridSpec(
            num_scalar_prefetch=1,
            grid=(1,),
            in_specs=[whole(first.shape)] * 4,
            out_specs=[whole((tall, D)) for tall in talls + [1]],
            scratch_shapes=[pltpu.VMEM((-(-rows // 8) * 8 + 8, D), jnp.float32)],
        ),
        out_shape=[
            jax.ShapeDtypeStruct((tall, D), kind)
            for tall, kind in zip(talls + [1], kinds + [jnp.float32])
        ],
        compiler_params=LIMIT,
        cost_estimate=cost(4),
        name="spread_rows",
    )(place.reshape(1), first, second, first_far, second_far)


def collect_rows(parts, total, peers, place):
    starts, counts, shared, height = pieces_of(total, peers)
    rows = -(-total // D)
    sizes = [min(part.shape[0], size) for part, size in zip(parts, tall_parts())]
    group = lax.axis_size("space")

    def body(place_ref, *refs):
        sources, keep, send, buffer = refs[:-3], refs[-3], refs[-2], refs[-1]
        start = 0
        for source, size in zip(sources, sizes):
            buffer[start : start + size, :] = source[:size, :]
            start = start + size
        if buffer.shape[0] > start:
            buffer[start:, :] = jnp.zeros((buffer.shape[0] - start, D), jnp.float32)
        me = place_ref[0]
        mine = me // group
        for d in range(peers):
            relative = (me ^ d) & (group - 1)

            @pl.when(mine == d // group)
            def _():
                keep[relative] = buffer[starts[d] : starts[d] + height, :]

            @pl.when(mine != d // group)
            def _():
                send[relative] = buffer[starts[d] : starts[d] + height, :].astype(jnp.bfloat16)

    shape = (group, height, D)
    return pl.pallas_call(
        body,
        grid_spec=pltpu.PrefetchScalarGridSpec(
            num_scalar_prefetch=1,
            grid=(1,),
            in_specs=[whole(part.shape) for part in parts],
            out_specs=[whole(shape), whole(shape)],
            scratch_shapes=[pltpu.VMEM((-(-rows // 8) * 8 + height + 8, D), jnp.float32)],
        ),
        out_shape=[
            jax.ShapeDtypeStruct(shape, jnp.float32),
            jax.ShapeDtypeStruct(shape, jnp.bfloat16),
        ],
        compiler_params=LIMIT,
        cost_estimate=cost(5),
        name="collect_rows",
    )(place.reshape(1), *parts)


def reduced_piece(keep, send, leaving):
    kept = keep + swapped(send, "dp", 1).astype(jnp.float32)
    half = kept.shape[1] // 2
    names = [bits_of("space")[::-1], bits_of("space")[::-1]]
    parts = [kept[:, :half], kept[:, half:]]
    parts = [part.reshape((2,) * len(names[0]) + (half, D)) for part in parts]
    for turn, bits in enumerate(zip(*orders())):
        for n, bit in enumerate(bits):
            spot = names[n].index(bit)
            names[n].pop(spot)
            stay = lax.index_in_dim(parts[n], 0, spot, keepdims=False)
            leave = lax.index_in_dim(parts[n], 1, spot, keepdims=False)
            parts[n] = stay + swapped(leave.astype(jnp.bfloat16), "space", bit).astype(jnp.float32)
        if turn == 1:
            parts[0], parts[1], leaving = lax.optimization_barrier((*parts, leaving))
    return jnp.concatenate(parts, 0), leaving


def tall_parts():
    return [CH, D, D, CH] + [D] * (5 * ROUNDS) + [2] + [1] * (1 + 2 * ROUNDS)


def weave(ref, value):
    rows = value.shape[0]
    ref[pl.ds(0, rows, stride=2), :] = value[:, :HALF]
    ref[pl.ds(1, rows, stride=2), :] = value[:, HALF:]


def unweave(ref):
    rows = ref.shape[0] // 2
    return ref[pl.ds(0, rows, stride=2), :], ref[pl.ds(1, rows, stride=2), :]


def whole(shape):
    return pl.BlockSpec(shape, lambda *_: (0,) * len(shape))


def index_block(tile):
    return pl.BlockSpec((K, tile), lambda i: (0, i), memory_space=pltpu.SMEM)


def round_forward(index, mesh, before, own, after, mats, bias, following):
    blocks = mesh.shape[0]
    tile, chunk = 512, 16
    turns, high = tile // chunk, 2 * chunk
    more = following is not None
    spans = [before.shape[0], own.shape[0], after.shape[0]]
    reach = sum(spans)

    def body(*refs):
        index_ref, mesh_ref, before_ref, own_ref, after_ref, mats_ref, bias_ref = refs[:7]
        next_ref, sent_ref = (refs[7], refs[13]) if more else (None, None)
        new_ref, back_ref, update_ref, agg_ref, slope_ref = refs[8:13] if more else refs[7:12]
        raw, table, rows, wide, wider, sems = refs[-6:]
        step = pl.program_id(0)

        @pl.when(step == 0)
        def _():
            copies = []
            start = 0
            for n, (source, span) in enumerate(zip((before_ref, own_ref, after_ref), spans)):
                copies.append(
                    pltpu.make_async_copy(source, raw.at[pl.ds(start, span)], sems.at[n])
                )
                start = start + span
            for copy in copies:
                copy.start()
            for copy in copies:
                copy.wait()

            @pl.loop(0, reach // 256)
            def _(i):
                at = pl.multiple_of(i * 256, 256)
                table[pl.ds(at, 256), :] = raw[pl.ds(at, 256), :].astype(jnp.float32)

        mesh_in = mesh_ref[...]
        lowered = mesh_in.astype(jnp.bfloat16)
        weave(wide, inner(lowered, mats_ref[1], 1, 0) + bias_ref[0:1, :])

        def fetch(turn):
            for edge in range(K):
                spots = [index_ref[edge, turn * chunk + u] for u in range(chunk)]
                values = [table[pl.ds(pl.multiple_of(spot, 2), 2), :] for spot in spots]
                for u in range(chunk):
                    spot = pl.multiple_of(edge * 2 * tile + turn * high + 2 * u, 2)
                    rows[pl.ds(spot, 2), :] = values[u]

        def load(turn):
            at = pl.multiple_of(turn * high, high)
            taken = [
                rows[pl.ds(pl.multiple_of(edge * 2 * tile + turn * high, high), high), :]
                for edge in range(K)
            ]
            return at, wide[pl.ds(at, high), :], taken

        def dense(at, dest, taken):
            total = None
            for edge in range(K):
                value = taken[edge] + dest
                sigma = sigmoid(value)
                out = value * sigma
                slope_ref[edge, pl.ds(at, high), :] = (sigma + out * (1.0 - sigma)).astype(
                    jnp.bfloat16
                )
                total = out if total is None else total + out
            wider[pl.ds(at, high), :] = total * (1.0 / K)

        def some(turn, carry):
            loaded = load(turn - 1)
            fetch(turn)
            dense(*loaded)
            return carry

        fetch(0)
        lax.fori_loop(1, turns, some, 0)
        dense(*load(turns - 1))
        first, second = unweave(wider)
        first, second = first.astype(jnp.bfloat16), second.astype(jnp.bfloat16)
        agg_ref[:, :HALF] = first
        agg_ref[:, HALF:] = second
        update_in = (
            inner(first, mats_ref[2, :HALF, :], 1, 0)
            + inner(second, mats_ref[2, HALF:, :], 1, 0)
            + inner(lowered, mats_ref[3], 1, 0)
            + bias_ref[1:2, :]
        )
        sigma = sigmoid(update_in)
        out = update_in * sigma
        back_ref[...] = sigma + out * (1.0 - sigma)
        update = out.astype(jnp.bfloat16)
        update_ref[...] = update
        new = mesh_in + inner(update, mats_ref[4], 1, 0)
        new_ref[...] = new
        if more:
            weave(wide, inner(new.astype(jnp.bfloat16), next_ref[0], 1, 0))
            sent_ref[...] = wide[...].astype(jnp.bfloat16)

    whole_rows = pl.BlockSpec((tile, D), lambda i: (i, 0))
    woven = pl.BlockSpec((2 * tile, HALF), lambda i: (i, 0))
    ins = [index_block(tile), whole_rows] + [pl.BlockSpec(memory_space=pl.ANY)] * 3 + [whole(mats.shape), whole(bias.shape)]
    outs = [whole_rows] * 4 + [pl.BlockSpec((K, 2 * tile, HALF), lambda i, *_: (0, i, 0))]
    shapes = [
        jax.ShapeDtypeStruct((blocks, D), jnp.float32),
        jax.ShapeDtypeStruct((blocks, D), jnp.float32),
        jax.ShapeDtypeStruct((blocks, D), jnp.bfloat16),
        jax.ShapeDtypeStruct((blocks, D), jnp.bfloat16),
        jax.ShapeDtypeStruct((K, 2 * blocks, HALF), jnp.bfloat16),
    ]
    args = [index, mesh, before, own, after, mats, bias]
    if more:
        ins.append(pl.BlockSpec((1, D, D), lambda *_: (0, 0, 0)))
        outs.append(woven)
        shapes.append(jax.ShapeDtypeStruct((2 * blocks, HALF), jnp.bfloat16))
        args.append(following)
    return pl.pallas_call(
        body,
        grid_spec=pl.GridSpec(
            grid=(blocks // tile,),
            in_specs=ins,
            out_specs=outs,
            scratch_shapes=[
                pltpu.VMEM((reach, HALF), jnp.bfloat16),
                pltpu.VMEM((reach, HALF), jnp.float32),
                pltpu.VMEM((K * 2 * tile, HALF), jnp.float32),
                pltpu.VMEM((2 * tile, HALF), jnp.float32),
                pltpu.VMEM((2 * tile, HALF), jnp.float32),
                pltpu.SemaphoreType.DMA((3,)),
            ],
        ),
        out_shape=shapes,
        compiler_params=LIMIT,
        cost_estimate=cost(25),
        name="round_forward",
    )(*args)


def edges_backward(index, grad_mesh, back, slopes, mats, carried=()):
    blocks = grad_mesh.shape[0]
    tile, chunk = 512, 16
    steps, turns, high = blocks // tile, tile // chunk, 2 * chunk
    reach = 2 * (blocks + 2 * H)

    def body(*refs):
        index_ref, grad_ref, back_ref, slope_ref, mats_ref = refs[:5]
        rest = refs[5:]
        if carried:
            past, rest = rest[:6], rest[6:]
            (new_ref, out_ref, sent_ref), rest = rest[:3], rest[3:]
        guin_ref, low_ref, before_ref, own_ref, after_ref, wide, wider, flows, *tables = rest
        step = pl.program_id(0)

        @pl.when(step == 0)
        def _():
            @pl.loop(0, reach // 256)
            def _(i):
                for table in tables:
                    table[pl.ds(pl.multiple_of(i * 256, 256), 256), :] = jnp.zeros(
                        (256, HALF), jnp.float32
                    )

        if carried:
            new = ended(grad_ref, *past, sent_ref, wide)
            new_ref[...] = new
            grad_out = new.astype(jnp.bfloat16)
            out_ref[...] = grad_out
        else:
            grad_out = grad_ref[...].astype(jnp.bfloat16)
        grad_uin = (inner(grad_out, mats_ref[4], 1, 1) * back_ref[...]).astype(jnp.bfloat16)
        guin_ref[...] = grad_uin
        weave(wide, inner(grad_uin, mats_ref[2], 1, 1) * (1.0 / K))

        def dense(turn):
            at = pl.multiple_of(turn * high, high)
            grad_agg = wide[pl.ds(at, high), :]
            total, parts = None, []
            for edge in range(K):
                flow = grad_agg * slope_ref[edge, pl.ds(at, high), :].astype(jnp.float32)
                parts.append(flow)
                total = flow if total is None else total + flow
            return at, total, parts

        def keep(turn, at, total, parts):
            for edge in range(K):
                spot = pl.multiple_of(edge * 2 * tile + turn * high, high)
                flows[pl.ds(spot, high), :] = parts[edge]
            wider[pl.ds(at, high), :] = total

        def scatter(turn):
            for u in range(chunk):
                spots, sums = [], []
                for edge in range(K):
                    spots.append(pl.multiple_of(index_ref[edge, turn * chunk + u], 2))
                for edge in range(K):
                    spot = pl.multiple_of(edge * 2 * tile + turn * high + 2 * u, 2)
                    sums.append(tables[edge][pl.ds(spots[edge], 2), :] + flows[pl.ds(spot, 2), :])
                for edge in range(K):
                    tables[edge][pl.ds(spots[edge], 2), :] = sums[edge]

        def some(turn, carry):
            found = dense(turn)
            scatter(turn - 1)
            keep(turn, *found)
            return carry

        keep(0, *dense(0))
        lax.fori_loop(1, turns, some, 0)
        scatter(turns - 1)
        first, second = unweave(wider)
        low_ref[:, :HALF] = first.astype(jnp.bfloat16)
        low_ref[:, HALF:] = second.astype(jnp.bfloat16)

        @pl.when(step == steps - 1)
        def _():
            def summed(at):
                value = tables[0][pl.ds(at, 256), :]
                for table in tables[1:]:
                    value = value + table[pl.ds(at, 256), :]
                return value

            @pl.loop(0, 2 * H // 256)
            def _(i):
                at = pl.multiple_of(i * 256, 256)
                far = pl.multiple_of(2 * H + 2 * blocks + at, 256)
                before_ref[pl.ds(at, 256), :] = summed(at).astype(jnp.bfloat16)
                after_ref[pl.ds(at, 256), :] = summed(far).astype(jnp.bfloat16)

            @pl.loop(0, 2 * blocks // 256)
            def _(i):
                at = pl.multiple_of(i * 256, 256)
                own_ref[pl.ds(at, 256), :] = summed(pl.multiple_of(2 * H + at, 256))

    rows = pl.BlockSpec((tile, D), lambda i: (i, 0))
    woven = pl.BlockSpec((2 * tile, HALF), lambda i: (i, 0))
    low = jax.ShapeDtypeStruct((blocks, D), jnp.bfloat16)
    return pl.pallas_call(
        body,
        grid_spec=pl.GridSpec(
            grid=(steps,),
            in_specs=[
                index_block(tile), rows, rows,
                pl.BlockSpec((K, 2 * tile, HALF), lambda i: (0, i, 0)),
                whole(mats.shape),
            ]
            + ([woven] * 3 + [rows] * 2 + [whole(mats.shape)] if carried else []),
            out_specs=([rows] * 3 if carried else []) + [
                rows, rows,
                whole((2 * H, HALF)), whole((2 * blocks, HALF)), whole((2 * H, HALF)),
            ],
            scratch_shapes=[
                pltpu.VMEM((2 * tile, HALF), jnp.float32),
                pltpu.VMEM((2 * tile, HALF), jnp.float32),
                pltpu.VMEM((2 * tile * K, HALF), jnp.float32),
            ]
            + [pltpu.VMEM((reach, HALF), jnp.float32)] * K,
        ),
        out_shape=(
            [jax.ShapeDtypeStruct((blocks, D), jnp.float32), low, low] if carried else []
        ) + [
            low,
            low,
            jax.ShapeDtypeStruct((2 * H, HALF), jnp.bfloat16),
            jax.ShapeDtypeStruct((2 * blocks, HALF), jnp.float32),
            jax.ShapeDtypeStruct((2 * H, HALF), jnp.bfloat16),
        ],
        compiler_params=LIMIT,
        cost_estimate=cost(28 if carried else 25),
        name="edges_backward",
    )(index, grad_mesh, back, slopes, mats, *carried)


def ended(grad_ref, own_ref, first_ref, last_ref, guin_ref, dest_ref, mats_ref, sent_ref, wide):
    wide[...] = (
        own_ref[...] + first_ref[...].astype(jnp.float32) + last_ref[...].astype(jnp.float32)
    )
    one, two = unweave(wide)
    one, two = one.astype(jnp.bfloat16), two.astype(jnp.bfloat16)
    sent_ref[:, :HALF] = one
    sent_ref[:, HALF:] = two
    return (
        grad_ref[...]
        + inner(guin_ref[...], mats_ref[3], 1, 1)
        + inner(dest_ref[...], mats_ref[1], 1, 1)
        + inner(one, mats_ref[0, :, :HALF], 1, 1)
        + inner(two, mats_ref[0, :, HALF:], 1, 1)
    )


def round_backward(grad_mesh, own, first, last, grad_uin, dest_low, mats):
    blocks = grad_mesh.shape[0]
    tile = 1024

    def body(*refs):
        new_ref, out_ref, sent_ref, wide = refs[-4:]
        new = ended(*refs[:-4], sent_ref, wide)
        new_ref[...] = new
        out_ref[...] = new.astype(jnp.bfloat16)

    rows = pl.BlockSpec((tile, D), lambda i: (i, 0))
    woven = pl.BlockSpec((2 * tile, HALF), lambda i: (i, 0))
    low = jax.ShapeDtypeStruct((blocks, D), jnp.bfloat16)
    return pl.pallas_call(
        body,
        grid=(blocks // tile,),
        in_specs=[rows, woven, woven, woven, rows, rows, whole(mats.shape)],
        out_specs=[rows, rows, rows],
        out_shape=[jax.ShapeDtypeStruct((blocks, D), jnp.float32), low, low],
        scratch_shapes=[pltpu.VMEM((2 * tile, HALF), jnp.float32)],
        compiler_params=LIMIT,
        cost_estimate=cost(7),
        name="round_backward",
    )(grad_mesh, own, first, last, grad_uin, dest_low, mats)


def encode_rows(arrived, ids, w_in, w_node, biases, source):
    posts = arrived.shape[0]
    tile = 512

    def body(arrived_ref, ids_ref, in_ref, node_ref, bias_ref, source_ref, mesh_ref, gathered_ref, sent_ref, encoded, wide):
        step = pl.program_id(0)

        @pl.when(step == 0)
        def _():
            entering = inner(arrived_ref[...], in_ref[...], 1, 0) + bias_ref[0:1, :]
            encoded[...] = silu(entering).astype(jnp.bfloat16)

        nodes = lax.broadcasted_iota(jnp.int32, (tile, posts), 0) + step * tile
        chooser = jnp.where(nodes == ids_ref[...], 1.0, 0.0).astype(jnp.bfloat16)
        gathered = inner(chooser, encoded[...], 1, 0).astype(jnp.bfloat16)
        gathered_ref[...] = gathered
        mesh = silu(inner(gathered, node_ref[...], 1, 0) + bias_ref[1:2, :])
        mesh_ref[...] = mesh
        weave(wide, inner(mesh.astype(jnp.bfloat16), source_ref[0], 1, 0))
        sent_ref[...] = wide[...].astype(jnp.bfloat16)

    rows = pl.BlockSpec((tile, D), lambda i: (i, 0))
    args = (arrived, ids, w_in, w_node, biases, source)
    return pl.pallas_call(
        body,
        grid=(H // tile,),
        in_specs=[whole(arg.shape) for arg in args[:-1]]
        + [pl.BlockSpec((1, D, D), lambda *_: (0, 0, 0))],
        out_specs=[rows, rows, pl.BlockSpec((2 * tile, HALF), lambda i: (i, 0))],
        out_shape=[
            jax.ShapeDtypeStruct((H, D), jnp.float32),
            jax.ShapeDtypeStruct((H, D), jnp.bfloat16),
            jax.ShapeDtypeStruct((2 * H, HALF), jnp.bfloat16),
        ],
        scratch_shapes=[pltpu.VMEM((posts, D), jnp.bfloat16), pltpu.VMEM((2 * tile, HALF), jnp.float32)],
        compiler_params=LIMIT,
        cost_estimate=cost(5),
        name="encode_rows",
    )(*args)


def encode_backward(grad_mesh, gathered, arrived, ids, w_in, w_node, biases):
    posts = arrived.shape[0]
    tile = 512
    steps = H // tile

    def body(grad_ref, gathered_ref, arrived_ref, ids_ref, in_ref, node_ref, bias_ref, gin_ref, gnode_ref, gbias_ref, total):
        step = pl.program_id(0)

        @pl.when(step == 0)
        def _():
            total[...] = jnp.zeros(total.shape, jnp.float32)
            gnode_ref[...] = jnp.zeros(gnode_ref.shape, jnp.float32)
            gbias_ref[...] = jnp.zeros(gbias_ref.shape, jnp.float32)

        node_in = inner(gathered_ref[...], node_ref[...], 1, 0) + bias_ref[1:2, :]
        grad_node = (grad_ref[...] * slope(node_in)).astype(jnp.bfloat16)
        gbias_ref[1:2, :] += jnp.sum(grad_node.astype(jnp.float32), 0, keepdims=True)
        gnode_ref[...] += inner(gathered_ref[...], grad_node, 0, 0)
        back = inner(grad_node, node_ref[...], 1, 1).astype(jnp.bfloat16)
        nodes = lax.broadcasted_iota(jnp.int32, (posts, tile), 1) + step * tile
        chooser = jnp.where(nodes == ids_ref[...], 1.0, 0.0).astype(jnp.bfloat16)
        total[...] += inner(chooser, back, 1, 0)

        @pl.when(step == steps - 1)
        def _():
            entering = inner(arrived_ref[...], in_ref[...], 1, 0) + bias_ref[0:1, :]
            grad_enc = (total[...] * slope(entering)).astype(jnp.bfloat16)
            gbias_ref[0:1, :] = jnp.sum(grad_enc.astype(jnp.float32), 0, keepdims=True)
            gin_ref[...] = inner(arrived_ref[...], grad_enc, 0, 0)

    rows = pl.BlockSpec((tile, D), lambda i: (i, 0))
    args = (grad_mesh, gathered, arrived, ids, w_in, w_node, biases)
    shapes = [(HALF, D), (D, D), (2, D)]
    return pl.pallas_call(
        body,
        grid=(steps,),
        in_specs=[rows, rows] + [whole(arg.shape) for arg in args[2:]],
        out_specs=[whole(shape) for shape in shapes],
        out_shape=[jax.ShapeDtypeStruct(shape, jnp.float32) for shape in shapes],
        scratch_shapes=[pltpu.VMEM((posts, D), jnp.float32)],
        compiler_params=LIMIT,
        cost_estimate=cost(7),
        name="encode_backward",
    )(*args)


def shards(walk, master, moment1, moment2, inputs, targets, valid, owner, slot, neighbours, partner):
    bands = lax.axis_size("space")
    band = lax.axis_index("space")
    peers = lax.axis_size(ALL)
    place = lax.axis_index(ALL)
    shard = master.shape[0]
    total_size = shard * peers
    height = pieces_of(total_size, peers)[3]
    offset = lax.rem(lax.rem(shard, D) * place, D)
    piece = lax.dynamic_update_slice_in_dim(
        jnp.zeros((height * D,), jnp.bfloat16), master.astype(jnp.bfloat16), offset, 0
    )
    state_in = inputs[0]
    counted = valid[0].astype(jnp.float32)
    local_count = jnp.sum(valid[0])
    digits = (local_count >> jnp.array([16, 8, 0], jnp.int32)) & 255
    piece = lax.dynamic_update_slice(
        piece.reshape(height, D), digits.astype(jnp.bfloat16)[None, :], (height - 1, 0)
    )
    points = state_in.shape[1]
    blocks = neighbours.shape[0]
    assert blocks == H
    capacity = max(2, 2 * points // bands)
    target_band = owner[0, :, 0]
    hits = (target_band[:, None] == jnp.arange(bands, dtype=jnp.int32)[None, :]).astype(jnp.int32)
    ranks = jnp.sum(jnp.cumsum(hits, 0) * hits, 1) - 1
    places_out = jnp.sum(hits * jnp.asarray(walk, jnp.int32)[None, :], 1) * capacity + ranks
    poster = (
        jnp.arange(bands * capacity, dtype=jnp.int32)[:, None] == places_out[None, :]
    ).astype(jnp.bfloat16)
    spots = slot[0][None, :]
    columns = jnp.concatenate(
        [
            state_in,
            (spots // 64).astype(jnp.bfloat16),
            (spots % 64).astype(jnp.bfloat16),
            jnp.ones((1, points), jnp.bfloat16),
            jnp.zeros((HALF - CH - 3, points), jnp.bfloat16),
        ],
        0,
    )

    def exchanged(rows):
        return lax.all_to_all(
            rows.reshape(bands, capacity, HALF), "space", split_axis=0, concat_axis=0, tiled=True
        ).reshape(bands * capacity, HALF)

    held, posted = gathered_blocks(piece, inner(poster, columns, 1, 1).astype(jnp.bfloat16))
    arrived = exchanged(posted)
    w_in, w_node, w_dec, w_out, *w_round, biases, digits = spread_rows(
        held, total_size, peers, place
    )
    count = digits[0, 0] * 65536.0 + digits[0, 1] * 256.0 + digits[0, 2]
    w_out = jnp.pad(w_out.reshape(D, CH), ((0, 0), (0, HALF - CH)))
    w_round = [mats.reshape(5, D, D) for mats in w_round]
    b_head = biases[:3]
    b_round = biases[3:].reshape(ROUNDS, 2, D)
    ids = arrived[:, CH : CH + 3].astype(jnp.int32)
    ids = jnp.where(ids[:, 2:3] > 0, ids[:, 0:1] * 64 + ids[:, 1:2], -1)
    chooser = (ids == jnp.arange(blocks, dtype=jnp.int32)[None, :]).astype(jnp.bfloat16)
    mesh, gathered, sent = encode_rows(
        arrived, ids.reshape(1, -1), w_in, w_node, biases, w_round[0]
    )
    sent, partner, neighbours, counted = lax.optimization_barrier(
        (sent, partner, neighbours, counted)
    )
    index = 2 * ((neighbours - band * blocks + H) % (blocks * bands)).T
    moved = [(n, place) for n, place in enumerate(walk) if n != place]
    stays = jnp.asarray([n == place for n, place in enumerate(walk)])[band]
    index = jnp.where(stays, index, lax.ppermute(index, "space", moved))

    def at_home(rows):
        return lax.ppermute(rows, "space", [(j, i) for i, j in moved])

    def settled(own, came):
        return jnp.where(stays, own, came.astype(jnp.float32))

    partner_by = partner - band * points - jnp.arange(points, dtype=jnp.int32)
    partner_by = jnp.concatenate(
        [shifted(partner_by[points - ROWW :], "space", 1), partner_by], 0
    )[None, :]
    low_valid = counted.astype(jnp.bfloat16)
    valid_around = jnp.concatenate(
        [
            shifted(low_valid[:, points - ROWW :], "space", 1),
            low_valid,
            shifted(low_valid[:, :ROWW], "space", -1),
        ],
        1,
    )
    kept = []
    for layer in range(ROUNDS):
        before, after = halo(walk, sent[2 * (blocks - H) :], sent[: 2 * H])
        if layer == 0:
            before, valid_around, partner_by = lax.optimization_barrier(
                (before, valid_around, partner_by)
            )
        following = w_round[layer + 1] if layer + 1 < ROUNDS else None
        new, back, update, agg, slopes, *rest = round_forward(
            index, mesh, before, sent, after, w_round[layer], b_round[layer], following
        )
        kept.append((mesh, back, update, agg, slopes))
        mesh = new
        sent = rest[0] if rest else None
    wide_valid = valid_around.astype(jnp.float32)
    weights = [
        (
            by,
            jnp.where(partner_by == by, 1.0, 0.0)
            * wide_valid[:, : points + ROWW]
            * wide_valid[:, by : by + points + ROWW],
        )
        for by in range(NEAR, ROWW + 1)
    ]
    fetched = inner(chooser, mesh.astype(jnp.bfloat16), 1, 0).astype(jnp.bfloat16)
    dec_in = inner(fetched, w_dec, 1, 0) + b_head[2]
    decoded = silu(dec_in).astype(jnp.bfloat16)
    returned = exchanged(inner(decoded, w_out, 1, 0).astype(jnp.bfloat16))
    branch = inner(returned, poster, 0, 0)[:CH]
    err = state_in.astype(jnp.float32) + branch - targets[0].astype(jnp.float32)
    def widened(values):
        low = values.astype(jnp.bfloat16)
        before = shifted(low[:, points - ROWW :], "space", 1).astype(jnp.float32)
        after = shifted(low[:, :ROWW], "space", -1).astype(jnp.float32)
        return jnp.concatenate([before, values, after], 1)

    wide_err = widened(err)
    paired = jnp.zeros((CH, points + ROWW), jnp.float32)
    pair_total = jnp.zeros((CH, points), jnp.float32)
    for by, both in weights:
        gap = both * (wide_err[:, : points + ROWW] - wide_err[:, by : by + points + ROWW])
        paired = paired + gap
        pair_total = pair_total + gap[:, ROWW:] * (
            wide_err[:, ROWW : ROWW + points] - wide_err[:, ROWW + by : ROWW + by + points]
        )
    local_total = jnp.sum(counted * err * err) + 0.5 * jnp.sum(pair_total)
    grad_pred = 2.0 * counted * err + paired[:, ROWW:]
    for by, both in weights:
        gap = both * (wide_err[:, : points + ROWW] - wide_err[:, by : by + points + ROWW])
        grad_pred = grad_pred - gap[:, ROWW - by : ROWW - by + points]
    grad_pred = grad_pred / count
    grad_rows = jnp.pad(grad_pred.astype(jnp.bfloat16), ((0, HALF - CH), (0, 0)))
    landed = exchanged(inner(poster, grad_rows, 1, 1).astype(jnp.bfloat16))
    grad_wout = inner(decoded, landed, 0, 0)[:, :CH]
    grad_dec = (inner(landed, w_out, 1, 1) * slope(dec_in)).astype(jnp.bfloat16)
    grad_bdec = jnp.sum(grad_dec.astype(jnp.float32), 0, keepdims=True)
    grad_wdec = inner(fetched, grad_dec, 0, 0)
    grad_fetched = inner(grad_dec, w_dec, 1, 1).astype(jnp.bfloat16)
    grad_mesh = inner(chooser, grad_fetched, 0, 0)
    grad_mesh, final_mesh = lax.optimization_barrier((grad_mesh, mesh.astype(jnp.bfloat16)))
    final_mesh = at_home(final_mesh)
    leaving = grad_mesh.astype(jnp.bfloat16)
    mats_grads = [None] * (5 * ROUNDS)
    bias_grads = [None] * (2 * ROUNDS)
    carried = ()
    for layer in reversed(range(ROUNDS)):
        old, back, update, agg, slopes = kept[layer]
        *ends, grad_uin, dest_low, to_before, own, to_after = edges_backward(
            index, grad_mesh, back, slopes, w_round[layer], carried
        )
        if ends:
            grad_mesh, leaving, sent_low = ends
            mats_grads[5 * layer + 5] = inner(
                kept[layer + 1][0].astype(jnp.bfloat16), sent_low, 0, 0
            )
        else:
            to_before, to_after, final_mesh = lax.optimization_barrier(
                (to_before, to_after, final_mesh)
            )
        from_before, from_after = halo(walk, to_after, to_before)
        if not ends:
            from_before, final_mesh = lax.optimization_barrier(
                (from_before, settled(mesh, final_mesh))
            )
        lowered = old.astype(jnp.bfloat16)
        mats_grads[5 * layer + 1 : 5 * layer + 5] = [
            inner(lowered, dest_low, 0, 0),
            inner(agg, grad_uin, 0, 0),
            inner(lowered, grad_uin, 0, 0),
            inner(update, leaving, 0, 0),
        ]
        bias_grads[2 * layer] = jnp.sum(dest_low.astype(jnp.float32), 0, keepdims=True)
        bias_grads[2 * layer + 1] = jnp.sum(grad_uin.astype(jnp.float32), 0, keepdims=True)
        carried = (own, from_before, from_after, grad_uin, dest_low, w_round[layer])
    grad_mesh, leaving, sent_low = round_backward(grad_mesh, *carried)
    mats_grads[0] = inner(kept[0][0].astype(jnp.bfloat16), sent_low, 0, 0)
    grad_win, grad_wnode, grad_bpair = encode_backward(
        grad_mesh, gathered, arrived, ids, w_in, w_node, biases
    )
    parts = [grad_win, grad_wnode, grad_wdec, grad_wout.reshape(CH, D)]
    parts = parts + mats_grads
    parts = parts + [grad_bpair, grad_bdec] + bias_grads
    keep, send = collect_rows(parts, total_size, peers, place)
    mine, leaving = reduced_piece(keep, send, leaving)
    late = at_home(leaving)
    mine = lax.dynamic_slice_in_dim(mine.reshape(-1), offset, shard)
    lane = lax.broadcasted_iota(jnp.int32, (8, HALF), 1)
    sums, late = summed_everywhere(
        jnp.where(lane == 0, local_total, jnp.sum(mine * mine)), late
    )
    total, norm = sums[0, 0], jnp.sqrt(sums[0, 1])
    node_grads = settled(grad_mesh, late)
    clipped = mine * jnp.minimum(1.0, 0.05 / norm)
    first = 0.9 * moment1 + 0.1 * clipped
    second = 0.999 * moment2 + 0.001 * clipped * clipped
    first_hat = first / (1.0 - 0.9**STEP)
    second_hat = second / (1.0 - 0.999**STEP)
    updated = master - 0.1 * (first_hat / (jnp.sqrt(second_hat) + 1e-08) + 0.1 * master)
    return (
        total.reshape(1),
        count.reshape(1),
        norm.reshape(1),
        updated,
        first,
        second,
        updated.astype(jnp.bfloat16),
        final_mesh.reshape(1, blocks, D),
        node_grads.reshape(1, blocks, D),
        grad_pred.reshape(1, grad_pred.shape[0], points),
    )


def solution(mesh):
    return jax.shard_map(
        functools.partial(shards, walk_of(mesh)),
        mesh=mesh,
        in_specs=(
            P(("dp", "space")),
            P(("dp", "space")),
            P(("dp", "space")),
            P("dp", None, "space"),
            P("dp", None, "space"),
            P("dp", None, "space"),
            P("dp", "space", None),
            P("dp", "space"),
            P("space", None),
            P("space"),
        ),
        out_specs=(
            P(),
            P(),
            P(),
            P(("dp", "space")),
            P(("dp", "space")),
            P(("dp", "space")),
            P(("dp", "space")),
            P("dp", "space", None),
            P("dp", "space", None),
            P("dp", None, "space"),
        ),
        check_vma=False,
    )
```

```python
import functools

import jax
import jax.numpy as jnp
from jax import lax
from jax.experimental import pallas as pl
from jax.experimental.pallas import tpu as pltpu
from jax.sharding import PartitionSpec as P

D = 256
HALF = 128
CH = 78
ROUNDS = 3
K = 6
ROWW = 360
NEAR = 358
STEP = 10
H = 2048
ALL = ("dp", "space")
LIMIT = pltpu.CompilerParams(vmem_limit_bytes=60 * 2**20)


def cost(micros):
    return pl.CostEstimate(flops=0, bytes_accessed=micros * 3_000_000, transcendentals=0)


def inner(left, right, left_dim, right_dim):
    return lax.dot_general(
        left, right, (((left_dim,), (right_dim,)), ((), ())), preferred_element_type=jnp.float32
    )


def sigmoid(value):
    return 0.5 * jnp.tanh(0.5 * value) + 0.5


def silu(value):
    return value * sigmoid(value)


def slope(value):
    sigma = sigmoid(value)
    return sigma * (1.0 + value * (1.0 - sigma))


def shifted(shard, axis, by):
    peers = lax.axis_size(axis)
    pairs = [(i, i + by) for i in range(peers) if 0 <= i + by < peers]
    return lax.ppermute(shard, axis, pairs)


def walk_of(mesh):
    count = mesh.shape["space"]
    chips = [getattr(device, "coords", None) for device in mesh.devices[0].reshape(-1)]
    if any(chip is None for chip in chips) or len(set(map(tuple, chips))) != count:
        return list(range(count))
    at = {tuple(chip): n for n, chip in enumerate(chips)}
    xs, ys, zs = (sorted({chip[n] for chip in at}) for n in range(3))
    if len(xs) * len(ys) * len(zs) != count:
        return list(range(count))
    if (len(xs), len(ys), len(zs)) == (2, 2, 4):
        corners = [(0, 0), (1, 0), (0, 1), (1, 1)]
        planes = [(0, 1, 3, 2), (2, 0, 1, 3), (3, 1, 0, 2), (2, 3, 1, 0)]
        steps = [(*corners[n], z) for z, plane in enumerate(planes) for n in plane]
        return [at[(xs[x], ys[y], zs[z])] for x, y, z in steps]
    walk, plane = [], []
    for n, y in enumerate(ys):
        plane = plane + [(x, y) for x in (xs if n % 2 == 0 else xs[::-1])]
    for n, z in enumerate(zs):
        walk = walk + [at[(x, y, z)] for x, y in (plane if n % 2 == 0 else plane[::-1])]
    return walk


def halo(walk, last, initial):
    up = list(zip(walk, walk[1:] + walk[:1]))
    down = [(j, i) for i, j in up]
    return lax.ppermute(last, "space", up), lax.ppermute(initial, "space", down)


def pieces_of(total, peers):
    share = total // peers
    starts = [share * d // D for d in range(peers)]
    counts = [-(-share * (d + 1) // D) - starts[d] for d in range(peers)]
    shared = [share * d % D != 0 for d in range(peers)]
    height = -(-(max(counts) + 1) // 16) * 16
    return starts, counts, shared, height


def parts_of():
    return [CH, D, D, CH] + [5 * D] * ROUNDS + [3 + 2 * ROUNDS]


def swapped(value, axis, bit):
    return lax.ppermute(value, axis, [(i, i ^ bit) for i in range(lax.axis_size(axis))])


def bits_of(axis):
    return [1 << n for n in range(lax.axis_size(axis).bit_length() - 1)]


def summed_everywhere(value, arriving):
    turns = [(axis, bit) for axis in ALL for bit in reversed(bits_of(axis))]
    for turn, (axis, bit) in enumerate(turns):
        value = value + swapped(value, axis, bit)
        if turn == len(turns) - 3:
            value, arriving = lax.optimization_barrier((value, arriving))
    return value, arriving


def orders():
    bits = bits_of("space")
    return bits, bits[1:2] + bits[:1] + bits[2:]


def gathered_blocks(piece, posted):
    half = piece.shape[0] // 2
    held = [piece[None, :half], piece[None, half:]]
    last = len(orders()[0]) - 1
    for turn, bits in enumerate(reversed(list(zip(*orders())))):
        if turn == last:
            held[0], held[1], posted = lax.optimization_barrier((*held, posted))
        for n, bit in enumerate(bits):
            held[n] = jnp.concatenate([held[n], swapped(held[n], "space", bit)], 0)
    return (held, [swapped(part, "dp", 1) for part in held]), posted


def spread_rows(gathered, total, peers, place):
    (first, second), (first_far, second_far) = gathered
    starts, counts, shared, height = pieces_of(total, peers)
    half, group = height // 2, first.shape[0]
    rows = -(-total // D)
    sizes = parts_of()
    ranks = []
    for order in orders():
        ranks.append({bit: group >> (n + 1) for n, bit in enumerate(order)})

    def at(rank, relative):
        spot = 0
        for bit, weight in rank.items():
            spot = spot + jnp.where((relative & bit) != 0, weight, 0)
        return spot

    def body(place_ref, *refs):
        sources, outs, buffer = refs[:4], refs[4:-1], refs[-1]
        me = place_ref[0]
        mine = me // group
        for d in range(peers):
            relative = (me ^ d) & (group - 1)
            spots = [at(rank, relative) for rank in ranks]

            def lay(one, two, d=d, spots=spots):
                piece = jnp.concatenate([one[spots[0]], two[spots[1]]], 0).astype(jnp.float32)
                start, count = starts[d], counts[d]
                if shared[d]:
                    buffer[start : start + 1, :] = buffer[start : start + 1, :] + piece[:1]
                    buffer[start + 1 : start + count, :] = piece[1:count]
                else:
                    buffer[start : start + count, :] = piece[:count]

            @pl.when(mine == d // group)
            def _():
                lay(sources[0], sources[1])

            @pl.when(mine != d // group)
            def _():
                lay(sources[2], sources[3])

        count = jnp.zeros((1, D), jnp.float32)
        for source in (sources[1], sources[3]):
            for spot in range(group):
                count = count + source[spot, half - 1 : half, :].astype(jnp.float32)
        outs[-1][...] = count
        start = 0
        for out, size in zip(outs[:-1], sizes):
            out[:size, :] = buffer[start : start + size, :].astype(out.dtype)
            if out.shape[0] > size:
                out[size:, :] = jnp.zeros((out.shape[0] - size, D), out.dtype)
            start = start + size

    kinds = [jnp.bfloat16] * (4 + ROUNDS) + [jnp.float32]
    talls = [HALF] + sizes[1:]
    return pl.pallas_call(
        body,
        grid_spec=pltpu.PrefetchScalarGridSpec(
            num_scalar_prefetch=1,
            grid=(1,),
            in_specs=[whole(first.shape)] * 4,
            out_specs=[whole((tall, D)) for tall in talls + [1]],
            scratch_shapes=[pltpu.VMEM((-(-rows // 8) * 8 + 8, D), jnp.float32)],
        ),
        out_shape=[
            jax.ShapeDtypeStruct((tall, D), kind)
            for tall, kind in zip(talls + [1], kinds + [jnp.float32])
        ],
        compiler_params=LIMIT,
        cost_estimate=cost(4),
        name="spread_rows",
    )(place.reshape(1), first, second, first_far, second_far)


def collect_rows(parts, total, peers, place):
    starts, counts, shared, height = pieces_of(total, peers)
    rows = -(-total // D)
    sizes = [min(part.shape[0], size) for part, size in zip(parts, tall_parts())]
    group = lax.axis_size("space")

    def body(place_ref, *refs):
        sources, keep, send, buffer = refs[:-3], refs[-3], refs[-2], refs[-1]
        start = 0
        for source, size in zip(sources, sizes):
            buffer[start : start + size, :] = source[:size, :]
            start = start + size
        if buffer.shape[0] > start:
            buffer[start:, :] = jnp.zeros((buffer.shape[0] - start, D), jnp.float32)
        me = place_ref[0]
        mine = me // group
        for d in range(peers):
            relative = (me ^ d) & (group - 1)

            @pl.when(mine == d // group)
            def _():
                keep[relative] = buffer[starts[d] : starts[d] + height, :]

            @pl.when(mine != d // group)
            def _():
                send[relative] = buffer[starts[d] : starts[d] + height, :].astype(jnp.bfloat16)

    shape = (group, height, D)
    return pl.pallas_call(
        body,
        grid_spec=pltpu.PrefetchScalarGridSpec(
            num_scalar_prefetch=1,
            grid=(1,),
            in_specs=[whole(part.shape) for part in parts],
            out_specs=[whole(shape), whole(shape)],
            scratch_shapes=[pltpu.VMEM((-(-rows // 8) * 8 + height + 8, D), jnp.float32)],
        ),
        out_shape=[
            jax.ShapeDtypeStruct(shape, jnp.float32),
            jax.ShapeDtypeStruct(shape, jnp.bfloat16),
        ],
        compiler_params=LIMIT,
        cost_estimate=cost(5),
        name="collect_rows",
    )(place.reshape(1), *parts)


def reduced_piece(keep, send, leaving):
    kept = keep + swapped(send, "dp", 1).astype(jnp.float32)
    half = kept.shape[1] // 2
    names = [bits_of("space")[::-1], bits_of("space")[::-1]]
    parts = [kept[:, :half], kept[:, half:]]
    parts = [part.reshape((2,) * len(names[0]) + (half, D)) for part in parts]
    for turn, bits in enumerate(zip(*orders())):
        for n, bit in enumerate(bits):
            spot = names[n].index(bit)
            names[n].pop(spot)
            stay = lax.index_in_dim(parts[n], 0, spot, keepdims=False)
            leave = lax.index_in_dim(parts[n], 1, spot, keepdims=False)
            parts[n] = stay + swapped(leave.astype(jnp.bfloat16), "space", bit).astype(jnp.float32)
        if turn == 1:
            parts[0], parts[1], leaving = lax.optimization_barrier((*parts, leaving))
    return jnp.concatenate(parts, 0), leaving


def tall_parts():
    return [CH, D, D, CH] + [D] * (5 * ROUNDS) + [2] + [1] * (1 + 2 * ROUNDS)


def weave(ref, value):
    rows = value.shape[0]
    ref[pl.ds(0, rows, stride=2), :] = value[:, :HALF]
    ref[pl.ds(1, rows, stride=2), :] = value[:, HALF:]


def unweave(ref):
    rows = ref.shape[0] // 2
    return ref[pl.ds(0, rows, stride=2), :], ref[pl.ds(1, rows, stride=2), :]


def whole(shape):
    return pl.BlockSpec(shape, lambda *_: (0,) * len(shape))


def round_forward(index, mesh, before, own, after, mats, bias, following):
    blocks = mesh.shape[0]
    tile, chunk = 512, 16
    turns, high = tile // chunk, 2 * chunk
    more = following is not None
    spans = [before.shape[0], own.shape[0], after.shape[0]]
    reach = sum(spans)

    def body(*refs):
        index_ref, mesh_ref, before_ref, own_ref, after_ref, mats_ref, bias_ref = refs[:7]
        next_ref, sent_ref = (refs[7], refs[13]) if more else (None, None)
        new_ref, back_ref, update_ref, agg_ref, slope_ref = refs[8:13] if more else refs[7:12]
        raw, table, rows, wide, wider, sems = refs[-6:]
        step = pl.program_id(0)

        @pl.when(step == 0)
        def _():
            copies = []
            start = 0
            for n, (source, span) in enumerate(zip((before_ref, own_ref, after_ref), spans)):
                copies.append(
                    pltpu.make_async_copy(source, raw.at[pl.ds(start, span)], sems.at[n])
                )
                start = start + span
            for copy in copies:
                copy.start()
            for copy in copies:
                copy.wait()

            @pl.loop(0, reach // 256)
            def _(i):
                at = pl.multiple_of(i * 256, 256)
                table[pl.ds(at, 256), :] = raw[pl.ds(at, 256), :].astype(jnp.float32)

        mesh_in = mesh_ref[...]
        lowered = mesh_in.astype(jnp.bfloat16)
        weave(wide, inner(lowered, mats_ref[1], 1, 0) + bias_ref[0:1, :])

        def fetch(turn):
            for edge in range(K):
                base = edge * blocks + step * tile + turn * chunk
                spots = [index_ref[base + u] for u in range(chunk)]
                values = [table[pl.ds(pl.multiple_of(spot, 2), 2), :] for spot in spots]
                for u in range(chunk):
                    spot = pl.multiple_of(edge * 2 * tile + turn * high + 2 * u, 2)
                    rows[pl.ds(spot, 2), :] = values[u]

        def load(turn):
            at = pl.multiple_of(turn * high, high)
            taken = [
                rows[pl.ds(pl.multiple_of(edge * 2 * tile + turn * high, high), high), :]
                for edge in range(K)
            ]
            return at, wide[pl.ds(at, high), :], taken

        def dense(at, dest, taken):
            total = None
            for edge in range(K):
                value = taken[edge] + dest
                sigma = sigmoid(value)
                out = value * sigma
                slope_ref[edge, pl.ds(at, high), :] = (sigma + out * (1.0 - sigma)).astype(
                    jnp.bfloat16
                )
                total = out if total is None else total + out
            wider[pl.ds(at, high), :] = total * (1.0 / K)

        def some(turn, carry):
            loaded = load(turn - 1)
            fetch(turn)
            dense(*loaded)
            return carry

        fetch(0)
        lax.fori_loop(1, turns, some, 0)
        dense(*load(turns - 1))
        first, second = unweave(wider)
        first, second = first.astype(jnp.bfloat16), second.astype(jnp.bfloat16)
        agg_ref[:, :HALF] = first
        agg_ref[:, HALF:] = second
        update_in = (
            inner(first, mats_ref[2, :HALF, :], 1, 0)
            + inner(second, mats_ref[2, HALF:, :], 1, 0)
            + inner(lowered, mats_ref[3], 1, 0)
            + bias_ref[1:2, :]
        )
        sigma = sigmoid(update_in)
        out = update_in * sigma
        back_ref[...] = sigma + out * (1.0 - sigma)
        update = out.astype(jnp.bfloat16)
        update_ref[...] = update
        new = mesh_in + inner(update, mats_ref[4], 1, 0)
        new_ref[...] = new
        if more:
            weave(wide, inner(new.astype(jnp.bfloat16), next_ref[0], 1, 0))
            sent_ref[...] = wide[...].astype(jnp.bfloat16)

    whole_rows = pl.BlockSpec((tile, D), lambda i, *_: (i, 0))
    woven = pl.BlockSpec((2 * tile, HALF), lambda i, *_: (i, 0))
    ins = [whole_rows] + [pl.BlockSpec(memory_space=pl.ANY)] * 3 + [whole(mats.shape), whole(bias.shape)]
    outs = [whole_rows] * 4 + [pl.BlockSpec((K, 2 * tile, HALF), lambda i, *_: (0, i, 0))]
    shapes = [
        jax.ShapeDtypeStruct((blocks, D), jnp.float32),
        jax.ShapeDtypeStruct((blocks, D), jnp.float32),
        jax.ShapeDtypeStruct((blocks, D), jnp.bfloat16),
        jax.ShapeDtypeStruct((blocks, D), jnp.bfloat16),
        jax.ShapeDtypeStruct((K, 2 * blocks, HALF), jnp.bfloat16),
    ]
    args = [index, mesh, before, own, after, mats, bias]
    if more:
        ins.append(pl.BlockSpec((1, D, D), lambda *_: (0, 0, 0)))
        outs.append(woven)
        shapes.append(jax.ShapeDtypeStruct((2 * blocks, HALF), jnp.bfloat16))
        args.append(following)
    return pl.pallas_call(
        body,
        grid_spec=pltpu.PrefetchScalarGridSpec(
            num_scalar_prefetch=1,
            grid=(blocks // tile,),
            in_specs=ins,
            out_specs=outs,
            scratch_shapes=[
                pltpu.VMEM((reach, HALF), jnp.bfloat16),
                pltpu.VMEM((reach, HALF), jnp.float32),
                pltpu.VMEM((K * 2 * tile, HALF), jnp.float32),
                pltpu.VMEM((2 * tile, HALF), jnp.float32),
                pltpu.VMEM((2 * tile, HALF), jnp.float32),
                pltpu.SemaphoreType.DMA((3,)),
            ],
        ),
        out_shape=shapes,
        compiler_params=LIMIT,
        cost_estimate=cost(25),
        name="round_forward",
    )(*args)


def edges_backward(index, grad_mesh, back, slopes, mats, carried=()):
    blocks = grad_mesh.shape[0]
    tile, chunk = 512, 16
    steps, turns, high = blocks // tile, tile // chunk, 2 * chunk
    reach = 2 * (blocks + 2 * H)

    def body(*refs):
        index_ref, grad_ref, back_ref, slope_ref, mats_ref = refs[:5]
        rest = refs[5:]
        if carried:
            past, rest = rest[:6], rest[6:]
            (new_ref, out_ref, sent_ref), rest = rest[:3], rest[3:]
        guin_ref, low_ref, before_ref, own_ref, after_ref, wide, wider, flows, *tables = rest
        step = pl.program_id(0)

        @pl.when(step == 0)
        def _():
            @pl.loop(0, reach // 256)
            def _(i):
                for table in tables:
                    table[pl.ds(pl.multiple_of(i * 256, 256), 256), :] = jnp.zeros(
                        (256, HALF), jnp.float32
                    )

        if carried:
            new = ended(grad_ref, *past, sent_ref, wide)
            new_ref[...] = new
            grad_out = new.astype(jnp.bfloat16)
            out_ref[...] = grad_out
        else:
            grad_out = grad_ref[...].astype(jnp.bfloat16)
        grad_uin = (inner(grad_out, mats_ref[4], 1, 1) * back_ref[...]).astype(jnp.bfloat16)
        guin_ref[...] = grad_uin
        weave(wide, inner(grad_uin, mats_ref[2], 1, 1) * (1.0 / K))

        def dense(turn):
            at = pl.multiple_of(turn * high, high)
            grad_agg = wide[pl.ds(at, high), :]
            total, parts = None, []
            for edge in range(K):
                flow = grad_agg * slope_ref[edge, pl.ds(at, high), :].astype(jnp.float32)
                parts.append(flow)
                total = flow if total is None else total + flow
            return at, total, parts

        def keep(turn, at, total, parts):
            for edge in range(K):
                spot = pl.multiple_of(edge * 2 * tile + turn * high, high)
                flows[pl.ds(spot, high), :] = parts[edge]
            wider[pl.ds(at, high), :] = total

        def scatter(turn):
            for u in range(chunk):
                spots, sums = [], []
                for edge in range(K):
                    base = edge * blocks + step * tile + turn * chunk
                    spots.append(pl.multiple_of(index_ref[base + u], 2))
                for edge in range(K):
                    spot = pl.multiple_of(edge * 2 * tile + turn * high + 2 * u, 2)
                    sums.append(tables[edge][pl.ds(spots[edge], 2), :] + flows[pl.ds(spot, 2), :])
                for edge in range(K):
                    tables[edge][pl.ds(spots[edge], 2), :] = sums[edge]

        def some(turn, carry):
            found = dense(turn)
            scatter(turn - 1)
            keep(turn, *found)
            return carry

        keep(0, *dense(0))
        lax.fori_loop(1, turns, some, 0)
        scatter(turns - 1)
        first, second = unweave(wider)
        low_ref[:, :HALF] = first.astype(jnp.bfloat16)
        low_ref[:, HALF:] = second.astype(jnp.bfloat16)

        @pl.when(step == steps - 1)
        def _():
            def summed(at):
                value = tables[0][pl.ds(at, 256), :]
                for table in tables[1:]:
                    value = value + table[pl.ds(at, 256), :]
                return value

            @pl.loop(0, 2 * H // 256)
            def _(i):
                at = pl.multiple_of(i * 256, 256)
                far = pl.multiple_of(2 * H + 2 * blocks + at, 256)
                before_ref[pl.ds(at, 256), :] = summed(at).astype(jnp.bfloat16)
                after_ref[pl.ds(at, 256), :] = summed(far).astype(jnp.bfloat16)

            @pl.loop(0, 2 * blocks // 256)
            def _(i):
                at = pl.multiple_of(i * 256, 256)
                own_ref[pl.ds(at, 256), :] = summed(pl.multiple_of(2 * H + at, 256))

    rows = pl.BlockSpec((tile, D), lambda i, *_: (i, 0))
    woven = pl.BlockSpec((2 * tile, HALF), lambda i, *_: (i, 0))
    low = jax.ShapeDtypeStruct((blocks, D), jnp.bfloat16)
    return pl.pallas_call(
        body,
        grid_spec=pltpu.PrefetchScalarGridSpec(
            num_scalar_prefetch=1,
            grid=(steps,),
            in_specs=[
                rows, rows,
                pl.BlockSpec((K, 2 * tile, HALF), lambda i, *_: (0, i, 0)),
                whole(mats.shape),
            ]
            + ([woven] * 3 + [rows] * 2 + [whole(mats.shape)] if carried else []),
            out_specs=([rows] * 3 if carried else []) + [
                rows, rows,
                whole((2 * H, HALF)), whole((2 * blocks, HALF)), whole((2 * H, HALF)),
            ],
            scratch_shapes=[
                pltpu.VMEM((2 * tile, HALF), jnp.float32),
                pltpu.VMEM((2 * tile, HALF), jnp.float32),
                pltpu.VMEM((2 * tile * K, HALF), jnp.float32),
            ]
            + [pltpu.VMEM((reach, HALF), jnp.float32)] * K,
        ),
        out_shape=(
            [jax.ShapeDtypeStruct((blocks, D), jnp.float32), low, low] if carried else []
        ) + [
            low,
            low,
            jax.ShapeDtypeStruct((2 * H, HALF), jnp.bfloat16),
            jax.ShapeDtypeStruct((2 * blocks, HALF), jnp.float32),
            jax.ShapeDtypeStruct((2 * H, HALF), jnp.bfloat16),
        ],
        compiler_params=LIMIT,
        cost_estimate=cost(28 if carried else 25),
        name="edges_backward",
    )(index, grad_mesh, back, slopes, mats, *carried)


def ended(grad_ref, own_ref, first_ref, last_ref, guin_ref, dest_ref, mats_ref, sent_ref, wide):
    wide[...] = (
        own_ref[...] + first_ref[...].astype(jnp.float32) + last_ref[...].astype(jnp.float32)
    )
    one, two = unweave(wide)
    one, two = one.astype(jnp.bfloat16), two.astype(jnp.bfloat16)
    sent_ref[:, :HALF] = one
    sent_ref[:, HALF:] = two
    return (
        grad_ref[...]
        + inner(guin_ref[...], mats_ref[3], 1, 1)
        + inner(dest_ref[...], mats_ref[1], 1, 1)
        + inner(one, mats_ref[0, :, :HALF], 1, 1)
        + inner(two, mats_ref[0, :, HALF:], 1, 1)
    )


def round_backward(grad_mesh, own, first, last, grad_uin, dest_low, mats):
    blocks = grad_mesh.shape[0]
    tile = 1024

    def body(*refs):
        new_ref, out_ref, sent_ref, wide = refs[-4:]
        new = ended(*refs[:-4], sent_ref, wide)
        new_ref[...] = new
        out_ref[...] = new.astype(jnp.bfloat16)

    rows = pl.BlockSpec((tile, D), lambda i: (i, 0))
    woven = pl.BlockSpec((2 * tile, HALF), lambda i: (i, 0))
    low = jax.ShapeDtypeStruct((blocks, D), jnp.bfloat16)
    return pl.pallas_call(
        body,
        grid=(blocks // tile,),
        in_specs=[rows, woven, woven, woven, rows, rows, whole(mats.shape)],
        out_specs=[rows, rows, rows],
        out_shape=[jax.ShapeDtypeStruct((blocks, D), jnp.float32), low, low],
        scratch_shapes=[pltpu.VMEM((2 * tile, HALF), jnp.float32)],
        compiler_params=LIMIT,
        cost_estimate=cost(7),
        name="round_backward",
    )(grad_mesh, own, first, last, grad_uin, dest_low, mats)


def encode_rows(arrived, ids, w_in, w_node, biases, source):
    posts = arrived.shape[0]
    tile = 512

    def body(arrived_ref, ids_ref, in_ref, node_ref, bias_ref, source_ref, mesh_ref, gathered_ref, sent_ref, encoded, wide):
        step = pl.program_id(0)

        @pl.when(step == 0)
        def _():
            entering = inner(arrived_ref[...], in_ref[...], 1, 0) + bias_ref[0:1, :]
            encoded[...] = silu(entering).astype(jnp.bfloat16)

        nodes = lax.broadcasted_iota(jnp.int32, (tile, posts), 0) + step * tile
        chooser = jnp.where(nodes == ids_ref[...], 1.0, 0.0).astype(jnp.bfloat16)
        gathered = inner(chooser, encoded[...], 1, 0).astype(jnp.bfloat16)
        gathered_ref[...] = gathered
        mesh = silu(inner(gathered, node_ref[...], 1, 0) + bias_ref[1:2, :])
        mesh_ref[...] = mesh
        weave(wide, inner(mesh.astype(jnp.bfloat16), source_ref[0], 1, 0))
        sent_ref[...] = wide[...].astype(jnp.bfloat16)

    rows = pl.BlockSpec((tile, D), lambda i: (i, 0))
    args = (arrived, ids, w_in, w_node, biases, source)
    return pl.pallas_call(
        body,
        grid=(H // tile,),
        in_specs=[whole(arg.shape) for arg in args[:-1]]
        + [pl.BlockSpec((1, D, D), lambda *_: (0, 0, 0))],
        out_specs=[rows, rows, pl.BlockSpec((2 * tile, HALF), lambda i: (i, 0))],
        out_shape=[
            jax.ShapeDtypeStruct((H, D), jnp.float32),
            jax.ShapeDtypeStruct((H, D), jnp.bfloat16),
            jax.ShapeDtypeStruct((2 * H, HALF), jnp.bfloat16),
        ],
        scratch_shapes=[pltpu.VMEM((posts, D), jnp.bfloat16), pltpu.VMEM((2 * tile, HALF), jnp.float32)],
        compiler_params=LIMIT,
        cost_estimate=cost(5),
        name="encode_rows",
    )(*args)


def encode_backward(grad_mesh, gathered, arrived, ids, w_in, w_node, biases):
    posts = arrived.shape[0]
    tile = 512
    steps = H // tile

    def body(grad_ref, gathered_ref, arrived_ref, ids_ref, in_ref, node_ref, bias_ref, gin_ref, gnode_ref, gbias_ref, total):
        step = pl.program_id(0)

        @pl.when(step == 0)
        def _():
            total[...] = jnp.zeros(total.shape, jnp.float32)
            gnode_ref[...] = jnp.zeros(gnode_ref.shape, jnp.float32)
            gbias_ref[...] = jnp.zeros(gbias_ref.shape, jnp.float32)

        node_in = inner(gathered_ref[...], node_ref[...], 1, 0) + bias_ref[1:2, :]
        grad_node = (grad_ref[...] * slope(node_in)).astype(jnp.bfloat16)
        gbias_ref[1:2, :] += jnp.sum(grad_node.astype(jnp.float32), 0, keepdims=True)
        gnode_ref[...] += inner(gathered_ref[...], grad_node, 0, 0)
        back = inner(grad_node, node_ref[...], 1, 1).astype(jnp.bfloat16)
        nodes = lax.broadcasted_iota(jnp.int32, (posts, tile), 1) + step * tile
        chooser = jnp.where(nodes == ids_ref[...], 1.0, 0.0).astype(jnp.bfloat16)
        total[...] += inner(chooser, back, 1, 0)

        @pl.when(step == steps - 1)
        def _():
            entering = inner(arrived_ref[...], in_ref[...], 1, 0) + bias_ref[0:1, :]
            grad_enc = (total[...] * slope(entering)).astype(jnp.bfloat16)
            gbias_ref[0:1, :] = jnp.sum(grad_enc.astype(jnp.float32), 0, keepdims=True)
            gin_ref[...] = inner(arrived_ref[...], grad_enc, 0, 0)

    rows = pl.BlockSpec((tile, D), lambda i: (i, 0))
    args = (grad_mesh, gathered, arrived, ids, w_in, w_node, biases)
    shapes = [(HALF, D), (D, D), (2, D)]
    return pl.pallas_call(
        body,
        grid=(steps,),
        in_specs=[rows, rows] + [whole(arg.shape) for arg in args[2:]],
        out_specs=[whole(shape) for shape in shapes],
        out_shape=[jax.ShapeDtypeStruct(shape, jnp.float32) for shape in shapes],
        scratch_shapes=[pltpu.VMEM((posts, D), jnp.float32)],
        compiler_params=LIMIT,
        cost_estimate=cost(7),
        name="encode_backward",
    )(*args)


def shards(walk, master, moment1, moment2, inputs, targets, valid, owner, slot, neighbours, partner):
    bands = lax.axis_size("space")
    band = lax.axis_index("space")
    peers = lax.axis_size(ALL)
    place = lax.axis_index(ALL)
    shard = master.shape[0]
    total_size = shard * peers
    height = pieces_of(total_size, peers)[3]
    offset = lax.rem(lax.rem(shard, D) * place, D)
    piece = lax.dynamic_update_slice_in_dim(
        jnp.zeros((height * D,), jnp.bfloat16), master.astype(jnp.bfloat16), offset, 0
    )
    state_in = inputs[0]
    counted = valid[0].astype(jnp.float32)
    local_count = jnp.sum(valid[0])
    digits = (local_count >> jnp.array([16, 8, 0], jnp.int32)) & 255
    piece = lax.dynamic_update_slice(
        piece.reshape(height, D), digits.astype(jnp.bfloat16)[None, :], (height - 1, 0)
    )
    points = state_in.shape[1]
    blocks = neighbours.shape[0]
    assert blocks == H
    capacity = max(2, 2 * points // bands)
    target_band = owner[0, :, 0]
    hits = (target_band[:, None] == jnp.arange(bands, dtype=jnp.int32)[None, :]).astype(jnp.int32)
    ranks = jnp.sum(jnp.cumsum(hits, 0) * hits, 1) - 1
    places_out = jnp.sum(hits * jnp.asarray(walk, jnp.int32)[None, :], 1) * capacity + ranks
    poster = (
        jnp.arange(bands * capacity, dtype=jnp.int32)[:, None] == places_out[None, :]
    ).astype(jnp.bfloat16)
    spots = slot[0][None, :]
    columns = jnp.concatenate(
        [
            state_in,
            (spots // 64).astype(jnp.bfloat16),
            (spots % 64).astype(jnp.bfloat16),
            jnp.ones((1, points), jnp.bfloat16),
            jnp.zeros((HALF - CH - 3, points), jnp.bfloat16),
        ],
        0,
    )

    def exchanged(rows):
        return lax.all_to_all(
            rows.reshape(bands, capacity, HALF), "space", split_axis=0, concat_axis=0, tiled=True
        ).reshape(bands * capacity, HALF)

    held, posted = gathered_blocks(piece, inner(poster, columns, 1, 1).astype(jnp.bfloat16))
    arrived = exchanged(posted)
    w_in, w_node, w_dec, w_out, *w_round, biases, digits = spread_rows(
        held, total_size, peers, place
    )
    count = digits[0, 0] * 65536.0 + digits[0, 1] * 256.0 + digits[0, 2]
    w_out = jnp.pad(w_out.reshape(D, CH), ((0, 0), (0, HALF - CH)))
    w_round = [mats.reshape(5, D, D) for mats in w_round]
    b_head = biases[:3]
    b_round = biases[3:].reshape(ROUNDS, 2, D)
    ids = arrived[:, CH : CH + 3].astype(jnp.int32)
    ids = jnp.where(ids[:, 2:3] > 0, ids[:, 0:1] * 64 + ids[:, 1:2], -1)
    chooser = (ids == jnp.arange(blocks, dtype=jnp.int32)[None, :]).astype(jnp.bfloat16)
    mesh, gathered, sent = encode_rows(
        arrived, ids.reshape(1, -1), w_in, w_node, biases, w_round[0]
    )
    sent, partner, neighbours, counted = lax.optimization_barrier(
        (sent, partner, neighbours, counted)
    )
    index = 2 * ((neighbours - band * blocks + H) % (blocks * bands)).T.reshape(-1)
    moved = [(n, place) for n, place in enumerate(walk) if n != place]
    stays = jnp.asarray([n == place for n, place in enumerate(walk)])[band]
    index = jnp.where(stays, index, lax.ppermute(index, "space", moved))

    def at_home(rows):
        return lax.ppermute(rows, "space", [(j, i) for i, j in moved])

    def settled(own, came):
        return jnp.where(stays, own, came.astype(jnp.float32))

    partner_by = partner - band * points - jnp.arange(points, dtype=jnp.int32)
    coded = jnp.where(partner_by >= NEAR, partner_by - NEAR + 1, 0).astype(jnp.bfloat16)
    low_valid = jnp.concatenate([counted.astype(jnp.bfloat16), coded[None, :]], 0)
    valid_around = jnp.concatenate(
        [
            shifted(low_valid[:, points - ROWW :], "space", 1),
            low_valid,
            shifted(low_valid[:, :ROWW], "space", -1),
        ],
        1,
    )
    kept = []
    for layer in range(ROUNDS):
        before, after = halo(walk, sent[2 * (blocks - H) :], sent[: 2 * H])
        if layer == 0:
            before, valid_around = lax.optimization_barrier((before, valid_around))
        following = w_round[layer + 1] if layer + 1 < ROUNDS else None
        new, back, update, agg, slopes, *rest = round_forward(
            index, mesh, before, sent, after, w_round[layer], b_round[layer], following
        )
        kept.append((mesh, back, update, agg, slopes))
        mesh = new
        sent = rest[0] if rest else None
    wide_valid = valid_around[:CH].astype(jnp.float32)
    coded = valid_around[CH : CH + 1, : points + ROWW].astype(jnp.float32)
    weights = [
        (
            by,
            jnp.where(coded == by - NEAR + 1, 1.0, 0.0)
            * wide_valid[:, : points + ROWW]
            * wide_valid[:, by : by + points + ROWW],
        )
        for by in range(NEAR, ROWW + 1)
    ]
    fetched = inner(chooser, mesh.astype(jnp.bfloat16), 1, 0).astype(jnp.bfloat16)
    dec_in = inner(fetched, w_dec, 1, 0) + b_head[2]
    decoded = silu(dec_in).astype(jnp.bfloat16)
    returned = exchanged(inner(decoded, w_out, 1, 0).astype(jnp.bfloat16))
    branch = inner(returned, poster, 0, 0)[:CH]
    err = state_in.astype(jnp.float32) + branch - targets[0].astype(jnp.float32)
    def widened(values):
        low = values.astype(jnp.bfloat16)
        before = shifted(low[:, points - ROWW :], "space", 1).astype(jnp.float32)
        after = shifted(low[:, :ROWW], "space", -1).astype(jnp.float32)
        return jnp.concatenate([before, values, after], 1)

    wide_err = widened(err)
    paired = jnp.zeros((CH, points + ROWW), jnp.float32)
    pair_total = jnp.zeros((CH, points), jnp.float32)
    for by, both in weights:
        gap = both * (wide_err[:, : points + ROWW] - wide_err[:, by : by + points + ROWW])
        paired = paired + gap
        pair_total = pair_total + gap[:, ROWW:] * (
            wide_err[:, ROWW : ROWW + points] - wide_err[:, ROWW + by : ROWW + by + points]
        )
    local_total = jnp.sum(counted * err * err) + 0.5 * jnp.sum(pair_total)
    grad_pred = 2.0 * counted * err + paired[:, ROWW:]
    for by, both in weights:
        gap = both * (wide_err[:, : points + ROWW] - wide_err[:, by : by + points + ROWW])
        grad_pred = grad_pred - gap[:, ROWW - by : ROWW - by + points]
    grad_pred = grad_pred / count
    grad_rows = jnp.pad(grad_pred.astype(jnp.bfloat16), ((0, HALF - CH), (0, 0)))
    landed = exchanged(inner(poster, grad_rows, 1, 1).astype(jnp.bfloat16))
    grad_wout = inner(decoded, landed, 0, 0)[:, :CH]
    grad_dec = (inner(landed, w_out, 1, 1) * slope(dec_in)).astype(jnp.bfloat16)
    grad_bdec = jnp.sum(grad_dec.astype(jnp.float32), 0, keepdims=True)
    grad_wdec = inner(fetched, grad_dec, 0, 0)
    grad_fetched = inner(grad_dec, w_dec, 1, 1).astype(jnp.bfloat16)
    grad_mesh = inner(chooser, grad_fetched, 0, 0)
    grad_mesh, final_mesh = lax.optimization_barrier((grad_mesh, mesh.astype(jnp.bfloat16)))
    final_mesh = at_home(final_mesh)
    leaving = grad_mesh.astype(jnp.bfloat16)
    mats_grads = [None] * (5 * ROUNDS)
    bias_grads = [None] * (2 * ROUNDS)
    carried = ()
    for layer in reversed(range(ROUNDS)):
        old, back, update, agg, slopes = kept[layer]
        *ends, grad_uin, dest_low, to_before, own, to_after = edges_backward(
            index, grad_mesh, back, slopes, w_round[layer], carried
        )
        if ends:
            grad_mesh, leaving, sent_low = ends
            mats_grads[5 * layer + 5] = inner(
                kept[layer + 1][0].astype(jnp.bfloat16), sent_low, 0, 0
            )
        else:
            to_before, to_after, final_mesh = lax.optimization_barrier(
                (to_before, to_after, final_mesh)
            )
        from_before, from_after = halo(walk, to_after, to_before)
        if not ends:
            from_before, final_mesh = lax.optimization_barrier(
                (from_before, settled(mesh, final_mesh))
            )
        lowered = old.astype(jnp.bfloat16)
        mats_grads[5 * layer + 1 : 5 * layer + 5] = [
            inner(lowered, dest_low, 0, 0),
            inner(agg, grad_uin, 0, 0),
            inner(lowered, grad_uin, 0, 0),
            inner(update, leaving, 0, 0),
        ]
        bias_grads[2 * layer] = jnp.sum(dest_low.astype(jnp.float32), 0, keepdims=True)
        bias_grads[2 * layer + 1] = jnp.sum(grad_uin.astype(jnp.float32), 0, keepdims=True)
        carried = (own, from_before, from_after, grad_uin, dest_low, w_round[layer])
    grad_mesh, leaving, sent_low = round_backward(grad_mesh, *carried)
    mats_grads[0] = inner(kept[0][0].astype(jnp.bfloat16), sent_low, 0, 0)
    grad_win, grad_wnode, grad_bpair = encode_backward(
        grad_mesh, gathered, arrived, ids, w_in, w_node, biases
    )
    parts = [grad_win, grad_wnode, grad_wdec, grad_wout.reshape(CH, D)]
    parts = parts + mats_grads
    parts = parts + [grad_bpair, grad_bdec] + bias_grads
    keep, send = collect_rows(parts, total_size, peers, place)
    mine, leaving = reduced_piece(keep, send, leaving)
    late = at_home(leaving)
    mine = lax.dynamic_slice_in_dim(mine.reshape(-1), offset, shard)
    lane = lax.broadcasted_iota(jnp.int32, (8, HALF), 1)
    sums, late = summed_everywhere(
        jnp.where(lane == 0, local_total, jnp.sum(mine * mine)), late
    )
    total, norm = sums[0, 0], jnp.sqrt(sums[0, 1])
    node_grads = settled(grad_mesh, late)
    clipped = mine * jnp.minimum(1.0, 0.05 / norm)
    first = 0.9 * moment1 + 0.1 * clipped
    second = 0.999 * moment2 + 0.001 * clipped * clipped
    first_hat = first / (1.0 - 0.9**STEP)
    second_hat = second / (1.0 - 0.999**STEP)
    updated = master - 0.1 * (first_hat / (jnp.sqrt(second_hat) + 1e-08) + 0.1 * master)
    return (
        total.reshape(1),
        count.reshape(1),
        norm.reshape(1),
        updated,
        first,
        second,
        updated.astype(jnp.bfloat16),
        final_mesh.reshape(1, blocks, D),
        node_grads.reshape(1, blocks, D),
        grad_pred.reshape(1, grad_pred.shape[0], points),
    )


def solution(mesh):
    return jax.shard_map(
        functools.partial(shards, walk_of(mesh)),
        mesh=mesh,
        in_specs=(
            P(("dp", "space")),
            P(("dp", "space")),
            P(("dp", "space")),
            P("dp", None, "space"),
            P("dp", None, "space"),
            P("dp", None, "space"),
            P("dp", "space", None),
            P("dp", "space"),
            P("space", None),
            P("space"),
        ),
        out_specs=(
            P(),
            P(),
            P(),
            P(("dp", "space")),
            P(("dp", "space")),
            P(("dp", "space")),
            P(("dp", "space")),
            P("dp", "space", None),
            P("dp", "space", None),
            P("dp", None, "space"),
        ),
        check_vma=False,
    )
```

```python
import functools

import jax
import jax.numpy as jnp
from jax import lax
from jax.experimental import pallas as pl
from jax.experimental.pallas import tpu as pltpu
from jax.sharding import PartitionSpec as P

D = 256
HALF = 128
CH = 78
ROUNDS = 3
K = 6
ROWW = 360
NEAR = 358
STEP = 10
H = 2048
ALL = ("dp", "space")
LIMIT = pltpu.CompilerParams(vmem_limit_bytes=60 * 2**20)


def cost(micros):
    return pl.CostEstimate(flops=0, bytes_accessed=micros * 3_000_000, transcendentals=0)


def inner(left, right, left_dim, right_dim):
    return lax.dot_general(
        left, right, (((left_dim,), (right_dim,)), ((), ())), preferred_element_type=jnp.float32
    )


def sigmoid(value):
    return 0.5 * jnp.tanh(0.5 * value) + 0.5


def silu(value):
    return value * sigmoid(value)


def slope(value):
    sigma = sigmoid(value)
    return sigma * (1.0 + value * (1.0 - sigma))


def shifted(shard, axis, by):
    peers = lax.axis_size(axis)
    pairs = [(i, i + by) for i in range(peers) if 0 <= i + by < peers]
    return lax.ppermute(shard, axis, pairs)


def walk_of(mesh):
    count = mesh.shape["space"]
    chips = [getattr(device, "coords", None) for device in mesh.devices[0].reshape(-1)]
    if any(chip is None for chip in chips) or len(set(map(tuple, chips))) != count:
        return list(range(count))
    at = {tuple(chip): n for n, chip in enumerate(chips)}
    xs, ys, zs = (sorted({chip[n] for chip in at}) for n in range(3))
    if len(xs) * len(ys) * len(zs) != count:
        return list(range(count))
    if (len(xs), len(ys), len(zs)) == (2, 2, 4):
        corners = [(0, 0), (1, 0), (0, 1), (1, 1)]
        planes = [(0, 1, 3, 2), (2, 0, 1, 3), (3, 1, 0, 2), (2, 3, 1, 0)]
        steps = [(*corners[n], z) for z, plane in enumerate(planes) for n in plane]
        return [at[(xs[x], ys[y], zs[z])] for x, y, z in steps]
    walk, plane = [], []
    for n, y in enumerate(ys):
        plane = plane + [(x, y) for x in (xs if n % 2 == 0 else xs[::-1])]
    for n, z in enumerate(zs):
        walk = walk + [at[(x, y, z)] for x, y in (plane if n % 2 == 0 else plane[::-1])]
    return walk


def halo(walk, last, initial):
    up = list(zip(walk, walk[1:] + walk[:1]))
    down = [(j, i) for i, j in up]
    return lax.ppermute(last, "space", up), lax.ppermute(initial, "space", down)


def pieces_of(total, peers):
    share = total // peers
    starts = [share * d // D for d in range(peers)]
    counts = [-(-share * (d + 1) // D) - starts[d] for d in range(peers)]
    shared = [share * d % D != 0 for d in range(peers)]
    height = -(-(max(counts) + 1) // 16) * 16
    return starts, counts, shared, height


def parts_of():
    return [CH, D, D, CH] + [5 * D] * ROUNDS + [3 + 2 * ROUNDS]


def swapped(value, axis, bit):
    return lax.ppermute(value, axis, [(i, i ^ bit) for i in range(lax.axis_size(axis))])


def bits_of(axis):
    return [1 << n for n in range(lax.axis_size(axis).bit_length() - 1)]


def others(value, axis, bits):
    masks = [sum(bit for n, bit in enumerate(bits) if m >> n & 1) for m in range(1, 1 << len(bits))]
    return [swapped(value, axis, mask) for mask in masks]


def upper_groups():
    bits = bits_of("space")[2:]
    return [tuple(bits[n : n + 2]) for n in range(0, len(bits), 2)]


def orders():
    return [(1, 2), (2, 1)]


def summed_everywhere(value, arriving):
    for bits in reversed(upper_groups()):
        value = sum(others(value, "space", bits), value)
    value = value + swapped(value, "dp", 1)
    value, arriving = lax.optimization_barrier((value, arriving))
    return sum(others(value, "space", (1, 2)), value), arriving


def gathered_blocks(piece, posted):
    held, weights, size = piece[None], {}, 1
    for bits in reversed(upper_groups()):
        held = jnp.concatenate([held] + others(held, "space", bits), 0)
        for n, bit in enumerate(bits):
            weights[bit] = size << n
        size = size << len(bits)
    half = piece.shape[0] // 2
    held = [held[:, :half], held[:, half:]]
    ranks = [dict(weights), dict(weights)]
    for turn in (1, 0):
        if turn == 0:
            held[0], held[1], posted = lax.optimization_barrier((*held, posted))
        for n, order in enumerate(orders()):
            held[n] = jnp.concatenate([held[n], swapped(held[n], "space", order[turn])], 0)
            ranks[n][order[turn]] = size
        size = size << 1
    return (held, [swapped(part, "dp", 1) for part in held], ranks), posted


def spread_rows(gathered, total, peers, place):
    (first, second), (first_far, second_far), ranks = gathered
    starts, counts, shared, height = pieces_of(total, peers)
    half, group = height // 2, first.shape[0]
    rows = -(-total // D)
    sizes = parts_of()
    def at(rank, relative):
        spot = 0
        for bit, weight in rank.items():
            spot = spot + jnp.where((relative & bit) != 0, weight, 0)
        return spot

    def body(place_ref, *refs):
        sources, outs, buffer = refs[:4], refs[4:-1], refs[-1]
        me = place_ref[0]
        mine = me // group
        for d in range(peers):
            relative = (me ^ d) & (group - 1)
            spots = [at(rank, relative) for rank in ranks]

            def lay(one, two, d=d, spots=spots):
                piece = jnp.concatenate([one[spots[0]], two[spots[1]]], 0).astype(jnp.float32)
                start, count = starts[d], counts[d]
                if shared[d]:
                    buffer[start : start + 1, :] = buffer[start : start + 1, :] + piece[:1]
                    buffer[start + 1 : start + count, :] = piece[1:count]
                else:
                    buffer[start : start + count, :] = piece[:count]

            @pl.when(mine == d // group)
            def _():
                lay(sources[0], sources[1])

            @pl.when(mine != d // group)
            def _():
                lay(sources[2], sources[3])

        count = jnp.zeros((1, D), jnp.float32)
        for source in (sources[1], sources[3]):
            for spot in range(group):
                count = count + source[spot, half - 1 : half, :].astype(jnp.float32)
        outs[-1][...] = count
        start = 0
        for out, size in zip(outs[:-1], sizes):
            out[:size, :] = buffer[start : start + size, :].astype(out.dtype)
            if out.shape[0] > size:
                out[size:, :] = jnp.zeros((out.shape[0] - size, D), out.dtype)
            start = start + size

    kinds = [jnp.bfloat16] * (4 + ROUNDS) + [jnp.float32]
    talls = [HALF] + sizes[1:]
    return pl.pallas_call(
        body,
        grid_spec=pltpu.PrefetchScalarGridSpec(
            num_scalar_prefetch=1,
            grid=(1,),
            in_specs=[whole(first.shape)] * 4,
            out_specs=[whole((tall, D)) for tall in talls + [1]],
            scratch_shapes=[pltpu.VMEM((-(-rows // 8) * 8 + 8, D), jnp.float32)],
        ),
        out_shape=[
            jax.ShapeDtypeStruct((tall, D), kind)
            for tall, kind in zip(talls + [1], kinds + [jnp.float32])
        ],
        compiler_params=LIMIT,
        cost_estimate=cost(4),
        name="spread_rows",
    )(place.reshape(1), first, second, first_far, second_far)


def collect_rows(parts, total, peers, place):
    starts, counts, shared, height = pieces_of(total, peers)
    rows = -(-total // D)
    sizes = [min(part.shape[0], size) for part, size in zip(parts, tall_parts())]
    group = lax.axis_size("space")

    def body(place_ref, *refs):
        sources, keep, send, buffer = refs[:-3], refs[-3], refs[-2], refs[-1]
        start = 0
        for source, size in zip(sources, sizes):
            buffer[start : start + size, :] = source[:size, :]
            start = start + size
        if buffer.shape[0] > start:
            buffer[start:, :] = jnp.zeros((buffer.shape[0] - start, D), jnp.float32)
        me = place_ref[0]
        mine = me // group
        for d in range(peers):
            relative = (me ^ d) & (group - 1)

            @pl.when(mine == d // group)
            def _():
                keep[relative] = buffer[starts[d] : starts[d] + height, :]

            @pl.when(mine != d // group)
            def _():
                send[relative] = buffer[starts[d] : starts[d] + height, :].astype(jnp.bfloat16)

    shape = (group, height, D)
    return pl.pallas_call(
        body,
        grid_spec=pltpu.PrefetchScalarGridSpec(
            num_scalar_prefetch=1,
            grid=(1,),
            in_specs=[whole(part.shape) for part in parts],
            out_specs=[whole(shape), whole(shape)],
            scratch_shapes=[pltpu.VMEM((-(-rows // 8) * 8 + height + 8, D), jnp.float32)],
        ),
        out_shape=[
            jax.ShapeDtypeStruct(shape, jnp.float32),
            jax.ShapeDtypeStruct(shape, jnp.bfloat16),
        ],
        compiler_params=LIMIT,
        cost_estimate=cost(5),
        name="collect_rows",
    )(place.reshape(1), *parts)


def reduced_piece(keep, send, leaving):
    kept = keep + swapped(send, "dp", 1).astype(jnp.float32)
    half = kept.shape[1] // 2
    groups = upper_groups()
    inner_shape = (kept.shape[0] // 4, 2, 2, half, D)
    parts = [kept[:, :half].reshape(inner_shape), kept[:, half:].reshape(inner_shape)]
    for n, order in enumerate(orders()):
        for bit in order:
            spot = 2 if bit == 1 and parts[n].ndim == 5 else 1
            stay = lax.index_in_dim(parts[n], 0, spot, keepdims=False)
            leave = lax.index_in_dim(parts[n], 1, spot, keepdims=False)
            parts[n] = stay + swapped(leave.astype(jnp.bfloat16), "space", bit).astype(jnp.float32)
    part = jnp.concatenate(parts, 1)
    part, leaving = lax.optimization_barrier((part, leaving))
    for bits in groups:
        part = part.reshape((-1, 1 << len(bits)) + part.shape[1:])
        masks = [sum(bit for n, bit in enumerate(bits) if m >> n & 1) for m in range(1 << len(bits))]
        low = part.astype(jnp.bfloat16)
        part = sum(
            [
                swapped(low[:, m], "space", mask).astype(jnp.float32)
                for m, mask in enumerate(masks)
                if m
            ],
            part[:, 0],
        )
    return part[0], leaving


def tall_parts():
    return [CH, D, D, CH] + [D] * (5 * ROUNDS) + [2] + [1] * (1 + 2 * ROUNDS)


def weave(ref, value):
    rows = value.shape[0]
    ref[pl.ds(0, rows, stride=2), :] = value[:, :HALF]
    ref[pl.ds(1, rows, stride=2), :] = value[:, HALF:]


def unweave(ref):
    rows = ref.shape[0] // 2
    return ref[pl.ds(0, rows, stride=2), :], ref[pl.ds(1, rows, stride=2), :]


def whole(shape):
    return pl.BlockSpec(shape, lambda *_: (0,) * len(shape))


def round_forward(index, mesh, before, own, after, mats, bias, following, decoder=()):
    blocks = mesh.shape[0]
    tile, chunk = 512, 16
    turns, high = tile // chunk, 2 * chunk
    more = following is not None
    spans = [before.shape[0], own.shape[0], after.shape[0]]
    reach = sum(spans)

    def body(*refs):
        index_ref, mesh_ref, before_ref, own_ref, after_ref, mats_ref, bias_ref = refs[:7]
        raw, table, rows, wide, wider, sems = refs[-6:]
        if more:
            next_ref, sent_ref = refs[7], refs[13]
            new_ref, back_ref, update_ref, agg_ref, slope_ref = refs[8:13]
        else:
            ids_ref, dec_ref, out_ref, head_ref = refs[7:11]
            new_ref, back_ref, update_ref, agg_ref, slope_ref = refs[11:16]
            branch_ref, fetched_ref, decoded_ref, turn_ref = refs[16:20]
            total_ref = refs[20]
        step = pl.program_id(0)

        @pl.when(step == 0)
        def _():
            copies = []
            start = 0
            for n, (source, span) in enumerate(zip((before_ref, own_ref, after_ref), spans)):
                copies.append(
                    pltpu.make_async_copy(source, raw.at[pl.ds(start, span)], sems.at[n])
                )
                start = start + span
            for copy in copies:
                copy.start()
            for copy in copies:
                copy.wait()

            @pl.loop(0, reach // 256)
            def _(i):
                at = pl.multiple_of(i * 256, 256)
                table[pl.ds(at, 256), :] = raw[pl.ds(at, 256), :].astype(jnp.float32)

        mesh_in = mesh_ref[...]
        lowered = mesh_in.astype(jnp.bfloat16)
        weave(wide, inner(lowered, mats_ref[1], 1, 0) + bias_ref[0:1, :])

        def fetch(turn):
            for edge in range(K):
                base = edge * blocks + step * tile + turn * chunk
                spots = [index_ref[base + u] for u in range(chunk)]
                values = [table[pl.ds(pl.multiple_of(spot, 2), 2), :] for spot in spots]
                for u in range(chunk):
                    spot = pl.multiple_of(edge * 2 * tile + turn * high + 2 * u, 2)
                    rows[pl.ds(spot, 2), :] = values[u]

        def load(turn):
            at = pl.multiple_of(turn * high, high)
            taken = [
                rows[pl.ds(pl.multiple_of(edge * 2 * tile + turn * high, high), high), :]
                for edge in range(K)
            ]
            return at, wide[pl.ds(at, high), :], taken

        def dense(at, dest, taken):
            total = None
            for edge in range(K):
                value = taken[edge] + dest
                sigma = sigmoid(value)
                out = value * sigma
                slope_ref[edge, pl.ds(at, high), :] = (sigma + out * (1.0 - sigma)).astype(
                    jnp.bfloat16
                )
                total = out if total is None else total + out
            wider[pl.ds(at, high), :] = total * (1.0 / K)

        def some(turn, carry):
            loaded = load(turn - 1)
            fetch(turn)
            dense(*loaded)
            return carry

        fetch(0)
        lax.fori_loop(1, turns, some, 0)
        dense(*load(turns - 1))
        first, second = unweave(wider)
        first, second = first.astype(jnp.bfloat16), second.astype(jnp.bfloat16)
        agg_ref[:, :HALF] = first
        agg_ref[:, HALF:] = second
        update_in = (
            inner(first, mats_ref[2, :HALF, :], 1, 0)
            + inner(second, mats_ref[2, HALF:, :], 1, 0)
            + inner(lowered, mats_ref[3], 1, 0)
            + bias_ref[1:2, :]
        )
        sigma = sigmoid(update_in)
        out = update_in * sigma
        back_ref[...] = sigma + out * (1.0 - sigma)
        update = out.astype(jnp.bfloat16)
        update_ref[...] = update
        new = mesh_in + inner(update, mats_ref[4], 1, 0)
        new_ref[...] = new
        lowered = new.astype(jnp.bfloat16)
        if more:
            weave(wide, inner(lowered, next_ref[0], 1, 0))
            sent_ref[...] = wide[...].astype(jnp.bfloat16)
            return
        nodes = lax.broadcasted_iota(jnp.int32, (ids_ref.shape[0], tile), 1) + step * tile
        chooser = jnp.where(nodes == ids_ref[...], 1.0, 0.0).astype(jnp.bfloat16)
        found = inner(chooser, lowered, 1, 0)

        @pl.when(step == 0)
        def _():
            total_ref[...] = found

        @pl.when(step > 0)
        def _():
            total_ref[...] += found

        @pl.when(step == blocks // tile - 1)
        def _():
            fetched = total_ref[...].astype(jnp.bfloat16)
            fetched_ref[...] = fetched
            value = inner(fetched, dec_ref[...], 1, 0) + head_ref[2:3, :]
            sigma = sigmoid(value)
            out = value * sigma
            turn_ref[...] = sigma + out * (1.0 - sigma)
            decoded = out.astype(jnp.bfloat16)
            decoded_ref[...] = decoded
            branch_ref[...] = inner(decoded, out_ref[...], 1, 0).astype(jnp.bfloat16)

    whole_rows = pl.BlockSpec((tile, D), lambda i, *_: (i, 0))
    woven = pl.BlockSpec((2 * tile, HALF), lambda i, *_: (i, 0))
    ins = [whole_rows] + [pl.BlockSpec(memory_space=pl.ANY)] * 3 + [whole(mats.shape), whole(bias.shape)]
    outs = [whole_rows] * 4 + [pl.BlockSpec((K, 2 * tile, HALF), lambda i, *_: (0, i, 0))]
    shapes = [
        jax.ShapeDtypeStruct((blocks, D), jnp.float32),
        jax.ShapeDtypeStruct((blocks, D), jnp.float32),
        jax.ShapeDtypeStruct((blocks, D), jnp.bfloat16),
        jax.ShapeDtypeStruct((blocks, D), jnp.bfloat16),
        jax.ShapeDtypeStruct((K, 2 * blocks, HALF), jnp.bfloat16),
    ]
    args = [index, mesh, before, own, after, mats, bias]
    if more:
        ins.append(pl.BlockSpec((1, D, D), lambda *_: (0, 0, 0)))
        outs.append(woven)
        shapes.append(jax.ShapeDtypeStruct((2 * blocks, HALF), jnp.bfloat16))
        args.append(following)
    scratch = []
    if decoder:
        posts = decoder[0].shape[0]
        ins = ins + [whole(arg.shape) for arg in decoder]
        args = args + list(decoder)
        for width, kind in ((HALF, jnp.bfloat16), (D, jnp.bfloat16), (D, jnp.bfloat16), (D, jnp.float32)):
            outs.append(whole((posts, width)))
            shapes.append(jax.ShapeDtypeStruct((posts, width), kind))
        scratch = [pltpu.VMEM((posts, D), jnp.float32)]
    return pl.pallas_call(
        body,
        grid_spec=pltpu.PrefetchScalarGridSpec(
            num_scalar_prefetch=1,
            grid=(blocks // tile,),
            in_specs=ins,
            out_specs=outs,
            scratch_shapes=scratch
            + [
                pltpu.VMEM((reach, HALF), jnp.bfloat16),
                pltpu.VMEM((reach, HALF), jnp.float32),
                pltpu.VMEM((K * 2 * tile, HALF), jnp.float32),
                pltpu.VMEM((2 * tile, HALF), jnp.float32),
                pltpu.VMEM((2 * tile, HALF), jnp.float32),
                pltpu.SemaphoreType.DMA((3,)),
            ],
        ),
        out_shape=shapes,
        compiler_params=LIMIT,
        cost_estimate=cost(25),
        name="round_forward",
    )(*args)


def edges_backward(index, grad_mesh, back, slopes, mats, carried=(), landed=()):
    blocks = back.shape[0]
    tile, chunk = 512, 16
    steps, turns, high = blocks // tile, tile // chunk, 2 * chunk
    reach = 2 * (blocks + 2 * H)

    def body(*refs):
        if carried:
            index_ref, grad_ref, back_ref, slope_ref, mats_ref = refs[:5]
            past, rest = refs[5:11], refs[11:]
            (new_ref, out_ref, sent_ref), rest = rest[:3], rest[3:]
        else:
            index_ref, back_ref, slope_ref, mats_ref = refs[:4]
            (ids_ref, landed_ref, turn_ref, w_out_ref, w_dec_ref), rest = refs[4:9], refs[9:]
            (new_ref, out_ref, gdec_ref), rest = rest[:3], rest[3:]
            gathered, rest = rest[5], rest[:5] + rest[6:]
        guin_ref, low_ref, before_ref, own_ref, after_ref, wide, wider, flows, *tables = rest
        step = pl.program_id(0)

        @pl.when(step == 0)
        def _():
            @pl.loop(0, reach // 256)
            def _(i):
                for table in tables:
                    table[pl.ds(pl.multiple_of(i * 256, 256), 256), :] = jnp.zeros(
                        (256, HALF), jnp.float32
                    )

        if carried:
            new = ended(grad_ref, *past, sent_ref, wide)
            new_ref[...] = new
            grad_out = new.astype(jnp.bfloat16)
            out_ref[...] = grad_out
        else:

            @pl.when(step == 0)
            def _():
                grad_dec = inner(landed_ref[...], w_out_ref[...], 1, 1) * turn_ref[...]
                grad_dec = grad_dec.astype(jnp.bfloat16)
                gdec_ref[...] = grad_dec
                gathered[...] = inner(grad_dec, w_dec_ref[...], 1, 1).astype(jnp.bfloat16)

            nodes = lax.broadcasted_iota(jnp.int32, (tile, landed_ref.shape[0]), 0) + step * tile
            chooser = jnp.where(nodes == ids_ref[...], 1.0, 0.0).astype(jnp.bfloat16)
            new = inner(chooser, gathered[...], 1, 0)
            new_ref[...] = new
            grad_out = new.astype(jnp.bfloat16)
            out_ref[...] = grad_out
        grad_uin = (inner(grad_out, mats_ref[4], 1, 1) * back_ref[...]).astype(jnp.bfloat16)
        guin_ref[...] = grad_uin
        weave(wide, inner(grad_uin, mats_ref[2], 1, 1) * (1.0 / K))

        def dense(turn):
            at = pl.multiple_of(turn * high, high)
            grad_agg = wide[pl.ds(at, high), :]
            total, parts = None, []
            for edge in range(K):
                flow = grad_agg * slope_ref[edge, pl.ds(at, high), :].astype(jnp.float32)
                parts.append(flow)
                total = flow if total is None else total + flow
            return at, total, parts

        def keep(turn, at, total, parts):
            for edge in range(K):
                spot = pl.multiple_of(edge * 2 * tile + turn * high, high)
                flows[pl.ds(spot, high), :] = parts[edge]
            wider[pl.ds(at, high), :] = total

        def scatter(turn):
            for u in range(chunk):
                spots, sums = [], []
                for edge in range(K):
                    base = edge * blocks + step * tile + turn * chunk
                    spots.append(pl.multiple_of(index_ref[base + u], 2))
                for edge in range(K):
                    spot = pl.multiple_of(edge * 2 * tile + turn * high + 2 * u, 2)
                    sums.append(tables[edge][pl.ds(spots[edge], 2), :] + flows[pl.ds(spot, 2), :])
                for edge in range(K):
                    tables[edge][pl.ds(spots[edge], 2), :] = sums[edge]

        def some(turn, carry):
            found = dense(turn)
            scatter(turn - 1)
            keep(turn, *found)
            return carry

        keep(0, *dense(0))
        lax.fori_loop(1, turns, some, 0)
        scatter(turns - 1)
        first, second = unweave(wider)
        low_ref[:, :HALF] = first.astype(jnp.bfloat16)
        low_ref[:, HALF:] = second.astype(jnp.bfloat16)

        @pl.when(step == steps - 1)
        def _():
            def summed(at):
                value = tables[0][pl.ds(at, 256), :]
                for table in tables[1:]:
                    value = value + table[pl.ds(at, 256), :]
                return value

            @pl.loop(0, 2 * H // 256)
            def _(i):
                at = pl.multiple_of(i * 256, 256)
                far = pl.multiple_of(2 * H + 2 * blocks + at, 256)
                before_ref[pl.ds(at, 256), :] = summed(at).astype(jnp.bfloat16)
                after_ref[pl.ds(at, 256), :] = summed(far).astype(jnp.bfloat16)

            @pl.loop(0, 2 * blocks // 256)
            def _(i):
                at = pl.multiple_of(i * 256, 256)
                own_ref[pl.ds(at, 256), :] = summed(pl.multiple_of(2 * H + at, 256))

    rows = pl.BlockSpec((tile, D), lambda i, *_: (i, 0))
    woven = pl.BlockSpec((2 * tile, HALF), lambda i, *_: (i, 0))
    low = jax.ShapeDtypeStruct((blocks, D), jnp.bfloat16)
    low_posts = (landed[1].shape[0], D) if landed else None
    last = low if carried else jax.ShapeDtypeStruct(low_posts, jnp.bfloat16)
    return pl.pallas_call(
        body,
        grid_spec=pltpu.PrefetchScalarGridSpec(
            num_scalar_prefetch=1,
            grid=(steps,),
            in_specs=([rows] if carried else [])
            + [
                rows,
                pl.BlockSpec((K, 2 * tile, HALF), lambda i, *_: (0, i, 0)),
                whole(mats.shape),
            ]
            + ([woven] * 3 + [rows] * 2 + [whole(mats.shape)] if carried else [])
            + [whole(arg.shape) for arg in landed],
            out_specs=([rows] * 3 if carried else [rows, rows, whole(low_posts)])
            + [
                rows, rows,
                whole((2 * H, HALF)), whole((2 * blocks, HALF)), whole((2 * H, HALF)),
            ],
            scratch_shapes=([] if carried else [pltpu.VMEM(low_posts, jnp.bfloat16)])
            + [
                pltpu.VMEM((2 * tile, HALF), jnp.float32),
                pltpu.VMEM((2 * tile, HALF), jnp.float32),
                pltpu.VMEM((2 * tile * K, HALF), jnp.float32),
            ]
            + [pltpu.VMEM((reach, HALF), jnp.float32)] * K,
        ),
        out_shape=[
            jax.ShapeDtypeStruct((blocks, D), jnp.float32),
            low,
            last,
            low,
            low,
            jax.ShapeDtypeStruct((2 * H, HALF), jnp.bfloat16),
            jax.ShapeDtypeStruct((2 * blocks, HALF), jnp.float32),
            jax.ShapeDtypeStruct((2 * H, HALF), jnp.bfloat16),
        ],
        compiler_params=LIMIT,
        cost_estimate=cost(28 if carried else 25),
        name="edges_backward",
    )(index, *([grad_mesh] if carried else []), back, slopes, mats, *carried, *landed)


def ended(grad_ref, own_ref, first_ref, last_ref, guin_ref, dest_ref, mats_ref, sent_ref, wide):
    wide[...] = (
        own_ref[...] + first_ref[...].astype(jnp.float32) + last_ref[...].astype(jnp.float32)
    )
    one, two = unweave(wide)
    one, two = one.astype(jnp.bfloat16), two.astype(jnp.bfloat16)
    sent_ref[:, :HALF] = one
    sent_ref[:, HALF:] = two
    return (
        grad_ref[...]
        + inner(guin_ref[...], mats_ref[3], 1, 1)
        + inner(dest_ref[...], mats_ref[1], 1, 1)
        + inner(one, mats_ref[0, :, :HALF], 1, 1)
        + inner(two, mats_ref[0, :, HALF:], 1, 1)
    )


def round_backward(grad_mesh, own, first, last, grad_uin, dest_low, mats):
    blocks = grad_mesh.shape[0]
    tile = 1024

    def body(*refs):
        new_ref, out_ref, sent_ref, wide = refs[-4:]
        new = ended(*refs[:-4], sent_ref, wide)
        new_ref[...] = new
        out_ref[...] = new.astype(jnp.bfloat16)

    rows = pl.BlockSpec((tile, D), lambda i: (i, 0))
    woven = pl.BlockSpec((2 * tile, HALF), lambda i: (i, 0))
    low = jax.ShapeDtypeStruct((blocks, D), jnp.bfloat16)
    return pl.pallas_call(
        body,
        grid=(blocks // tile,),
        in_specs=[rows, woven, woven, woven, rows, rows, whole(mats.shape)],
        out_specs=[rows, rows, rows],
        out_shape=[jax.ShapeDtypeStruct((blocks, D), jnp.float32), low, low],
        scratch_shapes=[pltpu.VMEM((2 * tile, HALF), jnp.float32)],
        compiler_params=LIMIT,
        cost_estimate=cost(7),
        name="round_backward",
    )(grad_mesh, own, first, last, grad_uin, dest_low, mats)


def encode_rows(arrived, ids, w_in, w_node, biases, source):
    posts = arrived.shape[0]
    tile = 512

    def body(arrived_ref, ids_ref, in_ref, node_ref, bias_ref, source_ref, mesh_ref, gathered_ref, sent_ref, encoded, wide):
        step = pl.program_id(0)

        @pl.when(step == 0)
        def _():
            entering = inner(arrived_ref[...], in_ref[...], 1, 0) + bias_ref[0:1, :]
            encoded[...] = silu(entering).astype(jnp.bfloat16)

        nodes = lax.broadcasted_iota(jnp.int32, (tile, posts), 0) + step * tile
        chooser = jnp.where(nodes == ids_ref[...], 1.0, 0.0).astype(jnp.bfloat16)
        gathered = inner(chooser, encoded[...], 1, 0).astype(jnp.bfloat16)
        gathered_ref[...] = gathered
        mesh = silu(inner(gathered, node_ref[...], 1, 0) + bias_ref[1:2, :])
        mesh_ref[...] = mesh
        weave(wide, inner(mesh.astype(jnp.bfloat16), source_ref[0], 1, 0))
        sent_ref[...] = wide[...].astype(jnp.bfloat16)

    rows = pl.BlockSpec((tile, D), lambda i: (i, 0))
    args = (arrived, ids, w_in, w_node, biases, source)
    return pl.pallas_call(
        body,
        grid=(H // tile,),
        in_specs=[whole(arg.shape) for arg in args[:-1]]
        + [pl.BlockSpec((1, D, D), lambda *_: (0, 0, 0))],
        out_specs=[rows, rows, pl.BlockSpec((2 * tile, HALF), lambda i: (i, 0))],
        out_shape=[
            jax.ShapeDtypeStruct((H, D), jnp.float32),
            jax.ShapeDtypeStruct((H, D), jnp.bfloat16),
            jax.ShapeDtypeStruct((2 * H, HALF), jnp.bfloat16),
        ],
        scratch_shapes=[pltpu.VMEM((posts, D), jnp.bfloat16), pltpu.VMEM((2 * tile, HALF), jnp.float32)],
        compiler_params=LIMIT,
        cost_estimate=cost(5),
        name="encode_rows",
    )(*args)


def encode_backward(grad_mesh, gathered, arrived, ids, w_in, w_node, biases):
    posts = arrived.shape[0]
    tile = 512
    steps = H // tile

    def body(grad_ref, gathered_ref, arrived_ref, ids_ref, in_ref, node_ref, bias_ref, gin_ref, gnode_ref, gbias_ref, total):
        step = pl.program_id(0)

        @pl.when(step == 0)
        def _():
            total[...] = jnp.zeros(total.shape, jnp.float32)
            gnode_ref[...] = jnp.zeros(gnode_ref.shape, jnp.float32)
            gbias_ref[...] = jnp.zeros(gbias_ref.shape, jnp.float32)

        node_in = inner(gathered_ref[...], node_ref[...], 1, 0) + bias_ref[1:2, :]
        grad_node = (grad_ref[...] * slope(node_in)).astype(jnp.bfloat16)
        gbias_ref[1:2, :] += jnp.sum(grad_node.astype(jnp.float32), 0, keepdims=True)
        gnode_ref[...] += inner(gathered_ref[...], grad_node, 0, 0)
        back = inner(grad_node, node_ref[...], 1, 1).astype(jnp.bfloat16)
        nodes = lax.broadcasted_iota(jnp.int32, (posts, tile), 1) + step * tile
        chooser = jnp.where(nodes == ids_ref[...], 1.0, 0.0).astype(jnp.bfloat16)
        total[...] += inner(chooser, back, 1, 0)

        @pl.when(step == steps - 1)
        def _():
            entering = inner(arrived_ref[...], in_ref[...], 1, 0) + bias_ref[0:1, :]
            grad_enc = (total[...] * slope(entering)).astype(jnp.bfloat16)
            gbias_ref[0:1, :] = jnp.sum(grad_enc.astype(jnp.float32), 0, keepdims=True)
            gin_ref[...] = inner(arrived_ref[...], grad_enc, 0, 0)

    rows = pl.BlockSpec((tile, D), lambda i: (i, 0))
    args = (grad_mesh, gathered, arrived, ids, w_in, w_node, biases)
    shapes = [(HALF, D), (D, D), (2, D)]
    return pl.pallas_call(
        body,
        grid=(steps,),
        in_specs=[rows, rows] + [whole(arg.shape) for arg in args[2:]],
        out_specs=[whole(shape) for shape in shapes],
        out_shape=[jax.ShapeDtypeStruct(shape, jnp.float32) for shape in shapes],
        scratch_shapes=[pltpu.VMEM((posts, D), jnp.float32)],
        compiler_params=LIMIT,
        cost_estimate=cost(7),
        name="encode_backward",
    )(*args)


def shards(walk, master, moment1, moment2, inputs, targets, valid, owner, slot, neighbours, partner):
    bands = lax.axis_size("space")
    band = lax.axis_index("space")
    peers = lax.axis_size(ALL)
    place = lax.axis_index(ALL)
    shard = master.shape[0]
    total_size = shard * peers
    height = pieces_of(total_size, peers)[3]
    offset = lax.rem(lax.rem(shard, D) * place, D)
    piece = lax.dynamic_update_slice_in_dim(
        jnp.zeros((height * D,), jnp.bfloat16), master.astype(jnp.bfloat16), offset, 0
    )
    state_in = inputs[0]
    counted = valid[0].astype(jnp.float32)
    local_count = jnp.sum(valid[0])
    digits = (local_count >> jnp.array([16, 8, 0], jnp.int32)) & 255
    piece = lax.dynamic_update_slice(
        piece.reshape(height, D), digits.astype(jnp.bfloat16)[None, :], (height - 1, 0)
    )
    points = state_in.shape[1]
    blocks = neighbours.shape[0]
    assert blocks == H
    capacity = max(2, 2 * points // bands)
    target_band = owner[0, :, 0]
    hits = (target_band[:, None] == jnp.arange(bands, dtype=jnp.int32)[None, :]).astype(jnp.int32)
    ranks = jnp.sum(jnp.cumsum(hits, 0) * hits, 1) - 1
    places_out = jnp.sum(hits * jnp.asarray(walk, jnp.int32)[None, :], 1) * capacity + ranks
    poster = (
        jnp.arange(bands * capacity, dtype=jnp.int32)[:, None] == places_out[None, :]
    ).astype(jnp.bfloat16)
    spots = slot[0][None, :]
    columns = jnp.concatenate(
        [
            state_in,
            (spots // 64).astype(jnp.bfloat16),
            (spots % 64).astype(jnp.bfloat16),
            jnp.ones((1, points), jnp.bfloat16),
            jnp.zeros((HALF - CH - 3, points), jnp.bfloat16),
        ],
        0,
    )

    def exchanged(rows):
        return lax.all_to_all(
            rows.reshape(bands, capacity, HALF), "space", split_axis=0, concat_axis=0, tiled=True
        ).reshape(bands * capacity, HALF)

    held, posted = gathered_blocks(piece, inner(poster, columns, 1, 1).astype(jnp.bfloat16))
    arrived = exchanged(posted)
    w_in, w_node, w_dec, w_out, *w_round, biases, digits = spread_rows(
        held, total_size, peers, place
    )
    count = digits[0, 0] * 65536.0 + digits[0, 1] * 256.0 + digits[0, 2]
    w_out = jnp.pad(w_out.reshape(D, CH), ((0, 0), (0, HALF - CH)))
    w_round = [mats.reshape(5, D, D) for mats in w_round]
    b_head = biases[:3]
    b_round = biases[3:].reshape(ROUNDS, 2, D)
    arrived, biases = lax.optimization_barrier((arrived, biases))
    ids = arrived[:, CH : CH + 3].astype(jnp.int32)
    ids = jnp.where(ids[:, 2:3] > 0, ids[:, 0:1] * 64 + ids[:, 1:2], -1)
    ids_row = ids.reshape(1, -1)
    mesh, gathered, sent = encode_rows(
        arrived, ids_row, w_in, w_node, biases, w_round[0]
    )
    sent, partner, neighbours, counted = lax.optimization_barrier(
        (sent, partner, neighbours, counted)
    )
    index = 2 * ((neighbours - band * blocks + H) % (blocks * bands)).T.reshape(-1)
    moved = [(n, place) for n, place in enumerate(walk) if n != place]
    stays = jnp.asarray([n == place for n, place in enumerate(walk)])[band]
    index = jnp.where(stays, index, lax.ppermute(index, "space", moved))

    def at_home(rows):
        return lax.ppermute(rows, "space", [(j, i) for i, j in moved])

    def settled(own, came):
        return jnp.where(stays, own, came.astype(jnp.float32))

    partner_by = partner - band * points - jnp.arange(points, dtype=jnp.int32)
    coded = jnp.where(partner_by >= NEAR, partner_by - NEAR + 1, 0).astype(jnp.bfloat16)
    low_valid = jnp.concatenate([counted.astype(jnp.bfloat16), coded[None, :]], 0)
    valid_around = jnp.concatenate(
        [
            shifted(low_valid[:, points - ROWW :], "space", 1),
            low_valid,
            shifted(low_valid[:, :ROWW], "space", -1),
        ],
        1,
    )
    kept = []
    for layer in range(ROUNDS):
        before, after = halo(walk, sent[2 * (blocks - H) :], sent[: 2 * H])
        if layer == 0:
            before, valid_around = lax.optimization_barrier((before, valid_around))
        following = w_round[layer + 1] if layer + 1 < ROUNDS else None
        new, back, update, agg, slopes, *rest = round_forward(
            index, mesh, before, sent, after, w_round[layer], b_round[layer], following,
            () if following is not None else (ids, w_dec, w_out, biases),
        )
        kept.append((mesh, back, update, agg, slopes))
        mesh = new
        sent = rest[0]
    wide_valid = valid_around[:CH].astype(jnp.float32)
    coded = valid_around[CH : CH + 1, : points + ROWW].astype(jnp.float32)
    weights = [
        (
            by,
            jnp.where(coded == by - NEAR + 1, 1.0, 0.0)
            * wide_valid[:, : points + ROWW]
            * wide_valid[:, by : by + points + ROWW],
        )
        for by in range(NEAR, ROWW + 1)
    ]
    branch_rows, fetched, decoded, dec_turn = rest
    returned = exchanged(branch_rows)
    branch = inner(returned, poster, 0, 0)[:CH]
    err = state_in.astype(jnp.float32) + branch - targets[0].astype(jnp.float32)
    def widened(values):
        low = values.astype(jnp.bfloat16)
        before = shifted(low[:, points - ROWW :], "space", 1).astype(jnp.float32)
        after = shifted(low[:, :ROWW], "space", -1).astype(jnp.float32)
        return jnp.concatenate([before, values, after], 1)

    wide_err = widened(err)
    paired = jnp.zeros((CH, points + ROWW), jnp.float32)
    pair_total = jnp.zeros((CH, points), jnp.float32)
    for by, both in weights:
        gap = both * (wide_err[:, : points + ROWW] - wide_err[:, by : by + points + ROWW])
        paired = paired + gap
        pair_total = pair_total + gap[:, ROWW:] * (
            wide_err[:, ROWW : ROWW + points] - wide_err[:, ROWW + by : ROWW + by + points]
        )
    local_total = jnp.sum(counted * err * err) + 0.5 * jnp.sum(pair_total)
    grad_pred = 2.0 * counted * err + paired[:, ROWW:]
    for by, both in weights:
        gap = both * (wide_err[:, : points + ROWW] - wide_err[:, by : by + points + ROWW])
        grad_pred = grad_pred - gap[:, ROWW - by : ROWW - by + points]
    grad_pred = grad_pred / count
    grad_rows = jnp.pad(grad_pred.astype(jnp.bfloat16), ((0, HALF - CH), (0, 0)))
    landed = exchanged(inner(poster, grad_rows, 1, 1).astype(jnp.bfloat16))
    landed, final_mesh = lax.optimization_barrier((landed, mesh.astype(jnp.bfloat16)))
    final_mesh = at_home(final_mesh)
    mats_grads = [None] * (5 * ROUNDS)
    bias_grads = [None] * (2 * ROUNDS)
    carried, grad_mesh = (), None
    for layer in reversed(range(ROUNDS)):
        old, back, update, agg, slopes = kept[layer]
        first_step = not carried
        grad_mesh, leaving, extra, grad_uin, dest_low, to_before, own, to_after = edges_backward(
            index, grad_mesh, back, slopes, w_round[layer], carried,
            (ids_row, landed, dec_turn, w_out, w_dec) if first_step else (),
        )
        if not first_step:
            mats_grads[5 * layer + 5] = inner(
                kept[layer + 1][0].astype(jnp.bfloat16), extra, 0, 0
            )
        else:
            grad_wout = inner(decoded, landed, 0, 0)[:, :CH]
            grad_bdec = jnp.sum(extra.astype(jnp.float32), 0, keepdims=True)
            grad_wdec = inner(fetched, extra, 0, 0)
            to_before, to_after, final_mesh = lax.optimization_barrier(
                (to_before, to_after, final_mesh)
            )
        from_before, from_after = halo(walk, to_after, to_before)
        if first_step:
            from_before, final_mesh = lax.optimization_barrier(
                (from_before, settled(mesh, final_mesh))
            )
        lowered = old.astype(jnp.bfloat16)
        mats_grads[5 * layer + 1 : 5 * layer + 5] = [
            inner(lowered, dest_low, 0, 0),
            inner(agg, grad_uin, 0, 0),
            inner(lowered, grad_uin, 0, 0),
            inner(update, leaving, 0, 0),
        ]
        bias_grads[2 * layer] = jnp.sum(dest_low.astype(jnp.float32), 0, keepdims=True)
        bias_grads[2 * layer + 1] = jnp.sum(grad_uin.astype(jnp.float32), 0, keepdims=True)
        carried = (own, from_before, from_after, grad_uin, dest_low, w_round[layer])
    grad_mesh, leaving, sent_low = round_backward(grad_mesh, *carried)
    mats_grads[0] = inner(kept[0][0].astype(jnp.bfloat16), sent_low, 0, 0)
    grad_win, grad_wnode, grad_bpair = encode_backward(
        grad_mesh, gathered, arrived, ids, w_in, w_node, biases
    )
    parts = [grad_win, grad_wnode, grad_wdec, grad_wout.reshape(CH, D)]
    parts = parts + mats_grads
    parts = parts + [grad_bpair, grad_bdec] + bias_grads
    keep, send = collect_rows(parts, total_size, peers, place)
    mine, leaving = reduced_piece(keep, send, leaving)
    late = at_home(leaving)
    mine = lax.dynamic_slice_in_dim(mine.reshape(-1), offset, shard)
    lane = lax.broadcasted_iota(jnp.int32, (8, HALF), 1)
    sums, late = summed_everywhere(
        jnp.where(lane == 0, local_total, jnp.sum(mine * mine)), late
    )
    total, norm = sums[0, 0], jnp.sqrt(sums[0, 1])
    node_grads = settled(grad_mesh, late)
    clipped = mine * jnp.minimum(1.0, 0.05 / norm)
    first = 0.9 * moment1 + 0.1 * clipped
    second = 0.999 * moment2 + 0.001 * clipped * clipped
    first_hat = first / (1.0 - 0.9**STEP)
    second_hat = second / (1.0 - 0.999**STEP)
    updated = master - 0.1 * (first_hat / (jnp.sqrt(second_hat) + 1e-08) + 0.1 * master)
    return (
        total.reshape(1),
        count.reshape(1),
        norm.reshape(1),
        updated,
        first,
        second,
        updated.astype(jnp.bfloat16),
        final_mesh.reshape(1, blocks, D),
        node_grads.reshape(1, blocks, D),
        grad_pred.reshape(1, grad_pred.shape[0], points),
    )


def solution(mesh):
    return jax.shard_map(
        functools.partial(shards, walk_of(mesh)),
        mesh=mesh,
        in_specs=(
            P(("dp", "space")),
            P(("dp", "space")),
            P(("dp", "space")),
            P("dp", None, "space"),
            P("dp", None, "space"),
            P("dp", None, "space"),
            P("dp", "space", None),
            P("dp", "space"),
            P("space", None),
            P("space"),
        ),
        out_specs=(
            P(),
            P(),
            P(),
            P(("dp", "space")),
            P(("dp", "space")),
            P(("dp", "space")),
            P(("dp", "space")),
            P("dp", "space", None),
            P("dp", "space", None),
            P("dp", None, "space"),
        ),
        check_vma=False,
    )
```

```python
import functools

import jax
import jax.numpy as jnp
from jax import lax
from jax.experimental import pallas as pl
from jax.experimental.pallas import tpu as pltpu
from jax.sharding import PartitionSpec as P

D = 256
HALF = 128
CH = 78
ROUNDS = 3
K = 6
ROWW = 360
NEAR = 358
STEP = 10
H = 2048
ALL = ("dp", "space")
LIMIT = pltpu.CompilerParams(vmem_limit_bytes=60 * 2**20)


def cost(micros):
    return pl.CostEstimate(flops=0, bytes_accessed=micros * 3_000_000, transcendentals=0)


def inner(left, right, left_dim, right_dim):
    return lax.dot_general(
        left, right, (((left_dim,), (right_dim,)), ((), ())), preferred_element_type=jnp.float32
    )


def sigmoid(value):
    return 0.5 * jnp.tanh(0.5 * value) + 0.5


def silu(value):
    return value * sigmoid(value)


def slope(value):
    sigma = sigmoid(value)
    return sigma * (1.0 + value * (1.0 - sigma))


def shifted(shard, axis, by):
    peers = lax.axis_size(axis)
    pairs = [(i, i + by) for i in range(peers) if 0 <= i + by < peers]
    return lax.ppermute(shard, axis, pairs)


def walk_of(mesh):
    count = mesh.shape["space"]
    chips = [getattr(device, "coords", None) for device in mesh.devices[0].reshape(-1)]
    if any(chip is None for chip in chips) or len(set(map(tuple, chips))) != count:
        return list(range(count))
    at = {tuple(chip): n for n, chip in enumerate(chips)}
    xs, ys, zs = (sorted({chip[n] for chip in at}) for n in range(3))
    if len(xs) * len(ys) * len(zs) != count:
        return list(range(count))
    if (len(xs), len(ys), len(zs)) == (2, 2, 4):
        corners = [(0, 0), (1, 0), (0, 1), (1, 1)]
        planes = [(0, 1, 3, 2), (2, 0, 1, 3), (3, 1, 0, 2), (2, 3, 1, 0)]
        steps = [(*corners[n], z) for z, plane in enumerate(planes) for n in plane]
        return [at[(xs[x], ys[y], zs[z])] for x, y, z in steps]
    walk, plane = [], []
    for n, y in enumerate(ys):
        plane = plane + [(x, y) for x in (xs if n % 2 == 0 else xs[::-1])]
    for n, z in enumerate(zs):
        walk = walk + [at[(x, y, z)] for x, y in (plane if n % 2 == 0 else plane[::-1])]
    return walk


def staggered(walk, last, initial):
    peers = lax.axis_size("space")
    up = list(zip(walk, walk[1:] + walk[:1]))
    before, after = [], []
    for core in (1, 0):
        pairs = [(core * peers + i, core * peers + j) for i, j in up]
        before.append(lax.ppermute(last, ALL, pairs))
        after.append(lax.ppermute(initial, ALL, [(j, i) for i, j in pairs]))
        if core == 1:
            word = jnp.concatenate([before[0][:16], after[0][:16]], 0)
            word = lax.ppermute(word, "dp", [(1, 0)])
            last, initial, word = lax.optimization_barrier((last, initial, word))
    return before, after + [word]


def halo(walk, last, initial):
    up = list(zip(walk, walk[1:] + walk[:1]))
    down = [(j, i) for i, j in up]
    return lax.ppermute(last, "space", up), lax.ppermute(initial, "space", down)


def pieces_of(total, peers):
    share = total // peers
    starts = [share * d // D for d in range(peers)]
    counts = [-(-share * (d + 1) // D) - starts[d] for d in range(peers)]
    shared = [share * d % D != 0 for d in range(peers)]
    height = -(-(max(counts) + 1) // 16) * 16
    return starts, counts, shared, height


def parts_of():
    return [CH, D, D, CH] + [5 * D] * ROUNDS + [3 + 2 * ROUNDS]


def swapped(value, axis, bit):
    return lax.ppermute(value, axis, [(i, i ^ bit) for i in range(lax.axis_size(axis))])


def bits_of(axis):
    return [1 << n for n in range(lax.axis_size(axis).bit_length() - 1)]


def others(value, axis, bits):
    masks = [sum(bit for n, bit in enumerate(bits) if m >> n & 1) for m in range(1, 1 << len(bits))]
    return [swapped(value, axis, mask) for mask in masks]


def upper_groups():
    bits = bits_of("space")[2:]
    return [tuple(bits[n : n + 2]) for n in range(0, len(bits), 2)]


def orders():
    return [(1, 2), (2, 1)]


def summed_everywhere(value, arriving):
    for bits in reversed(upper_groups()):
        value = sum(others(value, "space", bits), value)
    value = value + swapped(value, "dp", 1)
    value, arriving = lax.optimization_barrier((value, arriving))
    return sum(others(value, "space", (1, 2)), value), arriving


def gathered_blocks(piece, posted):
    held, weights, size = piece[None], {}, 1
    for bits in reversed(upper_groups()):
        held = jnp.concatenate([held] + others(held, "space", bits), 0)
        for n, bit in enumerate(bits):
            weights[bit] = size << n
        size = size << len(bits)
    half = piece.shape[0] // 2
    held = [held[:, :half], held[:, half:]]
    ranks = [dict(weights), dict(weights)]
    for turn in (1, 0):
        if turn == 1:
            held[0], held[1], posted = lax.optimization_barrier((*held, posted))
        for n, order in enumerate(orders()):
            held[n] = jnp.concatenate([held[n], swapped(held[n], "space", order[turn])], 0)
            ranks[n][order[turn]] = size
        size = size << 1
    return (held, [swapped(part, "dp", 1) for part in held], ranks), posted


def spread_rows(gathered, total, peers, place):
    (first, second), (first_far, second_far), ranks = gathered
    starts, counts, shared, height = pieces_of(total, peers)
    half, group = height // 2, first.shape[0]
    rows = -(-total // D)
    sizes = parts_of()
    def at(rank, relative):
        spot = 0
        for bit, weight in rank.items():
            spot = spot + jnp.where((relative & bit) != 0, weight, 0)
        return spot

    def body(place_ref, *refs):
        sources, outs, buffer = refs[:4], refs[4:-1], refs[-1]
        me = place_ref[0]
        mine = me // group
        for d in range(peers):
            relative = (me ^ d) & (group - 1)
            spots = [at(rank, relative) for rank in ranks]

            def lay(one, two, d=d, spots=spots):
                piece = jnp.concatenate([one[spots[0]], two[spots[1]]], 0).astype(jnp.float32)
                start, count = starts[d], counts[d]
                if shared[d]:
                    buffer[start : start + 1, :] = buffer[start : start + 1, :] + piece[:1]
                    buffer[start + 1 : start + count, :] = piece[1:count]
                else:
                    buffer[start : start + count, :] = piece[:count]

            @pl.when(mine == d // group)
            def _():
                lay(sources[0], sources[1])

            @pl.when(mine != d // group)
            def _():
                lay(sources[2], sources[3])

        count = jnp.zeros((1, D), jnp.float32)
        for source in (sources[1], sources[3]):
            for spot in range(group):
                count = count + source[spot, half - 1 : half, :].astype(jnp.float32)
        outs[-1][...] = count
        start = 0
        for out, size in zip(outs[:-1], sizes):
            out[:size, :] = buffer[start : start + size, :].astype(out.dtype)
            if out.shape[0] > size:
                out[size:, :] = jnp.zeros((out.shape[0] - size, D), out.dtype)
            start = start + size

    kinds = [jnp.bfloat16] * (4 + ROUNDS) + [jnp.float32]
    talls = [HALF] + sizes[1:]
    return pl.pallas_call(
        body,
        grid_spec=pltpu.PrefetchScalarGridSpec(
            num_scalar_prefetch=1,
            grid=(1,),
            in_specs=[whole(first.shape)] * 4,
            out_specs=[whole((tall, D)) for tall in talls + [1]],
            scratch_shapes=[pltpu.VMEM((-(-rows // 8) * 8 + 8, D), jnp.float32)],
        ),
        out_shape=[
            jax.ShapeDtypeStruct((tall, D), kind)
            for tall, kind in zip(talls + [1], kinds + [jnp.float32])
        ],
        compiler_params=LIMIT,
        cost_estimate=cost(4),
        name="spread_rows",
    )(place.reshape(1), first, second, first_far, second_far)


def collect_rows(parts, total, peers, place):
    starts, counts, shared, height = pieces_of(total, peers)
    rows = -(-total // D)
    sizes = [min(part.shape[0], size) for part, size in zip(parts, tall_parts())]
    group = lax.axis_size("space")

    def body(place_ref, *refs):
        sources, keep, send, buffer = refs[:-3], refs[-3], refs[-2], refs[-1]
        start = 0
        for source, size in zip(sources, sizes):
            buffer[start : start + size, :] = source[:size, :]
            start = start + size
        if buffer.shape[0] > start:
            buffer[start:, :] = jnp.zeros((buffer.shape[0] - start, D), jnp.float32)
        me = place_ref[0]
        mine = me // group
        for d in range(peers):
            relative = (me ^ d) & (group - 1)

            @pl.when(mine == d // group)
            def _():
                keep[relative] = buffer[starts[d] : starts[d] + height, :]

            @pl.when(mine != d // group)
            def _():
                send[relative] = buffer[starts[d] : starts[d] + height, :].astype(jnp.bfloat16)

    shape = (group, height, D)
    return pl.pallas_call(
        body,
        grid_spec=pltpu.PrefetchScalarGridSpec(
            num_scalar_prefetch=1,
            grid=(1,),
            in_specs=[whole(part.shape) for part in parts],
            out_specs=[whole(shape), whole(shape)],
            scratch_shapes=[pltpu.VMEM((-(-rows // 8) * 8 + height + 8, D), jnp.float32)],
        ),
        out_shape=[
            jax.ShapeDtypeStruct(shape, jnp.float32),
            jax.ShapeDtypeStruct(shape, jnp.bfloat16),
        ],
        compiler_params=LIMIT,
        cost_estimate=cost(5),
        name="collect_rows",
    )(place.reshape(1), *parts)


def reduced_piece(keep, send, leaving):
    kept = keep + swapped(send, "dp", 1).astype(jnp.float32)
    half = kept.shape[1] // 2
    groups = upper_groups()
    inner_shape = (kept.shape[0] // 4, 2, 2, half, D)
    parts = [kept[:, :half].reshape(inner_shape), kept[:, half:].reshape(inner_shape)]
    for n, order in enumerate(orders()):
        for bit in order:
            spot = 2 if bit == 1 and parts[n].ndim == 5 else 1
            stay = lax.index_in_dim(parts[n], 0, spot, keepdims=False)
            leave = lax.index_in_dim(parts[n], 1, spot, keepdims=False)
            parts[n] = stay + swapped(leave.astype(jnp.bfloat16), "space", bit).astype(jnp.float32)
    part = jnp.concatenate(parts, 1)
    part, leaving = lax.optimization_barrier((part, leaving))
    for bits in groups:
        part = part.reshape((-1, 1 << len(bits)) + part.shape[1:])
        masks = [sum(bit for n, bit in enumerate(bits) if m >> n & 1) for m in range(1 << len(bits))]
        low = part.astype(jnp.bfloat16)
        part = sum(
            [
                swapped(low[:, m], "space", mask).astype(jnp.float32)
                for m, mask in enumerate(masks)
                if m
            ],
            part[:, 0],
        )
    return part[0], leaving


def tall_parts():
    return [CH, D, D, CH] + [D] * (5 * ROUNDS) + [2] + [1] * (1 + 2 * ROUNDS)


def weave(ref, value):
    rows = value.shape[0]
    ref[pl.ds(0, rows, stride=2), :] = value[:, :HALF]
    ref[pl.ds(1, rows, stride=2), :] = value[:, HALF:]


def unweave(ref):
    rows = ref.shape[0] // 2
    return ref[pl.ds(0, rows, stride=2), :], ref[pl.ds(1, rows, stride=2), :]


def selector():
    row = lax.broadcasted_iota(jnp.int32, (8, HALF), 0)
    lane = lax.broadcasted_iota(jnp.int32, (8, HALF), 1)
    slot = jnp.where(lane == CH, 64.0, jnp.where(lane == CH + 1, 1.0, 0.0))
    known = jnp.where(lane == CH + 2, 1.0, 0.0)
    return jnp.where(row == 0, slot, jnp.where(row == 1, known, 0.0)).astype(jnp.bfloat16)


def ids_along(arrived):
    codes = inner(selector(), arrived, 1, 1)
    return jnp.where(codes[1:2, :] > 0, codes[0:1, :], -1.0).astype(jnp.int32)


def ids_down(arrived):
    codes = inner(arrived, selector(), 1, 1)
    return jnp.where(codes[:, 1:2] > 0, codes[:, 0:1], -1.0).astype(jnp.int32)


def whole(shape):
    return pl.BlockSpec(shape, lambda *_: (0,) * len(shape))


def round_forward(index, place, mesh, before, own, after, mats, bias, following, decoder=()):
    blocks = mesh.shape[0]
    choices = len(before)
    tile, chunk = 512, 16
    turns, high = tile // chunk, 2 * chunk
    more = following is not None
    spans = [before[0].shape[0], own.shape[0], after[0].shape[0]]
    reach = sum(spans)

    def body(*refs):
        index_ref, place_ref, mesh_ref, own_ref, mats_ref, bias_ref = refs[:6]
        sides = 2 * choices + choices - 1
        near, refs = refs[6 : 6 + sides], (None,) + refs[:6] + refs[6 + sides :]
        raw, table, rows, wide, wider, sems = refs[-6:]
        if more:
            next_ref, sent_ref = refs[7], refs[13]
            new_ref, back_ref, update_ref, agg_ref, slope_ref = refs[8:13]
        else:
            arrived_ref, dec_ref, out_ref, head_ref = refs[7:11]
            new_ref, back_ref, update_ref, agg_ref, slope_ref = refs[11:16]
            branch_ref, fetched_ref, decoded_ref, turn_ref = refs[16:20]
            total_ref = refs[20]
        step = pl.program_id(0)

        @pl.when(step == 0)
        def _():
            def brought(sources):
                starts = [0, spans[0], spans[0] + spans[1]]
                copies = [
                    pltpu.make_async_copy(source, raw.at[pl.ds(start, span)], sems.at[n])
                    for n, (source, start, span) in enumerate(zip(sources, starts, spans))
                ]
                for copy in copies:
                    copy.start()
                for copy in copies:
                    copy.wait()

            if choices == 1:
                brought((near[0], own_ref, near[1]))
            else:

                @pl.when(place_ref[0] == 1)
                def _():
                    brought((near[0], own_ref, near[2]))

                @pl.when(place_ref[0] == 0)
                def _():
                    brought((near[1], own_ref, near[3]))

            @pl.loop(0, reach // 256)
            def _(i):
                at = pl.multiple_of(i * 256, 256)
                table[pl.ds(at, 256), :] = raw[pl.ds(at, 256), :].astype(jnp.float32)

        mesh_in = mesh_ref[...]
        lowered = mesh_in.astype(jnp.bfloat16)
        weave(wide, inner(lowered, mats_ref[1], 1, 0) + bias_ref[0:1, :])

        def fetch(turn):
            for edge in range(K):
                base = edge * blocks + step * tile + turn * chunk
                spots = [index_ref[base + u] for u in range(chunk)]
                values = [table[pl.ds(pl.multiple_of(spot, 2), 2), :] for spot in spots]
                for u in range(chunk):
                    spot = pl.multiple_of(edge * 2 * tile + turn * high + 2 * u, 2)
                    rows[pl.ds(spot, 2), :] = values[u]

        def load(turn):
            at = pl.multiple_of(turn * high, high)
            taken = [
                rows[pl.ds(pl.multiple_of(edge * 2 * tile + turn * high, high), high), :]
                for edge in range(K)
            ]
            return at, wide[pl.ds(at, high), :], taken

        def dense(at, dest, taken):
            total = None
            for edge in range(K):
                value = taken[edge] + dest
                sigma = sigmoid(value)
                out = value * sigma
                slope_ref[edge, pl.ds(at, high), :] = (sigma + out * (1.0 - sigma)).astype(
                    jnp.bfloat16
                )
                total = out if total is None else total + out
            wider[pl.ds(at, high), :] = total * (1.0 / K)

        def some(turn, carry):
            loaded = load(turn - 1)
            fetch(turn)
            dense(*loaded)
            return carry

        fetch(0)
        lax.fori_loop(1, turns, some, 0)
        dense(*load(turns - 1))
        first, second = unweave(wider)
        first, second = first.astype(jnp.bfloat16), second.astype(jnp.bfloat16)
        agg_ref[:, :HALF] = first
        agg_ref[:, HALF:] = second
        update_in = (
            inner(first, mats_ref[2, :HALF, :], 1, 0)
            + inner(second, mats_ref[2, HALF:, :], 1, 0)
            + inner(lowered, mats_ref[3], 1, 0)
            + bias_ref[1:2, :]
        )
        sigma = sigmoid(update_in)
        out = update_in * sigma
        back_ref[...] = sigma + out * (1.0 - sigma)
        update = out.astype(jnp.bfloat16)
        update_ref[...] = update
        new = mesh_in + inner(update, mats_ref[4], 1, 0)
        new_ref[...] = new
        lowered = new.astype(jnp.bfloat16)
        if more:
            weave(wide, inner(lowered, next_ref[0], 1, 0))
            sent_ref[...] = wide[...].astype(jnp.bfloat16)
            return
        nodes = lax.broadcasted_iota(jnp.int32, (arrived_ref.shape[0], tile), 1) + step * tile
        chooser = jnp.where(nodes == ids_down(arrived_ref[...]), 1.0, 0.0).astype(jnp.bfloat16)
        found = inner(chooser, lowered, 1, 0)

        @pl.when(step == 0)
        def _():
            total_ref[...] = found

        @pl.when(step > 0)
        def _():
            total_ref[...] += found

        @pl.when(step == blocks // tile - 1)
        def _():
            fetched = total_ref[...].astype(jnp.bfloat16)
            fetched_ref[...] = fetched
            value = inner(fetched, dec_ref[...], 1, 0) + head_ref[2:3, :]
            sigma = sigmoid(value)
            out = value * sigma
            turn_ref[...] = sigma + out * (1.0 - sigma)
            decoded = out.astype(jnp.bfloat16)
            decoded_ref[...] = decoded
            branch_ref[...] = inner(decoded, out_ref[...], 1, 0).astype(jnp.bfloat16)

    whole_rows = pl.BlockSpec((tile, D), lambda i, *_: (i, 0))
    woven = pl.BlockSpec((2 * tile, HALF), lambda i, *_: (i, 0))
    far = pl.BlockSpec(memory_space=pl.ANY)
    ins = [whole_rows, far, whole(mats.shape), whole(bias.shape)] + [far] * (2 * choices + choices - 1)
    outs = [whole_rows] * 4 + [pl.BlockSpec((K, 2 * tile, HALF), lambda i, *_: (0, i, 0))]
    shapes = [
        jax.ShapeDtypeStruct((blocks, D), jnp.float32),
        jax.ShapeDtypeStruct((blocks, D), jnp.float32),
        jax.ShapeDtypeStruct((blocks, D), jnp.bfloat16),
        jax.ShapeDtypeStruct((blocks, D), jnp.bfloat16),
        jax.ShapeDtypeStruct((K, 2 * blocks, HALF), jnp.bfloat16),
    ]
    args = [index, place, mesh, own, mats, bias, *before, *after]
    if more:
        ins.append(pl.BlockSpec((1, D, D), lambda *_: (0, 0, 0)))
        outs.append(woven)
        shapes.append(jax.ShapeDtypeStruct((2 * blocks, HALF), jnp.bfloat16))
        args.append(following)
    scratch = []
    if decoder:
        posts = decoder[0].shape[0]
        ins = ins + [whole(arg.shape) for arg in decoder]
        args = args + list(decoder)
        for width, kind in ((HALF, jnp.bfloat16), (D, jnp.bfloat16), (D, jnp.bfloat16), (D, jnp.float32)):
            outs.append(whole((posts, width)))
            shapes.append(jax.ShapeDtypeStruct((posts, width), kind))
        scratch = [pltpu.VMEM((posts, D), jnp.float32)]
    return pl.pallas_call(
        body,
        grid_spec=pltpu.PrefetchScalarGridSpec(
            num_scalar_prefetch=2,
            grid=(blocks // tile,),
            in_specs=ins,
            out_specs=outs,
            scratch_shapes=scratch
            + [
                pltpu.VMEM((reach, HALF), jnp.bfloat16),
                pltpu.VMEM((reach, HALF), jnp.float32),
                pltpu.VMEM((K * 2 * tile, HALF), jnp.float32),
                pltpu.VMEM((2 * tile, HALF), jnp.float32),
                pltpu.VMEM((2 * tile, HALF), jnp.float32),
                pltpu.SemaphoreType.DMA((3,)),
            ],
        ),
        out_shape=shapes,
        compiler_params=LIMIT,
        cost_estimate=cost(25),
        name="round_forward",
    )(*args)


def edges_backward(index, grad_mesh, back, slopes, mats, carried=(), landed=()):
    blocks = back.shape[0]
    tile, chunk = 512, 16
    steps, turns, high = blocks // tile, tile // chunk, 2 * chunk
    reach = 2 * (blocks + 2 * H)

    def body(*refs):
        if carried:
            index_ref, grad_ref, back_ref, slope_ref, mats_ref = refs[:5]
            past, rest = refs[5:11], refs[11:]
            (new_ref, out_ref, sent_ref), rest = rest[:3], rest[3:]
        else:
            index_ref, back_ref, slope_ref, mats_ref = refs[:4]
            (arrived_ref, landed_ref, turn_ref, w_out_ref, w_dec_ref), rest = refs[4:9], refs[9:]
            (new_ref, out_ref, gdec_ref), rest = rest[:3], rest[3:]
            gathered, rest = rest[5], rest[:5] + rest[6:]
        guin_ref, low_ref, before_ref, own_ref, after_ref, wide, wider, flows, *tables = rest
        step = pl.program_id(0)

        @pl.when(step == 0)
        def _():
            @pl.loop(0, reach // 256)
            def _(i):
                for table in tables:
                    table[pl.ds(pl.multiple_of(i * 256, 256), 256), :] = jnp.zeros(
                        (256, HALF), jnp.float32
                    )

        if carried:
            new = ended(grad_ref, *past, sent_ref, wide)
            new_ref[...] = new
            grad_out = new.astype(jnp.bfloat16)
            out_ref[...] = grad_out
        else:

            @pl.when(step == 0)
            def _():
                grad_dec = inner(landed_ref[...], w_out_ref[...], 1, 1) * turn_ref[...]
                grad_dec = grad_dec.astype(jnp.bfloat16)
                gdec_ref[...] = grad_dec
                gathered[...] = inner(grad_dec, w_dec_ref[...], 1, 1).astype(jnp.bfloat16)

            nodes = lax.broadcasted_iota(jnp.int32, (tile, landed_ref.shape[0]), 0) + step * tile
            chooser = jnp.where(nodes == ids_along(arrived_ref[...]), 1.0, 0.0)
            chooser = chooser.astype(jnp.bfloat16)
            new = inner(chooser, gathered[...], 1, 0)
            new_ref[...] = new
            grad_out = new.astype(jnp.bfloat16)
            out_ref[...] = grad_out
        grad_uin = (inner(grad_out, mats_ref[4], 1, 1) * back_ref[...]).astype(jnp.bfloat16)
        guin_ref[...] = grad_uin
        weave(wide, inner(grad_uin, mats_ref[2], 1, 1) * (1.0 / K))

        def dense(turn):
            at = pl.multiple_of(turn * high, high)
            grad_agg = wide[pl.ds(at, high), :]
            total, parts = None, []
            for edge in range(K):
                flow = grad_agg * slope_ref[edge, pl.ds(at, high), :].astype(jnp.float32)
                parts.append(flow)
                total = flow if total is None else total + flow
            return at, total, parts

        def keep(turn, at, total, parts):
            for edge in range(K):
                spot = pl.multiple_of(edge * 2 * tile + turn * high, high)
                flows[pl.ds(spot, high), :] = parts[edge]
            wider[pl.ds(at, high), :] = total

        def scatter(turn):
            for u in range(chunk):
                spots, sums = [], []
                for edge in range(K):
                    base = edge * blocks + step * tile + turn * chunk
                    spots.append(pl.multiple_of(index_ref[base + u], 2))
                for edge in range(K):
                    spot = pl.multiple_of(edge * 2 * tile + turn * high + 2 * u, 2)
                    sums.append(tables[edge][pl.ds(spots[edge], 2), :] + flows[pl.ds(spot, 2), :])
                for edge in range(K):
                    tables[edge][pl.ds(spots[edge], 2), :] = sums[edge]

        def some(turn, carry):
            found = dense(turn)
            scatter(turn - 1)
            keep(turn, *found)
            return carry

        keep(0, *dense(0))
        lax.fori_loop(1, turns, some, 0)
        scatter(turns - 1)
        first, second = unweave(wider)
        low_ref[:, :HALF] = first.astype(jnp.bfloat16)
        low_ref[:, HALF:] = second.astype(jnp.bfloat16)

        @pl.when(step == steps - 1)
        def _():
            def summed(at):
                value = tables[0][pl.ds(at, 256), :]
                for table in tables[1:]:
                    value = value + table[pl.ds(at, 256), :]
                return value

            @pl.loop(0, 2 * H // 256)
            def _(i):
                at = pl.multiple_of(i * 256, 256)
                far = pl.multiple_of(2 * H + 2 * blocks + at, 256)
                before_ref[pl.ds(at, 256), :] = summed(at).astype(jnp.bfloat16)
                after_ref[pl.ds(at, 256), :] = summed(far).astype(jnp.bfloat16)

            @pl.loop(0, 2 * blocks // 256)
            def _(i):
                at = pl.multiple_of(i * 256, 256)
                own_ref[pl.ds(at, 256), :] = summed(pl.multiple_of(2 * H + at, 256))

    rows = pl.BlockSpec((tile, D), lambda i, *_: (i, 0))
    woven = pl.BlockSpec((2 * tile, HALF), lambda i, *_: (i, 0))
    low = jax.ShapeDtypeStruct((blocks, D), jnp.bfloat16)
    low_posts = (landed[1].shape[0], D) if landed else None
    last = low if carried else jax.ShapeDtypeStruct(low_posts, jnp.bfloat16)
    return pl.pallas_call(
        body,
        grid_spec=pltpu.PrefetchScalarGridSpec(
            num_scalar_prefetch=1,
            grid=(steps,),
            in_specs=([rows] if carried else [])
            + [
                rows,
                pl.BlockSpec((K, 2 * tile, HALF), lambda i, *_: (0, i, 0)),
                whole(mats.shape),
            ]
            + ([woven] * 3 + [rows] * 2 + [whole(mats.shape)] if carried else [])
            + [whole(arg.shape) for arg in landed],
            out_specs=([rows] * 3 if carried else [rows, rows, whole(low_posts)])
            + [
                rows, rows,
                whole((2 * H, HALF)), whole((2 * blocks, HALF)), whole((2 * H, HALF)),
            ],
            scratch_shapes=([] if carried else [pltpu.VMEM(low_posts, jnp.bfloat16)])
            + [
                pltpu.VMEM((2 * tile, HALF), jnp.float32),
                pltpu.VMEM((2 * tile, HALF), jnp.float32),
                pltpu.VMEM((2 * tile * K, HALF), jnp.float32),
            ]
            + [pltpu.VMEM((reach, HALF), jnp.float32)] * K,
        ),
        out_shape=[
            jax.ShapeDtypeStruct((blocks, D), jnp.float32),
            low,
            last,
            low,
            low,
            jax.ShapeDtypeStruct((2 * H, HALF), jnp.bfloat16),
            jax.ShapeDtypeStruct((2 * blocks, HALF), jnp.float32),
            jax.ShapeDtypeStruct((2 * H, HALF), jnp.bfloat16),
        ],
        compiler_params=LIMIT,
        cost_estimate=cost(28 if carried else 25),
        name="edges_backward",
    )(index, *([grad_mesh] if carried else []), back, slopes, mats, *carried, *landed)


def ended(grad_ref, own_ref, first_ref, last_ref, guin_ref, dest_ref, mats_ref, sent_ref, wide):
    wide[...] = (
        own_ref[...] + first_ref[...].astype(jnp.float32) + last_ref[...].astype(jnp.float32)
    )
    one, two = unweave(wide)
    one, two = one.astype(jnp.bfloat16), two.astype(jnp.bfloat16)
    sent_ref[:, :HALF] = one
    sent_ref[:, HALF:] = two
    return (
        grad_ref[...]
        + inner(guin_ref[...], mats_ref[3], 1, 1)
        + inner(dest_ref[...], mats_ref[1], 1, 1)
        + inner(one, mats_ref[0, :, :HALF], 1, 1)
        + inner(two, mats_ref[0, :, HALF:], 1, 1)
    )


def round_backward(grad_mesh, own, first, last, grad_uin, dest_low, mats):
    blocks = grad_mesh.shape[0]
    tile = 1024

    def body(*refs):
        new_ref, out_ref, sent_ref, wide = refs[-4:]
        new = ended(*refs[:-4], sent_ref, wide)
        new_ref[...] = new
        out_ref[...] = new.astype(jnp.bfloat16)

    rows = pl.BlockSpec((tile, D), lambda i: (i, 0))
    woven = pl.BlockSpec((2 * tile, HALF), lambda i: (i, 0))
    low = jax.ShapeDtypeStruct((blocks, D), jnp.bfloat16)
    return pl.pallas_call(
        body,
        grid=(blocks // tile,),
        in_specs=[rows, woven, woven, woven, rows, rows, whole(mats.shape)],
        out_specs=[rows, rows, rows],
        out_shape=[jax.ShapeDtypeStruct((blocks, D), jnp.float32), low, low],
        scratch_shapes=[pltpu.VMEM((2 * tile, HALF), jnp.float32)],
        compiler_params=LIMIT,
        cost_estimate=cost(7),
        name="round_backward",
    )(grad_mesh, own, first, last, grad_uin, dest_low, mats)


def encode_rows(arrived, w_in, w_node, biases, source):
    posts = arrived.shape[0]
    tile = 512

    def body(arrived_ref, in_ref, node_ref, bias_ref, source_ref, mesh_ref, gathered_ref, sent_ref, encoded, wide):
        step = pl.program_id(0)

        @pl.when(step == 0)
        def _():
            entering = inner(arrived_ref[...], in_ref[...], 1, 0) + bias_ref[0:1, :]
            encoded[...] = silu(entering).astype(jnp.bfloat16)

        nodes = lax.broadcasted_iota(jnp.int32, (tile, posts), 0) + step * tile
        chooser = jnp.where(nodes == ids_along(arrived_ref[...]), 1.0, 0.0).astype(jnp.bfloat16)
        gathered = inner(chooser, encoded[...], 1, 0).astype(jnp.bfloat16)
        gathered_ref[...] = gathered
        mesh = silu(inner(gathered, node_ref[...], 1, 0) + bias_ref[1:2, :])
        mesh_ref[...] = mesh
        weave(wide, inner(mesh.astype(jnp.bfloat16), source_ref[0], 1, 0))
        sent_ref[...] = wide[...].astype(jnp.bfloat16)

    rows = pl.BlockSpec((tile, D), lambda i: (i, 0))
    args = (arrived, w_in, w_node, biases, source)
    return pl.pallas_call(
        body,
        grid=(H // tile,),
        in_specs=[whole(arg.shape) for arg in args[:-1]]
        + [pl.BlockSpec((1, D, D), lambda *_: (0, 0, 0))],
        out_specs=[rows, rows, pl.BlockSpec((2 * tile, HALF), lambda i: (i, 0))],
        out_shape=[
            jax.ShapeDtypeStruct((H, D), jnp.float32),
            jax.ShapeDtypeStruct((H, D), jnp.bfloat16),
            jax.ShapeDtypeStruct((2 * H, HALF), jnp.bfloat16),
        ],
        scratch_shapes=[pltpu.VMEM((posts, D), jnp.bfloat16), pltpu.VMEM((2 * tile, HALF), jnp.float32)],
        compiler_params=LIMIT,
        cost_estimate=cost(5),
        name="encode_rows",
    )(*args)


def encode_backward(grad_mesh, gathered, arrived, w_in, w_node, biases):
    posts = arrived.shape[0]
    tile = 512
    steps = H // tile

    def body(grad_ref, gathered_ref, arrived_ref, in_ref, node_ref, bias_ref, gin_ref, gnode_ref, gbias_ref, total):
        step = pl.program_id(0)

        @pl.when(step == 0)
        def _():
            total[...] = jnp.zeros(total.shape, jnp.float32)
            gnode_ref[...] = jnp.zeros(gnode_ref.shape, jnp.float32)
            gbias_ref[...] = jnp.zeros(gbias_ref.shape, jnp.float32)

        node_in = inner(gathered_ref[...], node_ref[...], 1, 0) + bias_ref[1:2, :]
        grad_node = (grad_ref[...] * slope(node_in)).astype(jnp.bfloat16)
        gbias_ref[1:2, :] += jnp.sum(grad_node.astype(jnp.float32), 0, keepdims=True)
        gnode_ref[...] += inner(gathered_ref[...], grad_node, 0, 0)
        back = inner(grad_node, node_ref[...], 1, 1).astype(jnp.bfloat16)
        nodes = lax.broadcasted_iota(jnp.int32, (posts, tile), 1) + step * tile
        chooser = jnp.where(nodes == ids_down(arrived_ref[...]), 1.0, 0.0).astype(jnp.bfloat16)
        total[...] += inner(chooser, back, 1, 0)

        @pl.when(step == steps - 1)
        def _():
            entering = inner(arrived_ref[...], in_ref[...], 1, 0) + bias_ref[0:1, :]
            grad_enc = (total[...] * slope(entering)).astype(jnp.bfloat16)
            gbias_ref[0:1, :] = jnp.sum(grad_enc.astype(jnp.float32), 0, keepdims=True)
            gin_ref[...] = inner(arrived_ref[...], grad_enc, 0, 0)

    rows = pl.BlockSpec((tile, D), lambda i: (i, 0))
    args = (grad_mesh, gathered, arrived, w_in, w_node, biases)
    shapes = [(HALF, D), (D, D), (2, D)]
    return pl.pallas_call(
        body,
        grid=(steps,),
        in_specs=[rows, rows] + [whole(arg.shape) for arg in args[2:]],
        out_specs=[whole(shape) for shape in shapes],
        out_shape=[jax.ShapeDtypeStruct(shape, jnp.float32) for shape in shapes],
        scratch_shapes=[pltpu.VMEM((posts, D), jnp.float32)],
        compiler_params=LIMIT,
        cost_estimate=cost(7),
        name="encode_backward",
    )(*args)


def shards(walk, master, moment1, moment2, inputs, targets, valid, owner, slot, neighbours, partner):
    bands = lax.axis_size("space")
    band = lax.axis_index("space")
    peers = lax.axis_size(ALL)
    place = lax.axis_index(ALL)
    shard = master.shape[0]
    total_size = shard * peers
    height = pieces_of(total_size, peers)[3]
    offset = lax.rem(lax.rem(shard, D) * place, D)
    piece = lax.dynamic_update_slice_in_dim(
        jnp.zeros((height * D,), jnp.bfloat16), master.astype(jnp.bfloat16), offset, 0
    )
    state_in = inputs[0]
    counted = valid[0].astype(jnp.float32)
    local_count = jnp.sum(valid[0])
    digits = (local_count >> jnp.array([16, 8, 0], jnp.int32)) & 255
    piece = lax.dynamic_update_slice(
        piece.reshape(height, D), digits.astype(jnp.bfloat16)[None, :], (height - 1, 0)
    )
    points = state_in.shape[1]
    blocks = neighbours.shape[0]
    assert blocks == H
    capacity = max(2, 2 * points // bands)
    target_band = owner[0, :, 0]
    hits = (target_band[:, None] == jnp.arange(bands, dtype=jnp.int32)[None, :]).astype(jnp.int32)
    ranks = jnp.sum(jnp.cumsum(hits, 0) * hits, 1) - 1
    places_out = jnp.sum(hits * jnp.asarray(walk, jnp.int32)[None, :], 1) * capacity + ranks
    poster = (
        jnp.arange(bands * capacity, dtype=jnp.int32)[:, None] == places_out[None, :]
    ).astype(jnp.bfloat16)
    spots = slot[0][None, :]
    columns = jnp.concatenate(
        [
            state_in,
            (spots // 64).astype(jnp.bfloat16),
            (spots % 64).astype(jnp.bfloat16),
            jnp.ones((1, points), jnp.bfloat16),
            jnp.zeros((HALF - CH - 3, points), jnp.bfloat16),
        ],
        0,
    )

    def exchanged(rows):
        return lax.all_to_all(
            rows.reshape(bands, capacity, HALF), "space", split_axis=0, concat_axis=0, tiled=True
        ).reshape(bands * capacity, HALF)

    held, posted = gathered_blocks(piece, inner(poster, columns, 1, 1).astype(jnp.bfloat16))
    arrived = exchanged(posted)
    w_in, w_node, w_dec, w_out, *w_round, biases, digits = spread_rows(
        held, total_size, peers, place
    )
    arrived, biases = lax.optimization_barrier((arrived, biases))
    count = digits[0, 0] * 65536.0 + digits[0, 1] * 256.0 + digits[0, 2]
    w_out = jnp.pad(w_out.reshape(D, CH), ((0, 0), (0, HALF - CH)))
    w_round = [mats.reshape(5, D, D) for mats in w_round]
    b_head = biases[:3]
    b_round = biases[3:].reshape(ROUNDS, 2, D)
    mesh, gathered, sent = encode_rows(
        arrived, w_in, w_node, biases, w_round[0]
    )
    sent, partner, neighbours, counted = lax.optimization_barrier(
        (sent, partner, neighbours, counted)
    )
    index = 2 * ((neighbours - band * blocks + H) % (blocks * bands)).T.reshape(-1)
    moved = [(n, place) for n, place in enumerate(walk) if n != place]
    stays = jnp.asarray([n == place for n, place in enumerate(walk)])[band]
    index = lax.ppermute(index, "space", list(enumerate(walk)))

    def at_home(rows):
        return lax.ppermute(rows, "space", [(j, i) for i, j in moved])

    def settled(own, came):
        return jnp.where(stays, own, came.astype(jnp.float32))

    partner_by = partner - band * points - jnp.arange(points, dtype=jnp.int32)
    coded = jnp.where(partner_by >= NEAR, partner_by - NEAR + 1, 0).astype(jnp.bfloat16)
    low_valid = jnp.concatenate([counted.astype(jnp.bfloat16), coded[None, :]], 0)
    valid_around = jnp.concatenate(
        [
            shifted(low_valid[:, points - ROWW :], "space", 1),
            low_valid,
            shifted(low_valid[:, :ROWW], "space", -1),
        ],
        1,
    )
    core = lax.axis_index("dp").reshape(1)
    kept = []
    for layer in range(ROUNDS):
        if layer == 0:
            before, after = staggered(walk, sent, sent)
            before, valid_around = lax.optimization_barrier((before, valid_around))
        else:
            before, after = [[rows] for rows in halo(walk, sent, sent)]
        following = w_round[layer + 1] if layer + 1 < ROUNDS else None
        new, back, update, agg, slopes, *rest = round_forward(
            index, core, mesh, before, sent, after, w_round[layer], b_round[layer], following,
            () if following is not None else (arrived, w_dec, w_out, biases),
        )
        kept.append((mesh, back, update, agg, slopes))
        mesh = new
        sent = rest[0]
    wide_valid = valid_around[:CH].astype(jnp.float32)
    coded = valid_around[CH : CH + 1, : points + ROWW].astype(jnp.float32)
    weights = [
        (
            by,
            jnp.where(coded == by - NEAR + 1, 1.0, 0.0)
            * wide_valid[:, : points + ROWW]
            * wide_valid[:, by : by + points + ROWW],
        )
        for by in range(NEAR, ROWW + 1)
    ]
    branch_rows, fetched, decoded, dec_turn = rest
    returned = exchanged(branch_rows)
    branch = inner(returned, poster, 0, 0)[:CH]
    err = state_in.astype(jnp.float32) + branch - targets[0].astype(jnp.float32)
    def widened(values):
        low = values.astype(jnp.bfloat16)
        before = shifted(low[:, points - ROWW :], "space", 1).astype(jnp.float32)
        after = shifted(low[:, :ROWW], "space", -1).astype(jnp.float32)
        return jnp.concatenate([before, values, after], 1)

    wide_err = widened(err)
    paired = jnp.zeros((CH, points + ROWW), jnp.float32)
    pair_total = jnp.zeros((CH, points), jnp.float32)
    for by, both in weights:
        gap = both * (wide_err[:, : points + ROWW] - wide_err[:, by : by + points + ROWW])
        paired = paired + gap
        pair_total = pair_total + gap[:, ROWW:] * (
            wide_err[:, ROWW : ROWW + points] - wide_err[:, ROWW + by : ROWW + by + points]
        )
    local_total = jnp.sum(counted * err * err) + 0.5 * jnp.sum(pair_total)
    grad_pred = 2.0 * counted * err + paired[:, ROWW:]
    for by, both in weights:
        gap = both * (wide_err[:, : points + ROWW] - wide_err[:, by : by + points + ROWW])
        grad_pred = grad_pred - gap[:, ROWW - by : ROWW - by + points]
    grad_pred = grad_pred / count
    grad_rows = jnp.pad(grad_pred.astype(jnp.bfloat16), ((0, HALF - CH), (0, 0)))
    landed = exchanged(inner(poster, grad_rows, 1, 1).astype(jnp.bfloat16))
    landed, final_mesh = lax.optimization_barrier((landed, mesh.astype(jnp.bfloat16)))
    final_mesh = at_home(final_mesh)
    mats_grads = [None] * (5 * ROUNDS)
    bias_grads = [None] * (2 * ROUNDS)
    carried, grad_mesh = (), None
    for layer in reversed(range(ROUNDS)):
        old, back, update, agg, slopes = kept[layer]
        first_step = not carried
        grad_mesh, leaving, extra, grad_uin, dest_low, to_before, own, to_after = edges_backward(
            index, grad_mesh, back, slopes, w_round[layer], carried,
            (arrived, landed, dec_turn, w_out, w_dec) if first_step else (),
        )
        if not first_step:
            mats_grads[5 * layer + 5] = inner(
                kept[layer + 1][0].astype(jnp.bfloat16), extra, 0, 0
            )
        else:
            grad_wout = inner(decoded, landed, 0, 0)[:, :CH]
            grad_bdec = jnp.sum(extra.astype(jnp.float32), 0, keepdims=True)
            grad_wdec = inner(fetched, extra, 0, 0)
            to_before, to_after, final_mesh = lax.optimization_barrier(
                (to_before, to_after, final_mesh)
            )
        from_before, from_after = halo(walk, to_after, to_before)
        if first_step:
            from_before, final_mesh = lax.optimization_barrier(
                (from_before, settled(mesh, final_mesh))
            )
        lowered = old.astype(jnp.bfloat16)
        mats_grads[5 * layer + 1 : 5 * layer + 5] = [
            inner(lowered, dest_low, 0, 0),
            inner(agg, grad_uin, 0, 0),
            inner(lowered, grad_uin, 0, 0),
            inner(update, leaving, 0, 0),
        ]
        bias_grads[2 * layer] = jnp.sum(dest_low.astype(jnp.float32), 0, keepdims=True)
        bias_grads[2 * layer + 1] = jnp.sum(grad_uin.astype(jnp.float32), 0, keepdims=True)
        carried = (own, from_before, from_after, grad_uin, dest_low, w_round[layer])
    grad_mesh, leaving, sent_low = round_backward(grad_mesh, *carried)
    mats_grads[0] = inner(kept[0][0].astype(jnp.bfloat16), sent_low, 0, 0)
    grad_win, grad_wnode, grad_bpair = encode_backward(
        grad_mesh, gathered, arrived, w_in, w_node, biases
    )
    parts = [grad_win, grad_wnode, grad_wdec, grad_wout.reshape(CH, D)]
    parts = parts + mats_grads
    parts = parts + [grad_bpair, grad_bdec] + bias_grads
    keep, send = collect_rows(parts, total_size, peers, place)
    mine, leaving = reduced_piece(keep, send, leaving)
    late = at_home(leaving)
    mine = lax.dynamic_slice_in_dim(mine.reshape(-1), offset, shard)
    lane = lax.broadcasted_iota(jnp.int32, (8, HALF), 1)
    sums, late = summed_everywhere(
        jnp.where(lane == 0, local_total, jnp.sum(mine * mine)), late
    )
    total, norm = sums[0, 0], jnp.sqrt(sums[0, 1])
    node_grads = settled(grad_mesh, late)
    clipped = mine * jnp.minimum(1.0, 0.05 / norm)
    first = 0.9 * moment1 + 0.1 * clipped
    second = 0.999 * moment2 + 0.001 * clipped * clipped
    first_hat = first / (1.0 - 0.9**STEP)
    second_hat = second / (1.0 - 0.999**STEP)
    updated = master - 0.1 * (first_hat / (jnp.sqrt(second_hat) + 1e-08) + 0.1 * master)
    return (
        total.reshape(1),
        count.reshape(1),
        norm.reshape(1),
        updated,
        first,
        second,
        updated.astype(jnp.bfloat16),
        final_mesh.reshape(1, blocks, D),
        node_grads.reshape(1, blocks, D),
        grad_pred.reshape(1, grad_pred.shape[0], points),
    )


def solution(mesh):
    return jax.shard_map(
        functools.partial(shards, walk_of(mesh)),
        mesh=mesh,
        in_specs=(
            P(("dp", "space")),
            P(("dp", "space")),
            P(("dp", "space")),
            P("dp", None, "space"),
            P("dp", None, "space"),
            P("dp", None, "space"),
            P("dp", "space", None),
            P("dp", "space"),
            P("space", None),
            P("space"),
        ),
        out_specs=(
            P(),
            P(),
            P(),
            P(("dp", "space")),
            P(("dp", "space")),
            P(("dp", "space")),
            P(("dp", "space")),
            P("dp", "space", None),
            P("dp", "space", None),
            P("dp", None, "space"),
        ),
        check_vma=False,
    )
```

```python
import functools

import jax
import jax.numpy as jnp
from jax import lax
from jax.experimental import pallas as pl
from jax.experimental.pallas import tpu as pltpu
from jax.sharding import PartitionSpec as P

D = 256
HALF = 128
CH = 78
ROUNDS = 3
K = 6
ROWW = 360
NEAR = 358
STEP = 10
H = 2048
ALL = ("dp", "space")
LIMIT = pltpu.CompilerParams(vmem_limit_bytes=60 * 2**20)


def cost(micros):
    return pl.CostEstimate(flops=0, bytes_accessed=micros * 3_000_000, transcendentals=0)


def inner(left, right, left_dim, right_dim):
    return lax.dot_general(
        left, right, (((left_dim,), (right_dim,)), ((), ())), preferred_element_type=jnp.float32
    )


def sigmoid(value):
    return 0.5 * jnp.tanh(0.5 * value) + 0.5


def silu(value):
    return value * sigmoid(value)


def slope(value):
    sigma = sigmoid(value)
    return sigma * (1.0 + value * (1.0 - sigma))


def shifted(shard, axis, by):
    peers = lax.axis_size(axis)
    pairs = [(i, i + by) for i in range(peers) if 0 <= i + by < peers]
    return lax.ppermute(shard, axis, pairs)


def walk_of(mesh):
    count = mesh.shape["space"]
    chips = [getattr(device, "coords", None) for device in mesh.devices[0].reshape(-1)]
    if any(chip is None for chip in chips) or len(set(map(tuple, chips))) != count:
        return list(range(count))
    at = {tuple(chip): n for n, chip in enumerate(chips)}
    xs, ys, zs = (sorted({chip[n] for chip in at}) for n in range(3))
    if len(xs) * len(ys) * len(zs) != count:
        return list(range(count))
    if (len(xs), len(ys), len(zs)) == (2, 2, 4):
        corners = [(0, 0), (1, 0), (0, 1), (1, 1)]
        planes = [(0, 1, 3, 2), (2, 0, 1, 3), (3, 1, 0, 2), (2, 3, 1, 0)]
        steps = [(*corners[n], z) for z, plane in enumerate(planes) for n in plane]
        return [at[(xs[x], ys[y], zs[z])] for x, y, z in steps]
    walk, plane = [], []
    for n, y in enumerate(ys):
        plane = plane + [(x, y) for x in (xs if n % 2 == 0 else xs[::-1])]
    for n, z in enumerate(zs):
        walk = walk + [at[(x, y, z)] for x, y in (plane if n % 2 == 0 else plane[::-1])]
    return walk


def halo(walk, last, initial):
    up = list(zip(walk, walk[1:] + walk[:1]))
    down = [(j, i) for i, j in up]
    return lax.ppermute(last, "space", up), lax.ppermute(initial, "space", down)


def pieces_of(total, peers):
    share = total // peers
    starts = [share * d // D for d in range(peers)]
    counts = [-(-share * (d + 1) // D) - starts[d] for d in range(peers)]
    shared = [share * d % D != 0 for d in range(peers)]
    height = -(-(max(counts) + 1) // 16) * 16
    return starts, counts, shared, height


def parts_of():
    return [CH, D, D, CH] + [5 * D] * ROUNDS + [3 + 2 * ROUNDS]


def swapped(value, axis, bit):
    return lax.ppermute(value, axis, [(i, i ^ bit) for i in range(lax.axis_size(axis))])


def bits_of(axis):
    return [1 << n for n in range(lax.axis_size(axis).bit_length() - 1)]


def others(value, axis, bits):
    masks = [sum(bit for n, bit in enumerate(bits) if m >> n & 1) for m in range(1, 1 << len(bits))]
    return [swapped(value, axis, mask) for mask in masks]


def upper_groups():
    bits = bits_of("space")[2:]
    return [tuple(bits[n : n + 2]) for n in range(0, len(bits), 2)]


def orders():
    return [(1, 2), (2, 1)]


def summed_everywhere(value, arriving):
    for bits in reversed(upper_groups()):
        value = sum(others(value, "space", bits), value)
    value = value + swapped(value, "dp", 1)
    value, arriving = lax.optimization_barrier((value, arriving))
    return sum(others(value, "space", (1, 2)), value), arriving


def gathered_blocks(piece, posted):
    held, weights, size = piece[None], {}, 1
    for bits in reversed(upper_groups()):
        held = jnp.concatenate([held] + others(held, "space", bits), 0)
        for n, bit in enumerate(bits):
            weights[bit] = size << n
        size = size << len(bits)
    half = piece.shape[0] // 2
    held = [held[:, :half], held[:, half:]]
    ranks = [dict(weights), dict(weights)]
    for turn in (1, 0):
        if turn == 0:
            held[0], held[1], posted = lax.optimization_barrier((*held, posted))
        for n, order in enumerate(orders()):
            held[n] = jnp.concatenate([held[n], swapped(held[n], "space", order[turn])], 0)
            ranks[n][order[turn]] = size
        size = size << 1
    return (held, [swapped(part, "dp", 1) for part in held], ranks), posted


def spread_rows(gathered, total, peers, place):
    (first, second), (first_far, second_far), ranks = gathered
    starts, counts, shared, height = pieces_of(total, peers)
    half, group = height // 2, first.shape[0]
    rows = -(-total // D)
    sizes = parts_of()
    def at(rank, relative):
        spot = 0
        for bit, weight in rank.items():
            spot = spot + jnp.where((relative & bit) != 0, weight, 0)
        return spot

    def body(place_ref, *refs):
        sources, outs, buffer = refs[:4], refs[4:-1], refs[-1]
        me = place_ref[0]
        mine = me // group
        for d in range(peers):
            relative = (me ^ d) & (group - 1)
            spots = [at(rank, relative) for rank in ranks]

            def lay(one, two, d=d, spots=spots):
                piece = jnp.concatenate([one[spots[0]], two[spots[1]]], 0).astype(jnp.float32)
                start, count = starts[d], counts[d]
                if shared[d]:
                    buffer[start : start + 1, :] = buffer[start : start + 1, :] + piece[:1]
                    buffer[start + 1 : start + count, :] = piece[1:count]
                else:
                    buffer[start : start + count, :] = piece[:count]

            @pl.when(mine == d // group)
            def _():
                lay(sources[0], sources[1])

            @pl.when(mine != d // group)
            def _():
                lay(sources[2], sources[3])

        count = jnp.zeros((1, D), jnp.float32)
        for source in (sources[1], sources[3]):
            for spot in range(group):
                count = count + source[spot, half - 1 : half, :].astype(jnp.float32)
        outs[-1][...] = count
        start = 0
        for out, size in zip(outs[:-1], sizes):
            out[:size, :] = buffer[start : start + size, :].astype(out.dtype)
            if out.shape[0] > size:
                out[size:, :] = jnp.zeros((out.shape[0] - size, D), out.dtype)
            start = start + size

    kinds = [jnp.bfloat16] * (4 + ROUNDS) + [jnp.float32]
    talls = [HALF] + sizes[1:]
    return pl.pallas_call(
        body,
        grid_spec=pltpu.PrefetchScalarGridSpec(
            num_scalar_prefetch=1,
            grid=(1,),
            in_specs=[whole(first.shape)] * 4,
            out_specs=[whole((tall, D)) for tall in talls + [1]],
            scratch_shapes=[pltpu.VMEM((-(-rows // 8) * 8 + 8, D), jnp.float32)],
        ),
        out_shape=[
            jax.ShapeDtypeStruct((tall, D), kind)
            for tall, kind in zip(talls + [1], kinds + [jnp.float32])
        ],
        compiler_params=LIMIT,
        cost_estimate=cost(4),
        name="spread_rows",
    )(place.reshape(1), first, second, first_far, second_far)


def collect_rows(parts, total, peers, place):
    starts, counts, shared, height = pieces_of(total, peers)
    rows = -(-total // D)
    sizes = [min(part.shape[0], size) for part, size in zip(parts, tall_parts())]
    group = lax.axis_size("space")

    def body(place_ref, *refs):
        sources, keep, send, buffer = refs[:-3], refs[-3], refs[-2], refs[-1]
        start = 0
        for source, size in zip(sources, sizes):
            buffer[start : start + size, :] = source[:size, :]
            start = start + size
        if buffer.shape[0] > start:
            buffer[start:, :] = jnp.zeros((buffer.shape[0] - start, D), jnp.float32)
        me = place_ref[0]
        mine = me // group
        for d in range(peers):
            relative = (me ^ d) & (group - 1)

            @pl.when(mine == d // group)
            def _():
                keep[relative] = buffer[starts[d] : starts[d] + height, :]

            @pl.when(mine != d // group)
            def _():
                send[relative] = buffer[starts[d] : starts[d] + height, :].astype(jnp.bfloat16)

    shape = (group, height, D)
    return pl.pallas_call(
        body,
        grid_spec=pltpu.PrefetchScalarGridSpec(
            num_scalar_prefetch=1,
            grid=(1,),
            in_specs=[whole(part.shape) for part in parts],
            out_specs=[whole(shape), whole(shape)],
            scratch_shapes=[pltpu.VMEM((-(-rows // 8) * 8 + height + 8, D), jnp.float32)],
        ),
        out_shape=[
            jax.ShapeDtypeStruct(shape, jnp.float32),
            jax.ShapeDtypeStruct(shape, jnp.bfloat16),
        ],
        compiler_params=LIMIT,
        cost_estimate=cost(5),
        name="collect_rows",
    )(place.reshape(1), *parts)


def reduced_piece(keep, send, leaving):
    kept = keep + swapped(send, "dp", 1).astype(jnp.float32)
    half = kept.shape[1] // 2
    groups = upper_groups()
    inner_shape = (kept.shape[0] // 4, 2, 2, half, D)
    parts = [kept[:, :half].reshape(inner_shape), kept[:, half:].reshape(inner_shape)]
    for n, order in enumerate(orders()):
        for bit in order:
            spot = 2 if bit == 1 and parts[n].ndim == 5 else 1
            stay = lax.index_in_dim(parts[n], 0, spot, keepdims=False)
            leave = lax.index_in_dim(parts[n], 1, spot, keepdims=False)
            parts[n] = stay + swapped(leave.astype(jnp.bfloat16), "space", bit).astype(jnp.float32)
    part = jnp.concatenate(parts, 1)
    part, leaving = lax.optimization_barrier((part, leaving))
    for bits in groups:
        part = part.reshape((-1, 1 << len(bits)) + part.shape[1:])
        masks = [sum(bit for n, bit in enumerate(bits) if m >> n & 1) for m in range(1 << len(bits))]
        low = part.astype(jnp.bfloat16)
        part = sum(
            [
                swapped(low[:, m], "space", mask).astype(jnp.float32)
                for m, mask in enumerate(masks)
                if m
            ],
            part[:, 0],
        )
    return part[0], leaving


def tall_parts():
    return [CH, D, D, CH] + [D] * (5 * ROUNDS) + [2] + [1] * (1 + 2 * ROUNDS)


def weave(ref, value):
    rows = value.shape[0]
    ref[pl.ds(0, rows, stride=2), :] = value[:, :HALF]
    ref[pl.ds(1, rows, stride=2), :] = value[:, HALF:]


def unweave(ref):
    rows = ref.shape[0] // 2
    return ref[pl.ds(0, rows, stride=2), :], ref[pl.ds(1, rows, stride=2), :]


def selector():
    row = lax.broadcasted_iota(jnp.int32, (8, HALF), 0)
    lane = lax.broadcasted_iota(jnp.int32, (8, HALF), 1)
    slot = jnp.where(lane == CH, 64.0, jnp.where(lane == CH + 1, 1.0, 0.0))
    known = jnp.where(lane == CH + 2, 1.0, 0.0)
    return jnp.where(row == 0, slot, jnp.where(row == 1, known, 0.0)).astype(jnp.bfloat16)


def ids_along(arrived):
    codes = inner(selector(), arrived, 1, 1)
    return jnp.where(codes[1:2, :] > 0, codes[0:1, :], -1.0).astype(jnp.int32)


def ids_down(arrived):
    codes = inner(arrived, selector(), 1, 1)
    return jnp.where(codes[:, 1:2] > 0, codes[:, 0:1], -1.0).astype(jnp.int32)


def whole(shape):
    return pl.BlockSpec(shape, lambda *_: (0,) * len(shape))


def node_terms(mesh, mats, bias):
    blocks = mesh.shape[0]
    tile = 1024

    def body(mesh_ref, mats_ref, bias_ref, dest_ref, self_ref):
        lowered = mesh_ref[...].astype(jnp.bfloat16)
        weave(dest_ref, inner(lowered, mats_ref[1], 1, 0) + bias_ref[0:1, :])
        self_ref[...] = inner(lowered, mats_ref[3], 1, 0) + bias_ref[1:2, :]

    rows = pl.BlockSpec((tile, D), lambda i: (i, 0))
    woven = pl.BlockSpec((2 * tile, HALF), lambda i: (i, 0))
    return pl.pallas_call(
        body,
        grid=(blocks // tile,),
        in_specs=[rows, whole(mats.shape), whole(bias.shape)],
        out_specs=[woven, rows],
        out_shape=[
            jax.ShapeDtypeStruct((2 * blocks, HALF), jnp.float32),
            jax.ShapeDtypeStruct((blocks, D), jnp.float32),
        ],
        compiler_params=LIMIT,
        cost_estimate=cost(4),
        name="node_terms",
    )(mesh, mats, bias)


def round_forward(index, mesh, before, own, after, mats, terms, following, decoder=()):
    blocks = mesh.shape[0]
    tile, chunk = 512, 16
    turns, high = tile // chunk, 2 * chunk
    more = following is not None
    spans = [before.shape[0], own.shape[0], after.shape[0]]
    reach = sum(spans)

    def body(*refs):
        index_ref, mesh_ref, before_ref, own_ref, after_ref, mats_ref, dest_ref = refs[:7]
        self_ref, refs = refs[7], refs[:7] + refs[8:]
        raw, table, rows, wide, sems = refs[-5:]
        if more:
            next_ref, sent_ref = refs[7], refs[13]
            new_ref, back_ref, update_ref, agg_ref, slope_ref = refs[8:13]
        else:
            ids_ref, dec_ref, out_ref, head_ref = refs[7:11]
            new_ref, back_ref, update_ref, agg_ref, slope_ref = refs[11:16]
            branch_ref, fetched_ref, decoded_ref, turn_ref = refs[16:20]
            total_ref = refs[20]
        step = pl.program_id(0)

        @pl.when(step == 0)
        def _():
            copies = []
            start = 0
            for n, (source, span) in enumerate(zip((before_ref, own_ref, after_ref), spans)):
                copies.append(
                    pltpu.make_async_copy(source, raw.at[pl.ds(start, span)], sems.at[n])
                )
                start = start + span
            for copy in copies:
                copy.start()
            for copy in copies:
                copy.wait()

            @pl.loop(0, reach // 256)
            def _(i):
                at = pl.multiple_of(i * 256, 256)
                table[pl.ds(at, 256), :] = raw[pl.ds(at, 256), :].astype(jnp.float32)

        mesh_in = mesh_ref[...]

        def fetch(turn):
            for edge in range(K):
                base = edge * blocks + step * tile + turn * chunk
                spots = [index_ref[base + u] for u in range(chunk)]
                values = [table[pl.ds(pl.multiple_of(spot, 2), 2), :] for spot in spots]
                for u in range(chunk):
                    spot = pl.multiple_of(edge * 2 * tile + turn * high + 2 * u, 2)
                    rows[pl.ds(spot, 2), :] = values[u]

        def load(turn):
            at = pl.multiple_of(turn * high, high)
            taken = [
                rows[pl.ds(pl.multiple_of(edge * 2 * tile + turn * high, high), high), :]
                for edge in range(K)
            ]
            return at, dest_ref[pl.ds(at, high), :], taken

        def dense(at, dest, taken):
            total = None
            for edge in range(K):
                value = taken[edge] + dest
                sigma = sigmoid(value)
                out = value * sigma
                slope_ref[edge, pl.ds(at, high), :] = (sigma + out * (1.0 - sigma)).astype(
                    jnp.bfloat16
                )
                total = out if total is None else total + out
            wide[pl.ds(at, high), :] = total * (1.0 / K)

        def some(turn, carry):
            loaded = load(turn - 1)
            fetch(turn)
            dense(*loaded)
            return carry

        fetch(0)
        lax.fori_loop(1, turns, some, 0)
        dense(*load(turns - 1))
        first, second = unweave(wide)
        first, second = first.astype(jnp.bfloat16), second.astype(jnp.bfloat16)
        agg_ref[:, :HALF] = first
        agg_ref[:, HALF:] = second
        update_in = (
            inner(first, mats_ref[2, :HALF, :], 1, 0)
            + inner(second, mats_ref[2, HALF:, :], 1, 0)
            + self_ref[...]
        )
        sigma = sigmoid(update_in)
        out = update_in * sigma
        back_ref[...] = sigma + out * (1.0 - sigma)
        update = out.astype(jnp.bfloat16)
        update_ref[...] = update
        new = mesh_in + inner(update, mats_ref[4], 1, 0)
        new_ref[...] = new
        lowered = new.astype(jnp.bfloat16)
        if more:
            weave(wide, inner(lowered, next_ref[0], 1, 0))
            sent_ref[...] = wide[...].astype(jnp.bfloat16)
            return
        nodes = lax.broadcasted_iota(jnp.int32, (ids_ref.shape[0], tile), 1) + step * tile
        chooser = jnp.where(nodes == ids_ref[...], 1.0, 0.0).astype(jnp.bfloat16)
        found = inner(chooser, lowered, 1, 0)

        @pl.when(step == 0)
        def _():
            total_ref[...] = found

        @pl.when(step > 0)
        def _():
            total_ref[...] += found

        @pl.when(step == blocks // tile - 1)
        def _():
            fetched = total_ref[...].astype(jnp.bfloat16)
            fetched_ref[...] = fetched
            value = inner(fetched, dec_ref[...], 1, 0) + head_ref[2:3, :]
            sigma = sigmoid(value)
            out = value * sigma
            turn_ref[...] = sigma + out * (1.0 - sigma)
            decoded = out.astype(jnp.bfloat16)
            decoded_ref[...] = decoded
            branch_ref[...] = inner(decoded, out_ref[...], 1, 0).astype(jnp.bfloat16)

    whole_rows = pl.BlockSpec((tile, D), lambda i, *_: (i, 0))
    woven = pl.BlockSpec((2 * tile, HALF), lambda i, *_: (i, 0))
    ins = [whole_rows] + [pl.BlockSpec(memory_space=pl.ANY)] * 3
    ins = ins + [whole(mats.shape), woven, whole_rows]
    outs = [whole_rows] * 4 + [pl.BlockSpec((K, 2 * tile, HALF), lambda i, *_: (0, i, 0))]
    shapes = [
        jax.ShapeDtypeStruct((blocks, D), jnp.float32),
        jax.ShapeDtypeStruct((blocks, D), jnp.float32),
        jax.ShapeDtypeStruct((blocks, D), jnp.bfloat16),
        jax.ShapeDtypeStruct((blocks, D), jnp.bfloat16),
        jax.ShapeDtypeStruct((K, 2 * blocks, HALF), jnp.bfloat16),
    ]
    args = [index, mesh, before, own, after, mats, *terms]
    if more:
        ins.append(pl.BlockSpec((1, D, D), lambda *_: (0, 0, 0)))
        outs.append(woven)
        shapes.append(jax.ShapeDtypeStruct((2 * blocks, HALF), jnp.bfloat16))
        args.append(following)
    scratch = []
    if decoder:
        posts = decoder[0].shape[0]
        ins = ins + [whole(arg.shape) for arg in decoder]
        args = args + list(decoder)
        for width, kind in ((HALF, jnp.bfloat16), (D, jnp.bfloat16), (D, jnp.bfloat16), (D, jnp.float32)):
            outs.append(whole((posts, width)))
            shapes.append(jax.ShapeDtypeStruct((posts, width), kind))
        scratch = [pltpu.VMEM((posts, D), jnp.float32)]
    return pl.pallas_call(
        body,
        grid_spec=pltpu.PrefetchScalarGridSpec(
            num_scalar_prefetch=1,
            grid=(blocks // tile,),
            in_specs=ins,
            out_specs=outs,
            scratch_shapes=scratch
            + [
                pltpu.VMEM((reach, HALF), jnp.bfloat16),
                pltpu.VMEM((reach, HALF), jnp.float32),
                pltpu.VMEM((K * 2 * tile, HALF), jnp.float32),
                pltpu.VMEM((2 * tile, HALF), jnp.float32),
                pltpu.SemaphoreType.DMA((3,)),
            ],
        ),
        out_shape=shapes,
        compiler_params=LIMIT,
        cost_estimate=cost(25),
        name="round_forward",
    )(*args)


def edges_backward(index, back, slopes, mats, carried=(), landed=()):
    blocks = back.shape[0]
    tile, chunk = 512, 16
    steps, turns, high = blocks // tile, tile // chunk, 2 * chunk
    reach = 2 * (blocks + 2 * H)

    def body(*refs):
        if carried:
            index_ref, back_ref, slope_ref, mats_ref = refs[:4]
            past, rest = refs[4:9], refs[9:]
            (new_ref, out_ref, sent_ref), rest = rest[:3], rest[3:]
        else:
            index_ref, back_ref, slope_ref, mats_ref = refs[:4]
            (ids_ref, landed_ref, turn_ref, w_out_ref, w_dec_ref), rest = refs[4:9], refs[9:]
            (new_ref, out_ref, gdec_ref), rest = rest[:3], rest[3:]
            gathered, rest = rest[5], rest[:5] + rest[6:]
        guin_ref, low_ref, before_ref, own_ref, after_ref, wide, wider, flows, *tables = rest
        step = pl.program_id(0)

        @pl.when(step == 0)
        def _():
            @pl.loop(0, reach // 256)
            def _(i):
                for table in tables:
                    table[pl.ds(pl.multiple_of(i * 256, 256), 256), :] = jnp.zeros(
                        (256, HALF), jnp.float32
                    )

        if carried:
            new, one, two = ended(*past, wide)
            sent_ref[:, :HALF] = one
            sent_ref[:, HALF:] = two
            new_ref[...] = new
            grad_out = new.astype(jnp.bfloat16)
            out_ref[...] = grad_out
        else:

            @pl.when(step == 0)
            def _():
                grad_dec = inner(landed_ref[...], w_out_ref[...], 1, 1) * turn_ref[...]
                grad_dec = grad_dec.astype(jnp.bfloat16)
                gdec_ref[...] = grad_dec
                gathered[...] = inner(grad_dec, w_dec_ref[...], 1, 1).astype(jnp.bfloat16)

            nodes = lax.broadcasted_iota(jnp.int32, (tile, landed_ref.shape[0]), 0) + step * tile
            chooser = jnp.where(nodes == ids_ref[...], 1.0, 0.0).astype(jnp.bfloat16)
            new = inner(chooser, gathered[...], 1, 0)
            new_ref[...] = new
            grad_out = new.astype(jnp.bfloat16)
            out_ref[...] = grad_out
        grad_uin = (inner(grad_out, mats_ref[4], 1, 1) * back_ref[...]).astype(jnp.bfloat16)
        guin_ref[...] = grad_uin
        weave(wide, inner(grad_uin, mats_ref[2], 1, 1) * (1.0 / K))

        def dense(turn):
            at = pl.multiple_of(turn * high, high)
            grad_agg = wide[pl.ds(at, high), :]
            total, parts = None, []
            for edge in range(K):
                flow = grad_agg * slope_ref[edge, pl.ds(at, high), :].astype(jnp.float32)
                parts.append(flow)
                total = flow if total is None else total + flow
            return at, total, parts

        def keep(turn, at, total, parts):
            for edge in range(K):
                spot = pl.multiple_of(edge * 2 * tile + turn * high, high)
                flows[pl.ds(spot, high), :] = parts[edge]
            wider[pl.ds(at, high), :] = total

        def scatter(turn):
            for u in range(chunk):
                spots, sums = [], []
                for edge in range(K):
                    base = edge * blocks + step * tile + turn * chunk
                    spots.append(pl.multiple_of(index_ref[base + u], 2))
                for edge in range(K):
                    spot = pl.multiple_of(edge * 2 * tile + turn * high + 2 * u, 2)
                    sums.append(tables[edge][pl.ds(spots[edge], 2), :] + flows[pl.ds(spot, 2), :])
                for edge in range(K):
                    tables[edge][pl.ds(spots[edge], 2), :] = sums[edge]

        def some(turn, carry):
            found = dense(turn)
            scatter(turn - 1)
            keep(turn, *found)
            return carry

        keep(0, *dense(0))
        lax.fori_loop(1, turns, some, 0)
        scatter(turns - 1)
        first, second = unweave(wider)
        low_ref[:, :HALF] = first.astype(jnp.bfloat16)
        low_ref[:, HALF:] = second.astype(jnp.bfloat16)

        @pl.when(step == steps - 1)
        def _():
            def summed(at):
                value = tables[0][pl.ds(at, 256), :]
                for table in tables[1:]:
                    value = value + table[pl.ds(at, 256), :]
                return value

            @pl.loop(0, 2 * H // 256)
            def _(i):
                at = pl.multiple_of(i * 256, 256)
                far = pl.multiple_of(2 * H + 2 * blocks + at, 256)
                before_ref[pl.ds(at, 256), :] = summed(at).astype(jnp.bfloat16)
                after_ref[pl.ds(at, 256), :] = summed(far).astype(jnp.bfloat16)

            @pl.loop(0, 2 * blocks // 256)
            def _(i):
                at = pl.multiple_of(i * 256, 256)
                own_ref[pl.ds(at, 256), :] = summed(pl.multiple_of(2 * H + at, 256))

    rows = pl.BlockSpec((tile, D), lambda i, *_: (i, 0))
    woven = pl.BlockSpec((2 * tile, HALF), lambda i, *_: (i, 0))
    low = jax.ShapeDtypeStruct((blocks, D), jnp.bfloat16)
    low_posts = (landed[1].shape[0], D) if landed else None
    last = low if carried else jax.ShapeDtypeStruct(low_posts, jnp.bfloat16)
    return pl.pallas_call(
        body,
        grid_spec=pltpu.PrefetchScalarGridSpec(
            num_scalar_prefetch=1,
            grid=(steps,),
            in_specs=[
                rows,
                pl.BlockSpec((K, 2 * tile, HALF), lambda i, *_: (0, i, 0)),
                whole(mats.shape),
            ]
            + ([rows] + [woven] * 3 + [whole(mats.shape)] if carried else [])
            + [whole(arg.shape) for arg in landed],
            out_specs=([rows] * 3 if carried else [rows, rows, whole(low_posts)])
            + [
                rows, rows,
                whole((2 * H, HALF)), whole((2 * blocks, HALF)), whole((2 * H, HALF)),
            ],
            scratch_shapes=([] if carried else [pltpu.VMEM(low_posts, jnp.bfloat16)])
            + [
                pltpu.VMEM((2 * tile, HALF), jnp.float32),
                pltpu.VMEM((2 * tile, HALF), jnp.float32),
                pltpu.VMEM((2 * tile * K, HALF), jnp.float32),
            ]
            + [pltpu.VMEM((reach, HALF), jnp.float32)] * K,
        ),
        out_shape=[
            jax.ShapeDtypeStruct((blocks, D), jnp.float32),
            low,
            last,
            low,
            low,
            jax.ShapeDtypeStruct((2 * H, HALF), jnp.bfloat16),
            jax.ShapeDtypeStruct((2 * blocks, HALF), jnp.float32),
            jax.ShapeDtypeStruct((2 * H, HALF), jnp.bfloat16),
        ],
        compiler_params=LIMIT,
        cost_estimate=cost(28 if carried else 25),
        name="edges_backward",
    )(index, back, slopes, mats, *carried, *landed)


def ended(part_ref, own_ref, first_ref, last_ref, mats_ref, wide):
    wide[...] = (
        own_ref[...] + first_ref[...].astype(jnp.float32) + last_ref[...].astype(jnp.float32)
    )
    one, two = unweave(wide)
    one, two = one.astype(jnp.bfloat16), two.astype(jnp.bfloat16)
    new = (
        part_ref[...]
        + inner(one, mats_ref[0, :, :HALF], 1, 1)
        + inner(two, mats_ref[0, :, HALF:], 1, 1)
    )
    return new, one, two


def carried_terms(grad_mesh, grad_uin, dest_low, mats):
    blocks = grad_mesh.shape[0]
    tile = 1024

    def body(grad_ref, guin_ref, dest_ref, mats_ref, part_ref):
        part_ref[...] = (
            grad_ref[...]
            + inner(guin_ref[...], mats_ref[3], 1, 1)
            + inner(dest_ref[...], mats_ref[1], 1, 1)
        )

    rows = pl.BlockSpec((tile, D), lambda i: (i, 0))
    return pl.pallas_call(
        body,
        grid=(blocks // tile,),
        in_specs=[rows, rows, rows, whole(mats.shape)],
        out_specs=rows,
        out_shape=jax.ShapeDtypeStruct((blocks, D), jnp.float32),
        compiler_params=LIMIT,
        cost_estimate=cost(4),
        name="carried_terms",
    )(grad_mesh, grad_uin, dest_low, mats)


def encode_rows(arrived, w_in, w_node, biases, source):
    posts = arrived.shape[0]
    tile = 512

    def body(
        arrived_ref, in_ref, node_ref, bias_ref, source_ref,
        mesh_ref, gathered_ref, sent_ref, ids_ref, down_ref, encoded, wide,
    ):
        step = pl.program_id(0)

        @pl.when(step == 0)
        def _():
            entering = inner(arrived_ref[...], in_ref[...], 1, 0) + bias_ref[0:1, :]
            encoded[...] = silu(entering).astype(jnp.bfloat16)
            ids_ref[...] = ids_along(arrived_ref[...])
            down_ref[...] = ids_down(arrived_ref[...])

        nodes = lax.broadcasted_iota(jnp.int32, (tile, posts), 0) + step * tile
        chooser = jnp.where(nodes == ids_ref[...], 1.0, 0.0).astype(jnp.bfloat16)
        gathered = inner(chooser, encoded[...], 1, 0).astype(jnp.bfloat16)
        gathered_ref[...] = gathered
        mesh = silu(inner(gathered, node_ref[...], 1, 0) + bias_ref[1:2, :])
        mesh_ref[...] = mesh
        weave(wide, inner(mesh.astype(jnp.bfloat16), source_ref[0], 1, 0))
        sent_ref[...] = wide[...].astype(jnp.bfloat16)

    rows = pl.BlockSpec((tile, D), lambda i: (i, 0))
    args = (arrived, w_in, w_node, biases, source)
    return pl.pallas_call(
        body,
        grid=(H // tile,),
        in_specs=[whole(arg.shape) for arg in args[:-1]]
        + [pl.BlockSpec((1, D, D), lambda *_: (0, 0, 0))],
        out_specs=[rows, rows, pl.BlockSpec((2 * tile, HALF), lambda i: (i, 0))]
        + [whole((1, posts)), whole((posts, 1))],
        out_shape=[
            jax.ShapeDtypeStruct((H, D), jnp.float32),
            jax.ShapeDtypeStruct((H, D), jnp.bfloat16),
            jax.ShapeDtypeStruct((2 * H, HALF), jnp.bfloat16),
            jax.ShapeDtypeStruct((1, posts), jnp.int32),
            jax.ShapeDtypeStruct((posts, 1), jnp.int32),
        ],
        scratch_shapes=[pltpu.VMEM((posts, D), jnp.bfloat16), pltpu.VMEM((2 * tile, HALF), jnp.float32)],
        compiler_params=LIMIT,
        cost_estimate=cost(5),
        name="encode_rows",
    )(*args)


def encode_backward(carried, mesh, gathered, arrived, ids, w_in, w_node, biases):
    blocks = mesh.shape[0]
    posts = arrived.shape[0]
    tile = 512
    steps = blocks // tile

    def body(
        part_ref, own_ref, first_ref, last_ref, mats_ref,
        mesh_ref, gathered_ref, arrived_ref, ids_ref, in_ref, node_ref, bias_ref,
        new_ref, out_ref, gin_ref, gnode_ref, gbias_ref, gsource_ref, total, wide,
    ):
        step = pl.program_id(0)

        @pl.when(step == 0)
        def _():
            for ref in (total, gnode_ref, gbias_ref, gsource_ref):
                ref[...] = jnp.zeros(ref.shape, jnp.float32)

        new, one, two = ended(part_ref, own_ref, first_ref, last_ref, mats_ref, wide)
        new_ref[...] = new
        out_ref[...] = new.astype(jnp.bfloat16)
        lowered = mesh_ref[...].astype(jnp.bfloat16)
        gsource_ref[:, :HALF] += inner(lowered, one, 0, 0)
        gsource_ref[:, HALF:] += inner(lowered, two, 0, 0)
        node_in = inner(gathered_ref[...], node_ref[...], 1, 0) + bias_ref[1:2, :]
        grad_node = (new * slope(node_in)).astype(jnp.bfloat16)
        gbias_ref[1:2, :] += jnp.sum(grad_node.astype(jnp.float32), 0, keepdims=True)
        gnode_ref[...] += inner(gathered_ref[...], grad_node, 0, 0)
        back = inner(grad_node, node_ref[...], 1, 1).astype(jnp.bfloat16)
        nodes = lax.broadcasted_iota(jnp.int32, (posts, tile), 1) + step * tile
        chooser = jnp.where(nodes == ids_ref[...], 1.0, 0.0).astype(jnp.bfloat16)
        total[...] += inner(chooser, back, 1, 0)

        @pl.when(step == steps - 1)
        def _():
            entering = inner(arrived_ref[...], in_ref[...], 1, 0) + bias_ref[0:1, :]
            grad_enc = (total[...] * slope(entering)).astype(jnp.bfloat16)
            gbias_ref[0:1, :] = jnp.sum(grad_enc.astype(jnp.float32), 0, keepdims=True)
            gin_ref[...] = inner(arrived_ref[...], grad_enc, 0, 0)

    rows = pl.BlockSpec((tile, D), lambda i: (i, 0))
    woven = pl.BlockSpec((2 * tile, HALF), lambda i: (i, 0))
    args = (arrived, ids, w_in, w_node, biases)
    shapes = [(HALF, D), (D, D), (2, D), (D, D)]
    return pl.pallas_call(
        body,
        grid=(steps,),
        in_specs=[rows] + [woven] * 3 + [whole(carried[4].shape), rows, rows]
        + [whole(arg.shape) for arg in args],
        out_specs=[rows, rows] + [whole(shape) for shape in shapes],
        out_shape=[
            jax.ShapeDtypeStruct((blocks, D), jnp.float32),
            jax.ShapeDtypeStruct((blocks, D), jnp.bfloat16),
        ]
        + [jax.ShapeDtypeStruct(shape, jnp.float32) for shape in shapes],
        scratch_shapes=[pltpu.VMEM((posts, D), jnp.float32), pltpu.VMEM((2 * tile, HALF), jnp.float32)],
        compiler_params=LIMIT,
        cost_estimate=cost(10),
        name="encode_backward",
    )(*carried, mesh, gathered, *args)


def shards(walk, master, moment1, moment2, inputs, targets, valid, owner, slot, neighbours, partner):
    bands = lax.axis_size("space")
    band = lax.axis_index("space")
    peers = lax.axis_size(ALL)
    place = lax.axis_index(ALL)
    shard = master.shape[0]
    total_size = shard * peers
    height = pieces_of(total_size, peers)[3]
    offset = lax.rem(lax.rem(shard, D) * place, D)
    piece = lax.dynamic_update_slice_in_dim(
        jnp.zeros((height * D,), jnp.bfloat16), master.astype(jnp.bfloat16), offset, 0
    )
    state_in = inputs[0]
    counted = valid[0].astype(jnp.float32)
    local_count = jnp.sum(valid[0])
    digits = (local_count >> jnp.array([16, 8, 0], jnp.int32)) & 255
    piece = lax.dynamic_update_slice(
        piece.reshape(height, D), digits.astype(jnp.bfloat16)[None, :], (height - 1, 0)
    )
    points = state_in.shape[1]
    blocks = neighbours.shape[0]
    assert blocks == H
    capacity = max(2, 2 * points // bands)
    target_band = owner[0, :, 0]
    hits = (target_band[:, None] == jnp.arange(bands, dtype=jnp.int32)[None, :]).astype(jnp.int32)
    ranks = jnp.sum(jnp.cumsum(hits, 0) * hits, 1) - 1
    places_out = jnp.sum(hits * jnp.asarray(walk, jnp.int32)[None, :], 1) * capacity + ranks
    poster = (
        jnp.arange(bands * capacity, dtype=jnp.int32)[:, None] == places_out[None, :]
    ).astype(jnp.bfloat16)
    spots = slot[0][None, :]
    columns = jnp.concatenate(
        [
            state_in,
            (spots // 64).astype(jnp.bfloat16),
            (spots % 64).astype(jnp.bfloat16),
            jnp.ones((1, points), jnp.bfloat16),
            jnp.zeros((HALF - CH - 3, points), jnp.bfloat16),
        ],
        0,
    )

    def exchanged(rows):
        return lax.all_to_all(
            rows.reshape(bands, capacity, HALF), "space", split_axis=0, concat_axis=0, tiled=True
        ).reshape(bands * capacity, HALF)

    held, posted = gathered_blocks(piece, inner(poster, columns, 1, 1).astype(jnp.bfloat16))
    arrived = exchanged(posted)
    w_in, w_node, w_dec, w_out, *w_round, biases, digits = spread_rows(
        held, total_size, peers, place
    )
    arrived, biases = lax.optimization_barrier((arrived, biases))
    count = digits[0, 0] * 65536.0 + digits[0, 1] * 256.0 + digits[0, 2]
    w_out = jnp.pad(w_out.reshape(D, CH), ((0, 0), (0, HALF - CH)))
    w_round = [mats.reshape(5, D, D) for mats in w_round]
    b_head = biases[:3]
    b_round = biases[3:].reshape(ROUNDS, 2, D)
    mesh, gathered, sent, ids_row, ids = encode_rows(
        arrived, w_in, w_node, biases, w_round[0]
    )
    sent, partner, neighbours, counted = lax.optimization_barrier(
        (sent, partner, neighbours, counted)
    )
    index = 2 * ((neighbours - band * blocks + H) % (blocks * bands)).T.reshape(-1)
    moved = [(n, place) for n, place in enumerate(walk) if n != place]
    stays = jnp.asarray([n == place for n, place in enumerate(walk)])[band]
    index = lax.ppermute(index, "space", list(enumerate(walk)))

    def at_home(rows):
        return lax.ppermute(rows, "space", [(j, i) for i, j in moved])

    def settled(own, came):
        return jnp.where(stays, own, came.astype(jnp.float32))

    partner_by = partner - band * points - jnp.arange(points, dtype=jnp.int32)
    coded = jnp.where(partner_by >= NEAR, partner_by - NEAR + 1, 0).astype(jnp.bfloat16)
    low_valid = jnp.concatenate([counted.astype(jnp.bfloat16), coded[None, :]], 0)
    valid_around = jnp.concatenate(
        [
            shifted(low_valid[:, points - ROWW :], "space", 1),
            low_valid,
            shifted(low_valid[:, :ROWW], "space", -1),
        ],
        1,
    )
    kept = []
    for layer in range(ROUNDS):
        before, after = halo(walk, sent, sent)
        terms = node_terms(mesh, w_round[layer], b_round[layer])
        if layer == 0:
            before, valid_around = lax.optimization_barrier((before, valid_around))
        following = w_round[layer + 1] if layer + 1 < ROUNDS else None
        new, back, update, agg, slopes, *rest = round_forward(
            index, mesh, before, sent, after, w_round[layer], terms, following,
            () if following is not None else (ids, w_dec, w_out, biases),
        )
        kept.append((mesh, back, update, agg, slopes))
        mesh = new
        sent = rest[0]
    wide_valid = valid_around[:CH].astype(jnp.float32)
    coded = valid_around[CH : CH + 1, : points + ROWW].astype(jnp.float32)
    weights = [
        (
            by,
            jnp.where(coded == by - NEAR + 1, 1.0, 0.0)
            * wide_valid[:, : points + ROWW]
            * wide_valid[:, by : by + points + ROWW],
        )
        for by in range(NEAR, ROWW + 1)
    ]
    branch_rows, fetched, decoded, dec_turn = rest
    returned = exchanged(branch_rows)
    branch = inner(returned, poster, 0, 0)[:CH]
    err = state_in.astype(jnp.float32) + branch - targets[0].astype(jnp.float32)
    def widened(values):
        low = values.astype(jnp.bfloat16)
        before = shifted(low[:, points - ROWW :], "space", 1).astype(jnp.float32)
        after = shifted(low[:, :ROWW], "space", -1).astype(jnp.float32)
        return jnp.concatenate([before, values, after], 1)

    wide_err = widened(err)
    paired = jnp.zeros((CH, points + ROWW), jnp.float32)
    pair_total = jnp.zeros((CH, points), jnp.float32)
    for by, both in weights:
        gap = both * (wide_err[:, : points + ROWW] - wide_err[:, by : by + points + ROWW])
        paired = paired + gap
        pair_total = pair_total + gap[:, ROWW:] * (
            wide_err[:, ROWW : ROWW + points] - wide_err[:, ROWW + by : ROWW + by + points]
        )
    local_total = jnp.sum(counted * err * err) + 0.5 * jnp.sum(pair_total)
    grad_pred = 2.0 * counted * err + paired[:, ROWW:]
    for by, both in weights:
        gap = both * (wide_err[:, : points + ROWW] - wide_err[:, by : by + points + ROWW])
        grad_pred = grad_pred - gap[:, ROWW - by : ROWW - by + points]
    grad_pred = grad_pred / count
    grad_rows = jnp.pad(grad_pred.astype(jnp.bfloat16), ((0, HALF - CH), (0, 0)))
    landed = exchanged(inner(poster, grad_rows, 1, 1).astype(jnp.bfloat16))
    landed, final_mesh = lax.optimization_barrier((landed, mesh.astype(jnp.bfloat16)))
    final_mesh = at_home(final_mesh)
    mats_grads = [None] * (5 * ROUNDS)
    bias_grads = [None] * (2 * ROUNDS)
    carried, grad_mesh = (), None
    for layer in reversed(range(ROUNDS)):
        old, back, update, agg, slopes = kept[layer]
        first_step = not carried
        grad_mesh, leaving, extra, grad_uin, dest_low, to_before, own, to_after = edges_backward(
            index, back, slopes, w_round[layer], carried,
            (ids_row, landed, dec_turn, w_out, w_dec) if first_step else (),
        )
        if not first_step:
            mats_grads[5 * layer + 5] = inner(
                kept[layer + 1][0].astype(jnp.bfloat16), extra, 0, 0
            )
        else:
            grad_wout = inner(decoded, landed, 0, 0)[:, :CH]
            grad_bdec = jnp.sum(extra.astype(jnp.float32), 0, keepdims=True)
            grad_wdec = inner(fetched, extra, 0, 0)
            to_before, to_after, final_mesh = lax.optimization_barrier(
                (to_before, to_after, final_mesh)
            )
        from_before, from_after = halo(walk, to_after, to_before)
        if first_step:
            from_before, final_mesh = lax.optimization_barrier(
                (from_before, settled(mesh, final_mesh))
            )
        lowered = old.astype(jnp.bfloat16)
        mats_grads[5 * layer + 1 : 5 * layer + 5] = [
            inner(lowered, dest_low, 0, 0),
            inner(agg, grad_uin, 0, 0),
            inner(lowered, grad_uin, 0, 0),
            inner(update, leaving, 0, 0),
        ]
        bias_grads[2 * layer] = jnp.sum(dest_low.astype(jnp.float32), 0, keepdims=True)
        bias_grads[2 * layer + 1] = jnp.sum(grad_uin.astype(jnp.float32), 0, keepdims=True)
        part = carried_terms(grad_mesh, grad_uin, dest_low, w_round[layer])
        carried = (part, own, from_before, from_after, w_round[layer])
    grad_mesh, leaving, grad_win, grad_wnode, grad_bpair, mats_grads[0] = encode_backward(
        carried, kept[0][0], gathered, arrived, ids, w_in, w_node, biases
    )
    parts = [grad_win, grad_wnode, grad_wdec, grad_wout.reshape(CH, D)]
    parts = parts + mats_grads
    parts = parts + [grad_bpair, grad_bdec] + bias_grads
    keep, send = collect_rows(parts, total_size, peers, place)
    mine, leaving = reduced_piece(keep, send, leaving)
    late = at_home(leaving)
    mine = lax.dynamic_slice_in_dim(mine.reshape(-1), offset, shard)
    lane = lax.broadcasted_iota(jnp.int32, (8, HALF), 1)
    sums, late = summed_everywhere(
        jnp.where(lane == 0, local_total, jnp.sum(mine * mine)), late
    )
    total, norm = sums[0, 0], jnp.sqrt(sums[0, 1])
    node_grads = settled(grad_mesh, late)
    clipped = mine * jnp.minimum(1.0, 0.05 / norm)
    first = 0.9 * moment1 + 0.1 * clipped
    second = 0.999 * moment2 + 0.001 * clipped * clipped
    first_hat = first / (1.0 - 0.9**STEP)
    second_hat = second / (1.0 - 0.999**STEP)
    updated = master - 0.1 * (first_hat / (jnp.sqrt(second_hat) + 1e-08) + 0.1 * master)
    return (
        total.reshape(1),
        count.reshape(1),
        norm.reshape(1),
        updated,
        first,
        second,
        updated.astype(jnp.bfloat16),
        final_mesh.reshape(1, blocks, D),
        node_grads.reshape(1, blocks, D),
        grad_pred.reshape(1, grad_pred.shape[0], points),
    )


def solution(mesh):
    return jax.shard_map(
        functools.partial(shards, walk_of(mesh)),
        mesh=mesh,
        in_specs=(
            P(("dp", "space")),
            P(("dp", "space")),
            P(("dp", "space")),
            P("dp", None, "space"),
            P("dp", None, "space"),
            P("dp", None, "space"),
            P("dp", "space", None),
            P("dp", "space"),
            P("space", None),
            P("space"),
        ),
        out_specs=(
            P(),
            P(),
            P(),
            P(("dp", "space")),
            P(("dp", "space")),
            P(("dp", "space")),
            P(("dp", "space")),
            P("dp", "space", None),
            P("dp", "space", None),
            P("dp", None, "space"),
        ),
        check_vma=False,
    )
```

```python
import functools

import jax
import jax.numpy as jnp
from jax import lax
from jax.experimental import pallas as pl
from jax.experimental.pallas import tpu as pltpu
from jax.sharding import PartitionSpec as P

D = 256
HALF = 128
CH = 78
ROUNDS = 3
K = 6
ROWW = 360
NEAR = 358
STEP = 10
H = 2048
ALL = ("dp", "space")
LIMIT = pltpu.CompilerParams(vmem_limit_bytes=60 * 2**20)


def cost(micros):
    return pl.CostEstimate(flops=0, bytes_accessed=micros * 3_000_000, transcendentals=0)


def inner(left, right, left_dim, right_dim):
    return lax.dot_general(
        left, right, (((left_dim,), (right_dim,)), ((), ())), preferred_element_type=jnp.float32
    )


def sigmoid(value):
    return 0.5 * jnp.tanh(0.5 * value) + 0.5


def silu(value):
    return value * sigmoid(value)


def slope(value):
    sigma = sigmoid(value)
    return sigma * (1.0 + value * (1.0 - sigma))


def shifted(shard, axis, by):
    peers = lax.axis_size(axis)
    pairs = [(i, i + by) for i in range(peers) if 0 <= i + by < peers]
    return lax.ppermute(shard, axis, pairs)


def walk_of(mesh):
    count = mesh.shape["space"]
    chips = [getattr(device, "coords", None) for device in mesh.devices[0].reshape(-1)]
    if any(chip is None for chip in chips) or len(set(map(tuple, chips))) != count:
        return list(range(count))
    at = {tuple(chip): n for n, chip in enumerate(chips)}
    xs, ys, zs = (sorted({chip[n] for chip in at}) for n in range(3))
    if len(xs) * len(ys) * len(zs) != count:
        return list(range(count))
    if (len(xs), len(ys), len(zs)) == (2, 2, 4):
        corners = [(0, 0), (1, 0), (0, 1), (1, 1)]
        planes = [(0, 1, 3, 2), (2, 0, 1, 3), (3, 1, 0, 2), (2, 3, 1, 0)]
        steps = [(*corners[n], z) for z, plane in enumerate(planes) for n in plane]
        return [at[(xs[x], ys[y], zs[z])] for x, y, z in steps]
    walk, plane = [], []
    for n, y in enumerate(ys):
        plane = plane + [(x, y) for x in (xs if n % 2 == 0 else xs[::-1])]
    for n, z in enumerate(zs):
        walk = walk + [at[(x, y, z)] for x, y in (plane if n % 2 == 0 else plane[::-1])]
    return walk


def halo(walk, last, initial):
    up = list(zip(walk, walk[1:] + walk[:1]))
    down = [(j, i) for i, j in up]
    return lax.ppermute(last, "space", up), lax.ppermute(initial, "space", down)


def pieces_of(total, peers):
    share = total // peers
    starts = [share * d // D for d in range(peers)]
    counts = [-(-share * (d + 1) // D) - starts[d] for d in range(peers)]
    shared = [share * d % D != 0 for d in range(peers)]
    height = -(-max(counts) // 16) * 16
    return starts, counts, shared, height


def parts_of():
    return [CH, D, D, CH] + [5 * D] * ROUNDS + [3 + 2 * ROUNDS]


def swapped(value, axis, bit):
    return lax.ppermute(value, axis, [(i, i ^ bit) for i in range(lax.axis_size(axis))])


def bits_of(axis):
    return [1 << n for n in range(lax.axis_size(axis).bit_length() - 1)]


def others(value, axis, bits):
    masks = [sum(bit for n, bit in enumerate(bits) if m >> n & 1) for m in range(1, 1 << len(bits))]
    return [swapped(value, axis, mask) for mask in masks]


def upper_groups():
    bits = bits_of("space")[2:]
    return [tuple(bits[n : n + 2]) for n in range(0, len(bits), 2)]


def orders():
    return [(1, 2), (2, 1)]


def summed_everywhere(value, arriving):
    for bits in reversed(upper_groups()):
        value = sum(others(value, "space", bits), value)
    value = value + swapped(value, "dp", 1)
    value, arriving = lax.optimization_barrier((value, arriving))
    return sum(others(value, "space", (1, 2)), value), arriving


def gathered_blocks(piece, posted):
    held, weights, size = piece[None], {}, 1
    for bits in reversed(upper_groups()):
        held = jnp.concatenate([held] + others(held, "space", bits), 0)
        for n, bit in enumerate(bits):
            weights[bit] = size << n
        size = size << len(bits)
    half = piece.shape[0] // 2
    held = [held[:, :half], held[:, half:]]
    ranks = [dict(weights), dict(weights)]
    for turn in (1, 0):
        if turn == 0:
            held[0], held[1], posted = lax.optimization_barrier((*held, posted))
        for n, order in enumerate(orders()):
            held[n] = jnp.concatenate([held[n], swapped(held[n], "space", order[turn])], 0)
            ranks[n][order[turn]] = size
        size = size << 1
    return (held, [swapped(part, "dp", 1) for part in held], ranks), posted


def spread_rows(gathered, total, peers, place):
    (first, second), (first_far, second_far), ranks = gathered
    starts, counts, shared, height = pieces_of(total, peers)
    half, group = height // 2, first.shape[0]
    rows = -(-total // D)
    sizes = parts_of()
    def at(rank, relative):
        spot = 0
        for bit, weight in rank.items():
            spot = spot + jnp.where((relative & bit) != 0, weight, 0)
        return spot

    def body(place_ref, *refs):
        sources, outs, buffer = refs[:4], refs[4:-1], refs[-1]
        me = place_ref[0]
        mine = me // group
        for d in range(peers):
            relative = (me ^ d) & (group - 1)
            spots = [at(rank, relative) for rank in ranks]

            def lay(one, two, d=d, spots=spots):
                piece = jnp.concatenate([one[spots[0]], two[spots[1]]], 0).astype(jnp.float32)
                start, count = starts[d], counts[d]
                if shared[d]:
                    buffer[start : start + 1, :] = buffer[start : start + 1, :] + piece[:1]
                    buffer[start + 1 : start + count, :] = piece[1:count]
                else:
                    buffer[start : start + count, :] = piece[:count]

            @pl.when(mine == d // group)
            def _():
                lay(sources[0], sources[1])

            @pl.when(mine != d // group)
            def _():
                lay(sources[2], sources[3])

        start = 0
        for out, size in zip(outs, sizes):
            out[:size, :] = buffer[start : start + size, :].astype(out.dtype)
            if out.shape[0] > size:
                out[size:, :] = jnp.zeros((out.shape[0] - size, D), out.dtype)
            start = start + size

    kinds = [jnp.bfloat16] * (4 + ROUNDS) + [jnp.float32]
    talls = [HALF] + sizes[1:]
    return pl.pallas_call(
        body,
        grid_spec=pltpu.PrefetchScalarGridSpec(
            num_scalar_prefetch=1,
            grid=(1,),
            in_specs=[whole(first.shape)] * 4,
            out_specs=[whole((tall, D)) for tall in talls],
            scratch_shapes=[pltpu.VMEM((-(-rows // 8) * 8 + 8, D), jnp.float32)],
        ),
        out_shape=[jax.ShapeDtypeStruct((tall, D), kind) for tall, kind in zip(talls, kinds)],
        compiler_params=LIMIT,
        cost_estimate=cost(4),
        name="spread_rows",
    )(place.reshape(1), first, second, first_far, second_far)


def collect_rows(parts, total, peers, place):
    starts, counts, shared, height = pieces_of(total, peers)
    rows = -(-total // D)
    sizes = [min(part.shape[0], size) for part, size in zip(parts, tall_parts())]
    group = lax.axis_size("space")

    def body(place_ref, *refs):
        sources, keep, send, buffer = refs[:-3], refs[-3], refs[-2], refs[-1]
        start = 0
        for source, size in zip(sources, sizes):
            buffer[start : start + size, :] = source[:size, :]
            start = start + size
        if buffer.shape[0] > start:
            buffer[start:, :] = jnp.zeros((buffer.shape[0] - start, D), jnp.float32)
        me = place_ref[0]
        mine = me // group
        for d in range(peers):
            relative = (me ^ d) & (group - 1)

            @pl.when(mine == d // group)
            def _():
                keep[relative] = buffer[starts[d] : starts[d] + height, :]

            @pl.when(mine != d // group)
            def _():
                send[relative] = buffer[starts[d] : starts[d] + height, :].astype(jnp.bfloat16)

    shape = (group, height, D)
    return pl.pallas_call(
        body,
        grid_spec=pltpu.PrefetchScalarGridSpec(
            num_scalar_prefetch=1,
            grid=(1,),
            in_specs=[whole(part.shape) for part in parts],
            out_specs=[whole(shape), whole(shape)],
            scratch_shapes=[pltpu.VMEM((-(-rows // 8) * 8 + height + 8, D), jnp.float32)],
        ),
        out_shape=[
            jax.ShapeDtypeStruct(shape, jnp.float32),
            jax.ShapeDtypeStruct(shape, jnp.bfloat16),
        ],
        compiler_params=LIMIT,
        cost_estimate=cost(5),
        name="collect_rows",
    )(place.reshape(1), *parts)


def reduced_piece(keep, send, leaving):
    kept = keep + swapped(send, "dp", 1).astype(jnp.float32)
    half = kept.shape[1] // 2
    groups = upper_groups()
    inner_shape = (kept.shape[0] // 4, 2, 2, half, D)
    parts = [kept[:, :half].reshape(inner_shape), kept[:, half:].reshape(inner_shape)]
    for n, order in enumerate(orders()):
        for bit in order:
            spot = 2 if bit == 1 and parts[n].ndim == 5 else 1
            stay = lax.index_in_dim(parts[n], 0, spot, keepdims=False)
            leave = lax.index_in_dim(parts[n], 1, spot, keepdims=False)
            parts[n] = stay + swapped(leave.astype(jnp.bfloat16), "space", bit).astype(jnp.float32)
    part = jnp.concatenate(parts, 1)
    part, leaving = lax.optimization_barrier((part, leaving))
    for bits in groups:
        part = part.reshape((-1, 1 << len(bits)) + part.shape[1:])
        masks = [sum(bit for n, bit in enumerate(bits) if m >> n & 1) for m in range(1 << len(bits))]
        low = part.astype(jnp.bfloat16)
        part = sum(
            [
                swapped(low[:, m], "space", mask).astype(jnp.float32)
                for m, mask in enumerate(masks)
                if m
            ],
            part[:, 0],
        )
    return part[0], leaving


def tall_parts():
    return [CH, D, D, CH] + [D] * (5 * ROUNDS) + [2] + [1] * (1 + 2 * ROUNDS)


def weave(ref, value):
    rows = value.shape[0]
    ref[pl.ds(0, rows, stride=2), :] = value[:, :HALF]
    ref[pl.ds(1, rows, stride=2), :] = value[:, HALF:]


def unweave(ref):
    rows = ref.shape[0] // 2
    return ref[pl.ds(0, rows, stride=2), :], ref[pl.ds(1, rows, stride=2), :]


def selector():
    row = lax.broadcasted_iota(jnp.int32, (8, HALF), 0)
    lane = lax.broadcasted_iota(jnp.int32, (8, HALF), 1)
    slot = jnp.where(lane == CH, 64.0, jnp.where(lane == CH + 1, 1.0, 0.0))
    known = jnp.where(lane == CH + 2, 1.0, 0.0)
    return jnp.where(row == 0, slot, jnp.where(row == 1, known, 0.0)).astype(jnp.bfloat16)


def ids_along(arrived):
    codes = inner(selector(), arrived, 1, 1)
    return jnp.where(codes[1:2, :] > 0, codes[0:1, :], -1.0).astype(jnp.int32)


def ids_down(arrived):
    codes = inner(arrived, selector(), 1, 1)
    return jnp.where(codes[:, 1:2] > 0, codes[:, 0:1], -1.0).astype(jnp.int32)


def whole(shape):
    return pl.BlockSpec(shape, lambda *_: (0,) * len(shape))


def node_terms(mesh, mats, bias):
    blocks = mesh.shape[0]
    tile = 1024

    def body(mesh_ref, mats_ref, bias_ref, dest_ref, self_ref):
        lowered = mesh_ref[...].astype(jnp.bfloat16)
        weave(dest_ref, inner(lowered, mats_ref[1], 1, 0) + bias_ref[0:1, :])
        self_ref[...] = inner(lowered, mats_ref[3], 1, 0) + bias_ref[1:2, :]

    rows = pl.BlockSpec((tile, D), lambda i: (i, 0))
    woven = pl.BlockSpec((2 * tile, HALF), lambda i: (i, 0))
    return pl.pallas_call(
        body,
        grid=(blocks // tile,),
        in_specs=[rows, whole(mats.shape), whole(bias.shape)],
        out_specs=[woven, rows],
        out_shape=[
            jax.ShapeDtypeStruct((2 * blocks, HALF), jnp.float32),
            jax.ShapeDtypeStruct((blocks, D), jnp.float32),
        ],
        compiler_params=LIMIT,
        cost_estimate=cost(4),
        name="node_terms",
    )(mesh, mats, bias)


def round_forward(index, mesh, before, own, after, mats, terms, following, decoder=()):
    blocks = mesh.shape[0]
    tile, chunk = 512, 16
    turns, high = tile // chunk, 2 * chunk
    more = following is not None
    spans = [before.shape[0], own.shape[0], after.shape[0]]
    reach = sum(spans)

    def body(*refs):
        index_ref, mesh_ref, before_ref, own_ref, after_ref, mats_ref, dest_ref = refs[:7]
        self_ref, refs = refs[7], refs[:7] + refs[8:]
        raw, table, rows, wide, sems = refs[-5:]
        if more:
            next_ref, sent_ref = refs[7], refs[13]
            new_ref, back_ref, update_ref, agg_ref, slope_ref = refs[8:13]
        else:
            ids_ref, dec_ref, out_ref, head_ref = refs[7:11]
            new_ref, back_ref, update_ref, agg_ref, slope_ref = refs[11:16]
            branch_ref, fetched_ref, decoded_ref, turn_ref = refs[16:20]
            total_ref = refs[20]
        step = pl.program_id(0)

        @pl.when(step == 0)
        def _():
            copies = []
            start = 0
            for n, (source, span) in enumerate(zip((before_ref, own_ref, after_ref), spans)):
                copies.append(
                    pltpu.make_async_copy(source, raw.at[pl.ds(start, span)], sems.at[n])
                )
                start = start + span
            for copy in copies:
                copy.start()
            for copy in copies:
                copy.wait()

            @pl.loop(0, reach // 256)
            def _(i):
                at = pl.multiple_of(i * 256, 256)
                table[pl.ds(at, 256), :] = raw[pl.ds(at, 256), :].astype(jnp.float32)

        mesh_in = mesh_ref[...]

        def fetch(turn):
            for edge in range(K):
                base = edge * blocks + step * tile + turn * chunk
                spots = [index_ref[base + u] for u in range(chunk)]
                values = [table[pl.ds(pl.multiple_of(spot, 2), 2), :] for spot in spots]
                for u in range(chunk):
                    spot = pl.multiple_of(edge * 2 * tile + turn * high + 2 * u, 2)
                    rows[pl.ds(spot, 2), :] = values[u]

        def load(turn):
            at = pl.multiple_of(turn * high, high)
            taken = [
                rows[pl.ds(pl.multiple_of(edge * 2 * tile + turn * high, high), high), :]
                for edge in range(K)
            ]
            return at, dest_ref[pl.ds(at, high), :], taken

        def dense(at, dest, taken):
            total = None
            for edge in range(K):
                value = taken[edge] + dest
                sigma = sigmoid(value)
                out = value * sigma
                slope_ref[edge, pl.ds(at, high), :] = (sigma + out * (1.0 - sigma)).astype(
                    jnp.bfloat16
                )
                total = out if total is None else total + out
            wide[pl.ds(at, high), :] = total * (1.0 / K)

        def some(turn, carry):
            loaded = load(turn - 1)
            fetch(turn)
            dense(*loaded)
            return carry

        fetch(0)
        lax.fori_loop(1, turns, some, 0)
        dense(*load(turns - 1))
        first, second = unweave(wide)
        first, second = first.astype(jnp.bfloat16), second.astype(jnp.bfloat16)
        agg_ref[:, :HALF] = first
        agg_ref[:, HALF:] = second
        update_in = (
            inner(first, mats_ref[2, :HALF, :], 1, 0)
            + inner(second, mats_ref[2, HALF:, :], 1, 0)
            + self_ref[...]
        )
        sigma = sigmoid(update_in)
        out = update_in * sigma
        back_ref[...] = sigma + out * (1.0 - sigma)
        update = out.astype(jnp.bfloat16)
        update_ref[...] = update
        new = mesh_in + inner(update, mats_ref[4], 1, 0)
        new_ref[...] = new
        lowered = new.astype(jnp.bfloat16)
        if more:
            weave(wide, inner(lowered, next_ref[0], 1, 0))
            sent_ref[...] = wide[...].astype(jnp.bfloat16)
            return
        nodes = lax.broadcasted_iota(jnp.int32, (ids_ref.shape[0], tile), 1) + step * tile
        chooser = jnp.where(nodes == ids_ref[...], 1.0, 0.0).astype(jnp.bfloat16)
        found = inner(chooser, lowered, 1, 0)

        @pl.when(step == 0)
        def _():
            total_ref[...] = found

        @pl.when(step > 0)
        def _():
            total_ref[...] += found

        @pl.when(step == blocks // tile - 1)
        def _():
            fetched = total_ref[...].astype(jnp.bfloat16)
            fetched_ref[...] = fetched
            value = inner(fetched, dec_ref[...], 1, 0) + head_ref[2:3, :]
            sigma = sigmoid(value)
            out = value * sigma
            turn_ref[...] = sigma + out * (1.0 - sigma)
            decoded = out.astype(jnp.bfloat16)
            decoded_ref[...] = decoded
            branch_ref[...] = inner(decoded, out_ref[...], 1, 0).astype(jnp.bfloat16)

    whole_rows = pl.BlockSpec((tile, D), lambda i, *_: (i, 0))
    woven = pl.BlockSpec((2 * tile, HALF), lambda i, *_: (i, 0))
    ins = [whole_rows] + [pl.BlockSpec(memory_space=pltpu.HBM)] * 3
    ins = ins + [whole(mats.shape), woven, whole_rows]
    outs = [whole_rows] * 4 + [pl.BlockSpec((K, 2 * tile, HALF), lambda i, *_: (0, i, 0))]
    shapes = [
        jax.ShapeDtypeStruct((blocks, D), jnp.float32),
        jax.ShapeDtypeStruct((blocks, D), jnp.float32),
        jax.ShapeDtypeStruct((blocks, D), jnp.bfloat16),
        jax.ShapeDtypeStruct((blocks, D), jnp.bfloat16),
        jax.ShapeDtypeStruct((K, 2 * blocks, HALF), jnp.bfloat16),
    ]
    args = [index, mesh, before, own, after, mats, *terms]
    if more:
        ins.append(pl.BlockSpec((1, D, D), lambda *_: (0, 0, 0)))
        outs.append(woven)
        shapes.append(jax.ShapeDtypeStruct((2 * blocks, HALF), jnp.bfloat16))
        args.append(following)
    scratch = []
    if decoder:
        posts = decoder[0].shape[0]
        ins = ins + [whole(arg.shape) for arg in decoder]
        args = args + list(decoder)
        for width, kind in ((HALF, jnp.bfloat16), (D, jnp.bfloat16), (D, jnp.bfloat16), (D, jnp.float32)):
            outs.append(whole((posts, width)))
            shapes.append(jax.ShapeDtypeStruct((posts, width), kind))
        scratch = [pltpu.VMEM((posts, D), jnp.float32)]
    return pl.pallas_call(
        body,
        grid_spec=pltpu.PrefetchScalarGridSpec(
            num_scalar_prefetch=1,
            grid=(blocks // tile,),
            in_specs=ins,
            out_specs=outs,
            scratch_shapes=scratch
            + [
                pltpu.VMEM((reach, HALF), jnp.bfloat16),
                pltpu.VMEM((reach, HALF), jnp.float32),
                pltpu.VMEM((K * 2 * tile, HALF), jnp.float32),
                pltpu.VMEM((2 * tile, HALF), jnp.float32),
                pltpu.SemaphoreType.DMA((3,)),
            ],
        ),
        out_shape=shapes,
        compiler_params=LIMIT,
        cost_estimate=cost(25),
        name="round_forward",
    )(*args)


def edges_backward(index, back, slopes, mats, carried=(), landed=()):
    blocks = back.shape[0]
    tile, chunk = 512, 16
    steps, turns, high = blocks // tile, tile // chunk, 2 * chunk
    reach = 2 * (blocks + 2 * H)

    def body(*refs):
        if carried:
            index_ref, back_ref, slope_ref, mats_ref = refs[:4]
            past, rest = refs[4:9], refs[9:]
            (new_ref, out_ref, sent_ref), rest = rest[:3], rest[3:]
        else:
            index_ref, back_ref, slope_ref, mats_ref = refs[:4]
            (ids_ref, landed_ref, turn_ref, w_out_ref, w_dec_ref), rest = refs[4:9], refs[9:]
            (new_ref, out_ref, gdec_ref), rest = rest[:3], rest[3:]
            gathered, rest = rest[5], rest[:5] + rest[6:]
        guin_ref, low_ref, before_ref, own_ref, after_ref, wide, wider, flows, *tables = rest
        step = pl.program_id(0)

        @pl.when(step == 0)
        def _():
            @pl.loop(0, reach // 256)
            def _(i):
                for table in tables:
                    table[pl.ds(pl.multiple_of(i * 256, 256), 256), :] = jnp.zeros(
                        (256, HALF), jnp.float32
                    )

        if carried:
            new, one, two = ended(*past, wide)
            sent_ref[:, :HALF] = one
            sent_ref[:, HALF:] = two
            new_ref[...] = new
            grad_out = new.astype(jnp.bfloat16)
            out_ref[...] = grad_out
        else:

            @pl.when(step == 0)
            def _():
                grad_dec = inner(landed_ref[...], w_out_ref[...], 1, 1) * turn_ref[...]
                grad_dec = grad_dec.astype(jnp.bfloat16)
                gdec_ref[...] = grad_dec
                gathered[...] = inner(grad_dec, w_dec_ref[...], 1, 1).astype(jnp.bfloat16)

            nodes = lax.broadcasted_iota(jnp.int32, (tile, landed_ref.shape[0]), 0) + step * tile
            chooser = jnp.where(nodes == ids_ref[...], 1.0, 0.0).astype(jnp.bfloat16)
            new = inner(chooser, gathered[...], 1, 0)
            new_ref[...] = new
            grad_out = new.astype(jnp.bfloat16)
            out_ref[...] = grad_out
        grad_uin = (inner(grad_out, mats_ref[4], 1, 1) * back_ref[...]).astype(jnp.bfloat16)
        guin_ref[...] = grad_uin
        weave(wide, inner(grad_uin, mats_ref[2], 1, 1) * (1.0 / K))

        def dense(turn):
            at = pl.multiple_of(turn * high, high)
            grad_agg = wide[pl.ds(at, high), :]
            total, parts = None, []
            for edge in range(K):
                flow = grad_agg * slope_ref[edge, pl.ds(at, high), :].astype(jnp.float32)
                parts.append(flow)
                total = flow if total is None else total + flow
            return at, total, parts

        def keep(turn, at, total, parts):
            for edge in range(K):
                spot = pl.multiple_of(edge * 2 * tile + turn * high, high)
                flows[pl.ds(spot, high), :] = parts[edge]
            wider[pl.ds(at, high), :] = total

        def scatter(turn):
            for u in range(chunk):
                spots, sums = [], []
                for edge in range(K):
                    base = edge * blocks + step * tile + turn * chunk
                    spots.append(pl.multiple_of(index_ref[base + u], 2))
                for edge in range(K):
                    spot = pl.multiple_of(edge * 2 * tile + turn * high + 2 * u, 2)
                    sums.append(tables[edge][pl.ds(spots[edge], 2), :] + flows[pl.ds(spot, 2), :])
                for edge in range(K):
                    tables[edge][pl.ds(spots[edge], 2), :] = sums[edge]

        def some(turn, carry):
            found = dense(turn)
            scatter(turn - 1)
            keep(turn, *found)
            return carry

        keep(0, *dense(0))
        lax.fori_loop(1, turns, some, 0)
        scatter(turns - 1)
        first, second = unweave(wider)
        low_ref[:, :HALF] = first.astype(jnp.bfloat16)
        low_ref[:, HALF:] = second.astype(jnp.bfloat16)

        @pl.when(step == steps - 1)
        def _():
            def summed(at):
                value = tables[0][pl.ds(at, 256), :]
                for table in tables[1:]:
                    value = value + table[pl.ds(at, 256), :]
                return value

            @pl.loop(0, 2 * H // 256)
            def _(i):
                at = pl.multiple_of(i * 256, 256)
                far = pl.multiple_of(2 * H + 2 * blocks + at, 256)
                before_ref[pl.ds(at, 256), :] = summed(at).astype(jnp.bfloat16)
                after_ref[pl.ds(at, 256), :] = summed(far).astype(jnp.bfloat16)

            @pl.loop(0, 2 * blocks // 256)
            def _(i):
                at = pl.multiple_of(i * 256, 256)
                own_ref[pl.ds(at, 256), :] = summed(pl.multiple_of(2 * H + at, 256))

    rows = pl.BlockSpec((tile, D), lambda i, *_: (i, 0))
    woven = pl.BlockSpec((2 * tile, HALF), lambda i, *_: (i, 0))
    low = jax.ShapeDtypeStruct((blocks, D), jnp.bfloat16)
    low_posts = (landed[1].shape[0], D) if landed else None
    last = low if carried else jax.ShapeDtypeStruct(low_posts, jnp.bfloat16)
    return pl.pallas_call(
        body,
        grid_spec=pltpu.PrefetchScalarGridSpec(
            num_scalar_prefetch=1,
            grid=(steps,),
            in_specs=[
                rows,
                pl.BlockSpec((K, 2 * tile, HALF), lambda i, *_: (0, i, 0)),
                whole(mats.shape),
            ]
            + ([rows] + [woven] * 3 + [whole(mats.shape)] if carried else [])
            + [whole(arg.shape) for arg in landed],
            out_specs=([rows] * 3 if carried else [rows, rows, whole(low_posts)])
            + [
                rows, rows,
                whole((2 * H, HALF)), whole((2 * blocks, HALF)), whole((2 * H, HALF)),
            ],
            scratch_shapes=([] if carried else [pltpu.VMEM(low_posts, jnp.bfloat16)])
            + [
                pltpu.VMEM((2 * tile, HALF), jnp.float32),
                pltpu.VMEM((2 * tile, HALF), jnp.float32),
                pltpu.VMEM((2 * tile * K, HALF), jnp.float32),
            ]
            + [pltpu.VMEM((reach, HALF), jnp.float32)] * K,
        ),
        out_shape=[
            jax.ShapeDtypeStruct((blocks, D), jnp.float32),
            low,
            last,
            low,
            low,
            jax.ShapeDtypeStruct((2 * H, HALF), jnp.bfloat16),
            jax.ShapeDtypeStruct((2 * blocks, HALF), jnp.float32),
            jax.ShapeDtypeStruct((2 * H, HALF), jnp.bfloat16),
        ],
        compiler_params=LIMIT,
        cost_estimate=cost(28 if carried else 25),
        name="edges_backward",
    )(index, back, slopes, mats, *carried, *landed)


def ended(part_ref, own_ref, first_ref, last_ref, mats_ref, wide):
    wide[...] = (
        own_ref[...] + first_ref[...].astype(jnp.float32) + last_ref[...].astype(jnp.float32)
    )
    one, two = unweave(wide)
    one, two = one.astype(jnp.bfloat16), two.astype(jnp.bfloat16)
    new = (
        part_ref[...]
        + inner(one, mats_ref[0, :, :HALF], 1, 1)
        + inner(two, mats_ref[0, :, HALF:], 1, 1)
    )
    return new, one, two


def carried_terms(grad_mesh, grad_uin, dest_low, mats):
    blocks = grad_mesh.shape[0]
    tile = 1024

    def body(grad_ref, guin_ref, dest_ref, mats_ref, part_ref):
        part_ref[...] = (
            grad_ref[...]
            + inner(guin_ref[...], mats_ref[3], 1, 1)
            + inner(dest_ref[...], mats_ref[1], 1, 1)
        )

    rows = pl.BlockSpec((tile, D), lambda i: (i, 0))
    return pl.pallas_call(
        body,
        grid=(blocks // tile,),
        in_specs=[rows, rows, rows, whole(mats.shape)],
        out_specs=rows,
        out_shape=jax.ShapeDtypeStruct((blocks, D), jnp.float32),
        compiler_params=LIMIT,
        cost_estimate=cost(4),
        name="carried_terms",
    )(grad_mesh, grad_uin, dest_low, mats)


def encode_rows(arrived, w_in, w_node, biases, source):
    posts = arrived.shape[0]
    tile = 512

    def body(
        arrived_ref, in_ref, node_ref, bias_ref, source_ref,
        mesh_ref, gathered_ref, sent_ref, ids_ref, down_ref, encoded, wide,
    ):
        step = pl.program_id(0)

        @pl.when(step == 0)
        def _():
            entering = inner(arrived_ref[...], in_ref[...], 1, 0) + bias_ref[0:1, :]
            encoded[...] = silu(entering).astype(jnp.bfloat16)
            ids_ref[...] = ids_along(arrived_ref[...])
            down_ref[...] = ids_down(arrived_ref[...])

        nodes = lax.broadcasted_iota(jnp.int32, (tile, posts), 0) + step * tile
        chooser = jnp.where(nodes == ids_ref[...], 1.0, 0.0).astype(jnp.bfloat16)
        gathered = inner(chooser, encoded[...], 1, 0).astype(jnp.bfloat16)
        gathered_ref[...] = gathered
        mesh = silu(inner(gathered, node_ref[...], 1, 0) + bias_ref[1:2, :])
        mesh_ref[...] = mesh
        weave(wide, inner(mesh.astype(jnp.bfloat16), source_ref[0], 1, 0))
        sent_ref[...] = wide[...].astype(jnp.bfloat16)

    rows = pl.BlockSpec((tile, D), lambda i: (i, 0))
    args = (arrived, w_in, w_node, biases, source)
    return pl.pallas_call(
        body,
        grid=(H // tile,),
        in_specs=[whole(arg.shape) for arg in args[:-1]]
        + [pl.BlockSpec((1, D, D), lambda *_: (0, 0, 0))],
        out_specs=[rows, rows, pl.BlockSpec((2 * tile, HALF), lambda i: (i, 0))]
        + [whole((1, posts)), whole((posts, 1))],
        out_shape=[
            jax.ShapeDtypeStruct((H, D), jnp.float32),
            jax.ShapeDtypeStruct((H, D), jnp.bfloat16),
            jax.ShapeDtypeStruct((2 * H, HALF), jnp.bfloat16),
            jax.ShapeDtypeStruct((1, posts), jnp.int32),
            jax.ShapeDtypeStruct((posts, 1), jnp.int32),
        ],
        scratch_shapes=[pltpu.VMEM((posts, D), jnp.bfloat16), pltpu.VMEM((2 * tile, HALF), jnp.float32)],
        compiler_params=LIMIT,
        cost_estimate=cost(5),
        name="encode_rows",
    )(*args)


def encode_backward(carried, mesh, gathered, arrived, ids, w_in, w_node, biases):
    blocks = mesh.shape[0]
    posts = arrived.shape[0]
    tile = 512
    steps = blocks // tile

    def body(
        part_ref, own_ref, first_ref, last_ref, mats_ref,
        mesh_ref, gathered_ref, arrived_ref, ids_ref, in_ref, node_ref, bias_ref,
        new_ref, out_ref, gin_ref, gnode_ref, gbias_ref, gsource_ref, total, wide,
    ):
        step = pl.program_id(0)

        @pl.when(step == 0)
        def _():
            for ref in (total, gnode_ref, gbias_ref, gsource_ref):
                ref[...] = jnp.zeros(ref.shape, jnp.float32)

        new, one, two = ended(part_ref, own_ref, first_ref, last_ref, mats_ref, wide)
        new_ref[...] = new
        out_ref[...] = new.astype(jnp.bfloat16)
        lowered = mesh_ref[...].astype(jnp.bfloat16)
        gsource_ref[:, :HALF] += inner(lowered, one, 0, 0)
        gsource_ref[:, HALF:] += inner(lowered, two, 0, 0)
        node_in = inner(gathered_ref[...], node_ref[...], 1, 0) + bias_ref[1:2, :]
        grad_node = (new * slope(node_in)).astype(jnp.bfloat16)
        gbias_ref[1:2, :] += jnp.sum(grad_node.astype(jnp.float32), 0, keepdims=True)
        gnode_ref[...] += inner(gathered_ref[...], grad_node, 0, 0)
        back = inner(grad_node, node_ref[...], 1, 1).astype(jnp.bfloat16)
        nodes = lax.broadcasted_iota(jnp.int32, (posts, tile), 1) + step * tile
        chooser = jnp.where(nodes == ids_ref[...], 1.0, 0.0).astype(jnp.bfloat16)
        total[...] += inner(chooser, back, 1, 0)

        @pl.when(step == steps - 1)
        def _():
            entering = inner(arrived_ref[...], in_ref[...], 1, 0) + bias_ref[0:1, :]
            grad_enc = (total[...] * slope(entering)).astype(jnp.bfloat16)
            gbias_ref[0:1, :] = jnp.sum(grad_enc.astype(jnp.float32), 0, keepdims=True)
            gin_ref[...] = inner(arrived_ref[...], grad_enc, 0, 0)

    rows = pl.BlockSpec((tile, D), lambda i: (i, 0))
    woven = pl.BlockSpec((2 * tile, HALF), lambda i: (i, 0))
    args = (arrived, ids, w_in, w_node, biases)
    shapes = [(HALF, D), (D, D), (2, D), (D, D)]
    return pl.pallas_call(
        body,
        grid=(steps,),
        in_specs=[rows] + [woven] * 3 + [whole(carried[4].shape), rows, rows]
        + [whole(arg.shape) for arg in args],
        out_specs=[rows, rows] + [whole(shape) for shape in shapes],
        out_shape=[
            jax.ShapeDtypeStruct((blocks, D), jnp.float32),
            jax.ShapeDtypeStruct((blocks, D), jnp.bfloat16),
        ]
        + [jax.ShapeDtypeStruct(shape, jnp.float32) for shape in shapes],
        scratch_shapes=[pltpu.VMEM((posts, D), jnp.float32), pltpu.VMEM((2 * tile, HALF), jnp.float32)],
        compiler_params=LIMIT,
        cost_estimate=cost(10),
        name="encode_backward",
    )(*carried, mesh, gathered, *args)


def shards(walk, master, moment1, moment2, inputs, targets, valid, owner, slot, neighbours, partner):
    bands = lax.axis_size("space")
    band = lax.axis_index("space")
    peers = lax.axis_size(ALL)
    place = lax.axis_index(ALL)
    shard = master.shape[0]
    total_size = shard * peers
    height = pieces_of(total_size, peers)[3]
    offset = lax.rem(lax.rem(shard, D) * place, D)
    piece = lax.dynamic_update_slice_in_dim(
        jnp.zeros((height * D,), jnp.bfloat16), master.astype(jnp.bfloat16), offset, 0
    )
    state_in = inputs[0]
    counted = valid[0].astype(jnp.float32)
    local_count = jnp.sum(valid[0])
    digits = (local_count >> jnp.array([16, 8, 0], jnp.int32)) & 255
    digits = jnp.pad(digits, (CH + 3, HALF - CH - 6)).astype(jnp.float32)[None, :]
    points = state_in.shape[1]
    blocks = neighbours.shape[0]
    assert blocks == H
    capacity = max(2, 2 * points // bands)
    target_band = owner[0, :, 0]
    hits = (target_band[:, None] == jnp.arange(bands, dtype=jnp.int32)[None, :]).astype(jnp.int32)
    ranks = jnp.sum(jnp.cumsum(hits, 0) * hits, 1) - 1
    places_out = jnp.sum(hits * jnp.asarray(walk, jnp.int32)[None, :], 1) * capacity + ranks
    poster = (
        jnp.arange(bands * capacity, dtype=jnp.int32)[:, None] == places_out[None, :]
    ).astype(jnp.bfloat16)
    spots = slot[0][None, :]
    columns = jnp.concatenate(
        [
            state_in,
            (spots // 64).astype(jnp.bfloat16),
            (spots % 64).astype(jnp.bfloat16),
            jnp.ones((1, points), jnp.bfloat16),
            jnp.zeros((HALF - CH - 3, points), jnp.bfloat16),
        ],
        0,
    )

    def exchanged(rows):
        return lax.all_to_all(
            rows.reshape(bands, capacity, HALF), "space", split_axis=0, concat_axis=0, tiled=True
        ).reshape(bands * capacity, HALF)

    held, posted = gathered_blocks(
        piece.reshape(height, D), (inner(poster, columns, 1, 1) + digits).astype(jnp.bfloat16)
    )
    arrived = exchanged(posted)
    w_in, w_node, w_dec, w_out, *w_round, biases = spread_rows(
        held, total_size, peers, place
    )
    arrived, biases = lax.optimization_barrier((arrived, biases))
    counts = arrived.reshape(bands, capacity, HALF)[:, 0, CH + 3 : CH + 6].astype(jnp.float32)
    counts = jnp.sum(counts, 0, keepdims=True)
    w_out = jnp.pad(w_out.reshape(D, CH), ((0, 0), (0, HALF - CH)))
    w_round = [mats.reshape(5, D, D) for mats in w_round]
    b_head = biases[:3]
    b_round = biases[3:].reshape(ROUNDS, 2, D)
    mesh, gathered, sent, ids_row, ids = encode_rows(
        arrived, w_in, w_node, biases, w_round[0]
    )
    sent, partner, neighbours, counted, counts = lax.optimization_barrier(
        (sent, partner, neighbours, counted, counts)
    )
    counts = counts + swapped(counts, "dp", 1)
    index = 2 * ((neighbours - band * blocks + H) % (blocks * bands)).T.reshape(-1)
    moved = [(n, place) for n, place in enumerate(walk) if n != place]
    stays = jnp.asarray([n == place for n, place in enumerate(walk)])[band]
    index = lax.ppermute(index, "space", list(enumerate(walk)))

    def at_home(rows):
        return lax.ppermute(rows, "space", [(j, i) for i, j in moved])

    def settled(own, came):
        return jnp.where(stays, own, came.astype(jnp.float32))

    partner_by = partner - band * points - jnp.arange(points, dtype=jnp.int32)
    coded = jnp.where(partner_by >= NEAR, partner_by - NEAR + 1, 0).astype(jnp.bfloat16)
    low_valid = jnp.concatenate([counted.astype(jnp.bfloat16), coded[None, :]], 0)
    valid_around = jnp.concatenate(
        [
            shifted(low_valid[:, points - ROWW :], "space", 1),
            low_valid,
            shifted(low_valid[:, :ROWW], "space", -1),
        ],
        1,
    )
    kept = []
    for layer in range(ROUNDS):
        before, after = halo(walk, sent, sent)
        terms = node_terms(mesh, w_round[layer], b_round[layer])
        if layer == 0:
            before, valid_around, counts = lax.optimization_barrier((before, valid_around, counts))
        following = w_round[layer + 1] if layer + 1 < ROUNDS else None
        new, back, update, agg, slopes, *rest = round_forward(
            index, mesh, before, sent, after, w_round[layer], terms, following,
            () if following is not None else (ids, w_dec, w_out, biases),
        )
        kept.append((mesh, back, update, agg, slopes))
        mesh = new
        sent = rest[0]
    count = counts[0, 0] * 65536.0 + counts[0, 1] * 256.0 + counts[0, 2]
    wide_valid = valid_around[:CH].astype(jnp.float32)
    coded = valid_around[CH : CH + 1, : points + ROWW].astype(jnp.float32)
    weights = [
        (
            by,
            jnp.where(coded == by - NEAR + 1, 1.0, 0.0)
            * wide_valid[:, : points + ROWW]
            * wide_valid[:, by : by + points + ROWW],
        )
        for by in range(NEAR, ROWW + 1)
    ]
    branch_rows, fetched, decoded, dec_turn = rest
    returned = exchanged(branch_rows)
    branch = inner(returned, poster, 0, 0)[:CH]
    err = state_in.astype(jnp.float32) + branch - targets[0].astype(jnp.float32)
    def widened(values):
        low = values.astype(jnp.bfloat16)
        before = shifted(low[:, points - ROWW :], "space", 1).astype(jnp.float32)
        after = shifted(low[:, :ROWW], "space", -1).astype(jnp.float32)
        return jnp.concatenate([before, values, after], 1)

    wide_err = widened(err)
    paired = jnp.zeros((CH, points + ROWW), jnp.float32)
    pair_total = jnp.zeros((CH, points), jnp.float32)
    for by, both in weights:
        gap = both * (wide_err[:, : points + ROWW] - wide_err[:, by : by + points + ROWW])
        paired = paired + gap
        pair_total = pair_total + gap[:, ROWW:] * (
            wide_err[:, ROWW : ROWW + points] - wide_err[:, ROWW + by : ROWW + by + points]
        )
    local_total = jnp.sum(counted * err * err) + 0.5 * jnp.sum(pair_total)
    grad_pred = 2.0 * counted * err + paired[:, ROWW:]
    for by, both in weights:
        gap = both * (wide_err[:, : points + ROWW] - wide_err[:, by : by + points + ROWW])
        grad_pred = grad_pred - gap[:, ROWW - by : ROWW - by + points]
    grad_pred = grad_pred / count
    grad_rows = jnp.pad(grad_pred.astype(jnp.bfloat16), ((0, HALF - CH), (0, 0)))
    landed = exchanged(inner(poster, grad_rows, 1, 1).astype(jnp.bfloat16))
    landed, final_mesh = lax.optimization_barrier((landed, mesh.astype(jnp.bfloat16)))
    final_mesh = at_home(final_mesh)
    mats_grads = [None] * (5 * ROUNDS)
    bias_grads = [None] * (2 * ROUNDS)
    carried, grad_mesh = (), None
    for layer in reversed(range(ROUNDS)):
        old, back, update, agg, slopes = kept[layer]
        first_step = not carried
        grad_mesh, leaving, extra, grad_uin, dest_low, to_before, own, to_after = edges_backward(
            index, back, slopes, w_round[layer], carried,
            (ids_row, landed, dec_turn, w_out, w_dec) if first_step else (),
        )
        if not first_step:
            mats_grads[5 * layer + 5] = inner(
                kept[layer + 1][0].astype(jnp.bfloat16), extra, 0, 0
            )
        else:
            grad_wout = inner(decoded, landed, 0, 0)[:, :CH]
            grad_bdec = jnp.sum(extra.astype(jnp.float32), 0, keepdims=True)
            grad_wdec = inner(fetched, extra, 0, 0)
            to_before, to_after, final_mesh = lax.optimization_barrier(
                (to_before, to_after, final_mesh)
            )
        from_before, from_after = halo(walk, to_after, to_before)
        if first_step:
            from_before, final_mesh = lax.optimization_barrier(
                (from_before, settled(mesh, final_mesh))
            )
        lowered = old.astype(jnp.bfloat16)
        mats_grads[5 * layer + 1 : 5 * layer + 5] = [
            inner(lowered, dest_low, 0, 0),
            inner(agg, grad_uin, 0, 0),
            inner(lowered, grad_uin, 0, 0),
            inner(update, leaving, 0, 0),
        ]
        bias_grads[2 * layer] = jnp.sum(dest_low.astype(jnp.float32), 0, keepdims=True)
        bias_grads[2 * layer + 1] = jnp.sum(grad_uin.astype(jnp.float32), 0, keepdims=True)
        part = carried_terms(grad_mesh, grad_uin, dest_low, w_round[layer])
        carried = (part, own, from_before, from_after, w_round[layer])
    grad_mesh, leaving, grad_win, grad_wnode, grad_bpair, mats_grads[0] = encode_backward(
        carried, kept[0][0], gathered, arrived, ids, w_in, w_node, biases
    )
    parts = [grad_win, grad_wnode, grad_wdec, grad_wout.reshape(CH, D)]
    parts = parts + mats_grads
    parts = parts + [grad_bpair, grad_bdec] + bias_grads
    keep, send = collect_rows(parts, total_size, peers, place)
    mine, leaving = reduced_piece(keep, send, leaving)
    late = at_home(leaving)
    mine = lax.dynamic_slice_in_dim(mine.reshape(-1), offset, shard)
    lane = lax.broadcasted_iota(jnp.int32, (8, HALF), 1)
    sums, late = summed_everywhere(
        jnp.where(lane == 0, local_total, jnp.sum(mine * mine)), late
    )
    total, norm = sums[0, 0], jnp.sqrt(sums[0, 1])
    node_grads = settled(grad_mesh, late)
    clipped = mine * jnp.minimum(1.0, 0.05 / norm)
    first = 0.9 * moment1 + 0.1 * clipped
    second = 0.999 * moment2 + 0.001 * clipped * clipped
    first_hat = first / (1.0 - 0.9**STEP)
    second_hat = second / (1.0 - 0.999**STEP)
    updated = master - 0.1 * (first_hat / (jnp.sqrt(second_hat) + 1e-08) + 0.1 * master)
    return (
        total.reshape(1),
        count.reshape(1),
        norm.reshape(1),
        updated,
        first,
        second,
        updated.astype(jnp.bfloat16),
        final_mesh.reshape(1, blocks, D),
        node_grads.reshape(1, blocks, D),
        grad_pred.reshape(1, grad_pred.shape[0], points),
    )


def solution(mesh):
    return jax.shard_map(
        functools.partial(shards, walk_of(mesh)),
        mesh=mesh,
        in_specs=(
            P(("dp", "space")),
            P(("dp", "space")),
            P(("dp", "space")),
            P("dp", None, "space"),
            P("dp", None, "space"),
            P("dp", None, "space"),
            P("dp", "space", None),
            P("dp", "space"),
            P("space", None),
            P("space"),
        ),
        out_specs=(
            P(),
            P(),
            P(),
            P(("dp", "space")),
            P(("dp", "space")),
            P(("dp", "space")),
            P(("dp", "space")),
            P("dp", "space", None),
            P("dp", "space", None),
            P("dp", None, "space"),
        ),
        check_vma=False,
    )
```

```python
import functools

import jax
import jax.numpy as jnp
from jax import lax
from jax.experimental import pallas as pl
from jax.experimental.pallas import tpu as pltpu
from jax.sharding import PartitionSpec as P

D = 256
HALF = 128
CH = 78
ROUNDS = 3
K = 6
ROWW = 360
NEAR = 358
STEP = 10
H = 2048
ALL = ("dp", "space")
LIMIT = pltpu.CompilerParams(vmem_limit_bytes=60 * 2**20)


def cost(micros):
    return pl.CostEstimate(flops=0, bytes_accessed=micros * 3_000_000, transcendentals=0)


def inner(left, right, left_dim, right_dim):
    return lax.dot_general(
        left, right, (((left_dim,), (right_dim,)), ((), ())), preferred_element_type=jnp.float32
    )


def sigmoid(value):
    return 0.5 * jnp.tanh(0.5 * value) + 0.5


def silu(value):
    return value * sigmoid(value)


def slope(value):
    sigma = sigmoid(value)
    return sigma * (1.0 + value * (1.0 - sigma))


def shifted(shard, axis, by):
    peers = lax.axis_size(axis)
    pairs = [(i, i + by) for i in range(peers) if 0 <= i + by < peers]
    return lax.ppermute(shard, axis, pairs)


def walk_of(mesh):
    count = mesh.shape["space"]
    chips = [getattr(device, "coords", None) for device in mesh.devices[0].reshape(-1)]
    if any(chip is None for chip in chips) or len(set(map(tuple, chips))) != count:
        return list(range(count))
    at = {tuple(chip): n for n, chip in enumerate(chips)}
    xs, ys, zs = (sorted({chip[n] for chip in at}) for n in range(3))
    if len(xs) * len(ys) * len(zs) != count:
        return list(range(count))
    if (len(xs), len(ys), len(zs)) == (2, 2, 4):
        corners = [(0, 0), (1, 0), (0, 1), (1, 1)]
        planes = [(0, 1, 3, 2), (2, 0, 1, 3), (3, 1, 0, 2), (2, 3, 1, 0)]
        steps = [(*corners[n], z) for z, plane in enumerate(planes) for n in plane]
        return [at[(xs[x], ys[y], zs[z])] for x, y, z in steps]
    walk, plane = [], []
    for n, y in enumerate(ys):
        plane = plane + [(x, y) for x in (xs if n % 2 == 0 else xs[::-1])]
    for n, z in enumerate(zs):
        walk = walk + [at[(x, y, z)] for x, y in (plane if n % 2 == 0 else plane[::-1])]
    return walk


def halo(walk, last, initial):
    up = list(zip(walk, walk[1:] + walk[:1]))
    down = [(j, i) for i, j in up]
    return lax.ppermute(last, "space", up), lax.ppermute(initial, "space", down)


def pieces_of(total, peers):
    share = total // peers
    starts = [share * d // D for d in range(peers)]
    counts = [-(-share * (d + 1) // D) - starts[d] for d in range(peers)]
    shared = [share * d % D != 0 for d in range(peers)]
    height = -(-max(counts) // 16) * 16
    return starts, counts, shared, height


def parts_of():
    return [CH, D, D, CH] + [5 * D] * ROUNDS + [3 + 2 * ROUNDS]


def swapped(value, axis, bit):
    return lax.ppermute(value, axis, [(i, i ^ bit) for i in range(lax.axis_size(axis))])


def bits_of(axis):
    return [1 << n for n in range(lax.axis_size(axis).bit_length() - 1)]


def others(value, axis, bits):
    masks = [sum(bit for n, bit in enumerate(bits) if m >> n & 1) for m in range(1, 1 << len(bits))]
    return [swapped(value, axis, mask) for mask in masks]


def upper_groups():
    bits = bits_of("space")[2:]
    return [tuple(bits[n : n + 2]) for n in range(0, len(bits), 2)]


def orders():
    return [(1, 2), (2, 1)]


def summed_everywhere(value, arriving):
    for bits in reversed(upper_groups()):
        value = sum(others(value, "space", bits), value)
    value = value + swapped(value, "dp", 1)
    value, arriving = lax.optimization_barrier((value, arriving))
    return sum(others(value, "space", (1, 2)), value), arriving


def gathered_blocks(piece, sources, posting):
    held, weights, size = piece[None], {}, 1
    for bits in reversed(upper_groups()):
        held = jnp.concatenate([held] + others(held, "space", bits), 0)
        for n, bit in enumerate(bits):
            weights[bit] = size << n
        size = size << len(bits)
    held, sources = lax.optimization_barrier((held, sources))
    poster, posted = posting(*sources)
    half = piece.shape[0] // 2
    held = [held[:, :half], held[:, half:]]
    ranks = [dict(weights), dict(weights)]
    for turn in (1, 0):
        if turn == 0:
            held[0], held[1], posted = lax.optimization_barrier((*held, posted))
        for n, order in enumerate(orders()):
            held[n] = jnp.concatenate([held[n], swapped(held[n], "space", order[turn])], 0)
            ranks[n][order[turn]] = size
        size = size << 1
    return (held, [swapped(part, "dp", 1) for part in held], ranks), poster, posted


def spread_rows(gathered, total, peers, place):
    (first, second), (first_far, second_far), ranks = gathered
    starts, counts, shared, height = pieces_of(total, peers)
    half, group = height // 2, first.shape[0]
    rows = -(-total // D)
    sizes = parts_of()
    def at(rank, relative):
        spot = 0
        for bit, weight in rank.items():
            spot = spot + jnp.where((relative & bit) != 0, weight, 0)
        return spot

    def body(place_ref, *refs):
        sources, outs, buffer = refs[:4], refs[4:-1], refs[-1]
        me = place_ref[0]
        mine = me // group
        for d in range(peers):
            relative = (me ^ d) & (group - 1)
            spots = [at(rank, relative) for rank in ranks]

            def lay(one, two, d=d, spots=spots):
                piece = jnp.concatenate([one[spots[0]], two[spots[1]]], 0).astype(jnp.float32)
                start, count = starts[d], counts[d]
                if shared[d]:
                    buffer[start : start + 1, :] = buffer[start : start + 1, :] + piece[:1]
                    buffer[start + 1 : start + count, :] = piece[1:count]
                else:
                    buffer[start : start + count, :] = piece[:count]

            @pl.when(mine == d // group)
            def _():
                lay(sources[0], sources[1])

            @pl.when(mine != d // group)
            def _():
                lay(sources[2], sources[3])

        start = 0
        for out, size in zip(outs, sizes):
            out[:size, :] = buffer[start : start + size, :].astype(out.dtype)
            if out.shape[0] > size:
                out[size:, :] = jnp.zeros((out.shape[0] - size, D), out.dtype)
            start = start + size

    kinds = [jnp.bfloat16] * (4 + ROUNDS) + [jnp.float32]
    talls = [HALF] + sizes[1:]
    return pl.pallas_call(
        body,
        grid_spec=pltpu.PrefetchScalarGridSpec(
            num_scalar_prefetch=1,
            grid=(1,),
            in_specs=[whole(first.shape)] * 4,
            out_specs=[whole((tall, D)) for tall in talls],
            scratch_shapes=[pltpu.VMEM((-(-rows // 8) * 8 + 8, D), jnp.float32)],
        ),
        out_shape=[jax.ShapeDtypeStruct((tall, D), kind) for tall, kind in zip(talls, kinds)],
        compiler_params=LIMIT,
        cost_estimate=cost(4),
        name="spread_rows",
    )(place.reshape(1), first, second, first_far, second_far)


def collect_rows(parts, total, peers, place):
    starts, counts, shared, height = pieces_of(total, peers)
    rows = -(-total // D)
    sizes = [min(part.shape[0], size) for part, size in zip(parts, tall_parts())]
    group = lax.axis_size("space")

    def body(place_ref, *refs):
        sources, keep, send, buffer = refs[:-3], refs[-3], refs[-2], refs[-1]
        start = 0
        for source, size in zip(sources, sizes):
            buffer[start : start + size, :] = source[:size, :]
            start = start + size
        if buffer.shape[0] > start:
            buffer[start:, :] = jnp.zeros((buffer.shape[0] - start, D), jnp.float32)
        me = place_ref[0]
        mine = me // group
        for d in range(peers):
            relative = (me ^ d) & (group - 1)

            @pl.when(mine == d // group)
            def _():
                keep[relative] = buffer[starts[d] : starts[d] + height, :]

            @pl.when(mine != d // group)
            def _():
                send[relative] = buffer[starts[d] : starts[d] + height, :].astype(jnp.bfloat16)

    shape = (group, height, D)
    return pl.pallas_call(
        body,
        grid_spec=pltpu.PrefetchScalarGridSpec(
            num_scalar_prefetch=1,
            grid=(1,),
            in_specs=[whole(part.shape) for part in parts],
            out_specs=[whole(shape), whole(shape)],
            scratch_shapes=[pltpu.VMEM((-(-rows // 8) * 8 + height + 8, D), jnp.float32)],
        ),
        out_shape=[
            jax.ShapeDtypeStruct(shape, jnp.float32),
            jax.ShapeDtypeStruct(shape, jnp.bfloat16),
        ],
        compiler_params=LIMIT,
        cost_estimate=cost(5),
        name="collect_rows",
    )(place.reshape(1), *parts)


def reduced_piece(keep, send, leaving):
    kept = keep + swapped(send, "dp", 1).astype(jnp.float32)
    half = kept.shape[1] // 2
    groups = upper_groups()
    inner_shape = (kept.shape[0] // 4, 2, 2, half, D)
    parts = [kept[:, :half].reshape(inner_shape), kept[:, half:].reshape(inner_shape)]
    for n, order in enumerate(orders()):
        for bit in order:
            spot = 2 if bit == 1 and parts[n].ndim == 5 else 1
            stay = lax.index_in_dim(parts[n], 0, spot, keepdims=False)
            leave = lax.index_in_dim(parts[n], 1, spot, keepdims=False)
            parts[n] = stay + swapped(leave.astype(jnp.bfloat16), "space", bit).astype(jnp.float32)
    part = jnp.concatenate(parts, 1)
    part, leaving = lax.optimization_barrier((part, leaving))
    for bits in groups:
        part = part.reshape((-1, 1 << len(bits)) + part.shape[1:])
        masks = [sum(bit for n, bit in enumerate(bits) if m >> n & 1) for m in range(1 << len(bits))]
        low = part.astype(jnp.bfloat16)
        part = sum(
            [
                swapped(low[:, m], "space", mask).astype(jnp.float32)
                for m, mask in enumerate(masks)
                if m
            ],
            part[:, 0],
        )
    return part[0], leaving


def tall_parts():
    return [CH, D, D, CH] + [D] * (5 * ROUNDS) + [2] + [1] * (1 + 2 * ROUNDS)


def weave(ref, value):
    rows = value.shape[0]
    ref[pl.ds(0, rows, stride=2), :] = value[:, :HALF]
    ref[pl.ds(1, rows, stride=2), :] = value[:, HALF:]


def unweave(ref):
    rows = ref.shape[0] // 2
    return ref[pl.ds(0, rows, stride=2), :], ref[pl.ds(1, rows, stride=2), :]


def selector():
    row = lax.broadcasted_iota(jnp.int32, (8, HALF), 0)
    lane = lax.broadcasted_iota(jnp.int32, (8, HALF), 1)
    slot = jnp.where(lane == CH, 64.0, jnp.where(lane == CH + 1, 1.0, 0.0))
    known = jnp.where(lane == CH + 2, 1.0, 0.0)
    return jnp.where(row == 0, slot, jnp.where(row == 1, known, 0.0)).astype(jnp.bfloat16)


def ids_along(arrived):
    codes = inner(selector(), arrived, 1, 1)
    return jnp.where(codes[1:2, :] > 0, codes[0:1, :], -1.0).astype(jnp.int32)


def ids_down(arrived):
    codes = inner(arrived, selector(), 1, 1)
    return jnp.where(codes[:, 1:2] > 0, codes[:, 0:1], -1.0).astype(jnp.int32)


def whole(shape):
    return pl.BlockSpec(shape, lambda *_: (0,) * len(shape))


def node_terms(mesh, mats, bias):
    blocks = mesh.shape[0]
    tile = 1024

    def body(mesh_ref, mats_ref, bias_ref, dest_ref, self_ref):
        lowered = mesh_ref[...].astype(jnp.bfloat16)
        weave(dest_ref, inner(lowered, mats_ref[1], 1, 0) + bias_ref[0:1, :])
        self_ref[...] = inner(lowered, mats_ref[3], 1, 0) + bias_ref[1:2, :]

    rows = pl.BlockSpec((tile, D), lambda i: (i, 0))
    woven = pl.BlockSpec((2 * tile, HALF), lambda i: (i, 0))
    return pl.pallas_call(
        body,
        grid=(blocks // tile,),
        in_specs=[rows, whole(mats.shape), whole(bias.shape)],
        out_specs=[woven, rows],
        out_shape=[
            jax.ShapeDtypeStruct((2 * blocks, HALF), jnp.float32),
            jax.ShapeDtypeStruct((blocks, D), jnp.float32),
        ],
        compiler_params=LIMIT,
        cost_estimate=cost(4),
        name="node_terms",
    )(mesh, mats, bias)


def round_forward(index, mesh, before, own, after, mats, terms, following, decoder=()):
    blocks = mesh.shape[0]
    tile, chunk = 512, 16
    turns, high = tile // chunk, 2 * chunk
    more = following is not None
    spans = [before.shape[0], own.shape[0], after.shape[0]]
    reach = sum(spans)

    def body(*refs):
        index_ref, mesh_ref, before_ref, own_ref, after_ref, mats_ref, dest_ref = refs[:7]
        self_ref, refs = refs[7], refs[:7] + refs[8:]
        table, rows, wide = refs[-3:]
        if more:
            next_ref, sent_ref = refs[7], refs[13]
            new_ref, back_ref, update_ref, agg_ref, slope_ref = refs[8:13]
        else:
            ids_ref, dec_ref, out_ref, head_ref = refs[7:11]
            new_ref, back_ref, update_ref, agg_ref, slope_ref = refs[11:16]
            branch_ref, fetched_ref, decoded_ref, turn_ref = refs[16:20]
            total_ref = refs[20]
        step = pl.program_id(0)

        @pl.when(step == 0)
        def _():
            start = 0
            for source, span in zip((before_ref, own_ref, after_ref), spans):

                @pl.loop(0, span // 256)
                def _(i, source=source, start=start):
                    at = pl.multiple_of(i * 256, 256)
                    to = pl.multiple_of(start + at, 256)
                    table[pl.ds(to, 256), :] = source[pl.ds(at, 256), :].astype(jnp.float32)

                start = start + span

        mesh_in = mesh_ref[...]

        def fetch(turn):
            for edge in range(K):
                base = edge * blocks + step * tile + turn * chunk
                spots = [index_ref[base + u] for u in range(chunk)]
                values = [table[pl.ds(pl.multiple_of(spot, 2), 2), :] for spot in spots]
                for u in range(chunk):
                    spot = pl.multiple_of(edge * 2 * tile + turn * high + 2 * u, 2)
                    rows[pl.ds(spot, 2), :] = values[u]

        def load(turn):
            at = pl.multiple_of(turn * high, high)
            taken = [
                rows[pl.ds(pl.multiple_of(edge * 2 * tile + turn * high, high), high), :]
                for edge in range(K)
            ]
            return at, dest_ref[pl.ds(at, high), :], taken

        def dense(at, dest, taken):
            total = None
            for edge in range(K):
                value = taken[edge] + dest
                sigma = sigmoid(value)
                out = value * sigma
                slope_ref[edge, pl.ds(at, high), :] = (sigma + out * (1.0 - sigma)).astype(
                    jnp.bfloat16
                )
                total = out if total is None else total + out
            wide[pl.ds(at, high), :] = total * (1.0 / K)

        def some(turn, carry):
            loaded = load(turn - 1)
            fetch(turn)
            dense(*loaded)
            return carry

        fetch(0)
        lax.fori_loop(1, turns, some, 0)
        dense(*load(turns - 1))
        first, second = unweave(wide)
        first, second = first.astype(jnp.bfloat16), second.astype(jnp.bfloat16)
        agg_ref[:, :HALF] = first
        agg_ref[:, HALF:] = second
        update_in = (
            inner(first, mats_ref[2, :HALF, :], 1, 0)
            + inner(second, mats_ref[2, HALF:, :], 1, 0)
            + self_ref[...]
        )
        sigma = sigmoid(update_in)
        out = update_in * sigma
        back_ref[...] = sigma + out * (1.0 - sigma)
        update = out.astype(jnp.bfloat16)
        update_ref[...] = update
        new = mesh_in + inner(update, mats_ref[4], 1, 0)
        new_ref[...] = new
        lowered = new.astype(jnp.bfloat16)
        if more:
            weave(wide, inner(lowered, next_ref[0], 1, 0))
            sent_ref[...] = wide[...].astype(jnp.bfloat16)
            return
        nodes = lax.broadcasted_iota(jnp.int32, (ids_ref.shape[0], tile), 1) + step * tile
        chooser = jnp.where(nodes == ids_ref[...], 1.0, 0.0).astype(jnp.bfloat16)
        found = inner(chooser, lowered, 1, 0)

        @pl.when(step == 0)
        def _():
            total_ref[...] = found

        @pl.when(step > 0)
        def _():
            total_ref[...] += found

        @pl.when(step == blocks // tile - 1)
        def _():
            fetched = total_ref[...].astype(jnp.bfloat16)
            fetched_ref[...] = fetched
            value = inner(fetched, dec_ref[...], 1, 0) + head_ref[2:3, :]
            sigma = sigmoid(value)
            out = value * sigma
            turn_ref[...] = sigma + out * (1.0 - sigma)
            decoded = out.astype(jnp.bfloat16)
            decoded_ref[...] = decoded
            branch_ref[...] = inner(decoded, out_ref[...], 1, 0).astype(jnp.bfloat16)

    whole_rows = pl.BlockSpec((tile, D), lambda i, *_: (i, 0))
    woven = pl.BlockSpec((2 * tile, HALF), lambda i, *_: (i, 0))
    ins = [whole_rows] + [pl.BlockSpec(memory_space=pltpu.VMEM)] * 3
    ins = ins + [whole(mats.shape), woven, whole_rows]
    outs = [whole_rows] * 4 + [pl.BlockSpec((K, 2 * tile, HALF), lambda i, *_: (0, i, 0))]
    shapes = [
        jax.ShapeDtypeStruct((blocks, D), jnp.float32),
        jax.ShapeDtypeStruct((blocks, D), jnp.float32),
        jax.ShapeDtypeStruct((blocks, D), jnp.bfloat16),
        jax.ShapeDtypeStruct((blocks, D), jnp.bfloat16),
        jax.ShapeDtypeStruct((K, 2 * blocks, HALF), jnp.bfloat16),
    ]
    args = [index, mesh, before, own, after, mats, *terms]
    if more:
        ins.append(pl.BlockSpec((1, D, D), lambda *_: (0, 0, 0)))
        outs.append(woven)
        shapes.append(jax.ShapeDtypeStruct((2 * blocks, HALF), jnp.bfloat16))
        args.append(following)
    scratch = []
    if decoder:
        posts = decoder[0].shape[0]
        ins = ins + [whole(arg.shape) for arg in decoder]
        args = args + list(decoder)
        for width, kind in ((HALF, jnp.bfloat16), (D, jnp.bfloat16), (D, jnp.bfloat16), (D, jnp.float32)):
            outs.append(whole((posts, width)))
            shapes.append(jax.ShapeDtypeStruct((posts, width), kind))
        scratch = [pltpu.VMEM((posts, D), jnp.float32)]
    return pl.pallas_call(
        body,
        grid_spec=pltpu.PrefetchScalarGridSpec(
            num_scalar_prefetch=1,
            grid=(blocks // tile,),
            in_specs=ins,
            out_specs=outs,
            scratch_shapes=scratch
            + [
                pltpu.VMEM((reach, HALF), jnp.float32),
                pltpu.VMEM((K * 2 * tile, HALF), jnp.float32),
                pltpu.VMEM((2 * tile, HALF), jnp.float32),
            ],
        ),
        out_shape=shapes,
        compiler_params=pltpu.CompilerParams(vmem_limit_bytes=40 * 2**20),
        cost_estimate=cost(25),
        name="round_forward",
    )(*args)


def edges_backward(index, back, slopes, mats, carried=(), landed=()):
    blocks = back.shape[0]
    tile, chunk = 512, 16
    steps, turns, high = blocks // tile, tile // chunk, 2 * chunk
    reach = 2 * (blocks + 2 * H)

    def body(*refs):
        if carried:
            index_ref, back_ref, slope_ref, mats_ref = refs[:4]
            past, rest = refs[4:9], refs[9:]
            (new_ref, out_ref, sent_ref), rest = rest[:3], rest[3:]
        else:
            index_ref, back_ref, slope_ref, mats_ref = refs[:4]
            (ids_ref, landed_ref, turn_ref, w_out_ref, w_dec_ref), rest = refs[4:9], refs[9:]
            (new_ref, out_ref, gdec_ref), rest = rest[:3], rest[3:]
            gathered, rest = rest[5], rest[:5] + rest[6:]
        guin_ref, low_ref, before_ref, own_ref, after_ref, wide, wider, flows, *tables = rest
        step = pl.program_id(0)

        @pl.when(step == 0)
        def _():
            @pl.loop(0, reach // 256)
            def _(i):
                for table in tables:
                    table[pl.ds(pl.multiple_of(i * 256, 256), 256), :] = jnp.zeros(
                        (256, HALF), jnp.float32
                    )

        if carried:
            new, one, two = ended(*past, wide)
            sent_ref[:, :HALF] = one
            sent_ref[:, HALF:] = two
            new_ref[...] = new
            grad_out = new.astype(jnp.bfloat16)
            out_ref[...] = grad_out
        else:

            @pl.when(step == 0)
            def _():
                grad_dec = inner(landed_ref[...], w_out_ref[...], 1, 1) * turn_ref[...]
                grad_dec = grad_dec.astype(jnp.bfloat16)
                gdec_ref[...] = grad_dec
                gathered[...] = inner(grad_dec, w_dec_ref[...], 1, 1).astype(jnp.bfloat16)

            nodes = lax.broadcasted_iota(jnp.int32, (tile, landed_ref.shape[0]), 0) + step * tile
            chooser = jnp.where(nodes == ids_ref[...], 1.0, 0.0).astype(jnp.bfloat16)
            new = inner(chooser, gathered[...], 1, 0)
            new_ref[...] = new
            grad_out = new.astype(jnp.bfloat16)
            out_ref[...] = grad_out
        grad_uin = (inner(grad_out, mats_ref[4], 1, 1) * back_ref[...]).astype(jnp.bfloat16)
        guin_ref[...] = grad_uin
        weave(wide, inner(grad_uin, mats_ref[2], 1, 1) * (1.0 / K))

        def dense(turn):
            at = pl.multiple_of(turn * high, high)
            grad_agg = wide[pl.ds(at, high), :]
            total, parts = None, []
            for edge in range(K):
                flow = grad_agg * slope_ref[edge, pl.ds(at, high), :].astype(jnp.float32)
                parts.append(flow)
                total = flow if total is None else total + flow
            return at, total, parts

        def keep(turn, at, total, parts):
            for edge in range(K):
                spot = pl.multiple_of(edge * 2 * tile + turn * high, high)
                flows[pl.ds(spot, high), :] = parts[edge]
            wider[pl.ds(at, high), :] = total

        def scatter(turn):
            for u in range(chunk):
                spots, sums = [], []
                for edge in range(K):
                    base = edge * blocks + step * tile + turn * chunk
                    spots.append(pl.multiple_of(index_ref[base + u], 2))
                for edge in range(K):
                    spot = pl.multiple_of(edge * 2 * tile + turn * high + 2 * u, 2)
                    sums.append(tables[edge][pl.ds(spots[edge], 2), :] + flows[pl.ds(spot, 2), :])
                for edge in range(K):
                    tables[edge][pl.ds(spots[edge], 2), :] = sums[edge]

        def some(turn, carry):
            found = dense(turn)
            scatter(turn - 1)
            keep(turn, *found)
            return carry

        keep(0, *dense(0))
        lax.fori_loop(1, turns, some, 0)
        scatter(turns - 1)
        first, second = unweave(wider)
        low_ref[:, :HALF] = first.astype(jnp.bfloat16)
        low_ref[:, HALF:] = second.astype(jnp.bfloat16)

        @pl.when(step == steps - 1)
        def _():
            def summed(at):
                value = tables[0][pl.ds(at, 256), :]
                for table in tables[1:]:
                    value = value + table[pl.ds(at, 256), :]
                return value

            @pl.loop(0, 2 * H // 256)
            def _(i):
                at = pl.multiple_of(i * 256, 256)
                far = pl.multiple_of(2 * H + 2 * blocks + at, 256)
                before_ref[pl.ds(at, 256), :] = summed(at).astype(jnp.bfloat16)
                after_ref[pl.ds(at, 256), :] = summed(far).astype(jnp.bfloat16)

            @pl.loop(0, 2 * blocks // 256)
            def _(i):
                at = pl.multiple_of(i * 256, 256)
                own_ref[pl.ds(at, 256), :] = summed(pl.multiple_of(2 * H + at, 256))

    rows = pl.BlockSpec((tile, D), lambda i, *_: (i, 0))
    woven = pl.BlockSpec((2 * tile, HALF), lambda i, *_: (i, 0))
    low = jax.ShapeDtypeStruct((blocks, D), jnp.bfloat16)
    low_posts = (landed[1].shape[0], D) if landed else None
    last = low if carried else jax.ShapeDtypeStruct(low_posts, jnp.bfloat16)
    return pl.pallas_call(
        body,
        grid_spec=pltpu.PrefetchScalarGridSpec(
            num_scalar_prefetch=1,
            grid=(steps,),
            in_specs=[
                rows,
                pl.BlockSpec((K, 2 * tile, HALF), lambda i, *_: (0, i, 0)),
                whole(mats.shape),
            ]
            + ([rows] + [woven] * 3 + [whole(mats.shape)] if carried else [])
            + [whole(arg.shape) for arg in landed],
            out_specs=([rows] * 3 if carried else [rows, rows, whole(low_posts)])
            + [
                rows, rows,
                whole((2 * H, HALF)), whole((2 * blocks, HALF)), whole((2 * H, HALF)),
            ],
            scratch_shapes=([] if carried else [pltpu.VMEM(low_posts, jnp.bfloat16)])
            + [
                pltpu.VMEM((2 * tile, HALF), jnp.float32),
                pltpu.VMEM((2 * tile, HALF), jnp.float32),
                pltpu.VMEM((2 * tile * K, HALF), jnp.float32),
            ]
            + [pltpu.VMEM((reach, HALF), jnp.float32)] * K,
        ),
        out_shape=[
            jax.ShapeDtypeStruct((blocks, D), jnp.float32),
            low,
            last,
            low,
            low,
            jax.ShapeDtypeStruct((2 * H, HALF), jnp.bfloat16),
            jax.ShapeDtypeStruct((2 * blocks, HALF), jnp.float32),
            jax.ShapeDtypeStruct((2 * H, HALF), jnp.bfloat16),
        ],
        compiler_params=LIMIT,
        cost_estimate=cost(28 if carried else 25),
        name="edges_backward",
    )(index, back, slopes, mats, *carried, *landed)


def ended(part_ref, own_ref, first_ref, last_ref, mats_ref, wide):
    wide[...] = (
        own_ref[...] + first_ref[...].astype(jnp.float32) + last_ref[...].astype(jnp.float32)
    )
    one, two = unweave(wide)
    one, two = one.astype(jnp.bfloat16), two.astype(jnp.bfloat16)
    new = (
        part_ref[...]
        + inner(one, mats_ref[0, :, :HALF], 1, 1)
        + inner(two, mats_ref[0, :, HALF:], 1, 1)
    )
    return new, one, two


def carried_terms(grad_mesh, grad_uin, dest_low, mats):
    blocks = grad_mesh.shape[0]
    tile = 1024

    def body(grad_ref, guin_ref, dest_ref, mats_ref, part_ref):
        part_ref[...] = (
            grad_ref[...]
            + inner(guin_ref[...], mats_ref[3], 1, 1)
            + inner(dest_ref[...], mats_ref[1], 1, 1)
        )

    rows = pl.BlockSpec((tile, D), lambda i: (i, 0))
    return pl.pallas_call(
        body,
        grid=(blocks // tile,),
        in_specs=[rows, rows, rows, whole(mats.shape)],
        out_specs=rows,
        out_shape=jax.ShapeDtypeStruct((blocks, D), jnp.float32),
        compiler_params=LIMIT,
        cost_estimate=cost(4),
        name="carried_terms",
    )(grad_mesh, grad_uin, dest_low, mats)


def encode_rows(arrived, w_in, w_node, biases, source):
    posts = arrived.shape[0]
    tile = 512

    def body(
        arrived_ref, in_ref, node_ref, bias_ref, source_ref,
        mesh_ref, gathered_ref, sent_ref, ids_ref, down_ref, encoded, wide,
    ):
        step = pl.program_id(0)

        @pl.when(step == 0)
        def _():
            entering = inner(arrived_ref[...], in_ref[...], 1, 0) + bias_ref[0:1, :]
            encoded[...] = silu(entering).astype(jnp.bfloat16)
            ids_ref[...] = ids_along(arrived_ref[...])
            down_ref[...] = ids_down(arrived_ref[...])

        nodes = lax.broadcasted_iota(jnp.int32, (tile, posts), 0) + step * tile
        chooser = jnp.where(nodes == ids_ref[...], 1.0, 0.0).astype(jnp.bfloat16)
        gathered = inner(chooser, encoded[...], 1, 0).astype(jnp.bfloat16)
        gathered_ref[...] = gathered
        mesh = silu(inner(gathered, node_ref[...], 1, 0) + bias_ref[1:2, :])
        mesh_ref[...] = mesh
        weave(wide, inner(mesh.astype(jnp.bfloat16), source_ref[0], 1, 0))
        sent_ref[...] = wide[...].astype(jnp.bfloat16)

    rows = pl.BlockSpec((tile, D), lambda i: (i, 0))
    args = (arrived, w_in, w_node, biases, source)
    return pl.pallas_call(
        body,
        grid=(H // tile,),
        in_specs=[whole(arg.shape) for arg in args[:-1]]
        + [pl.BlockSpec((1, D, D), lambda *_: (0, 0, 0))],
        out_specs=[rows, rows, pl.BlockSpec((2 * tile, HALF), lambda i: (i, 0))]
        + [whole((1, posts)), whole((posts, 1))],
        out_shape=[
            jax.ShapeDtypeStruct((H, D), jnp.float32),
            jax.ShapeDtypeStruct((H, D), jnp.bfloat16),
            jax.ShapeDtypeStruct((2 * H, HALF), jnp.bfloat16),
            jax.ShapeDtypeStruct((1, posts), jnp.int32),
            jax.ShapeDtypeStruct((posts, 1), jnp.int32),
        ],
        scratch_shapes=[pltpu.VMEM((posts, D), jnp.bfloat16), pltpu.VMEM((2 * tile, HALF), jnp.float32)],
        compiler_params=LIMIT,
        cost_estimate=cost(5),
        name="encode_rows",
    )(*args)


def encode_backward(carried, mesh, gathered, arrived, ids, w_in, w_node, biases):
    blocks = mesh.shape[0]
    posts = arrived.shape[0]
    tile = 512
    steps = blocks // tile

    def body(
        part_ref, own_ref, first_ref, last_ref, mats_ref,
        mesh_ref, gathered_ref, arrived_ref, ids_ref, in_ref, node_ref, bias_ref,
        new_ref, out_ref, gin_ref, gnode_ref, gbias_ref, gsource_ref, total, wide,
    ):
        step = pl.program_id(0)

        @pl.when(step == 0)
        def _():
            for ref in (total, gnode_ref, gbias_ref, gsource_ref):
                ref[...] = jnp.zeros(ref.shape, jnp.float32)

        new, one, two = ended(part_ref, own_ref, first_ref, last_ref, mats_ref, wide)
        new_ref[...] = new
        out_ref[...] = new.astype(jnp.bfloat16)
        lowered = mesh_ref[...].astype(jnp.bfloat16)
        gsource_ref[:, :HALF] += inner(lowered, one, 0, 0)
        gsource_ref[:, HALF:] += inner(lowered, two, 0, 0)
        node_in = inner(gathered_ref[...], node_ref[...], 1, 0) + bias_ref[1:2, :]
        grad_node = (new * slope(node_in)).astype(jnp.bfloat16)
        gbias_ref[1:2, :] += jnp.sum(grad_node.astype(jnp.float32), 0, keepdims=True)
        gnode_ref[...] += inner(gathered_ref[...], grad_node, 0, 0)
        back = inner(grad_node, node_ref[...], 1, 1).astype(jnp.bfloat16)
        nodes = lax.broadcasted_iota(jnp.int32, (posts, tile), 1) + step * tile
        chooser = jnp.where(nodes == ids_ref[...], 1.0, 0.0).astype(jnp.bfloat16)
        total[...] += inner(chooser, back, 1, 0)

        @pl.when(step == steps - 1)
        def _():
            entering = inner(arrived_ref[...], in_ref[...], 1, 0) + bias_ref[0:1, :]
            grad_enc = (total[...] * slope(entering)).astype(jnp.bfloat16)
            gbias_ref[0:1, :] = jnp.sum(grad_enc.astype(jnp.float32), 0, keepdims=True)
            gin_ref[...] = inner(arrived_ref[...], grad_enc, 0, 0)

    rows = pl.BlockSpec((tile, D), lambda i: (i, 0))
    woven = pl.BlockSpec((2 * tile, HALF), lambda i: (i, 0))
    args = (arrived, ids, w_in, w_node, biases)
    shapes = [(HALF, D), (D, D), (2, D), (D, D)]
    return pl.pallas_call(
        body,
        grid=(steps,),
        in_specs=[rows] + [woven] * 3 + [whole(carried[4].shape), rows, rows]
        + [whole(arg.shape) for arg in args],
        out_specs=[rows, rows] + [whole(shape) for shape in shapes],
        out_shape=[
            jax.ShapeDtypeStruct((blocks, D), jnp.float32),
            jax.ShapeDtypeStruct((blocks, D), jnp.bfloat16),
        ]
        + [jax.ShapeDtypeStruct(shape, jnp.float32) for shape in shapes],
        scratch_shapes=[pltpu.VMEM((posts, D), jnp.float32), pltpu.VMEM((2 * tile, HALF), jnp.float32)],
        compiler_params=LIMIT,
        cost_estimate=cost(10),
        name="encode_backward",
    )(*carried, mesh, gathered, *args)


def shards(walk, master, moment1, moment2, inputs, targets, valid, owner, slot, neighbours, partner):
    bands = lax.axis_size("space")
    band = lax.axis_index("space")
    peers = lax.axis_size(ALL)
    place = lax.axis_index(ALL)
    shard = master.shape[0]
    total_size = shard * peers
    height = pieces_of(total_size, peers)[3]
    offset = lax.rem(lax.rem(shard, D) * place, D)
    piece = lax.dynamic_update_slice_in_dim(
        jnp.zeros((height * D,), jnp.bfloat16), master.astype(jnp.bfloat16), offset, 0
    )
    state_in = inputs[0]
    counted = valid[0].astype(jnp.float32)
    points = state_in.shape[1]
    blocks = neighbours.shape[0]
    assert blocks == H
    capacity = max(2, 2 * points // bands)

    def posting(state_in, valid, owner, slot):
        local_count = jnp.sum(valid[0])
        digits = (local_count >> jnp.array([16, 8, 0], jnp.int32)) & 255
        digits = jnp.pad(digits, (CH + 3, HALF - CH - 6)).astype(jnp.float32)[None, :]
        target_band = owner[0, :, 0]
        hits = (
            target_band[:, None] == jnp.arange(bands, dtype=jnp.int32)[None, :]
        ).astype(jnp.int32)
        ranks = jnp.sum(jnp.cumsum(hits, 0) * hits, 1) - 1
        places_out = jnp.sum(hits * jnp.asarray(walk, jnp.int32)[None, :], 1) * capacity + ranks
        poster = (
            jnp.arange(bands * capacity, dtype=jnp.int32)[:, None] == places_out[None, :]
        ).astype(jnp.bfloat16)
        spots = slot[0][None, :]
        columns = jnp.concatenate(
            [
                state_in,
                (spots // 64).astype(jnp.bfloat16),
                (spots % 64).astype(jnp.bfloat16),
                jnp.ones((1, points), jnp.bfloat16),
                jnp.zeros((HALF - CH - 3, points), jnp.bfloat16),
            ],
            0,
        )
        return poster, (inner(poster, columns, 1, 1) + digits).astype(jnp.bfloat16)

    def exchanged(rows):
        return lax.all_to_all(
            rows.reshape(bands, capacity, HALF), "space", split_axis=0, concat_axis=0, tiled=True
        ).reshape(bands * capacity, HALF)

    held, poster, posted = gathered_blocks(
        piece.reshape(height, D), (state_in, valid, owner, slot), posting
    )
    arrived = exchanged(posted)
    w_in, w_node, w_dec, w_out, *w_round, biases = spread_rows(
        held, total_size, peers, place
    )
    arrived, biases = lax.optimization_barrier((arrived, biases))
    counts = arrived.reshape(bands, capacity, HALF)[:, 0, CH + 3 : CH + 6].astype(jnp.float32)
    counts = jnp.sum(counts, 0, keepdims=True)
    w_out = jnp.pad(w_out.reshape(D, CH), ((0, 0), (0, HALF - CH)))
    w_round = [mats.reshape(5, D, D) for mats in w_round]
    b_head = biases[:3]
    b_round = biases[3:].reshape(ROUNDS, 2, D)
    mesh, gathered, sent, ids_row, ids = encode_rows(
        arrived, w_in, w_node, biases, w_round[0]
    )
    sent, partner, neighbours, counted, counts = lax.optimization_barrier(
        (sent, partner, neighbours, counted, counts)
    )
    counts = counts + swapped(counts, "dp", 1)
    index = 2 * ((neighbours - band * blocks + H) % (blocks * bands)).T.reshape(-1)
    moved = [(n, place) for n, place in enumerate(walk) if n != place]
    stays = jnp.asarray([n == place for n, place in enumerate(walk)])[band]
    index = lax.ppermute(index, "space", list(enumerate(walk)))

    def at_home(rows):
        return lax.ppermute(rows, "space", [(j, i) for i, j in moved])

    def settled(own, came):
        return jnp.where(stays, own, came.astype(jnp.float32))

    partner_by = partner - band * points - jnp.arange(points, dtype=jnp.int32)
    coded = jnp.where(partner_by >= NEAR, partner_by - NEAR + 1, 0).astype(jnp.bfloat16)
    low_valid = jnp.concatenate([counted.astype(jnp.bfloat16), coded[None, :]], 0)
    valid_around = jnp.concatenate(
        [
            shifted(low_valid[:, points - ROWW :], "space", 1),
            low_valid,
            shifted(low_valid[:, :ROWW], "space", -1),
        ],
        1,
    )
    kept = []
    for layer in range(ROUNDS):
        before, after = halo(walk, sent, sent)
        terms = node_terms(mesh, w_round[layer], b_round[layer])
        if layer == 0:
            before, valid_around, counts = lax.optimization_barrier((before, valid_around, counts))
        following = w_round[layer + 1] if layer + 1 < ROUNDS else None
        new, back, update, agg, slopes, *rest = round_forward(
            index, mesh, before, sent, after, w_round[layer], terms, following,
            () if following is not None else (ids, w_dec, w_out, biases),
        )
        kept.append((mesh, back, update, agg, slopes))
        mesh = new
        sent = rest[0]
    count = counts[0, 0] * 65536.0 + counts[0, 1] * 256.0 + counts[0, 2]
    wide_valid = valid_around[:CH].astype(jnp.float32)
    coded = valid_around[CH : CH + 1, : points + ROWW].astype(jnp.float32)
    weights = [
        (
            by,
            jnp.where(coded == by - NEAR + 1, 1.0, 0.0)
            * wide_valid[:, : points + ROWW]
            * wide_valid[:, by : by + points + ROWW],
        )
        for by in range(NEAR, ROWW + 1)
    ]
    branch_rows, fetched, decoded, dec_turn = rest
    returned = exchanged(branch_rows)
    branch = inner(returned, poster, 0, 0)[:CH]
    err = state_in.astype(jnp.float32) + branch - targets[0].astype(jnp.float32)
    def widened(values):
        low = values.astype(jnp.bfloat16)
        before = shifted(low[:, points - ROWW :], "space", 1).astype(jnp.float32)
        after = shifted(low[:, :ROWW], "space", -1).astype(jnp.float32)
        return jnp.concatenate([before, values, after], 1)

    wide_err = widened(err)
    paired = jnp.zeros((CH, points + ROWW), jnp.float32)
    pair_total = jnp.zeros((CH, points), jnp.float32)
    for by, both in weights:
        gap = both * (wide_err[:, : points + ROWW] - wide_err[:, by : by + points + ROWW])
        paired = paired + gap
        pair_total = pair_total + gap[:, ROWW:] * (
            wide_err[:, ROWW : ROWW + points] - wide_err[:, ROWW + by : ROWW + by + points]
        )
    local_total = jnp.sum(counted * err * err) + 0.5 * jnp.sum(pair_total)
    grad_pred = 2.0 * counted * err + paired[:, ROWW:]
    for by, both in weights:
        gap = both * (wide_err[:, : points + ROWW] - wide_err[:, by : by + points + ROWW])
        grad_pred = grad_pred - gap[:, ROWW - by : ROWW - by + points]
    grad_pred = grad_pred / count
    grad_rows = jnp.pad(grad_pred.astype(jnp.bfloat16), ((0, HALF - CH), (0, 0)))
    landed = exchanged(inner(poster, grad_rows, 1, 1).astype(jnp.bfloat16))
    landed, final_mesh = lax.optimization_barrier((landed, mesh.astype(jnp.bfloat16)))
    final_mesh = at_home(final_mesh)
    mats_grads = [None] * (5 * ROUNDS)
    bias_grads = [None] * (2 * ROUNDS)
    carried, grad_mesh = (), None
    for layer in reversed(range(ROUNDS)):
        old, back, update, agg, slopes = kept[layer]
        first_step = not carried
        grad_mesh, leaving, extra, grad_uin, dest_low, to_before, own, to_after = edges_backward(
            index, back, slopes, w_round[layer], carried,
            (ids_row, landed, dec_turn, w_out, w_dec) if first_step else (),
        )
        if not first_step:
            mats_grads[5 * layer + 5] = inner(
                kept[layer + 1][0].astype(jnp.bfloat16), extra, 0, 0
            )
        else:
            grad_wout = inner(decoded, landed, 0, 0)[:, :CH]
            grad_bdec = jnp.sum(extra.astype(jnp.float32), 0, keepdims=True)
            grad_wdec = inner(fetched, extra, 0, 0)
            to_before, to_after, final_mesh = lax.optimization_barrier(
                (to_before, to_after, final_mesh)
            )
        from_before, from_after = halo(walk, to_after, to_before)
        if first_step:
            from_before, final_mesh = lax.optimization_barrier(
                (from_before, settled(mesh, final_mesh))
            )
        lowered = old.astype(jnp.bfloat16)
        mats_grads[5 * layer + 1 : 5 * layer + 5] = [
            inner(lowered, dest_low, 0, 0),
            inner(agg, grad_uin, 0, 0),
            inner(lowered, grad_uin, 0, 0),
            inner(update, leaving, 0, 0),
        ]
        bias_grads[2 * layer] = jnp.sum(dest_low.astype(jnp.float32), 0, keepdims=True)
        bias_grads[2 * layer + 1] = jnp.sum(grad_uin.astype(jnp.float32), 0, keepdims=True)
        part = carried_terms(grad_mesh, grad_uin, dest_low, w_round[layer])
        carried = (part, own, from_before, from_after, w_round[layer])
    grad_mesh, leaving, grad_win, grad_wnode, grad_bpair, mats_grads[0] = encode_backward(
        carried, kept[0][0], gathered, arrived, ids, w_in, w_node, biases
    )
    parts = [grad_win, grad_wnode, grad_wdec, grad_wout.reshape(CH, D)]
    parts = parts + mats_grads
    parts = parts + [grad_bpair, grad_bdec] + bias_grads
    keep, send = collect_rows(parts, total_size, peers, place)
    mine, leaving = reduced_piece(keep, send, leaving)
    late = at_home(leaving)
    mine = lax.dynamic_slice_in_dim(mine.reshape(-1), offset, shard)
    lane = lax.broadcasted_iota(jnp.int32, (8, HALF), 1)
    sums, late = summed_everywhere(
        jnp.where(lane == 0, local_total, jnp.sum(mine * mine)), late
    )
    total, norm = sums[0, 0], jnp.sqrt(sums[0, 1])
    node_grads = settled(grad_mesh, late)
    clipped = mine * jnp.minimum(1.0, 0.05 / norm)
    first = 0.9 * moment1 + 0.1 * clipped
    second = 0.999 * moment2 + 0.001 * clipped * clipped
    first_hat = first / (1.0 - 0.9**STEP)
    second_hat = second / (1.0 - 0.999**STEP)
    updated = master - 0.1 * (first_hat / (jnp.sqrt(second_hat) + 1e-08) + 0.1 * master)
    return (
        total.reshape(1),
        count.reshape(1),
        norm.reshape(1),
        updated,
        first,
        second,
        updated.astype(jnp.bfloat16),
        final_mesh.reshape(1, blocks, D),
        node_grads.reshape(1, blocks, D),
        grad_pred.reshape(1, grad_pred.shape[0], points),
    )


def solution(mesh):
    return jax.shard_map(
        functools.partial(shards, walk_of(mesh)),
        mesh=mesh,
        in_specs=(
            P(("dp", "space")),
            P(("dp", "space")),
            P(("dp", "space")),
            P("dp", None, "space"),
            P("dp", None, "space"),
            P("dp", None, "space"),
            P("dp", "space", None),
            P("dp", "space"),
            P("space", None),
            P("space"),
        ),
        out_specs=(
            P(),
            P(),
            P(),
            P(("dp", "space")),
            P(("dp", "space")),
            P(("dp", "space")),
            P(("dp", "space")),
            P("dp", "space", None),
            P("dp", "space", None),
            P("dp", None, "space"),
        ),
        check_vma=False,
    )
```

```python
import functools

import jax
import jax.numpy as jnp
from jax import lax
from jax.experimental import pallas as pl
from jax.experimental.pallas import tpu as pltpu
from jax.sharding import PartitionSpec as P

D = 256
HALF = 128
CH = 78
ROUNDS = 3
K = 6
ROWW = 360
NEAR = 358
STEP = 10
H = 2048
ALL = ("dp", "space")
LIMIT = pltpu.CompilerParams(vmem_limit_bytes=60 * 2**20)


def cost(micros):
    return pl.CostEstimate(flops=0, bytes_accessed=micros * 3_000_000, transcendentals=0)


def inner(left, right, left_dim, right_dim):
    return lax.dot_general(
        left, right, (((left_dim,), (right_dim,)), ((), ())), preferred_element_type=jnp.float32
    )


def sigmoid(value):
    return 0.5 * jnp.tanh(0.5 * value) + 0.5


def silu(value):
    return value * sigmoid(value)


def slope(value):
    sigma = sigmoid(value)
    return sigma * (1.0 + value * (1.0 - sigma))


def shifted(shard, axis, by):
    peers = lax.axis_size(axis)
    pairs = [(i, i + by) for i in range(peers) if 0 <= i + by < peers]
    return lax.ppermute(shard, axis, pairs)


def walk_of(mesh):
    count = mesh.shape["space"]
    chips = [getattr(device, "coords", None) for device in mesh.devices[0].reshape(-1)]
    if any(chip is None for chip in chips) or len(set(map(tuple, chips))) != count:
        return list(range(count))
    at = {tuple(chip): n for n, chip in enumerate(chips)}
    xs, ys, zs = (sorted({chip[n] for chip in at}) for n in range(3))
    if len(xs) * len(ys) * len(zs) != count:
        return list(range(count))
    if (len(xs), len(ys), len(zs)) == (2, 2, 4):
        corners = [(0, 0), (1, 0), (0, 1), (1, 1)]
        planes = [(0, 1, 3, 2), (2, 0, 1, 3), (3, 1, 0, 2), (2, 3, 1, 0)]
        steps = [(*corners[n], z) for z, plane in enumerate(planes) for n in plane]
        return [at[(xs[x], ys[y], zs[z])] for x, y, z in steps]
    walk, plane = [], []
    for n, y in enumerate(ys):
        plane = plane + [(x, y) for x in (xs if n % 2 == 0 else xs[::-1])]
    for n, z in enumerate(zs):
        walk = walk + [at[(x, y, z)] for x, y in (plane if n % 2 == 0 else plane[::-1])]
    return walk


def halo(walk, last, initial):
    up = list(zip(walk, walk[1:] + walk[:1]))
    down = [(j, i) for i, j in up]
    return lax.ppermute(last, "space", up), lax.ppermute(initial, "space", down)


def pieces_of(total, peers):
    share = total // peers
    starts = [share * d // D for d in range(peers)]
    counts = [-(-share * (d + 1) // D) - starts[d] for d in range(peers)]
    shared = [share * d % D != 0 for d in range(peers)]
    height = -(-max(counts) // 16) * 16
    return starts, counts, shared, height


def parts_of():
    return [CH, D, D, CH] + [5 * D] * ROUNDS + [3 + 2 * ROUNDS]


def swapped(value, axis, bit):
    return lax.ppermute(value, axis, [(i, i ^ bit) for i in range(lax.axis_size(axis))])


def bits_of(axis):
    return [1 << n for n in range(lax.axis_size(axis).bit_length() - 1)]


def others(value, axis, bits):
    masks = [sum(bit for n, bit in enumerate(bits) if m >> n & 1) for m in range(1, 1 << len(bits))]
    return [swapped(value, axis, mask) for mask in masks]


def upper_groups():
    bits = bits_of("space")[2:]
    return [tuple(bits[n : n + 2]) for n in range(0, len(bits), 2)]


def orders():
    return [(1, 2), (2, 1)]


def summed_everywhere(value, arriving):
    for bits in reversed(upper_groups()):
        value = sum(others(value, "space", bits), value)
    value = value + swapped(value, "dp", 1)
    value, arriving = lax.optimization_barrier((value, arriving))
    return sum(others(value, "space", (1, 2)), value), arriving


def gathered_blocks(piece, posted):
    held, weights, size = piece[None], {}, 1
    for bits in reversed(upper_groups()):
        held = jnp.concatenate([held] + others(held, "space", bits), 0)
        for n, bit in enumerate(bits):
            weights[bit] = size << n
        size = size << len(bits)
    half = piece.shape[0] // 2
    held = [held[:, :half], held[:, half:]]
    ranks = [dict(weights), dict(weights)]
    for turn in (1, 0):
        if turn == 0:
            held[0], held[1], posted = lax.optimization_barrier((*held, posted))
        for n, order in enumerate(orders()):
            held[n] = jnp.concatenate([held[n], swapped(held[n], "space", order[turn])], 0)
            ranks[n][order[turn]] = size
        size = size << 1
    return (held, [swapped(part, "dp", 1) for part in held], ranks), posted


def spread_rows(gathered, total, peers, place):
    (first, second), (first_far, second_far), ranks = gathered
    starts, counts, shared, height = pieces_of(total, peers)
    half, group = height // 2, first.shape[0]
    rows = -(-total // D)
    sizes = parts_of()
    def at(rank, relative):
        spot = 0
        for bit, weight in rank.items():
            spot = spot + jnp.where((relative & bit) != 0, weight, 0)
        return spot

    def body(place_ref, *refs):
        sources, outs, buffer = refs[:4], refs[4:-1], refs[-1]
        me = place_ref[0]
        mine = me // group
        for d in range(peers):
            relative = (me ^ d) & (group - 1)
            spots = [at(rank, relative) for rank in ranks]

            def lay(one, two, d=d, spots=spots):
                piece = jnp.concatenate([one[spots[0]], two[spots[1]]], 0).astype(jnp.float32)
                start, count = starts[d], counts[d]
                if shared[d]:
                    buffer[start : start + 1, :] = buffer[start : start + 1, :] + piece[:1]
                    buffer[start + 1 : start + count, :] = piece[1:count]
                else:
                    buffer[start : start + count, :] = piece[:count]

            @pl.when(mine == d // group)
            def _():
                lay(sources[0], sources[1])

            @pl.when(mine != d // group)
            def _():
                lay(sources[2], sources[3])

        start = 0
        for out, size in zip(outs, sizes):
            out[:size, :] = buffer[start : start + size, :].astype(out.dtype)
            if out.shape[0] > size:
                out[size:, :] = jnp.zeros((out.shape[0] - size, D), out.dtype)
            start = start + size

    kinds = [jnp.bfloat16] * (4 + ROUNDS) + [jnp.float32]
    talls = [HALF] + sizes[1:]
    return pl.pallas_call(
        body,
        grid_spec=pltpu.PrefetchScalarGridSpec(
            num_scalar_prefetch=1,
            grid=(1,),
            in_specs=[whole(first.shape)] * 4,
            out_specs=[whole((tall, D)) for tall in talls],
            scratch_shapes=[pltpu.VMEM((-(-rows // 8) * 8 + 8, D), jnp.float32)],
        ),
        out_shape=[jax.ShapeDtypeStruct((tall, D), kind) for tall, kind in zip(talls, kinds)],
        compiler_params=LIMIT,
        cost_estimate=cost(4),
        name="spread_rows",
    )(place.reshape(1), first, second, first_far, second_far)


def collect_rows(parts, total, peers, place):
    starts, counts, shared, height = pieces_of(total, peers)
    rows = -(-total // D)
    sizes = [min(part.shape[0], size) for part, size in zip(parts, tall_parts())]
    group = lax.axis_size("space")

    def body(place_ref, *refs):
        sources, keep, send, buffer = refs[:-3], refs[-3], refs[-2], refs[-1]
        start = 0
        for source, size in zip(sources, sizes):
            buffer[start : start + size, :] = source[:size, :]
            start = start + size
        if buffer.shape[0] > start:
            buffer[start:, :] = jnp.zeros((buffer.shape[0] - start, D), jnp.float32)
        me = place_ref[0]
        mine = me // group
        for d in range(peers):
            relative = (me ^ d) & (group - 1)

            @pl.when(mine == d // group)
            def _():
                keep[relative] = buffer[starts[d] : starts[d] + height, :]

            @pl.when(mine != d // group)
            def _():
                send[relative] = buffer[starts[d] : starts[d] + height, :].astype(jnp.bfloat16)

    shape = (group, height, D)
    return pl.pallas_call(
        body,
        grid_spec=pltpu.PrefetchScalarGridSpec(
            num_scalar_prefetch=1,
            grid=(1,),
            in_specs=[whole(part.shape) for part in parts],
            out_specs=[whole(shape), whole(shape)],
            scratch_shapes=[pltpu.VMEM((-(-rows // 8) * 8 + height + 8, D), jnp.float32)],
        ),
        out_shape=[
            jax.ShapeDtypeStruct(shape, jnp.float32),
            jax.ShapeDtypeStruct(shape, jnp.bfloat16),
        ],
        compiler_params=LIMIT,
        cost_estimate=cost(5),
        name="collect_rows",
    )(place.reshape(1), *parts)


def reduced_piece(keep, send, leaving):
    kept = keep + swapped(send, "dp", 1).astype(jnp.float32)
    half = kept.shape[1] // 2
    groups = upper_groups()
    inner_shape = (kept.shape[0] // 4, 2, 2, half, D)
    parts = [kept[:, :half].reshape(inner_shape), kept[:, half:].reshape(inner_shape)]
    for n, order in enumerate(orders()):
        for bit in order:
            spot = 2 if bit == 1 and parts[n].ndim == 5 else 1
            stay = lax.index_in_dim(parts[n], 0, spot, keepdims=False)
            leave = lax.index_in_dim(parts[n], 1, spot, keepdims=False)
            parts[n] = stay + swapped(leave.astype(jnp.bfloat16), "space", bit).astype(jnp.float32)
    part = jnp.concatenate(parts, 1)
    part, leaving = lax.optimization_barrier((part, leaving))
    for bits in groups:
        part = part.reshape((-1, 1 << len(bits)) + part.shape[1:])
        masks = [sum(bit for n, bit in enumerate(bits) if m >> n & 1) for m in range(1 << len(bits))]
        low = part.astype(jnp.bfloat16)
        part = sum(
            [
                swapped(low[:, m], "space", mask).astype(jnp.float32)
                for m, mask in enumerate(masks)
                if m
            ],
            part[:, 0],
        )
    return part[0], leaving


def tall_parts():
    return [CH, D, D, CH] + [D] * (5 * ROUNDS) + [2] + [1] * (1 + 2 * ROUNDS)


def weave(ref, value):
    rows = value.shape[0]
    ref[pl.ds(0, rows, stride=2), :] = value[:, :HALF]
    ref[pl.ds(1, rows, stride=2), :] = value[:, HALF:]


def unweave(ref):
    rows = ref.shape[0] // 2
    return ref[pl.ds(0, rows, stride=2), :], ref[pl.ds(1, rows, stride=2), :]


def selector():
    row = lax.broadcasted_iota(jnp.int32, (8, HALF), 0)
    lane = lax.broadcasted_iota(jnp.int32, (8, HALF), 1)
    slot = jnp.where(lane == CH, 64.0, jnp.where(lane == CH + 1, 1.0, 0.0))
    known = jnp.where(lane == CH + 2, 1.0, 0.0)
    return jnp.where(row == 0, slot, jnp.where(row == 1, known, 0.0)).astype(jnp.bfloat16)


def ids_along(arrived):
    codes = inner(selector(), arrived, 1, 1)
    return jnp.where(codes[1:2, :] > 0, codes[0:1, :], -1.0).astype(jnp.int32)


def ids_down(arrived):
    codes = inner(arrived, selector(), 1, 1)
    return jnp.where(codes[:, 1:2] > 0, codes[:, 0:1], -1.0).astype(jnp.int32)


def whole(shape):
    return pl.BlockSpec(shape, lambda *_: (0,) * len(shape))


def node_terms(mesh, mats, bias):
    blocks = mesh.shape[0]
    tile = 1024

    def body(mesh_ref, mats_ref, bias_ref, dest_ref, self_ref):
        lowered = mesh_ref[...].astype(jnp.bfloat16)
        weave(dest_ref, inner(lowered, mats_ref[1], 1, 0) + bias_ref[0:1, :])
        self_ref[...] = inner(lowered, mats_ref[3], 1, 0) + bias_ref[1:2, :]

    rows = pl.BlockSpec((tile, D), lambda i: (i, 0))
    woven = pl.BlockSpec((2 * tile, HALF), lambda i: (i, 0))
    return pl.pallas_call(
        body,
        grid=(blocks // tile,),
        in_specs=[rows, whole(mats.shape), whole(bias.shape)],
        out_specs=[woven, rows],
        out_shape=[
            jax.ShapeDtypeStruct((2 * blocks, HALF), jnp.float32),
            jax.ShapeDtypeStruct((blocks, D), jnp.float32),
        ],
        compiler_params=LIMIT,
        cost_estimate=cost(4),
        name="node_terms",
    )(mesh, mats, bias)


def round_forward(index, mesh, before, own, after, mats, terms, following, decoder=()):
    blocks = mesh.shape[0]
    tile, chunk = 512, 16
    turns, high = tile // chunk, 2 * chunk
    more = following is not None
    spans = [before.shape[0], own.shape[0], after.shape[0]]
    reach = sum(spans)

    def body(*refs):
        index_ref, mesh_ref, before_ref, own_ref, after_ref, mats_ref, dest_ref = refs[:7]
        self_ref, refs = refs[7], refs[:7] + refs[8:]
        table, rows, wide = refs[-3:]
        if more:
            next_ref, sent_ref = refs[7], refs[13]
            new_ref, back_ref, update_ref, agg_ref, slope_ref = refs[8:13]
        else:
            ids_ref, dec_ref, out_ref, head_ref = refs[7:11]
            new_ref, back_ref, update_ref, agg_ref, slope_ref = refs[11:16]
            branch_ref, fetched_ref, decoded_ref, turn_ref = refs[16:20]
            total_ref = refs[20]
        step = pl.program_id(0)

        @pl.when(step == 0)
        def _():
            start = 0
            for source, span in zip((before_ref, own_ref, after_ref), spans):

                @pl.loop(0, span // 256)
                def _(i, source=source, start=start):
                    at = pl.multiple_of(i * 256, 256)
                    to = pl.multiple_of(start + at, 256)
                    table[pl.ds(to, 256), :] = source[pl.ds(at, 256), :].astype(jnp.float32)

                start = start + span

        mesh_in = mesh_ref[...]

        def fetch(turn):
            for edge in range(K):
                base = edge * blocks + step * tile + turn * chunk
                spots = [index_ref[base + u] for u in range(chunk)]
                values = [table[pl.ds(pl.multiple_of(spot, 2), 2), :] for spot in spots]
                for u in range(chunk):
                    spot = pl.multiple_of(edge * 2 * tile + turn * high + 2 * u, 2)
                    rows[pl.ds(spot, 2), :] = values[u]

        def load(turn):
            at = pl.multiple_of(turn * high, high)
            taken = [
                rows[pl.ds(pl.multiple_of(edge * 2 * tile + turn * high, high), high), :]
                for edge in range(K)
            ]
            return at, dest_ref[pl.ds(at, high), :], taken

        def dense(at, dest, taken):
            total = None
            for edge in range(K):
                value = taken[edge] + dest
                sigma = sigmoid(value)
                out = value * sigma
                slope_ref[edge, pl.ds(at, high), :] = (sigma + out * (1.0 - sigma)).astype(
                    jnp.bfloat16
                )
                total = out if total is None else total + out
            wide[pl.ds(at, high), :] = total * (1.0 / K)

        def some(turn, carry):
            loaded = load(turn - 1)
            fetch(turn)
            dense(*loaded)
            return carry

        fetch(0)
        lax.fori_loop(1, turns, some, 0)
        dense(*load(turns - 1))
        first, second = unweave(wide)
        first, second = first.astype(jnp.bfloat16), second.astype(jnp.bfloat16)
        agg_ref[:, :HALF] = first
        agg_ref[:, HALF:] = second
        update_in = (
            inner(first, mats_ref[2, :HALF, :], 1, 0)
            + inner(second, mats_ref[2, HALF:, :], 1, 0)
            + self_ref[...]
        )
        sigma = sigmoid(update_in)
        out = update_in * sigma
        back_ref[...] = sigma + out * (1.0 - sigma)
        update = out.astype(jnp.bfloat16)
        update_ref[...] = update
        new = mesh_in + inner(update, mats_ref[4], 1, 0)
        new_ref[...] = new
        lowered = new.astype(jnp.bfloat16)
        if more:
            weave(wide, inner(lowered, next_ref[0], 1, 0))
            sent_ref[...] = wide[...].astype(jnp.bfloat16)
            return
        nodes = lax.broadcasted_iota(jnp.int32, (ids_ref.shape[0], tile), 1) + step * tile
        chooser = jnp.where(nodes == ids_ref[...], 1.0, 0.0).astype(jnp.bfloat16)
        found = inner(chooser, lowered, 1, 0)

        @pl.when(step == 0)
        def _():
            total_ref[...] = found

        @pl.when(step > 0)
        def _():
            total_ref[...] += found

        @pl.when(step == blocks // tile - 1)
        def _():
            fetched = total_ref[...].astype(jnp.bfloat16)
            fetched_ref[...] = fetched
            value = inner(fetched, dec_ref[...], 1, 0) + head_ref[2:3, :]
            sigma = sigmoid(value)
            out = value * sigma
            turn_ref[...] = sigma + out * (1.0 - sigma)
            decoded = out.astype(jnp.bfloat16)
            decoded_ref[...] = decoded
            branch_ref[...] = inner(decoded, out_ref[...], 1, 0).astype(jnp.bfloat16)

    whole_rows = pl.BlockSpec((tile, D), lambda i, *_: (i, 0))
    woven = pl.BlockSpec((2 * tile, HALF), lambda i, *_: (i, 0))
    ins = [whole_rows] + [pl.BlockSpec(memory_space=pltpu.VMEM)] * 3
    ins = ins + [whole(mats.shape), woven, whole_rows]
    outs = [whole_rows] * 4 + [pl.BlockSpec((K, 2 * tile, HALF), lambda i, *_: (0, i, 0))]
    shapes = [
        jax.ShapeDtypeStruct((blocks, D), jnp.float32),
        jax.ShapeDtypeStruct((blocks, D), jnp.float32),
        jax.ShapeDtypeStruct((blocks, D), jnp.bfloat16),
        jax.ShapeDtypeStruct((blocks, D), jnp.bfloat16),
        jax.ShapeDtypeStruct((K, 2 * blocks, HALF), jnp.bfloat16),
    ]
    args = [index, mesh, before, own, after, mats, *terms]
    if more:
        ins.append(pl.BlockSpec((1, D, D), lambda *_: (0, 0, 0)))
        outs.append(woven)
        shapes.append(jax.ShapeDtypeStruct((2 * blocks, HALF), jnp.bfloat16))
        args.append(following)
    scratch = []
    if decoder:
        posts = decoder[0].shape[0]
        ins = ins + [whole(arg.shape) for arg in decoder]
        args = args + list(decoder)
        for width, kind in ((HALF, jnp.bfloat16), (D, jnp.bfloat16), (D, jnp.bfloat16), (D, jnp.float32)):
            outs.append(whole((posts, width)))
            shapes.append(jax.ShapeDtypeStruct((posts, width), kind))
        scratch = [pltpu.VMEM((posts, D), jnp.float32)]
    return pl.pallas_call(
        body,
        grid_spec=pltpu.PrefetchScalarGridSpec(
            num_scalar_prefetch=1,
            grid=(blocks // tile,),
            in_specs=ins,
            out_specs=outs,
            scratch_shapes=scratch
            + [
                pltpu.VMEM((reach, HALF), jnp.float32),
                pltpu.VMEM((K * 2 * tile, HALF), jnp.float32),
                pltpu.VMEM((2 * tile, HALF), jnp.float32),
            ],
        ),
        out_shape=shapes,
        compiler_params=pltpu.CompilerParams(vmem_limit_bytes=51 * 2**20),
        cost_estimate=cost(25),
        name="round_forward",
    )(*args)


def edges_backward(index, back, slopes, mats, carried=(), landed=()):
    blocks = back.shape[0]
    tile, chunk = 512, 16
    steps, turns, high = blocks // tile, tile // chunk, 2 * chunk
    reach = 2 * (blocks + 2 * H)

    def body(*refs):
        if carried:
            index_ref, back_ref, slope_ref, mats_ref = refs[:4]
            past, rest = refs[4:9], refs[9:]
            (new_ref, out_ref, sent_ref), rest = rest[:3], rest[3:]
        else:
            index_ref, back_ref, slope_ref, mats_ref = refs[:4]
            (ids_ref, landed_ref, turn_ref, w_out_ref, w_dec_ref), rest = refs[4:9], refs[9:]
            (new_ref, out_ref, gdec_ref), rest = rest[:3], rest[3:]
            gathered, rest = rest[5], rest[:5] + rest[6:]
        guin_ref, low_ref, before_ref, own_ref, after_ref, wide, wider, flows, *tables = rest
        step = pl.program_id(0)

        @pl.when(step == 0)
        def _():
            @pl.loop(0, reach // 256)
            def _(i):
                for table in tables:
                    table[pl.ds(pl.multiple_of(i * 256, 256), 256), :] = jnp.zeros(
                        (256, HALF), jnp.float32
                    )

        if carried:
            new, one, two = ended(*past, wide)
            sent_ref[:, :HALF] = one
            sent_ref[:, HALF:] = two
            new_ref[...] = new
            grad_out = new.astype(jnp.bfloat16)
            out_ref[...] = grad_out
        else:

            @pl.when(step == 0)
            def _():
                grad_dec = inner(landed_ref[...], w_out_ref[...], 1, 1) * turn_ref[...]
                grad_dec = grad_dec.astype(jnp.bfloat16)
                gdec_ref[...] = grad_dec
                gathered[...] = inner(grad_dec, w_dec_ref[...], 1, 1).astype(jnp.bfloat16)

            nodes = lax.broadcasted_iota(jnp.int32, (tile, landed_ref.shape[0]), 0) + step * tile
            chooser = jnp.where(nodes == ids_ref[...], 1.0, 0.0).astype(jnp.bfloat16)
            new = inner(chooser, gathered[...], 1, 0)
            new_ref[...] = new
            grad_out = new.astype(jnp.bfloat16)
            out_ref[...] = grad_out
        grad_uin = (inner(grad_out, mats_ref[4], 1, 1) * back_ref[...]).astype(jnp.bfloat16)
        guin_ref[...] = grad_uin
        weave(wide, inner(grad_uin, mats_ref[2], 1, 1) * (1.0 / K))

        def dense(turn):
            at = pl.multiple_of(turn * high, high)
            grad_agg = wide[pl.ds(at, high), :]
            total, parts = None, []
            for edge in range(K):
                flow = grad_agg * slope_ref[edge, pl.ds(at, high), :].astype(jnp.float32)
                parts.append(flow)
                total = flow if total is None else total + flow
            return at, total, parts

        def keep(turn, at, total, parts):
            for edge in range(K):
                spot = pl.multiple_of(edge * 2 * tile + turn * high, high)
                flows[pl.ds(spot, high), :] = parts[edge]
            wider[pl.ds(at, high), :] = total

        def scatter(turn):
            for u in range(chunk):
                spots, sums = [], []
                for edge in range(K):
                    base = edge * blocks + step * tile + turn * chunk
                    spots.append(pl.multiple_of(index_ref[base + u], 2))
                for edge in range(K):
                    spot = pl.multiple_of(edge * 2 * tile + turn * high + 2 * u, 2)
                    sums.append(tables[edge][pl.ds(spots[edge], 2), :] + flows[pl.ds(spot, 2), :])
                for edge in range(K):
                    tables[edge][pl.ds(spots[edge], 2), :] = sums[edge]

        def some(turn, carry):
            found = dense(turn)
            scatter(turn - 1)
            keep(turn, *found)
            return carry

        keep(0, *dense(0))
        lax.fori_loop(1, turns, some, 0)
        scatter(turns - 1)
        first, second = unweave(wider)
        low_ref[:, :HALF] = first.astype(jnp.bfloat16)
        low_ref[:, HALF:] = second.astype(jnp.bfloat16)

        @pl.when(step == steps - 1)
        def _():
            def summed(at):
                value = tables[0][pl.ds(at, 256), :]
                for table in tables[1:]:
                    value = value + table[pl.ds(at, 256), :]
                return value

            @pl.loop(0, 2 * H // 256)
            def _(i):
                at = pl.multiple_of(i * 256, 256)
                far = pl.multiple_of(2 * H + 2 * blocks + at, 256)
                before_ref[pl.ds(at, 256), :] = summed(at).astype(jnp.bfloat16)
                after_ref[pl.ds(at, 256), :] = summed(far).astype(jnp.bfloat16)

            @pl.loop(0, 2 * blocks // 256)
            def _(i):
                at = pl.multiple_of(i * 256, 256)
                own_ref[pl.ds(at, 256), :] = summed(pl.multiple_of(2 * H + at, 256))

    rows = pl.BlockSpec((tile, D), lambda i, *_: (i, 0))
    woven = pl.BlockSpec((2 * tile, HALF), lambda i, *_: (i, 0))
    low = jax.ShapeDtypeStruct((blocks, D), jnp.bfloat16)
    low_posts = (landed[1].shape[0], D) if landed else None
    last = low if carried else jax.ShapeDtypeStruct(low_posts, jnp.bfloat16)
    return pl.pallas_call(
        body,
        grid_spec=pltpu.PrefetchScalarGridSpec(
            num_scalar_prefetch=1,
            grid=(steps,),
            in_specs=[
                rows,
                pl.BlockSpec((K, 2 * tile, HALF), lambda i, *_: (0, i, 0)),
                whole(mats.shape),
            ]
            + ([rows] + [woven] * 3 + [whole(mats.shape)] if carried else [])
            + [whole(arg.shape) for arg in landed],
            out_specs=([rows] * 3 if carried else [rows, rows, whole(low_posts)])
            + [
                rows, rows,
                whole((2 * H, HALF)), whole((2 * blocks, HALF)), whole((2 * H, HALF)),
            ],
            scratch_shapes=([] if carried else [pltpu.VMEM(low_posts, jnp.bfloat16)])
            + [
                pltpu.VMEM((2 * tile, HALF), jnp.float32),
                pltpu.VMEM((2 * tile, HALF), jnp.float32),
                pltpu.VMEM((2 * tile * K, HALF), jnp.float32),
            ]
            + [pltpu.VMEM((reach, HALF), jnp.float32)] * K,
        ),
        out_shape=[
            jax.ShapeDtypeStruct((blocks, D), jnp.float32),
            low,
            last,
            low,
            low,
            jax.ShapeDtypeStruct((2 * H, HALF), jnp.bfloat16),
            jax.ShapeDtypeStruct((2 * blocks, HALF), jnp.float32),
            jax.ShapeDtypeStruct((2 * H, HALF), jnp.bfloat16),
        ],
        compiler_params=LIMIT,
        cost_estimate=cost(28 if carried else 25),
        name="edges_backward",
    )(index, back, slopes, mats, *carried, *landed)


def ended(part_ref, own_ref, first_ref, last_ref, mats_ref, wide):
    wide[...] = (
        own_ref[...] + first_ref[...].astype(jnp.float32) + last_ref[...].astype(jnp.float32)
    )
    one, two = unweave(wide)
    one, two = one.astype(jnp.bfloat16), two.astype(jnp.bfloat16)
    new = (
        part_ref[...]
        + inner(one, mats_ref[0, :, :HALF], 1, 1)
        + inner(two, mats_ref[0, :, HALF:], 1, 1)
    )
    return new, one, two


def carried_terms(grad_mesh, grad_uin, dest_low, mats):
    blocks = grad_mesh.shape[0]
    tile = 1024

    def body(grad_ref, guin_ref, dest_ref, mats_ref, part_ref):
        part_ref[...] = (
            grad_ref[...]
            + inner(guin_ref[...], mats_ref[3], 1, 1)
            + inner(dest_ref[...], mats_ref[1], 1, 1)
        )

    rows = pl.BlockSpec((tile, D), lambda i: (i, 0))
    return pl.pallas_call(
        body,
        grid=(blocks // tile,),
        in_specs=[rows, rows, rows, whole(mats.shape)],
        out_specs=rows,
        out_shape=jax.ShapeDtypeStruct((blocks, D), jnp.float32),
        compiler_params=LIMIT,
        cost_estimate=cost(4),
        name="carried_terms",
    )(grad_mesh, grad_uin, dest_low, mats)


def encode_rows(arrived, w_in, w_node, biases, source):
    posts = arrived.shape[0]
    tile = 512

    def body(
        arrived_ref, in_ref, node_ref, bias_ref, source_ref,
        mesh_ref, gathered_ref, sent_ref, ids_ref, down_ref, encoded, wide,
    ):
        step = pl.program_id(0)

        @pl.when(step == 0)
        def _():
            entering = inner(arrived_ref[...], in_ref[...], 1, 0) + bias_ref[0:1, :]
            encoded[...] = silu(entering).astype(jnp.bfloat16)
            ids_ref[...] = ids_along(arrived_ref[...])
            down_ref[...] = ids_down(arrived_ref[...])

        nodes = lax.broadcasted_iota(jnp.int32, (tile, posts), 0) + step * tile
        chooser = jnp.where(nodes == ids_ref[...], 1.0, 0.0).astype(jnp.bfloat16)
        gathered = inner(chooser, encoded[...], 1, 0).astype(jnp.bfloat16)
        gathered_ref[...] = gathered
        mesh = silu(inner(gathered, node_ref[...], 1, 0) + bias_ref[1:2, :])
        mesh_ref[...] = mesh
        weave(wide, inner(mesh.astype(jnp.bfloat16), source_ref[0], 1, 0))
        sent_ref[...] = wide[...].astype(jnp.bfloat16)

    rows = pl.BlockSpec((tile, D), lambda i: (i, 0))
    args = (arrived, w_in, w_node, biases, source)
    return pl.pallas_call(
        body,
        grid=(H // tile,),
        in_specs=[whole(arg.shape) for arg in args[:-1]]
        + [pl.BlockSpec((1, D, D), lambda *_: (0, 0, 0))],
        out_specs=[rows, rows, pl.BlockSpec((2 * tile, HALF), lambda i: (i, 0))]
        + [whole((1, posts)), whole((posts, 1))],
        out_shape=[
            jax.ShapeDtypeStruct((H, D), jnp.float32),
            jax.ShapeDtypeStruct((H, D), jnp.bfloat16),
            jax.ShapeDtypeStruct((2 * H, HALF), jnp.bfloat16),
            jax.ShapeDtypeStruct((1, posts), jnp.int32),
            jax.ShapeDtypeStruct((posts, 1), jnp.int32),
        ],
        scratch_shapes=[pltpu.VMEM((posts, D), jnp.bfloat16), pltpu.VMEM((2 * tile, HALF), jnp.float32)],
        compiler_params=LIMIT,
        cost_estimate=cost(5),
        name="encode_rows",
    )(*args)


def encode_backward(carried, mesh, gathered, arrived, ids, w_in, w_node, biases):
    blocks = mesh.shape[0]
    posts = arrived.shape[0]
    tile = 512
    steps = blocks // tile

    def body(
        part_ref, own_ref, first_ref, last_ref, mats_ref,
        mesh_ref, gathered_ref, arrived_ref, ids_ref, in_ref, node_ref, bias_ref,
        new_ref, out_ref, gin_ref, gnode_ref, gbias_ref, gsource_ref, total, wide,
    ):
        step = pl.program_id(0)

        @pl.when(step == 0)
        def _():
            for ref in (total, gnode_ref, gbias_ref, gsource_ref):
                ref[...] = jnp.zeros(ref.shape, jnp.float32)

        new, one, two = ended(part_ref, own_ref, first_ref, last_ref, mats_ref, wide)
        new_ref[...] = new
        out_ref[...] = new.astype(jnp.bfloat16)
        lowered = mesh_ref[...].astype(jnp.bfloat16)
        gsource_ref[:, :HALF] += inner(lowered, one, 0, 0)
        gsource_ref[:, HALF:] += inner(lowered, two, 0, 0)
        node_in = inner(gathered_ref[...], node_ref[...], 1, 0) + bias_ref[1:2, :]
        grad_node = (new * slope(node_in)).astype(jnp.bfloat16)
        gbias_ref[1:2, :] += jnp.sum(grad_node.astype(jnp.float32), 0, keepdims=True)
        gnode_ref[...] += inner(gathered_ref[...], grad_node, 0, 0)
        back = inner(grad_node, node_ref[...], 1, 1).astype(jnp.bfloat16)
        nodes = lax.broadcasted_iota(jnp.int32, (posts, tile), 1) + step * tile
        chooser = jnp.where(nodes == ids_ref[...], 1.0, 0.0).astype(jnp.bfloat16)
        total[...] += inner(chooser, back, 1, 0)

        @pl.when(step == steps - 1)
        def _():
            entering = inner(arrived_ref[...], in_ref[...], 1, 0) + bias_ref[0:1, :]
            grad_enc = (total[...] * slope(entering)).astype(jnp.bfloat16)
            gbias_ref[0:1, :] = jnp.sum(grad_enc.astype(jnp.float32), 0, keepdims=True)
            gin_ref[...] = inner(arrived_ref[...], grad_enc, 0, 0)

    rows = pl.BlockSpec((tile, D), lambda i: (i, 0))
    woven = pl.BlockSpec((2 * tile, HALF), lambda i: (i, 0))
    args = (arrived, ids, w_in, w_node, biases)
    shapes = [(HALF, D), (D, D), (2, D), (D, D)]
    return pl.pallas_call(
        body,
        grid=(steps,),
        in_specs=[rows] + [woven] * 3 + [whole(carried[4].shape), rows, rows]
        + [whole(arg.shape) for arg in args],
        out_specs=[rows, rows] + [whole(shape) for shape in shapes],
        out_shape=[
            jax.ShapeDtypeStruct((blocks, D), jnp.float32),
            jax.ShapeDtypeStruct((blocks, D), jnp.bfloat16),
        ]
        + [jax.ShapeDtypeStruct(shape, jnp.float32) for shape in shapes],
        scratch_shapes=[pltpu.VMEM((posts, D), jnp.float32), pltpu.VMEM((2 * tile, HALF), jnp.float32)],
        compiler_params=LIMIT,
        cost_estimate=cost(10),
        name="encode_backward",
    )(*carried, mesh, gathered, *args)


def shards(walk, master, moment1, moment2, inputs, targets, valid, owner, slot, neighbours, partner):
    bands = lax.axis_size("space")
    band = lax.axis_index("space")
    peers = lax.axis_size(ALL)
    place = lax.axis_index(ALL)
    shard = master.shape[0]
    total_size = shard * peers
    height = pieces_of(total_size, peers)[3]
    offset = lax.rem(lax.rem(shard, D) * place, D)
    piece = lax.dynamic_update_slice_in_dim(
        jnp.zeros((height * D,), jnp.bfloat16), master.astype(jnp.bfloat16), offset, 0
    )
    state_in = inputs[0]
    counted = valid[0].astype(jnp.float32)
    local_count = jnp.sum(valid[0])
    digits = (local_count >> jnp.array([16, 8, 0], jnp.int32)) & 255
    digits = jnp.pad(digits, (CH + 3, HALF - CH - 6)).astype(jnp.float32)[None, :]
    points = state_in.shape[1]
    blocks = neighbours.shape[0]
    assert blocks == H
    capacity = max(2, 2 * points // bands)
    target_band = owner[0, :, 0]
    hits = (target_band[:, None] == jnp.arange(bands, dtype=jnp.int32)[None, :]).astype(jnp.int32)
    ranks = jnp.sum(jnp.cumsum(hits, 0) * hits, 1) - 1
    places_out = jnp.sum(hits * jnp.asarray(walk, jnp.int32)[None, :], 1) * capacity + ranks
    poster = (
        jnp.arange(bands * capacity, dtype=jnp.int32)[:, None] == places_out[None, :]
    ).astype(jnp.bfloat16)
    spots = slot[0][None, :]
    columns = jnp.concatenate(
        [
            state_in,
            (spots // 64).astype(jnp.bfloat16),
            (spots % 64).astype(jnp.bfloat16),
            jnp.ones((1, points), jnp.bfloat16),
            jnp.zeros((HALF - CH - 3, points), jnp.bfloat16),
        ],
        0,
    )

    def exchanged(rows):
        return lax.all_to_all(
            rows.reshape(bands, capacity, HALF), "space", split_axis=0, concat_axis=0, tiled=True
        ).reshape(bands * capacity, HALF)

    held, posted = gathered_blocks(
        piece.reshape(height, D), (inner(poster, columns, 1, 1) + digits).astype(jnp.bfloat16)
    )
    arrived = exchanged(posted)
    w_in, w_node, w_dec, w_out, *w_round, biases = spread_rows(
        held, total_size, peers, place
    )
    arrived, biases = lax.optimization_barrier((arrived, biases))
    counts = arrived.reshape(bands, capacity, HALF)[:, 0, CH + 3 : CH + 6].astype(jnp.float32)
    counts = jnp.sum(counts, 0, keepdims=True)
    w_out = jnp.pad(w_out.reshape(D, CH), ((0, 0), (0, HALF - CH)))
    w_round = [mats.reshape(5, D, D) for mats in w_round]
    b_head = biases[:3]
    b_round = biases[3:].reshape(ROUNDS, 2, D)
    mesh, gathered, sent, ids_row, ids = encode_rows(
        arrived, w_in, w_node, biases, w_round[0]
    )
    sent, partner, neighbours, counted, counts = lax.optimization_barrier(
        (sent, partner, neighbours, counted, counts)
    )
    counts = counts + swapped(counts, "dp", 1)
    index = 2 * ((neighbours - band * blocks + H) % (blocks * bands)).T.reshape(-1)
    moved = [(n, place) for n, place in enumerate(walk) if n != place]
    stays = jnp.asarray([n == place for n, place in enumerate(walk)])[band]
    index = lax.ppermute(index, "space", list(enumerate(walk)))

    def at_home(rows):
        return lax.ppermute(rows, "space", [(j, i) for i, j in moved])

    def settled(own, came):
        return jnp.where(stays, own, came.astype(jnp.float32))

    partner_by = partner - band * points - jnp.arange(points, dtype=jnp.int32)
    coded = jnp.where(partner_by >= NEAR, partner_by - NEAR + 1, 0).astype(jnp.bfloat16)
    low_valid = jnp.concatenate([counted.astype(jnp.bfloat16), coded[None, :]], 0)
    valid_around = jnp.concatenate(
        [
            shifted(low_valid[:, points - ROWW :], "space", 1),
            low_valid,
            shifted(low_valid[:, :ROWW], "space", -1),
        ],
        1,
    )
    kept = []
    for layer in range(ROUNDS):
        before, after = halo(walk, sent, sent)
        terms = node_terms(mesh, w_round[layer], b_round[layer])
        if layer == 0:
            before, valid_around, counts = lax.optimization_barrier((before, valid_around, counts))
        following = w_round[layer + 1] if layer + 1 < ROUNDS else None
        new, back, update, agg, slopes, *rest = round_forward(
            index, mesh, before, sent, after, w_round[layer], terms, following,
            () if following is not None else (ids, w_dec, w_out, biases),
        )
        kept.append((mesh, back, update, agg, slopes))
        mesh = new
        sent = rest[0]
    count = counts[0, 0] * 65536.0 + counts[0, 1] * 256.0 + counts[0, 2]
    wide_valid = valid_around[:CH].astype(jnp.float32)
    coded = valid_around[CH : CH + 1, : points + ROWW].astype(jnp.float32)
    weights = [
        (
            by,
            jnp.where(coded == by - NEAR + 1, 1.0, 0.0)
            * wide_valid[:, : points + ROWW]
            * wide_valid[:, by : by + points + ROWW],
        )
        for by in range(NEAR, ROWW + 1)
    ]
    branch_rows, fetched, decoded, dec_turn = rest
    returned = exchanged(branch_rows)
    branch = inner(returned, poster, 0, 0)[:CH]
    err = state_in.astype(jnp.float32) + branch - targets[0].astype(jnp.float32)
    def widened(values):
        low = values.astype(jnp.bfloat16)
        before = shifted(low[:, points - ROWW :], "space", 1).astype(jnp.float32)
        after = shifted(low[:, :ROWW], "space", -1).astype(jnp.float32)
        return jnp.concatenate([before, values, after], 1)

    wide_err = widened(err)
    paired = jnp.zeros((CH, points + ROWW), jnp.float32)
    pair_total = jnp.zeros((CH, points), jnp.float32)
    for by, both in weights:
        gap = both * (wide_err[:, : points + ROWW] - wide_err[:, by : by + points + ROWW])
        paired = paired + gap
        pair_total = pair_total + gap[:, ROWW:] * (
            wide_err[:, ROWW : ROWW + points] - wide_err[:, ROWW + by : ROWW + by + points]
        )
    local_total = jnp.sum(counted * err * err) + 0.5 * jnp.sum(pair_total)
    grad_pred = 2.0 * counted * err + paired[:, ROWW:]
    for by, both in weights:
        gap = both * (wide_err[:, : points + ROWW] - wide_err[:, by : by + points + ROWW])
        grad_pred = grad_pred - gap[:, ROWW - by : ROWW - by + points]
    grad_pred = grad_pred / count
    grad_rows = jnp.pad(grad_pred.astype(jnp.bfloat16), ((0, HALF - CH), (0, 0)))
    landed = exchanged(inner(poster, grad_rows, 1, 1).astype(jnp.bfloat16))
    landed, final_mesh = lax.optimization_barrier((landed, mesh.astype(jnp.bfloat16)))
    final_mesh = at_home(final_mesh)
    mats_grads = [None] * (5 * ROUNDS)
    bias_grads = [None] * (2 * ROUNDS)
    carried, grad_mesh = (), None
    for layer in reversed(range(ROUNDS)):
        old, back, update, agg, slopes = kept[layer]
        first_step = not carried
        grad_mesh, leaving, extra, grad_uin, dest_low, to_before, own, to_after = edges_backward(
            index, back, slopes, w_round[layer], carried,
            (ids_row, landed, dec_turn, w_out, w_dec) if first_step else (),
        )
        if not first_step:
            mats_grads[5 * layer + 5] = inner(
                kept[layer + 1][0].astype(jnp.bfloat16), extra, 0, 0
            )
        else:
            grad_wout = inner(decoded, landed, 0, 0)[:, :CH]
            grad_bdec = jnp.sum(extra.astype(jnp.float32), 0, keepdims=True)
            grad_wdec = inner(fetched, extra, 0, 0)
            to_before, to_after, final_mesh = lax.optimization_barrier(
                (to_before, to_after, final_mesh)
            )
        from_before, from_after = halo(walk, to_after, to_before)
        if first_step:
            from_before, final_mesh = lax.optimization_barrier(
                (from_before, settled(mesh, final_mesh))
            )
        lowered = old.astype(jnp.bfloat16)
        mats_grads[5 * layer + 1 : 5 * layer + 5] = [
            inner(lowered, dest_low, 0, 0),
            inner(agg, grad_uin, 0, 0),
            inner(lowered, grad_uin, 0, 0),
            inner(update, leaving, 0, 0),
        ]
        bias_grads[2 * layer] = jnp.sum(dest_low.astype(jnp.float32), 0, keepdims=True)
        bias_grads[2 * layer + 1] = jnp.sum(grad_uin.astype(jnp.float32), 0, keepdims=True)
        part = carried_terms(grad_mesh, grad_uin, dest_low, w_round[layer])
        carried = (part, own, from_before, from_after, w_round[layer])
    grad_mesh, leaving, grad_win, grad_wnode, grad_bpair, mats_grads[0] = encode_backward(
        carried, kept[0][0], gathered, arrived, ids, w_in, w_node, biases
    )
    parts = [grad_win, grad_wnode, grad_wdec, grad_wout.reshape(CH, D)]
    parts = parts + mats_grads
    parts = parts + [grad_bpair, grad_bdec] + bias_grads
    keep, send = collect_rows(parts, total_size, peers, place)
    mine, leaving = reduced_piece(keep, send, leaving)
    late = at_home(leaving)
    mine = lax.dynamic_slice_in_dim(mine.reshape(-1), offset, shard)
    lane = lax.broadcasted_iota(jnp.int32, (8, HALF), 1)
    sums, late = summed_everywhere(
        jnp.where(lane == 0, local_total, jnp.sum(mine * mine)), late
    )
    total, norm = sums[0, 0], jnp.sqrt(sums[0, 1])
    node_grads = settled(grad_mesh, late)
    clipped = mine * jnp.minimum(1.0, 0.05 / norm)
    first = 0.9 * moment1 + 0.1 * clipped
    second = 0.999 * moment2 + 0.001 * clipped * clipped
    first_hat = first / (1.0 - 0.9**STEP)
    second_hat = second / (1.0 - 0.999**STEP)
    updated = master - 0.1 * (first_hat / (jnp.sqrt(second_hat) + 1e-08) + 0.1 * master)
    return (
        total.reshape(1),
        count.reshape(1),
        norm.reshape(1),
        updated,
        first,
        second,
        updated.astype(jnp.bfloat16),
        final_mesh.reshape(1, blocks, D),
        node_grads.reshape(1, blocks, D),
        grad_pred.reshape(1, grad_pred.shape[0], points),
    )


def solution(mesh):
    return jax.shard_map(
        functools.partial(shards, walk_of(mesh)),
        mesh=mesh,
        in_specs=(
            P(("dp", "space")),
            P(("dp", "space")),
            P(("dp", "space")),
            P("dp", None, "space"),
            P("dp", None, "space"),
            P("dp", None, "space"),
            P("dp", "space", None),
            P("dp", "space"),
            P("space", None),
            P("space"),
        ),
        out_specs=(
            P(),
            P(),
            P(),
            P(("dp", "space")),
            P(("dp", "space")),
            P(("dp", "space")),
            P(("dp", "space")),
            P("dp", "space", None),
            P("dp", "space", None),
            P("dp", None, "space"),
        ),
        check_vma=False,
    )
```

```python
import functools

import jax
import jax.numpy as jnp
from jax import lax
from jax.experimental import pallas as pl
from jax.experimental.pallas import tpu as pltpu
from jax.sharding import PartitionSpec as P

D = 256
HALF = 128
CH = 78
ROUNDS = 3
K = 6
ROWW = 360
NEAR = 358
STEP = 10
H = 2048
ALL = ("dp", "space")
LIMIT = pltpu.CompilerParams(vmem_limit_bytes=60 * 2**20)


def cost(micros):
    return pl.CostEstimate(flops=0, bytes_accessed=micros * 3_000_000, transcendentals=0)


def inner(left, right, left_dim, right_dim):
    return lax.dot_general(
        left, right, (((left_dim,), (right_dim,)), ((), ())), preferred_element_type=jnp.float32
    )


def sigmoid(value):
    return 0.5 * jnp.tanh(0.5 * value) + 0.5


def silu(value):
    return value * sigmoid(value)


def slope(value):
    sigma = sigmoid(value)
    return sigma * (1.0 + value * (1.0 - sigma))


def shifted(shard, axis, by):
    peers = lax.axis_size(axis)
    pairs = [(i, i + by) for i in range(peers) if 0 <= i + by < peers]
    return lax.ppermute(shard, axis, pairs)


def walk_of(mesh):
    count = mesh.shape["space"]
    chips = [getattr(device, "coords", None) for device in mesh.devices[0].reshape(-1)]
    if any(chip is None for chip in chips) or len(set(map(tuple, chips))) != count:
        return list(range(count))
    at = {tuple(chip): n for n, chip in enumerate(chips)}
    xs, ys, zs = (sorted({chip[n] for chip in at}) for n in range(3))
    if len(xs) * len(ys) * len(zs) != count:
        return list(range(count))
    if (len(xs), len(ys), len(zs)) == (2, 2, 4):
        corners = [(0, 0), (1, 0), (0, 1), (1, 1)]
        planes = [(0, 1, 3, 2), (2, 0, 1, 3), (3, 1, 0, 2), (2, 3, 1, 0)]
        steps = [(*corners[n], z) for z, plane in enumerate(planes) for n in plane]
        return [at[(xs[x], ys[y], zs[z])] for x, y, z in steps]
    walk, plane = [], []
    for n, y in enumerate(ys):
        plane = plane + [(x, y) for x in (xs if n % 2 == 0 else xs[::-1])]
    for n, z in enumerate(zs):
        walk = walk + [at[(x, y, z)] for x, y in (plane if n % 2 == 0 else plane[::-1])]
    return walk


def halo(walk, last, initial):
    up = list(zip(walk, walk[1:] + walk[:1]))
    down = [(j, i) for i, j in up]
    return lax.ppermute(last, "space", up), lax.ppermute(initial, "space", down)


def pieces_of(total, peers):
    share = total // peers
    starts = [share * d // D for d in range(peers)]
    counts = [-(-share * (d + 1) // D) - starts[d] for d in range(peers)]
    shared = [share * d % D != 0 for d in range(peers)]
    height = -(-max(counts) // 16) * 16
    return starts, counts, shared, height


def parts_of():
    return [CH, D, D, CH] + [5 * D] * ROUNDS + [3 + 2 * ROUNDS]


def swapped(value, axis, bit):
    return lax.ppermute(value, axis, [(i, i ^ bit) for i in range(lax.axis_size(axis))])


def bits_of(axis):
    return [1 << n for n in range(lax.axis_size(axis).bit_length() - 1)]


def others(value, axis, bits):
    masks = [sum(bit for n, bit in enumerate(bits) if m >> n & 1) for m in range(1, 1 << len(bits))]
    return [swapped(value, axis, mask) for mask in masks]


def upper_groups():
    bits = bits_of("space")[2:]
    return [tuple(bits[n : n + 2]) for n in range(0, len(bits), 2)]


def orders():
    return [(1, 2), (2, 1)]


def summed_everywhere(value, arriving):
    for bits in reversed(upper_groups()):
        value = sum(others(value, "space", bits), value)
    value = value + swapped(value, "dp", 1)
    value, arriving = lax.optimization_barrier((value, arriving))
    return sum(others(value, "space", (1, 2)), value), arriving


def gathered_blocks(piece, posted):
    held, weights, size = piece[None], {}, 1
    for bits in reversed(upper_groups()):
        held = jnp.concatenate([held] + others(held, "space", bits), 0)
        for n, bit in enumerate(bits):
            weights[bit] = size << n
        size = size << len(bits)
    half = piece.shape[0] // 2
    held = [held[:, :half], held[:, half:]]
    ranks = [dict(weights), dict(weights)]
    for turn in (1, 0):
        if turn == 0:
            held[0], held[1], posted = lax.optimization_barrier((*held, posted))
        for n, order in enumerate(orders()):
            held[n] = jnp.concatenate([held[n], swapped(held[n], "space", order[turn])], 0)
            ranks[n][order[turn]] = size
        size = size << 1
    return (held, [swapped(part, "dp", 1) for part in held], ranks), posted


def spread_rows(gathered, total, peers, place):
    (first, second), (first_far, second_far), ranks = gathered
    starts, counts, shared, height = pieces_of(total, peers)
    half, group = height // 2, first.shape[0]
    rows = -(-total // D)
    sizes = parts_of()
    def at(rank, relative):
        spot = 0
        for bit, weight in rank.items():
            spot = spot + jnp.where((relative & bit) != 0, weight, 0)
        return spot

    def body(place_ref, *refs):
        sources, outs, buffer = refs[:4], refs[4:-1], refs[-1]
        me = place_ref[0]
        mine = me // group
        for d in range(peers):
            relative = (me ^ d) & (group - 1)
            spots = [at(rank, relative) for rank in ranks]

            def lay(one, two, d=d, spots=spots):
                piece = jnp.concatenate([one[spots[0]], two[spots[1]]], 0).astype(jnp.float32)
                start, count = starts[d], counts[d]
                if shared[d]:
                    buffer[start : start + 1, :] = buffer[start : start + 1, :] + piece[:1]
                    buffer[start + 1 : start + count, :] = piece[1:count]
                else:
                    buffer[start : start + count, :] = piece[:count]

            @pl.when(mine == d // group)
            def _():
                lay(sources[0], sources[1])

            @pl.when(mine != d // group)
            def _():
                lay(sources[2], sources[3])

        start = 0
        for out, size in zip(outs, sizes):
            out[:size, :] = buffer[start : start + size, :].astype(out.dtype)
            if out.shape[0] > size:
                out[size:, :] = jnp.zeros((out.shape[0] - size, D), out.dtype)
            start = start + size

    kinds = [jnp.bfloat16] * (4 + ROUNDS) + [jnp.float32]
    talls = [HALF] + sizes[1:]
    return pl.pallas_call(
        body,
        grid_spec=pltpu.PrefetchScalarGridSpec(
            num_scalar_prefetch=1,
            grid=(1,),
            in_specs=[whole(first.shape)] * 4,
            out_specs=[whole((tall, D)) for tall in talls],
            scratch_shapes=[pltpu.VMEM((-(-rows // 8) * 8 + 8, D), jnp.float32)],
        ),
        out_shape=[jax.ShapeDtypeStruct((tall, D), kind) for tall, kind in zip(talls, kinds)],
        compiler_params=LIMIT,
        cost_estimate=cost(4),
        name="spread_rows",
    )(place.reshape(1), first, second, first_far, second_far)


def collect_rows(parts, total, peers, place):
    starts, counts, shared, height = pieces_of(total, peers)
    rows = -(-total // D)
    sizes = [min(part.shape[0], size) for part, size in zip(parts, tall_parts())]
    group = lax.axis_size("space")

    def body(place_ref, *refs):
        sources, keep, send, buffer = refs[:-3], refs[-3], refs[-2], refs[-1]
        start = 0
        for source, size in zip(sources, sizes):
            buffer[start : start + size, :] = source[:size, :]
            start = start + size
        if buffer.shape[0] > start:
            buffer[start:, :] = jnp.zeros((buffer.shape[0] - start, D), jnp.float32)
        me = place_ref[0]
        mine = me // group
        for d in range(peers):
            relative = (me ^ d) & (group - 1)

            @pl.when(mine == d // group)
            def _():
                keep[relative] = buffer[starts[d] : starts[d] + height, :]

            @pl.when(mine != d // group)
            def _():
                send[relative] = buffer[starts[d] : starts[d] + height, :].astype(jnp.bfloat16)

    shape = (group, height, D)
    return pl.pallas_call(
        body,
        grid_spec=pltpu.PrefetchScalarGridSpec(
            num_scalar_prefetch=1,
            grid=(1,),
            in_specs=[whole(part.shape) for part in parts],
            out_specs=[whole(shape), whole(shape)],
            scratch_shapes=[pltpu.VMEM((-(-rows // 8) * 8 + height + 8, D), jnp.float32)],
        ),
        out_shape=[
            jax.ShapeDtypeStruct(shape, jnp.float32),
            jax.ShapeDtypeStruct(shape, jnp.bfloat16),
        ],
        compiler_params=LIMIT,
        cost_estimate=cost(5),
        name="collect_rows",
    )(place.reshape(1), *parts)


def reduced_piece(keep, send, leaving):
    kept = keep + swapped(send, "dp", 1).astype(jnp.float32)
    half = kept.shape[1] // 2
    groups = upper_groups()
    inner_shape = (kept.shape[0] // 4, 2, 2, half, D)
    parts = [kept[:, :half].reshape(inner_shape), kept[:, half:].reshape(inner_shape)]
    for n, order in enumerate(orders()):
        for bit in order:
            spot = 2 if bit == 1 and parts[n].ndim == 5 else 1
            stay = lax.index_in_dim(parts[n], 0, spot, keepdims=False)
            leave = lax.index_in_dim(parts[n], 1, spot, keepdims=False)
            parts[n] = stay + swapped(leave.astype(jnp.bfloat16), "space", bit).astype(jnp.float32)
    part = jnp.concatenate(parts, 1)
    part, leaving = lax.optimization_barrier((part, leaving))
    for bits in groups:
        part = part.reshape((-1, 1 << len(bits)) + part.shape[1:])
        masks = [sum(bit for n, bit in enumerate(bits) if m >> n & 1) for m in range(1 << len(bits))]
        low = part.astype(jnp.bfloat16)
        part = sum(
            [
                swapped(low[:, m], "space", mask).astype(jnp.float32)
                for m, mask in enumerate(masks)
                if m
            ],
            part[:, 0],
        )
    return part[0], leaving


def tall_parts():
    return [CH, D, D, CH] + [D] * (5 * ROUNDS) + [2] + [1] * (1 + 2 * ROUNDS)


def weave(ref, value):
    rows = value.shape[0]
    ref[pl.ds(0, rows, stride=2), :] = value[:, :HALF]
    ref[pl.ds(1, rows, stride=2), :] = value[:, HALF:]


def unweave(ref):
    rows = ref.shape[0] // 2
    return ref[pl.ds(0, rows, stride=2), :], ref[pl.ds(1, rows, stride=2), :]


def selector():
    row = lax.broadcasted_iota(jnp.int32, (8, HALF), 0)
    lane = lax.broadcasted_iota(jnp.int32, (8, HALF), 1)
    slot = jnp.where(lane == CH, 64.0, jnp.where(lane == CH + 1, 1.0, 0.0))
    known = jnp.where(lane == CH + 2, 1.0, 0.0)
    return jnp.where(row == 0, slot, jnp.where(row == 1, known, 0.0)).astype(jnp.bfloat16)


def ids_along(arrived):
    codes = inner(selector(), arrived, 1, 1)
    return jnp.where(codes[1:2, :] > 0, codes[0:1, :], -1.0).astype(jnp.int32)


def ids_down(arrived):
    codes = inner(arrived, selector(), 1, 1)
    return jnp.where(codes[:, 1:2] > 0, codes[:, 0:1], -1.0).astype(jnp.int32)


def whole(shape):
    return pl.BlockSpec(shape, lambda *_: (0,) * len(shape))


def node_terms(mesh, mats, bias):
    blocks = mesh.shape[0]
    tile = 1024

    def body(mesh_ref, mats_ref, bias_ref, dest_ref, self_ref):
        lowered = mesh_ref[...].astype(jnp.bfloat16)
        weave(dest_ref, inner(lowered, mats_ref[1], 1, 0) + bias_ref[0:1, :])
        self_ref[...] = inner(lowered, mats_ref[3], 1, 0) + bias_ref[1:2, :]

    rows = pl.BlockSpec((tile, D), lambda i: (i, 0))
    woven = pl.BlockSpec((2 * tile, HALF), lambda i: (i, 0))
    return pl.pallas_call(
        body,
        grid=(blocks // tile,),
        in_specs=[rows, whole(mats.shape), whole(bias.shape)],
        out_specs=[woven, rows],
        out_shape=[
            jax.ShapeDtypeStruct((2 * blocks, HALF), jnp.float32),
            jax.ShapeDtypeStruct((blocks, D), jnp.float32),
        ],
        compiler_params=LIMIT,
        cost_estimate=cost(4),
        name="node_terms",
    )(mesh, mats, bias)


def round_forward(index, mesh, pieces, mats, terms, following, decoder=(), half=None, into=()):
    blocks = mesh.shape[0]
    tile, chunk = 512, 16
    turns, high = tile // chunk, 2 * chunk
    more = following is not None
    reach = 2 * (blocks + 2 * H)
    steps = blocks // tile if half is None else blocks // tile // 2
    shift = 0 if half is None else half * steps

    def body(index_ref, mesh_ref, *refs):
        sources, refs = refs[: len(pieces)], refs[len(pieces) :]
        (mats_ref, dest_ref, self_ref), refs = refs[:3], refs[3:]
        table, rows, wide = refs[-3:]
        if more:
            next_ref, refs = refs[0], refs[1 + len(into) :]
            new_ref, back_ref, update_ref, agg_ref, slope_ref, sent_ref = refs[:6]
        else:
            ids_ref, dec_ref, out_ref, head_ref = refs[:4]
            new_ref, back_ref, update_ref, agg_ref, slope_ref = refs[4:9]
            branch_ref, fetched_ref, decoded_ref, turn_ref, total_ref = refs[9:14]
        step = pl.program_id(0)

        @pl.when(step == 0)
        def _():
            for source, (_, start) in zip(sources, pieces):

                @pl.loop(0, source.shape[0] // 256)
                def _(i, source=source, start=start):
                    at = pl.multiple_of(i * 256, 256)
                    to = pl.multiple_of(start + at, 256)
                    table[pl.ds(to, 256), :] = source[pl.ds(at, 256), :].astype(jnp.float32)

        mesh_in = mesh_ref[...]

        def fetch(turn):
            for edge in range(K):
                base = edge * blocks + (step + shift) * tile + turn * chunk
                spots = [index_ref[base + u] for u in range(chunk)]
                values = [table[pl.ds(pl.multiple_of(spot, 2), 2), :] for spot in spots]
                for u in range(chunk):
                    spot = pl.multiple_of(edge * 2 * tile + turn * high + 2 * u, 2)
                    rows[pl.ds(spot, 2), :] = values[u]

        def load(turn):
            at = pl.multiple_of(turn * high, high)
            taken = [
                rows[pl.ds(pl.multiple_of(edge * 2 * tile + turn * high, high), high), :]
                for edge in range(K)
            ]
            return at, dest_ref[pl.ds(at, high), :], taken

        def dense(at, dest, taken):
            total = None
            for edge in range(K):
                value = taken[edge] + dest
                sigma = sigmoid(value)
                out = value * sigma
                slope_ref[edge, pl.ds(at, high), :] = (sigma + out * (1.0 - sigma)).astype(
                    jnp.bfloat16
                )
                total = out if total is None else total + out
            wide[pl.ds(at, high), :] = total * (1.0 / K)

        def some(turn, carry):
            loaded = load(turn - 1)
            fetch(turn)
            dense(*loaded)
            return carry

        fetch(0)
        lax.fori_loop(1, turns, some, 0)
        dense(*load(turns - 1))
        first, second = unweave(wide)
        first, second = first.astype(jnp.bfloat16), second.astype(jnp.bfloat16)
        agg_ref[:, :HALF] = first
        agg_ref[:, HALF:] = second
        update_in = (
            inner(first, mats_ref[2, :HALF, :], 1, 0)
            + inner(second, mats_ref[2, HALF:, :], 1, 0)
            + self_ref[...]
        )
        sigma = sigmoid(update_in)
        out = update_in * sigma
        back_ref[...] = sigma + out * (1.0 - sigma)
        update = out.astype(jnp.bfloat16)
        update_ref[...] = update
        new = mesh_in + inner(update, mats_ref[4], 1, 0)
        new_ref[...] = new
        lowered = new.astype(jnp.bfloat16)
        if more:
            weave(wide, inner(lowered, next_ref[0], 1, 0))
            sent_ref[...] = wide[...].astype(jnp.bfloat16)
            return
        nodes = lax.broadcasted_iota(jnp.int32, (ids_ref.shape[0], tile), 1) + step * tile
        chooser = jnp.where(nodes == ids_ref[...], 1.0, 0.0).astype(jnp.bfloat16)
        found = inner(chooser, lowered, 1, 0)

        @pl.when(step == 0)
        def _():
            total_ref[...] = found

        @pl.when(step > 0)
        def _():
            total_ref[...] += found

        @pl.when(step == blocks // tile - 1)
        def _():
            fetched = total_ref[...].astype(jnp.bfloat16)
            fetched_ref[...] = fetched
            value = inner(fetched, dec_ref[...], 1, 0) + head_ref[2:3, :]
            sigma = sigmoid(value)
            out = value * sigma
            turn_ref[...] = sigma + out * (1.0 - sigma)
            decoded = out.astype(jnp.bfloat16)
            decoded_ref[...] = decoded
            branch_ref[...] = inner(decoded, out_ref[...], 1, 0).astype(jnp.bfloat16)

    whole_rows = pl.BlockSpec((tile, D), lambda i, *_: (i + shift, 0))
    woven = pl.BlockSpec((2 * tile, HALF), lambda i, *_: (i + shift, 0))
    ins = [whole_rows] + [pl.BlockSpec(memory_space=pltpu.VMEM)] * len(pieces)
    ins = ins + [whole(mats.shape), woven, whole_rows]
    outs = [whole_rows] * 4 + [pl.BlockSpec((K, 2 * tile, HALF), lambda i, *_: (0, i + shift, 0))]
    shapes = [
        jax.ShapeDtypeStruct((blocks, D), jnp.float32),
        jax.ShapeDtypeStruct((blocks, D), jnp.float32),
        jax.ShapeDtypeStruct((blocks, D), jnp.bfloat16),
        jax.ShapeDtypeStruct((blocks, D), jnp.bfloat16),
        jax.ShapeDtypeStruct((K, 2 * blocks, HALF), jnp.bfloat16),
    ]
    args = [index, mesh] + [rows for rows, _ in pieces] + [mats, *terms]
    if more:
        ins.append(pl.BlockSpec((1, D, D), lambda *_: (0, 0, 0)))
        outs.append(pl.BlockSpec((2 * tile, HALF), lambda i, *_: (i, 0)))
        shapes.append(jax.ShapeDtypeStruct((2 * tile * steps, HALF), jnp.bfloat16))
        args.append(following)
    aliases = {len(args) + n: n for n in range(len(into))}
    ins = ins + [pl.BlockSpec(memory_space=pl.ANY)] * len(into)
    args = args + list(into)
    scratch = []
    if decoder:
        posts = decoder[0].shape[0]
        ins = ins + [whole(arg.shape) for arg in decoder]
        args = args + list(decoder)
        for width, kind in ((HALF, jnp.bfloat16), (D, jnp.bfloat16), (D, jnp.bfloat16), (D, jnp.float32)):
            outs.append(whole((posts, width)))
            shapes.append(jax.ShapeDtypeStruct((posts, width), kind))
        scratch = [pltpu.VMEM((posts, D), jnp.float32)]
    return pl.pallas_call(
        body,
        grid_spec=pltpu.PrefetchScalarGridSpec(
            num_scalar_prefetch=1,
            grid=(steps,),
            in_specs=ins,
            out_specs=outs,
            scratch_shapes=scratch
            + [
                pltpu.VMEM((reach, HALF), jnp.float32),
                pltpu.VMEM((K * 2 * tile, HALF), jnp.float32),
                pltpu.VMEM((2 * tile, HALF), jnp.float32),
            ],
        ),
        out_shape=shapes,
        input_output_aliases=aliases,
        compiler_params=pltpu.CompilerParams(vmem_limit_bytes=54 * 2**20),
        cost_estimate=cost(24 if half is None else 14),
        name="round_forward",
    )(*args)


def edges_backward(index, back, slopes, mats, carried=(), landed=()):
    blocks = back.shape[0]
    tile, chunk = 512, 16
    steps, turns, high = blocks // tile, tile // chunk, 2 * chunk
    reach = 2 * (blocks + 2 * H)

    def body(*refs):
        if carried:
            index_ref, back_ref, slope_ref, mats_ref = refs[:4]
            past, rest = refs[4:9], refs[9:]
            (new_ref, out_ref, sent_ref), rest = rest[:3], rest[3:]
        else:
            index_ref, back_ref, slope_ref, mats_ref = refs[:4]
            (ids_ref, landed_ref, turn_ref, w_out_ref, w_dec_ref), rest = refs[4:9], refs[9:]
            (new_ref, out_ref, gdec_ref), rest = rest[:3], rest[3:]
            gathered, rest = rest[5], rest[:5] + rest[6:]
        guin_ref, low_ref, before_ref, own_ref, after_ref, wide, wider, flows, *tables = rest
        step = pl.program_id(0)

        @pl.when(step == 0)
        def _():
            @pl.loop(0, reach // 256)
            def _(i):
                for table in tables:
                    table[pl.ds(pl.multiple_of(i * 256, 256), 256), :] = jnp.zeros(
                        (256, HALF), jnp.float32
                    )

        if carried:
            new, one, two = ended(*past, wide)
            sent_ref[:, :HALF] = one
            sent_ref[:, HALF:] = two
            new_ref[...] = new
            grad_out = new.astype(jnp.bfloat16)
            out_ref[...] = grad_out
        else:

            @pl.when(step == 0)
            def _():
                grad_dec = inner(landed_ref[...], w_out_ref[...], 1, 1) * turn_ref[...]
                grad_dec = grad_dec.astype(jnp.bfloat16)
                gdec_ref[...] = grad_dec
                gathered[...] = inner(grad_dec, w_dec_ref[...], 1, 1).astype(jnp.bfloat16)

            nodes = lax.broadcasted_iota(jnp.int32, (tile, landed_ref.shape[0]), 0) + step * tile
            chooser = jnp.where(nodes == ids_ref[...], 1.0, 0.0).astype(jnp.bfloat16)
            new = inner(chooser, gathered[...], 1, 0)
            new_ref[...] = new
            grad_out = new.astype(jnp.bfloat16)
            out_ref[...] = grad_out
        grad_uin = (inner(grad_out, mats_ref[4], 1, 1) * back_ref[...]).astype(jnp.bfloat16)
        guin_ref[...] = grad_uin
        weave(wide, inner(grad_uin, mats_ref[2], 1, 1) * (1.0 / K))

        def dense(turn):
            at = pl.multiple_of(turn * high, high)
            grad_agg = wide[pl.ds(at, high), :]
            total, parts = None, []
            for edge in range(K):
                flow = grad_agg * slope_ref[edge, pl.ds(at, high), :].astype(jnp.float32)
                parts.append(flow)
                total = flow if total is None else total + flow
            return at, total, parts

        def keep(turn, at, total, parts):
            for edge in range(K):
                spot = pl.multiple_of(edge * 2 * tile + turn * high, high)
                flows[pl.ds(spot, high), :] = parts[edge]
            wider[pl.ds(at, high), :] = total

        def scatter(turn):
            for u in range(chunk):
                spots, sums = [], []
                for edge in range(K):
                    base = edge * blocks + step * tile + turn * chunk
                    spots.append(pl.multiple_of(index_ref[base + u], 2))
                for edge in range(K):
                    spot = pl.multiple_of(edge * 2 * tile + turn * high + 2 * u, 2)
                    sums.append(tables[edge][pl.ds(spots[edge], 2), :] + flows[pl.ds(spot, 2), :])
                for edge in range(K):
                    tables[edge][pl.ds(spots[edge], 2), :] = sums[edge]

        def some(turn, carry):
            found = dense(turn)
            scatter(turn - 1)
            keep(turn, *found)
            return carry

        keep(0, *dense(0))
        lax.fori_loop(1, turns, some, 0)
        scatter(turns - 1)
        first, second = unweave(wider)
        low_ref[:, :HALF] = first.astype(jnp.bfloat16)
        low_ref[:, HALF:] = second.astype(jnp.bfloat16)

        @pl.when(step == steps - 1)
        def _():
            def summed(at):
                value = tables[0][pl.ds(at, 256), :]
                for table in tables[1:]:
                    value = value + table[pl.ds(at, 256), :]
                return value

            @pl.loop(0, 2 * H // 256)
            def _(i):
                at = pl.multiple_of(i * 256, 256)
                far = pl.multiple_of(2 * H + 2 * blocks + at, 256)
                before_ref[pl.ds(at, 256), :] = summed(at).astype(jnp.bfloat16)
                after_ref[pl.ds(at, 256), :] = summed(far).astype(jnp.bfloat16)

            @pl.loop(0, 2 * blocks // 256)
            def _(i):
                at = pl.multiple_of(i * 256, 256)
                own_ref[pl.ds(at, 256), :] = summed(pl.multiple_of(2 * H + at, 256))

    rows = pl.BlockSpec((tile, D), lambda i, *_: (i, 0))
    woven = pl.BlockSpec((2 * tile, HALF), lambda i, *_: (i, 0))
    low = jax.ShapeDtypeStruct((blocks, D), jnp.bfloat16)
    low_posts = (landed[1].shape[0], D) if landed else None
    last = low if carried else jax.ShapeDtypeStruct(low_posts, jnp.bfloat16)
    return pl.pallas_call(
        body,
        grid_spec=pltpu.PrefetchScalarGridSpec(
            num_scalar_prefetch=1,
            grid=(steps,),
            in_specs=[
                rows,
                pl.BlockSpec((K, 2 * tile, HALF), lambda i, *_: (0, i, 0)),
                whole(mats.shape),
            ]
            + ([rows] + [woven] * 3 + [whole(mats.shape)] if carried else [])
            + [whole(arg.shape) for arg in landed],
            out_specs=([rows] * 3 if carried else [rows, rows, whole(low_posts)])
            + [
                rows, rows,
                whole((2 * H, HALF)), whole((2 * blocks, HALF)), whole((2 * H, HALF)),
            ],
            scratch_shapes=([] if carried else [pltpu.VMEM(low_posts, jnp.bfloat16)])
            + [
                pltpu.VMEM((2 * tile, HALF), jnp.float32),
                pltpu.VMEM((2 * tile, HALF), jnp.float32),
                pltpu.VMEM((2 * tile * K, HALF), jnp.float32),
            ]
            + [pltpu.VMEM((reach, HALF), jnp.float32)] * K,
        ),
        out_shape=[
            jax.ShapeDtypeStruct((blocks, D), jnp.float32),
            low,
            last,
            low,
            low,
            jax.ShapeDtypeStruct((2 * H, HALF), jnp.bfloat16),
            jax.ShapeDtypeStruct((2 * blocks, HALF), jnp.float32),
            jax.ShapeDtypeStruct((2 * H, HALF), jnp.bfloat16),
        ],
        compiler_params=LIMIT,
        cost_estimate=cost(28 if carried else 25),
        name="edges_backward",
    )(index, back, slopes, mats, *carried, *landed)


def ended(part_ref, own_ref, first_ref, last_ref, mats_ref, wide):
    wide[...] = (
        own_ref[...] + first_ref[...].astype(jnp.float32) + last_ref[...].astype(jnp.float32)
    )
    one, two = unweave(wide)
    one, two = one.astype(jnp.bfloat16), two.astype(jnp.bfloat16)
    new = (
        part_ref[...]
        + inner(one, mats_ref[0, :, :HALF], 1, 1)
        + inner(two, mats_ref[0, :, HALF:], 1, 1)
    )
    return new, one, two


def carried_terms(grad_mesh, grad_uin, dest_low, mats):
    blocks = grad_mesh.shape[0]
    tile = 1024

    def body(grad_ref, guin_ref, dest_ref, mats_ref, part_ref):
        part_ref[...] = (
            grad_ref[...]
            + inner(guin_ref[...], mats_ref[3], 1, 1)
            + inner(dest_ref[...], mats_ref[1], 1, 1)
        )

    rows = pl.BlockSpec((tile, D), lambda i: (i, 0))
    return pl.pallas_call(
        body,
        grid=(blocks // tile,),
        in_specs=[rows, rows, rows, whole(mats.shape)],
        out_specs=rows,
        out_shape=jax.ShapeDtypeStruct((blocks, D), jnp.float32),
        compiler_params=LIMIT,
        cost_estimate=cost(4),
        name="carried_terms",
    )(grad_mesh, grad_uin, dest_low, mats)


def encode_rows(arrived, w_in, w_node, biases, source):
    posts = arrived.shape[0]
    tile = 512

    def body(
        arrived_ref, in_ref, node_ref, bias_ref, source_ref,
        mesh_ref, gathered_ref, sent_ref, ids_ref, down_ref, encoded, wide,
    ):
        step = pl.program_id(0)

        @pl.when(step == 0)
        def _():
            entering = inner(arrived_ref[...], in_ref[...], 1, 0) + bias_ref[0:1, :]
            encoded[...] = silu(entering).astype(jnp.bfloat16)
            ids_ref[...] = ids_along(arrived_ref[...])
            down_ref[...] = ids_down(arrived_ref[...])

        nodes = lax.broadcasted_iota(jnp.int32, (tile, posts), 0) + step * tile
        chooser = jnp.where(nodes == ids_ref[...], 1.0, 0.0).astype(jnp.bfloat16)
        gathered = inner(chooser, encoded[...], 1, 0).astype(jnp.bfloat16)
        gathered_ref[...] = gathered
        mesh = silu(inner(gathered, node_ref[...], 1, 0) + bias_ref[1:2, :])
        mesh_ref[...] = mesh
        weave(wide, inner(mesh.astype(jnp.bfloat16), source_ref[0], 1, 0))
        sent_ref[...] = wide[...].astype(jnp.bfloat16)

    rows = pl.BlockSpec((tile, D), lambda i: (i, 0))
    args = (arrived, w_in, w_node, biases, source)
    return pl.pallas_call(
        body,
        grid=(H // tile,),
        in_specs=[whole(arg.shape) for arg in args[:-1]]
        + [pl.BlockSpec((1, D, D), lambda *_: (0, 0, 0))],
        out_specs=[rows, rows, pl.BlockSpec((2 * tile, HALF), lambda i: (i, 0))]
        + [whole((1, posts)), whole((posts, 1))],
        out_shape=[
            jax.ShapeDtypeStruct((H, D), jnp.float32),
            jax.ShapeDtypeStruct((H, D), jnp.bfloat16),
            jax.ShapeDtypeStruct((2 * H, HALF), jnp.bfloat16),
            jax.ShapeDtypeStruct((1, posts), jnp.int32),
            jax.ShapeDtypeStruct((posts, 1), jnp.int32),
        ],
        scratch_shapes=[pltpu.VMEM((posts, D), jnp.bfloat16), pltpu.VMEM((2 * tile, HALF), jnp.float32)],
        compiler_params=LIMIT,
        cost_estimate=cost(5),
        name="encode_rows",
    )(*args)


def encode_backward(carried, mesh, gathered, arrived, ids, w_in, w_node, biases):
    blocks = mesh.shape[0]
    posts = arrived.shape[0]
    tile = 512
    steps = blocks // tile

    def body(
        part_ref, own_ref, first_ref, last_ref, mats_ref,
        mesh_ref, gathered_ref, arrived_ref, ids_ref, in_ref, node_ref, bias_ref,
        new_ref, out_ref, gin_ref, gnode_ref, gbias_ref, gsource_ref, total, wide,
    ):
        step = pl.program_id(0)

        @pl.when(step == 0)
        def _():
            for ref in (total, gnode_ref, gbias_ref, gsource_ref):
                ref[...] = jnp.zeros(ref.shape, jnp.float32)

        new, one, two = ended(part_ref, own_ref, first_ref, last_ref, mats_ref, wide)
        new_ref[...] = new
        out_ref[...] = new.astype(jnp.bfloat16)
        lowered = mesh_ref[...].astype(jnp.bfloat16)
        gsource_ref[:, :HALF] += inner(lowered, one, 0, 0)
        gsource_ref[:, HALF:] += inner(lowered, two, 0, 0)
        node_in = inner(gathered_ref[...], node_ref[...], 1, 0) + bias_ref[1:2, :]
        grad_node = (new * slope(node_in)).astype(jnp.bfloat16)
        gbias_ref[1:2, :] += jnp.sum(grad_node.astype(jnp.float32), 0, keepdims=True)
        gnode_ref[...] += inner(gathered_ref[...], grad_node, 0, 0)
        back = inner(grad_node, node_ref[...], 1, 1).astype(jnp.bfloat16)
        nodes = lax.broadcasted_iota(jnp.int32, (posts, tile), 1) + step * tile
        chooser = jnp.where(nodes == ids_ref[...], 1.0, 0.0).astype(jnp.bfloat16)
        total[...] += inner(chooser, back, 1, 0)

        @pl.when(step == steps - 1)
        def _():
            entering = inner(arrived_ref[...], in_ref[...], 1, 0) + bias_ref[0:1, :]
            grad_enc = (total[...] * slope(entering)).astype(jnp.bfloat16)
            gbias_ref[0:1, :] = jnp.sum(grad_enc.astype(jnp.float32), 0, keepdims=True)
            gin_ref[...] = inner(arrived_ref[...], grad_enc, 0, 0)

    rows = pl.BlockSpec((tile, D), lambda i: (i, 0))
    woven = pl.BlockSpec((2 * tile, HALF), lambda i: (i, 0))
    args = (arrived, ids, w_in, w_node, biases)
    shapes = [(HALF, D), (D, D), (2, D), (D, D)]
    return pl.pallas_call(
        body,
        grid=(steps,),
        in_specs=[rows] + [woven] * 3 + [whole(carried[4].shape), rows, rows]
        + [whole(arg.shape) for arg in args],
        out_specs=[rows, rows] + [whole(shape) for shape in shapes],
        out_shape=[
            jax.ShapeDtypeStruct((blocks, D), jnp.float32),
            jax.ShapeDtypeStruct((blocks, D), jnp.bfloat16),
        ]
        + [jax.ShapeDtypeStruct(shape, jnp.float32) for shape in shapes],
        scratch_shapes=[pltpu.VMEM((posts, D), jnp.float32), pltpu.VMEM((2 * tile, HALF), jnp.float32)],
        compiler_params=LIMIT,
        cost_estimate=cost(10),
        name="encode_backward",
    )(*carried, mesh, gathered, *args)


def shards(walk, master, moment1, moment2, inputs, targets, valid, owner, slot, neighbours, partner):
    bands = lax.axis_size("space")
    band = lax.axis_index("space")
    peers = lax.axis_size(ALL)
    place = lax.axis_index(ALL)
    shard = master.shape[0]
    total_size = shard * peers
    height = pieces_of(total_size, peers)[3]
    offset = lax.rem(lax.rem(shard, D) * place, D)
    piece = lax.dynamic_update_slice_in_dim(
        jnp.zeros((height * D,), jnp.bfloat16), master.astype(jnp.bfloat16), offset, 0
    )
    state_in = inputs[0]
    counted = valid[0].astype(jnp.float32)
    local_count = jnp.sum(valid[0])
    digits = (local_count >> jnp.array([16, 8, 0], jnp.int32)) & 255
    digits = jnp.pad(digits, (CH + 3, HALF - CH - 6)).astype(jnp.float32)[None, :]
    points = state_in.shape[1]
    blocks = neighbours.shape[0]
    assert blocks == H
    capacity = max(2, 2 * points // bands)
    target_band = owner[0, :, 0]
    hits = (target_band[:, None] == jnp.arange(bands, dtype=jnp.int32)[None, :]).astype(jnp.int32)
    ranks = jnp.sum(jnp.cumsum(hits, 0) * hits, 1) - 1
    places_out = jnp.sum(hits * jnp.asarray(walk, jnp.int32)[None, :], 1) * capacity + ranks
    poster = (
        jnp.arange(bands * capacity, dtype=jnp.int32)[:, None] == places_out[None, :]
    ).astype(jnp.bfloat16)
    spots = slot[0][None, :]
    columns = jnp.concatenate(
        [
            state_in,
            (spots // 64).astype(jnp.bfloat16),
            (spots % 64).astype(jnp.bfloat16),
            jnp.ones((1, points), jnp.bfloat16),
            jnp.zeros((HALF - CH - 3, points), jnp.bfloat16),
        ],
        0,
    )

    def exchanged(rows):
        return lax.all_to_all(
            rows.reshape(bands, capacity, HALF), "space", split_axis=0, concat_axis=0, tiled=True
        ).reshape(bands * capacity, HALF)

    held, posted = gathered_blocks(
        piece.reshape(height, D), (inner(poster, columns, 1, 1) + digits).astype(jnp.bfloat16)
    )
    arrived = exchanged(posted)
    w_in, w_node, w_dec, w_out, *w_round, biases = spread_rows(
        held, total_size, peers, place
    )
    arrived, biases = lax.optimization_barrier((arrived, biases))
    counts = arrived.reshape(bands, capacity, HALF)[:, 0, CH + 3 : CH + 6].astype(jnp.float32)
    counts = jnp.sum(counts, 0, keepdims=True)
    w_out = jnp.pad(w_out.reshape(D, CH), ((0, 0), (0, HALF - CH)))
    w_round = [mats.reshape(5, D, D) for mats in w_round]
    b_head = biases[:3]
    b_round = biases[3:].reshape(ROUNDS, 2, D)
    mesh, gathered, sent, ids_row, ids = encode_rows(
        arrived, w_in, w_node, biases, w_round[0]
    )
    sent, partner, neighbours, counted, counts = lax.optimization_barrier(
        (sent, partner, neighbours, counted, counts)
    )
    counts = counts + swapped(counts, "dp", 1)
    index = 2 * ((neighbours - band * blocks + H) % (blocks * bands)).T.reshape(-1)
    moved = [(n, place) for n, place in enumerate(walk) if n != place]
    stays = jnp.asarray([n == place for n, place in enumerate(walk)])[band]
    index = lax.ppermute(index, "space", list(enumerate(walk)))

    def at_home(rows):
        return lax.ppermute(rows, "space", [(j, i) for i, j in moved])

    def settled(own, came):
        return jnp.where(stays, own, came.astype(jnp.float32))

    partner_by = partner - band * points - jnp.arange(points, dtype=jnp.int32)
    coded = jnp.where(partner_by >= NEAR, partner_by - NEAR + 1, 0).astype(jnp.bfloat16)
    low_valid = jnp.concatenate([counted.astype(jnp.bfloat16), coded[None, :]], 0)
    valid_around = jnp.concatenate(
        [
            shifted(low_valid[:, points - ROWW :], "space", 1),
            low_valid,
            shifted(low_valid[:, :ROWW], "space", -1),
        ],
        1,
    )
    kept = []
    sent = [sent]
    for layer in range(ROUNDS):
        pieces, start = [], 0
        arrivals = [halo(walk, sent[0], sent[0])]
        if len(sent) > 1:
            sent[1], arrivals[0] = lax.optimization_barrier((sent[1], arrivals[0]))
            arrivals.append(halo(walk, sent[1], sent[1]))
        terms = node_terms(mesh, w_round[layer], b_round[layer])
        if layer == 0:
            (before, after), valid_around, counts = lax.optimization_barrier(
                (arrivals[0], valid_around, counts)
            )
            arrivals = [(before, after)]
        for side in ([rows for rows, _ in arrivals], sent, [rows for _, rows in arrivals]):
            for rows in side:
                pieces.append((rows, start))
                start = start + rows.shape[0]
        mats = w_round[layer]
        if layer + 1 < ROUNDS:
            following = w_round[layer + 1]
            *outs, first = round_forward(index, mesh, pieces, mats, terms, following, half=0)
            *outs, second = round_forward(
                index, mesh, pieces, mats, terms, following, half=1, into=outs
            )
            sent = [first, second]
        else:
            decoder = (ids, w_dec, w_out, biases)
            outs = round_forward(index, mesh, pieces, mats, terms, None, decoder)
            outs, rest = outs[:5], outs[5:]
        kept.append((mesh, *outs[1:]))
        mesh = outs[0]
    count = counts[0, 0] * 65536.0 + counts[0, 1] * 256.0 + counts[0, 2]
    wide_valid = valid_around[:CH].astype(jnp.float32)
    coded = valid_around[CH : CH + 1, : points + ROWW].astype(jnp.float32)
    weights = [
        (
            by,
            jnp.where(coded == by - NEAR + 1, 1.0, 0.0)
            * wide_valid[:, : points + ROWW]
            * wide_valid[:, by : by + points + ROWW],
        )
        for by in range(NEAR, ROWW + 1)
    ]
    branch_rows, fetched, decoded, dec_turn = rest
    returned = exchanged(branch_rows)
    branch = inner(returned, poster, 0, 0)[:CH]
    err = state_in.astype(jnp.float32) + branch - targets[0].astype(jnp.float32)
    def widened(values):
        low = values.astype(jnp.bfloat16)
        before = shifted(low[:, points - ROWW :], "space", 1).astype(jnp.float32)
        after = shifted(low[:, :ROWW], "space", -1).astype(jnp.float32)
        return jnp.concatenate([before, values, after], 1)

    wide_err = widened(err)
    paired = jnp.zeros((CH, points + ROWW), jnp.float32)
    pair_total = jnp.zeros((CH, points), jnp.float32)
    for by, both in weights:
        gap = both * (wide_err[:, : points + ROWW] - wide_err[:, by : by + points + ROWW])
        paired = paired + gap
        pair_total = pair_total + gap[:, ROWW:] * (
            wide_err[:, ROWW : ROWW + points] - wide_err[:, ROWW + by : ROWW + by + points]
        )
    local_total = jnp.sum(counted * err * err) + 0.5 * jnp.sum(pair_total)
    grad_pred = 2.0 * counted * err + paired[:, ROWW:]
    for by, both in weights:
        gap = both * (wide_err[:, : points + ROWW] - wide_err[:, by : by + points + ROWW])
        grad_pred = grad_pred - gap[:, ROWW - by : ROWW - by + points]
    grad_pred = grad_pred / count
    grad_rows = jnp.pad(grad_pred.astype(jnp.bfloat16), ((0, HALF - CH), (0, 0)))
    landed = exchanged(inner(poster, grad_rows, 1, 1).astype(jnp.bfloat16))
    landed, final_mesh = lax.optimization_barrier((landed, mesh.astype(jnp.bfloat16)))
    final_mesh = at_home(final_mesh)
    mats_grads = [None] * (5 * ROUNDS)
    bias_grads = [None] * (2 * ROUNDS)
    carried, grad_mesh = (), None
    for layer in reversed(range(ROUNDS)):
        old, back, update, agg, slopes = kept[layer]
        first_step = not carried
        grad_mesh, leaving, extra, grad_uin, dest_low, to_before, own, to_after = edges_backward(
            index, back, slopes, w_round[layer], carried,
            (ids_row, landed, dec_turn, w_out, w_dec) if first_step else (),
        )
        if not first_step:
            mats_grads[5 * layer + 5] = inner(
                kept[layer + 1][0].astype(jnp.bfloat16), extra, 0, 0
            )
        else:
            grad_wout = inner(decoded, landed, 0, 0)[:, :CH]
            grad_bdec = jnp.sum(extra.astype(jnp.float32), 0, keepdims=True)
            grad_wdec = inner(fetched, extra, 0, 0)
            to_before, to_after, final_mesh = lax.optimization_barrier(
                (to_before, to_after, final_mesh)
            )
        from_before, from_after = halo(walk, to_after, to_before)
        if first_step:
            from_before, final_mesh = lax.optimization_barrier(
                (from_before, settled(mesh, final_mesh))
            )
        lowered = old.astype(jnp.bfloat16)
        mats_grads[5 * layer + 1 : 5 * layer + 5] = [
            inner(lowered, dest_low, 0, 0),
            inner(agg, grad_uin, 0, 0),
            inner(lowered, grad_uin, 0, 0),
            inner(update, leaving, 0, 0),
        ]
        bias_grads[2 * layer] = jnp.sum(dest_low.astype(jnp.float32), 0, keepdims=True)
        bias_grads[2 * layer + 1] = jnp.sum(grad_uin.astype(jnp.float32), 0, keepdims=True)
        part = carried_terms(grad_mesh, grad_uin, dest_low, w_round[layer])
        carried = (part, own, from_before, from_after, w_round[layer])
    grad_mesh, leaving, grad_win, grad_wnode, grad_bpair, mats_grads[0] = encode_backward(
        carried, kept[0][0], gathered, arrived, ids, w_in, w_node, biases
    )
    parts = [grad_win, grad_wnode, grad_wdec, grad_wout.reshape(CH, D)]
    parts = parts + mats_grads
    parts = parts + [grad_bpair, grad_bdec] + bias_grads
    keep, send = collect_rows(parts, total_size, peers, place)
    mine, leaving = reduced_piece(keep, send, leaving)
    late = at_home(leaving)
    mine = lax.dynamic_slice_in_dim(mine.reshape(-1), offset, shard)
    lane = lax.broadcasted_iota(jnp.int32, (8, HALF), 1)
    sums, late = summed_everywhere(
        jnp.where(lane == 0, local_total, jnp.sum(mine * mine)), late
    )
    total, norm = sums[0, 0], jnp.sqrt(sums[0, 1])
    node_grads = settled(grad_mesh, late)
    clipped = mine * jnp.minimum(1.0, 0.05 / norm)
    first = 0.9 * moment1 + 0.1 * clipped
    second = 0.999 * moment2 + 0.001 * clipped * clipped
    first_hat = first / (1.0 - 0.9**STEP)
    second_hat = second / (1.0 - 0.999**STEP)
    updated = master - 0.1 * (first_hat / (jnp.sqrt(second_hat) + 1e-08) + 0.1 * master)
    return (
        total.reshape(1),
        count.reshape(1),
        norm.reshape(1),
        updated,
        first,
        second,
        updated.astype(jnp.bfloat16),
        final_mesh.reshape(1, blocks, D),
        node_grads.reshape(1, blocks, D),
        grad_pred.reshape(1, grad_pred.shape[0], points),
    )


def solution(mesh):
    return jax.shard_map(
        functools.partial(shards, walk_of(mesh)),
        mesh=mesh,
        in_specs=(
            P(("dp", "space")),
            P(("dp", "space")),
            P(("dp", "space")),
            P("dp", None, "space"),
            P("dp", None, "space"),
            P("dp", None, "space"),
            P("dp", "space", None),
            P("dp", "space"),
            P("space", None),
            P("space"),
        ),
        out_specs=(
            P(),
            P(),
            P(),
            P(("dp", "space")),
            P(("dp", "space")),
            P(("dp", "space")),
            P(("dp", "space")),
            P("dp", "space", None),
            P("dp", "space", None),
            P("dp", None, "space"),
        ),
        check_vma=False,
    )
```

```python
import functools

import jax
import jax.numpy as jnp
from jax import lax
from jax.experimental import pallas as pl
from jax.experimental.pallas import tpu as pltpu
from jax.sharding import PartitionSpec as P

D = 256
HALF = 128
CH = 78
ROUNDS = 3
K = 6
ROWW = 360
NEAR = 358
STEP = 10
H = 2048
ALL = ("dp", "space")
LIMIT = pltpu.CompilerParams(vmem_limit_bytes=60 * 2**20)


def cost(micros):
    return pl.CostEstimate(flops=0, bytes_accessed=micros * 3_000_000, transcendentals=0)


def inner(left, right, left_dim, right_dim):
    return lax.dot_general(
        left, right, (((left_dim,), (right_dim,)), ((), ())), preferred_element_type=jnp.float32
    )


def sigmoid(value):
    return 0.5 * jnp.tanh(0.5 * value) + 0.5


def silu(value):
    return value * sigmoid(value)


def slope(value):
    sigma = sigmoid(value)
    return sigma * (1.0 + value * (1.0 - sigma))


def shifted(shard, axis, by):
    peers = lax.axis_size(axis)
    pairs = [(i, i + by) for i in range(peers) if 0 <= i + by < peers]
    return lax.ppermute(shard, axis, pairs)


def walk_of(mesh):
    count = mesh.shape["space"]
    chips = [getattr(device, "coords", None) for device in mesh.devices[0].reshape(-1)]
    if any(chip is None for chip in chips) or len(set(map(tuple, chips))) != count:
        return list(range(count))
    at = {tuple(chip): n for n, chip in enumerate(chips)}
    xs, ys, zs = (sorted({chip[n] for chip in at}) for n in range(3))
    if len(xs) * len(ys) * len(zs) != count:
        return list(range(count))
    if (len(xs), len(ys), len(zs)) == (2, 2, 4):
        corners = [(0, 0), (1, 0), (0, 1), (1, 1)]
        planes = [(0, 1, 3, 2), (2, 0, 1, 3), (3, 1, 0, 2), (2, 3, 1, 0)]
        steps = [(*corners[n], z) for z, plane in enumerate(planes) for n in plane]
        return [at[(xs[x], ys[y], zs[z])] for x, y, z in steps]
    walk, plane = [], []
    for n, y in enumerate(ys):
        plane = plane + [(x, y) for x in (xs if n % 2 == 0 else xs[::-1])]
    for n, z in enumerate(zs):
        walk = walk + [at[(x, y, z)] for x, y in (plane if n % 2 == 0 else plane[::-1])]
    return walk


def halo(walk, last, initial):
    up = list(zip(walk, walk[1:] + walk[:1]))
    down = [(j, i) for i, j in up]
    return lax.ppermute(last, "space", up), lax.ppermute(initial, "space", down)


def pieces_of(total, peers):
    share = total // peers
    starts = [share * d // D for d in range(peers)]
    counts = [-(-share * (d + 1) // D) - starts[d] for d in range(peers)]
    shared = [share * d % D != 0 for d in range(peers)]
    height = -(-max(counts) // 16) * 16
    return starts, counts, shared, height


def parts_of():
    return [CH, D, D, CH] + [5 * D] * ROUNDS + [3 + 2 * ROUNDS]


def swapped(value, axis, bit):
    return lax.ppermute(value, axis, [(i, i ^ bit) for i in range(lax.axis_size(axis))])


def bits_of(axis):
    return [1 << n for n in range(lax.axis_size(axis).bit_length() - 1)]


def others(value, axis, bits):
    masks = [sum(bit for n, bit in enumerate(bits) if m >> n & 1) for m in range(1, 1 << len(bits))]
    return [swapped(value, axis, mask) for mask in masks]


def upper_groups():
    bits = bits_of("space")[2:]
    return [tuple(bits[n : n + 2]) for n in range(0, len(bits), 2)]


def orders():
    return [(1, 2), (2, 1)]


def summed_everywhere(value, arriving):
    for bits in reversed(upper_groups()):
        value = sum(others(value, "space", bits), value)
    value = value + swapped(value, "dp", 1)
    value, arriving = lax.optimization_barrier((value, arriving))
    return sum(others(value, "space", (1, 2)), value), arriving


def gathered_blocks(piece, posted):
    held, weights, size = piece[None], {}, 1
    for bits in reversed(upper_groups()):
        held = jnp.concatenate([held] + others(held, "space", bits), 0)
        for n, bit in enumerate(bits):
            weights[bit] = size << n
        size = size << len(bits)
    half = piece.shape[0] // 2
    held = [held[:, :half], held[:, half:]]
    ranks = [dict(weights), dict(weights)]
    for turn in (1, 0):
        if turn == 0:
            held[0], held[1], posted = lax.optimization_barrier((*held, posted))
        for n, order in enumerate(orders()):
            held[n] = jnp.concatenate([held[n], swapped(held[n], "space", order[turn])], 0)
            ranks[n][order[turn]] = size
        size = size << 1
    return (held, [swapped(part, "dp", 1) for part in held], ranks), posted


def spread_rows(gathered, total, peers, place):
    (first, second), (first_far, second_far), ranks = gathered
    starts, counts, shared, height = pieces_of(total, peers)
    half, group = height // 2, first.shape[0]
    rows = -(-total // D)
    sizes = parts_of()
    def at(rank, relative):
        spot = 0
        for bit, weight in rank.items():
            spot = spot + jnp.where((relative & bit) != 0, weight, 0)
        return spot

    def body(place_ref, *refs):
        sources, outs, buffer = refs[:4], refs[4:-1], refs[-1]
        me = place_ref[0]
        mine = me // group
        for d in range(peers):
            relative = (me ^ d) & (group - 1)
            spots = [at(rank, relative) for rank in ranks]

            def lay(one, two, d=d, spots=spots):
                piece = jnp.concatenate([one[spots[0]], two[spots[1]]], 0).astype(jnp.float32)
                start, count = starts[d], counts[d]
                if shared[d]:
                    buffer[start : start + 1, :] = buffer[start : start + 1, :] + piece[:1]
                    buffer[start + 1 : start + count, :] = piece[1:count]
                else:
                    buffer[start : start + count, :] = piece[:count]

            @pl.when(mine == d // group)
            def _():
                lay(sources[0], sources[1])

            @pl.when(mine != d // group)
            def _():
                lay(sources[2], sources[3])

        start = 0
        for out, size in zip(outs, sizes):
            out[:size, :] = buffer[start : start + size, :].astype(out.dtype)
            if out.shape[0] > size:
                out[size:, :] = jnp.zeros((out.shape[0] - size, D), out.dtype)
            start = start + size

    kinds = [jnp.bfloat16] * (4 + ROUNDS) + [jnp.float32]
    talls = [HALF] + sizes[1:]
    return pl.pallas_call(
        body,
        grid_spec=pltpu.PrefetchScalarGridSpec(
            num_scalar_prefetch=1,
            grid=(1,),
            in_specs=[whole(first.shape)] * 4,
            out_specs=[whole((tall, D)) for tall in talls],
            scratch_shapes=[pltpu.VMEM((-(-rows // 8) * 8 + 8, D), jnp.float32)],
        ),
        out_shape=[jax.ShapeDtypeStruct((tall, D), kind) for tall, kind in zip(talls, kinds)],
        compiler_params=LIMIT,
        cost_estimate=cost(4),
        name="spread_rows",
    )(place.reshape(1), first, second, first_far, second_far)


def collect_rows(parts, total, peers, place):
    starts, counts, shared, height = pieces_of(total, peers)
    rows = -(-total // D)
    sizes = [min(part.shape[0], size) for part, size in zip(parts, tall_parts())]
    group = lax.axis_size("space")

    def body(place_ref, *refs):
        sources, keep, send, buffer = refs[:-3], refs[-3], refs[-2], refs[-1]
        start = 0
        for source, size in zip(sources, sizes):
            buffer[start : start + size, :] = source[:size, :]
            start = start + size
        if buffer.shape[0] > start:
            buffer[start:, :] = jnp.zeros((buffer.shape[0] - start, D), jnp.float32)
        me = place_ref[0]
        mine = me // group
        for d in range(peers):
            relative = (me ^ d) & (group - 1)

            @pl.when(mine == d // group)
            def _():
                keep[relative] = buffer[starts[d] : starts[d] + height, :]

            @pl.when(mine != d // group)
            def _():
                send[relative] = buffer[starts[d] : starts[d] + height, :].astype(jnp.bfloat16)

    shape = (group, height, D)
    return pl.pallas_call(
        body,
        grid_spec=pltpu.PrefetchScalarGridSpec(
            num_scalar_prefetch=1,
            grid=(1,),
            in_specs=[whole(part.shape) for part in parts],
            out_specs=[whole(shape), whole(shape)],
            scratch_shapes=[pltpu.VMEM((-(-rows // 8) * 8 + height + 8, D), jnp.float32)],
        ),
        out_shape=[
            jax.ShapeDtypeStruct(shape, jnp.float32),
            jax.ShapeDtypeStruct(shape, jnp.bfloat16),
        ],
        compiler_params=LIMIT,
        cost_estimate=cost(5),
        name="collect_rows",
    )(place.reshape(1), *parts)


def reduced_piece(keep, send, leaving):
    kept = keep + swapped(send, "dp", 1).astype(jnp.float32)
    half = kept.shape[1] // 2
    groups = upper_groups()
    inner_shape = (kept.shape[0] // 4, 2, 2, half, D)
    parts = [kept[:, :half].reshape(inner_shape), kept[:, half:].reshape(inner_shape)]
    for n, order in enumerate(orders()):
        for bit in order:
            spot = 2 if bit == 1 and parts[n].ndim == 5 else 1
            stay = lax.index_in_dim(parts[n], 0, spot, keepdims=False)
            leave = lax.index_in_dim(parts[n], 1, spot, keepdims=False)
            parts[n] = stay + swapped(leave.astype(jnp.bfloat16), "space", bit).astype(jnp.float32)
    part = jnp.concatenate(parts, 1)
    part, leaving = lax.optimization_barrier((part, leaving))
    for bits in groups:
        part = part.reshape((-1, 1 << len(bits)) + part.shape[1:])
        masks = [sum(bit for n, bit in enumerate(bits) if m >> n & 1) for m in range(1 << len(bits))]
        low = part.astype(jnp.bfloat16)
        part = sum(
            [
                swapped(low[:, m], "space", mask).astype(jnp.float32)
                for m, mask in enumerate(masks)
                if m
            ],
            part[:, 0],
        )
    return part[0], leaving


def tall_parts():
    return [CH, D, D, CH] + [D, 4 * D] * ROUNDS + [2, 1] + [2] * ROUNDS


def weave(ref, value):
    rows = value.shape[0]
    ref[pl.ds(0, rows, stride=2), :] = value[:, :HALF]
    ref[pl.ds(1, rows, stride=2), :] = value[:, HALF:]


def unweave(ref):
    rows = ref.shape[0] // 2
    return ref[pl.ds(0, rows, stride=2), :], ref[pl.ds(1, rows, stride=2), :]


def selector():
    row = lax.broadcasted_iota(jnp.int32, (8, HALF), 0)
    lane = lax.broadcasted_iota(jnp.int32, (8, HALF), 1)
    slot = jnp.where(lane == CH, 64.0, jnp.where(lane == CH + 1, 1.0, 0.0))
    known = jnp.where(lane == CH + 2, 1.0, 0.0)
    return jnp.where(row == 0, slot, jnp.where(row == 1, known, 0.0)).astype(jnp.bfloat16)


def ids_along(arrived):
    codes = inner(selector(), arrived, 1, 1)
    return jnp.where(codes[1:2, :] > 0, codes[0:1, :], -1.0).astype(jnp.int32)


def ids_down(arrived):
    codes = inner(arrived, selector(), 1, 1)
    return jnp.where(codes[:, 1:2] > 0, codes[:, 0:1], -1.0).astype(jnp.int32)


def whole(shape):
    return pl.BlockSpec(shape, lambda *_: (0,) * len(shape))


def node_terms(mesh, mats, bias):
    blocks = mesh.shape[0]
    tile = 1024

    def body(mesh_ref, mats_ref, bias_ref, dest_ref, self_ref):
        lowered = mesh_ref[...].astype(jnp.bfloat16)
        weave(dest_ref, inner(lowered, mats_ref[1], 1, 0) + bias_ref[0:1, :])
        self_ref[...] = inner(lowered, mats_ref[3], 1, 0) + bias_ref[1:2, :]

    rows = pl.BlockSpec((tile, D), lambda i: (i, 0))
    woven = pl.BlockSpec((2 * tile, HALF), lambda i: (i, 0))
    return pl.pallas_call(
        body,
        grid=(blocks // tile,),
        in_specs=[rows, whole(mats.shape), whole(bias.shape)],
        out_specs=[woven, rows],
        out_shape=[
            jax.ShapeDtypeStruct((2 * blocks, HALF), jnp.float32),
            jax.ShapeDtypeStruct((blocks, D), jnp.float32),
        ],
        compiler_params=LIMIT,
        cost_estimate=cost(4),
        name="node_terms",
    )(mesh, mats, bias)


def round_forward(index, mesh, pieces, mats, terms, following, decoder=(), half=None, into=()):
    blocks = mesh.shape[0]
    tile, chunk = 512, 16
    turns, high = tile // chunk, 2 * chunk
    more = following is not None
    reach = 2 * (blocks + 2 * H)
    steps = blocks // tile if half is None else blocks // tile // 2
    shift = 0 if half is None else half * steps

    def body(index_ref, mesh_ref, *refs):
        sources, refs = refs[: len(pieces)], refs[len(pieces) :]
        (mats_ref, dest_ref, self_ref), refs = refs[:3], refs[3:]
        table, rows, wide = refs[-3:]
        if more:
            next_ref, refs = refs[0], refs[1 + len(into) :]
            new_ref, back_ref, update_ref, agg_ref, slope_ref, sent_ref = refs[:6]
        else:
            ids_ref, dec_ref, out_ref, head_ref = refs[:4]
            new_ref, back_ref, update_ref, agg_ref, slope_ref = refs[4:9]
            branch_ref, fetched_ref, decoded_ref, turn_ref, total_ref = refs[9:14]
        step = pl.program_id(0)

        @pl.when(step == 0)
        def _():
            for source, (_, start) in zip(sources, pieces):

                @pl.loop(0, source.shape[0] // 256)
                def _(i, source=source, start=start):
                    at = pl.multiple_of(i * 256, 256)
                    to = pl.multiple_of(start + at, 256)
                    table[pl.ds(to, 256), :] = source[pl.ds(at, 256), :].astype(jnp.float32)

        mesh_in = mesh_ref[...]

        def fetch(turn):
            for edge in range(K):
                base = edge * blocks + (step + shift) * tile + turn * chunk
                spots = [index_ref[base + u] for u in range(chunk)]
                values = [table[pl.ds(pl.multiple_of(spot, 2), 2), :] for spot in spots]
                for u in range(chunk):
                    spot = pl.multiple_of(edge * 2 * tile + turn * high + 2 * u, 2)
                    rows[pl.ds(spot, 2), :] = values[u]

        def load(turn):
            at = pl.multiple_of(turn * high, high)
            taken = [
                rows[pl.ds(pl.multiple_of(edge * 2 * tile + turn * high, high), high), :]
                for edge in range(K)
            ]
            return at, dest_ref[pl.ds(at, high), :], taken

        def dense(at, dest, taken):
            total = None
            for edge in range(K):
                value = taken[edge] + dest
                sigma = sigmoid(value)
                out = value * sigma
                slope_ref[edge, pl.ds(at, high), :] = (sigma + out * (1.0 - sigma)).astype(
                    jnp.bfloat16
                )
                total = out if total is None else total + out
            wide[pl.ds(at, high), :] = total * (1.0 / K)

        def some(turn, carry):
            loaded = load(turn - 1)
            fetch(turn)
            dense(*loaded)
            return carry

        fetch(0)
        lax.fori_loop(1, turns, some, 0)
        dense(*load(turns - 1))
        first, second = unweave(wide)
        first, second = first.astype(jnp.bfloat16), second.astype(jnp.bfloat16)
        agg_ref[:, :HALF] = first
        agg_ref[:, HALF:] = second
        update_in = (
            inner(first, mats_ref[2, :HALF, :], 1, 0)
            + inner(second, mats_ref[2, HALF:, :], 1, 0)
            + self_ref[...]
        )
        sigma = sigmoid(update_in)
        out = update_in * sigma
        back_ref[...] = sigma + out * (1.0 - sigma)
        update = out.astype(jnp.bfloat16)
        update_ref[...] = update
        new = mesh_in + inner(update, mats_ref[4], 1, 0)
        new_ref[...] = new
        lowered = new.astype(jnp.bfloat16)
        if more:
            weave(wide, inner(lowered, next_ref[0], 1, 0))
            sent_ref[...] = wide[...].astype(jnp.bfloat16)
            return
        nodes = lax.broadcasted_iota(jnp.int32, (ids_ref.shape[0], tile), 1) + step * tile
        chooser = jnp.where(nodes == ids_ref[...], 1.0, 0.0).astype(jnp.bfloat16)
        found = inner(chooser, lowered, 1, 0)

        @pl.when(step == 0)
        def _():
            total_ref[...] = found

        @pl.when(step > 0)
        def _():
            total_ref[...] += found

        @pl.when(step == blocks // tile - 1)
        def _():
            fetched = total_ref[...].astype(jnp.bfloat16)
            fetched_ref[...] = fetched
            value = inner(fetched, dec_ref[...], 1, 0) + head_ref[2:3, :]
            sigma = sigmoid(value)
            out = value * sigma
            turn_ref[...] = sigma + out * (1.0 - sigma)
            decoded = out.astype(jnp.bfloat16)
            decoded_ref[...] = decoded
            branch_ref[...] = inner(decoded, out_ref[...], 1, 0).astype(jnp.bfloat16)

    whole_rows = pl.BlockSpec((tile, D), lambda i, *_: (i + shift, 0))
    woven = pl.BlockSpec((2 * tile, HALF), lambda i, *_: (i + shift, 0))
    ins = [whole_rows] + [pl.BlockSpec(memory_space=pltpu.VMEM)] * len(pieces)
    ins = ins + [whole(mats.shape), woven, whole_rows]
    outs = [whole_rows] * 4 + [pl.BlockSpec((K, 2 * tile, HALF), lambda i, *_: (0, i + shift, 0))]
    shapes = [
        jax.ShapeDtypeStruct((blocks, D), jnp.float32),
        jax.ShapeDtypeStruct((blocks, D), jnp.float32),
        jax.ShapeDtypeStruct((blocks, D), jnp.bfloat16),
        jax.ShapeDtypeStruct((blocks, D), jnp.bfloat16),
        jax.ShapeDtypeStruct((K, 2 * blocks, HALF), jnp.bfloat16),
    ]
    args = [index, mesh] + [rows for rows, _ in pieces] + [mats, *terms]
    if more:
        ins.append(pl.BlockSpec((1, D, D), lambda *_: (0, 0, 0)))
        outs.append(pl.BlockSpec((2 * tile, HALF), lambda i, *_: (i, 0)))
        shapes.append(jax.ShapeDtypeStruct((2 * tile * steps, HALF), jnp.bfloat16))
        args.append(following)
    aliases = {len(args) + n: n for n in range(len(into))}
    ins = ins + [pl.BlockSpec(memory_space=pl.ANY)] * len(into)
    args = args + list(into)
    scratch = []
    if decoder:
        posts = decoder[0].shape[0]
        ins = ins + [whole(arg.shape) for arg in decoder]
        args = args + list(decoder)
        for width, kind in ((HALF, jnp.bfloat16), (D, jnp.bfloat16), (D, jnp.bfloat16), (D, jnp.float32)):
            outs.append(whole((posts, width)))
            shapes.append(jax.ShapeDtypeStruct((posts, width), kind))
        scratch = [pltpu.VMEM((posts, D), jnp.float32)]
    return pl.pallas_call(
        body,
        grid_spec=pltpu.PrefetchScalarGridSpec(
            num_scalar_prefetch=1,
            grid=(steps,),
            in_specs=ins,
            out_specs=outs,
            scratch_shapes=scratch
            + [
                pltpu.VMEM((reach, HALF), jnp.float32),
                pltpu.VMEM((K * 2 * tile, HALF), jnp.float32),
                pltpu.VMEM((2 * tile, HALF), jnp.float32),
            ],
        ),
        out_shape=shapes,
        input_output_aliases=aliases,
        compiler_params=pltpu.CompilerParams(vmem_limit_bytes=54 * 2**20),
        cost_estimate=cost(24 if half is None else 14),
        name="round_forward",
    )(*args)


def edges_backward(index, back, slopes, mats, carried=(), landed=()):
    blocks = back.shape[0]
    tile, chunk = 512, 16
    steps, turns, high = blocks // tile, tile // chunk, 2 * chunk
    reach = 2 * (blocks + 2 * H)

    def body(*refs):
        if carried:
            index_ref, back_ref, slope_ref, mats_ref = refs[:4]
            past, rest = refs[4:9], refs[9:]
            (new_ref, out_ref, sent_ref), rest = rest[:3], rest[3:]
        else:
            index_ref, back_ref, slope_ref, mats_ref = refs[:4]
            (ids_ref, landed_ref, turn_ref, w_out_ref, w_dec_ref), rest = refs[4:9], refs[9:]
            (new_ref, out_ref, gdec_ref), rest = rest[:3], rest[3:]
            gathered, rest = rest[5], rest[:5] + rest[6:]
        guin_ref, low_ref, before_ref, own_ref, after_ref, wide, wider, flows, *tables = rest
        step = pl.program_id(0)

        @pl.when(step == 0)
        def _():
            @pl.loop(0, reach // 256)
            def _(i):
                for table in tables:
                    table[pl.ds(pl.multiple_of(i * 256, 256), 256), :] = jnp.zeros(
                        (256, HALF), jnp.float32
                    )

        if carried:
            new, one, two = ended(*past, wide)
            sent_ref[:, :HALF] = one
            sent_ref[:, HALF:] = two
            new_ref[...] = new
            grad_out = new.astype(jnp.bfloat16)
            out_ref[...] = grad_out
        else:

            @pl.when(step == 0)
            def _():
                grad_dec = inner(landed_ref[...], w_out_ref[...], 1, 1) * turn_ref[...]
                grad_dec = grad_dec.astype(jnp.bfloat16)
                gdec_ref[...] = grad_dec
                gathered[...] = inner(grad_dec, w_dec_ref[...], 1, 1).astype(jnp.bfloat16)

            nodes = lax.broadcasted_iota(jnp.int32, (tile, landed_ref.shape[0]), 0) + step * tile
            chooser = jnp.where(nodes == ids_ref[...], 1.0, 0.0).astype(jnp.bfloat16)
            new = inner(chooser, gathered[...], 1, 0)
            new_ref[...] = new
            grad_out = new.astype(jnp.bfloat16)
            out_ref[...] = grad_out
        grad_uin = (inner(grad_out, mats_ref[4], 1, 1) * back_ref[...]).astype(jnp.bfloat16)
        guin_ref[...] = grad_uin
        weave(wide, inner(grad_uin, mats_ref[2], 1, 1) * (1.0 / K))

        def dense(turn):
            at = pl.multiple_of(turn * high, high)
            grad_agg = wide[pl.ds(at, high), :]
            total, parts = None, []
            for edge in range(K):
                flow = grad_agg * slope_ref[edge, pl.ds(at, high), :].astype(jnp.float32)
                parts.append(flow)
                total = flow if total is None else total + flow
            return at, total, parts

        def keep(turn, at, total, parts):
            for edge in range(K):
                spot = pl.multiple_of(edge * 2 * tile + turn * high, high)
                flows[pl.ds(spot, high), :] = parts[edge]
            wider[pl.ds(at, high), :] = total

        def scatter(turn):
            for u in range(chunk):
                spots, sums = [], []
                for edge in range(K):
                    base = edge * blocks + step * tile + turn * chunk
                    spots.append(pl.multiple_of(index_ref[base + u], 2))
                for edge in range(K):
                    spot = pl.multiple_of(edge * 2 * tile + turn * high + 2 * u, 2)
                    sums.append(tables[edge][pl.ds(spots[edge], 2), :] + flows[pl.ds(spot, 2), :])
                for edge in range(K):
                    tables[edge][pl.ds(spots[edge], 2), :] = sums[edge]

        def some(turn, carry):
            found = dense(turn)
            scatter(turn - 1)
            keep(turn, *found)
            return carry

        keep(0, *dense(0))
        lax.fori_loop(1, turns, some, 0)
        scatter(turns - 1)
        first, second = unweave(wider)
        low_ref[:, :HALF] = first.astype(jnp.bfloat16)
        low_ref[:, HALF:] = second.astype(jnp.bfloat16)

        @pl.when(step == steps - 1)
        def _():
            def summed(at):
                value = tables[0][pl.ds(at, 256), :]
                for table in tables[1:]:
                    value = value + table[pl.ds(at, 256), :]
                return value

            @pl.loop(0, 2 * H // 256)
            def _(i):
                at = pl.multiple_of(i * 256, 256)
                far = pl.multiple_of(2 * H + 2 * blocks + at, 256)
                before_ref[pl.ds(at, 256), :] = summed(at).astype(jnp.bfloat16)
                after_ref[pl.ds(at, 256), :] = summed(far).astype(jnp.bfloat16)

            @pl.loop(0, 2 * blocks // 256)
            def _(i):
                at = pl.multiple_of(i * 256, 256)
                own_ref[pl.ds(at, 256), :] = summed(pl.multiple_of(2 * H + at, 256))

    rows = pl.BlockSpec((tile, D), lambda i, *_: (i, 0))
    woven = pl.BlockSpec((2 * tile, HALF), lambda i, *_: (i, 0))
    low = jax.ShapeDtypeStruct((blocks, D), jnp.bfloat16)
    low_posts = (landed[1].shape[0], D) if landed else None
    last = low if carried else jax.ShapeDtypeStruct(low_posts, jnp.bfloat16)
    return pl.pallas_call(
        body,
        grid_spec=pltpu.PrefetchScalarGridSpec(
            num_scalar_prefetch=1,
            grid=(steps,),
            in_specs=[
                rows,
                pl.BlockSpec((K, 2 * tile, HALF), lambda i, *_: (0, i, 0)),
                whole(mats.shape),
            ]
            + ([rows] + [woven] * 3 + [whole(mats.shape)] if carried else [])
            + [whole(arg.shape) for arg in landed],
            out_specs=([rows] * 3 if carried else [rows, rows, whole(low_posts)])
            + [
                rows, rows,
                whole((2 * H, HALF)), whole((2 * blocks, HALF)), whole((2 * H, HALF)),
            ],
            scratch_shapes=([] if carried else [pltpu.VMEM(low_posts, jnp.bfloat16)])
            + [
                pltpu.VMEM((2 * tile, HALF), jnp.float32),
                pltpu.VMEM((2 * tile, HALF), jnp.float32),
                pltpu.VMEM((2 * tile * K, HALF), jnp.float32),
            ]
            + [pltpu.VMEM((reach, HALF), jnp.float32)] * K,
        ),
        out_shape=[
            jax.ShapeDtypeStruct((blocks, D), jnp.float32),
            low,
            last,
            low,
            low,
            jax.ShapeDtypeStruct((2 * H, HALF), jnp.bfloat16),
            jax.ShapeDtypeStruct((2 * blocks, HALF), jnp.float32),
            jax.ShapeDtypeStruct((2 * H, HALF), jnp.bfloat16),
        ],
        compiler_params=LIMIT,
        cost_estimate=cost(28 if carried else 25),
        name="edges_backward",
    )(index, back, slopes, mats, *carried, *landed)


def ended(part_ref, own_ref, first_ref, last_ref, mats_ref, wide):
    wide[...] = (
        own_ref[...] + first_ref[...].astype(jnp.float32) + last_ref[...].astype(jnp.float32)
    )
    one, two = unweave(wide)
    one, two = one.astype(jnp.bfloat16), two.astype(jnp.bfloat16)
    new = (
        part_ref[...]
        + inner(one, mats_ref[0, :, :HALF], 1, 1)
        + inner(two, mats_ref[0, :, HALF:], 1, 1)
    )
    return new, one, two


def weight_grads(mesh, dest_low, agg, grad_uin, update, leaving, grad_mesh, mats, past=()):
    blocks = mesh.shape[0]
    tile = 512

    def body(mesh_ref, dest_ref, agg_ref, guin_ref, update_ref, out_ref, grad_ref, mats_ref, *refs):
        if past:
            (old_ref, sent_ref), refs = refs[:2], refs[2:]
        part_ref, grads_ref, bias_ref = refs[:3]

        @pl.when(pl.program_id(0) == 0)
        def _():
            for ref in refs[1:]:
                ref[...] = jnp.zeros(ref.shape, jnp.float32)

        lowered = mesh_ref[...].astype(jnp.bfloat16)
        dest, guin = dest_ref[...], guin_ref[...]
        grads_ref[:D, :] += inner(lowered, dest, 0, 0)
        grads_ref[D : 2 * D, :] += inner(agg_ref[...], guin, 0, 0)
        grads_ref[2 * D : 3 * D, :] += inner(lowered, guin, 0, 0)
        grads_ref[3 * D :, :] += inner(update_ref[...], out_ref[...], 0, 0)
        bias_ref[0:1, :] += jnp.sum(dest.astype(jnp.float32), 0, keepdims=True)
        bias_ref[1:2, :] += jnp.sum(guin.astype(jnp.float32), 0, keepdims=True)
        part_ref[...] = (
            grad_ref[...] + inner(guin, mats_ref[3], 1, 1) + inner(dest, mats_ref[1], 1, 1)
        )
        if past:
            refs[3][...] += inner(old_ref[...].astype(jnp.bfloat16), sent_ref[...], 0, 0)

    rows = pl.BlockSpec((tile, D), lambda i: (i, 0))
    shapes = [(4 * D, D), (2, D)] + ([(D, D)] if past else [])
    return pl.pallas_call(
        body,
        grid=(blocks // tile,),
        in_specs=[rows] * 7 + [whole(mats.shape)] + [rows] * len(past),
        out_specs=[rows] + [whole(shape) for shape in shapes],
        out_shape=[jax.ShapeDtypeStruct((blocks, D), jnp.float32)]
        + [jax.ShapeDtypeStruct(shape, jnp.float32) for shape in shapes],
        compiler_params=LIMIT,
        cost_estimate=cost(10),
        name="weight_grads",
    )(mesh, dest_low, agg, grad_uin, update, leaving, grad_mesh, mats, *past)


def decode_grads(decoded, landed, fetched, grad_dec):
    def body(decoded_ref, landed_ref, fetched_ref, grad_ref, gout_ref, gdec_ref, bias_ref):
        gout_ref[...] = inner(decoded_ref[...], landed_ref[...], 0, 0)
        gdec_ref[...] = inner(fetched_ref[...], grad_ref[...], 0, 0)
        bias_ref[...] = jnp.sum(grad_ref[...].astype(jnp.float32), 0, keepdims=True)

    return pl.pallas_call(
        body,
        out_shape=[jax.ShapeDtypeStruct(shape, jnp.float32) for shape in ((D, HALF), (D, D), (1, D))],
        compiler_params=LIMIT,
        cost_estimate=cost(3),
        name="decode_grads",
    )(decoded, landed, fetched, grad_dec)


def encode_rows(arrived, w_in, w_node, biases, source):
    posts = arrived.shape[0]
    tile = 512

    def body(
        arrived_ref, in_ref, node_ref, bias_ref, source_ref,
        mesh_ref, gathered_ref, sent_ref, ids_ref, down_ref, encoded, wide,
    ):
        step = pl.program_id(0)

        @pl.when(step == 0)
        def _():
            entering = inner(arrived_ref[...], in_ref[...], 1, 0) + bias_ref[0:1, :]
            encoded[...] = silu(entering).astype(jnp.bfloat16)
            ids_ref[...] = ids_along(arrived_ref[...])
            down_ref[...] = ids_down(arrived_ref[...])

        nodes = lax.broadcasted_iota(jnp.int32, (tile, posts), 0) + step * tile
        chooser = jnp.where(nodes == ids_ref[...], 1.0, 0.0).astype(jnp.bfloat16)
        gathered = inner(chooser, encoded[...], 1, 0).astype(jnp.bfloat16)
        gathered_ref[...] = gathered
        mesh = silu(inner(gathered, node_ref[...], 1, 0) + bias_ref[1:2, :])
        mesh_ref[...] = mesh
        weave(wide, inner(mesh.astype(jnp.bfloat16), source_ref[0], 1, 0))
        sent_ref[...] = wide[...].astype(jnp.bfloat16)

    rows = pl.BlockSpec((tile, D), lambda i: (i, 0))
    args = (arrived, w_in, w_node, biases, source)
    return pl.pallas_call(
        body,
        grid=(H // tile,),
        in_specs=[whole(arg.shape) for arg in args[:-1]]
        + [pl.BlockSpec((1, D, D), lambda *_: (0, 0, 0))],
        out_specs=[rows, rows, pl.BlockSpec((2 * tile, HALF), lambda i: (i, 0))]
        + [whole((1, posts)), whole((posts, 1))],
        out_shape=[
            jax.ShapeDtypeStruct((H, D), jnp.float32),
            jax.ShapeDtypeStruct((H, D), jnp.bfloat16),
            jax.ShapeDtypeStruct((2 * H, HALF), jnp.bfloat16),
            jax.ShapeDtypeStruct((1, posts), jnp.int32),
            jax.ShapeDtypeStruct((posts, 1), jnp.int32),
        ],
        scratch_shapes=[pltpu.VMEM((posts, D), jnp.bfloat16), pltpu.VMEM((2 * tile, HALF), jnp.float32)],
        compiler_params=LIMIT,
        cost_estimate=cost(5),
        name="encode_rows",
    )(*args)


def encode_backward(carried, mesh, gathered, arrived, ids, w_in, w_node, biases):
    blocks = mesh.shape[0]
    posts = arrived.shape[0]
    tile = 512
    steps = blocks // tile

    def body(
        part_ref, own_ref, first_ref, last_ref, mats_ref,
        mesh_ref, gathered_ref, arrived_ref, ids_ref, in_ref, node_ref, bias_ref,
        new_ref, out_ref, gin_ref, gnode_ref, gbias_ref, gsource_ref, total, wide,
    ):
        step = pl.program_id(0)

        @pl.when(step == 0)
        def _():
            for ref in (total, gnode_ref, gbias_ref, gsource_ref):
                ref[...] = jnp.zeros(ref.shape, jnp.float32)

        new, one, two = ended(part_ref, own_ref, first_ref, last_ref, mats_ref, wide)
        new_ref[...] = new
        out_ref[...] = new.astype(jnp.bfloat16)
        lowered = mesh_ref[...].astype(jnp.bfloat16)
        gsource_ref[:, :HALF] += inner(lowered, one, 0, 0)
        gsource_ref[:, HALF:] += inner(lowered, two, 0, 0)
        node_in = inner(gathered_ref[...], node_ref[...], 1, 0) + bias_ref[1:2, :]
        grad_node = (new * slope(node_in)).astype(jnp.bfloat16)
        gbias_ref[1:2, :] += jnp.sum(grad_node.astype(jnp.float32), 0, keepdims=True)
        gnode_ref[...] += inner(gathered_ref[...], grad_node, 0, 0)
        back = inner(grad_node, node_ref[...], 1, 1).astype(jnp.bfloat16)
        nodes = lax.broadcasted_iota(jnp.int32, (posts, tile), 1) + step * tile
        chooser = jnp.where(nodes == ids_ref[...], 1.0, 0.0).astype(jnp.bfloat16)
        total[...] += inner(chooser, back, 1, 0)

        @pl.when(step == steps - 1)
        def _():
            entering = inner(arrived_ref[...], in_ref[...], 1, 0) + bias_ref[0:1, :]
            grad_enc = (total[...] * slope(entering)).astype(jnp.bfloat16)
            gbias_ref[0:1, :] = jnp.sum(grad_enc.astype(jnp.float32), 0, keepdims=True)
            gin_ref[...] = inner(arrived_ref[...], grad_enc, 0, 0)

    rows = pl.BlockSpec((tile, D), lambda i: (i, 0))
    woven = pl.BlockSpec((2 * tile, HALF), lambda i: (i, 0))
    args = (arrived, ids, w_in, w_node, biases)
    shapes = [(HALF, D), (D, D), (2, D), (D, D)]
    return pl.pallas_call(
        body,
        grid=(steps,),
        in_specs=[rows] + [woven] * 3 + [whole(carried[4].shape), rows, rows]
        + [whole(arg.shape) for arg in args],
        out_specs=[rows, rows] + [whole(shape) for shape in shapes],
        out_shape=[
            jax.ShapeDtypeStruct((blocks, D), jnp.float32),
            jax.ShapeDtypeStruct((blocks, D), jnp.bfloat16),
        ]
        + [jax.ShapeDtypeStruct(shape, jnp.float32) for shape in shapes],
        scratch_shapes=[pltpu.VMEM((posts, D), jnp.float32), pltpu.VMEM((2 * tile, HALF), jnp.float32)],
        compiler_params=LIMIT,
        cost_estimate=cost(10),
        name="encode_backward",
    )(*carried, mesh, gathered, *args)


def shards(walk, master, moment1, moment2, inputs, targets, valid, owner, slot, neighbours, partner):
    bands = lax.axis_size("space")
    band = lax.axis_index("space")
    peers = lax.axis_size(ALL)
    place = lax.axis_index(ALL)
    shard = master.shape[0]
    total_size = shard * peers
    height = pieces_of(total_size, peers)[3]
    offset = lax.rem(lax.rem(shard, D) * place, D)
    piece = lax.dynamic_update_slice_in_dim(
        jnp.zeros((height * D,), jnp.bfloat16), master.astype(jnp.bfloat16), offset, 0
    )
    state_in = inputs[0]
    counted = valid[0].astype(jnp.float32)
    local_count = jnp.sum(valid[0])
    digits = (local_count >> jnp.array([16, 8, 0], jnp.int32)) & 255
    digits = jnp.pad(digits, (CH + 3, HALF - CH - 6)).astype(jnp.float32)[None, :]
    points = state_in.shape[1]
    blocks = neighbours.shape[0]
    assert blocks == H
    capacity = max(2, 2 * points // bands)
    target_band = owner[0, :, 0]
    hits = (target_band[:, None] == jnp.arange(bands, dtype=jnp.int32)[None, :]).astype(jnp.int32)
    ranks = jnp.sum(jnp.cumsum(hits, 0) * hits, 1) - 1
    places_out = jnp.sum(hits * jnp.asarray(walk, jnp.int32)[None, :], 1) * capacity + ranks
    poster = (
        jnp.arange(bands * capacity, dtype=jnp.int32)[:, None] == places_out[None, :]
    ).astype(jnp.bfloat16)
    spots = slot[0][None, :]
    columns = jnp.concatenate(
        [
            state_in,
            (spots // 64).astype(jnp.bfloat16),
            (spots % 64).astype(jnp.bfloat16),
            jnp.ones((1, points), jnp.bfloat16),
            jnp.zeros((HALF - CH - 3, points), jnp.bfloat16),
        ],
        0,
    )

    def exchanged(rows):
        return lax.all_to_all(
            rows.reshape(bands, capacity, HALF), "space", split_axis=0, concat_axis=0, tiled=True
        ).reshape(bands * capacity, HALF)

    held, posted = gathered_blocks(
        piece.reshape(height, D), (inner(poster, columns, 1, 1) + digits).astype(jnp.bfloat16)
    )
    arrived = exchanged(posted)
    w_in, w_node, w_dec, w_out, *w_round, biases = spread_rows(
        held, total_size, peers, place
    )
    arrived, biases = lax.optimization_barrier((arrived, biases))
    counts = arrived.reshape(bands, capacity, HALF)[:, 0, CH + 3 : CH + 6].astype(jnp.float32)
    counts = jnp.sum(counts, 0, keepdims=True)
    w_out = jnp.pad(w_out.reshape(D, CH), ((0, 0), (0, HALF - CH)))
    w_round = [mats.reshape(5, D, D) for mats in w_round]
    b_head = biases[:3]
    b_round = biases[3:].reshape(ROUNDS, 2, D)
    mesh, gathered, sent, ids_row, ids = encode_rows(
        arrived, w_in, w_node, biases, w_round[0]
    )
    sent, partner, neighbours, counted, counts = lax.optimization_barrier(
        (sent, partner, neighbours, counted, counts)
    )
    counts = counts + swapped(counts, "dp", 1)
    index = 2 * ((neighbours - band * blocks + H) % (blocks * bands)).T.reshape(-1)
    moved = [(n, place) for n, place in enumerate(walk) if n != place]
    stays = jnp.asarray([n == place for n, place in enumerate(walk)])[band]
    index = lax.ppermute(index, "space", list(enumerate(walk)))

    def at_home(rows):
        return lax.ppermute(rows, "space", [(j, i) for i, j in moved])

    def settled(own, came):
        return jnp.where(stays, own, came.astype(jnp.float32))

    partner_by = partner - band * points - jnp.arange(points, dtype=jnp.int32)
    coded = jnp.where(partner_by >= NEAR, partner_by - NEAR + 1, 0).astype(jnp.bfloat16)
    low_valid = jnp.concatenate([counted.astype(jnp.bfloat16), coded[None, :]], 0)
    valid_around = jnp.concatenate(
        [
            shifted(low_valid[:, points - ROWW :], "space", 1),
            low_valid,
            shifted(low_valid[:, :ROWW], "space", -1),
        ],
        1,
    )
    kept = []
    sent = [sent]
    for layer in range(ROUNDS):
        pieces, start = [], 0
        arrivals = [halo(walk, sent[0], sent[0])]
        if len(sent) > 1:
            sent[1], arrivals[0] = lax.optimization_barrier((sent[1], arrivals[0]))
            arrivals.append(halo(walk, sent[1], sent[1]))
        terms = node_terms(mesh, w_round[layer], b_round[layer])
        if layer == 0:
            (before, after), valid_around, counts = lax.optimization_barrier(
                (arrivals[0], valid_around, counts)
            )
            arrivals = [(before, after)]
        for side in ([rows for rows, _ in arrivals], sent, [rows for _, rows in arrivals]):
            for rows in side:
                pieces.append((rows, start))
                start = start + rows.shape[0]
        mats = w_round[layer]
        if layer + 1 < ROUNDS:
            following = w_round[layer + 1]
            *outs, first = round_forward(index, mesh, pieces, mats, terms, following, half=0)
            *outs, second = round_forward(
                index, mesh, pieces, mats, terms, following, half=1, into=outs
            )
            sent = [first, second]
        else:
            decoder = (ids, w_dec, w_out, biases)
            outs = round_forward(index, mesh, pieces, mats, terms, None, decoder)
            outs, rest = outs[:5], outs[5:]
        kept.append((mesh, *outs[1:]))
        mesh = outs[0]
    count = counts[0, 0] * 65536.0 + counts[0, 1] * 256.0 + counts[0, 2]
    wide_valid = valid_around[:CH].astype(jnp.float32)
    coded = valid_around[CH : CH + 1, : points + ROWW].astype(jnp.float32)
    weights = [
        (
            by,
            jnp.where(coded == by - NEAR + 1, 1.0, 0.0)
            * wide_valid[:, : points + ROWW]
            * wide_valid[:, by : by + points + ROWW],
        )
        for by in range(NEAR, ROWW + 1)
    ]
    branch_rows, fetched, decoded, dec_turn = rest
    returned = exchanged(branch_rows)
    branch = inner(returned, poster, 0, 0)[:CH]
    err = state_in.astype(jnp.float32) + branch - targets[0].astype(jnp.float32)
    def widened(values):
        low = values.astype(jnp.bfloat16)
        before = shifted(low[:, points - ROWW :], "space", 1).astype(jnp.float32)
        after = shifted(low[:, :ROWW], "space", -1).astype(jnp.float32)
        return jnp.concatenate([before, values, after], 1)

    wide_err = widened(err)
    paired = jnp.zeros((CH, points + ROWW), jnp.float32)
    pair_total = jnp.zeros((CH, points), jnp.float32)
    for by, both in weights:
        gap = both * (wide_err[:, : points + ROWW] - wide_err[:, by : by + points + ROWW])
        paired = paired + gap
        pair_total = pair_total + gap[:, ROWW:] * (
            wide_err[:, ROWW : ROWW + points] - wide_err[:, ROWW + by : ROWW + by + points]
        )
    local_total = jnp.sum(counted * err * err) + 0.5 * jnp.sum(pair_total)
    grad_pred = 2.0 * counted * err + paired[:, ROWW:]
    for by, both in weights:
        gap = both * (wide_err[:, : points + ROWW] - wide_err[:, by : by + points + ROWW])
        grad_pred = grad_pred - gap[:, ROWW - by : ROWW - by + points]
    grad_pred = grad_pred / count
    grad_rows = jnp.pad(grad_pred.astype(jnp.bfloat16), ((0, HALF - CH), (0, 0)))
    landed = exchanged(inner(poster, grad_rows, 1, 1).astype(jnp.bfloat16))
    landed, final_mesh = lax.optimization_barrier((landed, mesh.astype(jnp.bfloat16)))
    final_mesh = at_home(final_mesh)
    mats_grads = [None] * (2 * ROUNDS)
    bias_grads = [None] * ROUNDS
    carried = ()
    for layer in reversed(range(ROUNDS)):
        old, back, update, agg, slopes = kept[layer]
        first_step = not carried
        grad_mesh, leaving, extra, grad_uin, dest_low, to_before, own, to_after = edges_backward(
            index, back, slopes, w_round[layer], carried,
            (ids_row, landed, dec_turn, w_out, w_dec) if first_step else (),
        )
        if first_step:
            to_before, to_after, final_mesh = lax.optimization_barrier(
                (to_before, to_after, final_mesh)
            )
        from_before, from_after = halo(walk, to_after, to_before)
        if first_step:
            grad_wout, grad_wdec, grad_bdec = decode_grads(decoded, landed, fetched, extra)
            from_before, final_mesh = lax.optimization_barrier(
                (from_before, settled(mesh, final_mesh))
            )
        past = () if first_step else (kept[layer + 1][0], extra)
        part, mats_grads[2 * layer + 1], bias_grads[layer], *source = weight_grads(
            old, dest_low, agg, grad_uin, update, leaving, grad_mesh, w_round[layer], past
        )
        if past:
            mats_grads[2 * layer + 2] = source[0]
        carried = (part, own, from_before, from_after, w_round[layer])
    grad_mesh, leaving, grad_win, grad_wnode, grad_bpair, mats_grads[0] = encode_backward(
        carried, kept[0][0], gathered, arrived, ids, w_in, w_node, biases
    )
    parts = [grad_win, grad_wnode, grad_wdec, grad_wout[:, :CH].reshape(CH, D)]
    parts = parts + mats_grads
    parts = parts + [grad_bpair, grad_bdec] + bias_grads
    keep, send = collect_rows(parts, total_size, peers, place)
    mine, leaving = reduced_piece(keep, send, leaving)
    late = at_home(leaving)
    mine = lax.dynamic_slice_in_dim(mine.reshape(-1), offset, shard)
    lane = lax.broadcasted_iota(jnp.int32, (8, HALF), 1)
    sums, late = summed_everywhere(
        jnp.where(lane == 0, local_total, jnp.sum(mine * mine)), late
    )
    total, norm = sums[0, 0], jnp.sqrt(sums[0, 1])
    node_grads = settled(grad_mesh, late)
    clipped = mine * jnp.minimum(1.0, 0.05 / norm)
    first = 0.9 * moment1 + 0.1 * clipped
    second = 0.999 * moment2 + 0.001 * clipped * clipped
    first_hat = first / (1.0 - 0.9**STEP)
    second_hat = second / (1.0 - 0.999**STEP)
    updated = master - 0.1 * (first_hat / (jnp.sqrt(second_hat) + 1e-08) + 0.1 * master)
    return (
        total.reshape(1),
        count.reshape(1),
        norm.reshape(1),
        updated,
        first,
        second,
        updated.astype(jnp.bfloat16),
        final_mesh.reshape(1, blocks, D),
        node_grads.reshape(1, blocks, D),
        grad_pred.reshape(1, grad_pred.shape[0], points),
    )


def solution(mesh):
    return jax.shard_map(
        functools.partial(shards, walk_of(mesh)),
        mesh=mesh,
        in_specs=(
            P(("dp", "space")),
            P(("dp", "space")),
            P(("dp", "space")),
            P("dp", None, "space"),
            P("dp", None, "space"),
            P("dp", None, "space"),
            P("dp", "space", None),
            P("dp", "space"),
            P("space", None),
            P("space"),
        ),
        out_specs=(
            P(),
            P(),
            P(),
            P(("dp", "space")),
            P(("dp", "space")),
            P(("dp", "space")),
            P(("dp", "space")),
            P("dp", "space", None),
            P("dp", "space", None),
            P("dp", None, "space"),
        ),
        check_vma=False,
    )
```

```python
import functools

import jax
import jax.numpy as jnp
from jax import lax
from jax.experimental import pallas as pl
from jax.experimental.pallas import tpu as pltpu
from jax.sharding import PartitionSpec as P

D = 256
HALF = 128
CH = 78
ROUNDS = 3
K = 6
ROWW = 360
NEAR = 358
STEP = 10
H = 2048
ALL = ("dp", "space")
LIMIT = pltpu.CompilerParams(vmem_limit_bytes=60 * 2**20)


def cost(micros):
    return pl.CostEstimate(flops=0, bytes_accessed=micros * 3_000_000, transcendentals=0)


def inner(left, right, left_dim, right_dim):
    return lax.dot_general(
        left, right, (((left_dim,), (right_dim,)), ((), ())), preferred_element_type=jnp.float32
    )


def sigmoid(value):
    return 0.5 * jnp.tanh(0.5 * value) + 0.5


def silu(value):
    return value * sigmoid(value)


def slope(value):
    sigma = sigmoid(value)
    return sigma * (1.0 + value * (1.0 - sigma))


def shifted(shard, axis, by):
    peers = lax.axis_size(axis)
    pairs = [(i, i + by) for i in range(peers) if 0 <= i + by < peers]
    return lax.ppermute(shard, axis, pairs)


def walk_of(mesh):
    count = mesh.shape["space"]
    chips = [getattr(device, "coords", None) for device in mesh.devices[0].reshape(-1)]
    if any(chip is None for chip in chips) or len(set(map(tuple, chips))) != count:
        return list(range(count))
    at = {tuple(chip): n for n, chip in enumerate(chips)}
    xs, ys, zs = (sorted({chip[n] for chip in at}) for n in range(3))
    if len(xs) * len(ys) * len(zs) != count:
        return list(range(count))
    if (len(xs), len(ys), len(zs)) == (2, 2, 4):
        corners = [(0, 0), (1, 0), (0, 1), (1, 1)]
        planes = [(0, 1, 3, 2), (2, 0, 1, 3), (3, 1, 0, 2), (2, 3, 1, 0)]
        steps = [(*corners[n], z) for z, plane in enumerate(planes) for n in plane]
        return [at[(xs[x], ys[y], zs[z])] for x, y, z in steps]
    walk, plane = [], []
    for n, y in enumerate(ys):
        plane = plane + [(x, y) for x in (xs if n % 2 == 0 else xs[::-1])]
    for n, z in enumerate(zs):
        walk = walk + [at[(x, y, z)] for x, y in (plane if n % 2 == 0 else plane[::-1])]
    return walk


def halo(walk, last, initial):
    up = list(zip(walk, walk[1:] + walk[:1]))
    down = [(j, i) for i, j in up]
    return lax.ppermute(last, "space", up), lax.ppermute(initial, "space", down)


def pieces_of(total, peers):
    share = total // peers
    starts = [share * d // D for d in range(peers)]
    counts = [-(-share * (d + 1) // D) - starts[d] for d in range(peers)]
    shared = [share * d % D != 0 for d in range(peers)]
    height = -(-max(counts) // 16) * 16
    return starts, counts, shared, height


def parts_of():
    return [CH, D, D, CH] + [5 * D] * ROUNDS + [3 + 2 * ROUNDS]


def swapped(value, axis, bit):
    return lax.ppermute(value, axis, [(i, i ^ bit) for i in range(lax.axis_size(axis))])


def bits_of(axis):
    return [1 << n for n in range(lax.axis_size(axis).bit_length() - 1)]


def others(value, axis, bits):
    masks = [sum(bit for n, bit in enumerate(bits) if m >> n & 1) for m in range(1, 1 << len(bits))]
    return [swapped(value, axis, mask) for mask in masks]


def upper_groups():
    bits = bits_of("space")[2:]
    return [tuple(bits[n : n + 2]) for n in range(0, len(bits), 2)]


def orders():
    return [(1, 2), (2, 1)]


def summed_everywhere(value, arriving):
    for bits in reversed(upper_groups()):
        value = sum(others(value, "space", bits), value)
    value = value + swapped(value, "dp", 1)
    value, arriving = lax.optimization_barrier((value, arriving))
    return sum(others(value, "space", (1, 2)), value), arriving


def gathered_blocks(piece, posted):
    held, weights, size = piece[None], {}, 1
    for bits in reversed(upper_groups()):
        held = jnp.concatenate([held] + others(held, "space", bits), 0)
        for n, bit in enumerate(bits):
            weights[bit] = size << n
        size = size << len(bits)
    half = piece.shape[0] // 2
    held = [held[:, :half], held[:, half:]]
    ranks = [dict(weights), dict(weights)]
    for turn in (1, 0):
        if turn == 0:
            held[0], held[1], posted = lax.optimization_barrier((*held, posted))
        for n, order in enumerate(orders()):
            held[n] = jnp.concatenate([held[n], swapped(held[n], "space", order[turn])], 0)
            ranks[n][order[turn]] = size
        size = size << 1
    return (held, [swapped(part, "dp", 1) for part in held], ranks), posted


def spread_rows(gathered, total, peers, place):
    (first, second), (first_far, second_far), ranks = gathered
    starts, counts, shared, height = pieces_of(total, peers)
    half, group = height // 2, first.shape[0]
    rows = -(-total // D)
    sizes = parts_of()
    def at(rank, relative):
        spot = 0
        for bit, weight in rank.items():
            spot = spot + jnp.where((relative & bit) != 0, weight, 0)
        return spot

    def body(place_ref, *refs):
        sources, outs, buffer = refs[:4], refs[4:-1], refs[-1]
        me = place_ref[0]
        mine = me // group
        for d in range(peers):
            relative = (me ^ d) & (group - 1)
            spots = [at(rank, relative) for rank in ranks]

            def lay(one, two, d=d, spots=spots):
                piece = jnp.concatenate([one[spots[0]], two[spots[1]]], 0).astype(jnp.float32)
                start, count = starts[d], counts[d]
                if shared[d]:
                    buffer[start : start + 1, :] = buffer[start : start + 1, :] + piece[:1]
                    buffer[start + 1 : start + count, :] = piece[1:count]
                else:
                    buffer[start : start + count, :] = piece[:count]

            @pl.when(mine == d // group)
            def _():
                lay(sources[0], sources[1])

            @pl.when(mine != d // group)
            def _():
                lay(sources[2], sources[3])

        start = 0
        for out, size in zip(outs, sizes):
            out[:size, :] = buffer[start : start + size, :].astype(out.dtype)
            if out.shape[0] > size:
                out[size:, :] = jnp.zeros((out.shape[0] - size, D), out.dtype)
            start = start + size

    kinds = [jnp.bfloat16] * (4 + ROUNDS) + [jnp.float32]
    talls = [HALF] + sizes[1:]
    return pl.pallas_call(
        body,
        grid_spec=pltpu.PrefetchScalarGridSpec(
            num_scalar_prefetch=1,
            grid=(1,),
            in_specs=[whole(first.shape)] * 4,
            out_specs=[whole((tall, D)) for tall in talls],
            scratch_shapes=[pltpu.VMEM((-(-rows // 8) * 8 + 8, D), jnp.float32)],
        ),
        out_shape=[jax.ShapeDtypeStruct((tall, D), kind) for tall, kind in zip(talls, kinds)],
        compiler_params=LIMIT,
        cost_estimate=cost(4),
        name="spread_rows",
    )(place.reshape(1), first, second, first_far, second_far)


def collect_rows(parts, total, peers, place):
    starts, counts, shared, height = pieces_of(total, peers)
    rows = -(-total // D)
    sizes = [min(part.shape[0], size) for part, size in zip(parts, tall_parts())]
    group = lax.axis_size("space")

    def body(place_ref, *refs):
        sources, keep, send, buffer = refs[:-3], refs[-3], refs[-2], refs[-1]
        start = 0
        for source, size in zip(sources, sizes):
            buffer[start : start + size, :] = source[:size, :]
            start = start + size
        if buffer.shape[0] > start:
            buffer[start:, :] = jnp.zeros((buffer.shape[0] - start, D), jnp.float32)
        me = place_ref[0]
        mine = me // group
        for d in range(peers):
            relative = (me ^ d) & (group - 1)

            @pl.when(mine == d // group)
            def _():
                keep[relative] = buffer[starts[d] : starts[d] + height, :]

            @pl.when(mine != d // group)
            def _():
                send[relative] = buffer[starts[d] : starts[d] + height, :].astype(jnp.bfloat16)

    shape = (group, height, D)
    return pl.pallas_call(
        body,
        grid_spec=pltpu.PrefetchScalarGridSpec(
            num_scalar_prefetch=1,
            grid=(1,),
            in_specs=[whole(part.shape) for part in parts],
            out_specs=[whole(shape), whole(shape)],
            scratch_shapes=[pltpu.VMEM((-(-rows // 8) * 8 + height + 8, D), jnp.float32)],
        ),
        out_shape=[
            jax.ShapeDtypeStruct(shape, jnp.float32),
            jax.ShapeDtypeStruct(shape, jnp.bfloat16),
        ],
        compiler_params=LIMIT,
        cost_estimate=cost(5),
        name="collect_rows",
    )(place.reshape(1), *parts)


def reduced_piece(keep, send, leaving):
    kept = keep + swapped(send, "dp", 1).astype(jnp.float32)
    half = kept.shape[1] // 2
    groups = upper_groups()
    inner_shape = (kept.shape[0] // 4, 2, 2, half, D)
    parts = [kept[:, :half].reshape(inner_shape), kept[:, half:].reshape(inner_shape)]
    for n, order in enumerate(orders()):
        for bit in order:
            spot = 2 if bit == 1 and parts[n].ndim == 5 else 1
            stay = lax.index_in_dim(parts[n], 0, spot, keepdims=False)
            leave = lax.index_in_dim(parts[n], 1, spot, keepdims=False)
            parts[n] = stay + swapped(leave.astype(jnp.bfloat16), "space", bit).astype(jnp.float32)
    part = jnp.concatenate(parts, 1)
    part, leaving = lax.optimization_barrier((part, leaving))
    for bits in groups:
        part = part.reshape((-1, 1 << len(bits)) + part.shape[1:])
        masks = [sum(bit for n, bit in enumerate(bits) if m >> n & 1) for m in range(1 << len(bits))]
        low = part.astype(jnp.bfloat16)
        part = sum(
            [
                swapped(low[:, m], "space", mask).astype(jnp.float32)
                for m, mask in enumerate(masks)
                if m
            ],
            part[:, 0],
        )
    return part[0], leaving


def tall_parts():
    return [CH, D, D, CH] + [D, 4 * D] * ROUNDS + [2, 1] + [2] * ROUNDS


def weave(ref, value):
    rows = value.shape[0]
    ref[pl.ds(0, rows, stride=2), :] = value[:, :HALF]
    ref[pl.ds(1, rows, stride=2), :] = value[:, HALF:]


def unweave(ref):
    rows = ref.shape[0] // 2
    return ref[pl.ds(0, rows, stride=2), :], ref[pl.ds(1, rows, stride=2), :]


def selector():
    row = lax.broadcasted_iota(jnp.int32, (8, HALF), 0)
    lane = lax.broadcasted_iota(jnp.int32, (8, HALF), 1)
    slot = jnp.where(lane == CH, 64.0, jnp.where(lane == CH + 1, 1.0, 0.0))
    known = jnp.where(lane == CH + 2, 1.0, 0.0)
    return jnp.where(row == 0, slot, jnp.where(row == 1, known, 0.0)).astype(jnp.bfloat16)


def ids_along(arrived):
    codes = inner(selector(), arrived, 1, 1)
    return jnp.where(codes[1:2, :] > 0, codes[0:1, :], -1.0).astype(jnp.int32)


def ids_down(arrived):
    codes = inner(arrived, selector(), 1, 1)
    return jnp.where(codes[:, 1:2] > 0, codes[:, 0:1], -1.0).astype(jnp.int32)


def whole(shape):
    return pl.BlockSpec(shape, lambda *_: (0,) * len(shape))


def node_terms(mesh, mats, bias):
    blocks = mesh.shape[0]
    tile = 1024

    def body(mesh_ref, mats_ref, bias_ref, dest_ref, self_ref):
        lowered = mesh_ref[...].astype(jnp.bfloat16)
        weave(dest_ref, inner(lowered, mats_ref[1], 1, 0) + bias_ref[0:1, :])
        self_ref[...] = inner(lowered, mats_ref[3], 1, 0) + bias_ref[1:2, :]

    rows = pl.BlockSpec((tile, D), lambda i: (i, 0))
    woven = pl.BlockSpec((2 * tile, HALF), lambda i: (i, 0))
    return pl.pallas_call(
        body,
        grid=(blocks // tile,),
        in_specs=[rows, whole(mats.shape), whole(bias.shape)],
        out_specs=[woven, rows],
        out_shape=[
            jax.ShapeDtypeStruct((2 * blocks, HALF), jnp.float32),
            jax.ShapeDtypeStruct((blocks, D), jnp.float32),
        ],
        compiler_params=LIMIT,
        cost_estimate=cost(4),
        name="node_terms",
    )(mesh, mats, bias)


def round_forward(index, mesh, pieces, mats, terms, following, decoder=(), half=None, into=()):
    blocks = mesh.shape[0]
    tile, chunk = 512, 16
    turns, high = tile // chunk, 2 * chunk
    more = following is not None
    reach = 2 * (blocks + 2 * H)
    steps = blocks // tile if half is None else blocks // tile // 2
    shift = 0 if half is None else half * steps

    def body(index_ref, mesh_ref, *refs):
        sources, refs = refs[: len(pieces)], refs[len(pieces) :]
        (mats_ref, dest_ref, self_ref), refs = refs[:3], refs[3:]
        table, rows, wide = refs[-3:]
        if more:
            next_ref, refs = refs[0], refs[1 + len(into) :]
            new_ref, back_ref, update_ref, agg_ref, slope_ref, sent_ref = refs[:6]
        else:
            ids_ref, dec_ref, out_ref, head_ref = refs[:4]
            new_ref, back_ref, update_ref, agg_ref, slope_ref = refs[4:9]
            branch_ref, fetched_ref, decoded_ref, turn_ref, total_ref = refs[9:14]
        step = pl.program_id(0)

        @pl.when(step == 0)
        def _():
            for source, (_, start) in zip(sources, pieces):

                @pl.loop(0, source.shape[0] // 256)
                def _(i, source=source, start=start):
                    at = pl.multiple_of(i * 256, 256)
                    to = pl.multiple_of(start + at, 256)
                    table[pl.ds(to, 256), :] = source[pl.ds(at, 256), :].astype(jnp.float32)

        mesh_in = mesh_ref[...]

        part = blocks // 2
        if half is None:
            origin = step // (steps // 2) * (K * part) + lax.rem(step, steps // 2) * tile
        else:
            origin = step * tile

        def fetch(turn):
            for edge in range(K):
                base = edge * part + turn * chunk + origin
                spots = [index_ref[base + u] for u in range(chunk)]
                values = [table[pl.ds(pl.multiple_of(spot, 2), 2), :] for spot in spots]
                for u in range(chunk):
                    spot = pl.multiple_of(edge * 2 * tile + turn * high + 2 * u, 2)
                    rows[pl.ds(spot, 2), :] = values[u]

        def load(turn):
            at = pl.multiple_of(turn * high, high)
            taken = [
                rows[pl.ds(pl.multiple_of(edge * 2 * tile + turn * high, high), high), :]
                for edge in range(K)
            ]
            return at, dest_ref[pl.ds(at, high), :], taken

        def dense(at, dest, taken):
            total = None
            for edge in range(K):
                value = taken[edge] + dest
                sigma = sigmoid(value)
                out = value * sigma
                slope_ref[edge, pl.ds(at, high), :] = (sigma + out * (1.0 - sigma)).astype(
                    jnp.bfloat16
                )
                total = out if total is None else total + out
            wide[pl.ds(at, high), :] = total * (1.0 / K)

        def some(turn, carry):
            loaded = load(turn - 1)
            fetch(turn)
            dense(*loaded)
            return carry

        fetch(0)
        lax.fori_loop(1, turns, some, 0)
        dense(*load(turns - 1))
        first, second = unweave(wide)
        first, second = first.astype(jnp.bfloat16), second.astype(jnp.bfloat16)
        agg_ref[:, :HALF] = first
        agg_ref[:, HALF:] = second
        update_in = (
            inner(first, mats_ref[2, :HALF, :], 1, 0)
            + inner(second, mats_ref[2, HALF:, :], 1, 0)
            + self_ref[...]
        )
        sigma = sigmoid(update_in)
        out = update_in * sigma
        back_ref[...] = sigma + out * (1.0 - sigma)
        update = out.astype(jnp.bfloat16)
        update_ref[...] = update
        new = mesh_in + inner(update, mats_ref[4], 1, 0)
        new_ref[...] = new
        lowered = new.astype(jnp.bfloat16)
        if more:
            weave(wide, inner(lowered, next_ref[0], 1, 0))
            sent_ref[...] = wide[...].astype(jnp.bfloat16)
            return
        nodes = lax.broadcasted_iota(jnp.int32, (ids_ref.shape[0], tile), 1) + step * tile
        chooser = jnp.where(nodes == ids_ref[...], 1.0, 0.0).astype(jnp.bfloat16)
        found = inner(chooser, lowered, 1, 0)

        @pl.when(step == 0)
        def _():
            total_ref[...] = found

        @pl.when(step > 0)
        def _():
            total_ref[...] += found

        @pl.when(step == blocks // tile - 1)
        def _():
            fetched = total_ref[...].astype(jnp.bfloat16)
            fetched_ref[...] = fetched
            value = inner(fetched, dec_ref[...], 1, 0) + head_ref[2:3, :]
            sigma = sigmoid(value)
            out = value * sigma
            turn_ref[...] = sigma + out * (1.0 - sigma)
            decoded = out.astype(jnp.bfloat16)
            decoded_ref[...] = decoded
            branch_ref[...] = inner(decoded, out_ref[...], 1, 0).astype(jnp.bfloat16)

    whole_rows = pl.BlockSpec((tile, D), lambda i, *_: (i + shift, 0))
    woven = pl.BlockSpec((2 * tile, HALF), lambda i, *_: (i + shift, 0))
    ins = [whole_rows] + [pl.BlockSpec(memory_space=pltpu.VMEM)] * len(pieces)
    ins = ins + [whole(mats.shape), woven, whole_rows]
    outs = [whole_rows] * 4 + [pl.BlockSpec((K, 2 * tile, HALF), lambda i, *_: (0, i + shift, 0))]
    shapes = [
        jax.ShapeDtypeStruct((blocks, D), jnp.float32),
        jax.ShapeDtypeStruct((blocks, D), jnp.float32),
        jax.ShapeDtypeStruct((blocks, D), jnp.bfloat16),
        jax.ShapeDtypeStruct((blocks, D), jnp.bfloat16),
        jax.ShapeDtypeStruct((K, 2 * blocks, HALF), jnp.bfloat16),
    ]
    args = [index, mesh] + [rows for rows, _ in pieces] + [mats, *terms]
    if more:
        ins.append(pl.BlockSpec((1, D, D), lambda *_: (0, 0, 0)))
        outs.append(pl.BlockSpec((2 * tile, HALF), lambda i, *_: (i, 0)))
        shapes.append(jax.ShapeDtypeStruct((2 * tile * steps, HALF), jnp.bfloat16))
        args.append(following)
    aliases = {len(args) + n: n for n in range(len(into))}
    ins = ins + [pl.BlockSpec(memory_space=pl.ANY)] * len(into)
    args = args + list(into)
    scratch = []
    if decoder:
        posts = decoder[0].shape[0]
        ins = ins + [whole(arg.shape) for arg in decoder]
        args = args + list(decoder)
        for width, kind in ((HALF, jnp.bfloat16), (D, jnp.bfloat16), (D, jnp.bfloat16), (D, jnp.float32)):
            outs.append(whole((posts, width)))
            shapes.append(jax.ShapeDtypeStruct((posts, width), kind))
        scratch = [pltpu.VMEM((posts, D), jnp.float32)]
    return pl.pallas_call(
        body,
        grid_spec=pltpu.PrefetchScalarGridSpec(
            num_scalar_prefetch=1,
            grid=(steps,),
            in_specs=ins,
            out_specs=outs,
            scratch_shapes=scratch
            + [
                pltpu.VMEM((reach, HALF), jnp.float32),
                pltpu.VMEM((K * 2 * tile, HALF), jnp.float32),
                pltpu.VMEM((2 * tile, HALF), jnp.float32),
            ],
        ),
        out_shape=shapes,
        input_output_aliases=aliases,
        compiler_params=pltpu.CompilerParams(vmem_limit_bytes=54 * 2**20),
        cost_estimate=cost(24 if half is None else 14),
        name="round_forward",
    )(*args)


def edges_backward(index, back, slopes, mats, carried=(), landed=()):
    blocks = back.shape[0]
    tile, chunk = 512, 16
    steps, turns, high = blocks // tile, tile // chunk, 2 * chunk
    reach = 2 * (blocks + 2 * H)

    def body(*refs):
        if carried:
            index_ref, back_ref, slope_ref, mats_ref = refs[:4]
            past, rest = refs[4:9], refs[9:]
            (new_ref, out_ref, sent_ref), rest = rest[:3], rest[3:]
        else:
            index_ref, back_ref, slope_ref, mats_ref = refs[:4]
            (ids_ref, landed_ref, turn_ref, w_out_ref, w_dec_ref), rest = refs[4:9], refs[9:]
            (new_ref, out_ref, gdec_ref), rest = rest[:3], rest[3:]
            gathered, rest = rest[5], rest[:5] + rest[6:]
        guin_ref, low_ref, before_ref, own_ref, after_ref, wide, wider, flows, *tables = rest
        step = pl.program_id(0)

        @pl.when(step == 0)
        def _():
            @pl.loop(0, reach // 256)
            def _(i):
                for table in tables:
                    table[pl.ds(pl.multiple_of(i * 256, 256), 256), :] = jnp.zeros(
                        (256, HALF), jnp.float32
                    )

        if carried:
            new, one, two = ended(*past, wide)
            sent_ref[:, :HALF] = one
            sent_ref[:, HALF:] = two
            new_ref[...] = new
            grad_out = new.astype(jnp.bfloat16)
            out_ref[...] = grad_out
        else:

            @pl.when(step == 0)
            def _():
                grad_dec = inner(landed_ref[...], w_out_ref[...], 1, 1) * turn_ref[...]
                grad_dec = grad_dec.astype(jnp.bfloat16)
                gdec_ref[...] = grad_dec
                gathered[...] = inner(grad_dec, w_dec_ref[...], 1, 1).astype(jnp.bfloat16)

            nodes = lax.broadcasted_iota(jnp.int32, (tile, landed_ref.shape[0]), 0) + step * tile
            chooser = jnp.where(nodes == ids_ref[...], 1.0, 0.0).astype(jnp.bfloat16)
            new = inner(chooser, gathered[...], 1, 0)
            new_ref[...] = new
            grad_out = new.astype(jnp.bfloat16)
            out_ref[...] = grad_out
        grad_uin = (inner(grad_out, mats_ref[4], 1, 1) * back_ref[...]).astype(jnp.bfloat16)
        guin_ref[...] = grad_uin
        weave(wide, inner(grad_uin, mats_ref[2], 1, 1) * (1.0 / K))

        def dense(turn):
            at = pl.multiple_of(turn * high, high)
            grad_agg = wide[pl.ds(at, high), :]
            total, parts = None, []
            for edge in range(K):
                flow = grad_agg * slope_ref[edge, pl.ds(at, high), :].astype(jnp.float32)
                parts.append(flow)
                total = flow if total is None else total + flow
            return at, total, parts

        def keep(turn, at, total, parts):
            for edge in range(K):
                spot = pl.multiple_of(edge * 2 * tile + turn * high, high)
                flows[pl.ds(spot, high), :] = parts[edge]
            wider[pl.ds(at, high), :] = total

        part = blocks // 2
        origin = step // (steps // 2) * (K * part) + lax.rem(step, steps // 2) * tile

        def scatter(turn):
            for u in range(chunk):
                spots, sums = [], []
                for edge in range(K):
                    base = edge * part + turn * chunk + origin
                    spots.append(pl.multiple_of(index_ref[base + u], 2))
                for edge in range(K):
                    spot = pl.multiple_of(edge * 2 * tile + turn * high + 2 * u, 2)
                    sums.append(tables[edge][pl.ds(spots[edge], 2), :] + flows[pl.ds(spot, 2), :])
                for edge in range(K):
                    tables[edge][pl.ds(spots[edge], 2), :] = sums[edge]

        def some(turn, carry):
            found = dense(turn)
            scatter(turn - 1)
            keep(turn, *found)
            return carry

        keep(0, *dense(0))
        lax.fori_loop(1, turns, some, 0)
        scatter(turns - 1)
        first, second = unweave(wider)
        low_ref[:, :HALF] = first.astype(jnp.bfloat16)
        low_ref[:, HALF:] = second.astype(jnp.bfloat16)

        @pl.when(step == steps - 1)
        def _():
            def summed(at):
                value = tables[0][pl.ds(at, 256), :]
                for table in tables[1:]:
                    value = value + table[pl.ds(at, 256), :]
                return value

            @pl.loop(0, 2 * H // 256)
            def _(i):
                at = pl.multiple_of(i * 256, 256)
                far = pl.multiple_of(2 * H + 2 * blocks + at, 256)
                before_ref[pl.ds(at, 256), :] = summed(at).astype(jnp.bfloat16)
                after_ref[pl.ds(at, 256), :] = summed(far).astype(jnp.bfloat16)

            @pl.loop(0, 2 * blocks // 256)
            def _(i):
                at = pl.multiple_of(i * 256, 256)
                own_ref[pl.ds(at, 256), :] = summed(pl.multiple_of(2 * H + at, 256))

    rows = pl.BlockSpec((tile, D), lambda i, *_: (i, 0))
    woven = pl.BlockSpec((2 * tile, HALF), lambda i, *_: (i, 0))
    low = jax.ShapeDtypeStruct((blocks, D), jnp.bfloat16)
    low_posts = (landed[1].shape[0], D) if landed else None
    last = low if carried else jax.ShapeDtypeStruct(low_posts, jnp.bfloat16)
    return pl.pallas_call(
        body,
        grid_spec=pltpu.PrefetchScalarGridSpec(
            num_scalar_prefetch=1,
            grid=(steps,),
            in_specs=[
                rows,
                pl.BlockSpec((K, 2 * tile, HALF), lambda i, *_: (0, i, 0)),
                whole(mats.shape),
            ]
            + ([rows] + [woven] * 3 + [whole(mats.shape)] if carried else [])
            + [whole(arg.shape) for arg in landed],
            out_specs=([rows] * 3 if carried else [rows, rows, whole(low_posts)])
            + [
                rows, rows,
                whole((2 * H, HALF)), whole((2 * blocks, HALF)), whole((2 * H, HALF)),
            ],
            scratch_shapes=([] if carried else [pltpu.VMEM(low_posts, jnp.bfloat16)])
            + [
                pltpu.VMEM((2 * tile, HALF), jnp.float32),
                pltpu.VMEM((2 * tile, HALF), jnp.float32),
                pltpu.VMEM((2 * tile * K, HALF), jnp.float32),
            ]
            + [pltpu.VMEM((reach, HALF), jnp.float32)] * K,
        ),
        out_shape=[
            jax.ShapeDtypeStruct((blocks, D), jnp.float32),
            low,
            last,
            low,
            low,
            jax.ShapeDtypeStruct((2 * H, HALF), jnp.bfloat16),
            jax.ShapeDtypeStruct((2 * blocks, HALF), jnp.float32),
            jax.ShapeDtypeStruct((2 * H, HALF), jnp.bfloat16),
        ],
        compiler_params=LIMIT,
        cost_estimate=cost(28 if carried else 25),
        name="edges_backward",
    )(index, back, slopes, mats, *carried, *landed)


def ended(part_ref, own_ref, first_ref, last_ref, mats_ref, wide):
    wide[...] = (
        own_ref[...] + first_ref[...].astype(jnp.float32) + last_ref[...].astype(jnp.float32)
    )
    one, two = unweave(wide)
    one, two = one.astype(jnp.bfloat16), two.astype(jnp.bfloat16)
    new = (
        part_ref[...]
        + inner(one, mats_ref[0, :, :HALF], 1, 1)
        + inner(two, mats_ref[0, :, HALF:], 1, 1)
    )
    return new, one, two


def weight_grads(mesh, dest_low, agg, grad_uin, update, leaving, grad_mesh, mats, past=()):
    blocks = mesh.shape[0]
    tile = 512

    def body(mesh_ref, dest_ref, agg_ref, guin_ref, update_ref, out_ref, grad_ref, mats_ref, *refs):
        if past:
            (old_ref, sent_ref), refs = refs[:2], refs[2:]
        part_ref, grads_ref, bias_ref = refs[:3]

        @pl.when(pl.program_id(0) == 0)
        def _():
            for ref in refs[1:]:
                ref[...] = jnp.zeros(ref.shape, jnp.float32)

        lowered = mesh_ref[...].astype(jnp.bfloat16)
        dest, guin = dest_ref[...], guin_ref[...]
        grads_ref[:D, :] += inner(lowered, dest, 0, 0)
        grads_ref[D : 2 * D, :] += inner(agg_ref[...], guin, 0, 0)
        grads_ref[2 * D : 3 * D, :] += inner(lowered, guin, 0, 0)
        grads_ref[3 * D :, :] += inner(update_ref[...], out_ref[...], 0, 0)
        bias_ref[0:1, :] += jnp.sum(dest.astype(jnp.float32), 0, keepdims=True)
        bias_ref[1:2, :] += jnp.sum(guin.astype(jnp.float32), 0, keepdims=True)
        part_ref[...] = (
            grad_ref[...] + inner(guin, mats_ref[3], 1, 1) + inner(dest, mats_ref[1], 1, 1)
        )
        if past:
            refs[3][...] += inner(old_ref[...].astype(jnp.bfloat16), sent_ref[...], 0, 0)

    rows = pl.BlockSpec((tile, D), lambda i: (i, 0))
    shapes = [(4 * D, D), (2, D)] + ([(D, D)] if past else [])
    return pl.pallas_call(
        body,
        grid=(blocks // tile,),
        in_specs=[rows] * 7 + [whole(mats.shape)] + [rows] * len(past),
        out_specs=[rows] + [whole(shape) for shape in shapes],
        out_shape=[jax.ShapeDtypeStruct((blocks, D), jnp.float32)]
        + [jax.ShapeDtypeStruct(shape, jnp.float32) for shape in shapes],
        compiler_params=LIMIT,
        cost_estimate=cost(10),
        name="weight_grads",
    )(mesh, dest_low, agg, grad_uin, update, leaving, grad_mesh, mats, *past)


def decode_grads(decoded, landed, fetched, grad_dec):
    def body(decoded_ref, landed_ref, fetched_ref, grad_ref, gout_ref, gdec_ref, bias_ref):
        gout_ref[...] = inner(decoded_ref[...], landed_ref[...], 0, 0)
        gdec_ref[...] = inner(fetched_ref[...], grad_ref[...], 0, 0)
        bias_ref[...] = jnp.sum(grad_ref[...].astype(jnp.float32), 0, keepdims=True)

    return pl.pallas_call(
        body,
        out_shape=[jax.ShapeDtypeStruct(shape, jnp.float32) for shape in ((D, HALF), (D, D), (1, D))],
        compiler_params=LIMIT,
        cost_estimate=cost(3),
        name="decode_grads",
    )(decoded, landed, fetched, grad_dec)


def encode_rows(arrived, w_in, w_node, biases, source):
    posts = arrived.shape[0]
    tile = 512

    def body(
        arrived_ref, in_ref, node_ref, bias_ref, source_ref,
        mesh_ref, gathered_ref, sent_ref, ids_ref, down_ref, encoded, wide,
    ):
        step = pl.program_id(0)

        @pl.when(step == 0)
        def _():
            entering = inner(arrived_ref[...], in_ref[...], 1, 0) + bias_ref[0:1, :]
            encoded[...] = silu(entering).astype(jnp.bfloat16)
            ids_ref[...] = ids_along(arrived_ref[...])
            down_ref[...] = ids_down(arrived_ref[...])

        nodes = lax.broadcasted_iota(jnp.int32, (tile, posts), 0) + step * tile
        chooser = jnp.where(nodes == ids_ref[...], 1.0, 0.0).astype(jnp.bfloat16)
        gathered = inner(chooser, encoded[...], 1, 0).astype(jnp.bfloat16)
        gathered_ref[...] = gathered
        mesh = silu(inner(gathered, node_ref[...], 1, 0) + bias_ref[1:2, :])
        mesh_ref[...] = mesh
        weave(wide, inner(mesh.astype(jnp.bfloat16), source_ref[0], 1, 0))
        sent_ref[...] = wide[...].astype(jnp.bfloat16)

    rows = pl.BlockSpec((tile, D), lambda i: (i, 0))
    args = (arrived, w_in, w_node, biases, source)
    return pl.pallas_call(
        body,
        grid=(H // tile,),
        in_specs=[whole(arg.shape) for arg in args[:-1]]
        + [pl.BlockSpec((1, D, D), lambda *_: (0, 0, 0))],
        out_specs=[rows, rows, pl.BlockSpec((2 * tile, HALF), lambda i: (i, 0))]
        + [whole((1, posts)), whole((posts, 1))],
        out_shape=[
            jax.ShapeDtypeStruct((H, D), jnp.float32),
            jax.ShapeDtypeStruct((H, D), jnp.bfloat16),
            jax.ShapeDtypeStruct((2 * H, HALF), jnp.bfloat16),
            jax.ShapeDtypeStruct((1, posts), jnp.int32),
            jax.ShapeDtypeStruct((posts, 1), jnp.int32),
        ],
        scratch_shapes=[pltpu.VMEM((posts, D), jnp.bfloat16), pltpu.VMEM((2 * tile, HALF), jnp.float32)],
        compiler_params=LIMIT,
        cost_estimate=cost(5),
        name="encode_rows",
    )(*args)


def encode_backward(carried, mesh, gathered, arrived, ids, w_in, w_node, biases):
    blocks = mesh.shape[0]
    posts = arrived.shape[0]
    tile = 512
    steps = blocks // tile

    def body(
        part_ref, own_ref, first_ref, last_ref, mats_ref,
        mesh_ref, gathered_ref, arrived_ref, ids_ref, in_ref, node_ref, bias_ref,
        new_ref, out_ref, gin_ref, gnode_ref, gbias_ref, gsource_ref, total, wide,
    ):
        step = pl.program_id(0)

        @pl.when(step == 0)
        def _():
            for ref in (total, gnode_ref, gbias_ref, gsource_ref):
                ref[...] = jnp.zeros(ref.shape, jnp.float32)

        new, one, two = ended(part_ref, own_ref, first_ref, last_ref, mats_ref, wide)
        new_ref[...] = new
        out_ref[...] = new.astype(jnp.bfloat16)
        lowered = mesh_ref[...].astype(jnp.bfloat16)
        gsource_ref[:, :HALF] += inner(lowered, one, 0, 0)
        gsource_ref[:, HALF:] += inner(lowered, two, 0, 0)
        node_in = inner(gathered_ref[...], node_ref[...], 1, 0) + bias_ref[1:2, :]
        grad_node = (new * slope(node_in)).astype(jnp.bfloat16)
        gbias_ref[1:2, :] += jnp.sum(grad_node.astype(jnp.float32), 0, keepdims=True)
        gnode_ref[...] += inner(gathered_ref[...], grad_node, 0, 0)
        back = inner(grad_node, node_ref[...], 1, 1).astype(jnp.bfloat16)
        nodes = lax.broadcasted_iota(jnp.int32, (posts, tile), 1) + step * tile
        chooser = jnp.where(nodes == ids_ref[...], 1.0, 0.0).astype(jnp.bfloat16)
        total[...] += inner(chooser, back, 1, 0)

        @pl.when(step == steps - 1)
        def _():
            entering = inner(arrived_ref[...], in_ref[...], 1, 0) + bias_ref[0:1, :]
            grad_enc = (total[...] * slope(entering)).astype(jnp.bfloat16)
            gbias_ref[0:1, :] = jnp.sum(grad_enc.astype(jnp.float32), 0, keepdims=True)
            gin_ref[...] = inner(arrived_ref[...], grad_enc, 0, 0)

    rows = pl.BlockSpec((tile, D), lambda i: (i, 0))
    woven = pl.BlockSpec((2 * tile, HALF), lambda i: (i, 0))
    args = (arrived, ids, w_in, w_node, biases)
    shapes = [(HALF, D), (D, D), (2, D), (D, D)]
    return pl.pallas_call(
        body,
        grid=(steps,),
        in_specs=[rows] + [woven] * 3 + [whole(carried[4].shape), rows, rows]
        + [whole(arg.shape) for arg in args],
        out_specs=[rows, rows] + [whole(shape) for shape in shapes],
        out_shape=[
            jax.ShapeDtypeStruct((blocks, D), jnp.float32),
            jax.ShapeDtypeStruct((blocks, D), jnp.bfloat16),
        ]
        + [jax.ShapeDtypeStruct(shape, jnp.float32) for shape in shapes],
        scratch_shapes=[pltpu.VMEM((posts, D), jnp.float32), pltpu.VMEM((2 * tile, HALF), jnp.float32)],
        compiler_params=LIMIT,
        cost_estimate=cost(10),
        name="encode_backward",
    )(*carried, mesh, gathered, *args)


def shards(walk, master, moment1, moment2, inputs, targets, valid, owner, slot, neighbours, partner):
    bands = lax.axis_size("space")
    band = lax.axis_index("space")
    peers = lax.axis_size(ALL)
    place = lax.axis_index(ALL)
    shard = master.shape[0]
    total_size = shard * peers
    height = pieces_of(total_size, peers)[3]
    offset = lax.rem(lax.rem(shard, D) * place, D)
    piece = lax.dynamic_update_slice_in_dim(
        jnp.zeros((height * D,), jnp.bfloat16), master.astype(jnp.bfloat16), offset, 0
    )
    state_in = inputs[0]
    counted = valid[0].astype(jnp.float32)
    local_count = jnp.sum(valid[0])
    digits = (local_count >> jnp.array([16, 8, 0], jnp.int32)) & 255
    digits = jnp.pad(digits, (CH + 3, HALF - CH - 6)).astype(jnp.float32)[None, :]
    points = state_in.shape[1]
    blocks = neighbours.shape[0]
    assert blocks == H
    capacity = max(2, 2 * points // bands)
    target_band = owner[0, :, 0]
    hits = (target_band[:, None] == jnp.arange(bands, dtype=jnp.int32)[None, :]).astype(jnp.int32)
    ranks = jnp.sum(jnp.cumsum(hits, 0) * hits, 1) - 1
    places_out = jnp.sum(hits * jnp.asarray(walk, jnp.int32)[None, :], 1) * capacity + ranks
    poster = (
        jnp.arange(bands * capacity, dtype=jnp.int32)[:, None] == places_out[None, :]
    ).astype(jnp.bfloat16)
    spots = slot[0][None, :]
    columns = jnp.concatenate(
        [
            state_in,
            (spots // 64).astype(jnp.bfloat16),
            (spots % 64).astype(jnp.bfloat16),
            jnp.ones((1, points), jnp.bfloat16),
            jnp.zeros((HALF - CH - 3, points), jnp.bfloat16),
        ],
        0,
    )

    def exchanged(rows):
        return lax.all_to_all(
            rows.reshape(bands, capacity, HALF), "space", split_axis=0, concat_axis=0, tiled=True
        ).reshape(bands * capacity, HALF)

    held, posted = gathered_blocks(
        piece.reshape(height, D), (inner(poster, columns, 1, 1) + digits).astype(jnp.bfloat16)
    )
    arrived = exchanged(posted)
    w_in, w_node, w_dec, w_out, *w_round, biases = spread_rows(
        held, total_size, peers, place
    )
    arrived, biases = lax.optimization_barrier((arrived, biases))
    counts = arrived.reshape(bands, capacity, HALF)[:, 0, CH + 3 : CH + 6].astype(jnp.float32)
    counts = jnp.sum(counts, 0, keepdims=True)
    w_out = jnp.pad(w_out.reshape(D, CH), ((0, 0), (0, HALF - CH)))
    w_round = [mats.reshape(5, D, D) for mats in w_round]
    b_head = biases[:3]
    b_round = biases[3:].reshape(ROUNDS, 2, D)
    mesh, gathered, sent, ids_row, ids = encode_rows(
        arrived, w_in, w_node, biases, w_round[0]
    )
    sent, partner, neighbours, counted, counts = lax.optimization_barrier(
        (sent, partner, neighbours, counted, counts)
    )
    counts = counts + swapped(counts, "dp", 1)
    index = 2 * ((neighbours - band * blocks + H) % (blocks * bands)).T
    index = index.reshape(K, 2, blocks // 2).swapaxes(0, 1).reshape(-1)
    moved = [(n, place) for n, place in enumerate(walk) if n != place]
    stays = jnp.asarray([n == place for n, place in enumerate(walk)])[band]
    index = lax.ppermute(index, "space", list(enumerate(walk)))

    def at_home(rows):
        return lax.ppermute(rows, "space", [(j, i) for i, j in moved])

    def settled(own, came):
        return jnp.where(stays, own, came.astype(jnp.float32))

    partner_by = partner - band * points - jnp.arange(points, dtype=jnp.int32)
    coded = jnp.where(partner_by >= NEAR, partner_by - NEAR + 1, 0).astype(jnp.bfloat16)
    low_valid = jnp.concatenate([counted.astype(jnp.bfloat16), coded[None, :]], 0)
    valid_around = jnp.concatenate(
        [
            shifted(low_valid[:, points - ROWW :], "space", 1),
            low_valid,
            shifted(low_valid[:, :ROWW], "space", -1),
        ],
        1,
    )
    kept = []
    sent = [sent]
    for layer in range(ROUNDS):
        pieces, start = [], 0
        arrivals = [halo(walk, sent[0], sent[0])]
        if len(sent) > 1:
            sent[1], arrivals[0] = lax.optimization_barrier((sent[1], arrivals[0]))
            arrivals.append(halo(walk, sent[1], sent[1]))
        terms = node_terms(mesh, w_round[layer], b_round[layer])
        if layer == 0:
            (before, after), valid_around, counts = lax.optimization_barrier(
                (arrivals[0], valid_around, counts)
            )
            arrivals = [(before, after)]
        for side in ([rows for rows, _ in arrivals], sent, [rows for _, rows in arrivals]):
            for rows in side:
                pieces.append((rows, start))
                start = start + rows.shape[0]
        mats = w_round[layer]
        if layer + 1 < ROUNDS:
            following = w_round[layer + 1]
            reached = [pieces, pieces] if layer == 0 else [pieces[:-1], pieces[1:]]
            indexes = [index[: K * blocks // 2], index[K * blocks // 2 :]]
            *outs, first = round_forward(
                indexes[0], mesh, reached[0], mats, terms, following, half=0
            )
            *outs, second = round_forward(
                indexes[1], mesh, reached[1], mats, terms, following, half=1, into=outs
            )
            sent = [first, second]
        else:
            decoder = (ids, w_dec, w_out, biases)
            outs = round_forward(index, mesh, pieces, mats, terms, None, decoder)
            outs, rest = outs[:5], outs[5:]
        kept.append((mesh, *outs[1:]))
        mesh = outs[0]
    count = counts[0, 0] * 65536.0 + counts[0, 1] * 256.0 + counts[0, 2]
    wide_valid = valid_around[:CH].astype(jnp.float32)
    coded = valid_around[CH : CH + 1, : points + ROWW].astype(jnp.float32)
    weights = [
        (
            by,
            jnp.where(coded == by - NEAR + 1, 1.0, 0.0)
            * wide_valid[:, : points + ROWW]
            * wide_valid[:, by : by + points + ROWW],
        )
        for by in range(NEAR, ROWW + 1)
    ]
    branch_rows, fetched, decoded, dec_turn = rest
    returned = exchanged(branch_rows)
    branch = inner(returned, poster, 0, 0)[:CH]
    err = state_in.astype(jnp.float32) + branch - targets[0].astype(jnp.float32)
    def widened(values):
        low = values.astype(jnp.bfloat16)
        before = shifted(low[:, points - ROWW :], "space", 1).astype(jnp.float32)
        after = shifted(low[:, :ROWW], "space", -1).astype(jnp.float32)
        return jnp.concatenate([before, values, after], 1)

    wide_err = widened(err)
    paired = jnp.zeros((CH, points + ROWW), jnp.float32)
    pair_total = jnp.zeros((CH, points), jnp.float32)
    for by, both in weights:
        gap = both * (wide_err[:, : points + ROWW] - wide_err[:, by : by + points + ROWW])
        paired = paired + gap
        pair_total = pair_total + gap[:, ROWW:] * (
            wide_err[:, ROWW : ROWW + points] - wide_err[:, ROWW + by : ROWW + by + points]
        )
    local_total = jnp.sum(counted * err * err) + 0.5 * jnp.sum(pair_total)
    grad_pred = 2.0 * counted * err + paired[:, ROWW:]
    for by, both in weights:
        gap = both * (wide_err[:, : points + ROWW] - wide_err[:, by : by + points + ROWW])
        grad_pred = grad_pred - gap[:, ROWW - by : ROWW - by + points]
    grad_pred = grad_pred / count
    grad_rows = jnp.pad(grad_pred.astype(jnp.bfloat16), ((0, HALF - CH), (0, 0)))
    landed = exchanged(inner(poster, grad_rows, 1, 1).astype(jnp.bfloat16))
    landed, final_mesh = lax.optimization_barrier((landed, mesh.astype(jnp.bfloat16)))
    final_mesh = at_home(final_mesh)
    mats_grads = [None] * (2 * ROUNDS)
    bias_grads = [None] * ROUNDS
    carried = ()
    for layer in reversed(range(ROUNDS)):
        old, back, update, agg, slopes = kept[layer]
        first_step = not carried
        grad_mesh, leaving, extra, grad_uin, dest_low, to_before, own, to_after = edges_backward(
            index, back, slopes, w_round[layer], carried,
            (ids_row, landed, dec_turn, w_out, w_dec) if first_step else (),
        )
        if first_step:
            to_before, to_after, final_mesh = lax.optimization_barrier(
                (to_before, to_after, final_mesh)
            )
        from_before, from_after = halo(walk, to_after, to_before)
        if first_step:
            from_before, final_mesh, head_grads = lax.optimization_barrier(
                (
                    from_before,
                    settled(mesh, final_mesh),
                    decode_grads(decoded, landed, fetched, extra),
                )
            )
            grad_wout, grad_wdec, grad_bdec = head_grads
        past = () if first_step else (kept[layer + 1][0], extra)
        part, mats_grads[2 * layer + 1], bias_grads[layer], *source = weight_grads(
            old, dest_low, agg, grad_uin, update, leaving, grad_mesh, w_round[layer], past
        )
        if past:
            mats_grads[2 * layer + 2] = source[0]
        carried = (part, own, from_before, from_after, w_round[layer])
    grad_mesh, leaving, grad_win, grad_wnode, grad_bpair, mats_grads[0] = encode_backward(
        carried, kept[0][0], gathered, arrived, ids, w_in, w_node, biases
    )
    parts = [grad_win, grad_wnode, grad_wdec, grad_wout[:, :CH].reshape(CH, D)]
    parts = parts + mats_grads
    parts = parts + [grad_bpair, grad_bdec] + bias_grads
    keep, send = collect_rows(parts, total_size, peers, place)
    mine, leaving = reduced_piece(keep, send, leaving)
    late = at_home(leaving)
    mine = lax.dynamic_slice_in_dim(mine.reshape(-1), offset, shard)
    lane = lax.broadcasted_iota(jnp.int32, (8, HALF), 1)
    sums, late = summed_everywhere(
        jnp.where(lane == 0, local_total, jnp.sum(mine * mine)), late
    )
    total, norm = sums[0, 0], jnp.sqrt(sums[0, 1])
    node_grads = settled(grad_mesh, late)
    clipped = mine * jnp.minimum(1.0, 0.05 / norm)
    first = 0.9 * moment1 + 0.1 * clipped
    second = 0.999 * moment2 + 0.001 * clipped * clipped
    first_hat = first / (1.0 - 0.9**STEP)
    second_hat = second / (1.0 - 0.999**STEP)
    updated = master - 0.1 * (first_hat / (jnp.sqrt(second_hat) + 1e-08) + 0.1 * master)
    return (
        total.reshape(1),
        count.reshape(1),
        norm.reshape(1),
        updated,
        first,
        second,
        updated.astype(jnp.bfloat16),
        final_mesh.reshape(1, blocks, D),
        node_grads.reshape(1, blocks, D),
        grad_pred.reshape(1, grad_pred.shape[0], points),
    )


def solution(mesh):
    return jax.shard_map(
        functools.partial(shards, walk_of(mesh)),
        mesh=mesh,
        in_specs=(
            P(("dp", "space")),
            P(("dp", "space")),
            P(("dp", "space")),
            P("dp", None, "space"),
            P("dp", None, "space"),
            P("dp", None, "space"),
            P("dp", "space", None),
            P("dp", "space"),
            P("space", None),
            P("space"),
        ),
        out_specs=(
            P(),
            P(),
            P(),
            P(("dp", "space")),
            P(("dp", "space")),
            P(("dp", "space")),
            P(("dp", "space")),
            P("dp", "space", None),
            P("dp", "space", None),
            P("dp", None, "space"),
        ),
        check_vma=False,
    )
```

```python
import functools

import jax
import jax.numpy as jnp
from jax import lax
from jax.experimental import pallas as pl
from jax.experimental.pallas import tpu as pltpu
from jax.sharding import PartitionSpec as P

D = 256
HALF = 128
CH = 78
ROUNDS = 3
K = 6
ROWW = 360
NEAR = 358
STEP = 10
H = 2048
ALL = ("dp", "space")
LIMIT = pltpu.CompilerParams(vmem_limit_bytes=60 * 2**20)


def cost(micros):
    return pl.CostEstimate(flops=0, bytes_accessed=micros * 3_000_000, transcendentals=0)


def inner(left, right, left_dim, right_dim):
    return lax.dot_general(
        left, right, (((left_dim,), (right_dim,)), ((), ())), preferred_element_type=jnp.float32
    )


def sigmoid(value):
    return 0.5 * jnp.tanh(0.5 * value) + 0.5


def silu(value):
    return value * sigmoid(value)


def slope(value):
    sigma = sigmoid(value)
    return sigma * (1.0 + value * (1.0 - sigma))


def shifted(shard, axis, by):
    peers = lax.axis_size(axis)
    pairs = [(i, i + by) for i in range(peers) if 0 <= i + by < peers]
    return lax.ppermute(shard, axis, pairs)


def walk_of(mesh):
    count = mesh.shape["space"]
    chips = [getattr(device, "coords", None) for device in mesh.devices[0].reshape(-1)]
    if any(chip is None for chip in chips) or len(set(map(tuple, chips))) != count:
        return list(range(count))
    at = {tuple(chip): n for n, chip in enumerate(chips)}
    xs, ys, zs = (sorted({chip[n] for chip in at}) for n in range(3))
    if len(xs) * len(ys) * len(zs) != count:
        return list(range(count))
    if (len(xs), len(ys), len(zs)) == (2, 2, 4):
        corners = [(0, 0), (1, 0), (0, 1), (1, 1)]
        planes = [(0, 1, 3, 2), (2, 0, 1, 3), (3, 1, 0, 2), (2, 3, 1, 0)]
        steps = [(*corners[n], z) for z, plane in enumerate(planes) for n in plane]
        return [at[(xs[x], ys[y], zs[z])] for x, y, z in steps]
    walk, plane = [], []
    for n, y in enumerate(ys):
        plane = plane + [(x, y) for x in (xs if n % 2 == 0 else xs[::-1])]
    for n, z in enumerate(zs):
        walk = walk + [at[(x, y, z)] for x, y in (plane if n % 2 == 0 else plane[::-1])]
    return walk


def halo(walk, last, initial):
    up = list(zip(walk, walk[1:] + walk[:1]))
    down = [(j, i) for i, j in up]
    return lax.ppermute(last, "space", up), lax.ppermute(initial, "space", down)


def pieces_of(total, peers):
    share = total // peers
    starts = [share * d // D for d in range(peers)]
    counts = [-(-share * (d + 1) // D) - starts[d] for d in range(peers)]
    shared = [share * d % D != 0 for d in range(peers)]
    height = -(-max(counts) // 16) * 16
    return starts, counts, shared, height


def parts_of():
    return [CH, D, D, CH] + [5 * D] * ROUNDS + [3 + 2 * ROUNDS]


def swapped(value, axis, bit):
    return lax.ppermute(value, axis, [(i, i ^ bit) for i in range(lax.axis_size(axis))])


def bits_of(axis):
    return [1 << n for n in range(lax.axis_size(axis).bit_length() - 1)]


def others(value, axis, bits):
    masks = [sum(bit for n, bit in enumerate(bits) if m >> n & 1) for m in range(1, 1 << len(bits))]
    return [swapped(value, axis, mask) for mask in masks]


def upper_groups():
    bits = bits_of("space")[2:]
    return [tuple(bits[n : n + 2]) for n in range(0, len(bits), 2)]


def orders():
    return [(1, 2), (2, 1)]


def summed_everywhere(value, arriving):
    for bits in reversed(upper_groups()):
        value = sum(others(value, "space", bits), value)
    value = value + swapped(value, "dp", 1)
    value, arriving = lax.optimization_barrier((value, arriving))
    return sum(others(value, "space", (1, 2)), value), arriving


def gathered_blocks(piece, posted):
    held, weights, size = piece[None], {}, 1
    for bits in reversed(upper_groups()):
        held = jnp.concatenate([held] + others(held, "space", bits), 0)
        for n, bit in enumerate(bits):
            weights[bit] = size << n
        size = size << len(bits)
    half = piece.shape[0] // 2
    held = [held[:, :half], held[:, half:]]
    ranks = [dict(weights), dict(weights)]
    for turn in (1, 0):
        if turn == 0:
            held[0], held[1], posted = lax.optimization_barrier((*held, posted))
        for n, order in enumerate(orders()):
            held[n] = jnp.concatenate([held[n], swapped(held[n], "space", order[turn])], 0)
            ranks[n][order[turn]] = size
        size = size << 1
    return (held, [swapped(part, "dp", 1) for part in held], ranks), posted


def spread_rows(gathered, total, peers, place):
    (first, second), (first_far, second_far), ranks = gathered
    starts, counts, shared, height = pieces_of(total, peers)
    half, group = height // 2, first.shape[0]
    rows = -(-total // D)
    sizes = parts_of()
    def at(rank, relative):
        spot = 0
        for bit, weight in rank.items():
            spot = spot + jnp.where((relative & bit) != 0, weight, 0)
        return spot

    def body(place_ref, *refs):
        sources, outs, buffer = refs[:4], refs[4:-1], refs[-1]
        me = place_ref[0]
        mine = me // group
        for d in range(peers):
            relative = (me ^ d) & (group - 1)
            spots = [at(rank, relative) for rank in ranks]

            def lay(one, two, d=d, spots=spots):
                piece = jnp.concatenate([one[spots[0]], two[spots[1]]], 0).astype(jnp.float32)
                start, count = starts[d], counts[d]
                if shared[d]:
                    buffer[start : start + 1, :] = buffer[start : start + 1, :] + piece[:1]
                    buffer[start + 1 : start + count, :] = piece[1:count]
                else:
                    buffer[start : start + count, :] = piece[:count]

            @pl.when(mine == d // group)
            def _():
                lay(sources[0], sources[1])

            @pl.when(mine != d // group)
            def _():
                lay(sources[2], sources[3])

        start = 0
        for out, size in zip(outs, sizes):
            out[:size, :] = buffer[start : start + size, :].astype(out.dtype)
            if out.shape[0] > size:
                out[size:, :] = jnp.zeros((out.shape[0] - size, D), out.dtype)
            start = start + size

    kinds = [jnp.bfloat16] * (4 + ROUNDS) + [jnp.float32]
    talls = [HALF] + sizes[1:]
    return pl.pallas_call(
        body,
        grid_spec=pltpu.PrefetchScalarGridSpec(
            num_scalar_prefetch=1,
            grid=(1,),
            in_specs=[whole(first.shape)] * 4,
            out_specs=[whole((tall, D)) for tall in talls],
            scratch_shapes=[pltpu.VMEM((-(-rows // 8) * 8 + 8, D), jnp.float32)],
        ),
        out_shape=[jax.ShapeDtypeStruct((tall, D), kind) for tall, kind in zip(talls, kinds)],
        compiler_params=LIMIT,
        cost_estimate=cost(4),
        name="spread_rows",
    )(place.reshape(1), first, second, first_far, second_far)


def collect_rows(parts, total, peers, place):
    starts, counts, shared, height = pieces_of(total, peers)
    rows = -(-total // D)
    sizes = [min(part.shape[0], size) for part, size in zip(parts, tall_parts())]
    group = lax.axis_size("space")

    def body(place_ref, *refs):
        sources, keep, send, buffer = refs[:-3], refs[-3], refs[-2], refs[-1]
        start = 0
        for source, size in zip(sources, sizes):
            buffer[start : start + size, :] = source[:size, :]
            start = start + size
        if buffer.shape[0] > start:
            buffer[start:, :] = jnp.zeros((buffer.shape[0] - start, D), jnp.float32)
        me = place_ref[0]
        mine = me // group
        for d in range(peers):
            relative = (me ^ d) & (group - 1)

            @pl.when(mine == d // group)
            def _():
                keep[relative] = buffer[starts[d] : starts[d] + height, :]

            @pl.when(mine != d // group)
            def _():
                send[relative] = buffer[starts[d] : starts[d] + height, :].astype(jnp.bfloat16)

    shape = (group, height, D)
    return pl.pallas_call(
        body,
        grid_spec=pltpu.PrefetchScalarGridSpec(
            num_scalar_prefetch=1,
            grid=(1,),
            in_specs=[whole(part.shape) for part in parts],
            out_specs=[whole(shape), whole(shape)],
            scratch_shapes=[pltpu.VMEM((-(-rows // 8) * 8 + height + 8, D), jnp.float32)],
        ),
        out_shape=[
            jax.ShapeDtypeStruct(shape, jnp.float32),
            jax.ShapeDtypeStruct(shape, jnp.bfloat16),
        ],
        compiler_params=LIMIT,
        cost_estimate=cost(5),
        name="collect_rows",
    )(place.reshape(1), *parts)


def reduced_piece(keep, send, leaving):
    kept = keep + swapped(send, "dp", 1).astype(jnp.float32)
    half = kept.shape[1] // 2
    groups = upper_groups()
    inner_shape = (kept.shape[0] // 4, 2, 2, half, D)
    parts = [kept[:, :half].reshape(inner_shape), kept[:, half:].reshape(inner_shape)]
    for n, order in enumerate(orders()):
        for bit in order:
            spot = 2 if bit == 1 and parts[n].ndim == 5 else 1
            stay = lax.index_in_dim(parts[n], 0, spot, keepdims=False)
            leave = lax.index_in_dim(parts[n], 1, spot, keepdims=False)
            parts[n] = stay + swapped(leave.astype(jnp.bfloat16), "space", bit).astype(jnp.float32)
    part = jnp.concatenate(parts, 1)
    part, leaving = lax.optimization_barrier((part, leaving))
    for bits in groups:
        part = part.reshape((-1, 1 << len(bits)) + part.shape[1:])
        masks = [sum(bit for n, bit in enumerate(bits) if m >> n & 1) for m in range(1 << len(bits))]
        low = part.astype(jnp.bfloat16)
        part = sum(
            [
                swapped(low[:, m], "space", mask).astype(jnp.float32)
                for m, mask in enumerate(masks)
                if m
            ],
            part[:, 0],
        )
    return part[0], leaving


def tall_parts():
    return [CH, D, D, CH] + [D, 4 * D] * ROUNDS + [2, 1] + [2] * ROUNDS


def weave(ref, value):
    rows = value.shape[0]
    ref[pl.ds(0, rows, stride=2), :] = value[:, :HALF]
    ref[pl.ds(1, rows, stride=2), :] = value[:, HALF:]


def unweave(ref):
    rows = ref.shape[0] // 2
    return ref[pl.ds(0, rows, stride=2), :], ref[pl.ds(1, rows, stride=2), :]


def selector():
    row = lax.broadcasted_iota(jnp.int32, (8, HALF), 0)
    lane = lax.broadcasted_iota(jnp.int32, (8, HALF), 1)
    slot = jnp.where(lane == CH, 64.0, jnp.where(lane == CH + 1, 1.0, 0.0))
    known = jnp.where(lane == CH + 2, 1.0, 0.0)
    return jnp.where(row == 0, slot, jnp.where(row == 1, known, 0.0)).astype(jnp.bfloat16)


def ids_along(arrived):
    codes = inner(selector(), arrived, 1, 1)
    return jnp.where(codes[1:2, :] > 0, codes[0:1, :], -1.0).astype(jnp.int32)


def ids_down(arrived):
    codes = inner(arrived, selector(), 1, 1)
    return jnp.where(codes[:, 1:2] > 0, codes[:, 0:1], -1.0).astype(jnp.int32)


def whole(shape):
    return pl.BlockSpec(shape, lambda *_: (0,) * len(shape))


def node_terms(mesh, mats, bias):
    blocks = mesh.shape[0]
    tile = 1024

    def body(mesh_ref, mats_ref, bias_ref, dest_ref, self_ref):
        lowered = mesh_ref[...].astype(jnp.bfloat16)
        weave(dest_ref, inner(lowered, mats_ref[1], 1, 0) + bias_ref[0:1, :])
        self_ref[...] = inner(lowered, mats_ref[3], 1, 0) + bias_ref[1:2, :]

    rows = pl.BlockSpec((tile, D), lambda i: (i, 0))
    woven = pl.BlockSpec((2 * tile, HALF), lambda i: (i, 0))
    return pl.pallas_call(
        body,
        grid=(blocks // tile,),
        in_specs=[rows, whole(mats.shape), whole(bias.shape)],
        out_specs=[woven, rows],
        out_shape=[
            jax.ShapeDtypeStruct((2 * blocks, HALF), jnp.float32),
            jax.ShapeDtypeStruct((blocks, D), jnp.float32),
        ],
        compiler_params=pltpu.CompilerParams(vmem_limit_bytes=63 * 2**20),
        cost_estimate=cost(4),
        name="node_terms",
    )(mesh, mats, bias)


def round_forward(index, mesh, pieces, mats, terms, following, decoder=(), half=None, into=()):
    blocks = mesh.shape[0]
    tile, chunk = 512, 16
    turns, high = tile // chunk, 2 * chunk
    more = following is not None
    reach = 2 * (blocks + 2 * H)
    steps = blocks // tile if half is None else blocks // tile // 2
    shift = 0 if half is None else half * steps

    def body(index_ref, mesh_ref, *refs):
        sources, refs = refs[: len(pieces)], refs[len(pieces) :]
        (mats_ref, dest_ref, self_ref), refs = refs[:3], refs[3:]
        table, rows, wide = refs[-3:]
        if more:
            next_ref, refs = refs[0], refs[1 + len(into) :]
            new_ref, back_ref, update_ref, agg_ref, slope_ref, sent_ref = refs[:6]
        else:
            ids_ref, dec_ref, out_ref, head_ref = refs[:4]
            new_ref, back_ref, update_ref, agg_ref, slope_ref = refs[4:9]
            branch_ref, fetched_ref, decoded_ref, turn_ref, total_ref = refs[9:14]
        step = pl.program_id(0)

        @pl.when(step == 0)
        def _():
            for source, (_, start) in zip(sources, pieces):

                @pl.loop(0, source.shape[0] // 256)
                def _(i, source=source, start=start):
                    at = pl.multiple_of(i * 256, 256)
                    to = pl.multiple_of(start + at, 256)
                    table[pl.ds(to, 256), :] = source[pl.ds(at, 256), :].astype(jnp.float32)

        mesh_in = mesh_ref[...]

        part = blocks // 2
        if half is None:
            origin = step // (steps // 2) * (K * part) + lax.rem(step, steps // 2) * tile
        else:
            origin = step * tile

        def fetch(turn):
            for edge in range(K):
                base = edge * part + turn * chunk + origin
                spots = [index_ref[base + u] for u in range(chunk)]
                values = [table[pl.ds(pl.multiple_of(spot, 2), 2), :] for spot in spots]
                for u in range(chunk):
                    spot = pl.multiple_of(edge * 2 * tile + turn * high + 2 * u, 2)
                    rows[pl.ds(spot, 2), :] = values[u]

        def load(turn):
            at = pl.multiple_of(turn * high, high)
            taken = [
                rows[pl.ds(pl.multiple_of(edge * 2 * tile + turn * high, high), high), :]
                for edge in range(K)
            ]
            return at, dest_ref[pl.ds(at, high), :], taken

        def dense(at, dest, taken):
            total = None
            for edge in range(K):
                value = taken[edge] + dest
                sigma = sigmoid(value)
                out = value * sigma
                slope_ref[edge, pl.ds(at, high), :] = (sigma + out * (1.0 - sigma)).astype(
                    jnp.bfloat16
                )
                total = out if total is None else total + out
            wide[pl.ds(at, high), :] = total * (1.0 / K)

        def some(turn, carry):
            loaded = load(turn - 1)
            fetch(turn)
            dense(*loaded)
            return carry

        fetch(0)
        lax.fori_loop(1, turns, some, 0)
        dense(*load(turns - 1))
        first, second = unweave(wide)
        first, second = first.astype(jnp.bfloat16), second.astype(jnp.bfloat16)
        agg_ref[:, :HALF] = first
        agg_ref[:, HALF:] = second
        update_in = (
            inner(first, mats_ref[2, :HALF, :], 1, 0)
            + inner(second, mats_ref[2, HALF:, :], 1, 0)
            + self_ref[...]
        )
        sigma = sigmoid(update_in)
        out = update_in * sigma
        back_ref[...] = sigma + out * (1.0 - sigma)
        update = out.astype(jnp.bfloat16)
        update_ref[...] = update
        new = mesh_in + inner(update, mats_ref[4], 1, 0)
        new_ref[...] = new
        lowered = new.astype(jnp.bfloat16)
        if more:
            weave(wide, inner(lowered, next_ref[0], 1, 0))
            sent_ref[...] = wide[...].astype(jnp.bfloat16)
            return
        nodes = lax.broadcasted_iota(jnp.int32, (ids_ref.shape[0], tile), 1) + step * tile
        chooser = jnp.where(nodes == ids_ref[...], 1.0, 0.0).astype(jnp.bfloat16)
        found = inner(chooser, lowered, 1, 0)

        @pl.when(step == 0)
        def _():
            total_ref[...] = found

        @pl.when(step > 0)
        def _():
            total_ref[...] += found

        @pl.when(step == blocks // tile - 1)
        def _():
            fetched = total_ref[...].astype(jnp.bfloat16)
            fetched_ref[...] = fetched
            value = inner(fetched, dec_ref[...], 1, 0) + head_ref[2:3, :]
            sigma = sigmoid(value)
            out = value * sigma
            turn_ref[...] = sigma + out * (1.0 - sigma)
            decoded = out.astype(jnp.bfloat16)
            decoded_ref[...] = decoded
            branch_ref[...] = inner(decoded, out_ref[...], 1, 0).astype(jnp.bfloat16)

    whole_rows = pl.BlockSpec((tile, D), lambda i, *_: (i + shift, 0))
    woven = pl.BlockSpec((2 * tile, HALF), lambda i, *_: (i + shift, 0))
    ins = [whole_rows] + [pl.BlockSpec(memory_space=pltpu.VMEM)] * len(pieces)
    ins = ins + [whole(mats.shape), woven, whole_rows]
    outs = [whole_rows] * 4 + [pl.BlockSpec((K, 2 * tile, HALF), lambda i, *_: (0, i + shift, 0))]
    shapes = [
        jax.ShapeDtypeStruct((blocks, D), jnp.float32),
        jax.ShapeDtypeStruct((blocks, D), jnp.float32),
        jax.ShapeDtypeStruct((blocks, D), jnp.bfloat16),
        jax.ShapeDtypeStruct((blocks, D), jnp.bfloat16),
        jax.ShapeDtypeStruct((K, 2 * blocks, HALF), jnp.bfloat16),
    ]
    args = [index, mesh] + [rows for rows, _ in pieces] + [mats, *terms]
    if more:
        ins.append(pl.BlockSpec((1, D, D), lambda *_: (0, 0, 0)))
        outs.append(pl.BlockSpec((2 * tile, HALF), lambda i, *_: (i, 0)))
        shapes.append(jax.ShapeDtypeStruct((2 * tile * steps, HALF), jnp.bfloat16))
        args.append(following)
    aliases = {len(args) + n: n for n in range(len(into))}
    ins = ins + [pl.BlockSpec(memory_space=pl.ANY)] * len(into)
    args = args + list(into)
    scratch = []
    if decoder:
        posts = decoder[0].shape[0]
        ins = ins + [whole(arg.shape) for arg in decoder]
        args = args + list(decoder)
        for width, kind in ((HALF, jnp.bfloat16), (D, jnp.bfloat16), (D, jnp.bfloat16), (D, jnp.float32)):
            outs.append(whole((posts, width)))
            shapes.append(jax.ShapeDtypeStruct((posts, width), kind))
        scratch = [pltpu.VMEM((posts, D), jnp.float32)]
    return pl.pallas_call(
        body,
        grid_spec=pltpu.PrefetchScalarGridSpec(
            num_scalar_prefetch=1,
            grid=(steps,),
            in_specs=ins,
            out_specs=outs,
            scratch_shapes=scratch
            + [
                pltpu.VMEM((reach, HALF), jnp.float32),
                pltpu.VMEM((K * 2 * tile, HALF), jnp.float32),
                pltpu.VMEM((2 * tile, HALF), jnp.float32),
            ],
        ),
        out_shape=shapes,
        input_output_aliases=aliases,
        compiler_params=pltpu.CompilerParams(vmem_limit_bytes=54 * 2**20),
        cost_estimate=cost(24 if half is None else 14),
        name="round_forward",
    )(*args)


def edges_backward(index, back, slopes, mats, carried=(), landed=()):
    blocks = back.shape[0]
    tile, chunk = 512, 16
    steps, turns, high = blocks // tile, tile // chunk, 2 * chunk
    reach = 2 * (blocks + 2 * H)

    def body(*refs):
        if carried:
            index_ref, back_ref, slope_ref, mats_ref = refs[:4]
            past, rest = refs[4:9], refs[9:]
            (new_ref, out_ref, sent_ref), rest = rest[:3], rest[3:]
        else:
            index_ref, back_ref, slope_ref, mats_ref = refs[:4]
            (ids_ref, landed_ref, turn_ref, w_out_ref, w_dec_ref), rest = refs[4:9], refs[9:]
            (new_ref, out_ref, gdec_ref), rest = rest[:3], rest[3:]
            gathered, rest = rest[5], rest[:5] + rest[6:]
        guin_ref, low_ref, before_ref, own_ref, after_ref, wide, wider, flows, *tables = rest
        step = pl.program_id(0)

        @pl.when(step == 0)
        def _():
            @pl.loop(0, reach // 256)
            def _(i):
                for table in tables:
                    table[pl.ds(pl.multiple_of(i * 256, 256), 256), :] = jnp.zeros(
                        (256, HALF), jnp.float32
                    )

        if carried:
            new, one, two = ended(*past, wide)
            sent_ref[:, :HALF] = one
            sent_ref[:, HALF:] = two
            new_ref[...] = new
            grad_out = new.astype(jnp.bfloat16)
            out_ref[...] = grad_out
        else:

            @pl.when(step == 0)
            def _():
                grad_dec = inner(landed_ref[...], w_out_ref[...], 1, 1) * turn_ref[...]
                grad_dec = grad_dec.astype(jnp.bfloat16)
                gdec_ref[...] = grad_dec
                gathered[...] = inner(grad_dec, w_dec_ref[...], 1, 1).astype(jnp.bfloat16)

            nodes = lax.broadcasted_iota(jnp.int32, (tile, landed_ref.shape[0]), 0) + step * tile
            chooser = jnp.where(nodes == ids_ref[...], 1.0, 0.0).astype(jnp.bfloat16)
            new = inner(chooser, gathered[...], 1, 0)
            new_ref[...] = new
            grad_out = new.astype(jnp.bfloat16)
            out_ref[...] = grad_out
        grad_uin = (inner(grad_out, mats_ref[4], 1, 1) * back_ref[...]).astype(jnp.bfloat16)
        guin_ref[...] = grad_uin
        weave(wide, inner(grad_uin, mats_ref[2], 1, 1) * (1.0 / K))

        def dense(turn):
            at = pl.multiple_of(turn * high, high)
            grad_agg = wide[pl.ds(at, high), :]
            total, parts = None, []
            for edge in range(K):
                flow = grad_agg * slope_ref[edge, pl.ds(at, high), :].astype(jnp.float32)
                parts.append(flow)
                total = flow if total is None else total + flow
            return at, total, parts

        def keep(turn, at, total, parts):
            for edge in range(K):
                spot = pl.multiple_of(edge * 2 * tile + turn * high, high)
                flows[pl.ds(spot, high), :] = parts[edge]
            wider[pl.ds(at, high), :] = total

        part = blocks // 2
        origin = step // (steps // 2) * (K * part) + lax.rem(step, steps // 2) * tile

        def scatter(turn):
            for u in range(chunk):
                spots, sums = [], []
                for edge in range(K):
                    base = edge * part + turn * chunk + origin
                    spots.append(pl.multiple_of(index_ref[base + u], 2))
                for edge in range(K):
                    spot = pl.multiple_of(edge * 2 * tile + turn * high + 2 * u, 2)
                    sums.append(tables[edge][pl.ds(spots[edge], 2), :] + flows[pl.ds(spot, 2), :])
                for edge in range(K):
                    tables[edge][pl.ds(spots[edge], 2), :] = sums[edge]

        def some(turn, carry):
            found = dense(turn)
            scatter(turn - 1)
            keep(turn, *found)
            return carry

        keep(0, *dense(0))
        lax.fori_loop(1, turns, some, 0)
        scatter(turns - 1)
        first, second = unweave(wider)
        low_ref[:, :HALF] = first.astype(jnp.bfloat16)
        low_ref[:, HALF:] = second.astype(jnp.bfloat16)

        @pl.when(step == steps - 1)
        def _():
            def summed(at):
                value = tables[0][pl.ds(at, 256), :]
                for table in tables[1:]:
                    value = value + table[pl.ds(at, 256), :]
                return value

            @pl.loop(0, 2 * H // 256)
            def _(i):
                at = pl.multiple_of(i * 256, 256)
                far = pl.multiple_of(2 * H + 2 * blocks + at, 256)
                before_ref[pl.ds(at, 256), :] = summed(at).astype(jnp.bfloat16)
                after_ref[pl.ds(at, 256), :] = summed(far).astype(jnp.bfloat16)

            @pl.loop(0, 2 * blocks // 256)
            def _(i):
                at = pl.multiple_of(i * 256, 256)
                own_ref[pl.ds(at, 256), :] = summed(pl.multiple_of(2 * H + at, 256))

    rows = pl.BlockSpec((tile, D), lambda i, *_: (i, 0))
    woven = pl.BlockSpec((2 * tile, HALF), lambda i, *_: (i, 0))
    low = jax.ShapeDtypeStruct((blocks, D), jnp.bfloat16)
    low_posts = (landed[1].shape[0], D) if landed else None
    last = low if carried else jax.ShapeDtypeStruct(low_posts, jnp.bfloat16)
    return pl.pallas_call(
        body,
        grid_spec=pltpu.PrefetchScalarGridSpec(
            num_scalar_prefetch=1,
            grid=(steps,),
            in_specs=[
                rows,
                pl.BlockSpec((K, 2 * tile, HALF), lambda i, *_: (0, i, 0)),
                whole(mats.shape),
            ]
            + ([rows] + [woven] * 3 + [whole(mats.shape)] if carried else [])
            + [whole(arg.shape) for arg in landed],
            out_specs=([rows] * 3 if carried else [rows, rows, whole(low_posts)])
            + [
                rows, rows,
                whole((2 * H, HALF)), whole((2 * blocks, HALF)), whole((2 * H, HALF)),
            ],
            scratch_shapes=([] if carried else [pltpu.VMEM(low_posts, jnp.bfloat16)])
            + [
                pltpu.VMEM((2 * tile, HALF), jnp.float32),
                pltpu.VMEM((2 * tile, HALF), jnp.float32),
                pltpu.VMEM((2 * tile * K, HALF), jnp.float32),
            ]
            + [pltpu.VMEM((reach, HALF), jnp.float32)] * K,
        ),
        out_shape=[
            jax.ShapeDtypeStruct((blocks, D), jnp.float32),
            low,
            last,
            low,
            low,
            jax.ShapeDtypeStruct((2 * H, HALF), jnp.bfloat16),
            jax.ShapeDtypeStruct((2 * blocks, HALF), jnp.float32),
            jax.ShapeDtypeStruct((2 * H, HALF), jnp.bfloat16),
        ],
        compiler_params=LIMIT,
        cost_estimate=cost(28 if carried else 25),
        name="edges_backward",
    )(index, back, slopes, mats, *carried, *landed)


def ended(part_ref, own_ref, first_ref, last_ref, mats_ref, wide):
    wide[...] = (
        own_ref[...] + first_ref[...].astype(jnp.float32) + last_ref[...].astype(jnp.float32)
    )
    one, two = unweave(wide)
    one, two = one.astype(jnp.bfloat16), two.astype(jnp.bfloat16)
    new = (
        part_ref[...]
        + inner(one, mats_ref[0, :, :HALF], 1, 1)
        + inner(two, mats_ref[0, :, HALF:], 1, 1)
    )
    return new, one, two


def weight_grads(mesh, dest_low, agg, grad_uin, update, leaving, grad_mesh, mats, past=()):
    blocks = mesh.shape[0]
    tile = 512

    def body(mesh_ref, dest_ref, agg_ref, guin_ref, update_ref, out_ref, grad_ref, mats_ref, *refs):
        if past:
            (old_ref, sent_ref), refs = refs[:2], refs[2:]
        part_ref, grads_ref, bias_ref = refs[:3]

        @pl.when(pl.program_id(0) == 0)
        def _():
            for ref in refs[1:]:
                ref[...] = jnp.zeros(ref.shape, jnp.float32)

        lowered = mesh_ref[...].astype(jnp.bfloat16)
        dest, guin = dest_ref[...], guin_ref[...]
        grads_ref[:D, :] += inner(lowered, dest, 0, 0)
        grads_ref[D : 2 * D, :] += inner(agg_ref[...], guin, 0, 0)
        grads_ref[2 * D : 3 * D, :] += inner(lowered, guin, 0, 0)
        grads_ref[3 * D :, :] += inner(update_ref[...], out_ref[...], 0, 0)
        bias_ref[0:1, :] += jnp.sum(dest.astype(jnp.float32), 0, keepdims=True)
        bias_ref[1:2, :] += jnp.sum(guin.astype(jnp.float32), 0, keepdims=True)
        part_ref[...] = (
            grad_ref[...] + inner(guin, mats_ref[3], 1, 1) + inner(dest, mats_ref[1], 1, 1)
        )
        if past:
            refs[3][...] += inner(old_ref[...].astype(jnp.bfloat16), sent_ref[...], 0, 0)

    rows = pl.BlockSpec((tile, D), lambda i: (i, 0))
    shapes = [(4 * D, D), (2, D)] + ([(D, D)] if past else [])
    return pl.pallas_call(
        body,
        grid=(blocks // tile,),
        in_specs=[rows] * 7 + [whole(mats.shape)] + [rows] * len(past),
        out_specs=[rows] + [whole(shape) for shape in shapes],
        out_shape=[jax.ShapeDtypeStruct((blocks, D), jnp.float32)]
        + [jax.ShapeDtypeStruct(shape, jnp.float32) for shape in shapes],
        compiler_params=pltpu.CompilerParams(vmem_limit_bytes=63 * 2**20),
        cost_estimate=cost(10),
        name="weight_grads",
    )(mesh, dest_low, agg, grad_uin, update, leaving, grad_mesh, mats, *past)


def decode_grads(decoded, landed, fetched, grad_dec):
    def body(decoded_ref, landed_ref, fetched_ref, grad_ref, gout_ref, gdec_ref, bias_ref):
        gout_ref[...] = inner(decoded_ref[...], landed_ref[...], 0, 0)
        gdec_ref[...] = inner(fetched_ref[...], grad_ref[...], 0, 0)
        bias_ref[...] = jnp.sum(grad_ref[...].astype(jnp.float32), 0, keepdims=True)

    return pl.pallas_call(
        body,
        out_shape=[jax.ShapeDtypeStruct(shape, jnp.float32) for shape in ((D, HALF), (D, D), (1, D))],
        compiler_params=pltpu.CompilerParams(vmem_limit_bytes=63 * 2**20),
        cost_estimate=cost(3),
        name="decode_grads",
    )(decoded, landed, fetched, grad_dec)


def encode_rows(arrived, w_in, w_node, biases, source):
    posts = arrived.shape[0]
    tile = 512

    def body(
        arrived_ref, in_ref, node_ref, bias_ref, source_ref,
        mesh_ref, gathered_ref, sent_ref, ids_ref, down_ref, encoded, wide,
    ):
        step = pl.program_id(0)

        @pl.when(step == 0)
        def _():
            entering = inner(arrived_ref[...], in_ref[...], 1, 0) + bias_ref[0:1, :]
            encoded[...] = silu(entering).astype(jnp.bfloat16)
            ids_ref[...] = ids_along(arrived_ref[...])
            down_ref[...] = ids_down(arrived_ref[...])

        nodes = lax.broadcasted_iota(jnp.int32, (tile, posts), 0) + step * tile
        chooser = jnp.where(nodes == ids_ref[...], 1.0, 0.0).astype(jnp.bfloat16)
        gathered = inner(chooser, encoded[...], 1, 0).astype(jnp.bfloat16)
        gathered_ref[...] = gathered
        mesh = silu(inner(gathered, node_ref[...], 1, 0) + bias_ref[1:2, :])
        mesh_ref[...] = mesh
        weave(wide, inner(mesh.astype(jnp.bfloat16), source_ref[0], 1, 0))
        sent_ref[...] = wide[...].astype(jnp.bfloat16)

    rows = pl.BlockSpec((tile, D), lambda i: (i, 0))
    args = (arrived, w_in, w_node, biases, source)
    return pl.pallas_call(
        body,
        grid=(H // tile,),
        in_specs=[whole(arg.shape) for arg in args[:-1]]
        + [pl.BlockSpec((1, D, D), lambda *_: (0, 0, 0))],
        out_specs=[rows, rows, pl.BlockSpec((2 * tile, HALF), lambda i: (i, 0))]
        + [whole((1, posts)), whole((posts, 1))],
        out_shape=[
            jax.ShapeDtypeStruct((H, D), jnp.float32),
            jax.ShapeDtypeStruct((H, D), jnp.bfloat16),
            jax.ShapeDtypeStruct((2 * H, HALF), jnp.bfloat16),
            jax.ShapeDtypeStruct((1, posts), jnp.int32),
            jax.ShapeDtypeStruct((posts, 1), jnp.int32),
        ],
        scratch_shapes=[pltpu.VMEM((posts, D), jnp.bfloat16), pltpu.VMEM((2 * tile, HALF), jnp.float32)],
        compiler_params=LIMIT,
        cost_estimate=cost(5),
        name="encode_rows",
    )(*args)


def encode_backward(carried, mesh, gathered, arrived, ids, w_in, w_node, biases):
    blocks = mesh.shape[0]
    posts = arrived.shape[0]
    tile = 512
    steps = blocks // tile

    def body(
        part_ref, own_ref, first_ref, last_ref, mats_ref,
        mesh_ref, gathered_ref, arrived_ref, ids_ref, in_ref, node_ref, bias_ref,
        new_ref, out_ref, gin_ref, gnode_ref, gbias_ref, gsource_ref, total, wide,
    ):
        step = pl.program_id(0)

        @pl.when(step == 0)
        def _():
            for ref in (total, gnode_ref, gbias_ref, gsource_ref):
                ref[...] = jnp.zeros(ref.shape, jnp.float32)

        new, one, two = ended(part_ref, own_ref, first_ref, last_ref, mats_ref, wide)
        new_ref[...] = new
        out_ref[...] = new.astype(jnp.bfloat16)
        lowered = mesh_ref[...].astype(jnp.bfloat16)
        gsource_ref[:, :HALF] += inner(lowered, one, 0, 0)
        gsource_ref[:, HALF:] += inner(lowered, two, 0, 0)
        node_in = inner(gathered_ref[...], node_ref[...], 1, 0) + bias_ref[1:2, :]
        grad_node = (new * slope(node_in)).astype(jnp.bfloat16)
        gbias_ref[1:2, :] += jnp.sum(grad_node.astype(jnp.float32), 0, keepdims=True)
        gnode_ref[...] += inner(gathered_ref[...], grad_node, 0, 0)
        back = inner(grad_node, node_ref[...], 1, 1).astype(jnp.bfloat16)
        nodes = lax.broadcasted_iota(jnp.int32, (posts, tile), 1) + step * tile
        chooser = jnp.where(nodes == ids_ref[...], 1.0, 0.0).astype(jnp.bfloat16)
        total[...] += inner(chooser, back, 1, 0)

        @pl.when(step == steps - 1)
        def _():
            entering = inner(arrived_ref[...], in_ref[...], 1, 0) + bias_ref[0:1, :]
            grad_enc = (total[...] * slope(entering)).astype(jnp.bfloat16)
            gbias_ref[0:1, :] = jnp.sum(grad_enc.astype(jnp.float32), 0, keepdims=True)
            gin_ref[...] = inner(arrived_ref[...], grad_enc, 0, 0)

    rows = pl.BlockSpec((tile, D), lambda i: (i, 0))
    woven = pl.BlockSpec((2 * tile, HALF), lambda i: (i, 0))
    args = (arrived, ids, w_in, w_node, biases)
    shapes = [(HALF, D), (D, D), (2, D), (D, D)]
    return pl.pallas_call(
        body,
        grid=(steps,),
        in_specs=[rows] + [woven] * 3 + [whole(carried[4].shape), rows, rows]
        + [whole(arg.shape) for arg in args],
        out_specs=[rows, rows] + [whole(shape) for shape in shapes],
        out_shape=[
            jax.ShapeDtypeStruct((blocks, D), jnp.float32),
            jax.ShapeDtypeStruct((blocks, D), jnp.bfloat16),
        ]
        + [jax.ShapeDtypeStruct(shape, jnp.float32) for shape in shapes],
        scratch_shapes=[pltpu.VMEM((posts, D), jnp.float32), pltpu.VMEM((2 * tile, HALF), jnp.float32)],
        compiler_params=LIMIT,
        cost_estimate=cost(10),
        name="encode_backward",
    )(*carried, mesh, gathered, *args)


def shards(walk, master, moment1, moment2, inputs, targets, valid, owner, slot, neighbours, partner):
    bands = lax.axis_size("space")
    band = lax.axis_index("space")
    peers = lax.axis_size(ALL)
    place = lax.axis_index(ALL)
    shard = master.shape[0]
    total_size = shard * peers
    height = pieces_of(total_size, peers)[3]
    offset = lax.rem(lax.rem(shard, D) * place, D)
    piece = lax.dynamic_update_slice_in_dim(
        jnp.zeros((height * D,), jnp.bfloat16), master.astype(jnp.bfloat16), offset, 0
    )
    state_in = inputs[0]
    counted = valid[0].astype(jnp.float32)
    local_count = jnp.sum(valid[0])
    digits = (local_count >> jnp.array([16, 8, 0], jnp.int32)) & 255
    digits = jnp.pad(digits, (CH + 3, HALF - CH - 6)).astype(jnp.float32)[None, :]
    points = state_in.shape[1]
    blocks = neighbours.shape[0]
    assert blocks == H
    capacity = max(2, 2 * points // bands)
    target_band = owner[0, :, 0]
    hits = (target_band[:, None] == jnp.arange(bands, dtype=jnp.int32)[None, :]).astype(jnp.int32)
    ranks = jnp.sum(jnp.cumsum(hits, 0) * hits, 1) - 1
    places_out = jnp.sum(hits * jnp.asarray(walk, jnp.int32)[None, :], 1) * capacity + ranks
    poster = (
        jnp.arange(bands * capacity, dtype=jnp.int32)[:, None] == places_out[None, :]
    ).astype(jnp.bfloat16)
    spots = slot[0][None, :]
    columns = jnp.concatenate(
        [
            state_in,
            (spots // 64).astype(jnp.bfloat16),
            (spots % 64).astype(jnp.bfloat16),
            jnp.ones((1, points), jnp.bfloat16),
            jnp.zeros((HALF - CH - 3, points), jnp.bfloat16),
        ],
        0,
    )

    def exchanged(rows):
        return lax.all_to_all(
            rows.reshape(bands, capacity, HALF), "space", split_axis=0, concat_axis=0, tiled=True
        ).reshape(bands * capacity, HALF)

    held, posted = gathered_blocks(
        piece.reshape(height, D), (inner(poster, columns, 1, 1) + digits).astype(jnp.bfloat16)
    )
    arrived = exchanged(posted)
    w_in, w_node, w_dec, w_out, *w_round, biases = spread_rows(
        held, total_size, peers, place
    )
    arrived, biases = lax.optimization_barrier((arrived, biases))
    counts = arrived.reshape(bands, capacity, HALF)[:, 0, CH + 3 : CH + 6].astype(jnp.float32)
    counts = jnp.sum(counts, 0, keepdims=True)
    w_out = jnp.pad(w_out.reshape(D, CH), ((0, 0), (0, HALF - CH)))
    w_round = [mats.reshape(5, D, D) for mats in w_round]
    b_head = biases[:3]
    b_round = biases[3:].reshape(ROUNDS, 2, D)
    mesh, gathered, sent, ids_row, ids = encode_rows(
        arrived, w_in, w_node, biases, w_round[0]
    )
    sent, partner, neighbours, counted, counts = lax.optimization_barrier(
        (sent, partner, neighbours, counted, counts)
    )
    counts = counts + swapped(counts, "dp", 1)
    index = 2 * ((neighbours - band * blocks + H) % (blocks * bands)).T
    index = index.reshape(K, 2, blocks // 2).swapaxes(0, 1).reshape(-1)
    moved = [(n, place) for n, place in enumerate(walk) if n != place]
    stays = jnp.asarray([n == place for n, place in enumerate(walk)])[band]
    index = lax.ppermute(index, "space", list(enumerate(walk)))

    def at_home(rows):
        return lax.ppermute(rows, "space", [(j, i) for i, j in moved])

    def settled(own, came):
        return jnp.where(stays, own, came.astype(jnp.float32))

    partner_by = partner - band * points - jnp.arange(points, dtype=jnp.int32)
    coded = jnp.where(partner_by >= NEAR, partner_by - NEAR + 1, 0).astype(jnp.bfloat16)
    low_valid = jnp.concatenate([counted.astype(jnp.bfloat16), coded[None, :]], 0)
    valid_around = jnp.concatenate(
        [
            shifted(low_valid[:, points - ROWW :], "space", 1),
            low_valid,
            shifted(low_valid[:, :ROWW], "space", -1),
        ],
        1,
    )
    kept = []
    sent = [sent]
    for layer in range(ROUNDS):
        pieces, start = [], 0
        arrivals = [halo(walk, sent[0], sent[0])]
        if len(sent) > 1:
            sent[1], arrivals[0] = lax.optimization_barrier((sent[1], arrivals[0]))
            arrivals.append(halo(walk, sent[1], sent[1]))
        terms = node_terms(mesh, w_round[layer], b_round[layer])
        if layer == 0:
            (before, after), valid_around, counts = lax.optimization_barrier(
                (arrivals[0], valid_around, counts)
            )
            arrivals = [(before, after)]
        for side in ([rows for rows, _ in arrivals], sent, [rows for _, rows in arrivals]):
            for rows in side:
                pieces.append((rows, start))
                start = start + rows.shape[0]
        mats = w_round[layer]
        if layer + 1 < ROUNDS:
            following = w_round[layer + 1]
            reached = [pieces, pieces] if layer == 0 else [pieces[:-1], pieces[1:]]
            indexes = [index[: K * blocks // 2], index[K * blocks // 2 :]]
            *outs, first = round_forward(
                indexes[0], mesh, reached[0], mats, terms, following, half=0
            )
            *outs, second = round_forward(
                indexes[1], mesh, reached[1], mats, terms, following, half=1, into=outs
            )
            sent = [first, second]
        else:
            decoder = (ids, w_dec, w_out, biases)
            outs = round_forward(index, mesh, pieces, mats, terms, None, decoder)
            outs, rest = outs[:5], outs[5:]
        kept.append((mesh, *outs[1:]))
        mesh = outs[0]
    count = counts[0, 0] * 65536.0 + counts[0, 1] * 256.0 + counts[0, 2]
    wide_valid = valid_around[:CH].astype(jnp.float32)
    coded = valid_around[CH : CH + 1, : points + ROWW].astype(jnp.float32)
    weights = [
        (
            by,
            jnp.where(coded == by - NEAR + 1, 1.0, 0.0)
            * wide_valid[:, : points + ROWW]
            * wide_valid[:, by : by + points + ROWW],
        )
        for by in range(NEAR, ROWW + 1)
    ]
    branch_rows, fetched, decoded, dec_turn = rest
    returned = exchanged(branch_rows)
    branch = inner(returned, poster, 0, 0)[:CH]
    err = state_in.astype(jnp.float32) + branch - targets[0].astype(jnp.float32)
    def widened(values):
        low = values.astype(jnp.bfloat16)
        before = shifted(low[:, points - ROWW :], "space", 1).astype(jnp.float32)
        after = shifted(low[:, :ROWW], "space", -1).astype(jnp.float32)
        return jnp.concatenate([before, values, after], 1)

    wide_err = widened(err)
    paired = jnp.zeros((CH, points + ROWW), jnp.float32)
    pair_total = jnp.zeros((CH, points), jnp.float32)
    for by, both in weights:
        gap = both * (wide_err[:, : points + ROWW] - wide_err[:, by : by + points + ROWW])
        paired = paired + gap
        pair_total = pair_total + gap[:, ROWW:] * (
            wide_err[:, ROWW : ROWW + points] - wide_err[:, ROWW + by : ROWW + by + points]
        )
    local_total = jnp.sum(counted * err * err) + 0.5 * jnp.sum(pair_total)
    grad_pred = 2.0 * counted * err + paired[:, ROWW:]
    for by, both in weights:
        gap = both * (wide_err[:, : points + ROWW] - wide_err[:, by : by + points + ROWW])
        grad_pred = grad_pred - gap[:, ROWW - by : ROWW - by + points]
    grad_pred = grad_pred / count
    grad_rows = jnp.pad(grad_pred.astype(jnp.bfloat16), ((0, HALF - CH), (0, 0)))
    landed = exchanged(inner(poster, grad_rows, 1, 1).astype(jnp.bfloat16))
    landed, final_mesh = lax.optimization_barrier((landed, mesh.astype(jnp.bfloat16)))
    final_mesh = at_home(final_mesh)
    mats_grads = [None] * (2 * ROUNDS)
    bias_grads = [None] * ROUNDS
    carried = ()
    for layer in reversed(range(ROUNDS)):
        old, back, update, agg, slopes = kept[layer]
        first_step = not carried
        grad_mesh, leaving, extra, grad_uin, dest_low, to_before, own, to_after = edges_backward(
            index, back, slopes, w_round[layer], carried,
            (ids_row, landed, dec_turn, w_out, w_dec) if first_step else (),
        )
        if first_step:
            to_before, to_after, final_mesh = lax.optimization_barrier(
                (to_before, to_after, final_mesh)
            )
        from_before, from_after = halo(walk, to_after, to_before)
        if first_step:
            from_before, final_mesh, head_grads = lax.optimization_barrier(
                (
                    from_before,
                    settled(mesh, final_mesh),
                    decode_grads(decoded, landed, fetched, extra),
                )
            )
            grad_wout, grad_wdec, grad_bdec = head_grads
        past = () if first_step else (kept[layer + 1][0], extra)
        part, mats_grads[2 * layer + 1], bias_grads[layer], *source = weight_grads(
            old, dest_low, agg, grad_uin, update, leaving, grad_mesh, w_round[layer], past
        )
        if past:
            mats_grads[2 * layer + 2] = source[0]
        carried = (part, own, from_before, from_after, w_round[layer])
    grad_mesh, leaving, grad_win, grad_wnode, grad_bpair, mats_grads[0] = encode_backward(
        carried, kept[0][0], gathered, arrived, ids, w_in, w_node, biases
    )
    parts = [grad_win, grad_wnode, grad_wdec, grad_wout[:, :CH].reshape(CH, D)]
    parts = parts + mats_grads
    parts = parts + [grad_bpair, grad_bdec] + bias_grads
    keep, send = collect_rows(parts, total_size, peers, place)
    mine, leaving = reduced_piece(keep, send, leaving)
    late = at_home(leaving)
    mine = lax.dynamic_slice_in_dim(mine.reshape(-1), offset, shard)
    lane = lax.broadcasted_iota(jnp.int32, (8, HALF), 1)
    sums, late = summed_everywhere(
        jnp.where(lane == 0, local_total, jnp.sum(mine * mine)), late
    )
    total, norm = sums[0, 0], jnp.sqrt(sums[0, 1])
    node_grads = settled(grad_mesh, late)
    clipped = mine * jnp.minimum(1.0, 0.05 / norm)
    first = 0.9 * moment1 + 0.1 * clipped
    second = 0.999 * moment2 + 0.001 * clipped * clipped
    first_hat = first / (1.0 - 0.9**STEP)
    second_hat = second / (1.0 - 0.999**STEP)
    updated = master - 0.1 * (first_hat / (jnp.sqrt(second_hat) + 1e-08) + 0.1 * master)
    return (
        total.reshape(1),
        count.reshape(1),
        norm.reshape(1),
        updated,
        first,
        second,
        updated.astype(jnp.bfloat16),
        final_mesh.reshape(1, blocks, D),
        node_grads.reshape(1, blocks, D),
        grad_pred.reshape(1, grad_pred.shape[0], points),
    )


def solution(mesh):
    return jax.shard_map(
        functools.partial(shards, walk_of(mesh)),
        mesh=mesh,
        in_specs=(
            P(("dp", "space")),
            P(("dp", "space")),
            P(("dp", "space")),
            P("dp", None, "space"),
            P("dp", None, "space"),
            P("dp", None, "space"),
            P("dp", "space", None),
            P("dp", "space"),
            P("space", None),
            P("space"),
        ),
        out_specs=(
            P(),
            P(),
            P(),
            P(("dp", "space")),
            P(("dp", "space")),
            P(("dp", "space")),
            P(("dp", "space")),
            P("dp", "space", None),
            P("dp", "space", None),
            P("dp", None, "space"),
        ),
        check_vma=False,
    )
```

```python
import functools

import jax
import jax.numpy as jnp
from jax import lax
from jax.experimental import pallas as pl
from jax.experimental.pallas import tpu as pltpu
from jax.sharding import PartitionSpec as P

D = 256
HALF = 128
CH = 78
ROUNDS = 3
K = 6
ROWW = 360
NEAR = 358
STEP = 10
H = 2048
ALL = ("dp", "space")
LIMIT = pltpu.CompilerParams(vmem_limit_bytes=60 * 2**20)


def cost(micros):
    return pl.CostEstimate(flops=0, bytes_accessed=micros * 3_000_000, transcendentals=0)


def inner(left, right, left_dim, right_dim):
    return lax.dot_general(
        left, right, (((left_dim,), (right_dim,)), ((), ())), preferred_element_type=jnp.float32
    )


def sigmoid(value):
    return 0.5 * jnp.tanh(0.5 * value) + 0.5


def silu(value):
    return value * sigmoid(value)


def slope(value):
    sigma = sigmoid(value)
    return sigma * (1.0 + value * (1.0 - sigma))


def shifted(shard, axis, by):
    peers = lax.axis_size(axis)
    pairs = [(i, i + by) for i in range(peers) if 0 <= i + by < peers]
    return lax.ppermute(shard, axis, pairs)


def walk_of(mesh):
    count = mesh.shape["space"]
    chips = [getattr(device, "coords", None) for device in mesh.devices[0].reshape(-1)]
    if any(chip is None for chip in chips) or len(set(map(tuple, chips))) != count:
        return list(range(count))
    at = {tuple(chip): n for n, chip in enumerate(chips)}
    xs, ys, zs = (sorted({chip[n] for chip in at}) for n in range(3))
    if len(xs) * len(ys) * len(zs) != count:
        return list(range(count))
    if (len(xs), len(ys), len(zs)) == (2, 2, 4):
        corners = [(0, 0), (1, 0), (0, 1), (1, 1)]
        planes = [(0, 1, 3, 2), (2, 0, 1, 3), (3, 1, 0, 2), (2, 3, 1, 0)]
        steps = [(*corners[n], z) for z, plane in enumerate(planes) for n in plane]
        return [at[(xs[x], ys[y], zs[z])] for x, y, z in steps]
    walk, plane = [], []
    for n, y in enumerate(ys):
        plane = plane + [(x, y) for x in (xs if n % 2 == 0 else xs[::-1])]
    for n, z in enumerate(zs):
        walk = walk + [at[(x, y, z)] for x, y in (plane if n % 2 == 0 else plane[::-1])]
    return walk


def halo(walk, last, initial):
    up = list(zip(walk, walk[1:] + walk[:1]))
    down = [(j, i) for i, j in up]
    return lax.ppermute(last, "space", up), lax.ppermute(initial, "space", down)


def pieces_of(total, peers):
    share = total // peers
    starts = [share * d // D for d in range(peers)]
    counts = [-(-share * (d + 1) // D) - starts[d] for d in range(peers)]
    shared = [share * d % D != 0 for d in range(peers)]
    height = -(-max(counts) // 16) * 16
    return starts, counts, shared, height


def parts_of():
    return [CH, D, D, CH] + [5 * D] * ROUNDS + [3 + 2 * ROUNDS]


def swapped(value, axis, bit):
    return lax.ppermute(value, axis, [(i, i ^ bit) for i in range(lax.axis_size(axis))])


def bits_of(axis):
    return [1 << n for n in range(lax.axis_size(axis).bit_length() - 1)]


def others(value, axis, bits):
    masks = [sum(bit for n, bit in enumerate(bits) if m >> n & 1) for m in range(1, 1 << len(bits))]
    return [swapped(value, axis, mask) for mask in masks]


def upper_groups():
    bits = bits_of("space")[2:]
    return [tuple(bits[n : n + 2]) for n in range(0, len(bits), 2)]


def orders():
    return [(1, 2), (2, 1)]


def summed_everywhere(value, arriving):
    for bits in reversed(upper_groups()):
        value = sum(others(value, "space", bits), value)
    value = value + swapped(value, "dp", 1)
    value, arriving = lax.optimization_barrier((value, arriving))
    return sum(others(value, "space", (1, 2)), value), arriving


def gathered_blocks(piece, posted):
    held, weights, size = piece[None], {}, 1
    for bits in reversed(upper_groups()):
        held = jnp.concatenate([held] + others(held, "space", bits), 0)
        for n, bit in enumerate(bits):
            weights[bit] = size << n
        size = size << len(bits)
    half = piece.shape[0] // 2
    held = [held[:, :half], held[:, half:]]
    ranks = [dict(weights), dict(weights)]
    for turn in (1, 0):
        if turn == 0:
            held[0], held[1], posted = lax.optimization_barrier((*held, posted))
        for n, order in enumerate(orders()):
            held[n] = jnp.concatenate([held[n], swapped(held[n], "space", order[turn])], 0)
            ranks[n][order[turn]] = size
        size = size << 1
    return (held, [swapped(part, "dp", 1) for part in held], ranks), posted


def spread_rows(gathered, total, peers, place):
    (first, second), (first_far, second_far), ranks = gathered
    starts, counts, shared, height = pieces_of(total, peers)
    half, group = height // 2, first.shape[0]
    rows = -(-total // D)
    sizes = parts_of()
    def at(rank, relative):
        spot = 0
        for bit, weight in rank.items():
            spot = spot + jnp.where((relative & bit) != 0, weight, 0)
        return spot

    def body(place_ref, *refs):
        sources, outs, buffer = refs[:4], refs[4:-1], refs[-1]
        me = place_ref[0]
        mine = me // group
        for d in range(peers):
            relative = (me ^ d) & (group - 1)
            spots = [at(rank, relative) for rank in ranks]

            def lay(one, two, d=d, spots=spots):
                piece = jnp.concatenate([one[spots[0]], two[spots[1]]], 0).astype(jnp.float32)
                start, count = starts[d], counts[d]
                if shared[d]:
                    buffer[start : start + 1, :] = buffer[start : start + 1, :] + piece[:1]
                    buffer[start + 1 : start + count, :] = piece[1:count]
                else:
                    buffer[start : start + count, :] = piece[:count]

            @pl.when(mine == d // group)
            def _():
                lay(sources[0], sources[1])

            @pl.when(mine != d // group)
            def _():
                lay(sources[2], sources[3])

        start = 0
        for out, size in zip(outs, sizes):
            out[:size, :] = buffer[start : start + size, :].astype(out.dtype)
            if out.shape[0] > size:
                out[size:, :] = jnp.zeros((out.shape[0] - size, D), out.dtype)
            start = start + size

    kinds = [jnp.bfloat16] * (4 + ROUNDS) + [jnp.float32]
    talls = [HALF] + sizes[1:]
    return pl.pallas_call(
        body,
        grid_spec=pltpu.PrefetchScalarGridSpec(
            num_scalar_prefetch=1,
            grid=(1,),
            in_specs=[whole(first.shape)] * 4,
            out_specs=[whole((tall, D)) for tall in talls],
            scratch_shapes=[pltpu.VMEM((-(-rows // 8) * 8 + 8, D), jnp.float32)],
        ),
        out_shape=[jax.ShapeDtypeStruct((tall, D), kind) for tall, kind in zip(talls, kinds)],
        compiler_params=LIMIT,
        cost_estimate=cost(4),
        name="spread_rows",
    )(place.reshape(1), first, second, first_far, second_far)


def collect_rows(parts, total, peers, place):
    starts, counts, shared, height = pieces_of(total, peers)
    rows = -(-total // D)
    sizes = [min(part.shape[0], size) for part, size in zip(parts, tall_parts())]
    group = lax.axis_size("space")

    def body(place_ref, *refs):
        sources, keep, send, buffer = refs[:-3], refs[-3], refs[-2], refs[-1]
        start = 0
        for source, size in zip(sources, sizes):
            buffer[start : start + size, :] = source[:size, :]
            start = start + size
        if buffer.shape[0] > start:
            buffer[start:, :] = jnp.zeros((buffer.shape[0] - start, D), jnp.float32)
        me = place_ref[0]
        mine = me // group
        for d in range(peers):
            relative = (me ^ d) & (group - 1)

            @pl.when(mine == d // group)
            def _():
                keep[relative] = buffer[starts[d] : starts[d] + height, :]

            @pl.when(mine != d // group)
            def _():
                send[relative] = buffer[starts[d] : starts[d] + height, :].astype(jnp.bfloat16)

    shape = (group, height, D)
    return pl.pallas_call(
        body,
        grid_spec=pltpu.PrefetchScalarGridSpec(
            num_scalar_prefetch=1,
            grid=(1,),
            in_specs=[whole(part.shape) for part in parts],
            out_specs=[whole(shape), whole(shape)],
            scratch_shapes=[pltpu.VMEM((-(-rows // 8) * 8 + height + 8, D), jnp.float32)],
        ),
        out_shape=[
            jax.ShapeDtypeStruct(shape, jnp.float32),
            jax.ShapeDtypeStruct(shape, jnp.bfloat16),
        ],
        compiler_params=LIMIT,
        cost_estimate=cost(5),
        name="collect_rows",
    )(place.reshape(1), *parts)


def reduced_piece(keep, send, leaving):
    kept = keep + swapped(send, "dp", 1).astype(jnp.float32)
    half = kept.shape[1] // 2
    groups = upper_groups()
    inner_shape = (kept.shape[0] // 4, 2, 2, half, D)
    parts = [kept[:, :half].reshape(inner_shape), kept[:, half:].reshape(inner_shape)]
    for n, order in enumerate(orders()):
        for bit in order:
            spot = 2 if bit == 1 and parts[n].ndim == 5 else 1
            stay = lax.index_in_dim(parts[n], 0, spot, keepdims=False)
            leave = lax.index_in_dim(parts[n], 1, spot, keepdims=False)
            parts[n] = stay + swapped(leave.astype(jnp.bfloat16), "space", bit).astype(jnp.float32)
    part = jnp.concatenate(parts, 1)
    part, leaving = lax.optimization_barrier((part, leaving))
    for bits in groups:
        part = part.reshape((-1, 1 << len(bits)) + part.shape[1:])
        masks = [sum(bit for n, bit in enumerate(bits) if m >> n & 1) for m in range(1 << len(bits))]
        low = part.astype(jnp.bfloat16)
        part = sum(
            [
                swapped(low[:, m], "space", mask).astype(jnp.float32)
                for m, mask in enumerate(masks)
                if m
            ],
            part[:, 0],
        )
    return part[0], leaving


def tall_parts():
    return [CH, D, D, CH] + [D, 4 * D] * ROUNDS + [2, 1] + [2] * ROUNDS


def weave(ref, value):
    rows = value.shape[0]
    ref[pl.ds(0, rows, stride=2), :] = value[:, :HALF]
    ref[pl.ds(1, rows, stride=2), :] = value[:, HALF:]


def unweave(ref):
    rows = ref.shape[0] // 2
    return ref[pl.ds(0, rows, stride=2), :], ref[pl.ds(1, rows, stride=2), :]


def selector():
    row = lax.broadcasted_iota(jnp.int32, (8, HALF), 0)
    lane = lax.broadcasted_iota(jnp.int32, (8, HALF), 1)
    slot = jnp.where(lane == CH, 64.0, jnp.where(lane == CH + 1, 1.0, 0.0))
    known = jnp.where(lane == CH + 2, 1.0, 0.0)
    return jnp.where(row == 0, slot, jnp.where(row == 1, known, 0.0)).astype(jnp.bfloat16)


def ids_along(arrived):
    codes = inner(selector(), arrived, 1, 1)
    return jnp.where(codes[1:2, :] > 0, codes[0:1, :], -1.0).astype(jnp.int32)


def ids_down(arrived):
    codes = inner(arrived, selector(), 1, 1)
    return jnp.where(codes[:, 1:2] > 0, codes[:, 0:1], -1.0).astype(jnp.int32)


def whole(shape):
    return pl.BlockSpec(shape, lambda *_: (0,) * len(shape))


def node_terms(mesh, mats, bias):
    blocks = mesh.shape[0]
    tile = 1024

    def body(mesh_ref, mats_ref, bias_ref, dest_ref, self_ref):
        lowered = mesh_ref[...].astype(jnp.bfloat16)
        weave(dest_ref, inner(lowered, mats_ref[1], 1, 0) + bias_ref[0:1, :])
        self_ref[...] = inner(lowered, mats_ref[3], 1, 0) + bias_ref[1:2, :]

    rows = pl.BlockSpec((tile, D), lambda i: (i, 0))
    woven = pl.BlockSpec((2 * tile, HALF), lambda i: (i, 0))
    return pl.pallas_call(
        body,
        grid=(blocks // tile,),
        in_specs=[rows, whole(mats.shape), whole(bias.shape)],
        out_specs=[woven, rows],
        out_shape=[
            jax.ShapeDtypeStruct((2 * blocks, HALF), jnp.float32),
            jax.ShapeDtypeStruct((blocks, D), jnp.float32),
        ],
        compiler_params=pltpu.CompilerParams(vmem_limit_bytes=63 * 2**20),
        cost_estimate=cost(4),
        name="node_terms",
    )(mesh, mats, bias)


def round_forward(index, mesh, pieces, mats, terms, following, decoder=(), half=None, into=()):
    blocks = mesh.shape[0]
    tile, chunk = 512, 16
    turns, high = tile // chunk, 2 * chunk
    more = following is not None
    reach = 2 * (blocks + 2 * H)
    steps = blocks // tile if half is None else blocks // tile // 2
    shift = 0 if half is None else half * steps

    def body(index_ref, mesh_ref, *refs):
        sources, refs = refs[: len(pieces)], refs[len(pieces) :]
        (mats_ref, dest_ref, self_ref), refs = refs[:3], refs[3:]
        table, rows, wide = refs[-3:]
        if more:
            next_ref, refs = refs[0], refs[1 + len(into) :]
            new_ref, back_ref, update_ref, agg_ref, slope_ref, sent_ref = refs[:6]
        else:
            ids_ref, dec_ref, out_ref, head_ref = refs[:4]
            new_ref, back_ref, update_ref, agg_ref, slope_ref = refs[4:9]
            branch_ref, fetched_ref, decoded_ref, turn_ref, total_ref = refs[9:14]
        step = pl.program_id(0)

        @pl.when(step == 0)
        def _():
            for source, (_, start) in zip(sources, pieces):

                @pl.loop(0, source.shape[0] // 256)
                def _(i, source=source, start=start):
                    at = pl.multiple_of(i * 256, 256)
                    to = pl.multiple_of(start + at, 256)
                    table[pl.ds(to, 256), :] = source[pl.ds(at, 256), :].astype(jnp.float32)

        mesh_in = mesh_ref[...]

        part = blocks // 2
        if half is None:
            origin = step // (steps // 2) * (K * part) + lax.rem(step, steps // 2) * tile
        else:
            origin = step * tile

        def fetch(turn):
            for edge in range(K):
                base = edge * part + turn * chunk + origin
                spots = [index_ref[base + u] for u in range(chunk)]
                values = [table[pl.ds(pl.multiple_of(spot, 2), 2), :] for spot in spots]
                for u in range(chunk):
                    spot = pl.multiple_of(edge * 2 * tile + turn * high + 2 * u, 2)
                    rows[pl.ds(spot, 2), :] = values[u]

        def load(turn):
            at = pl.multiple_of(turn * high, high)
            taken = [
                rows[pl.ds(pl.multiple_of(edge * 2 * tile + turn * high, high), high), :]
                for edge in range(K)
            ]
            return at, dest_ref[pl.ds(at, high), :], taken

        def dense(at, dest, taken):
            total = None
            for edge in range(K):
                value = taken[edge] + dest
                sigma = sigmoid(value)
                out = value * sigma
                slope_ref[edge, pl.ds(at, high), :] = (sigma + out * (1.0 - sigma)).astype(
                    jnp.bfloat16
                )
                total = out if total is None else total + out
            wide[pl.ds(at, high), :] = total * (1.0 / K)

        def some(turn, carry):
            loaded = load(turn - 1)
            fetch(turn)
            dense(*loaded)
            return carry

        fetch(0)
        lax.fori_loop(1, turns, some, 0)
        dense(*load(turns - 1))
        first, second = unweave(wide)
        first, second = first.astype(jnp.bfloat16), second.astype(jnp.bfloat16)
        agg_ref[:, :HALF] = first
        agg_ref[:, HALF:] = second
        update_in = (
            inner(first, mats_ref[2, :HALF, :], 1, 0)
            + inner(second, mats_ref[2, HALF:, :], 1, 0)
            + self_ref[...]
        )
        sigma = sigmoid(update_in)
        out = update_in * sigma
        back_ref[...] = sigma + out * (1.0 - sigma)
        update = out.astype(jnp.bfloat16)
        update_ref[...] = update
        new = mesh_in + inner(update, mats_ref[4], 1, 0)
        new_ref[...] = new
        lowered = new.astype(jnp.bfloat16)
        if more:
            weave(wide, inner(lowered, next_ref[0], 1, 0))
            sent_ref[...] = wide[...].astype(jnp.bfloat16)
            return
        nodes = lax.broadcasted_iota(jnp.int32, (ids_ref.shape[0], tile), 1) + step * tile
        chooser = jnp.where(nodes == ids_ref[...], 1.0, 0.0).astype(jnp.bfloat16)
        found = inner(chooser, lowered, 1, 0)

        @pl.when(step == 0)
        def _():
            total_ref[...] = found

        @pl.when(step > 0)
        def _():
            total_ref[...] += found

        @pl.when(step == blocks // tile - 1)
        def _():
            fetched = total_ref[...].astype(jnp.bfloat16)
            fetched_ref[...] = fetched
            value = inner(fetched, dec_ref[...], 1, 0) + head_ref[2:3, :]
            sigma = sigmoid(value)
            out = value * sigma
            turn_ref[...] = sigma + out * (1.0 - sigma)
            decoded = out.astype(jnp.bfloat16)
            decoded_ref[...] = decoded
            branch_ref[...] = inner(decoded, out_ref[...], 1, 0).astype(jnp.bfloat16)

    whole_rows = pl.BlockSpec((tile, D), lambda i, *_: (i + shift, 0))
    woven = pl.BlockSpec((2 * tile, HALF), lambda i, *_: (i + shift, 0))
    ins = [whole_rows] + [pl.BlockSpec(memory_space=pltpu.VMEM)] * len(pieces)
    ins = ins + [whole(mats.shape), woven, whole_rows]
    outs = [whole_rows] * 4 + [pl.BlockSpec((K, 2 * tile, HALF), lambda i, *_: (0, i + shift, 0))]
    shapes = [
        jax.ShapeDtypeStruct((blocks, D), jnp.float32),
        jax.ShapeDtypeStruct((blocks, D), jnp.float32),
        jax.ShapeDtypeStruct((blocks, D), jnp.bfloat16),
        jax.ShapeDtypeStruct((blocks, D), jnp.bfloat16),
        jax.ShapeDtypeStruct((K, 2 * blocks, HALF), jnp.bfloat16),
    ]
    args = [index, mesh] + [rows for rows, _ in pieces] + [mats, *terms]
    if more:
        ins.append(pl.BlockSpec((1, D, D), lambda *_: (0, 0, 0)))
        outs.append(pl.BlockSpec((2 * tile, HALF), lambda i, *_: (i, 0)))
        shapes.append(jax.ShapeDtypeStruct((2 * tile * steps, HALF), jnp.bfloat16))
        args.append(following)
    aliases = {len(args) + n: n for n in range(len(into))}
    ins = ins + [pl.BlockSpec(memory_space=pl.ANY)] * len(into)
    args = args + list(into)
    scratch = []
    if decoder:
        posts = decoder[0].shape[0]
        ins = ins + [whole(arg.shape) for arg in decoder]
        args = args + list(decoder)
        for width, kind in ((HALF, jnp.bfloat16), (D, jnp.bfloat16), (D, jnp.bfloat16), (D, jnp.float32)):
            outs.append(whole((posts, width)))
            shapes.append(jax.ShapeDtypeStruct((posts, width), kind))
        scratch = [pltpu.VMEM((posts, D), jnp.float32)]
    return pl.pallas_call(
        body,
        grid_spec=pltpu.PrefetchScalarGridSpec(
            num_scalar_prefetch=1,
            grid=(steps,),
            in_specs=ins,
            out_specs=outs,
            scratch_shapes=scratch
            + [
                pltpu.VMEM((reach, HALF), jnp.float32),
                pltpu.VMEM((K * 2 * tile, HALF), jnp.float32),
                pltpu.VMEM((2 * tile, HALF), jnp.float32),
            ],
        ),
        out_shape=shapes,
        input_output_aliases=aliases,
        compiler_params=pltpu.CompilerParams(vmem_limit_bytes=63 * 2**20),
        cost_estimate=cost(24 if half is None else 14),
        name="round_forward",
    )(*args)


def edges_backward(index, back, slopes, mats, carried=(), landed=()):
    blocks = back.shape[0]
    tile, chunk = 512, 16
    steps, turns, high = blocks // tile, tile // chunk, 2 * chunk
    reach = 2 * (blocks + 2 * H)

    def body(*refs):
        if carried:
            index_ref, back_ref, slope_ref, mats_ref = refs[:4]
            past, rest = refs[4:9], refs[9:]
            (new_ref, out_ref, sent_ref), rest = rest[:3], rest[3:]
        else:
            index_ref, back_ref, slope_ref, mats_ref = refs[:4]
            (ids_ref, landed_ref, turn_ref, w_out_ref, w_dec_ref), rest = refs[4:9], refs[9:]
            (new_ref, out_ref, gdec_ref), rest = rest[:3], rest[3:]
            gathered, rest = rest[5], rest[:5] + rest[6:]
        guin_ref, low_ref, before_ref, own_ref, after_ref, wide, wider, flows, *tables = rest
        step = pl.program_id(0)

        @pl.when(step == 0)
        def _():
            @pl.loop(0, reach // 256)
            def _(i):
                for table in tables:
                    table[pl.ds(pl.multiple_of(i * 256, 256), 256), :] = jnp.zeros(
                        (256, HALF), jnp.float32
                    )

        if carried:
            new, one, two = ended(*past, wide)
            sent_ref[:, :HALF] = one
            sent_ref[:, HALF:] = two
            new_ref[...] = new
            grad_out = new.astype(jnp.bfloat16)
            out_ref[...] = grad_out
        else:

            @pl.when(step == 0)
            def _():
                grad_dec = inner(landed_ref[...], w_out_ref[...], 1, 1) * turn_ref[...]
                grad_dec = grad_dec.astype(jnp.bfloat16)
                gdec_ref[...] = grad_dec
                gathered[...] = inner(grad_dec, w_dec_ref[...], 1, 1).astype(jnp.bfloat16)

            nodes = lax.broadcasted_iota(jnp.int32, (tile, landed_ref.shape[0]), 0) + step * tile
            chooser = jnp.where(nodes == ids_ref[...], 1.0, 0.0).astype(jnp.bfloat16)
            new = inner(chooser, gathered[...], 1, 0)
            new_ref[...] = new
            grad_out = new.astype(jnp.bfloat16)
            out_ref[...] = grad_out
        grad_uin = (inner(grad_out, mats_ref[4], 1, 1) * back_ref[...]).astype(jnp.bfloat16)
        guin_ref[...] = grad_uin
        weave(wide, inner(grad_uin, mats_ref[2], 1, 1) * (1.0 / K))

        def dense(turn):
            at = pl.multiple_of(turn * high, high)
            grad_agg = wide[pl.ds(at, high), :]
            total, parts = None, []
            for edge in range(K):
                flow = grad_agg * slope_ref[edge, pl.ds(at, high), :].astype(jnp.float32)
                parts.append(flow)
                total = flow if total is None else total + flow
            return at, total, parts

        def keep(turn, at, total, parts):
            for edge in range(K):
                spot = pl.multiple_of(edge * 2 * tile + turn * high, high)
                flows[pl.ds(spot, high), :] = parts[edge]
            wider[pl.ds(at, high), :] = total

        part = blocks // 2
        origin = step // (steps // 2) * (K * part) + lax.rem(step, steps // 2) * tile

        def scatter(turn):
            for u in range(chunk):
                spots, sums = [], []
                for edge in range(K):
                    base = edge * part + turn * chunk + origin
                    spots.append(pl.multiple_of(index_ref[base + u], 2))
                for edge in range(K):
                    spot = pl.multiple_of(edge * 2 * tile + turn * high + 2 * u, 2)
                    sums.append(tables[edge][pl.ds(spots[edge], 2), :] + flows[pl.ds(spot, 2), :])
                for edge in range(K):
                    tables[edge][pl.ds(spots[edge], 2), :] = sums[edge]

        def some(turn, carry):
            found = dense(turn)
            scatter(turn - 1)
            keep(turn, *found)
            return carry

        keep(0, *dense(0))
        lax.fori_loop(1, turns, some, 0)
        scatter(turns - 1)
        first, second = unweave(wider)
        low_ref[:, :HALF] = first.astype(jnp.bfloat16)
        low_ref[:, HALF:] = second.astype(jnp.bfloat16)

        @pl.when(step == steps - 1)
        def _():
            def summed(at):
                value = tables[0][pl.ds(at, 256), :]
                for table in tables[1:]:
                    value = value + table[pl.ds(at, 256), :]
                return value

            @pl.loop(0, 2 * H // 256)
            def _(i):
                at = pl.multiple_of(i * 256, 256)
                far = pl.multiple_of(2 * H + 2 * blocks + at, 256)
                before_ref[pl.ds(at, 256), :] = summed(at).astype(jnp.bfloat16)
                after_ref[pl.ds(at, 256), :] = summed(far).astype(jnp.bfloat16)

            @pl.loop(0, 2 * blocks // 256)
            def _(i):
                at = pl.multiple_of(i * 256, 256)
                own_ref[pl.ds(at, 256), :] = summed(pl.multiple_of(2 * H + at, 256))

    rows = pl.BlockSpec((tile, D), lambda i, *_: (i, 0))
    woven = pl.BlockSpec((2 * tile, HALF), lambda i, *_: (i, 0))
    low = jax.ShapeDtypeStruct((blocks, D), jnp.bfloat16)
    low_posts = (landed[1].shape[0], D) if landed else None
    last = low if carried else jax.ShapeDtypeStruct(low_posts, jnp.bfloat16)
    return pl.pallas_call(
        body,
        grid_spec=pltpu.PrefetchScalarGridSpec(
            num_scalar_prefetch=1,
            grid=(steps,),
            in_specs=[
                rows,
                pl.BlockSpec((K, 2 * tile, HALF), lambda i, *_: (0, i, 0)),
                whole(mats.shape),
            ]
            + ([rows] + [woven] * 3 + [whole(mats.shape)] if carried else [])
            + [whole(arg.shape) for arg in landed],
            out_specs=([rows] * 3 if carried else [rows, rows, whole(low_posts)])
            + [
                rows, rows,
                whole((2 * H, HALF)), whole((2 * blocks, HALF)), whole((2 * H, HALF)),
            ],
            scratch_shapes=([] if carried else [pltpu.VMEM(low_posts, jnp.bfloat16)])
            + [
                pltpu.VMEM((2 * tile, HALF), jnp.float32),
                pltpu.VMEM((2 * tile, HALF), jnp.float32),
                pltpu.VMEM((2 * tile * K, HALF), jnp.float32),
            ]
            + [pltpu.VMEM((reach, HALF), jnp.float32)] * K,
        ),
        out_shape=[
            jax.ShapeDtypeStruct((blocks, D), jnp.float32),
            low,
            last,
            low,
            low,
            jax.ShapeDtypeStruct((2 * H, HALF), jnp.bfloat16),
            jax.ShapeDtypeStruct((2 * blocks, HALF), jnp.float32),
            jax.ShapeDtypeStruct((2 * H, HALF), jnp.bfloat16),
        ],
        compiler_params=pltpu.CompilerParams(vmem_limit_bytes=63 * 2**20),
        cost_estimate=cost(28 if carried else 25),
        name="edges_backward",
    )(index, back, slopes, mats, *carried, *landed)


def ended(part_ref, own_ref, first_ref, last_ref, mats_ref, wide):
    wide[...] = (
        own_ref[...] + first_ref[...].astype(jnp.float32) + last_ref[...].astype(jnp.float32)
    )
    one, two = unweave(wide)
    one, two = one.astype(jnp.bfloat16), two.astype(jnp.bfloat16)
    new = (
        part_ref[...]
        + inner(one, mats_ref[0, :, :HALF], 1, 1)
        + inner(two, mats_ref[0, :, HALF:], 1, 1)
    )
    return new, one, two


def weight_grads(mesh, dest_low, agg, grad_uin, update, leaving, grad_mesh, mats, past=()):
    blocks = mesh.shape[0]
    tile = 512

    def body(mesh_ref, dest_ref, agg_ref, guin_ref, update_ref, out_ref, grad_ref, mats_ref, *refs):
        if past:
            (old_ref, sent_ref), refs = refs[:2], refs[2:]
        part_ref, grads_ref, bias_ref = refs[:3]

        @pl.when(pl.program_id(0) == 0)
        def _():
            for ref in refs[1:]:
                ref[...] = jnp.zeros(ref.shape, jnp.float32)

        lowered = mesh_ref[...].astype(jnp.bfloat16)
        dest, guin = dest_ref[...], guin_ref[...]
        grads_ref[:D, :] += inner(lowered, dest, 0, 0)
        grads_ref[D : 2 * D, :] += inner(agg_ref[...], guin, 0, 0)
        grads_ref[2 * D : 3 * D, :] += inner(lowered, guin, 0, 0)
        grads_ref[3 * D :, :] += inner(update_ref[...], out_ref[...], 0, 0)
        bias_ref[0:1, :] += jnp.sum(dest.astype(jnp.float32), 0, keepdims=True)
        bias_ref[1:2, :] += jnp.sum(guin.astype(jnp.float32), 0, keepdims=True)
        part_ref[...] = (
            grad_ref[...] + inner(guin, mats_ref[3], 1, 1) + inner(dest, mats_ref[1], 1, 1)
        )
        if past:
            refs[3][...] += inner(old_ref[...].astype(jnp.bfloat16), sent_ref[...], 0, 0)

    rows = pl.BlockSpec((tile, D), lambda i: (i, 0))
    shapes = [(4 * D, D), (2, D)] + ([(D, D)] if past else [])
    return pl.pallas_call(
        body,
        grid=(blocks // tile,),
        in_specs=[rows] * 7 + [whole(mats.shape)] + [rows] * len(past),
        out_specs=[rows] + [whole(shape) for shape in shapes],
        out_shape=[jax.ShapeDtypeStruct((blocks, D), jnp.float32)]
        + [jax.ShapeDtypeStruct(shape, jnp.float32) for shape in shapes],
        compiler_params=pltpu.CompilerParams(vmem_limit_bytes=63 * 2**20),
        cost_estimate=cost(10),
        name="weight_grads",
    )(mesh, dest_low, agg, grad_uin, update, leaving, grad_mesh, mats, *past)


def decode_grads(decoded, landed, fetched, grad_dec):
    def body(decoded_ref, landed_ref, fetched_ref, grad_ref, gout_ref, gdec_ref, bias_ref):
        gout_ref[...] = inner(decoded_ref[...], landed_ref[...], 0, 0)
        gdec_ref[...] = inner(fetched_ref[...], grad_ref[...], 0, 0)
        bias_ref[...] = jnp.sum(grad_ref[...].astype(jnp.float32), 0, keepdims=True)

    return pl.pallas_call(
        body,
        out_shape=[jax.ShapeDtypeStruct(shape, jnp.float32) for shape in ((D, HALF), (D, D), (1, D))],
        compiler_params=pltpu.CompilerParams(vmem_limit_bytes=63 * 2**20),
        cost_estimate=cost(3),
        name="decode_grads",
    )(decoded, landed, fetched, grad_dec)


def encode_rows(arrived, w_in, w_node, biases, source):
    posts = arrived.shape[0]
    tile = 512

    def body(
        arrived_ref, in_ref, node_ref, bias_ref, source_ref,
        mesh_ref, gathered_ref, sent_ref, ids_ref, down_ref, encoded, wide,
    ):
        step = pl.program_id(0)

        @pl.when(step == 0)
        def _():
            entering = inner(arrived_ref[...], in_ref[...], 1, 0) + bias_ref[0:1, :]
            encoded[...] = silu(entering).astype(jnp.bfloat16)
            ids_ref[...] = ids_along(arrived_ref[...])
            down_ref[...] = ids_down(arrived_ref[...])

        nodes = lax.broadcasted_iota(jnp.int32, (tile, posts), 0) + step * tile
        chooser = jnp.where(nodes == ids_ref[...], 1.0, 0.0).astype(jnp.bfloat16)
        gathered = inner(chooser, encoded[...], 1, 0).astype(jnp.bfloat16)
        gathered_ref[...] = gathered
        mesh = silu(inner(gathered, node_ref[...], 1, 0) + bias_ref[1:2, :])
        mesh_ref[...] = mesh
        weave(wide, inner(mesh.astype(jnp.bfloat16), source_ref[0], 1, 0))
        sent_ref[...] = wide[...].astype(jnp.bfloat16)

    rows = pl.BlockSpec((tile, D), lambda i: (i, 0))
    args = (arrived, w_in, w_node, biases, source)
    return pl.pallas_call(
        body,
        grid=(H // tile,),
        in_specs=[whole(arg.shape) for arg in args[:-1]]
        + [pl.BlockSpec((1, D, D), lambda *_: (0, 0, 0))],
        out_specs=[rows, rows, pl.BlockSpec((2 * tile, HALF), lambda i: (i, 0))]
        + [whole((1, posts)), whole((posts, 1))],
        out_shape=[
            jax.ShapeDtypeStruct((H, D), jnp.float32),
            jax.ShapeDtypeStruct((H, D), jnp.bfloat16),
            jax.ShapeDtypeStruct((2 * H, HALF), jnp.bfloat16),
            jax.ShapeDtypeStruct((1, posts), jnp.int32),
            jax.ShapeDtypeStruct((posts, 1), jnp.int32),
        ],
        scratch_shapes=[pltpu.VMEM((posts, D), jnp.bfloat16), pltpu.VMEM((2 * tile, HALF), jnp.float32)],
        compiler_params=LIMIT,
        cost_estimate=cost(5),
        name="encode_rows",
    )(*args)


def encode_backward(carried, mesh, gathered, arrived, ids, w_in, w_node, biases):
    blocks = mesh.shape[0]
    posts = arrived.shape[0]
    tile = 512
    steps = blocks // tile

    def body(
        part_ref, own_ref, first_ref, last_ref, mats_ref,
        mesh_ref, gathered_ref, arrived_ref, ids_ref, in_ref, node_ref, bias_ref,
        new_ref, out_ref, gin_ref, gnode_ref, gbias_ref, gsource_ref, total, wide,
    ):
        step = pl.program_id(0)

        @pl.when(step == 0)
        def _():
            for ref in (total, gnode_ref, gbias_ref, gsource_ref):
                ref[...] = jnp.zeros(ref.shape, jnp.float32)

        new, one, two = ended(part_ref, own_ref, first_ref, last_ref, mats_ref, wide)
        new_ref[...] = new
        out_ref[...] = new.astype(jnp.bfloat16)
        lowered = mesh_ref[...].astype(jnp.bfloat16)
        gsource_ref[:, :HALF] += inner(lowered, one, 0, 0)
        gsource_ref[:, HALF:] += inner(lowered, two, 0, 0)
        node_in = inner(gathered_ref[...], node_ref[...], 1, 0) + bias_ref[1:2, :]
        grad_node = (new * slope(node_in)).astype(jnp.bfloat16)
        gbias_ref[1:2, :] += jnp.sum(grad_node.astype(jnp.float32), 0, keepdims=True)
        gnode_ref[...] += inner(gathered_ref[...], grad_node, 0, 0)
        back = inner(grad_node, node_ref[...], 1, 1).astype(jnp.bfloat16)
        nodes = lax.broadcasted_iota(jnp.int32, (posts, tile), 1) + step * tile
        chooser = jnp.where(nodes == ids_ref[...], 1.0, 0.0).astype(jnp.bfloat16)
        total[...] += inner(chooser, back, 1, 0)

        @pl.when(step == steps - 1)
        def _():
            entering = inner(arrived_ref[...], in_ref[...], 1, 0) + bias_ref[0:1, :]
            grad_enc = (total[...] * slope(entering)).astype(jnp.bfloat16)
            gbias_ref[0:1, :] = jnp.sum(grad_enc.astype(jnp.float32), 0, keepdims=True)
            gin_ref[...] = inner(arrived_ref[...], grad_enc, 0, 0)

    rows = pl.BlockSpec((tile, D), lambda i: (i, 0))
    woven = pl.BlockSpec((2 * tile, HALF), lambda i: (i, 0))
    args = (arrived, ids, w_in, w_node, biases)
    shapes = [(HALF, D), (D, D), (2, D), (D, D)]
    return pl.pallas_call(
        body,
        grid=(steps,),
        in_specs=[rows] + [woven] * 3 + [whole(carried[4].shape), rows, rows]
        + [whole(arg.shape) for arg in args],
        out_specs=[rows, rows] + [whole(shape) for shape in shapes],
        out_shape=[
            jax.ShapeDtypeStruct((blocks, D), jnp.float32),
            jax.ShapeDtypeStruct((blocks, D), jnp.bfloat16),
        ]
        + [jax.ShapeDtypeStruct(shape, jnp.float32) for shape in shapes],
        scratch_shapes=[pltpu.VMEM((posts, D), jnp.float32), pltpu.VMEM((2 * tile, HALF), jnp.float32)],
        compiler_params=LIMIT,
        cost_estimate=cost(10),
        name="encode_backward",
    )(*carried, mesh, gathered, *args)


def shards(walk, master, moment1, moment2, inputs, targets, valid, owner, slot, neighbours, partner):
    bands = lax.axis_size("space")
    band = lax.axis_index("space")
    peers = lax.axis_size(ALL)
    place = lax.axis_index(ALL)
    shard = master.shape[0]
    total_size = shard * peers
    height = pieces_of(total_size, peers)[3]
    offset = lax.rem(lax.rem(shard, D) * place, D)
    piece = lax.dynamic_update_slice_in_dim(
        jnp.zeros((height * D,), jnp.bfloat16), master.astype(jnp.bfloat16), offset, 0
    )
    state_in = inputs[0]
    counted = valid[0].astype(jnp.float32)
    local_count = jnp.sum(valid[0])
    digits = (local_count >> jnp.array([16, 8, 0], jnp.int32)) & 255
    digits = jnp.pad(digits, (CH + 3, HALF - CH - 6)).astype(jnp.float32)[None, :]
    points = state_in.shape[1]
    blocks = neighbours.shape[0]
    assert blocks == H
    capacity = max(2, 2 * points // bands)
    target_band = owner[0, :, 0]
    hits = (target_band[:, None] == jnp.arange(bands, dtype=jnp.int32)[None, :]).astype(jnp.int32)
    ranks = jnp.sum(jnp.cumsum(hits, 0) * hits, 1) - 1
    places_out = jnp.sum(hits * jnp.asarray(walk, jnp.int32)[None, :], 1) * capacity + ranks
    poster = (
        jnp.arange(bands * capacity, dtype=jnp.int32)[:, None] == places_out[None, :]
    ).astype(jnp.bfloat16)
    spots = slot[0][None, :]
    columns = jnp.concatenate(
        [
            state_in,
            (spots // 64).astype(jnp.bfloat16),
            (spots % 64).astype(jnp.bfloat16),
            jnp.ones((1, points), jnp.bfloat16),
            jnp.zeros((HALF - CH - 3, points), jnp.bfloat16),
        ],
        0,
    )

    def exchanged(rows):
        return lax.all_to_all(
            rows.reshape(bands, capacity, HALF), "space", split_axis=0, concat_axis=0, tiled=True
        ).reshape(bands * capacity, HALF)

    held, posted = gathered_blocks(
        piece.reshape(height, D), (inner(poster, columns, 1, 1) + digits).astype(jnp.bfloat16)
    )
    arrived = exchanged(posted)
    w_in, w_node, w_dec, w_out, *w_round, biases = spread_rows(
        held, total_size, peers, place
    )
    arrived, biases = lax.optimization_barrier((arrived, biases))
    counts = arrived.reshape(bands, capacity, HALF)[:, 0, CH + 3 : CH + 6].astype(jnp.float32)
    counts = jnp.sum(counts, 0, keepdims=True)
    w_out = jnp.pad(w_out.reshape(D, CH), ((0, 0), (0, HALF - CH)))
    w_round = [mats.reshape(5, D, D) for mats in w_round]
    b_head = biases[:3]
    b_round = biases[3:].reshape(ROUNDS, 2, D)
    mesh, gathered, sent, ids_row, ids = encode_rows(
        arrived, w_in, w_node, biases, w_round[0]
    )
    sent, partner, neighbours, counted, counts = lax.optimization_barrier(
        (sent, partner, neighbours, counted, counts)
    )
    counts = counts + swapped(counts, "dp", 1)
    index = 2 * ((neighbours - band * blocks + H) % (blocks * bands)).T
    index = index.reshape(K, 2, blocks // 2).swapaxes(0, 1).reshape(-1)
    moved = [(n, place) for n, place in enumerate(walk) if n != place]
    stays = jnp.asarray([n == place for n, place in enumerate(walk)])[band]
    index = lax.ppermute(index, "space", list(enumerate(walk)))

    def at_home(rows):
        return lax.ppermute(rows, "space", [(j, i) for i, j in moved])

    def settled(own, came):
        return jnp.where(stays, own, came.astype(jnp.float32))

    partner_by = partner - band * points - jnp.arange(points, dtype=jnp.int32)
    coded = jnp.where(partner_by >= NEAR, partner_by - NEAR + 1, 0).astype(jnp.bfloat16)
    low_valid = jnp.concatenate([counted.astype(jnp.bfloat16), coded[None, :]], 0)
    valid_around = jnp.concatenate(
        [
            shifted(low_valid[:, points - ROWW :], "space", 1),
            low_valid,
            shifted(low_valid[:, :ROWW], "space", -1),
        ],
        1,
    )
    kept = []
    sent = [sent]
    for layer in range(ROUNDS):
        pieces, start = [], 0
        arrivals = [halo(walk, sent[0], sent[0])]
        if len(sent) > 1:
            sent[1], arrivals[0] = lax.optimization_barrier((sent[1], arrivals[0]))
            arrivals.append(halo(walk, sent[1], sent[1]))
        terms = node_terms(mesh, w_round[layer], b_round[layer])
        if layer == 0:
            (before, after), valid_around, counts = lax.optimization_barrier(
                (arrivals[0], valid_around, counts)
            )
            arrivals = [(before, after)]
        for side in ([rows for rows, _ in arrivals], sent, [rows for _, rows in arrivals]):
            for rows in side:
                pieces.append((rows, start))
                start = start + rows.shape[0]
        mats = w_round[layer]
        if layer + 1 < ROUNDS:
            following = w_round[layer + 1]
            reached = [pieces, pieces] if layer == 0 else [pieces[:-1], pieces[1:]]
            indexes = [index[: K * blocks // 2], index[K * blocks // 2 :]]
            *outs, first = round_forward(
                indexes[0], mesh, reached[0], mats, terms, following, half=0
            )
            *outs, second = round_forward(
                indexes[1], mesh, reached[1], mats, terms, following, half=1, into=outs
            )
            sent = [first, second]
        else:
            decoder = (ids, w_dec, w_out, biases)
            outs = round_forward(index, mesh, pieces, mats, terms, None, decoder)
            outs, rest = outs[:5], outs[5:]
        kept.append((mesh, *outs[1:]))
        mesh = outs[0]
    count = counts[0, 0] * 65536.0 + counts[0, 1] * 256.0 + counts[0, 2]
    wide_valid = valid_around[:CH].astype(jnp.float32)
    coded = valid_around[CH : CH + 1, : points + ROWW].astype(jnp.float32)
    weights = [
        (
            by,
            jnp.where(coded == by - NEAR + 1, 1.0, 0.0)
            * wide_valid[:, : points + ROWW]
            * wide_valid[:, by : by + points + ROWW],
        )
        for by in range(NEAR, ROWW + 1)
    ]
    branch_rows, fetched, decoded, dec_turn = rest
    returned = exchanged(branch_rows)
    branch = inner(returned, poster, 0, 0)[:CH]
    err = state_in.astype(jnp.float32) + branch - targets[0].astype(jnp.float32)
    def widened(values):
        low = values.astype(jnp.bfloat16)
        before = shifted(low[:, points - ROWW :], "space", 1).astype(jnp.float32)
        after = shifted(low[:, :ROWW], "space", -1).astype(jnp.float32)
        return jnp.concatenate([before, values, after], 1)

    wide_err = widened(err)
    paired = jnp.zeros((CH, points + ROWW), jnp.float32)
    pair_total = jnp.zeros((CH, points), jnp.float32)
    for by, both in weights:
        gap = both * (wide_err[:, : points + ROWW] - wide_err[:, by : by + points + ROWW])
        paired = paired + gap
        pair_total = pair_total + gap[:, ROWW:] * (
            wide_err[:, ROWW : ROWW + points] - wide_err[:, ROWW + by : ROWW + by + points]
        )
    local_total = jnp.sum(counted * err * err) + 0.5 * jnp.sum(pair_total)
    grad_pred = 2.0 * counted * err + paired[:, ROWW:]
    for by, both in weights:
        gap = both * (wide_err[:, : points + ROWW] - wide_err[:, by : by + points + ROWW])
        grad_pred = grad_pred - gap[:, ROWW - by : ROWW - by + points]
    grad_pred = grad_pred / count
    grad_rows = jnp.pad(grad_pred.astype(jnp.bfloat16), ((0, HALF - CH), (0, 0)))
    landed = exchanged(inner(poster, grad_rows, 1, 1).astype(jnp.bfloat16))
    landed, final_mesh = lax.optimization_barrier((landed, mesh.astype(jnp.bfloat16)))
    final_mesh = at_home(final_mesh)
    mats_grads = [None] * (2 * ROUNDS)
    bias_grads = [None] * ROUNDS
    carried = ()
    for layer in reversed(range(ROUNDS)):
        old, back, update, agg, slopes = kept[layer]
        first_step = not carried
        grad_mesh, leaving, extra, grad_uin, dest_low, to_before, own, to_after = edges_backward(
            index, back, slopes, w_round[layer], carried,
            (ids_row, landed, dec_turn, w_out, w_dec) if first_step else (),
        )
        if first_step:
            to_before, to_after, final_mesh = lax.optimization_barrier(
                (to_before, to_after, final_mesh)
            )
        from_before, from_after = halo(walk, to_after, to_before)
        if first_step:
            from_before, final_mesh, head_grads = lax.optimization_barrier(
                (
                    from_before,
                    settled(mesh, final_mesh),
                    decode_grads(decoded, landed, fetched, extra),
                )
            )
            grad_wout, grad_wdec, grad_bdec = head_grads
        past = () if first_step else (kept[layer + 1][0], extra)
        part, mats_grads[2 * layer + 1], bias_grads[layer], *source = weight_grads(
            old, dest_low, agg, grad_uin, update, leaving, grad_mesh, w_round[layer], past
        )
        if past:
            mats_grads[2 * layer + 2] = source[0]
        carried = (part, own, from_before, from_after, w_round[layer])
    grad_mesh, leaving, grad_win, grad_wnode, grad_bpair, mats_grads[0] = encode_backward(
        carried, kept[0][0], gathered, arrived, ids, w_in, w_node, biases
    )
    parts = [grad_win, grad_wnode, grad_wdec, grad_wout[:, :CH].reshape(CH, D)]
    parts = parts + mats_grads
    parts = parts + [grad_bpair, grad_bdec] + bias_grads
    keep, send = collect_rows(parts, total_size, peers, place)
    mine, leaving = reduced_piece(keep, send, leaving)
    late = at_home(leaving)
    mine = lax.dynamic_slice_in_dim(mine.reshape(-1), offset, shard)
    lane = lax.broadcasted_iota(jnp.int32, (8, HALF), 1)
    sums, late = summed_everywhere(
        jnp.where(lane == 0, local_total, jnp.sum(mine * mine)), late
    )
    total, norm = sums[0, 0], jnp.sqrt(sums[0, 1])
    node_grads = settled(grad_mesh, late)
    clipped = mine * jnp.minimum(1.0, 0.05 / norm)
    first = 0.9 * moment1 + 0.1 * clipped
    second = 0.999 * moment2 + 0.001 * clipped * clipped
    first_hat = first / (1.0 - 0.9**STEP)
    second_hat = second / (1.0 - 0.999**STEP)
    updated = master - 0.1 * (first_hat / (jnp.sqrt(second_hat) + 1e-08) + 0.1 * master)
    return (
        total.reshape(1),
        count.reshape(1),
        norm.reshape(1),
        updated,
        first,
        second,
        updated.astype(jnp.bfloat16),
        final_mesh.reshape(1, blocks, D),
        node_grads.reshape(1, blocks, D),
        grad_pred.reshape(1, grad_pred.shape[0], points),
    )


def solution(mesh):
    return jax.shard_map(
        functools.partial(shards, walk_of(mesh)),
        mesh=mesh,
        in_specs=(
            P(("dp", "space")),
            P(("dp", "space")),
            P(("dp", "space")),
            P("dp", None, "space"),
            P("dp", None, "space"),
            P("dp", None, "space"),
            P("dp", "space", None),
            P("dp", "space"),
            P("space", None),
            P("space"),
        ),
        out_specs=(
            P(),
            P(),
            P(),
            P(("dp", "space")),
            P(("dp", "space")),
            P(("dp", "space")),
            P(("dp", "space")),
            P("dp", "space", None),
            P("dp", "space", None),
            P("dp", None, "space"),
        ),
        check_vma=False,
    )
```

```python
import functools

import jax
import jax.numpy as jnp
from jax import lax
from jax.experimental import pallas as pl
from jax.experimental.pallas import tpu as pltpu
from jax.sharding import PartitionSpec as P

D = 256
HALF = 128
CH = 78
ROUNDS = 3
K = 6
ROWW = 360
NEAR = 358
STEP = 10
H = 2048
ALL = ("dp", "space")
LIMIT = pltpu.CompilerParams(vmem_limit_bytes=60 * 2**20)


def cost(micros):
    return pl.CostEstimate(flops=0, bytes_accessed=micros * 3_000_000, transcendentals=0)


def inner(left, right, left_dim, right_dim):
    return lax.dot_general(
        left, right, (((left_dim,), (right_dim,)), ((), ())), preferred_element_type=jnp.float32
    )


def sigmoid(value):
    return 0.5 * jnp.tanh(0.5 * value) + 0.5


def silu(value):
    return value * sigmoid(value)


def slope(value):
    sigma = sigmoid(value)
    return sigma * (1.0 + value * (1.0 - sigma))


def shifted(shard, axis, by):
    peers = lax.axis_size(axis)
    pairs = [(i, i + by) for i in range(peers) if 0 <= i + by < peers]
    return lax.ppermute(shard, axis, pairs)


def walk_of(mesh):
    count = mesh.shape["space"]
    chips = [getattr(device, "coords", None) for device in mesh.devices[0].reshape(-1)]
    if any(chip is None for chip in chips) or len(set(map(tuple, chips))) != count:
        return list(range(count))
    at = {tuple(chip): n for n, chip in enumerate(chips)}
    xs, ys, zs = (sorted({chip[n] for chip in at}) for n in range(3))
    if len(xs) * len(ys) * len(zs) != count:
        return list(range(count))
    if (len(xs), len(ys), len(zs)) == (2, 2, 4):
        corners = [(0, 0), (1, 0), (0, 1), (1, 1)]
        planes = [(0, 1, 3, 2), (2, 0, 1, 3), (3, 1, 0, 2), (2, 3, 1, 0)]
        steps = [(*corners[n], z) for z, plane in enumerate(planes) for n in plane]
        return [at[(xs[x], ys[y], zs[z])] for x, y, z in steps]
    walk, plane = [], []
    for n, y in enumerate(ys):
        plane = plane + [(x, y) for x in (xs if n % 2 == 0 else xs[::-1])]
    for n, z in enumerate(zs):
        walk = walk + [at[(x, y, z)] for x, y in (plane if n % 2 == 0 else plane[::-1])]
    return walk


def halo(walk, last, initial):
    up = list(zip(walk, walk[1:] + walk[:1]))
    down = [(j, i) for i, j in up]
    return lax.ppermute(last, "space", up), lax.ppermute(initial, "space", down)


def pieces_of(total, peers):
    share = total // peers
    starts = [share * d // D for d in range(peers)]
    counts = [-(-share * (d + 1) // D) - starts[d] for d in range(peers)]
    shared = [share * d % D != 0 for d in range(peers)]
    height = -(-max(counts) // 16) * 16
    return starts, counts, shared, height


def parts_of():
    return [CH, D, D, CH] + [5 * D] * ROUNDS + [3 + 2 * ROUNDS]


def swapped(value, axis, bit):
    return lax.ppermute(value, axis, [(i, i ^ bit) for i in range(lax.axis_size(axis))])


def bits_of(axis):
    return [1 << n for n in range(lax.axis_size(axis).bit_length() - 1)]


def others(value, axis, bits):
    masks = [sum(bit for n, bit in enumerate(bits) if m >> n & 1) for m in range(1, 1 << len(bits))]
    return [swapped(value, axis, mask) for mask in masks]


def upper_groups():
    bits = bits_of("space")[2:]
    return [tuple(bits[n : n + 2]) for n in range(0, len(bits), 2)]


def orders():
    return [(1, 2), (2, 1)]


def summed_everywhere(value, arriving):
    for bits in reversed(upper_groups()):
        value = sum(others(value, "space", bits), value)
    value = value + swapped(value, "dp", 1)
    value, arriving = lax.optimization_barrier((value, arriving))
    return sum(others(value, "space", (1, 2)), value), arriving


def gathered_blocks(piece, posted):
    held, weights, size = piece[None], {}, 1
    for bits in reversed(upper_groups()):
        held = jnp.concatenate([held] + others(held, "space", bits), 0)
        for n, bit in enumerate(bits):
            weights[bit] = size << n
        size = size << len(bits)
    half = piece.shape[0] // 2
    held = [held[:, :half], held[:, half:]]
    ranks = [dict(weights), dict(weights)]
    for turn in (1, 0):
        if turn == 0:
            held[0], held[1], posted = lax.optimization_barrier((*held, posted))
        for n, order in enumerate(orders()):
            held[n] = jnp.concatenate([held[n], swapped(held[n], "space", order[turn])], 0)
            ranks[n][order[turn]] = size
        size = size << 1
    return (held, [swapped(part, "dp", 1) for part in held], ranks), posted


def spread_rows(gathered, total, peers, place):
    (first, second), (first_far, second_far), ranks = gathered
    starts, counts, shared, height = pieces_of(total, peers)
    half, group = height // 2, first.shape[0]
    rows = -(-total // D)
    sizes = parts_of()
    def at(rank, relative):
        spot = 0
        for bit, weight in rank.items():
            spot = spot + jnp.where((relative & bit) != 0, weight, 0)
        return spot

    def body(place_ref, *refs):
        sources, outs, buffer = refs[:4], refs[4:-1], refs[-1]
        me = place_ref[0]
        mine = me // group
        for d in range(peers):
            relative = (me ^ d) & (group - 1)
            spots = [at(rank, relative) for rank in ranks]

            def lay(one, two, d=d, spots=spots):
                piece = jnp.concatenate([one[spots[0]], two[spots[1]]], 0).astype(jnp.float32)
                start, count = starts[d], counts[d]
                if shared[d]:
                    buffer[start : start + 1, :] = buffer[start : start + 1, :] + piece[:1]
                    buffer[start + 1 : start + count, :] = piece[1:count]
                else:
                    buffer[start : start + count, :] = piece[:count]

            @pl.when(mine == d // group)
            def _():
                lay(sources[0], sources[1])

            @pl.when(mine != d // group)
            def _():
                lay(sources[2], sources[3])

        start = 0
        for out, size in zip(outs, sizes):
            out[:size, :] = buffer[start : start + size, :].astype(out.dtype)
            if out.shape[0] > size:
                out[size:, :] = jnp.zeros((out.shape[0] - size, D), out.dtype)
            start = start + size

    kinds = [jnp.bfloat16] * (4 + ROUNDS) + [jnp.float32]
    talls = [HALF] + sizes[1:]
    return pl.pallas_call(
        body,
        grid_spec=pltpu.PrefetchScalarGridSpec(
            num_scalar_prefetch=1,
            grid=(1,),
            in_specs=[whole(first.shape)] * 4,
            out_specs=[whole((tall, D)) for tall in talls],
            scratch_shapes=[pltpu.VMEM((-(-rows // 8) * 8 + 8, D), jnp.float32)],
        ),
        out_shape=[jax.ShapeDtypeStruct((tall, D), kind) for tall, kind in zip(talls, kinds)],
        compiler_params=LIMIT,
        cost_estimate=cost(4),
        name="spread_rows",
    )(place.reshape(1), first, second, first_far, second_far)


def collect_rows(parts, total, peers, place):
    starts, counts, shared, height = pieces_of(total, peers)
    rows = -(-total // D)
    sizes = [min(part.shape[0], size) for part, size in zip(parts, tall_parts())]
    group = lax.axis_size("space")

    def body(place_ref, *refs):
        sources, keep, send, buffer = refs[:-3], refs[-3], refs[-2], refs[-1]
        start = 0
        for source, size in zip(sources, sizes):
            buffer[start : start + size, :] = source[:size, :]
            start = start + size
        if buffer.shape[0] > start:
            buffer[start:, :] = jnp.zeros((buffer.shape[0] - start, D), jnp.float32)
        me = place_ref[0]
        mine = me // group
        for d in range(peers):
            relative = (me ^ d) & (group - 1)

            @pl.when(mine == d // group)
            def _():
                keep[relative] = buffer[starts[d] : starts[d] + height, :]

            @pl.when(mine != d // group)
            def _():
                send[relative] = buffer[starts[d] : starts[d] + height, :].astype(jnp.bfloat16)

    shape = (group, height, D)
    return pl.pallas_call(
        body,
        grid_spec=pltpu.PrefetchScalarGridSpec(
            num_scalar_prefetch=1,
            grid=(1,),
            in_specs=[whole(part.shape) for part in parts],
            out_specs=[whole(shape), whole(shape)],
            scratch_shapes=[pltpu.VMEM((-(-rows // 8) * 8 + height + 8, D), jnp.float32)],
        ),
        out_shape=[
            jax.ShapeDtypeStruct(shape, jnp.float32),
            jax.ShapeDtypeStruct(shape, jnp.bfloat16),
        ],
        compiler_params=LIMIT,
        cost_estimate=cost(5),
        name="collect_rows",
    )(place.reshape(1), *parts)


def reduced_piece(keep, send, leaving):
    kept = keep + swapped(send, "dp", 1).astype(jnp.float32)
    half = kept.shape[1] // 2
    groups = upper_groups()
    inner_shape = (kept.shape[0] // 4, 2, 2, half, D)
    parts = [kept[:, :half].reshape(inner_shape), kept[:, half:].reshape(inner_shape)]
    for n, order in enumerate(orders()):
        for bit in order:
            spot = 2 if bit == 1 and parts[n].ndim == 5 else 1
            stay = lax.index_in_dim(parts[n], 0, spot, keepdims=False)
            leave = lax.index_in_dim(parts[n], 1, spot, keepdims=False)
            parts[n] = stay + swapped(leave.astype(jnp.bfloat16), "space", bit).astype(jnp.float32)
    part = jnp.concatenate(parts, 1)
    part, leaving = lax.optimization_barrier((part, leaving))
    for bits in groups:
        part = part.reshape((-1, 1 << len(bits)) + part.shape[1:])
        masks = [sum(bit for n, bit in enumerate(bits) if m >> n & 1) for m in range(1 << len(bits))]
        low = part.astype(jnp.bfloat16)
        part = sum(
            [
                swapped(low[:, m], "space", mask).astype(jnp.float32)
                for m, mask in enumerate(masks)
                if m
            ],
            part[:, 0],
        )
    return part[0], leaving


def tall_parts():
    return [CH, D, D, CH] + [D, 4 * D] * ROUNDS + [2, 1] + [2] * ROUNDS


def weave(ref, value):
    rows = value.shape[0]
    ref[pl.ds(0, rows, stride=2), :] = value[:, :HALF]
    ref[pl.ds(1, rows, stride=2), :] = value[:, HALF:]


def unweave(ref):
    rows = ref.shape[0] // 2
    return ref[pl.ds(0, rows, stride=2), :], ref[pl.ds(1, rows, stride=2), :]


def selector():
    row = lax.broadcasted_iota(jnp.int32, (8, HALF), 0)
    lane = lax.broadcasted_iota(jnp.int32, (8, HALF), 1)
    slot = jnp.where(lane == CH, 64.0, jnp.where(lane == CH + 1, 1.0, 0.0))
    known = jnp.where(lane == CH + 2, 1.0, 0.0)
    return jnp.where(row == 0, slot, jnp.where(row == 1, known, 0.0)).astype(jnp.bfloat16)


def ids_along(arrived):
    codes = inner(selector(), arrived, 1, 1)
    return jnp.where(codes[1:2, :] > 0, codes[0:1, :], -1.0).astype(jnp.int32)


def ids_down(arrived):
    codes = inner(arrived, selector(), 1, 1)
    return jnp.where(codes[:, 1:2] > 0, codes[:, 0:1], -1.0).astype(jnp.int32)


def whole(shape):
    return pl.BlockSpec(shape, lambda *_: (0,) * len(shape))


def node_terms(mesh, mats, bias):
    blocks = mesh.shape[0]
    tile = 1024

    def body(mesh_ref, mats_ref, bias_ref, dest_ref, self_ref):
        lowered = mesh_ref[...].astype(jnp.bfloat16)
        weave(dest_ref, inner(lowered, mats_ref[1], 1, 0) + bias_ref[0:1, :])
        self_ref[...] = inner(lowered, mats_ref[3], 1, 0) + bias_ref[1:2, :]

    rows = pl.BlockSpec((tile, D), lambda i: (i, 0))
    woven = pl.BlockSpec((2 * tile, HALF), lambda i: (i, 0))
    return pl.pallas_call(
        body,
        grid=(blocks // tile,),
        in_specs=[rows, whole(mats.shape), whole(bias.shape)],
        out_specs=[woven, rows],
        out_shape=[
            jax.ShapeDtypeStruct((2 * blocks, HALF), jnp.float32),
            jax.ShapeDtypeStruct((blocks, D), jnp.float32),
        ],
        compiler_params=pltpu.CompilerParams(vmem_limit_bytes=63 * 2**20),
        cost_estimate=cost(4),
        name="node_terms",
    )(mesh, mats, bias)


def round_forward(index, mesh, pieces, mats, terms, following, decoder=(), half=None, into=()):
    blocks = mesh.shape[0]
    tile, chunk = 512, 16
    turns, high = tile // chunk, 2 * chunk
    more = following is not None
    reach = 2 * (blocks + 2 * H)
    steps = blocks // tile if half is None else blocks // tile // 2
    shift = 0 if half is None else half * steps

    def body(index_ref, mesh_ref, *refs):
        sources, refs = refs[: len(pieces)], refs[len(pieces) :]
        (mats_ref, dest_ref, self_ref), refs = refs[:3], refs[3:]
        table, rows, wide = refs[-3:]
        if more:
            next_ref, refs = refs[0], refs[1 + len(into) :]
            new_ref, back_ref, update_ref, agg_ref, slope_ref, sent_ref = refs[:6]
        else:
            ids_ref, dec_ref, out_ref, head_ref = refs[:4]
            new_ref, back_ref, update_ref, agg_ref, slope_ref = refs[4:9]
            branch_ref, fetched_ref, decoded_ref, turn_ref, total_ref = refs[9:14]
        step = pl.program_id(0)

        @pl.when(step == 0)
        def _():
            for source, (_, start) in zip(sources, pieces):

                @pl.loop(0, source.shape[0] // 256)
                def _(i, source=source, start=start):
                    at = pl.multiple_of(i * 256, 256)
                    to = pl.multiple_of(start + at, 256)
                    table[pl.ds(to, 256), :] = source[pl.ds(at, 256), :].astype(jnp.float32)

        mesh_in = mesh_ref[...]

        part = blocks // 2
        if half is None:
            origin = step // (steps // 2) * (K * part) + lax.rem(step, steps // 2) * tile
        else:
            origin = step * tile

        def fetch(turn):
            for edge in range(K):
                base = edge * part + turn * chunk + origin
                spots = [index_ref[base + u] for u in range(chunk)]
                values = [table[pl.ds(pl.multiple_of(spot, 2), 2), :] for spot in spots]
                for u in range(chunk):
                    spot = pl.multiple_of(edge * 2 * tile + turn * high + 2 * u, 2)
                    rows[pl.ds(spot, 2), :] = values[u]

        def load(turn):
            at = pl.multiple_of(turn * high, high)
            taken = [
                rows[pl.ds(pl.multiple_of(edge * 2 * tile + turn * high, high), high), :]
                for edge in range(K)
            ]
            return at, dest_ref[pl.ds(at, high), :], taken

        def dense(at, dest, taken):
            total = None
            for edge in range(K):
                value = taken[edge] + dest
                sigma = sigmoid(value)
                out = value * sigma
                slope_ref[edge, pl.ds(at, high), :] = (sigma + out * (1.0 - sigma)).astype(
                    jnp.bfloat16
                )
                total = out if total is None else total + out
            wide[pl.ds(at, high), :] = total * (1.0 / K)

        def some(turn, carry):
            loaded = load(turn - 1)
            fetch(turn)
            dense(*loaded)
            return carry

        fetch(0)
        lax.fori_loop(1, turns, some, 0)
        dense(*load(turns - 1))
        first, second = unweave(wide)
        first, second = first.astype(jnp.bfloat16), second.astype(jnp.bfloat16)
        agg_ref[:, :HALF] = first
        agg_ref[:, HALF:] = second
        update_in = (
            inner(first, mats_ref[2, :HALF, :], 1, 0)
            + inner(second, mats_ref[2, HALF:, :], 1, 0)
            + self_ref[...]
        )
        sigma = sigmoid(update_in)
        out = update_in * sigma
        back_ref[...] = sigma + out * (1.0 - sigma)
        update = out.astype(jnp.bfloat16)
        update_ref[...] = update
        new = mesh_in + inner(update, mats_ref[4], 1, 0)
        new_ref[...] = new
        lowered = new.astype(jnp.bfloat16)
        if more:
            weave(wide, inner(lowered, next_ref[0], 1, 0))
            sent_ref[...] = wide[...].astype(jnp.bfloat16)
            return
        nodes = lax.broadcasted_iota(jnp.int32, (ids_ref.shape[0], tile), 1) + step * tile
        chooser = jnp.where(nodes == ids_ref[...], 1.0, 0.0).astype(jnp.bfloat16)
        found = inner(chooser, lowered, 1, 0)

        @pl.when(step == 0)
        def _():
            total_ref[...] = found

        @pl.when(step > 0)
        def _():
            total_ref[...] += found

        @pl.when(step == blocks // tile - 1)
        def _():
            fetched = total_ref[...].astype(jnp.bfloat16)
            fetched_ref[...] = fetched
            value = inner(fetched, dec_ref[...], 1, 0) + head_ref[2:3, :]
            sigma = sigmoid(value)
            out = value * sigma
            turn_ref[...] = sigma + out * (1.0 - sigma)
            decoded = out.astype(jnp.bfloat16)
            decoded_ref[...] = decoded
            branch_ref[...] = inner(decoded, out_ref[...], 1, 0).astype(jnp.bfloat16)

    whole_rows = pl.BlockSpec((tile, D), lambda i, *_: (i + shift, 0))
    woven = pl.BlockSpec((2 * tile, HALF), lambda i, *_: (i + shift, 0))
    ins = [whole_rows] + [pl.BlockSpec(memory_space=pltpu.VMEM)] * len(pieces)
    ins = ins + [whole(mats.shape), woven, whole_rows]
    outs = [whole_rows] * 4 + [pl.BlockSpec((K, 2 * tile, HALF), lambda i, *_: (0, i + shift, 0))]
    shapes = [
        jax.ShapeDtypeStruct((blocks, D), jnp.float32),
        jax.ShapeDtypeStruct((blocks, D), jnp.float32),
        jax.ShapeDtypeStruct((blocks, D), jnp.bfloat16),
        jax.ShapeDtypeStruct((blocks, D), jnp.bfloat16),
        jax.ShapeDtypeStruct((K, 2 * blocks, HALF), jnp.bfloat16),
    ]
    args = [index, mesh] + [rows for rows, _ in pieces] + [mats, *terms]
    if more:
        ins.append(pl.BlockSpec((1, D, D), lambda *_: (0, 0, 0)))
        outs.append(pl.BlockSpec((2 * tile, HALF), lambda i, *_: (i, 0)))
        shapes.append(jax.ShapeDtypeStruct((2 * tile * steps, HALF), jnp.bfloat16))
        args.append(following)
    aliases = {len(args) + n: n for n in range(len(into))}
    ins = ins + [pl.BlockSpec(memory_space=pl.ANY)] * len(into)
    args = args + list(into)
    scratch = []
    if decoder:
        posts = decoder[0].shape[0]
        ins = ins + [whole(arg.shape) for arg in decoder]
        args = args + list(decoder)
        for width, kind in ((HALF, jnp.bfloat16), (D, jnp.bfloat16), (D, jnp.bfloat16), (D, jnp.float32)):
            outs.append(whole((posts, width)))
            shapes.append(jax.ShapeDtypeStruct((posts, width), kind))
        scratch = [pltpu.VMEM((posts, D), jnp.float32)]
    return pl.pallas_call(
        body,
        grid_spec=pltpu.PrefetchScalarGridSpec(
            num_scalar_prefetch=1,
            grid=(steps,),
            in_specs=ins,
            out_specs=outs,
            scratch_shapes=scratch
            + [
                pltpu.VMEM((reach, HALF), jnp.float32),
                pltpu.VMEM((K * 2 * tile, HALF), jnp.float32),
                pltpu.VMEM((2 * tile, HALF), jnp.float32),
            ],
        ),
        out_shape=shapes,
        input_output_aliases=aliases,
        compiler_params=pltpu.CompilerParams(vmem_limit_bytes=63 * 2**20),
        cost_estimate=cost(24 if half is None else 14),
        name="round_forward",
    )(*args)


def edges_backward(index, back, slopes, mats, carried=(), landed=()):
    blocks = back.shape[0]
    tile, chunk = 512, 16
    steps, turns, high = blocks // tile, tile // chunk, 2 * chunk
    reach = 2 * (blocks + 2 * H)

    def body(*refs):
        if carried:
            index_ref, back_ref, slope_ref, mats_ref = refs[:4]
            past, rest = refs[4:9], refs[9:]
            (new_ref, out_ref, sent_ref), rest = rest[:3], rest[3:]
        else:
            index_ref, back_ref, slope_ref, mats_ref = refs[:4]
            (ids_ref, landed_ref, turn_ref, w_out_ref, w_dec_ref), rest = refs[4:9], refs[9:]
            (new_ref, out_ref, gdec_ref), rest = rest[:3], rest[3:]
            gathered, rest = rest[5], rest[:5] + rest[6:]
        guin_ref, low_ref, before_ref, own_ref, after_ref, wide, wider, flows, *tables = rest
        step = pl.program_id(0)

        @pl.when(step == 0)
        def _():
            @pl.loop(0, reach // 256)
            def _(i):
                for table in tables:
                    table[pl.ds(pl.multiple_of(i * 256, 256), 256), :] = jnp.zeros(
                        (256, HALF), jnp.float32
                    )

        if carried:
            new, one, two = ended(*past, wide)
            sent_ref[:, :HALF] = one
            sent_ref[:, HALF:] = two
            new_ref[...] = new
            grad_out = new.astype(jnp.bfloat16)
            out_ref[...] = grad_out
        else:

            @pl.when(step == 0)
            def _():
                grad_dec = inner(landed_ref[...], w_out_ref[...], 1, 1) * turn_ref[...]
                grad_dec = grad_dec.astype(jnp.bfloat16)
                gdec_ref[...] = grad_dec
                gathered[...] = inner(grad_dec, w_dec_ref[...], 1, 1).astype(jnp.bfloat16)

            nodes = lax.broadcasted_iota(jnp.int32, (tile, landed_ref.shape[0]), 0) + step * tile
            chooser = jnp.where(nodes == ids_ref[...], 1.0, 0.0).astype(jnp.bfloat16)
            new = inner(chooser, gathered[...], 1, 0)
            new_ref[...] = new
            grad_out = new.astype(jnp.bfloat16)
            out_ref[...] = grad_out
        grad_uin = (inner(grad_out, mats_ref[4], 1, 1) * back_ref[...]).astype(jnp.bfloat16)
        guin_ref[...] = grad_uin
        weave(wide, inner(grad_uin, mats_ref[2], 1, 1) * (1.0 / K))

        def dense(turn):
            at = pl.multiple_of(turn * high, high)
            grad_agg = wide[pl.ds(at, high), :]
            total, parts = None, []
            for edge in range(K):
                flow = grad_agg * slope_ref[edge, pl.ds(at, high), :].astype(jnp.float32)
                parts.append(flow)
                total = flow if total is None else total + flow
            return at, total, parts

        def keep(turn, at, total, parts):
            for edge in range(K):
                spot = pl.multiple_of(edge * 2 * tile + turn * high, high)
                flows[pl.ds(spot, high), :] = parts[edge]
            wider[pl.ds(at, high), :] = total

        part = blocks // 2
        origin = step // (steps // 2) * (K * part) + lax.rem(step, steps // 2) * tile

        def scatter(turn):
            for u in range(chunk):
                spots, sums = [], []
                for edge in range(K):
                    base = edge * part + turn * chunk + origin
                    spots.append(pl.multiple_of(index_ref[base + u], 2))
                for edge in range(K):
                    spot = pl.multiple_of(edge * 2 * tile + turn * high + 2 * u, 2)
                    sums.append(tables[edge][pl.ds(spots[edge], 2), :] + flows[pl.ds(spot, 2), :])
                for edge in range(K):
                    tables[edge][pl.ds(spots[edge], 2), :] = sums[edge]

        def some(turn, carry):
            found = dense(turn)
            scatter(turn - 1)
            keep(turn, *found)
            return carry

        keep(0, *dense(0))
        lax.fori_loop(1, turns, some, 0)
        scatter(turns - 1)
        first, second = unweave(wider)
        low_ref[:, :HALF] = first.astype(jnp.bfloat16)
        low_ref[:, HALF:] = second.astype(jnp.bfloat16)

        @pl.when(step == steps - 1)
        def _():
            def summed(at):
                value = tables[0][pl.ds(at, 256), :]
                for table in tables[1:]:
                    value = value + table[pl.ds(at, 256), :]
                return value

            @pl.loop(0, 2 * H // 256)
            def _(i):
                at = pl.multiple_of(i * 256, 256)
                far = pl.multiple_of(2 * H + 2 * blocks + at, 256)
                before_ref[pl.ds(at, 256), :] = summed(at).astype(jnp.bfloat16)
                after_ref[pl.ds(at, 256), :] = summed(far).astype(jnp.bfloat16)

            @pl.loop(0, 2 * blocks // 256)
            def _(i):
                at = pl.multiple_of(i * 256, 256)
                own_ref[pl.ds(at, 256), :] = summed(pl.multiple_of(2 * H + at, 256))

    rows = pl.BlockSpec((tile, D), lambda i, *_: (i, 0))
    woven = pl.BlockSpec((2 * tile, HALF), lambda i, *_: (i, 0))
    low = jax.ShapeDtypeStruct((blocks, D), jnp.bfloat16)
    low_posts = (landed[1].shape[0], D) if landed else None
    last = low if carried else jax.ShapeDtypeStruct(low_posts, jnp.bfloat16)
    return pl.pallas_call(
        body,
        grid_spec=pltpu.PrefetchScalarGridSpec(
            num_scalar_prefetch=1,
            grid=(steps,),
            in_specs=[
                rows,
                pl.BlockSpec((K, 2 * tile, HALF), lambda i, *_: (0, i, 0)),
                whole(mats.shape),
            ]
            + ([rows] + [woven] * 3 + [whole(mats.shape)] if carried else [])
            + [whole(arg.shape) for arg in landed],
            out_specs=([rows] * 3 if carried else [rows, rows, whole(low_posts)])
            + [
                rows, rows,
                whole((2 * H, HALF)), whole((2 * blocks, HALF)), whole((2 * H, HALF)),
            ],
            scratch_shapes=([] if carried else [pltpu.VMEM(low_posts, jnp.bfloat16)])
            + [
                pltpu.VMEM((2 * tile, HALF), jnp.float32),
                pltpu.VMEM((2 * tile, HALF), jnp.float32),
                pltpu.VMEM((2 * tile * K, HALF), jnp.float32),
            ]
            + [pltpu.VMEM((reach, HALF), jnp.float32)] * K,
        ),
        out_shape=[
            jax.ShapeDtypeStruct((blocks, D), jnp.float32),
            low,
            last,
            low,
            low,
            jax.ShapeDtypeStruct((2 * H, HALF), jnp.bfloat16),
            jax.ShapeDtypeStruct((2 * blocks, HALF), jnp.float32),
            jax.ShapeDtypeStruct((2 * H, HALF), jnp.bfloat16),
        ],
        compiler_params=pltpu.CompilerParams(vmem_limit_bytes=63 * 2**20),
        cost_estimate=cost(28 if carried else 25),
        name="edges_backward",
    )(index, back, slopes, mats, *carried, *landed)


def ended(part_ref, own_ref, first_ref, last_ref, mats_ref, wide):
    wide[...] = (
        own_ref[...] + first_ref[...].astype(jnp.float32) + last_ref[...].astype(jnp.float32)
    )
    one, two = unweave(wide)
    one, two = one.astype(jnp.bfloat16), two.astype(jnp.bfloat16)
    new = (
        part_ref[...]
        + inner(one, mats_ref[0, :, :HALF], 1, 1)
        + inner(two, mats_ref[0, :, HALF:], 1, 1)
    )
    return new, one, two


def weight_grads(mesh, dest_low, agg, grad_uin, update, leaving, grad_mesh, mats, past=()):
    blocks = mesh.shape[0]
    tile = 512

    def body(mesh_ref, dest_ref, agg_ref, guin_ref, update_ref, out_ref, grad_ref, mats_ref, *refs):
        if past:
            (old_ref, sent_ref), refs = refs[:2], refs[2:]
        part_ref, grads_ref, bias_ref = refs[:3]

        @pl.when(pl.program_id(0) == 0)
        def _():
            for ref in refs[1:]:
                ref[...] = jnp.zeros(ref.shape, jnp.float32)

        lowered = mesh_ref[...].astype(jnp.bfloat16)
        dest, guin = dest_ref[...], guin_ref[...]
        grads_ref[:D, :] += inner(lowered, dest, 0, 0)
        grads_ref[D : 2 * D, :] += inner(agg_ref[...], guin, 0, 0)
        grads_ref[2 * D : 3 * D, :] += inner(lowered, guin, 0, 0)
        grads_ref[3 * D :, :] += inner(update_ref[...], out_ref[...], 0, 0)
        bias_ref[0:1, :] += jnp.sum(dest.astype(jnp.float32), 0, keepdims=True)
        bias_ref[1:2, :] += jnp.sum(guin.astype(jnp.float32), 0, keepdims=True)
        part_ref[...] = (
            grad_ref[...] + inner(guin, mats_ref[3], 1, 1) + inner(dest, mats_ref[1], 1, 1)
        )
        if past:
            refs[3][...] += inner(old_ref[...].astype(jnp.bfloat16), sent_ref[...], 0, 0)

    rows = pl.BlockSpec((tile, D), lambda i: (i, 0))
    shapes = [(4 * D, D), (2, D)] + ([(D, D)] if past else [])
    return pl.pallas_call(
        body,
        grid=(blocks // tile,),
        in_specs=[rows] * 7 + [whole(mats.shape)] + [rows] * len(past),
        out_specs=[rows] + [whole(shape) for shape in shapes],
        out_shape=[jax.ShapeDtypeStruct((blocks, D), jnp.float32)]
        + [jax.ShapeDtypeStruct(shape, jnp.float32) for shape in shapes],
        compiler_params=pltpu.CompilerParams(vmem_limit_bytes=63 * 2**20),
        cost_estimate=cost(10),
        name="weight_grads",
    )(mesh, dest_low, agg, grad_uin, update, leaving, grad_mesh, mats, *past)


def decode_grads(decoded, landed, fetched, grad_dec):
    def body(decoded_ref, landed_ref, fetched_ref, grad_ref, gout_ref, gdec_ref, bias_ref):
        gout_ref[...] = inner(decoded_ref[...], landed_ref[...], 0, 0)
        gdec_ref[...] = inner(fetched_ref[...], grad_ref[...], 0, 0)
        bias_ref[...] = jnp.sum(grad_ref[...].astype(jnp.float32), 0, keepdims=True)

    return pl.pallas_call(
        body,
        out_shape=[jax.ShapeDtypeStruct(shape, jnp.float32) for shape in ((D, HALF), (D, D), (1, D))],
        compiler_params=pltpu.CompilerParams(vmem_limit_bytes=63 * 2**20),
        cost_estimate=cost(3),
        name="decode_grads",
    )(decoded, landed, fetched, grad_dec)


def encode_rows(arrived, w_in, w_node, biases, source):
    posts = arrived.shape[0]
    tile = 1024

    def body(
        arrived_ref, in_ref, node_ref, bias_ref, source_ref,
        mesh_ref, gathered_ref, sent_ref, ids_ref, down_ref, encoded, wide,
    ):
        step = pl.program_id(0)

        @pl.when(step == 0)
        def _():
            entering = inner(arrived_ref[...], in_ref[...], 1, 0) + bias_ref[0:1, :]
            encoded[...] = silu(entering).astype(jnp.bfloat16)
            ids_ref[...] = ids_along(arrived_ref[...])
            down_ref[...] = ids_down(arrived_ref[...])

        nodes = lax.broadcasted_iota(jnp.int32, (tile, posts), 0) + step * tile
        chooser = jnp.where(nodes == ids_ref[...], 1.0, 0.0).astype(jnp.bfloat16)
        gathered = inner(chooser, encoded[...], 1, 0).astype(jnp.bfloat16)
        gathered_ref[...] = gathered
        mesh = silu(inner(gathered, node_ref[...], 1, 0) + bias_ref[1:2, :])
        mesh_ref[...] = mesh
        weave(wide, inner(mesh.astype(jnp.bfloat16), source_ref[0], 1, 0))
        sent_ref[...] = wide[...].astype(jnp.bfloat16)

    rows = pl.BlockSpec((tile, D), lambda i: (i, 0))
    args = (arrived, w_in, w_node, biases, source)
    return pl.pallas_call(
        body,
        grid=(H // tile,),
        in_specs=[whole(arg.shape) for arg in args[:-1]]
        + [pl.BlockSpec((1, D, D), lambda *_: (0, 0, 0))],
        out_specs=[rows, rows, pl.BlockSpec((2 * tile, HALF), lambda i: (i, 0))]
        + [whole((1, posts)), whole((posts, 1))],
        out_shape=[
            jax.ShapeDtypeStruct((H, D), jnp.float32),
            jax.ShapeDtypeStruct((H, D), jnp.bfloat16),
            jax.ShapeDtypeStruct((2 * H, HALF), jnp.bfloat16),
            jax.ShapeDtypeStruct((1, posts), jnp.int32),
            jax.ShapeDtypeStruct((posts, 1), jnp.int32),
        ],
        scratch_shapes=[pltpu.VMEM((posts, D), jnp.bfloat16), pltpu.VMEM((2 * tile, HALF), jnp.float32)],
        compiler_params=LIMIT,
        cost_estimate=cost(5),
        name="encode_rows",
    )(*args)


def encode_backward(carried, mesh, gathered, arrived, ids, w_in, w_node, biases):
    blocks = mesh.shape[0]
    posts = arrived.shape[0]
    tile = 512
    steps = blocks // tile

    def body(
        part_ref, own_ref, first_ref, last_ref, mats_ref,
        mesh_ref, gathered_ref, arrived_ref, ids_ref, in_ref, node_ref, bias_ref,
        new_ref, out_ref, gin_ref, gnode_ref, gbias_ref, gsource_ref, total, wide,
    ):
        step = pl.program_id(0)

        @pl.when(step == 0)
        def _():
            for ref in (total, gnode_ref, gbias_ref, gsource_ref):
                ref[...] = jnp.zeros(ref.shape, jnp.float32)

        new, one, two = ended(part_ref, own_ref, first_ref, last_ref, mats_ref, wide)
        new_ref[...] = new
        out_ref[...] = new.astype(jnp.bfloat16)
        lowered = mesh_ref[...].astype(jnp.bfloat16)
        gsource_ref[:, :HALF] += inner(lowered, one, 0, 0)
        gsource_ref[:, HALF:] += inner(lowered, two, 0, 0)
        node_in = inner(gathered_ref[...], node_ref[...], 1, 0) + bias_ref[1:2, :]
        grad_node = (new * slope(node_in)).astype(jnp.bfloat16)
        gbias_ref[1:2, :] += jnp.sum(grad_node.astype(jnp.float32), 0, keepdims=True)
        gnode_ref[...] += inner(gathered_ref[...], grad_node, 0, 0)
        back = inner(grad_node, node_ref[...], 1, 1).astype(jnp.bfloat16)
        nodes = lax.broadcasted_iota(jnp.int32, (posts, tile), 1) + step * tile
        chooser = jnp.where(nodes == ids_ref[...], 1.0, 0.0).astype(jnp.bfloat16)
        total[...] += inner(chooser, back, 1, 0)

        @pl.when(step == steps - 1)
        def _():
            entering = inner(arrived_ref[...], in_ref[...], 1, 0) + bias_ref[0:1, :]
            grad_enc = (total[...] * slope(entering)).astype(jnp.bfloat16)
            gbias_ref[0:1, :] = jnp.sum(grad_enc.astype(jnp.float32), 0, keepdims=True)
            gin_ref[...] = inner(arrived_ref[...], grad_enc, 0, 0)

    rows = pl.BlockSpec((tile, D), lambda i: (i, 0))
    woven = pl.BlockSpec((2 * tile, HALF), lambda i: (i, 0))
    args = (arrived, ids, w_in, w_node, biases)
    shapes = [(HALF, D), (D, D), (2, D), (D, D)]
    return pl.pallas_call(
        body,
        grid=(steps,),
        in_specs=[rows] + [woven] * 3 + [whole(carried[4].shape), rows, rows]
        + [whole(arg.shape) for arg in args],
        out_specs=[rows, rows] + [whole(shape) for shape in shapes],
        out_shape=[
            jax.ShapeDtypeStruct((blocks, D), jnp.float32),
            jax.ShapeDtypeStruct((blocks, D), jnp.bfloat16),
        ]
        + [jax.ShapeDtypeStruct(shape, jnp.float32) for shape in shapes],
        scratch_shapes=[pltpu.VMEM((posts, D), jnp.float32), pltpu.VMEM((2 * tile, HALF), jnp.float32)],
        compiler_params=LIMIT,
        cost_estimate=cost(10),
        name="encode_backward",
    )(*carried, mesh, gathered, *args)


def settled_rows(stays, own, came):
    tile = 512

    def body(stays_ref, own_ref, came_ref, out_ref):
        @pl.when(stays_ref[0] == 1)
        def _():
            out_ref[...] = own_ref[...]

        @pl.when(stays_ref[0] == 0)
        def _():
            out_ref[...] = came_ref[...].astype(jnp.float32)

    return pl.pallas_call(
        body,
        grid_spec=pltpu.PrefetchScalarGridSpec(
            num_scalar_prefetch=1,
            grid=(own.shape[0] // tile,),
            in_specs=[
                pl.BlockSpec((tile, D), lambda i, stay: (i * stay[0], 0)),
                pl.BlockSpec((tile, D), lambda i, stay: (i * (1 - stay[0]), 0)),
            ],
            out_specs=pl.BlockSpec((tile, D), lambda i, stay: (i, 0)),
        ),
        out_shape=jax.ShapeDtypeStruct(own.shape, jnp.float32),
        compiler_params=LIMIT,
        cost_estimate=cost(2),
        name="settled_rows",
    )(stays.astype(jnp.int32).reshape(1), own, came)


def shards(walk, master, moment1, moment2, inputs, targets, valid, owner, slot, neighbours, partner):
    bands = lax.axis_size("space")
    band = lax.axis_index("space")
    peers = lax.axis_size(ALL)
    place = lax.axis_index(ALL)
    shard = master.shape[0]
    total_size = shard * peers
    height = pieces_of(total_size, peers)[3]
    offset = lax.rem(lax.rem(shard, D) * place, D)
    piece = lax.dynamic_update_slice_in_dim(
        jnp.zeros((height * D,), jnp.bfloat16), master.astype(jnp.bfloat16), offset, 0
    )
    state_in = inputs[0]
    counted = valid[0].astype(jnp.float32)
    local_count = jnp.sum(valid[0])
    digits = (local_count >> jnp.array([16, 8, 0], jnp.int32)) & 255
    digits = jnp.pad(digits, (CH + 3, HALF - CH - 6)).astype(jnp.float32)[None, :]
    points = state_in.shape[1]
    blocks = neighbours.shape[0]
    assert blocks == H
    capacity = max(2, 2 * points // bands)
    target_band = owner[0, :, 0]
    hits = (target_band[:, None] == jnp.arange(bands, dtype=jnp.int32)[None, :]).astype(jnp.int32)
    ranks = jnp.sum(jnp.cumsum(hits, 0) * hits, 1) - 1
    places_out = jnp.sum(hits * jnp.asarray(walk, jnp.int32)[None, :], 1) * capacity + ranks
    poster = (
        jnp.arange(bands * capacity, dtype=jnp.int32)[:, None] == places_out[None, :]
    ).astype(jnp.bfloat16)
    spots = slot[0][None, :]
    columns = jnp.concatenate(
        [
            state_in,
            (spots // 64).astype(jnp.bfloat16),
            (spots % 64).astype(jnp.bfloat16),
            jnp.ones((1, points), jnp.bfloat16),
            jnp.zeros((HALF - CH - 3, points), jnp.bfloat16),
        ],
        0,
    )

    def exchanged(rows):
        return lax.all_to_all(
            rows.reshape(bands, capacity, HALF), "space", split_axis=0, concat_axis=0, tiled=True
        ).reshape(bands * capacity, HALF)

    held, posted = gathered_blocks(
        piece.reshape(height, D), (inner(poster, columns, 1, 1) + digits).astype(jnp.bfloat16)
    )
    arrived = exchanged(posted)
    w_in, w_node, w_dec, w_out, *w_round, biases = spread_rows(
        held, total_size, peers, place
    )
    arrived, biases = lax.optimization_barrier((arrived, biases))
    counts = arrived.reshape(bands, capacity, HALF)[:, 0, CH + 3 : CH + 6].astype(jnp.float32)
    counts = jnp.sum(counts, 0, keepdims=True)
    w_out = jnp.pad(w_out.reshape(D, CH), ((0, 0), (0, HALF - CH)))
    w_round = [mats.reshape(5, D, D) for mats in w_round]
    b_head = biases[:3]
    b_round = biases[3:].reshape(ROUNDS, 2, D)
    mesh, gathered, sent, ids_row, ids = encode_rows(
        arrived, w_in, w_node, biases, w_round[0]
    )
    sent, partner, neighbours, counted, counts = lax.optimization_barrier(
        (sent, partner, neighbours, counted, counts)
    )
    counts = counts + swapped(counts, "dp", 1)
    index = 2 * ((neighbours - band * blocks + H) % (blocks * bands)).T
    index = index.reshape(K, 2, blocks // 2).swapaxes(0, 1).reshape(-1)
    moved = [(n, place) for n, place in enumerate(walk) if n != place]
    stays = jnp.asarray([n == place for n, place in enumerate(walk)])[band]
    index = lax.ppermute(index, "space", list(enumerate(walk)))

    def at_home(rows):
        return lax.ppermute(rows, "space", [(j, i) for i, j in moved])

    def settled(own, came):
        return jnp.where(stays, own, came.astype(jnp.float32))

    partner_by = partner - band * points - jnp.arange(points, dtype=jnp.int32)
    coded = jnp.where(partner_by >= NEAR, partner_by - NEAR + 1, 0).astype(jnp.bfloat16)
    low_valid = jnp.concatenate([counted.astype(jnp.bfloat16), coded[None, :]], 0)
    valid_around = jnp.concatenate(
        [
            shifted(low_valid[:, points - ROWW :], "space", 1),
            low_valid,
            shifted(low_valid[:, :ROWW], "space", -1),
        ],
        1,
    )
    kept = []
    sent = [sent]
    for layer in range(ROUNDS):
        pieces, start = [], 0
        arrivals = [halo(walk, sent[0], sent[0])]
        if len(sent) > 1:
            sent[1], arrivals[0] = lax.optimization_barrier((sent[1], arrivals[0]))
            arrivals.append(halo(walk, sent[1], sent[1]))
        terms = node_terms(mesh, w_round[layer], b_round[layer])
        if layer == 0:
            (before, after), valid_around, counts = lax.optimization_barrier(
                (arrivals[0], valid_around, counts)
            )
            arrivals = [(before, after)]
        for side in ([rows for rows, _ in arrivals], sent, [rows for _, rows in arrivals]):
            for rows in side:
                pieces.append((rows, start))
                start = start + rows.shape[0]
        mats = w_round[layer]
        if layer + 1 < ROUNDS:
            following = w_round[layer + 1]
            reached = [pieces, pieces] if layer == 0 else [pieces[:-1], pieces[1:]]
            indexes = [index[: K * blocks // 2], index[K * blocks // 2 :]]
            *outs, first = round_forward(
                indexes[0], mesh, reached[0], mats, terms, following, half=0
            )
            *outs, second = round_forward(
                indexes[1], mesh, reached[1], mats, terms, following, half=1, into=outs
            )
            sent = [first, second]
        else:
            decoder = (ids, w_dec, w_out, biases)
            outs = round_forward(index, mesh, pieces, mats, terms, None, decoder)
            outs, rest = outs[:5], outs[5:]
        kept.append((mesh, *outs[1:]))
        mesh = outs[0]
    count = counts[0, 0] * 65536.0 + counts[0, 1] * 256.0 + counts[0, 2]
    wide_valid = valid_around[:CH].astype(jnp.float32)
    coded = valid_around[CH : CH + 1, : points + ROWW].astype(jnp.float32)
    weights = [
        (
            by,
            jnp.where(coded == by - NEAR + 1, 1.0, 0.0)
            * wide_valid[:, : points + ROWW]
            * wide_valid[:, by : by + points + ROWW],
        )
        for by in range(NEAR, ROWW + 1)
    ]
    branch_rows, fetched, decoded, dec_turn = rest
    returned = exchanged(branch_rows)
    branch = inner(returned, poster, 0, 0)[:CH]
    err = state_in.astype(jnp.float32) + branch - targets[0].astype(jnp.float32)
    def widened(values):
        low = values.astype(jnp.bfloat16)
        before = shifted(low[:, points - ROWW :], "space", 1).astype(jnp.float32)
        after = shifted(low[:, :ROWW], "space", -1).astype(jnp.float32)
        return jnp.concatenate([before, values, after], 1)

    wide_err = widened(err)
    paired = jnp.zeros((CH, points + ROWW), jnp.float32)
    pair_total = jnp.zeros((CH, points), jnp.float32)
    for by, both in weights:
        gap = both * (wide_err[:, : points + ROWW] - wide_err[:, by : by + points + ROWW])
        paired = paired + gap
        pair_total = pair_total + gap[:, ROWW:] * (
            wide_err[:, ROWW : ROWW + points] - wide_err[:, ROWW + by : ROWW + by + points]
        )
    local_total = jnp.sum(counted * err * err) + 0.5 * jnp.sum(pair_total)
    grad_pred = 2.0 * counted * err + paired[:, ROWW:]
    for by, both in weights:
        gap = both * (wide_err[:, : points + ROWW] - wide_err[:, by : by + points + ROWW])
        grad_pred = grad_pred - gap[:, ROWW - by : ROWW - by + points]
    grad_pred = grad_pred / count
    grad_rows = jnp.pad(grad_pred.astype(jnp.bfloat16), ((0, HALF - CH), (0, 0)))
    landed = exchanged(inner(poster, grad_rows, 1, 1).astype(jnp.bfloat16))
    landed, final_mesh = lax.optimization_barrier((landed, mesh.astype(jnp.bfloat16)))
    final_mesh = at_home(final_mesh)
    mats_grads = [None] * (2 * ROUNDS)
    bias_grads = [None] * ROUNDS
    carried = ()
    for layer in reversed(range(ROUNDS)):
        old, back, update, agg, slopes = kept[layer]
        first_step = not carried
        grad_mesh, leaving, extra, grad_uin, dest_low, to_before, own, to_after = edges_backward(
            index, back, slopes, w_round[layer], carried,
            (ids_row, landed, dec_turn, w_out, w_dec) if first_step else (),
        )
        if first_step:
            to_before, to_after, final_mesh = lax.optimization_barrier(
                (to_before, to_after, final_mesh)
            )
        from_before, from_after = halo(walk, to_after, to_before)
        if first_step:
            from_before, final_mesh, head_grads = lax.optimization_barrier(
                (
                    from_before,
                    settled(mesh, final_mesh),
                    decode_grads(decoded, landed, fetched, extra),
                )
            )
            grad_wout, grad_wdec, grad_bdec = head_grads
        past = () if first_step else (kept[layer + 1][0], extra)
        part, mats_grads[2 * layer + 1], bias_grads[layer], *source = weight_grads(
            old, dest_low, agg, grad_uin, update, leaving, grad_mesh, w_round[layer], past
        )
        if past:
            mats_grads[2 * layer + 2] = source[0]
        carried = (part, own, from_before, from_after, w_round[layer])
    grad_mesh, leaving, grad_win, grad_wnode, grad_bpair, mats_grads[0] = encode_backward(
        carried, kept[0][0], gathered, arrived, ids, w_in, w_node, biases
    )
    parts = [grad_win, grad_wnode, grad_wdec, grad_wout[:, :CH].reshape(CH, D)]
    parts = parts + mats_grads
    parts = parts + [grad_bpair, grad_bdec] + bias_grads
    keep, send = collect_rows(parts, total_size, peers, place)
    mine, leaving = reduced_piece(keep, send, leaving)
    late = at_home(leaving)
    mine = lax.dynamic_slice_in_dim(mine.reshape(-1), offset, shard)
    lane = lax.broadcasted_iota(jnp.int32, (8, HALF), 1)
    sums, late = summed_everywhere(
        jnp.where(lane == 0, local_total, jnp.sum(mine * mine)), late
    )
    total, norm = sums[0, 0], jnp.sqrt(sums[0, 1])
    node_grads = settled_rows(stays, grad_mesh, late)
    clipped = mine * jnp.minimum(1.0, 0.05 / norm)
    first = 0.9 * moment1 + 0.1 * clipped
    second = 0.999 * moment2 + 0.001 * clipped * clipped
    first_hat = first / (1.0 - 0.9**STEP)
    second_hat = second / (1.0 - 0.999**STEP)
    updated = master - 0.1 * (first_hat / (jnp.sqrt(second_hat) + 1e-08) + 0.1 * master)
    return (
        total.reshape(1),
        count.reshape(1),
        norm.reshape(1),
        updated,
        first,
        second,
        updated.astype(jnp.bfloat16),
        final_mesh.reshape(1, blocks, D),
        node_grads.reshape(1, blocks, D),
        grad_pred.reshape(1, grad_pred.shape[0], points),
    )


def solution(mesh):
    return jax.shard_map(
        functools.partial(shards, walk_of(mesh)),
        mesh=mesh,
        in_specs=(
            P(("dp", "space")),
            P(("dp", "space")),
            P(("dp", "space")),
            P("dp", None, "space"),
            P("dp", None, "space"),
            P("dp", None, "space"),
            P("dp", "space", None),
            P("dp", "space"),
            P("space", None),
            P("space"),
        ),
        out_specs=(
            P(),
            P(),
            P(),
            P(("dp", "space")),
            P(("dp", "space")),
            P(("dp", "space")),
            P(("dp", "space")),
            P("dp", "space", None),
            P("dp", "space", None),
            P("dp", None, "space"),
        ),
        check_vma=False,
    )
```

```python
import functools

import jax
import jax.numpy as jnp
from jax import lax
from jax.experimental import pallas as pl
from jax.experimental.pallas import tpu as pltpu
from jax.sharding import PartitionSpec as P

D = 256
HALF = 128
CH = 78
ROUNDS = 3
K = 6
ROWW = 360
NEAR = 358
STEP = 10
H = 2048
ALL = ("dp", "space")
LIMIT = pltpu.CompilerParams(vmem_limit_bytes=60 * 2**20)


def cost(micros):
    return pl.CostEstimate(flops=0, bytes_accessed=micros * 3_000_000, transcendentals=0)


def inner(left, right, left_dim, right_dim):
    return lax.dot_general(
        left, right, (((left_dim,), (right_dim,)), ((), ())), preferred_element_type=jnp.float32
    )


def sigmoid(value):
    return 0.5 * jnp.tanh(0.5 * value) + 0.5


def silu(value):
    return value * sigmoid(value)


def slope(value):
    sigma = sigmoid(value)
    return sigma * (1.0 + value * (1.0 - sigma))


def shifted(shard, axis, by):
    peers = lax.axis_size(axis)
    pairs = [(i, i + by) for i in range(peers) if 0 <= i + by < peers]
    return lax.ppermute(shard, axis, pairs)


def walk_of(mesh):
    count = mesh.shape["space"]
    chips = [getattr(device, "coords", None) for device in mesh.devices[0].reshape(-1)]
    if any(chip is None for chip in chips) or len(set(map(tuple, chips))) != count:
        return list(range(count))
    at = {tuple(chip): n for n, chip in enumerate(chips)}
    xs, ys, zs = (sorted({chip[n] for chip in at}) for n in range(3))
    if len(xs) * len(ys) * len(zs) != count:
        return list(range(count))
    if (len(xs), len(ys), len(zs)) == (2, 2, 4):
        corners = [(0, 0), (1, 0), (0, 1), (1, 1)]
        planes = [(0, 1, 3, 2), (2, 0, 1, 3), (3, 1, 0, 2), (2, 3, 1, 0)]
        steps = [(*corners[n], z) for z, plane in enumerate(planes) for n in plane]
        return [at[(xs[x], ys[y], zs[z])] for x, y, z in steps]
    walk, plane = [], []
    for n, y in enumerate(ys):
        plane = plane + [(x, y) for x in (xs if n % 2 == 0 else xs[::-1])]
    for n, z in enumerate(zs):
        walk = walk + [at[(x, y, z)] for x, y in (plane if n % 2 == 0 else plane[::-1])]
    return walk


def halo(walk, last, initial):
    up = list(zip(walk, walk[1:] + walk[:1]))
    down = [(j, i) for i, j in up]
    return lax.ppermute(last, "space", up), lax.ppermute(initial, "space", down)


def pieces_of(total, peers):
    share = total // peers
    starts = [share * d // D for d in range(peers)]
    counts = [-(-share * (d + 1) // D) - starts[d] for d in range(peers)]
    shared = [share * d % D != 0 for d in range(peers)]
    height = -(-max(counts) // 16) * 16
    return starts, counts, shared, height


def parts_of():
    return [CH, D, D, CH] + [5 * D] * ROUNDS + [3 + 2 * ROUNDS]


def swapped(value, axis, bit):
    return lax.ppermute(value, axis, [(i, i ^ bit) for i in range(lax.axis_size(axis))])


def bits_of(axis):
    return [1 << n for n in range(lax.axis_size(axis).bit_length() - 1)]


def others(value, axis, bits):
    masks = [sum(bit for n, bit in enumerate(bits) if m >> n & 1) for m in range(1, 1 << len(bits))]
    return [swapped(value, axis, mask) for mask in masks]


def upper_groups():
    bits = bits_of("space")[2:]
    return [tuple(bits[n : n + 2]) for n in range(0, len(bits), 2)]


def orders():
    return [(1, 2), (2, 1)]


def summed_everywhere(value, arriving):
    for bits in reversed(upper_groups()):
        value = sum(others(value, "space", bits), value)
    value = value + swapped(value, "dp", 1)
    value, arriving = lax.optimization_barrier((value, arriving))
    return sum(others(value, "space", (1, 2)), value), arriving


def gathered_blocks(piece, posted):
    held, weights, size = piece[None], {}, 1
    for bits in reversed(upper_groups()):
        held = jnp.concatenate([held] + others(held, "space", bits), 0)
        for n, bit in enumerate(bits):
            weights[bit] = size << n
        size = size << len(bits)
    half = piece.shape[0] // 2
    held = [held[:, :half], held[:, half:]]
    ranks = [dict(weights), dict(weights)]
    for turn in (1, 0):
        if turn == 0:
            held[0], held[1], posted = lax.optimization_barrier((*held, posted))
        for n, order in enumerate(orders()):
            held[n] = jnp.concatenate([held[n], swapped(held[n], "space", order[turn])], 0)
            ranks[n][order[turn]] = size
        size = size << 1
    return (held, [swapped(part, "dp", 1) for part in held], ranks), posted


def spread_rows(gathered, total, peers, place):
    (first, second), (first_far, second_far), ranks = gathered
    starts, counts, shared, height = pieces_of(total, peers)
    half, group = height // 2, first.shape[0]
    rows = -(-total // D)
    sizes = parts_of()
    def at(rank, relative):
        spot = 0
        for bit, weight in rank.items():
            spot = spot + jnp.where((relative & bit) != 0, weight, 0)
        return spot

    def body(place_ref, *refs):
        sources, outs, buffer = refs[:4], refs[4:-1], refs[-1]
        me = place_ref[0]
        mine = me // group
        for d in range(peers):
            relative = (me ^ d) & (group - 1)
            spots = [at(rank, relative) for rank in ranks]

            def lay(one, two, d=d, spots=spots):
                piece = jnp.concatenate([one[spots[0]], two[spots[1]]], 0).astype(jnp.float32)
                start, count = starts[d], counts[d]
                if shared[d]:
                    buffer[start : start + 1, :] = buffer[start : start + 1, :] + piece[:1]
                    buffer[start + 1 : start + count, :] = piece[1:count]
                else:
                    buffer[start : start + count, :] = piece[:count]

            @pl.when(mine == d // group)
            def _():
                lay(sources[0], sources[1])

            @pl.when(mine != d // group)
            def _():
                lay(sources[2], sources[3])

        start = 0
        for out, size in zip(outs, sizes):
            out[:size, :] = buffer[start : start + size, :].astype(out.dtype)
            if out.shape[0] > size:
                out[size:, :] = jnp.zeros((out.shape[0] - size, D), out.dtype)
            start = start + size

    kinds = [jnp.bfloat16] * (4 + ROUNDS) + [jnp.float32]
    talls = [HALF] + sizes[1:]
    return pl.pallas_call(
        body,
        grid_spec=pltpu.PrefetchScalarGridSpec(
            num_scalar_prefetch=1,
            grid=(1,),
            in_specs=[whole(first.shape)] * 4,
            out_specs=[whole((tall, D)) for tall in talls],
            scratch_shapes=[pltpu.VMEM((-(-rows // 8) * 8 + 8, D), jnp.float32)],
        ),
        out_shape=[jax.ShapeDtypeStruct((tall, D), kind) for tall, kind in zip(talls, kinds)],
        compiler_params=LIMIT,
        cost_estimate=cost(4),
        name="spread_rows",
    )(place.reshape(1), first, second, first_far, second_far)


def collect_rows(parts, total, peers, place):
    starts, counts, shared, height = pieces_of(total, peers)
    rows = -(-total // D)
    sizes = [min(part.shape[0], size) for part, size in zip(parts, tall_parts())]
    group = lax.axis_size("space")

    def body(place_ref, *refs):
        sources, keep, send, buffer = refs[:-3], refs[-3], refs[-2], refs[-1]
        start = 0
        for source, size in zip(sources, sizes):
            buffer[start : start + size, :] = source[:size, :]
            start = start + size
        if buffer.shape[0] > start:
            buffer[start:, :] = jnp.zeros((buffer.shape[0] - start, D), jnp.float32)
        me = place_ref[0]
        mine = me // group
        for d in range(peers):
            relative = (me ^ d) & (group - 1)

            @pl.when(mine == d // group)
            def _():
                keep[relative] = buffer[starts[d] : starts[d] + height, :]

            @pl.when(mine != d // group)
            def _():
                send[relative] = buffer[starts[d] : starts[d] + height, :].astype(jnp.bfloat16)

    shape = (group, height, D)
    return pl.pallas_call(
        body,
        grid_spec=pltpu.PrefetchScalarGridSpec(
            num_scalar_prefetch=1,
            grid=(1,),
            in_specs=[whole(part.shape) for part in parts],
            out_specs=[whole(shape), whole(shape)],
            scratch_shapes=[pltpu.VMEM((-(-rows // 8) * 8 + height + 8, D), jnp.float32)],
        ),
        out_shape=[
            jax.ShapeDtypeStruct(shape, jnp.float32),
            jax.ShapeDtypeStruct(shape, jnp.bfloat16),
        ],
        compiler_params=LIMIT,
        cost_estimate=cost(5),
        name="collect_rows",
    )(place.reshape(1), *parts)


def reduced_piece(keep, send, leaving):
    kept = keep + swapped(send, "dp", 1).astype(jnp.float32)
    half = kept.shape[1] // 2
    groups = upper_groups()
    inner_shape = (kept.shape[0] // 4, 2, 2, half, D)
    parts = [kept[:, :half].reshape(inner_shape), kept[:, half:].reshape(inner_shape)]
    for n, order in enumerate(orders()):
        for bit in order:
            spot = 2 if bit == 1 and parts[n].ndim == 5 else 1
            stay = lax.index_in_dim(parts[n], 0, spot, keepdims=False)
            leave = lax.index_in_dim(parts[n], 1, spot, keepdims=False)
            parts[n] = stay + swapped(leave.astype(jnp.bfloat16), "space", bit).astype(jnp.float32)
    part = jnp.concatenate(parts, 1)
    part, leaving = lax.optimization_barrier((part, leaving))
    for bits in groups:
        part = part.reshape((-1, 1 << len(bits)) + part.shape[1:])
        masks = [sum(bit for n, bit in enumerate(bits) if m >> n & 1) for m in range(1 << len(bits))]
        low = part.astype(jnp.bfloat16)
        part = sum(
            [
                swapped(low[:, m], "space", mask).astype(jnp.float32)
                for m, mask in enumerate(masks)
                if m
            ],
            part[:, 0],
        )
    return part[0], leaving


def tall_parts():
    return [CH, D, D, CH] + [D, 4 * D] * ROUNDS + [2, 1] + [2] * ROUNDS


def weave(ref, value):
    rows = value.shape[0]
    ref[pl.ds(0, rows, stride=2), :] = value[:, :HALF]
    ref[pl.ds(1, rows, stride=2), :] = value[:, HALF:]


def unweave(ref):
    rows = ref.shape[0] // 2
    return ref[pl.ds(0, rows, stride=2), :], ref[pl.ds(1, rows, stride=2), :]


def selector():
    row = lax.broadcasted_iota(jnp.int32, (8, HALF), 0)
    lane = lax.broadcasted_iota(jnp.int32, (8, HALF), 1)
    slot = jnp.where(lane == CH, 64.0, jnp.where(lane == CH + 1, 1.0, 0.0))
    known = jnp.where(lane == CH + 2, 1.0, 0.0)
    return jnp.where(row == 0, slot, jnp.where(row == 1, known, 0.0)).astype(jnp.bfloat16)


def ids_along(arrived):
    codes = inner(selector(), arrived, 1, 1)
    return jnp.where(codes[1:2, :] > 0, codes[0:1, :], -1.0).astype(jnp.int32)


def ids_down(arrived):
    codes = inner(arrived, selector(), 1, 1)
    return jnp.where(codes[:, 1:2] > 0, codes[:, 0:1], -1.0).astype(jnp.int32)


def whole(shape):
    return pl.BlockSpec(shape, lambda *_: (0,) * len(shape))


def node_terms(mesh, mats, bias):
    blocks = mesh.shape[0]
    tile = 1024

    def body(mesh_ref, mats_ref, bias_ref, dest_ref, self_ref):
        lowered = mesh_ref[...].astype(jnp.bfloat16)
        weave(dest_ref, inner(lowered, mats_ref[1], 1, 0) + bias_ref[0:1, :])
        self_ref[...] = inner(lowered, mats_ref[3], 1, 0) + bias_ref[1:2, :]

    rows = pl.BlockSpec((tile, D), lambda i: (i, 0))
    woven = pl.BlockSpec((2 * tile, HALF), lambda i: (i, 0))
    return pl.pallas_call(
        body,
        grid=(blocks // tile,),
        in_specs=[rows, whole(mats.shape), whole(bias.shape)],
        out_specs=[woven, rows],
        out_shape=[
            jax.ShapeDtypeStruct((2 * blocks, HALF), jnp.float32),
            jax.ShapeDtypeStruct((blocks, D), jnp.float32),
        ],
        compiler_params=pltpu.CompilerParams(vmem_limit_bytes=63 * 2**20),
        cost_estimate=cost(4),
        name="node_terms",
    )(mesh, mats, bias)


def round_forward(index, mesh, pieces, mats, terms, following, decoder=(), half=None, into=()):
    blocks = mesh.shape[0]
    tile, chunk = 512, 16
    turns, high = tile // chunk, 2 * chunk
    more = following is not None
    reach = 2 * (blocks + 2 * H)
    steps = blocks // tile if half is None else blocks // tile // 2
    shift = 0 if half is None else half * steps

    def body(index_ref, mesh_ref, *refs):
        sources, refs = refs[: len(pieces)], refs[len(pieces) :]
        (mats_ref, dest_ref, self_ref), refs = refs[:3], refs[3:]
        table, rows, wide = refs[-3:]
        if more:
            next_ref, refs = refs[0], refs[1 + len(into) :]
            new_ref, back_ref, update_ref, agg_ref, slope_ref, sent_ref = refs[:6]
        else:
            ids_ref, dec_ref, out_ref, head_ref = refs[:4]
            new_ref, back_ref, update_ref, agg_ref, slope_ref = refs[4:9]
            branch_ref, fetched_ref, decoded_ref, turn_ref, total_ref = refs[9:14]
        step = pl.program_id(0)

        @pl.when(step == 0)
        def _():
            for source, (_, start) in zip(sources, pieces):

                @pl.loop(0, source.shape[0] // 256)
                def _(i, source=source, start=start):
                    at = pl.multiple_of(i * 256, 256)
                    to = pl.multiple_of(start + at, 256)
                    table[pl.ds(to, 256), :] = source[pl.ds(at, 256), :].astype(jnp.float32)

        mesh_in = mesh_ref[...]

        part = blocks // 2
        if half is None:
            origin = step // (steps // 2) * (K * part) + lax.rem(step, steps // 2) * tile
        else:
            origin = step * tile

        def fetch(turn):
            for edge in range(K):
                base = edge * part + turn * chunk + origin
                spots = [index_ref[base + u] for u in range(chunk)]
                values = [table[pl.ds(pl.multiple_of(spot, 2), 2), :] for spot in spots]
                for u in range(chunk):
                    spot = pl.multiple_of(edge * 2 * tile + turn * high + 2 * u, 2)
                    rows[pl.ds(spot, 2), :] = values[u]

        def load(turn):
            at = pl.multiple_of(turn * high, high)
            taken = [
                rows[pl.ds(pl.multiple_of(edge * 2 * tile + turn * high, high), high), :]
                for edge in range(K)
            ]
            return at, dest_ref[pl.ds(at, high), :], taken

        def dense(at, dest, taken):
            total = None
            for edge in range(K):
                value = taken[edge] + dest
                sigma = sigmoid(value)
                out = value * sigma
                slope_ref[edge, pl.ds(at, high), :] = (sigma + out * (1.0 - sigma)).astype(
                    jnp.bfloat16
                )
                total = out if total is None else total + out
            wide[pl.ds(at, high), :] = total * (1.0 / K)

        def some(turn, carry):
            loaded = load(turn - 1)
            fetch(turn)
            dense(*loaded)
            return carry

        fetch(0)
        lax.fori_loop(1, turns, some, 0)
        dense(*load(turns - 1))
        first, second = unweave(wide)
        first, second = first.astype(jnp.bfloat16), second.astype(jnp.bfloat16)
        agg_ref[:, :HALF] = first
        agg_ref[:, HALF:] = second
        update_in = (
            inner(first, mats_ref[2, :HALF, :], 1, 0)
            + inner(second, mats_ref[2, HALF:, :], 1, 0)
            + self_ref[...]
        )
        sigma = sigmoid(update_in)
        out = update_in * sigma
        back_ref[...] = sigma + out * (1.0 - sigma)
        update = out.astype(jnp.bfloat16)
        update_ref[...] = update
        new = mesh_in + inner(update, mats_ref[4], 1, 0)
        new_ref[...] = new
        lowered = new.astype(jnp.bfloat16)
        if more:
            weave(wide, inner(lowered, next_ref[0], 1, 0))
            sent_ref[...] = wide[...].astype(jnp.bfloat16)
            return
        nodes = lax.broadcasted_iota(jnp.int32, (ids_ref.shape[0], tile), 1) + step * tile
        chooser = jnp.where(nodes == ids_ref[...], 1.0, 0.0).astype(jnp.bfloat16)
        found = inner(chooser, lowered, 1, 0)

        @pl.when(step == 0)
        def _():
            total_ref[...] = found

        @pl.when(step > 0)
        def _():
            total_ref[...] += found

        @pl.when(step == blocks // tile - 1)
        def _():
            fetched = total_ref[...].astype(jnp.bfloat16)
            fetched_ref[...] = fetched
            value = inner(fetched, dec_ref[...], 1, 0) + head_ref[2:3, :]
            sigma = sigmoid(value)
            out = value * sigma
            turn_ref[...] = sigma + out * (1.0 - sigma)
            decoded = out.astype(jnp.bfloat16)
            decoded_ref[...] = decoded
            branch_ref[...] = inner(decoded, out_ref[...], 1, 0).astype(jnp.bfloat16)

    whole_rows = pl.BlockSpec((tile, D), lambda i, *_: (i + shift, 0))
    woven = pl.BlockSpec((2 * tile, HALF), lambda i, *_: (i + shift, 0))
    ins = [whole_rows] + [pl.BlockSpec(memory_space=pltpu.VMEM)] * len(pieces)
    ins = ins + [whole(mats.shape), woven, whole_rows]
    outs = [whole_rows] * 4 + [pl.BlockSpec((K, 2 * tile, HALF), lambda i, *_: (0, i + shift, 0))]
    shapes = [
        jax.ShapeDtypeStruct((blocks, D), jnp.float32),
        jax.ShapeDtypeStruct((blocks, D), jnp.float32),
        jax.ShapeDtypeStruct((blocks, D), jnp.bfloat16),
        jax.ShapeDtypeStruct((blocks, D), jnp.bfloat16),
        jax.ShapeDtypeStruct((K, 2 * blocks, HALF), jnp.bfloat16),
    ]
    args = [index, mesh] + [rows for rows, _ in pieces] + [mats, *terms]
    if more:
        ins.append(pl.BlockSpec((1, D, D), lambda *_: (0, 0, 0)))
        outs.append(pl.BlockSpec((2 * tile, HALF), lambda i, *_: (i, 0)))
        shapes.append(jax.ShapeDtypeStruct((2 * tile * steps, HALF), jnp.bfloat16))
        args.append(following)
    aliases = {len(args) + n: n for n in range(len(into))}
    ins = ins + [pl.BlockSpec(memory_space=pl.ANY)] * len(into)
    args = args + list(into)
    scratch = []
    if decoder:
        posts = decoder[0].shape[0]
        ins = ins + [whole(arg.shape) for arg in decoder]
        args = args + list(decoder)
        for width, kind in ((HALF, jnp.bfloat16), (D, jnp.bfloat16), (D, jnp.bfloat16), (D, jnp.float32)):
            outs.append(whole((posts, width)))
            shapes.append(jax.ShapeDtypeStruct((posts, width), kind))
        scratch = [pltpu.VMEM((posts, D), jnp.float32)]
    return pl.pallas_call(
        body,
        grid_spec=pltpu.PrefetchScalarGridSpec(
            num_scalar_prefetch=1,
            grid=(steps,),
            in_specs=ins,
            out_specs=outs,
            scratch_shapes=scratch
            + [
                pltpu.VMEM((reach, HALF), jnp.float32),
                pltpu.VMEM((K * 2 * tile, HALF), jnp.float32),
                pltpu.VMEM((2 * tile, HALF), jnp.float32),
            ],
        ),
        out_shape=shapes,
        input_output_aliases=aliases,
        compiler_params=pltpu.CompilerParams(vmem_limit_bytes=63 * 2**20),
        cost_estimate=cost(24 if half is None else 14),
        name="round_forward",
    )(*args)


def edges_backward(index, back, slopes, mats, carried=(), landed=()):
    blocks = back.shape[0]
    tile, chunk = 512, 16
    steps, turns, high = blocks // tile, tile // chunk, 2 * chunk
    reach = 2 * (blocks + 2 * H)

    def body(*refs):
        if carried:
            index_ref, back_ref, slope_ref, mats_ref = refs[:4]
            past, rest = refs[4:9], refs[9:]
            (new_ref, out_ref, sent_ref), rest = rest[:3], rest[3:]
        else:
            index_ref, back_ref, slope_ref, mats_ref = refs[:4]
            (ids_ref, landed_ref, turn_ref, w_out_ref, w_dec_ref), rest = refs[4:9], refs[9:]
            (new_ref, out_ref, gdec_ref), rest = rest[:3], rest[3:]
            gathered, rest = rest[5], rest[:5] + rest[6:]
        guin_ref, low_ref, before_ref, own_ref, after_ref, wide, wider, flows, *tables = rest
        step = pl.program_id(0)

        @pl.when(step == 0)
        def _():
            @pl.loop(0, reach // 256)
            def _(i):
                for table in tables:
                    table[pl.ds(pl.multiple_of(i * 256, 256), 256), :] = jnp.zeros(
                        (256, HALF), jnp.float32
                    )

        if carried:
            new, one, two = ended(*past, wide)
            sent_ref[:, :HALF] = one
            sent_ref[:, HALF:] = two
            new_ref[...] = new
            grad_out = new.astype(jnp.bfloat16)
            out_ref[...] = grad_out
        else:

            @pl.when(step == 0)
            def _():
                grad_dec = inner(landed_ref[...], w_out_ref[...], 1, 1) * turn_ref[...]
                grad_dec = grad_dec.astype(jnp.bfloat16)
                gdec_ref[...] = grad_dec
                gathered[...] = inner(grad_dec, w_dec_ref[...], 1, 1).astype(jnp.bfloat16)

            nodes = lax.broadcasted_iota(jnp.int32, (tile, landed_ref.shape[0]), 0) + step * tile
            chooser = jnp.where(nodes == ids_ref[...], 1.0, 0.0).astype(jnp.bfloat16)
            new = inner(chooser, gathered[...], 1, 0)
            new_ref[...] = new
            grad_out = new.astype(jnp.bfloat16)
            out_ref[...] = grad_out
        grad_uin = (inner(grad_out, mats_ref[4], 1, 1) * back_ref[...]).astype(jnp.bfloat16)
        guin_ref[...] = grad_uin
        weave(wide, inner(grad_uin, mats_ref[2], 1, 1) * (1.0 / K))

        def dense(turn):
            at = pl.multiple_of(turn * high, high)
            grad_agg = wide[pl.ds(at, high), :]
            total, parts = None, []
            for edge in range(K):
                flow = grad_agg * slope_ref[edge, pl.ds(at, high), :].astype(jnp.float32)
                parts.append(flow)
                total = flow if total is None else total + flow
            return at, total, parts

        def keep(turn, at, total, parts):
            for edge in range(K):
                spot = pl.multiple_of(edge * 2 * tile + turn * high, high)
                flows[pl.ds(spot, high), :] = parts[edge]
            wider[pl.ds(at, high), :] = total

        part = blocks // 2
        origin = step // (steps // 2) * (K * part) + lax.rem(step, steps // 2) * tile

        def scatter(turn):
            for u in range(chunk):
                spots, sums = [], []
                for edge in range(K):
                    base = edge * part + turn * chunk + origin
                    spots.append(pl.multiple_of(index_ref[base + u], 2))
                for edge in range(K):
                    spot = pl.multiple_of(edge * 2 * tile + turn * high + 2 * u, 2)
                    sums.append(tables[edge][pl.ds(spots[edge], 2), :] + flows[pl.ds(spot, 2), :])
                for edge in range(K):
                    tables[edge][pl.ds(spots[edge], 2), :] = sums[edge]

        def some(turn, carry):
            found = dense(turn)
            scatter(turn - 1)
            keep(turn, *found)
            return carry

        keep(0, *dense(0))
        lax.fori_loop(1, turns, some, 0)
        scatter(turns - 1)
        first, second = unweave(wider)
        low_ref[:, :HALF] = first.astype(jnp.bfloat16)
        low_ref[:, HALF:] = second.astype(jnp.bfloat16)

        @pl.when(step == steps - 1)
        def _():
            def summed(at):
                value = tables[0][pl.ds(at, 256), :]
                for table in tables[1:]:
                    value = value + table[pl.ds(at, 256), :]
                return value

            @pl.loop(0, 2 * H // 256)
            def _(i):
                at = pl.multiple_of(i * 256, 256)
                far = pl.multiple_of(2 * H + 2 * blocks + at, 256)
                before_ref[pl.ds(at, 256), :] = summed(at).astype(jnp.bfloat16)
                after_ref[pl.ds(at, 256), :] = summed(far).astype(jnp.bfloat16)

            @pl.loop(0, 2 * blocks // 256)
            def _(i):
                at = pl.multiple_of(i * 256, 256)
                own_ref[pl.ds(at, 256), :] = summed(pl.multiple_of(2 * H + at, 256))

    rows = pl.BlockSpec((tile, D), lambda i, *_: (i, 0))
    woven = pl.BlockSpec((2 * tile, HALF), lambda i, *_: (i, 0))
    low = jax.ShapeDtypeStruct((blocks, D), jnp.bfloat16)
    low_posts = (landed[1].shape[0], D) if landed else None
    last = low if carried else jax.ShapeDtypeStruct(low_posts, jnp.bfloat16)
    return pl.pallas_call(
        body,
        grid_spec=pltpu.PrefetchScalarGridSpec(
            num_scalar_prefetch=1,
            grid=(steps,),
            in_specs=[
                rows,
                pl.BlockSpec((K, 2 * tile, HALF), lambda i, *_: (0, i, 0)),
                whole(mats.shape),
            ]
            + ([rows] + [woven] * 3 + [whole(mats.shape)] if carried else [])
            + [whole(arg.shape) for arg in landed],
            out_specs=([rows] * 3 if carried else [rows, rows, whole(low_posts)])
            + [
                rows, rows,
                whole((2 * H, HALF)), whole((2 * blocks, HALF)), whole((2 * H, HALF)),
            ],
            scratch_shapes=([] if carried else [pltpu.VMEM(low_posts, jnp.bfloat16)])
            + [
                pltpu.VMEM((2 * tile, HALF), jnp.float32),
                pltpu.VMEM((2 * tile, HALF), jnp.float32),
                pltpu.VMEM((2 * tile * K, HALF), jnp.float32),
            ]
            + [pltpu.VMEM((reach, HALF), jnp.float32)] * K,
        ),
        out_shape=[
            jax.ShapeDtypeStruct((blocks, D), jnp.float32),
            low,
            last,
            low,
            low,
            jax.ShapeDtypeStruct((2 * H, HALF), jnp.bfloat16),
            jax.ShapeDtypeStruct((2 * blocks, HALF), jnp.float32),
            jax.ShapeDtypeStruct((2 * H, HALF), jnp.bfloat16),
        ],
        compiler_params=pltpu.CompilerParams(vmem_limit_bytes=63 * 2**20),
        cost_estimate=cost(28 if carried else 25),
        name="edges_backward",
    )(index, back, slopes, mats, *carried, *landed)


def ended(part_ref, own_ref, first_ref, last_ref, mats_ref, wide):
    wide[...] = (
        own_ref[...] + first_ref[...].astype(jnp.float32) + last_ref[...].astype(jnp.float32)
    )
    one, two = unweave(wide)
    one, two = one.astype(jnp.bfloat16), two.astype(jnp.bfloat16)
    new = (
        part_ref[...]
        + inner(one, mats_ref[0, :, :HALF], 1, 1)
        + inner(two, mats_ref[0, :, HALF:], 1, 1)
    )
    return new, one, two


def weight_grads(mesh, dest_low, agg, grad_uin, update, leaving, grad_mesh, mats, past=()):
    blocks = mesh.shape[0]
    tile = 512

    def body(mesh_ref, dest_ref, agg_ref, guin_ref, update_ref, out_ref, grad_ref, mats_ref, *refs):
        if past:
            (old_ref, sent_ref), refs = refs[:2], refs[2:]
        part_ref, grads_ref, bias_ref = refs[:3]

        @pl.when(pl.program_id(0) == 0)
        def _():
            for ref in refs[1:]:
                ref[...] = jnp.zeros(ref.shape, jnp.float32)

        lowered = mesh_ref[...].astype(jnp.bfloat16)
        dest, guin = dest_ref[...], guin_ref[...]
        grads_ref[:D, :] += inner(lowered, dest, 0, 0)
        grads_ref[D : 2 * D, :] += inner(agg_ref[...], guin, 0, 0)
        grads_ref[2 * D : 3 * D, :] += inner(lowered, guin, 0, 0)
        grads_ref[3 * D :, :] += inner(update_ref[...], out_ref[...], 0, 0)
        bias_ref[0:1, :] += jnp.sum(dest.astype(jnp.float32), 0, keepdims=True)
        bias_ref[1:2, :] += jnp.sum(guin.astype(jnp.float32), 0, keepdims=True)
        part_ref[...] = (
            grad_ref[...] + inner(guin, mats_ref[3], 1, 1) + inner(dest, mats_ref[1], 1, 1)
        )
        if past:
            refs[3][...] += inner(old_ref[...].astype(jnp.bfloat16), sent_ref[...], 0, 0)

    rows = pl.BlockSpec((tile, D), lambda i: (i, 0))
    shapes = [(4 * D, D), (2, D)] + ([(D, D)] if past else [])
    return pl.pallas_call(
        body,
        grid=(blocks // tile,),
        in_specs=[rows] * 7 + [whole(mats.shape)] + [rows] * len(past),
        out_specs=[rows] + [whole(shape) for shape in shapes],
        out_shape=[jax.ShapeDtypeStruct((blocks, D), jnp.float32)]
        + [jax.ShapeDtypeStruct(shape, jnp.float32) for shape in shapes],
        compiler_params=pltpu.CompilerParams(vmem_limit_bytes=63 * 2**20),
        cost_estimate=cost(10),
        name="weight_grads",
    )(mesh, dest_low, agg, grad_uin, update, leaving, grad_mesh, mats, *past)


def decode_grads(decoded, landed, fetched, grad_dec):
    def body(decoded_ref, landed_ref, fetched_ref, grad_ref, gout_ref, gdec_ref, bias_ref):
        gout_ref[...] = inner(decoded_ref[...], landed_ref[...], 0, 0)
        gdec_ref[...] = inner(fetched_ref[...], grad_ref[...], 0, 0)
        bias_ref[...] = jnp.sum(grad_ref[...].astype(jnp.float32), 0, keepdims=True)

    return pl.pallas_call(
        body,
        out_shape=[jax.ShapeDtypeStruct(shape, jnp.float32) for shape in ((D, HALF), (D, D), (1, D))],
        compiler_params=pltpu.CompilerParams(vmem_limit_bytes=63 * 2**20),
        cost_estimate=cost(3),
        name="decode_grads",
    )(decoded, landed, fetched, grad_dec)


def encode_rows(arrived, w_in, w_node, biases, source):
    posts = arrived.shape[0]
    tile = 1024

    def body(
        arrived_ref, in_ref, node_ref, bias_ref, source_ref,
        mesh_ref, gathered_ref, sent_ref, ids_ref, down_ref, encoded, wide,
    ):
        step = pl.program_id(0)

        @pl.when(step == 0)
        def _():
            entering = inner(arrived_ref[...], in_ref[...], 1, 0) + bias_ref[0:1, :]
            encoded[...] = silu(entering).astype(jnp.bfloat16)
            ids_ref[...] = ids_along(arrived_ref[...])
            down_ref[...] = ids_down(arrived_ref[...])

        nodes = lax.broadcasted_iota(jnp.int32, (tile, posts), 0) + step * tile
        chooser = jnp.where(nodes == ids_ref[...], 1.0, 0.0).astype(jnp.bfloat16)
        gathered = inner(chooser, encoded[...], 1, 0).astype(jnp.bfloat16)
        gathered_ref[...] = gathered
        mesh = silu(inner(gathered, node_ref[...], 1, 0) + bias_ref[1:2, :])
        mesh_ref[...] = mesh
        weave(wide, inner(mesh.astype(jnp.bfloat16), source_ref[0], 1, 0))
        sent_ref[...] = wide[...].astype(jnp.bfloat16)

    rows = pl.BlockSpec((tile, D), lambda i: (i, 0))
    args = (arrived, w_in, w_node, biases, source)
    return pl.pallas_call(
        body,
        grid=(H // tile,),
        in_specs=[whole(arg.shape) for arg in args[:-1]]
        + [pl.BlockSpec((1, D, D), lambda *_: (0, 0, 0))],
        out_specs=[rows, rows, pl.BlockSpec((2 * tile, HALF), lambda i: (i, 0))]
        + [whole((1, posts)), whole((posts, 1))],
        out_shape=[
            jax.ShapeDtypeStruct((H, D), jnp.float32),
            jax.ShapeDtypeStruct((H, D), jnp.bfloat16),
            jax.ShapeDtypeStruct((2 * H, HALF), jnp.bfloat16),
            jax.ShapeDtypeStruct((1, posts), jnp.int32),
            jax.ShapeDtypeStruct((posts, 1), jnp.int32),
        ],
        scratch_shapes=[pltpu.VMEM((posts, D), jnp.bfloat16), pltpu.VMEM((2 * tile, HALF), jnp.float32)],
        compiler_params=LIMIT,
        cost_estimate=cost(5),
        name="encode_rows",
    )(*args)


def encode_backward(carried, mesh, gathered, arrived, ids, w_in, w_node, biases):
    blocks = mesh.shape[0]
    posts = arrived.shape[0]
    tile = 512
    steps = blocks // tile

    def body(
        part_ref, own_ref, first_ref, last_ref, mats_ref,
        mesh_ref, gathered_ref, arrived_ref, ids_ref, in_ref, node_ref, bias_ref,
        new_ref, out_ref, gin_ref, gnode_ref, gbias_ref, gsource_ref, total, wide,
    ):
        step = pl.program_id(0)

        @pl.when(step == 0)
        def _():
            for ref in (total, gnode_ref, gbias_ref, gsource_ref):
                ref[...] = jnp.zeros(ref.shape, jnp.float32)

        new, one, two = ended(part_ref, own_ref, first_ref, last_ref, mats_ref, wide)
        new_ref[...] = new
        out_ref[...] = new.astype(jnp.bfloat16)
        lowered = mesh_ref[...].astype(jnp.bfloat16)
        gsource_ref[:, :HALF] += inner(lowered, one, 0, 0)
        gsource_ref[:, HALF:] += inner(lowered, two, 0, 0)
        node_in = inner(gathered_ref[...], node_ref[...], 1, 0) + bias_ref[1:2, :]
        grad_node = (new * slope(node_in)).astype(jnp.bfloat16)
        gbias_ref[1:2, :] += jnp.sum(grad_node.astype(jnp.float32), 0, keepdims=True)
        gnode_ref[...] += inner(gathered_ref[...], grad_node, 0, 0)
        back = inner(grad_node, node_ref[...], 1, 1).astype(jnp.bfloat16)
        nodes = lax.broadcasted_iota(jnp.int32, (posts, tile), 1) + step * tile
        chooser = jnp.where(nodes == ids_ref[...], 1.0, 0.0).astype(jnp.bfloat16)
        total[...] += inner(chooser, back, 1, 0)

        @pl.when(step == steps - 1)
        def _():
            entering = inner(arrived_ref[...], in_ref[...], 1, 0) + bias_ref[0:1, :]
            grad_enc = (total[...] * slope(entering)).astype(jnp.bfloat16)
            gbias_ref[0:1, :] = jnp.sum(grad_enc.astype(jnp.float32), 0, keepdims=True)
            gin_ref[...] = inner(arrived_ref[...], grad_enc, 0, 0)

    rows = pl.BlockSpec((tile, D), lambda i: (i, 0))
    woven = pl.BlockSpec((2 * tile, HALF), lambda i: (i, 0))
    args = (arrived, ids, w_in, w_node, biases)
    shapes = [(HALF, D), (D, D), (2, D), (D, D)]
    return pl.pallas_call(
        body,
        grid=(steps,),
        in_specs=[rows] + [woven] * 3 + [whole(carried[4].shape), rows, rows]
        + [whole(arg.shape) for arg in args],
        out_specs=[rows, rows] + [whole(shape) for shape in shapes],
        out_shape=[
            jax.ShapeDtypeStruct((blocks, D), jnp.float32),
            jax.ShapeDtypeStruct((blocks, D), jnp.bfloat16),
        ]
        + [jax.ShapeDtypeStruct(shape, jnp.float32) for shape in shapes],
        scratch_shapes=[pltpu.VMEM((posts, D), jnp.float32), pltpu.VMEM((2 * tile, HALF), jnp.float32)],
        compiler_params=LIMIT,
        cost_estimate=cost(10),
        name="encode_backward",
    )(*carried, mesh, gathered, *args)


def shards(walk, master, moment1, moment2, inputs, targets, valid, owner, slot, neighbours, partner):
    bands = lax.axis_size("space")
    band = lax.axis_index("space")
    peers = lax.axis_size(ALL)
    place = lax.axis_index(ALL)
    shard = master.shape[0]
    total_size = shard * peers
    height = pieces_of(total_size, peers)[3]
    offset = lax.rem(lax.rem(shard, D) * place, D)
    piece = lax.dynamic_update_slice_in_dim(
        jnp.zeros((height * D,), jnp.bfloat16), master.astype(jnp.bfloat16), offset, 0
    )
    state_in = inputs[0]
    counted = valid[0].astype(jnp.float32)
    local_count = jnp.sum(valid[0])
    digits = (local_count >> jnp.array([16, 8, 0], jnp.int32)) & 255
    digits = jnp.pad(digits, (CH + 3, HALF - CH - 6)).astype(jnp.float32)[None, :]
    points = state_in.shape[1]
    blocks = neighbours.shape[0]
    assert blocks == H
    capacity = max(2, 2 * points // bands)
    target_band = owner[0, :, 0]
    hits = (target_band[:, None] == jnp.arange(bands, dtype=jnp.int32)[None, :]).astype(jnp.int32)
    ranks = jnp.sum(jnp.cumsum(hits, 0) * hits, 1) - 1
    places_out = jnp.sum(hits * jnp.asarray(walk, jnp.int32)[None, :], 1) * capacity + ranks
    poster = (
        jnp.arange(bands * capacity, dtype=jnp.int32)[:, None] == places_out[None, :]
    ).astype(jnp.bfloat16)
    spots = slot[0][None, :]
    columns = jnp.concatenate(
        [
            state_in,
            (spots // 64).astype(jnp.bfloat16),
            (spots % 64).astype(jnp.bfloat16),
            jnp.ones((1, points), jnp.bfloat16),
            jnp.zeros((HALF - CH - 3, points), jnp.bfloat16),
        ],
        0,
    )

    def exchanged(rows):
        return lax.all_to_all(
            rows.reshape(bands, capacity, HALF), "space", split_axis=0, concat_axis=0, tiled=True
        ).reshape(bands * capacity, HALF)

    held, posted = gathered_blocks(
        piece.reshape(height, D), (inner(poster, columns, 1, 1) + digits).astype(jnp.bfloat16)
    )
    arrived = exchanged(posted)
    w_in, w_node, w_dec, w_out, *w_round, biases = spread_rows(
        held, total_size, peers, place
    )
    index = 2 * ((neighbours - band * blocks + H) % (blocks * bands)).T
    index = index.reshape(K, 2, blocks // 2).swapaxes(0, 1).reshape(-1)
    index = lax.ppermute(index, "space", list(enumerate(walk)))
    arrived, biases, index = lax.optimization_barrier((arrived, biases, index))
    counts = arrived.reshape(bands, capacity, HALF)[:, 0, CH + 3 : CH + 6].astype(jnp.float32)
    counts = jnp.sum(counts, 0, keepdims=True)
    w_out = jnp.pad(w_out.reshape(D, CH), ((0, 0), (0, HALF - CH)))
    w_round = [mats.reshape(5, D, D) for mats in w_round]
    b_head = biases[:3]
    b_round = biases[3:].reshape(ROUNDS, 2, D)
    mesh, gathered, sent, ids_row, ids = encode_rows(
        arrived, w_in, w_node, biases, w_round[0]
    )
    sent, partner, counted, counts = lax.optimization_barrier((sent, partner, counted, counts))
    counts = counts + swapped(counts, "dp", 1)
    moved = [(n, place) for n, place in enumerate(walk) if n != place]
    stays = jnp.asarray([n == place for n, place in enumerate(walk)])[band]

    def at_home(rows):
        return lax.ppermute(rows, "space", [(j, i) for i, j in moved])

    def settled(own, came):
        return jnp.where(stays, own, came.astype(jnp.float32))

    partner_by = partner - band * points - jnp.arange(points, dtype=jnp.int32)
    coded = jnp.where(partner_by >= NEAR, partner_by - NEAR + 1, 0).astype(jnp.bfloat16)
    low_valid = jnp.concatenate([counted.astype(jnp.bfloat16), coded[None, :]], 0)
    valid_around = jnp.concatenate(
        [
            shifted(low_valid[:, points - ROWW :], "space", 1),
            low_valid,
            shifted(low_valid[:, :ROWW], "space", -1),
        ],
        1,
    )
    kept = []
    sent = [sent]
    for layer in range(ROUNDS):
        pieces, start = [], 0
        arrivals = [halo(walk, sent[0], sent[0])]
        if len(sent) > 1:
            sent[1], arrivals[0] = lax.optimization_barrier((sent[1], arrivals[0]))
            arrivals.append(halo(walk, sent[1], sent[1]))
        terms = node_terms(mesh, w_round[layer], b_round[layer])
        if layer == 1:
            (before, after), valid_around, counts = lax.optimization_barrier(
                (arrivals[0], valid_around, counts)
            )
            arrivals[0] = (before, after)
        for side in ([rows for rows, _ in arrivals], sent, [rows for _, rows in arrivals]):
            for rows in side:
                pieces.append((rows, start))
                start = start + rows.shape[0]
        mats = w_round[layer]
        if layer + 1 < ROUNDS:
            following = w_round[layer + 1]
            reached = [pieces, pieces] if layer == 0 else [pieces[:-1], pieces[1:]]
            indexes = [index[: K * blocks // 2], index[K * blocks // 2 :]]
            *outs, first = round_forward(
                indexes[0], mesh, reached[0], mats, terms, following, half=0
            )
            *outs, second = round_forward(
                indexes[1], mesh, reached[1], mats, terms, following, half=1, into=outs
            )
            sent = [first, second]
        else:
            decoder = (ids, w_dec, w_out, biases)
            outs = round_forward(index, mesh, pieces, mats, terms, None, decoder)
            outs, rest = outs[:5], outs[5:]
        kept.append((mesh, *outs[1:]))
        mesh = outs[0]
    count = counts[0, 0] * 65536.0 + counts[0, 1] * 256.0 + counts[0, 2]
    wide_valid = valid_around[:CH].astype(jnp.float32)
    coded = valid_around[CH : CH + 1, : points + ROWW].astype(jnp.float32)
    weights = [
        (
            by,
            jnp.where(coded == by - NEAR + 1, 1.0, 0.0)
            * wide_valid[:, : points + ROWW]
            * wide_valid[:, by : by + points + ROWW],
        )
        for by in range(NEAR, ROWW + 1)
    ]
    branch_rows, fetched, decoded, dec_turn = rest
    returned = exchanged(branch_rows)
    branch = inner(returned, poster, 0, 0)[:CH]
    err = state_in.astype(jnp.float32) + branch - targets[0].astype(jnp.float32)
    def widened(values):
        low = values.astype(jnp.bfloat16)
        before = shifted(low[:, points - ROWW :], "space", 1).astype(jnp.float32)
        after = shifted(low[:, :ROWW], "space", -1).astype(jnp.float32)
        return jnp.concatenate([before, values, after], 1)

    wide_err = widened(err)
    paired = jnp.zeros((CH, points + ROWW), jnp.float32)
    pair_total = jnp.zeros((CH, points), jnp.float32)
    for by, both in weights:
        gap = both * (wide_err[:, : points + ROWW] - wide_err[:, by : by + points + ROWW])
        paired = paired + gap
        pair_total = pair_total + gap[:, ROWW:] * (
            wide_err[:, ROWW : ROWW + points] - wide_err[:, ROWW + by : ROWW + by + points]
        )
    local_total = jnp.sum(counted * err * err) + 0.5 * jnp.sum(pair_total)
    grad_pred = 2.0 * counted * err + paired[:, ROWW:]
    for by, both in weights:
        gap = both * (wide_err[:, : points + ROWW] - wide_err[:, by : by + points + ROWW])
        grad_pred = grad_pred - gap[:, ROWW - by : ROWW - by + points]
    grad_pred = grad_pred / count
    grad_rows = jnp.pad(grad_pred.astype(jnp.bfloat16), ((0, HALF - CH), (0, 0)))
    landed = exchanged(inner(poster, grad_rows, 1, 1).astype(jnp.bfloat16))
    landed, final_mesh = lax.optimization_barrier((landed, mesh.astype(jnp.bfloat16)))
    final_mesh = at_home(final_mesh)
    mats_grads = [None] * (2 * ROUNDS)
    bias_grads = [None] * ROUNDS
    carried = ()
    for layer in reversed(range(ROUNDS)):
        old, back, update, agg, slopes = kept[layer]
        first_step = not carried
        grad_mesh, leaving, extra, grad_uin, dest_low, to_before, own, to_after = edges_backward(
            index, back, slopes, w_round[layer], carried,
            (ids_row, landed, dec_turn, w_out, w_dec) if first_step else (),
        )
        if first_step:
            to_before, to_after, final_mesh = lax.optimization_barrier(
                (to_before, to_after, final_mesh)
            )
        from_before, from_after = halo(walk, to_after, to_before)
        if first_step:
            from_before, final_mesh, head_grads = lax.optimization_barrier(
                (
                    from_before,
                    settled(mesh, final_mesh),
                    decode_grads(decoded, landed, fetched, extra),
                )
            )
            grad_wout, grad_wdec, grad_bdec = head_grads
        past = () if first_step else (kept[layer + 1][0], extra)
        part, mats_grads[2 * layer + 1], bias_grads[layer], *source = weight_grads(
            old, dest_low, agg, grad_uin, update, leaving, grad_mesh, w_round[layer], past
        )
        if past:
            mats_grads[2 * layer + 2] = source[0]
        carried = (part, own, from_before, from_after, w_round[layer])
    grad_mesh, leaving, grad_win, grad_wnode, grad_bpair, mats_grads[0] = encode_backward(
        carried, kept[0][0], gathered, arrived, ids, w_in, w_node, biases
    )
    parts = [grad_win, grad_wnode, grad_wdec, grad_wout[:, :CH].reshape(CH, D)]
    parts = parts + mats_grads
    parts = parts + [grad_bpair, grad_bdec] + bias_grads
    keep, send = collect_rows(parts, total_size, peers, place)
    mine, leaving = reduced_piece(keep, send, leaving)
    late = at_home(leaving)
    mine = lax.dynamic_slice_in_dim(mine.reshape(-1), offset, shard)
    lane = lax.broadcasted_iota(jnp.int32, (8, HALF), 1)
    sums, late = summed_everywhere(
        jnp.where(lane == 0, local_total, jnp.sum(mine * mine)), late
    )
    total, norm = sums[0, 0], jnp.sqrt(sums[0, 1])
    node_grads = settled(grad_mesh, late)
    clipped = mine * jnp.minimum(1.0, 0.05 / norm)
    first = 0.9 * moment1 + 0.1 * clipped
    second = 0.999 * moment2 + 0.001 * clipped * clipped
    first_hat = first / (1.0 - 0.9**STEP)
    second_hat = second / (1.0 - 0.999**STEP)
    updated = master - 0.1 * (first_hat / (jnp.sqrt(second_hat) + 1e-08) + 0.1 * master)
    return (
        total.reshape(1),
        count.reshape(1),
        norm.reshape(1),
        updated,
        first,
        second,
        updated.astype(jnp.bfloat16),
        final_mesh.reshape(1, blocks, D),
        node_grads.reshape(1, blocks, D),
        grad_pred.reshape(1, grad_pred.shape[0], points),
    )


def solution(mesh):
    return jax.shard_map(
        functools.partial(shards, walk_of(mesh)),
        mesh=mesh,
        in_specs=(
            P(("dp", "space")),
            P(("dp", "space")),
            P(("dp", "space")),
            P("dp", None, "space"),
            P("dp", None, "space"),
            P("dp", None, "space"),
            P("dp", "space", None),
            P("dp", "space"),
            P("space", None),
            P("space"),
        ),
        out_specs=(
            P(),
            P(),
            P(),
            P(("dp", "space")),
            P(("dp", "space")),
            P(("dp", "space")),
            P(("dp", "space")),
            P("dp", "space", None),
            P("dp", "space", None),
            P("dp", None, "space"),
        ),
        check_vma=False,
    )
```

```python
import functools

import jax
import jax.numpy as jnp
from jax import lax
from jax.experimental import pallas as pl
from jax.experimental.pallas import tpu as pltpu
from jax.sharding import PartitionSpec as P

D = 256
HALF = 128
CH = 78
ROUNDS = 3
K = 6
ROWW = 360
NEAR = 358
STEP = 10
H = 2048
ALL = ("dp", "space")
LIMIT = pltpu.CompilerParams(vmem_limit_bytes=60 * 2**20)


def cost(micros):
    return pl.CostEstimate(flops=0, bytes_accessed=micros * 3_000_000, transcendentals=0)


def inner(left, right, left_dim, right_dim):
    return lax.dot_general(
        left, right, (((left_dim,), (right_dim,)), ((), ())), preferred_element_type=jnp.float32
    )


def sigmoid(value):
    return 0.5 * jnp.tanh(0.5 * value) + 0.5


def silu(value):
    return value * sigmoid(value)


def slope(value):
    sigma = sigmoid(value)
    return sigma * (1.0 + value * (1.0 - sigma))


def shifted(shard, axis, by):
    peers = lax.axis_size(axis)
    pairs = [(i, i + by) for i in range(peers) if 0 <= i + by < peers]
    return lax.ppermute(shard, axis, pairs)


def walk_of(mesh):
    count = mesh.shape["space"]
    chips = [getattr(device, "coords", None) for device in mesh.devices[0].reshape(-1)]
    if any(chip is None for chip in chips) or len(set(map(tuple, chips))) != count:
        return list(range(count))
    at = {tuple(chip): n for n, chip in enumerate(chips)}
    xs, ys, zs = (sorted({chip[n] for chip in at}) for n in range(3))
    if len(xs) * len(ys) * len(zs) != count:
        return list(range(count))
    if (len(xs), len(ys), len(zs)) == (2, 2, 4):
        corners = [(0, 0), (1, 0), (0, 1), (1, 1)]
        planes = [(0, 1, 3, 2), (2, 0, 1, 3), (3, 1, 0, 2), (2, 3, 1, 0)]
        steps = [(*corners[n], z) for z, plane in enumerate(planes) for n in plane]
        return [at[(xs[x], ys[y], zs[z])] for x, y, z in steps]
    walk, plane = [], []
    for n, y in enumerate(ys):
        plane = plane + [(x, y) for x in (xs if n % 2 == 0 else xs[::-1])]
    for n, z in enumerate(zs):
        walk = walk + [at[(x, y, z)] for x, y in (plane if n % 2 == 0 else plane[::-1])]
    return walk


def halo(walk, last, initial):
    up = list(zip(walk, walk[1:] + walk[:1]))
    down = [(j, i) for i, j in up]
    return lax.ppermute(last, "space", up), lax.ppermute(initial, "space", down)


def pieces_of(total, peers):
    share = total // peers
    starts = [share * d // D for d in range(peers)]
    counts = [-(-share * (d + 1) // D) - starts[d] for d in range(peers)]
    shared = [share * d % D != 0 for d in range(peers)]
    height = -(-max(counts) // 16) * 16
    return starts, counts, shared, height


def parts_of():
    return [CH, D, D, CH] + [5 * D] * ROUNDS + [3 + 2 * ROUNDS]


def swapped(value, axis, bit):
    return lax.ppermute(value, axis, [(i, i ^ bit) for i in range(lax.axis_size(axis))])


def bits_of(axis):
    return [1 << n for n in range(lax.axis_size(axis).bit_length() - 1)]


def others(value, axis, bits):
    masks = [sum(bit for n, bit in enumerate(bits) if m >> n & 1) for m in range(1, 1 << len(bits))]
    return [swapped(value, axis, mask) for mask in masks]


def upper_groups():
    bits = bits_of("space")[2:]
    return [tuple(bits[n : n + 2]) for n in range(0, len(bits), 2)]


def orders():
    return [(1, 2), (2, 1)]


def summed_everywhere(value, arriving):
    for bits in reversed(upper_groups()):
        value = sum(others(value, "space", bits), value)
    value = value + swapped(value, "dp", 1)
    value, arriving = lax.optimization_barrier((value, arriving))
    return sum(others(value, "space", (1, 2)), value), arriving


def gathered_blocks(piece, posted):
    held, weights, size = piece[None], {}, 1
    for bits in reversed(upper_groups()):
        held = jnp.concatenate([held] + others(held, "space", bits), 0)
        for n, bit in enumerate(bits):
            weights[bit] = size << n
        size = size << len(bits)
    half = piece.shape[0] // 2
    held = [held[:, :half], held[:, half:]]
    ranks = [dict(weights), dict(weights)]
    for turn in (1, 0):
        if turn == 0:
            held[0], held[1], posted = lax.optimization_barrier((*held, posted))
        for n, order in enumerate(orders()):
            held[n] = jnp.concatenate([held[n], swapped(held[n], "space", order[turn])], 0)
            ranks[n][order[turn]] = size
        size = size << 1
    return (held, [swapped(part, "dp", 1) for part in held], ranks), posted


def spread_rows(gathered, total, peers, place):
    (first, second), (first_far, second_far), ranks = gathered
    starts, counts, shared, height = pieces_of(total, peers)
    half, group = height // 2, first.shape[0]
    rows = -(-total // D)
    sizes = parts_of()
    def at(rank, relative):
        spot = 0
        for bit, weight in rank.items():
            spot = spot + jnp.where((relative & bit) != 0, weight, 0)
        return spot

    def body(place_ref, *refs):
        sources, outs, buffer = refs[:4], refs[4:-1], refs[-1]
        me = place_ref[0]
        mine = me // group
        for d in range(peers):
            relative = (me ^ d) & (group - 1)
            spots = [at(rank, relative) for rank in ranks]

            def lay(one, two, d=d, spots=spots):
                piece = jnp.concatenate([one[spots[0]], two[spots[1]]], 0).astype(jnp.float32)
                start, count = starts[d], counts[d]
                if shared[d]:
                    buffer[start : start + 1, :] = buffer[start : start + 1, :] + piece[:1]
                    buffer[start + 1 : start + count, :] = piece[1:count]
                else:
                    buffer[start : start + count, :] = piece[:count]

            @pl.when(mine == d // group)
            def _():
                lay(sources[0], sources[1])

            @pl.when(mine != d // group)
            def _():
                lay(sources[2], sources[3])

        start = 0
        for out, size in zip(outs, sizes):
            out[:size, :] = buffer[start : start + size, :].astype(out.dtype)
            if out.shape[0] > size:
                out[size:, :] = jnp.zeros((out.shape[0] - size, D), out.dtype)
            start = start + size

    kinds = [jnp.bfloat16] * (4 + ROUNDS) + [jnp.float32]
    talls = [HALF] + sizes[1:]
    return pl.pallas_call(
        body,
        grid_spec=pltpu.PrefetchScalarGridSpec(
            num_scalar_prefetch=1,
            grid=(1,),
            in_specs=[whole(first.shape)] * 4,
            out_specs=[whole((tall, D)) for tall in talls],
            scratch_shapes=[pltpu.VMEM((-(-rows // 8) * 8 + 8, D), jnp.float32)],
        ),
        out_shape=[jax.ShapeDtypeStruct((tall, D), kind) for tall, kind in zip(talls, kinds)],
        compiler_params=LIMIT,
        cost_estimate=cost(4),
        name="spread_rows",
    )(place.reshape(1), first, second, first_far, second_far)


def collect_rows(parts, total, peers, place):
    starts, counts, shared, height = pieces_of(total, peers)
    rows = -(-total // D)
    sizes = [min(part.shape[0], size) for part, size in zip(parts, tall_parts())]
    group = lax.axis_size("space")

    def body(place_ref, *refs):
        sources, keep, send, buffer = refs[:-3], refs[-3], refs[-2], refs[-1]
        start = 0
        for source, size in zip(sources, sizes):
            buffer[start : start + size, :] = source[:size, :]
            start = start + size
        if buffer.shape[0] > start:
            buffer[start:, :] = jnp.zeros((buffer.shape[0] - start, D), jnp.float32)
        me = place_ref[0]
        mine = me // group
        for d in range(peers):
            relative = (me ^ d) & (group - 1)

            @pl.when(mine == d // group)
            def _():
                keep[relative] = buffer[starts[d] : starts[d] + height, :]

            @pl.when(mine != d // group)
            def _():
                send[relative] = buffer[starts[d] : starts[d] + height, :].astype(jnp.bfloat16)

    shape = (group, height, D)
    return pl.pallas_call(
        body,
        grid_spec=pltpu.PrefetchScalarGridSpec(
            num_scalar_prefetch=1,
            grid=(1,),
            in_specs=[whole(part.shape) for part in parts],
            out_specs=[whole(shape), whole(shape)],
            scratch_shapes=[pltpu.VMEM((-(-rows // 8) * 8 + height + 8, D), jnp.float32)],
        ),
        out_shape=[
            jax.ShapeDtypeStruct(shape, jnp.float32),
            jax.ShapeDtypeStruct(shape, jnp.bfloat16),
        ],
        compiler_params=LIMIT,
        cost_estimate=cost(5),
        name="collect_rows",
    )(place.reshape(1), *parts)


def reduced_piece(keep, send, leaving):
    kept = keep + swapped(send, "dp", 1).astype(jnp.float32)
    half = kept.shape[1] // 2
    groups = upper_groups()
    inner_shape = (kept.shape[0] // 4, 2, 2, half, D)
    parts = [kept[:, :half].reshape(inner_shape), kept[:, half:].reshape(inner_shape)]
    for n, order in enumerate(orders()):
        for bit in order:
            spot = 2 if bit == 1 and parts[n].ndim == 5 else 1
            stay = lax.index_in_dim(parts[n], 0, spot, keepdims=False)
            leave = lax.index_in_dim(parts[n], 1, spot, keepdims=False)
            parts[n] = stay + swapped(leave.astype(jnp.bfloat16), "space", bit).astype(jnp.float32)
    part = jnp.concatenate(parts, 1)
    part, leaving = lax.optimization_barrier((part, leaving))
    for bits in groups:
        part = part.reshape((-1, 1 << len(bits)) + part.shape[1:])
        masks = [sum(bit for n, bit in enumerate(bits) if m >> n & 1) for m in range(1 << len(bits))]
        low = part.astype(jnp.bfloat16)
        part = sum(
            [
                swapped(low[:, m], "space", mask).astype(jnp.float32)
                for m, mask in enumerate(masks)
                if m
            ],
            part[:, 0],
        )
    return part[0], leaving


def tall_parts():
    return [CH, D, D, CH] + [D, 4 * D] * ROUNDS + [2, 1] + [2] * ROUNDS


def weave(ref, value):
    rows = value.shape[0]
    ref[pl.ds(0, rows, stride=2), :] = value[:, :HALF]
    ref[pl.ds(1, rows, stride=2), :] = value[:, HALF:]


def unweave(ref):
    rows = ref.shape[0] // 2
    return ref[pl.ds(0, rows, stride=2), :], ref[pl.ds(1, rows, stride=2), :]


def selector():
    row = lax.broadcasted_iota(jnp.int32, (8, HALF), 0)
    lane = lax.broadcasted_iota(jnp.int32, (8, HALF), 1)
    slot = jnp.where(lane == CH, 64.0, jnp.where(lane == CH + 1, 1.0, 0.0))
    known = jnp.where(lane == CH + 2, 1.0, 0.0)
    return jnp.where(row == 0, slot, jnp.where(row == 1, known, 0.0)).astype(jnp.bfloat16)


def ids_along(arrived):
    codes = inner(selector(), arrived, 1, 1)
    return jnp.where(codes[1:2, :] > 0, codes[0:1, :], -1.0).astype(jnp.int32)


def ids_down(arrived):
    codes = inner(arrived, selector(), 1, 1)
    return jnp.where(codes[:, 1:2] > 0, codes[:, 0:1], -1.0).astype(jnp.int32)


def whole(shape):
    return pl.BlockSpec(shape, lambda *_: (0,) * len(shape))


def node_terms(mesh, mats, bias):
    blocks = mesh.shape[0]
    tile = 1024

    def body(mesh_ref, mats_ref, bias_ref, dest_ref, self_ref):
        lowered = mesh_ref[...].astype(jnp.bfloat16)
        weave(dest_ref, inner(lowered, mats_ref[1], 1, 0) + bias_ref[0:1, :])
        self_ref[...] = inner(lowered, mats_ref[3], 1, 0) + bias_ref[1:2, :]

    rows = pl.BlockSpec((tile, D), lambda i: (i, 0))
    woven = pl.BlockSpec((2 * tile, HALF), lambda i: (i, 0))
    return pl.pallas_call(
        body,
        grid=(blocks // tile,),
        in_specs=[rows, whole(mats.shape), whole(bias.shape)],
        out_specs=[woven, rows],
        out_shape=[
            jax.ShapeDtypeStruct((2 * blocks, HALF), jnp.float32),
            jax.ShapeDtypeStruct((blocks, D), jnp.float32),
        ],
        compiler_params=pltpu.CompilerParams(vmem_limit_bytes=63 * 2**20),
        cost_estimate=cost(4),
        name="node_terms",
    )(mesh, mats, bias)


def round_forward(index, mesh, pieces, mats, terms, following, decoder=(), half=None, into=()):
    blocks = mesh.shape[0]
    tile, chunk = 512, 16
    turns, high = tile // chunk, 2 * chunk
    more = following is not None
    reach = 2 * (blocks + 2 * H)
    steps = blocks // tile if half is None else blocks // tile // 2
    shift = 0 if half is None else half * steps

    def body(index_ref, mesh_ref, *refs):
        sources, refs = refs[: len(pieces)], refs[len(pieces) :]
        (mats_ref, dest_ref, self_ref), refs = refs[:3], refs[3:]
        table, rows, wide = refs[-3:]
        if more:
            next_ref, refs = refs[0], refs[1 + len(into) :]
            new_ref, back_ref, update_ref, agg_ref, slope_ref, sent_ref = refs[:6]
        else:
            ids_ref, dec_ref, out_ref, head_ref = refs[:4]
            new_ref, back_ref, update_ref, agg_ref, slope_ref = refs[4:9]
            branch_ref, fetched_ref, decoded_ref, turn_ref, total_ref = refs[9:14]
        step = pl.program_id(0)

        @pl.when(step == 0)
        def _():
            for source, (_, start) in zip(sources, pieces):

                @pl.loop(0, source.shape[0] // 256)
                def _(i, source=source, start=start):
                    at = pl.multiple_of(i * 256, 256)
                    to = pl.multiple_of(start + at, 256)
                    table[pl.ds(to, 256), :] = source[pl.ds(at, 256), :].astype(jnp.float32)

        mesh_in = mesh_ref[...]

        part = blocks // 2
        if half is None:
            origin = step // (steps // 2) * (K * part) + lax.rem(step, steps // 2) * tile
        else:
            origin = step * tile

        def fetch(turn):
            for edge in range(K):
                base = edge * part + turn * chunk + origin
                spots = [index_ref[base + u] for u in range(chunk)]
                values = [table[pl.ds(pl.multiple_of(spot, 2), 2), :] for spot in spots]
                for u in range(chunk):
                    spot = pl.multiple_of(edge * 2 * tile + turn * high + 2 * u, 2)
                    rows[pl.ds(spot, 2), :] = values[u]

        def load(turn):
            at = pl.multiple_of(turn * high, high)
            taken = [
                rows[pl.ds(pl.multiple_of(edge * 2 * tile + turn * high, high), high), :]
                for edge in range(K)
            ]
            return at, dest_ref[pl.ds(at, high), :], taken

        def dense(at, dest, taken):
            total = None
            for edge in range(K):
                value = taken[edge] + dest
                sigma = sigmoid(value)
                out = value * sigma
                slope_ref[edge, pl.ds(at, high), :] = (sigma + out * (1.0 - sigma)).astype(
                    jnp.bfloat16
                )
                total = out if total is None else total + out
            wide[pl.ds(at, high), :] = total * (1.0 / K)

        def some(turn, carry):
            loaded = load(turn - 1)
            fetch(turn)
            dense(*loaded)
            return carry

        fetch(0)
        lax.fori_loop(1, turns, some, 0)
        dense(*load(turns - 1))
        first, second = unweave(wide)
        first, second = first.astype(jnp.bfloat16), second.astype(jnp.bfloat16)
        agg_ref[:, :HALF] = first
        agg_ref[:, HALF:] = second
        update_in = (
            inner(first, mats_ref[2, :HALF, :], 1, 0)
            + inner(second, mats_ref[2, HALF:, :], 1, 0)
            + self_ref[...]
        )
        sigma = sigmoid(update_in)
        out = update_in * sigma
        back_ref[...] = sigma + out * (1.0 - sigma)
        update = out.astype(jnp.bfloat16)
        update_ref[...] = update
        new = mesh_in + inner(update, mats_ref[4], 1, 0)
        new_ref[...] = new
        lowered = new.astype(jnp.bfloat16)
        if more:
            weave(wide, inner(lowered, next_ref[0], 1, 0))
            sent_ref[...] = wide[...].astype(jnp.bfloat16)
            return
        nodes = lax.broadcasted_iota(jnp.int32, (ids_ref.shape[0], tile), 1) + step * tile
        chooser = jnp.where(nodes == ids_ref[...], 1.0, 0.0).astype(jnp.bfloat16)
        found = inner(chooser, lowered, 1, 0)

        @pl.when(step == 0)
        def _():
            total_ref[...] = found

        @pl.when(step > 0)
        def _():
            total_ref[...] += found

        @pl.when(step == blocks // tile - 1)
        def _():
            fetched = total_ref[...].astype(jnp.bfloat16)
            fetched_ref[...] = fetched
            value = inner(fetched, dec_ref[...], 1, 0) + head_ref[2:3, :]
            sigma = sigmoid(value)
            out = value * sigma
            turn_ref[...] = sigma + out * (1.0 - sigma)
            decoded = out.astype(jnp.bfloat16)
            decoded_ref[...] = decoded
            branch_ref[...] = inner(decoded, out_ref[...], 1, 0).astype(jnp.bfloat16)

    whole_rows = pl.BlockSpec((tile, D), lambda i, *_: (i + shift, 0))
    woven = pl.BlockSpec((2 * tile, HALF), lambda i, *_: (i + shift, 0))
    ins = [whole_rows] + [pl.BlockSpec(memory_space=pltpu.VMEM)] * len(pieces)
    ins = ins + [whole(mats.shape), woven, whole_rows]
    outs = [whole_rows] * 4 + [pl.BlockSpec((K, 2 * tile, HALF), lambda i, *_: (0, i + shift, 0))]
    shapes = [
        jax.ShapeDtypeStruct((blocks, D), jnp.float32),
        jax.ShapeDtypeStruct((blocks, D), jnp.float32),
        jax.ShapeDtypeStruct((blocks, D), jnp.bfloat16),
        jax.ShapeDtypeStruct((blocks, D), jnp.bfloat16),
        jax.ShapeDtypeStruct((K, 2 * blocks, HALF), jnp.bfloat16),
    ]
    args = [index, mesh] + [rows for rows, _ in pieces] + [mats, *terms]
    if more:
        ins.append(pl.BlockSpec((1, D, D), lambda *_: (0, 0, 0)))
        outs.append(pl.BlockSpec((2 * tile, HALF), lambda i, *_: (i, 0)))
        shapes.append(jax.ShapeDtypeStruct((2 * tile * steps, HALF), jnp.bfloat16))
        args.append(following)
    aliases = {len(args) + n: n for n in range(len(into))}
    ins = ins + [pl.BlockSpec(memory_space=pl.ANY)] * len(into)
    args = args + list(into)
    scratch = []
    if decoder:
        posts = decoder[0].shape[0]
        ins = ins + [whole(arg.shape) for arg in decoder]
        args = args + list(decoder)
        for width, kind in ((HALF, jnp.bfloat16), (D, jnp.bfloat16), (D, jnp.bfloat16), (D, jnp.float32)):
            outs.append(whole((posts, width)))
            shapes.append(jax.ShapeDtypeStruct((posts, width), kind))
        scratch = [pltpu.VMEM((posts, D), jnp.float32)]
    return pl.pallas_call(
        body,
        grid_spec=pltpu.PrefetchScalarGridSpec(
            num_scalar_prefetch=1,
            grid=(steps,),
            in_specs=ins,
            out_specs=outs,
            scratch_shapes=scratch
            + [
                pltpu.VMEM((reach, HALF), jnp.float32),
                pltpu.VMEM((K * 2 * tile, HALF), jnp.float32),
                pltpu.VMEM((2 * tile, HALF), jnp.float32),
            ],
        ),
        out_shape=shapes,
        input_output_aliases=aliases,
        compiler_params=pltpu.CompilerParams(vmem_limit_bytes=63 * 2**20),
        cost_estimate=cost(24 if half is None else 14),
        name="round_forward",
    )(*args)


def edges_backward(index, back, slopes, mats, carried=(), landed=()):
    blocks = back.shape[0]
    tile, chunk = 512, 16
    steps, turns, high = blocks // tile, tile // chunk, 2 * chunk
    reach = 2 * (blocks + 2 * H)

    def body(*refs):
        if carried:
            index_ref, back_ref, slope_ref, mats_ref = refs[:4]
            past, rest = refs[4:9], refs[9:]
            (new_ref, out_ref, sent_ref), rest = rest[:3], rest[3:]
        else:
            index_ref, back_ref, slope_ref, mats_ref = refs[:4]
            (ids_ref, landed_ref, turn_ref, w_out_ref, w_dec_ref), rest = refs[4:9], refs[9:]
            (new_ref, out_ref, gdec_ref), rest = rest[:3], rest[3:]
            gathered, rest = rest[5], rest[:5] + rest[6:]
        guin_ref, low_ref, before_ref, own_ref, after_ref, wide, wider, flows, *tables = rest
        step = pl.program_id(0)

        @pl.when(step == 0)
        def _():
            @pl.loop(0, reach // 256)
            def _(i):
                for table in tables:
                    table[pl.ds(pl.multiple_of(i * 256, 256), 256), :] = jnp.zeros(
                        (256, HALF), jnp.float32
                    )

        if carried:
            new, one, two = ended(*past, wide)
            sent_ref[:, :HALF] = one
            sent_ref[:, HALF:] = two
            new_ref[...] = new
            grad_out = new.astype(jnp.bfloat16)
            out_ref[...] = grad_out
        else:

            @pl.when(step == 0)
            def _():
                grad_dec = inner(landed_ref[...], w_out_ref[...], 1, 1) * turn_ref[...]
                grad_dec = grad_dec.astype(jnp.bfloat16)
                gdec_ref[...] = grad_dec
                gathered[...] = inner(grad_dec, w_dec_ref[...], 1, 1).astype(jnp.bfloat16)

            nodes = lax.broadcasted_iota(jnp.int32, (tile, landed_ref.shape[0]), 0) + step * tile
            chooser = jnp.where(nodes == ids_ref[...], 1.0, 0.0).astype(jnp.bfloat16)
            new = inner(chooser, gathered[...], 1, 0)
            new_ref[...] = new
            grad_out = new.astype(jnp.bfloat16)
            out_ref[...] = grad_out
        grad_uin = (inner(grad_out, mats_ref[4], 1, 1) * back_ref[...]).astype(jnp.bfloat16)
        guin_ref[...] = grad_uin
        weave(wide, inner(grad_uin, mats_ref[2], 1, 1) * (1.0 / K))

        def dense(turn):
            at = pl.multiple_of(turn * high, high)
            grad_agg = wide[pl.ds(at, high), :]
            total, parts = None, []
            for edge in range(K):
                flow = grad_agg * slope_ref[edge, pl.ds(at, high), :].astype(jnp.float32)
                parts.append(flow)
                total = flow if total is None else total + flow
            return at, total, parts

        def keep(turn, at, total, parts):
            for edge in range(K):
                spot = pl.multiple_of(edge * 2 * tile + turn * high, high)
                flows[pl.ds(spot, high), :] = parts[edge]
            wider[pl.ds(at, high), :] = total

        part = blocks // 2
        origin = step // (steps // 2) * (K * part) + lax.rem(step, steps // 2) * tile

        def scatter(turn):
            for u in range(chunk):
                spots, sums = [], []
                for edge in range(K):
                    base = edge * part + turn * chunk + origin
                    spots.append(pl.multiple_of(index_ref[base + u], 2))
                for edge in range(K):
                    spot = pl.multiple_of(edge * 2 * tile + turn * high + 2 * u, 2)
                    sums.append(tables[edge][pl.ds(spots[edge], 2), :] + flows[pl.ds(spot, 2), :])
                for edge in range(K):
                    tables[edge][pl.ds(spots[edge], 2), :] = sums[edge]

        def some(turn, carry):
            found = dense(turn)
            scatter(turn - 1)
            keep(turn, *found)
            return carry

        keep(0, *dense(0))
        lax.fori_loop(1, turns, some, 0)
        scatter(turns - 1)
        first, second = unweave(wider)
        low_ref[:, :HALF] = first.astype(jnp.bfloat16)
        low_ref[:, HALF:] = second.astype(jnp.bfloat16)

        @pl.when(step == steps - 1)
        def _():
            def summed(at):
                value = tables[0][pl.ds(at, 256), :]
                for table in tables[1:]:
                    value = value + table[pl.ds(at, 256), :]
                return value

            @pl.loop(0, 2 * H // 256)
            def _(i):
                at = pl.multiple_of(i * 256, 256)
                far = pl.multiple_of(2 * H + 2 * blocks + at, 256)
                before_ref[pl.ds(at, 256), :] = summed(at).astype(jnp.bfloat16)
                after_ref[pl.ds(at, 256), :] = summed(far).astype(jnp.bfloat16)

            @pl.loop(0, 2 * blocks // 256)
            def _(i):
                at = pl.multiple_of(i * 256, 256)
                own_ref[pl.ds(at, 256), :] = summed(pl.multiple_of(2 * H + at, 256))

    rows = pl.BlockSpec((tile, D), lambda i, *_: (i, 0))
    woven = pl.BlockSpec((2 * tile, HALF), lambda i, *_: (i, 0))
    low = jax.ShapeDtypeStruct((blocks, D), jnp.bfloat16)
    low_posts = (landed[1].shape[0], D) if landed else None
    last = low if carried else jax.ShapeDtypeStruct(low_posts, jnp.bfloat16)
    return pl.pallas_call(
        body,
        grid_spec=pltpu.PrefetchScalarGridSpec(
            num_scalar_prefetch=1,
            grid=(steps,),
            in_specs=[
                rows,
                pl.BlockSpec((K, 2 * tile, HALF), lambda i, *_: (0, i, 0)),
                whole(mats.shape),
            ]
            + ([rows] + [woven] * 3 + [whole(mats.shape)] if carried else [])
            + [whole(arg.shape) for arg in landed],
            out_specs=([rows] * 3 if carried else [rows, rows, whole(low_posts)])
            + [
                rows, rows,
                whole((2 * H, HALF)), whole((2 * blocks, HALF)), whole((2 * H, HALF)),
            ],
            scratch_shapes=([] if carried else [pltpu.VMEM(low_posts, jnp.bfloat16)])
            + [
                pltpu.VMEM((2 * tile, HALF), jnp.float32),
                pltpu.VMEM((2 * tile, HALF), jnp.float32),
                pltpu.VMEM((2 * tile * K, HALF), jnp.float32),
            ]
            + [pltpu.VMEM((reach, HALF), jnp.float32)] * K,
        ),
        out_shape=[
            jax.ShapeDtypeStruct((blocks, D), jnp.float32),
            low,
            last,
            low,
            low,
            jax.ShapeDtypeStruct((2 * H, HALF), jnp.bfloat16),
            jax.ShapeDtypeStruct((2 * blocks, HALF), jnp.float32),
            jax.ShapeDtypeStruct((2 * H, HALF), jnp.bfloat16),
        ],
        compiler_params=pltpu.CompilerParams(vmem_limit_bytes=63 * 2**20),
        cost_estimate=cost(28 if carried else 25),
        name="edges_backward",
    )(index, back, slopes, mats, *carried, *landed)


def ended(part_ref, own_ref, first_ref, last_ref, mats_ref, wide):
    wide[...] = (
        own_ref[...] + first_ref[...].astype(jnp.float32) + last_ref[...].astype(jnp.float32)
    )
    one, two = unweave(wide)
    one, two = one.astype(jnp.bfloat16), two.astype(jnp.bfloat16)
    new = (
        part_ref[...]
        + inner(one, mats_ref[0, :, :HALF], 1, 1)
        + inner(two, mats_ref[0, :, HALF:], 1, 1)
    )
    return new, one, two


def weight_grads(mesh, dest_low, agg, grad_uin, update, leaving, grad_mesh, mats, past=()):
    blocks = mesh.shape[0]
    tile = 512

    def body(mesh_ref, dest_ref, agg_ref, guin_ref, update_ref, out_ref, grad_ref, mats_ref, *refs):
        if past:
            (old_ref, sent_ref), refs = refs[:2], refs[2:]
        part_ref, grads_ref, bias_ref = refs[:3]

        @pl.when(pl.program_id(0) == 0)
        def _():
            for ref in refs[1:]:
                ref[...] = jnp.zeros(ref.shape, jnp.float32)

        lowered = mesh_ref[...].astype(jnp.bfloat16)
        dest, guin = dest_ref[...], guin_ref[...]
        grads_ref[:D, :] += inner(lowered, dest, 0, 0)
        grads_ref[D : 2 * D, :] += inner(agg_ref[...], guin, 0, 0)
        grads_ref[2 * D : 3 * D, :] += inner(lowered, guin, 0, 0)
        grads_ref[3 * D :, :] += inner(update_ref[...], out_ref[...], 0, 0)
        bias_ref[0:1, :] += jnp.sum(dest.astype(jnp.float32), 0, keepdims=True)
        bias_ref[1:2, :] += jnp.sum(guin.astype(jnp.float32), 0, keepdims=True)
        part_ref[...] = (
            grad_ref[...] + inner(guin, mats_ref[3], 1, 1) + inner(dest, mats_ref[1], 1, 1)
        )
        if past:
            refs[3][...] += inner(old_ref[...].astype(jnp.bfloat16), sent_ref[...], 0, 0)

    rows = pl.BlockSpec((tile, D), lambda i: (i, 0))
    shapes = [(4 * D, D), (2, D)] + ([(D, D)] if past else [])
    return pl.pallas_call(
        body,
        grid=(blocks // tile,),
        in_specs=[rows] * 7 + [whole(mats.shape)] + [rows] * len(past),
        out_specs=[rows] + [whole(shape) for shape in shapes],
        out_shape=[jax.ShapeDtypeStruct((blocks, D), jnp.float32)]
        + [jax.ShapeDtypeStruct(shape, jnp.float32) for shape in shapes],
        compiler_params=pltpu.CompilerParams(vmem_limit_bytes=63 * 2**20),
        cost_estimate=cost(10),
        name="weight_grads",
    )(mesh, dest_low, agg, grad_uin, update, leaving, grad_mesh, mats, *past)


def decode_grads(decoded, landed, fetched, grad_dec):
    def body(decoded_ref, landed_ref, fetched_ref, grad_ref, gout_ref, gdec_ref, bias_ref):
        gout_ref[...] = inner(decoded_ref[...], landed_ref[...], 0, 0)
        gdec_ref[...] = inner(fetched_ref[...], grad_ref[...], 0, 0)
        bias_ref[...] = jnp.sum(grad_ref[...].astype(jnp.float32), 0, keepdims=True)

    return pl.pallas_call(
        body,
        out_shape=[jax.ShapeDtypeStruct(shape, jnp.float32) for shape in ((D, HALF), (D, D), (1, D))],
        compiler_params=pltpu.CompilerParams(vmem_limit_bytes=63 * 2**20),
        cost_estimate=cost(3),
        name="decode_grads",
    )(decoded, landed, fetched, grad_dec)


def encode_rows(arrived, w_in, w_node, biases, source):
    posts = arrived.shape[0]
    tile = 1024

    def body(
        arrived_ref, in_ref, node_ref, bias_ref, source_ref,
        mesh_ref, gathered_ref, sent_ref, ids_ref, down_ref, encoded, wide,
    ):
        step = pl.program_id(0)

        @pl.when(step == 0)
        def _():
            entering = inner(arrived_ref[...], in_ref[...], 1, 0) + bias_ref[0:1, :]
            encoded[...] = silu(entering).astype(jnp.bfloat16)
            ids_ref[...] = ids_along(arrived_ref[...])
            down_ref[...] = ids_down(arrived_ref[...])

        nodes = lax.broadcasted_iota(jnp.int32, (tile, posts), 0) + step * tile
        chooser = jnp.where(nodes == ids_ref[...], 1.0, 0.0).astype(jnp.bfloat16)
        gathered = inner(chooser, encoded[...], 1, 0).astype(jnp.bfloat16)
        gathered_ref[...] = gathered
        mesh = silu(inner(gathered, node_ref[...], 1, 0) + bias_ref[1:2, :])
        mesh_ref[...] = mesh
        weave(wide, inner(mesh.astype(jnp.bfloat16), source_ref[0], 1, 0))
        sent_ref[...] = wide[...].astype(jnp.bfloat16)

    rows = pl.BlockSpec((tile, D), lambda i: (i, 0))
    args = (arrived, w_in, w_node, biases, source)
    return pl.pallas_call(
        body,
        grid=(H // tile,),
        in_specs=[whole(arg.shape) for arg in args[:-1]]
        + [pl.BlockSpec((1, D, D), lambda *_: (0, 0, 0))],
        out_specs=[rows, rows, pl.BlockSpec((2 * tile, HALF), lambda i: (i, 0))]
        + [whole((1, posts)), whole((posts, 1))],
        out_shape=[
            jax.ShapeDtypeStruct((H, D), jnp.float32),
            jax.ShapeDtypeStruct((H, D), jnp.bfloat16),
            jax.ShapeDtypeStruct((2 * H, HALF), jnp.bfloat16),
            jax.ShapeDtypeStruct((1, posts), jnp.int32),
            jax.ShapeDtypeStruct((posts, 1), jnp.int32),
        ],
        scratch_shapes=[pltpu.VMEM((posts, D), jnp.bfloat16), pltpu.VMEM((2 * tile, HALF), jnp.float32)],
        compiler_params=LIMIT,
        cost_estimate=cost(5),
        name="encode_rows",
    )(*args)


def encode_backward(carried, mesh, gathered, arrived, ids, w_in, w_node, biases):
    blocks = mesh.shape[0]
    posts = arrived.shape[0]
    tile = 512
    steps = blocks // tile

    def body(
        part_ref, own_ref, first_ref, last_ref, mats_ref,
        mesh_ref, gathered_ref, arrived_ref, ids_ref, in_ref, node_ref, bias_ref,
        new_ref, out_ref, gin_ref, gnode_ref, gbias_ref, gsource_ref, total, wide,
    ):
        step = pl.program_id(0)

        @pl.when(step == 0)
        def _():
            for ref in (total, gnode_ref, gbias_ref, gsource_ref):
                ref[...] = jnp.zeros(ref.shape, jnp.float32)

        new, one, two = ended(part_ref, own_ref, first_ref, last_ref, mats_ref, wide)
        new_ref[...] = new
        out_ref[...] = new.astype(jnp.bfloat16)
        lowered = mesh_ref[...].astype(jnp.bfloat16)
        gsource_ref[:, :HALF] += inner(lowered, one, 0, 0)
        gsource_ref[:, HALF:] += inner(lowered, two, 0, 0)
        node_in = inner(gathered_ref[...], node_ref[...], 1, 0) + bias_ref[1:2, :]
        grad_node = (new * slope(node_in)).astype(jnp.bfloat16)
        gbias_ref[1:2, :] += jnp.sum(grad_node.astype(jnp.float32), 0, keepdims=True)
        gnode_ref[...] += inner(gathered_ref[...], grad_node, 0, 0)
        back = inner(grad_node, node_ref[...], 1, 1).astype(jnp.bfloat16)
        nodes = lax.broadcasted_iota(jnp.int32, (posts, tile), 1) + step * tile
        chooser = jnp.where(nodes == ids_ref[...], 1.0, 0.0).astype(jnp.bfloat16)
        total[...] += inner(chooser, back, 1, 0)

        @pl.when(step == steps - 1)
        def _():
            entering = inner(arrived_ref[...], in_ref[...], 1, 0) + bias_ref[0:1, :]
            grad_enc = (total[...] * slope(entering)).astype(jnp.bfloat16)
            gbias_ref[0:1, :] = jnp.sum(grad_enc.astype(jnp.float32), 0, keepdims=True)
            gin_ref[...] = inner(arrived_ref[...], grad_enc, 0, 0)

    rows = pl.BlockSpec((tile, D), lambda i: (i, 0))
    woven = pl.BlockSpec((2 * tile, HALF), lambda i: (i, 0))
    args = (arrived, ids, w_in, w_node, biases)
    shapes = [(HALF, D), (D, D), (2, D), (D, D)]
    return pl.pallas_call(
        body,
        grid=(steps,),
        in_specs=[rows] + [woven] * 3 + [whole(carried[4].shape), rows, rows]
        + [whole(arg.shape) for arg in args],
        out_specs=[rows, rows] + [whole(shape) for shape in shapes],
        out_shape=[
            jax.ShapeDtypeStruct((blocks, D), jnp.float32),
            jax.ShapeDtypeStruct((blocks, D), jnp.bfloat16),
        ]
        + [jax.ShapeDtypeStruct(shape, jnp.float32) for shape in shapes],
        scratch_shapes=[pltpu.VMEM((posts, D), jnp.float32), pltpu.VMEM((2 * tile, HALF), jnp.float32)],
        compiler_params=LIMIT,
        cost_estimate=cost(10),
        name="encode_backward",
    )(*carried, mesh, gathered, *args)


def shards(walk, master, moment1, moment2, inputs, targets, valid, owner, slot, neighbours, partner):
    bands = lax.axis_size("space")
    band = lax.axis_index("space")
    peers = lax.axis_size(ALL)
    place = lax.axis_index(ALL)
    shard = master.shape[0]
    total_size = shard * peers
    height = pieces_of(total_size, peers)[3]
    offset = lax.rem(lax.rem(shard, D) * place, D)
    piece = lax.dynamic_update_slice_in_dim(
        jnp.zeros((height * D,), jnp.bfloat16), master.astype(jnp.bfloat16), offset, 0
    )
    state_in = inputs[0]
    counted = valid[0].astype(jnp.float32)
    local_count = jnp.sum(valid[0])
    digits = (local_count >> jnp.array([16, 8, 0], jnp.int32)) & 255
    digits = jnp.pad(digits, (CH + 3, HALF - CH - 6)).astype(jnp.float32)[None, :]
    points = state_in.shape[1]
    blocks = neighbours.shape[0]
    assert blocks == H
    capacity = max(2, 2 * points // bands)
    target_band = owner[0, :, 0]
    hits = (target_band[:, None] == jnp.arange(bands, dtype=jnp.int32)[None, :]).astype(jnp.int32)
    ranks = jnp.sum(jnp.cumsum(hits, 0) * hits, 1) - 1
    places_out = jnp.sum(hits * jnp.asarray(walk, jnp.int32)[None, :], 1) * capacity + ranks
    poster = (
        jnp.arange(bands * capacity, dtype=jnp.int32)[:, None] == places_out[None, :]
    ).astype(jnp.bfloat16)
    spots = slot[0][None, :]
    columns = jnp.concatenate(
        [
            state_in,
            (spots // 64).astype(jnp.bfloat16),
            (spots % 64).astype(jnp.bfloat16),
            jnp.ones((1, points), jnp.bfloat16),
            jnp.zeros((HALF - CH - 3, points), jnp.bfloat16),
        ],
        0,
    )

    def exchanged(rows):
        return lax.all_to_all(
            rows.reshape(bands, capacity, HALF), "space", split_axis=0, concat_axis=0, tiled=True
        ).reshape(bands * capacity, HALF)

    held, posted = gathered_blocks(
        piece.reshape(height, D), (inner(poster, columns, 1, 1) + digits).astype(jnp.bfloat16)
    )
    arrived = exchanged(posted)
    w_in, w_node, w_dec, w_out, *w_round, biases = spread_rows(
        held, total_size, peers, place
    )
    index = 2 * ((neighbours - band * blocks + H) % (blocks * bands)).T
    index = index.reshape(K, 2, blocks // 2).swapaxes(0, 1).reshape(-1)
    index = lax.ppermute(index, "space", list(enumerate(walk)))
    arrived, biases, index = lax.optimization_barrier((arrived, biases, index))
    counts = arrived.reshape(bands, capacity, HALF)[:, 0, CH + 3 : CH + 6].astype(jnp.float32)
    counts = jnp.sum(counts, 0, keepdims=True)
    w_out = jnp.pad(w_out.reshape(D, CH), ((0, 0), (0, HALF - CH)))
    w_round = [mats.reshape(5, D, D) for mats in w_round]
    b_head = biases[:3]
    b_round = biases[3:].reshape(ROUNDS, 2, D)
    mesh, gathered, sent, ids_row, ids = encode_rows(
        arrived, w_in, w_node, biases, w_round[0]
    )
    sent, partner, counted, counts = lax.optimization_barrier((sent, partner, counted, counts))
    counts = counts + swapped(counts, "dp", 1)
    moved = [(n, place) for n, place in enumerate(walk) if n != place]
    stays = jnp.asarray([n == place for n, place in enumerate(walk)])[band]

    def at_home(rows):
        return lax.ppermute(rows, "space", [(j, i) for i, j in moved])

    def settled(own, came):
        return jnp.where(stays, own, came.astype(jnp.float32))

    partner_by = partner - band * points - jnp.arange(points, dtype=jnp.int32)
    coded = jnp.where(partner_by >= NEAR, partner_by - NEAR + 1, 0).astype(jnp.bfloat16)
    low_valid = jnp.concatenate([counted.astype(jnp.bfloat16), coded[None, :]], 0)
    valid_around = jnp.concatenate(
        [
            shifted(low_valid[:, points - ROWW :], "space", 1),
            low_valid,
            shifted(low_valid[:, :ROWW], "space", -1),
        ],
        1,
    )
    kept = []
    sent = [sent]
    for layer in range(ROUNDS):
        pieces, start = [], 0
        arrivals = [halo(walk, sent[0], sent[0])]
        if len(sent) > 1:
            sent[1], arrivals[0] = lax.optimization_barrier((sent[1], arrivals[0]))
            arrivals.append(halo(walk, sent[1], sent[1]))
        terms = node_terms(mesh, w_round[layer], b_round[layer])
        if layer == 0:
            (before, after), valid_around, counts = lax.optimization_barrier(
                (arrivals[0], valid_around, counts)
            )
            arrivals[0] = (before, after)
        for side in ([rows for rows, _ in arrivals], sent, [rows for _, rows in arrivals]):
            for rows in side:
                pieces.append((rows, start))
                start = start + rows.shape[0]
        mats = w_round[layer]
        if layer + 1 < ROUNDS:
            following = w_round[layer + 1]
            reached = [pieces, pieces] if layer == 0 else [pieces[:-1], pieces[1:]]
            indexes = [index[: K * blocks // 2], index[K * blocks // 2 :]]
            *outs, first = round_forward(
                indexes[0], mesh, reached[0], mats, terms, following, half=0
            )
            *outs, second = round_forward(
                indexes[1], mesh, reached[1], mats, terms, following, half=1, into=outs
            )
            sent = [first, second]
        else:
            decoder = (ids, w_dec, w_out, biases)
            outs = round_forward(index, mesh, pieces, mats, terms, None, decoder)
            outs, rest = outs[:5], outs[5:]
        kept.append((mesh, *outs[1:]))
        mesh = outs[0]
    count = counts[0, 0] * 65536.0 + counts[0, 1] * 256.0 + counts[0, 2]
    wide_valid = valid_around[:CH].astype(jnp.float32)
    coded = valid_around[CH : CH + 1, : points + ROWW].astype(jnp.float32)
    weights = [
        (
            by,
            jnp.where(coded == by - NEAR + 1, 1.0, 0.0)
            * wide_valid[:, : points + ROWW]
            * wide_valid[:, by : by + points + ROWW],
        )
        for by in range(NEAR, ROWW + 1)
    ]
    branch_rows, fetched, decoded, dec_turn = rest
    returned = exchanged(branch_rows)
    branch = inner(returned, poster, 0, 0)[:CH]
    err = state_in.astype(jnp.float32) + branch - targets[0].astype(jnp.float32)
    def widened(values):
        low = values.astype(jnp.bfloat16)
        before = shifted(low[:, points - ROWW :], "space", 1).astype(jnp.float32)
        after = shifted(low[:, :ROWW], "space", -1).astype(jnp.float32)
        return jnp.concatenate([before, values, after], 1)

    wide_err = widened(err)
    paired = jnp.zeros((CH, points + ROWW), jnp.float32)
    pair_total = jnp.zeros((CH, points), jnp.float32)
    for by, both in weights:
        gap = both * (wide_err[:, : points + ROWW] - wide_err[:, by : by + points + ROWW])
        paired = paired + gap
        pair_total = pair_total + gap[:, ROWW:] * (
            wide_err[:, ROWW : ROWW + points] - wide_err[:, ROWW + by : ROWW + by + points]
        )
    local_total = jnp.sum(counted * err * err) + 0.5 * jnp.sum(pair_total)
    grad_pred = 2.0 * counted * err + paired[:, ROWW:]
    for by, both in weights:
        gap = both * (wide_err[:, : points + ROWW] - wide_err[:, by : by + points + ROWW])
        grad_pred = grad_pred - gap[:, ROWW - by : ROWW - by + points]
    grad_pred = grad_pred / count
    grad_rows = jnp.pad(grad_pred.astype(jnp.bfloat16), ((0, HALF - CH), (0, 0)))
    landed = exchanged(inner(poster, grad_rows, 1, 1).astype(jnp.bfloat16))
    landed, final_mesh = lax.optimization_barrier((landed, mesh.astype(jnp.bfloat16)))
    final_mesh = at_home(final_mesh)
    mats_grads = [None] * (2 * ROUNDS)
    bias_grads = [None] * ROUNDS
    carried = ()
    for layer in reversed(range(ROUNDS)):
        old, back, update, agg, slopes = kept[layer]
        first_step = not carried
        grad_mesh, leaving, extra, grad_uin, dest_low, to_before, own, to_after = edges_backward(
            index, back, slopes, w_round[layer], carried,
            (ids_row, landed, dec_turn, w_out, w_dec) if first_step else (),
        )
        if first_step:
            to_before, to_after, final_mesh = lax.optimization_barrier(
                (to_before, to_after, final_mesh)
            )
        from_before, from_after = halo(walk, to_after, to_before)
        if first_step:
            from_before, final_mesh, head_grads = lax.optimization_barrier(
                (
                    from_before,
                    settled(mesh, final_mesh),
                    decode_grads(decoded, landed, fetched, extra),
                )
            )
            grad_wout, grad_wdec, grad_bdec = head_grads
        past = () if first_step else (kept[layer + 1][0], extra)
        part, mats_grads[2 * layer + 1], bias_grads[layer], *source = weight_grads(
            old, dest_low, agg, grad_uin, update, leaving, grad_mesh, w_round[layer], past
        )
        if past:
            mats_grads[2 * layer + 2] = source[0]
        carried = (part, own, from_before, from_after, w_round[layer])
    grad_mesh, leaving, grad_win, grad_wnode, grad_bpair, mats_grads[0] = encode_backward(
        carried, kept[0][0], gathered, arrived, ids, w_in, w_node, biases
    )
    parts = [grad_win, grad_wnode, grad_wdec, grad_wout[:, :CH].reshape(CH, D)]
    parts = parts + mats_grads
    parts = parts + [grad_bpair, grad_bdec] + bias_grads
    keep, send = collect_rows(parts, total_size, peers, place)
    mine, leaving = reduced_piece(keep, send, leaving)
    late = at_home(leaving)
    mine = lax.dynamic_slice_in_dim(mine.reshape(-1), offset, shard)
    lane = lax.broadcasted_iota(jnp.int32, (8, HALF), 1)
    sums, late = summed_everywhere(
        jnp.where(lane == 0, local_total, jnp.sum(mine * mine)), late
    )
    total, norm = sums[0, 0], jnp.sqrt(sums[0, 1])
    node_grads = settled(grad_mesh, late)
    clipped = mine * jnp.minimum(1.0, 0.05 / norm)
    first = 0.9 * moment1 + 0.1 * clipped
    second = 0.999 * moment2 + 0.001 * clipped * clipped
    first_hat = first / (1.0 - 0.9**STEP)
    second_hat = second / (1.0 - 0.999**STEP)
    updated = master - 0.1 * (first_hat / (jnp.sqrt(second_hat) + 1e-08) + 0.1 * master)
    return (
        total.reshape(1),
        count.reshape(1),
        norm.reshape(1),
        updated,
        first,
        second,
        updated.astype(jnp.bfloat16),
        final_mesh.reshape(1, blocks, D),
        node_grads.reshape(1, blocks, D),
        grad_pred.reshape(1, grad_pred.shape[0], points),
    )


def solution(mesh):
    return jax.shard_map(
        functools.partial(shards, walk_of(mesh)),
        mesh=mesh,
        in_specs=(
            P(("dp", "space")),
            P(("dp", "space")),
            P(("dp", "space")),
            P("dp", None, "space"),
            P("dp", None, "space"),
            P("dp", None, "space"),
            P("dp", "space", None),
            P("dp", "space"),
            P("space", None),
            P("space"),
        ),
        out_specs=(
            P(),
            P(),
            P(),
            P(("dp", "space")),
            P(("dp", "space")),
            P(("dp", "space")),
            P(("dp", "space")),
            P("dp", "space", None),
            P("dp", "space", None),
            P("dp", None, "space"),
        ),
        check_vma=False,
    )
```
